32 devices in a mesh: shard: 4 (over y, x), context: 2 (over core), tensor: 4 (over z).
Axes of the slice: x: 2, y: 2, z: 4, core: 2. Of those that a mesh axis runs over, the one named last changes fastest.
Arguments:
- hidden: bfloat16 [4, 2048, 2048], P('shard', 'context'), may hold values from -6 to 6
- segment_ids: int32 [4, 2048], P('shard', 'context'), may hold values from 0 to 3, as said below
- norm1_gain: float32 [2048], replicated, may hold values from 0.25 to 1.75
- w_query: bfloat16 [2048, 2048], P(('shard', 'context'), 'tensor'), may hold values from -0.125 to 0.125
- w_forget: bfloat16 [2048, 2048], P(('shard', 'context'), 'tensor'), may hold values from -0.125 to 0.125
- w_input: bfloat16 [2048, 2048], P(('shard', 'context'), 'tensor'), may hold values from -0.125 to 0.125
- w_gate_out: bfloat16 [2048, 2048], P(('shard', 'context'), 'tensor'), may hold values from -0.125 to 0.125
- forget_floor: float32 [16, 128], P('tensor'), may hold values from 0.9 to 0.99975
- head_gain: float32 [128], replicated, may hold values from 0.25 to 1.75
- w_out: bfloat16 [2048, 2048], P('tensor', ('shard', 'context')), may hold values from -0.1875 to 0.1875
- norm2_gain: float32 [2048], replicated, may hold values from 0.25 to 1.75
- w_ffn_gate: bfloat16 [2048, 5632], P(('shard', 'context'), 'tensor'), may hold values from -0.125 to 0.125
- w_ffn_up: bfloat16 [2048, 5632], P(('shard', 'context'), 'tensor'), may hold values from -0.125 to 0.125
- w_ffn_down: bfloat16 [5632, 2048], P('tensor', ('shard', 'context')), may hold values from -0.15625 to 0.15625
- out_grad: bfloat16 [4, 2048, 2048], P('shard', 'context'), may hold values from -6 to 6
Outputs:
- block_out: bfloat16 [4, 2048, 2048], P('shard', 'context')
- input_grad: bfloat16 [4, 2048, 2048], P('shard', 'context')
- grad_norm1: float32 [2048], P(('shard', 'context'))
- grad_query: float32 [2048, 2048], P(('shard', 'context'), 'tensor')
- grad_forget: float32 [2048, 2048], P(('shard', 'context'), 'tensor')
- grad_input: float32 [2048, 2048], P(('shard', 'context'), 'tensor')
- grad_gate_out: float32 [2048, 2048], P(('shard', 'context'), 'tensor')
- grad_floor: float32 [16, 128], P('tensor', ('shard', 'context'))
- grad_head_gain: float32 [128], P(('shard', 'context'))
- grad_out_proj: float32 [2048, 2048], P('tensor', ('shard', 'context'))
- grad_norm2: float32 [2048], P(('shard', 'context'))
- grad_ffn_gate: float32 [2048, 5632], P(('shard', 'context'), 'tensor')
- grad_ffn_up: float32 [2048, 5632], P(('shard', 'context'), 'tensor')
- grad_ffn_down: float32 [5632, 2048], P('tensor', ('shard', 'context'))
The draws below stay inside these ranges and needn't reach their ends.
Inputs may be any that keep to these rules, and one draw needn't show every extreme that they name: `segment_ids`: in each sequence a document's tokens are consecutive and share one positive id that differs from the ids of the neighbouring documents; every sequence holds three or more documents and ends with one or more pad slots (id 0), and pads stand nowhere else.
All inputs are finite; a program needn't handle non-finite values.
Results may differ from the reference program's by a relative error of at most 0.018.
Values may be sent and summed in bfloat16 or wider, within the bound.
A program may use at most 256 MiB of HBM per device.

```python
import math
from functools import partial
import jax
import jax.numpy as jnp
from jax import lax

D = 2048
H = 16
DK = 128
DV = 128
FF = 5632
STRETCH = 64
HK = 2048
SEQ_LEN = 2048
BATCH = 4


def draw_segment_ids(key, part):
    base_key = jax.random.fold_in(key, 101)
    power_key = jax.random.fold_in(base_key, 1)
    offset_key = jax.random.fold_in(base_key, 2)
    padding_key = jax.random.fold_in(base_key, 3)
    doc_count = SEQ_LEN // 4
    top_power = max(3, SEQ_LEN.bit_length() - 1)
    powers = jax.random.randint(power_key, (BATCH, doc_count), 2, top_power)
    lowest = jnp.left_shift(jnp.ones_like(powers), powers)
    offsets = jax.random.randint(offset_key, (BATCH, doc_count), 0, 1 << 20)
    lengths = lowest + offsets % lowest
    columns = jnp.arange(doc_count, dtype=jnp.int32)[None, :]
    lengths = jnp.where(columns < 2, 4 + offsets % 4, lengths)
    doc_ends = jnp.minimum(jnp.cumsum(lengths, axis=1), SEQ_LEN)
    row_index = jnp.broadcast_to(jnp.arange(BATCH, dtype=jnp.int32)[:, None], doc_ends.shape)
    marks = jnp.zeros((BATCH, SEQ_LEN + 1), jnp.int32).at[row_index, doc_ends].add(1)
    counted = jnp.cumsum(marks, axis=1)[:, :SEQ_LEN]
    labels = 1 + counted % 3
    positions = jnp.arange(SEQ_LEN, dtype=jnp.int32)
    padding = jax.random.randint(padding_key, (BATCH, 1), 1, max(2, SEQ_LEN // 16))
    return jnp.where(positions[None, :] >= SEQ_LEN - padding, 0, labels).astype(jnp.int32)


def draw_forget_floor(key, part):
    floor_key = jax.random.fold_in(key, 7)
    powers = jax.random.uniform(floor_key, (H, DK), jnp.float32, -3.3, -1.0)
    return 1.0 - jnp.power(10.0, powers)


def level_of(stream_key, dims, cuts, smallest, high):
    factor_of, own = 1.0, jax.random.fold_in(stream_key, 6)
    for position, blocks in cuts:
        steps = jnp.exp(jax.random.uniform(jax.random.fold_in(own, position), (blocks,), jnp.float32, smallest / len(cuts), high / len(cuts)))
        factor_of = factor_of * jnp.repeat(steps, dims[position] // blocks).reshape([-1 if axis == position else 1 for axis in range(len(dims))])
    return factor_of


def centred(key, extent, scale, most, cuts=(), kind=jnp.bfloat16):
    factor_of = level_of(key, extent, cuts, -0.22, 0.18) if cuts else 1.0
    array = jax.random.normal(key, extent, jnp.float32) * scale * factor_of
    return jnp.minimum(jnp.maximum(array, -most), most).astype(kind)


def setup_inputs(seed: int = 0) -> dict:
    key_list = jax.random.split(jax.random.key(seed), 16)
    return {
        "hidden": centred(key_list[0], (BATCH, SEQ_LEN, D), 1.0, 6.0, ((0, 4), (1, 2))),
        "segment_ids": draw_segment_ids(jax.random.fold_in(key_list[15], 71), 0),
        "norm1_gain": jnp.clip(1.0 + 0.15 * jax.random.normal(key_list[2], (D,), jnp.float32), 0.25, 1.75),
        "w_query": centred(key_list[3], (D, HK), D ** -0.5, 0.125, ((0, 8), (1, 4))),
        "w_forget": centred(key_list[4], (D, HK), D ** -0.5, 0.125, ((0, 8), (1, 4))),
        "w_input": centred(key_list[5], (D, D), D ** -0.5, 0.125, ((0, 8), (1, 4))),
        "w_gate_out": centred(key_list[6], (D, D), D ** -0.5, 0.125, ((0, 8), (1, 4))),
        "forget_floor": draw_forget_floor(jax.random.fold_in(key_list[15], 71), 0),
        "head_gain": jnp.clip(1.0 + 0.15 * jax.random.normal(key_list[8], (DV,), jnp.float32), 0.25, 1.75),
        "w_out": centred(key_list[9], (D, D), (D // 2) ** -0.5, 0.1875, ((0, 4), (1, 8))),
        "norm2_gain": jnp.clip(1.0 + 0.15 * jax.random.normal(key_list[10], (D,), jnp.float32), 0.25, 1.75),
        "w_ffn_gate": centred(key_list[11], (D, FF), D ** -0.5, 0.125, ((0, 8), (1, 4))),
        "w_ffn_up": centred(key_list[12], (D, FF), D ** -0.5, 0.125, ((0, 8), (1, 4))),
        "w_ffn_down": centred(key_list[13], (FF, D), (FF // 4) ** -0.5, 0.15625, ((0, 4), (1, 8))),
        "out_grad": centred(key_list[14], (BATCH, SEQ_LEN, D), 1.0, 6.0, ((0, 4), (1, 2))),
    }


@jax.custom_vjp
def low(v):
    return lax.optimization_barrier(v.astype(jnp.bfloat16)).astype(jnp.float32)

@jax.custom_vjp
def low_back(v):
    return v

def low_keep(v):
    return (low(v), None)

def low_pass(kept, grad):
    return (grad,)

def back_keep(v):
    return (v, None)

def back_low(kept, grad):
    return (low(grad),)
low.defvjp(low_keep, low_pass)
low_back.defvjp(back_keep, back_low)
EPSILON = 1e-05
HIGHEST = lax.Precision.HIGHEST

def product(left, right):
    return jnp.dot(left, right, precision=HIGHEST, preferred_element_type=jnp.float32)

def rms_scale(values, weights):
    return values * lax.rsqrt(lax.optimization_barrier(jnp.mean(values * values, axis=-1, keepdims=True)) + EPSILON) * weights

def block_step(key_scale, carried, block_in):
    queries, inputs_in, values, log_decay, starts, keep_flags = block_in
    counter = jnp.cumsum(starts, axis=-1)
    cumulated = jnp.cumsum(log_decay, axis=2)
    keep_col = keep_flags[:, None, :, None]
    length = starts.shape[-1]
    positions = jnp.arange(length)
    causal = positions[:, None] >= positions[None, :]
    linked = jnp.logical_and(counter[:, :, None] == counter[:, None, :], causal[None]).astype(jnp.float32)
    lifted = queries * jnp.exp(cumulated)
    lowered = inputs_in * jnp.exp(-cumulated) * keep_col
    scores = jnp.einsum('ghtk,ghsk->ghts', lifted, lowered, precision=HIGHEST) * linked[:, None]
    fresh_mask = (counter == 0).astype(jnp.float32)[:, None, :, None]
    results = jnp.einsum('ghts,ghsv->ghtv', scores, values, precision=HIGHEST)
    results = results + jnp.einsum('ghtk,ghkv->ghtv', lifted * fresh_mask, carried, precision=HIGHEST)
    results = results * key_scale * keep_col
    ending = cumulated[:, :, -1:, :]
    tail_mask = (counter == counter[:, -1:]).astype(jnp.float32)[:, None, :, None]
    moved_in = inputs_in * jnp.exp(ending - cumulated) * keep_col * tail_mask
    closing = (counter[:, -1] == 0).astype(jnp.float32)[:, None, None, None]
    updated = jnp.exp(ending[:, :, 0, :])[..., None] * closing * carried
    updated = updated + jnp.einsum('ghsk,ghsv->ghkv', moved_in, values, precision=HIGHEST)
    return (updated, results)

def recurrence(key_scale, block_len, starts, keep_flags, queries, inputs_in, values, log_decay, carried):
    groups, length, head_count, key_dim = queries.shape
    value_dim = values.shape[-1]
    blocks = length // block_len

    def split_heads(matrix):
        return matrix.reshape(groups, blocks, block_len, head_count, matrix.shape[-1]).transpose(1, 0, 3, 2, 4)

    def split_flags(matrix):
        return matrix.reshape(groups, blocks, block_len).transpose(1, 0, 2)
    stepper = jax.checkpoint(partial(block_step, key_scale))
    ending, results = lax.scan(stepper, carried, (split_heads(queries), split_heads(inputs_in), split_heads(values), split_heads(log_decay), split_flags(starts), split_flags(keep_flags)))
    return (results.transpose(1, 0, 3, 2, 4).reshape(groups, length, head_count, value_dim), ending)

def block_forward(block_len, starts, keep_flags, inputs, gain_one, query_w, forget_w, input_w, gate_w, floor_w, head_w, out_w, gain_two, ffn_gate_w, ffn_up_w, ffn_down_w):
    groups, length, model_width = inputs.shape
    head_count, key_dim = floor_w.shape
    value_dim = head_w.shape[0]
    tokens = groups * length
    rows_flat = inputs.reshape(tokens, model_width)
    normed_one = low(rms_scale(rows_flat, gain_one))
    query_pre = low_back(product(normed_one, query_w))
    forget_pre = low_back(product(normed_one, forget_w))
    input_pre = low_back(product(normed_one, input_w))
    gate_pre = low_back(product(normed_one, gate_w))
    queries = jax.nn.silu(query_pre)
    open_part = (1.0 - floor_w).reshape(1, head_count * key_dim)
    inputs_in = open_part * jax.nn.sigmoid(-forget_pre)
    log_decay = jnp.log1p(-inputs_in)
    empty_state = jnp.zeros((groups, head_count, key_dim, value_dim), jnp.float32)
    mixed, _ = recurrence(key_dim ** (-0.5), block_len, starts, keep_flags, queries.reshape(groups, length, head_count, key_dim), inputs_in.reshape(groups, length, head_count, key_dim), input_pre.reshape(groups, length, head_count, value_dim), log_decay.reshape(groups, length, head_count, key_dim), empty_state)
    mixed = mixed.reshape(tokens, head_count, value_dim)
    gated_rows = rms_scale(mixed, head_w) * jax.nn.silu(gate_pre.reshape(tokens, head_count, value_dim))
    gated_low = low(gated_rows.reshape(tokens, head_count * value_dim))
    mixer_sum = low_back(product(gated_low, out_w))
    residual = rows_flat + mixer_sum
    normed_two = low(rms_scale(residual, gain_two))
    gate_ffn = low_back(product(normed_two, ffn_gate_w))
    up_ffn = low_back(product(normed_two, ffn_up_w))
    hidden_low = low(jax.nn.silu(gate_ffn) * up_ffn)
    feed_sum = low_back(product(hidden_low, ffn_down_w))
    return (residual + feed_sum).reshape(groups, length, model_width)

def add_pair(left_term, right_term):
    return left_term + right_term

def reference(hidden, segment_ids, norm1_gain, w_query, w_forget, w_input, w_gate_out, forget_floor, head_gain, w_out, norm2_gain, w_ffn_gate, w_ffn_up, w_ffn_down, out_grad):
    group_size = math.gcd(BATCH, max(1, 4096 // SEQ_LEN))
    group_count = BATCH // group_size
    boundary = (segment_ids[:, 1:] != segment_ids[:, :-1]).astype(jnp.float32)
    starts_all = jnp.concatenate([jnp.ones((BATCH, 1), jnp.float32), boundary], axis=1)
    keeps_all = (segment_ids > 0).astype(jnp.float32)
    params = (norm1_gain.astype(jnp.float32), w_query.astype(jnp.float32), w_forget.astype(jnp.float32), w_input.astype(jnp.float32), w_gate_out.astype(jnp.float32), forget_floor.astype(jnp.float32), head_gain.astype(jnp.float32), w_out.astype(jnp.float32), norm2_gain.astype(jnp.float32), w_ffn_gate.astype(jnp.float32), w_ffn_up.astype(jnp.float32), w_ffn_down.astype(jnp.float32))

    def regroup(matrix):
        return matrix.reshape((group_count, group_size) + matrix.shape[1:])

    def one_group(running, pieces):
        inputs, starts, keep_flags, cotangent = pieces
        forward_fn = partial(block_forward, STRETCH, starts, keep_flags)
        result, pull_back = jax.vjp(forward_fn, inputs, *params)
        gradients = pull_back(cotangent)
        running = jax.tree.map(add_pair, running, tuple(gradients[1:]))
        return (running, (result, gradients[0]))
    zeros_init = tuple((jnp.zeros_like(entry) for entry in params))
    running, (result, grad_in) = lax.scan(one_group, zeros_init, (regroup(hidden.astype(jnp.float32)), regroup(starts_all), regroup(keeps_all), regroup(out_grad.astype(jnp.float32))))
    block_out = result.reshape(BATCH, SEQ_LEN, D).astype(jnp.bfloat16)
    input_grad = grad_in.reshape(BATCH, SEQ_LEN, D).astype(jnp.bfloat16)
    return (block_out, input_grad, running[0], running[1], running[2], running[3], running[4], running[5], running[6], running[7], running[8], running[9], running[10], running[11])
```

```python
from functools import partial

import jax
import jax.numpy as jnp
from jax import lax
from jax.sharding import PartitionSpec as P

STRETCH = 64


EPSILON = 1e-05
HIGHEST = lax.Precision.HIGHEST


def prefix(part, axis, combine, identity):
    place = lax.axis_index(axis)
    gathered = jax.tree.map(lambda a: lax.all_gather(a, axis), part)
    state = jax.tree.map(lambda a, e: jnp.zeros_like(a) + jnp.asarray(e, a.dtype), part, identity)

    def one(step, state):
        return combine(
            state, jax.tree.map(lambda a: lax.dynamic_index_in_dim(a, step, 0, False), gathered)
        )

    return lax.fori_loop(0, place, one, state)


def prefix_2(x, axis, join, neutral):
    count = lax.axis_size(axis)
    place = lax.axis_index(axis)
    ahead = count - 1 - place
    gathered = jax.tree.map(
        lambda a, kind: lax.all_gather(a.astype(kind), axis),
        x,
        jax.tree.map(lambda a: jnp.bfloat16 if a.dtype == jnp.float32 else a.dtype, x),
    )
    state = jax.tree.map(lambda a, e: jnp.zeros_like(a) + jnp.asarray(e, a.dtype), x, neutral)

    def one(step, state):
        source = count - 1 - step
        return join(
            state,
            jax.tree.map(
                lambda a, own: lax.dynamic_index_in_dim(a, source, 0, False).astype(own.dtype),
                gathered,
                x,
            ),
        )

    return lax.fori_loop(0, ahead, one, state)


def rms_parts(values):
    inverse = lax.rsqrt(jnp.mean(values * values, axis=-1, keepdims=True) + EPSILON)
    return (values * inverse, inverse)


def head_gated(results, weights, gating):
    unit_rows, _ = rms_parts(results)
    return unit_rows * weights * jax.nn.silu(gating)


def block_step(key_scale, carried, block_in):
    queries, inputs_in, values, log_decay, starts, keep_flags = block_in
    counter = jnp.cumsum(starts, axis=-1)
    cumulated = jnp.cumsum(log_decay, axis=2)
    keep_col = keep_flags[:, None, :, None]
    length = starts.shape[-1]
    positions = jnp.arange(length)
    causal = positions[:, None] >= positions[None, :]
    linked = jnp.logical_and(counter[:, :, None] == counter[:, None, :], causal[None]).astype(
        jnp.float32
    )
    lifted = queries * jnp.exp(cumulated)
    lowered = inputs_in * jnp.exp(-cumulated) * keep_col
    scores = jnp.einsum("ghtk,ghsk->ghts", lifted, lowered, precision=HIGHEST) * linked[:, None]
    fresh_mask = (counter == 0).astype(jnp.float32)[:, None, :, None]
    results = jnp.einsum("ghts,ghsv->ghtv", scores, values, precision=HIGHEST)
    results = results + jnp.einsum(
        "ghtk,ghkv->ghtv", lifted * fresh_mask, carried, precision=HIGHEST
    )
    results = results * key_scale * keep_col
    ending = cumulated[:, :, -1:, :]
    tail_mask = (counter == counter[:, -1:]).astype(jnp.float32)[:, None, :, None]
    moved_in = inputs_in * jnp.exp(ending - cumulated) * keep_col * tail_mask
    closing = (counter[:, -1] == 0).astype(jnp.float32)[:, None, None, None]
    updated = jnp.exp(ending[:, :, 0, :])[..., None] * closing * carried
    updated = updated + jnp.einsum("ghsk,ghsv->ghkv", moved_in, values, precision=HIGHEST)
    return (updated, results)


def recurrence(
    key_scale, block_len, starts, keep_flags, queries, inputs_in, values, log_decay, carried
):
    groups, length, head_count, key_dim = queries.shape
    value_dim = values.shape[-1]
    blocks = length // block_len

    def split_heads(matrix):
        return matrix.reshape(groups, blocks, block_len, head_count, matrix.shape[-1]).transpose(
            1, 0, 3, 2, 4
        )

    def split_flags(matrix):
        return matrix.reshape(groups, blocks, block_len).transpose(1, 0, 2)

    stepper = jax.checkpoint(partial(block_step, key_scale))
    ending, results = lax.scan(
        stepper,
        carried,
        (
            split_heads(queries),
            split_heads(inputs_in),
            split_heads(values),
            split_heads(log_decay),
            split_flags(starts),
            split_flags(keep_flags),
        ),
    )
    return (results.transpose(1, 0, 3, 2, 4).reshape(groups, length, head_count, value_dim), ending)


def choose_side(take_two, take_one, joined, option_one, option_two):
    shaping = (-1,) + (1,) * (joined.ndim - 1)
    return jnp.where(
        take_two.reshape(shaping),
        option_two,
        jnp.where(take_one.reshape(shaping), option_one, joined),
    )


def join_states(earlier, follower):
    decay_one, state_one, first_one, last_one, valid_one = earlier
    decay_two, state_two, first_two, last_two, valid_two = follower
    linked = (last_one == first_two).astype(jnp.float32)
    decay_join = decay_one * decay_two * linked[:, None, None]
    state_join = decay_two[..., None] * linked[:, None, None, None] * state_one + state_two
    take_two = valid_one == 0
    take_one = valid_two == 0
    return (
        choose_side(take_two, take_one, decay_join, decay_one, decay_two),
        choose_side(take_two, take_one, state_join, state_one, state_two),
        choose_side(take_two, take_one, first_one, first_one, first_two),
        choose_side(take_two, take_one, last_two, last_one, last_two),
        jnp.maximum(valid_one, valid_two),
    )


def join_grads(earlier, follower):
    decay_one, state_one = earlier
    decay_two, state_two = follower
    return (decay_one * decay_two, state_two + decay_two[..., None] * state_one)


def scatter_sum(values):
    return lax.psum_scatter(
        values.astype(jnp.bfloat16), "tensor", scatter_dimension=0, tiled=True
    ).astype(jnp.float32)


def gather_rows(values):
    return lax.all_gather(values, "tensor", axis=0, tiled=True)


def local(
    hidden,
    segment_ids,
    norm1_gain,
    w_query,
    w_forget,
    w_input,
    w_gate_out,
    forget_floor,
    head_gain,
    w_out,
    norm2_gain,
    w_ffn_gate,
    w_ffn_up,
    w_ffn_down,
    out_grad,
):
    sequences, span_len, model_width = hidden.shape
    tokens = sequences * span_len
    head_count, key_dim = forget_floor.shape
    value_dim = head_gain.shape[0]
    key_scale = key_dim ** (-0.5)
    mixer_shards = (w_query, w_forget, w_input, w_gate_out, w_out)
    feed_shards = (w_ffn_gate, w_ffn_up, w_ffn_down)
    query_full, forget_full, input_full, gate_out_full, out_full = (
        lax.all_gather(mixer_shards[0], ("shard", "context"), axis=0, tiled=True),
        lax.all_gather(mixer_shards[1], ("shard", "context"), axis=0, tiled=True),
        lax.all_gather(mixer_shards[2], ("shard", "context"), axis=0, tiled=True),
        lax.all_gather(mixer_shards[3], ("shard", "context"), axis=0, tiled=True),
        lax.all_gather(mixer_shards[4], ("shard", "context"), axis=1, tiled=True),
    )
    gate_full, up_full, down_full = (
        lax.all_gather(feed_shards[0], ("shard", "context"), axis=0, tiled=True),
        lax.all_gather(feed_shards[1], ("shard", "context"), axis=0, tiled=True),
        lax.all_gather(feed_shards[2], ("shard", "context"), axis=1, tiled=True),
    )
    inputs = hidden.reshape(tokens, model_width).astype(jnp.float32)
    unit_one, inverse_one = rms_parts(inputs)
    normed_one = (unit_one * norm1_gain).astype(jnp.bfloat16)
    query_pre = jnp.dot(normed_one, query_full, preferred_element_type=jnp.float32)
    forget_pre = jnp.dot(normed_one, forget_full, preferred_element_type=jnp.float32)
    input_pre = jnp.dot(normed_one, input_full, preferred_element_type=jnp.float32)
    gate_pre = jnp.dot(normed_one, gate_out_full, preferred_element_type=jnp.float32)
    queries = jax.nn.silu(query_pre).reshape(sequences, span_len, head_count, key_dim)
    open_part = (1.0 - forget_floor).reshape(1, head_count * key_dim)
    closed = jax.nn.sigmoid(-forget_pre)
    inputs_in = open_part * closed
    log_decay = jnp.log1p(-inputs_in)
    key_blocks = inputs_in.reshape(sequences, span_len, head_count, key_dim)
    decay_blocks = log_decay.reshape(sequences, span_len, head_count, key_dim)
    value_blocks = input_pre.reshape(sequences, span_len, head_count, value_dim)
    boundary = (segment_ids[:, 1:] != segment_ids[:, :-1]).astype(jnp.float32)
    starts = jnp.concatenate([jnp.zeros((sequences, 1), jnp.float32), boundary], axis=1)
    keep_flags = (segment_ids > 0).astype(jnp.float32)
    mixer_fn = partial(recurrence, key_scale, STRETCH, starts, keep_flags)
    empty_state = jnp.zeros((sequences, head_count, key_dim, value_dim), jnp.float32)
    local_out, local_state = mixer_fn(queries, key_blocks, value_blocks, decay_blocks, empty_state)
    reach_mask = (jnp.cumsum(starts, axis=1) == 0).astype(jnp.float32)
    rising = jnp.cumsum(decay_blocks, axis=1)
    lead_rows = queries * jnp.exp(rising) * (reach_mask * keep_flags * key_scale)[:, :, None, None]
    kept_all = (jnp.sum(starts, axis=1) == 0).astype(jnp.float32)
    decay_all = jnp.exp(rising[:, -1]) * kept_all[:, None, None]
    first_ids = segment_ids[:, 0].astype(jnp.float32)
    last_ids = segment_ids[:, -1].astype(jnp.float32)
    ones_seq = jnp.ones((sequences,), jnp.float32)
    identity = (
        jnp.ones_like(decay_all),
        jnp.zeros_like(local_state),
        jnp.zeros_like(first_ids),
        jnp.zeros_like(first_ids),
        jnp.zeros_like(first_ids),
    )
    prefix_in = prefix(
        (decay_all, local_state, first_ids, last_ids, ones_seq), "context", join_states, identity
    )
    link_in = (prefix_in[3] == first_ids).astype(jnp.float32) * prefix_in[4]
    carry_in = prefix_in[1] * link_in[:, None, None, None]
    mixed_out = local_out + jnp.einsum("sthk,shkv->sthv", lead_rows, carry_in, precision=HIGHEST)
    gate_heads = gate_pre.reshape(tokens, head_count, value_dim)
    mixed_rows = mixed_out.reshape(tokens, head_count, value_dim)
    gated_rows = head_gated(mixed_rows, head_gain, gate_heads)
    gated_low = gated_rows.reshape(tokens, head_count * value_dim).astype(jnp.bfloat16)
    mix_part = jnp.dot(gated_low, out_full, preferred_element_type=jnp.float32)
    part_rows = tokens // lax.axis_size("tensor")
    place = lax.axis_index("tensor") * part_rows

    def own_rows(values):
        return lax.dynamic_slice_in_dim(values, place, part_rows, 0)

    inputs_own = own_rows(hidden.reshape(tokens, model_width)).astype(jnp.float32)
    residual = inputs_own + scatter_sum(mix_part)
    unit_two, inverse_two = rms_parts(residual)
    normed_two = gather_rows((unit_two * norm2_gain).astype(jnp.bfloat16))
    gate_ffn = jnp.dot(normed_two, gate_full, preferred_element_type=jnp.float32)
    up_ffn = jnp.dot(normed_two, up_full, preferred_element_type=jnp.float32)
    sigma_gate = jax.nn.sigmoid(gate_ffn)
    active = gate_ffn * sigma_gate
    hidden_low = (active * up_ffn).astype(jnp.bfloat16)
    feed_part = jnp.dot(hidden_low, down_full, preferred_element_type=jnp.float32)
    output_rows = gather_rows((residual + scatter_sum(feed_part)).astype(jnp.bfloat16))
    gate_full, up_full, down_full = (
        lax.all_gather(feed_shards[0], ("shard", "context"), axis=0, tiled=True),
        lax.all_gather(feed_shards[1], ("shard", "context"), axis=0, tiled=True),
        lax.all_gather(feed_shards[2], ("shard", "context"), axis=1, tiled=True),
    )
    query_full, forget_full, input_full, gate_out_full, out_full = (
        lax.all_gather(mixer_shards[0], ("shard", "context"), axis=0, tiled=True),
        lax.all_gather(mixer_shards[1], ("shard", "context"), axis=0, tiled=True),
        lax.all_gather(mixer_shards[2], ("shard", "context"), axis=0, tiled=True),
        lax.all_gather(mixer_shards[3], ("shard", "context"), axis=0, tiled=True),
        lax.all_gather(mixer_shards[4], ("shard", "context"), axis=1, tiled=True),
    )
    grad_rows = out_grad.reshape(tokens, model_width)
    grad_down = jnp.einsum("tf,td->fd", hidden_low, grad_rows, preferred_element_type=jnp.float32)
    grad_hidden = jnp.einsum("td,fd->tf", grad_rows, down_full, preferred_element_type=jnp.float32)
    grad_gate_low = (
        grad_hidden * up_ffn * sigma_gate * (1.0 + gate_ffn * (1.0 - sigma_gate))
    ).astype(jnp.bfloat16)
    grad_up_low = (grad_hidden * active).astype(jnp.bfloat16)
    grad_gate = jnp.einsum(
        "td,tf->df", normed_two, grad_gate_low, preferred_element_type=jnp.float32
    )
    grad_up = jnp.einsum("td,tf->df", normed_two, grad_up_low, preferred_element_type=jnp.float32)
    back_two = jnp.einsum("tf,df->td", grad_gate_low, gate_full, preferred_element_type=jnp.float32)
    back_two = back_two + jnp.einsum(
        "tf,df->td", grad_up_low, up_full, preferred_element_type=jnp.float32
    )
    grad_normed_two = scatter_sum(back_two)
    cotangent_rows = own_rows(grad_rows).astype(jnp.float32)
    grad_norm_two = jnp.sum(grad_normed_two * unit_two, axis=0)
    lifted_two = grad_normed_two * norm2_gain
    grad_residual = cotangent_rows + inverse_two * (
        lifted_two - unit_two * jnp.mean(lifted_two * unit_two, axis=-1, keepdims=True)
    )
    grad_mix_low = gather_rows(grad_residual.astype(jnp.bfloat16))
    grad_out = jnp.einsum("tv,td->vd", gated_low, grad_mix_low, preferred_element_type=jnp.float32)
    grad_gated = jnp.einsum(
        "td,vd->tv", grad_mix_low, out_full, preferred_element_type=jnp.float32
    ).reshape(tokens, head_count, value_dim)
    _, pull_gate = jax.vjp(head_gated, mixed_rows, head_gain, gate_heads)
    grad_mixed, grad_head_part, grad_gate_heads = pull_gate(grad_gated)
    grad_mixed_blocks = grad_mixed.reshape(sequences, span_len, head_count, value_dim)
    carry_back = (
        jnp.einsum("sthk,sthv->shkv", lead_rows, grad_mixed_blocks, precision=HIGHEST)
        * link_in[:, None, None, None]
    )
    decay_back = decay_all * link_in[:, None, None]
    after_back = prefix_2(
        (decay_back, carry_back),
        "context",
        join_grads,
        (jnp.ones_like(decay_back), jnp.zeros_like(carry_back)),
    )
    _, pull_mixer = jax.vjp(mixer_fn, queries, key_blocks, value_blocks, decay_blocks, carry_in)
    grad_queries, grad_keys, grad_values, grad_decay, _ = pull_mixer(
        (grad_mixed_blocks, after_back[1])
    )
    sigma_query = jax.nn.sigmoid(query_pre)
    grad_query_low = (
        grad_queries.reshape(tokens, head_count * key_dim)
        * sigma_query
        * (1.0 + query_pre * (1.0 - sigma_query))
    ).astype(jnp.bfloat16)
    key_total = grad_keys.reshape(tokens, head_count * key_dim) - grad_decay.reshape(
        tokens, head_count * key_dim
    ) / (1.0 - inputs_in)
    grad_floor_part = -jnp.sum(key_total * closed, axis=0).reshape(head_count, key_dim)
    grad_forget_low = (-key_total * open_part * closed * (1.0 - closed)).astype(jnp.bfloat16)
    grad_input_low = grad_values.reshape(tokens, head_count * value_dim).astype(jnp.bfloat16)
    grad_gatepre_low = grad_gate_heads.reshape(tokens, head_count * value_dim).astype(jnp.bfloat16)
    grad_query_w = jnp.einsum(
        "td,tk->dk", normed_one, grad_query_low, preferred_element_type=jnp.float32
    )
    grad_forget_w = jnp.einsum(
        "td,tk->dk", normed_one, grad_forget_low, preferred_element_type=jnp.float32
    )
    grad_input_w = jnp.einsum(
        "td,tk->dk", normed_one, grad_input_low, preferred_element_type=jnp.float32
    )
    grad_gate_w = jnp.einsum(
        "td,tk->dk", normed_one, grad_gatepre_low, preferred_element_type=jnp.float32
    )
    back_one = jnp.einsum(
        "tk,dk->td", grad_query_low, query_full, preferred_element_type=jnp.float32
    )
    back_one = back_one + jnp.einsum(
        "tk,dk->td", grad_forget_low, forget_full, preferred_element_type=jnp.float32
    )
    back_one = back_one + jnp.einsum(
        "tk,dk->td", grad_input_low, input_full, preferred_element_type=jnp.float32
    )
    back_one = back_one + jnp.einsum(
        "tk,dk->td", grad_gatepre_low, gate_out_full, preferred_element_type=jnp.float32
    )
    grad_normed_one = scatter_sum(back_one)
    unit_one, inverse_one = rms_parts(inputs_own)
    grad_norm_one = jnp.sum(grad_normed_one * unit_one, axis=0)
    grad_norm_one, grad_norm_two, head_total = lax.psum(
        (grad_norm_one, grad_norm_two, grad_head_part), "tensor"
    )
    lifted_one = grad_normed_one * norm1_gain
    grad_inputs = grad_residual + inverse_one * (
        lifted_one - unit_one * jnp.mean(lifted_one * unit_one, axis=-1, keepdims=True)
    )
    input_rows = gather_rows(grad_inputs.astype(jnp.bfloat16))
    block_out = output_rows.reshape(sequences, span_len, model_width)
    input_grad = input_rows.reshape(sequences, span_len, model_width)
    shares = (
        lax.psum_scatter(
            grad_query_w.astype(jnp.bfloat16), ("shard", "context"), scatter_dimension=0, tiled=True
        ).astype(jnp.float32),
        lax.psum_scatter(
            grad_forget_w.astype(jnp.bfloat16),
            ("shard", "context"),
            scatter_dimension=0,
            tiled=True,
        ).astype(jnp.float32),
        lax.psum_scatter(
            grad_input_w.astype(jnp.bfloat16), ("shard", "context"), scatter_dimension=0, tiled=True
        ).astype(jnp.float32),
        lax.psum_scatter(
            grad_gate_w.astype(jnp.bfloat16), ("shard", "context"), scatter_dimension=0, tiled=True
        ).astype(jnp.float32),
        lax.psum_scatter(
            grad_floor_part.astype(jnp.bfloat16),
            ("shard", "context"),
            scatter_dimension=1,
            tiled=True,
        ).astype(jnp.float32),
        lax.psum_scatter(
            head_total.astype(jnp.bfloat16), ("shard", "context"), scatter_dimension=0, tiled=True
        ).astype(jnp.float32),
        lax.psum_scatter(
            grad_out.astype(jnp.bfloat16), ("shard", "context"), scatter_dimension=1, tiled=True
        ).astype(jnp.float32),
        lax.psum_scatter(
            grad_norm_one.astype(jnp.bfloat16),
            ("shard", "context"),
            scatter_dimension=0,
            tiled=True,
        ).astype(jnp.float32),
        lax.psum_scatter(
            grad_gate.astype(jnp.bfloat16), ("shard", "context"), scatter_dimension=0, tiled=True
        ).astype(jnp.float32),
        lax.psum_scatter(
            grad_up.astype(jnp.bfloat16), ("shard", "context"), scatter_dimension=0, tiled=True
        ).astype(jnp.float32),
        lax.psum_scatter(
            grad_down.astype(jnp.bfloat16), ("shard", "context"), scatter_dimension=1, tiled=True
        ).astype(jnp.float32),
        lax.psum_scatter(
            grad_norm_two.astype(jnp.bfloat16),
            ("shard", "context"),
            scatter_dimension=0,
            tiled=True,
        ).astype(jnp.float32),
    )
    (
        share_query,
        share_forget,
        share_input,
        share_gate,
        share_floor,
        share_head,
        share_out,
        share_one,
        share_ffn_gate,
        share_ffn_up,
        share_ffn_down,
        share_two,
    ) = shares
    return (
        block_out,
        input_grad,
        share_one,
        share_query,
        share_forget,
        share_input,
        share_gate,
        share_floor,
        share_head,
        share_out,
        share_two,
        share_ffn_gate,
        share_ffn_up,
        share_ffn_down,
    )


def solution(mesh):
    in_specs = (
        P("shard", "context", None),
        P("shard", "context"),
        P(),
        P(("shard", "context"), "tensor"),
        P(("shard", "context"), "tensor"),
        P(("shard", "context"), "tensor"),
        P(("shard", "context"), "tensor"),
        P("tensor", None),
        P(),
        P("tensor", ("shard", "context")),
        P(),
        P(("shard", "context"), "tensor"),
        P(("shard", "context"), "tensor"),
        P("tensor", ("shard", "context")),
        P("shard", "context", None),
    )
    out_specs = (
        P("shard", "context", None),
        P("shard", "context", None),
        P(("shard", "context")),
        P(("shard", "context"), "tensor"),
        P(("shard", "context"), "tensor"),
        P(("shard", "context"), "tensor"),
        P(("shard", "context"), "tensor"),
        P("tensor", ("shard", "context")),
        P(("shard", "context")),
        P("tensor", ("shard", "context")),
        P(("shard", "context")),
        P(("shard", "context"), "tensor"),
        P(("shard", "context"), "tensor"),
        P("tensor", ("shard", "context")),
    )
    return jax.shard_map(local, mesh=mesh, in_specs=in_specs, out_specs=out_specs, check_vma=False)
```

```python
from functools import partial

import jax
import jax.numpy as jnp
from jax import lax
from jax.experimental import pallas as pl
from jax.experimental.pallas import tpu as pltpu
from jax.sharding import PartitionSpec as P

EPSILON = 1e-05


BLOCK = 128
F32 = jnp.float32
BF16 = jnp.bfloat16


def mm(a, b, dims):
    return lax.dot_general(a, b, (dims, ((), ())), preferred_element_type=F32)


def mm_nn(a, b):
    return mm(a, b, ((1,), (0,)))


def mm_nt(a, b):
    return mm(a, b, ((1,), (1,)))


def mm_tn(a, b):
    return mm(a, b, ((0,), (0,)))


def split_sum(tri, values):
    high = values.astype(BF16)
    low = (values - high.astype(F32)).astype(BF16)
    return mm_nn(tri, high) + mm_nn(tri, low)


def block_masks(counts, flags_row):
    rows = counts.shape[0]
    row_ids = lax.broadcasted_iota(jnp.int32, (rows, rows), 0)
    col_ids = lax.broadcasted_iota(jnp.int32, (rows, rows), 1)
    linked = jnp.logical_and(counts == flags_row[0:1], row_ids >= col_ids)
    fresh = (counts == flags_row[1:2, 0:1]).astype(F32)
    tail = (counts == flags_row[2:3, 0:1]).astype(F32)
    closing = (flags_row[1:2, 0:1] == flags_row[2:3, 0:1]).astype(F32)
    return row_ids, col_ids, linked, fresh, tail, closing


def mixer_forward_kernel(
    head_count,
    key_scale,
    pre_ref,
    open_ref,
    count_ref,
    keep_ref,
    flags_ref,
    mixed_ref,
    lead_ref,
    start_ref,
    run_ref,
    end_ref,
    total_ref,
    state_scr,
    run_scr,
):
    step = pl.program_id(0)
    width = open_ref.shape[1]
    lanes = width // head_count

    @pl.when(step == 0)
    def _():
        state_scr[...] = jnp.zeros_like(state_scr)
        run_scr[...] = jnp.zeros_like(run_scr)

    counts, keep = count_ref[...], keep_ref[...]
    row_ids, col_ids, linked, fresh, tail, closing = block_masks(counts, flags_ref[0])
    tri = (row_ids >= col_ids).astype(BF16)
    query_pre = pre_ref[:, :width]
    values = pre_ref[:, 2 * width : 3 * width].astype(BF16)
    keys = open_ref[...] * jax.nn.sigmoid(-pre_ref[:, width : 2 * width])
    cum = split_sum(tri, jnp.log1p(-keys))
    rows = cum.shape[0]
    ending = cum[rows - 1 : rows, :]
    lifted = query_pre * jax.nn.sigmoid(query_pre) * jnp.exp(cum)
    lowered = (keys * jnp.exp(-cum) * keep).astype(BF16)
    moved = (keys * jnp.exp(ending - cum) * (keep * tail)).astype(BF16)
    run = run_scr[...]
    lead_ref[...] = (lifted * jnp.exp(run) * (counts == 0).astype(F32)).astype(BF16)
    run_ref[0] = run
    run_scr[...] = run + ending
    total_ref[...] = run + ending
    fresh_lifted = (lifted * fresh).astype(BF16)
    lifted = lifted.astype(BF16)
    end_decay = jnp.exp(ending) * closing
    for head in range(head_count):
        part = slice(head * lanes, (head + 1) * lanes)
        state = state_scr[head]
        start_ref[0, head] = state
        scores = jnp.where(linked, mm_nt(lifted[:, part], lowered[:, part]), 0.0)
        results = mm_nn(scores.astype(BF16), values[:, part])
        results = results + mm_nt(fresh_lifted[:, part], state.astype(BF16))
        mixed_ref[:, part] = results * (key_scale * keep)
        state = state * end_decay[:, part] + mm_tn(values[:, part], moved[:, part])
        state_scr[head] = state
        end_ref[head] = state


def mixer_forward(pre, open_part, counts, keep, flags, head_count, key_scale):
    tokens, all_width = pre.shape
    width = open_part.shape[1]
    lanes = width // head_count
    blocks = tokens // BLOCK
    return pl.pallas_call(
        partial(mixer_forward_kernel, head_count, key_scale),
        grid=(blocks,),
        in_specs=[
            pl.BlockSpec((BLOCK, all_width), lambda i: (i, 0)),
            pl.BlockSpec((1, width), lambda i: (0, 0)),
            pl.BlockSpec((BLOCK, 1), lambda i: (i, 0)),
            pl.BlockSpec((BLOCK, 1), lambda i: (i, 0)),
            pl.BlockSpec((1, 8, BLOCK), lambda i: (i, 0, 0)),
        ],
        out_specs=[
            pl.BlockSpec((BLOCK, width), lambda i: (i, 0)),
            pl.BlockSpec((BLOCK, width), lambda i: (i, 0)),
            pl.BlockSpec((1, head_count, lanes, lanes), lambda i: (i, 0, 0, 0)),
            pl.BlockSpec((1, 1, width), lambda i: (i, 0, 0)),
            pl.BlockSpec((head_count, lanes, lanes), lambda i: (0, 0, 0)),
            pl.BlockSpec((1, width), lambda i: (0, 0)),
        ],
        out_shape=[
            jax.ShapeDtypeStruct((tokens, width), F32),
            jax.ShapeDtypeStruct((tokens, width), BF16),
            jax.ShapeDtypeStruct((blocks, head_count, lanes, lanes), F32),
            jax.ShapeDtypeStruct((blocks, 1, width), F32),
            jax.ShapeDtypeStruct((head_count, lanes, lanes), F32),
            jax.ShapeDtypeStruct((1, width), F32),
        ],
        scratch_shapes=[
            pltpu.VMEM((head_count, lanes, lanes), F32),
            pltpu.VMEM((1, width), F32),
        ],
        compiler_params=pltpu.CompilerParams(
            dimension_semantics=("arbitrary",), vmem_limit_bytes=40 << 20
        ),
        cost_estimate=pl.CostEstimate(
            flops=tokens * width * BLOCK * 12,
            bytes_accessed=tokens * width * 30,
            transcendentals=tokens * width * 7,
        ),
        name="mixer_forward",
    )(pre, open_part, counts, keep, flags)


def gate_forward_kernel(
    head_count,
    key_scale,
    local_ref,
    lead_ref,
    carry_ref,
    gate_ref,
    gain_ref,
    keep_ref,
    mixed_ref,
    gated_ref,
):
    lanes = gain_ref.shape[1]
    for head in range(head_count):
        part = slice(head * lanes, (head + 1) * lanes)
        carried = mm_nt(lead_ref[:, part], carry_ref[head])
        mixed = local_ref[:, part] + carried * (key_scale * keep_ref[...])
        mixed_ref[:, part] = mixed
        inverse = lax.rsqrt(jnp.mean(mixed * mixed, axis=-1, keepdims=True) + EPSILON)
        gate = gate_ref[:, part]
        gated = mixed * inverse * gain_ref[...] * (gate * jax.nn.sigmoid(gate))
        gated_ref[:, part] = gated.astype(BF16)


def gate_forward(local, lead, carry, pre, gain, keep, key_scale):
    tokens, width = local.shape
    head_count, lanes = carry.shape[0], carry.shape[2]
    rows = 2 * BLOCK
    return pl.pallas_call(
        partial(gate_forward_kernel, head_count, key_scale),
        grid=(tokens // rows,),
        in_specs=[
            pl.BlockSpec((rows, width), lambda i: (i, 0)),
            pl.BlockSpec((rows, width), lambda i: (i, 0)),
            pl.BlockSpec((head_count, lanes, lanes), lambda i: (0, 0, 0)),
            pl.BlockSpec((rows, width), lambda i: (i, 3)),
            pl.BlockSpec((1, lanes), lambda i: (0, 0)),
            pl.BlockSpec((rows, 1), lambda i: (i, 0)),
        ],
        out_specs=[
            pl.BlockSpec((rows, width), lambda i: (i, 0)),
            pl.BlockSpec((rows, width), lambda i: (i, 0)),
        ],
        out_shape=[
            jax.ShapeDtypeStruct((tokens, width), F32),
            jax.ShapeDtypeStruct((tokens, width), BF16),
        ],
        compiler_params=pltpu.CompilerParams(
            dimension_semantics=("arbitrary",), vmem_limit_bytes=40 << 20
        ),
        cost_estimate=pl.CostEstimate(
            flops=tokens * width * 300,
            bytes_accessed=tokens * width * 16,
            transcendentals=tokens * width,
        ),
        name="gate_forward",
    )(local, lead, carry, pre, gain, keep)


def gate_backward_kernel(
    head_count,
    key_scale,
    grad_ref,
    mixed_ref,
    lead_ref,
    gate_ref,
    gain_ref,
    keep_ref,
    grad_mixed_ref,
    grad_gate_ref,
    grad_gain_ref,
    back_ref,
):
    lanes = gain_ref.shape[1]

    @pl.when(pl.program_id(0) == 0)
    def _():
        grad_gain_ref[...] = jnp.zeros_like(grad_gain_ref)
        back_ref[...] = jnp.zeros_like(back_ref)

    gain = gain_ref[...]
    total = jnp.zeros_like(gain)
    for head in range(head_count):
        part = slice(head * lanes, (head + 1) * lanes)
        mixed, gate, grad = mixed_ref[:, part], gate_ref[:, part], grad_ref[:, part]
        inverse = lax.rsqrt(jnp.mean(mixed * mixed, axis=-1, keepdims=True) + EPSILON)
        unit = mixed * inverse
        sigma = jax.nn.sigmoid(gate)
        scaled = grad * unit
        total = total + jnp.sum(scaled * (gate * sigma), axis=0, keepdims=True)
        grad_gate = scaled * gain * sigma * (1.0 + gate * (1.0 - sigma))
        grad_gate_ref[:, part] = grad_gate.astype(BF16)
        lifted = grad * gain * (gate * sigma)
        mean = jnp.mean(lifted * unit, axis=-1, keepdims=True)
        grad_mixed = inverse * (lifted - unit * mean) * (key_scale * keep_ref[...])
        grad_mixed = grad_mixed.astype(BF16)
        grad_mixed_ref[:, part] = grad_mixed
        back_ref[head] += mm_tn(grad_mixed, lead_ref[:, part])
    grad_gain_ref[...] += total


def gate_backward(grad, mixed, lead, pre, gain, keep, head_count, key_scale):
    tokens, width = mixed.shape
    lanes = gain.shape[1]
    rows = 2 * BLOCK
    return pl.pallas_call(
        partial(gate_backward_kernel, head_count, key_scale),
        grid=(tokens // rows,),
        in_specs=[
            pl.BlockSpec((rows, width), lambda i: (i, 0)),
            pl.BlockSpec((rows, width), lambda i: (i, 0)),
            pl.BlockSpec((rows, width), lambda i: (i, 0)),
            pl.BlockSpec((rows, width), lambda i: (i, 3)),
            pl.BlockSpec((1, lanes), lambda i: (0, 0)),
            pl.BlockSpec((rows, 1), lambda i: (i, 0)),
        ],
        out_specs=[
            pl.BlockSpec((rows, width), lambda i: (i, 0)),
            pl.BlockSpec((rows, width), lambda i: (i, 0)),
            pl.BlockSpec((1, lanes), lambda i: (0, 0)),
            pl.BlockSpec((head_count, lanes, lanes), lambda i: (0, 0, 0)),
        ],
        out_shape=[
            jax.ShapeDtypeStruct((tokens, width), BF16),
            jax.ShapeDtypeStruct((tokens, width), BF16),
            jax.ShapeDtypeStruct((1, lanes), F32),
            jax.ShapeDtypeStruct((head_count, lanes, lanes), F32),
        ],
        compiler_params=pltpu.CompilerParams(
            dimension_semantics=("arbitrary",), vmem_limit_bytes=40 << 20
        ),
        cost_estimate=pl.CostEstimate(
            flops=tokens * width * 300,
            bytes_accessed=tokens * width * 18,
            transcendentals=tokens * width,
        ),
        name="gate_backward",
    )(grad, mixed, lead, pre, gain, keep)


def mixer_backward_kernel(
    head_count,
    pre_ref,
    grad_mixed_ref,
    grad_gate_ref,
    start_ref,
    run_ref,
    carry_ref,
    after_ref,
    open_ref,
    count_ref,
    keep_ref,
    flags_ref,
    grads_ref,
    floor_ref,
    grad_scr,
    lifted_scr,
    lowered_scr,
    moved_scr,
    value_scr,
):
    width = open_ref.shape[1]
    lanes = width // head_count

    @pl.when(pl.program_id(0) == 0)
    def _():
        grad_scr[...] = after_ref[...]
        floor_ref[...] = jnp.zeros_like(floor_ref)

    counts, keep = count_ref[...], keep_ref[...]
    flags = flags_ref[0]
    row_ids, col_ids, linked, fresh, tail, closing = block_masks(counts, flags)
    tri = (row_ids >= col_ids).astype(BF16)
    tri_back = (row_ids <= col_ids).astype(BF16)
    query_pre = pre_ref[:, :width]
    values = pre_ref[:, 2 * width : 3 * width].astype(BF16)
    opened = open_ref[...]
    closed = jax.nn.sigmoid(-pre_ref[:, width : 2 * width])
    keys = opened * closed
    cum = split_sum(tri, jnp.log1p(-keys))
    rows = cum.shape[0]
    ending = cum[rows - 1 : rows, :]
    rise, fall = jnp.exp(cum), jnp.exp(-cum) * keep
    shift = jnp.exp(ending - cum) * (keep * tail)
    sigma_query = jax.nn.sigmoid(query_pre)
    lifted = (query_pre * sigma_query * rise).astype(BF16)
    lowered = (keys * fall).astype(BF16)
    moved = (keys * shift).astype(BF16)
    fresh_lifted = (lifted.astype(F32) * fresh).astype(BF16)
    end_decay = jnp.exp(ending) * closing
    lead_in = jnp.exp(run_ref[0]) * (flags[1:2, 0:1] == 0).astype(F32)
    for head in range(head_count):
        part = slice(head * lanes, (head + 1) * lanes)
        grad_out, value = grad_mixed_ref[:, part], values[:, part]
        lift, lower, move = lifted[:, part], lowered[:, part], moved[:, part]
        scores = jnp.where(linked, mm_nt(lift, lower), 0.0).astype(BF16)
        pulls = jnp.where(linked, mm_nt(grad_out, value), 0.0).astype(BF16)
        state = start_ref[0, head] + lead_in[:, part] * carry_ref[head]
        grad_state = grad_scr[head]
        grad_low = grad_state.astype(BF16)
        lifted_scr[:, part] = mm_nn(pulls, lower) + fresh * mm_nn(grad_out, state.astype(BF16))
        lowered_scr[:, part] = mm_tn(pulls, lift)
        grad_moved = mm_nn(value, grad_low)
        moved_scr[:, part] = grad_moved
        grads_ref[:, 2 * width + head * lanes : 2 * width + (head + 1) * lanes] = (
            mm_tn(scores, grad_out) + mm_nt(move, grad_low)
        ).astype(BF16)
        value_scr[:, part] = jnp.sum(
            grad_moved * move.astype(F32), axis=0, keepdims=True
        ) + end_decay[:, part] * jnp.sum(state * grad_state, axis=0, keepdims=True)
        grad_scr[head] = grad_state * end_decay[:, part] + mm_tn(grad_out, fresh_lifted[:, part])
    grad_lifted, grad_lowered, grad_moved = lifted_scr[...], lowered_scr[...], moved_scr[...]
    grad_cum = (
        grad_lifted * lifted.astype(F32)
        - grad_lowered * lowered.astype(F32)
        - grad_moved * moved.astype(F32)
    )
    grad_decay = split_sum(tri_back, grad_cum) + value_scr[...]
    key_total = grad_lowered * fall + grad_moved * shift - grad_decay / (1.0 - keys)
    floor_ref[...] -= jnp.sum(key_total * closed, axis=0, keepdims=True)
    grads_ref[:, :width] = (
        grad_lifted * rise * sigma_query * (1.0 + query_pre * (1.0 - sigma_query))
    ).astype(BF16)
    grads_ref[:, width : 2 * width] = (-key_total * opened * closed * (1.0 - closed)).astype(BF16)
    grads_ref[:, 3 * width :] = grad_gate_ref[...]


def mixer_backward(
    pre, grad_mixed, grad_gate, starts, runs, carry, after, open_part, counts, keep, flags
):
    tokens, all_width = pre.shape
    width = open_part.shape[1]
    head_count, lanes = carry.shape[0], carry.shape[2]
    blocks = tokens // BLOCK
    last = blocks - 1
    return pl.pallas_call(
        partial(mixer_backward_kernel, head_count),
        grid=(blocks,),
        in_specs=[
            pl.BlockSpec((BLOCK, all_width), lambda i: (last - i, 0)),
            pl.BlockSpec((BLOCK, width), lambda i: (last - i, 0)),
            pl.BlockSpec((BLOCK, width), lambda i: (last - i, 0)),
            pl.BlockSpec((1, head_count, lanes, lanes), lambda i: (last - i, 0, 0, 0)),
            pl.BlockSpec((1, 1, width), lambda i: (last - i, 0, 0)),
            pl.BlockSpec((head_count, lanes, lanes), lambda i: (0, 0, 0)),
            pl.BlockSpec((head_count, lanes, lanes), lambda i: (0, 0, 0)),
            pl.BlockSpec((1, width), lambda i: (0, 0)),
            pl.BlockSpec((BLOCK, 1), lambda i: (last - i, 0)),
            pl.BlockSpec((BLOCK, 1), lambda i: (last - i, 0)),
            pl.BlockSpec((1, 8, BLOCK), lambda i: (last - i, 0, 0)),
        ],
        out_specs=[
            pl.BlockSpec((BLOCK, all_width), lambda i: (last - i, 0)),
            pl.BlockSpec((1, width), lambda i: (0, 0)),
        ],
        out_shape=[
            jax.ShapeDtypeStruct((tokens, all_width), BF16),
            jax.ShapeDtypeStruct((1, width), F32),
        ],
        scratch_shapes=[
            pltpu.VMEM((head_count, lanes, lanes), F32),
            pltpu.VMEM((BLOCK, width), F32),
            pltpu.VMEM((BLOCK, width), F32),
            pltpu.VMEM((BLOCK, width), F32),
            pltpu.VMEM((1, width), F32),
        ],
        compiler_params=pltpu.CompilerParams(
            dimension_semantics=("arbitrary",), vmem_limit_bytes=40 << 20
        ),
        cost_estimate=pl.CostEstimate(
            flops=tokens * width * BLOCK * 30,
            bytes_accessed=tokens * width * 36,
            transcendentals=tokens * width * 9,
        ),
        name="mixer_backward",
    )(pre, grad_mixed, grad_gate, starts, runs, carry, after, open_part, counts, keep, flags)


def row_flags(segment_ids):
    ids = segment_ids.reshape(-1)
    tokens = ids.shape[0]
    starts = jnp.concatenate([jnp.zeros((1,), F32), (ids[1:] != ids[:-1]).astype(F32)])
    positions = jnp.arange(tokens)
    counts = jnp.sum(
        jnp.where(positions[None, :] <= positions[:, None], starts[None, :], 0.0), axis=1
    )
    keep = (ids > 0).astype(F32)
    blocks = tokens // BLOCK
    by_block = counts.reshape(blocks, BLOCK)
    lasts = by_block[:, -1]
    before = jnp.concatenate([jnp.zeros((1,), F32), lasts[:-1]])
    wide = (blocks, BLOCK)
    flags = jnp.stack(
        [by_block, jnp.broadcast_to(before[:, None], wide), jnp.broadcast_to(lasts[:, None], wide)]
        + [jnp.zeros(wide, F32)] * 5,
        axis=1,
    )
    return counts[:, None], keep[:, None], flags, lasts[-1]


def from_earlier(values, axis, shift):
    count = lax.axis_size(axis)
    return lax.ppermute(values, axis, [(i, i + shift) for i in range(count - shift)])


def from_later(values, axis, shift):
    count = lax.axis_size(axis)
    return lax.ppermute(values, axis, [(i + shift, i) for i in range(count - shift)])


def state_before(state, decay, first_id, last_id, axis):
    head_count, lanes, _ = state.shape
    ids = jnp.stack([first_id, last_id, jnp.float32(1.0)] + [jnp.float32(0.0)] * 5)
    message = jnp.concatenate(
        [
            state.reshape(head_count * lanes, lanes),
            decay.reshape(head_count, lanes),
            jnp.broadcast_to(ids[:, None], (8, lanes)),
        ]
    )
    rows = head_count * lanes
    total = jnp.zeros_like(state)
    factor = jnp.ones((head_count, 1, lanes), F32)
    follower = first_id
    link_in = jnp.float32(0.0)
    for shift in range(1, lax.axis_size(axis)):
        got = from_earlier(message, axis, shift)
        got_ids = got[rows + head_count :, 0]
        linked = (got_ids[1] == follower).astype(F32) * got_ids[2]
        if shift == 1:
            link_in = linked
        factor = factor * linked
        total = total + factor * got[:rows].reshape(state.shape)
        factor = factor * got[rows : rows + head_count].reshape(head_count, 1, lanes)
        follower = got_ids[0]
    return total, link_in


def grad_after(back, decay, link_in, axis):
    head_count, lanes, _ = back.shape
    rows = head_count * lanes
    message = (
        jnp.concatenate([back.reshape(rows, lanes), decay.reshape(head_count, lanes)]) * link_in
    )
    message = jnp.pad(message, ((0, 8 - head_count % 8 if head_count % 8 else 0), (0, 0)))
    total = jnp.zeros_like(back)
    factor = jnp.ones((head_count, 1, lanes), F32)
    for shift in range(1, lax.axis_size(axis)):
        got = from_later(message, axis, shift)
        total = total + factor * got[:rows].reshape(back.shape)
        factor = factor * got[rows : rows + head_count].reshape(head_count, 1, lanes)
    return total


def scatter_sum(values):
    return lax.psum_scatter(
        values.astype(jnp.bfloat16), "tensor", scatter_dimension=0, tiled=True
    ).astype(jnp.float32)


def gather_rows(values):
    return lax.all_gather(values, "tensor", axis=0, tiled=True)


def rms_parts(values):
    inverse = lax.rsqrt(jnp.mean(values * values, axis=-1, keepdims=True) + EPSILON)
    return (values * inverse, inverse)


def local(
    hidden,
    segment_ids,
    norm1_gain,
    w_query,
    w_forget,
    w_input,
    w_gate_out,
    forget_floor,
    head_gain,
    w_out,
    norm2_gain,
    w_ffn_gate,
    w_ffn_up,
    w_ffn_down,
    out_grad,
):
    sequences, span_len, model_width = hidden.shape
    tokens = sequences * span_len
    head_count, key_dim = forget_floor.shape
    width = head_count * key_dim
    key_scale = key_dim ** (-0.5)
    both = ("shard", "context")
    mixer_full = lax.all_gather(
        jnp.concatenate([w_query, w_forget, w_input, w_gate_out], axis=1), both, axis=0, tiled=True
    )
    out_full = lax.all_gather(w_out, both, axis=1, tiled=True)
    gate_full = lax.all_gather(w_ffn_gate, both, axis=0, tiled=True)
    up_full = lax.all_gather(w_ffn_up, both, axis=0, tiled=True)
    down_full = lax.all_gather(w_ffn_down, both, axis=1, tiled=True)
    part_rows = tokens // lax.axis_size("tensor")
    place = lax.axis_index("tensor") * part_rows

    def own_rows(values):
        return lax.dynamic_slice_in_dim(values, place, part_rows, 0)

    hidden_rows = hidden.reshape(tokens, model_width)
    unit_rows, _ = rms_parts(hidden_rows.astype(F32))
    normed_one = (unit_rows * norm1_gain).astype(BF16)
    pre = jnp.dot(normed_one, mixer_full, preferred_element_type=F32)
    open_part = (1.0 - forget_floor).reshape(1, width)
    counts, keep, flags, last_count = row_flags(segment_ids)
    mixed_local, lead, starts, runs, state_end, run_end = mixer_forward(
        pre, open_part, counts, keep, flags, head_count, key_scale
    )
    decay = (jnp.exp(run_end) * (last_count == 0).astype(F32)).reshape(head_count, 1, key_dim)
    ids = segment_ids.reshape(-1).astype(F32)
    carry, link_in = state_before(state_end, decay, ids[0], ids[-1], "context")
    gain_row = head_gain.reshape(1, -1)
    mixed, gated_low = gate_forward(
        mixed_local, lead, carry.astype(BF16), pre, gain_row, keep, key_scale
    )
    mix_part = jnp.dot(gated_low, out_full, preferred_element_type=F32)
    inputs_own = own_rows(hidden_rows).astype(F32)
    residual = inputs_own + scatter_sum(mix_part)
    unit_two, inverse_two = rms_parts(residual)
    normed_two = gather_rows((unit_two * norm2_gain).astype(BF16))
    gate_ffn = jnp.dot(normed_two, gate_full, preferred_element_type=F32)
    up_ffn = jnp.dot(normed_two, up_full, preferred_element_type=F32)
    sigma_gate = jax.nn.sigmoid(gate_ffn)
    active = gate_ffn * sigma_gate
    hidden_low = (active * up_ffn).astype(BF16)
    feed_part = jnp.dot(hidden_low, down_full, preferred_element_type=F32)
    output_rows = gather_rows((residual + scatter_sum(feed_part)).astype(BF16))
    grad_rows = out_grad.reshape(tokens, model_width)
    grad_down = jnp.einsum("tf,td->fd", hidden_low, grad_rows, preferred_element_type=F32)
    grad_hidden = jnp.einsum("td,fd->tf", grad_rows, down_full, preferred_element_type=F32)
    grad_gate_low = (
        grad_hidden * up_ffn * sigma_gate * (1.0 + gate_ffn * (1.0 - sigma_gate))
    ).astype(BF16)
    grad_up_low = (grad_hidden * active).astype(BF16)
    grad_gate = jnp.einsum("td,tf->df", normed_two, grad_gate_low, preferred_element_type=F32)
    grad_up = jnp.einsum("td,tf->df", normed_two, grad_up_low, preferred_element_type=F32)
    back_two = jnp.einsum("tf,df->td", grad_gate_low, gate_full, preferred_element_type=F32)
    back_two = back_two + jnp.einsum(
        "tf,df->td", grad_up_low, up_full, preferred_element_type=F32
    )
    grad_normed_two = scatter_sum(back_two)
    cotangent_rows = own_rows(grad_rows).astype(F32)
    grad_norm_two = jnp.sum(grad_normed_two * unit_two, axis=0)
    lifted_two = grad_normed_two * norm2_gain
    grad_residual = cotangent_rows + inverse_two * (
        lifted_two - unit_two * jnp.mean(lifted_two * unit_two, axis=-1, keepdims=True)
    )
    grad_mix_low = gather_rows(grad_residual.astype(BF16))
    grad_out = jnp.einsum("tv,td->vd", gated_low, grad_mix_low, preferred_element_type=F32)
    grad_gated = jnp.einsum("td,vd->tv", grad_mix_low, out_full, preferred_element_type=F32)
    grad_mixed, grad_gate_pre, grad_head_part, back = gate_backward(
        grad_gated, mixed, lead, pre, gain_row, keep, head_count, key_scale
    )
    after = grad_after(back, decay, link_in, "context")
    grad_pre, grad_floor_part = mixer_backward(
        pre,
        grad_mixed,
        grad_gate_pre,
        starts,
        runs,
        carry,
        after,
        open_part,
        counts,
        keep,
        flags,
    )
    grad_mixer = jnp.einsum("td,tk->dk", normed_one, grad_pre, preferred_element_type=F32)
    back_one = jnp.einsum("tk,dk->td", grad_pre, mixer_full, preferred_element_type=F32)
    grad_normed_one = scatter_sum(back_one)
    unit_one, inverse_one = rms_parts(inputs_own)
    grad_norm_one = jnp.sum(grad_normed_one * unit_one, axis=0)
    grad_norm_one, grad_norm_two, head_total = lax.psum(
        (grad_norm_one, grad_norm_two, grad_head_part.reshape(-1)), "tensor"
    )
    lifted_one = grad_normed_one * norm1_gain
    grad_inputs = grad_residual + inverse_one * (
        lifted_one - unit_one * jnp.mean(lifted_one * unit_one, axis=-1, keepdims=True)
    )
    input_rows = gather_rows(grad_inputs.astype(BF16))

    def share(values, dim):
        return lax.psum_scatter(
            values.astype(BF16), both, scatter_dimension=dim, tiled=True
        ).astype(F32)

    share_mixer = share(grad_mixer, 0)
    return (
        output_rows.reshape(hidden.shape),
        input_rows.reshape(hidden.shape),
        share(grad_norm_one, 0),
        share_mixer[:, :width],
        share_mixer[:, width : 2 * width],
        share_mixer[:, 2 * width : 3 * width],
        share_mixer[:, 3 * width :],
        share(grad_floor_part.reshape(head_count, key_dim), 1),
        share(head_total, 0),
        share(grad_out, 1),
        share(grad_norm_two, 0),
        share(grad_gate, 0),
        share(grad_up, 0),
        share(grad_down, 1),
    )


def solution(mesh):
    in_specs = (
        P("shard", "context", None),
        P("shard", "context"),
        P(),
        P(("shard", "context"), "tensor"),
        P(("shard", "context"), "tensor"),
        P(("shard", "context"), "tensor"),
        P(("shard", "context"), "tensor"),
        P("tensor", None),
        P(),
        P("tensor", ("shard", "context")),
        P(),
        P(("shard", "context"), "tensor"),
        P(("shard", "context"), "tensor"),
        P("tensor", ("shard", "context")),
        P("shard", "context", None),
    )
    out_specs = (
        P("shard", "context", None),
        P("shard", "context", None),
        P(("shard", "context")),
        P(("shard", "context"), "tensor"),
        P(("shard", "context"), "tensor"),
        P(("shard", "context"), "tensor"),
        P(("shard", "context"), "tensor"),
        P("tensor", ("shard", "context")),
        P(("shard", "context")),
        P("tensor", ("shard", "context")),
        P(("shard", "context")),
        P(("shard", "context"), "tensor"),
        P(("shard", "context"), "tensor"),
        P("tensor", ("shard", "context")),
    )
    return jax.shard_map(local, mesh=mesh, in_specs=in_specs, out_specs=out_specs, check_vma=False)
```

```python
from functools import partial

import jax
import jax.numpy as jnp
from jax import lax
from jax.experimental import pallas as pl
from jax.experimental.pallas import tpu as pltpu
from jax.sharding import PartitionSpec as P

EPSILON = 1e-05


BLOCK = 128
F32 = jnp.float32
BF16 = jnp.bfloat16


def mm(a, b, dims):
    return lax.dot_general(a, b, (dims, ((), ())), preferred_element_type=F32)


def mm_nn(a, b):
    return mm(a, b, ((1,), (0,)))


def mm_nt(a, b):
    return mm(a, b, ((1,), (1,)))


def mm_tn(a, b):
    return mm(a, b, ((0,), (0,)))


def split_sum(tri, values):
    high = values.astype(BF16)
    low = (values - high.astype(F32)).astype(BF16)
    return mm_nn(tri, high) + mm_nn(tri, low)


def block_masks(counts, flags_row):
    rows = counts.shape[0]
    row_ids = lax.broadcasted_iota(jnp.int32, (rows, rows), 0)
    col_ids = lax.broadcasted_iota(jnp.int32, (rows, rows), 1)
    linked = jnp.logical_and(counts == flags_row[0:1], row_ids >= col_ids)
    fresh = (counts == flags_row[1:2, 0:1]).astype(F32)
    tail = (counts == flags_row[2:3, 0:1]).astype(F32)
    closing = (flags_row[1:2, 0:1] == flags_row[2:3, 0:1]).astype(F32)
    return row_ids, col_ids, linked, fresh, tail, closing


def mixer_forward_kernel(
    head_count,
    key_scale,
    pre_ref,
    open_ref,
    count_ref,
    keep_ref,
    flags_ref,
    mixed_ref,
    lead_ref,
    start_ref,
    run_ref,
    end_ref,
    total_ref,
    state_scr,
    run_scr,
):
    step = pl.program_id(0)
    width = open_ref.shape[1]
    lanes = width // head_count

    @pl.when(step == 0)
    def _():
        state_scr[...] = jnp.zeros_like(state_scr)
        run_scr[...] = jnp.zeros_like(run_scr)

    counts, keep = count_ref[...], keep_ref[...]
    row_ids, col_ids, linked, fresh, tail, closing = block_masks(counts, flags_ref[0])
    tri = (row_ids >= col_ids).astype(BF16)
    query_pre = pre_ref[:, :width]
    values = pre_ref[:, 2 * width : 3 * width].astype(BF16)
    keys = open_ref[...] * jax.nn.sigmoid(-pre_ref[:, width : 2 * width])
    cum = split_sum(tri, jnp.log1p(-keys))
    rows = cum.shape[0]
    ending = cum[rows - 1 : rows, :]
    lifted = query_pre * jax.nn.sigmoid(query_pre) * jnp.exp(cum)
    lowered = (keys * jnp.exp(-cum) * keep).astype(BF16)
    moved = (keys * jnp.exp(ending - cum) * (keep * tail)).astype(BF16)
    run = run_scr[...]
    lead_ref[...] = (lifted * jnp.exp(run) * (counts == 0).astype(F32)).astype(BF16)
    run_ref[0] = run
    run_scr[...] = run + ending
    total_ref[...] = run + ending
    fresh_lifted = (lifted * fresh).astype(BF16)
    lifted = lifted.astype(BF16)
    end_decay = jnp.exp(ending) * closing
    for head in range(head_count):
        part = slice(head * lanes, (head + 1) * lanes)
        state = state_scr[head]
        start_ref[0, head] = state
        scores = jnp.where(linked, mm_nt(lifted[:, part], lowered[:, part]), 0.0)
        results = mm_nn(scores.astype(BF16), values[:, part])
        results = results + mm_nt(fresh_lifted[:, part], state.astype(BF16))
        mixed_ref[:, part] = results * (key_scale * keep)
        state = state * end_decay[:, part] + mm_tn(values[:, part], moved[:, part])
        state_scr[head] = state
        end_ref[head] = state


def mixer_forward(pre, open_part, counts, keep, flags, head_count, key_scale):
    tokens, all_width = pre.shape
    width = open_part.shape[1]
    lanes = width // head_count
    blocks = tokens // BLOCK
    return pl.pallas_call(
        partial(mixer_forward_kernel, head_count, key_scale),
        grid=(blocks,),
        in_specs=[
            pl.BlockSpec((BLOCK, all_width), lambda i: (i, 0)),
            pl.BlockSpec((1, width), lambda i: (0, 0)),
            pl.BlockSpec((BLOCK, 1), lambda i: (i, 0)),
            pl.BlockSpec((BLOCK, 1), lambda i: (i, 0)),
            pl.BlockSpec((1, 8, BLOCK), lambda i: (i, 0, 0)),
        ],
        out_specs=[
            pl.BlockSpec((BLOCK, width), lambda i: (i, 0)),
            pl.BlockSpec((BLOCK, width), lambda i: (i, 0)),
            pl.BlockSpec((1, head_count, lanes, lanes), lambda i: (i, 0, 0, 0)),
            pl.BlockSpec((1, 1, width), lambda i: (i, 0, 0)),
            pl.BlockSpec((head_count, lanes, lanes), lambda i: (0, 0, 0)),
            pl.BlockSpec((1, width), lambda i: (0, 0)),
        ],
        out_shape=[
            jax.ShapeDtypeStruct((tokens, width), F32),
            jax.ShapeDtypeStruct((tokens, width), BF16),
            jax.ShapeDtypeStruct((blocks, head_count, lanes, lanes), F32),
            jax.ShapeDtypeStruct((blocks, 1, width), F32),
            jax.ShapeDtypeStruct((head_count, lanes, lanes), F32),
            jax.ShapeDtypeStruct((1, width), F32),
        ],
        scratch_shapes=[
            pltpu.VMEM((head_count, lanes, lanes), F32),
            pltpu.VMEM((1, width), F32),
        ],
        compiler_params=pltpu.CompilerParams(
            dimension_semantics=("arbitrary",), vmem_limit_bytes=40 << 20
        ),
        cost_estimate=pl.CostEstimate(
            flops=tokens * width * BLOCK * 12,
            bytes_accessed=tokens * width * 30,
            transcendentals=tokens * width * 7,
        ),
        name="mixer_forward",
    )(pre, open_part, counts, keep, flags)


def gate_forward_kernel(
    head_count,
    key_scale,
    local_ref,
    lead_ref,
    carry_ref,
    gate_ref,
    gain_ref,
    keep_ref,
    mixed_ref,
    gated_ref,
):
    lanes = gain_ref.shape[1]
    for head in range(head_count):
        part = slice(head * lanes, (head + 1) * lanes)
        carried = mm_nt(lead_ref[:, part], carry_ref[head])
        mixed = local_ref[:, part] + carried * (key_scale * keep_ref[...])
        mixed_ref[:, part] = mixed
        inverse = lax.rsqrt(jnp.mean(mixed * mixed, axis=-1, keepdims=True) + EPSILON)
        gate = gate_ref[:, part]
        gated = mixed * inverse * gain_ref[...] * (gate * jax.nn.sigmoid(gate))
        gated_ref[:, part] = gated.astype(BF16)


def gate_forward(local, lead, carry, pre, gain, keep, key_scale):
    tokens, width = local.shape
    head_count, lanes = carry.shape[0], carry.shape[2]
    rows = 2 * BLOCK
    return pl.pallas_call(
        partial(gate_forward_kernel, head_count, key_scale),
        grid=(tokens // rows,),
        in_specs=[
            pl.BlockSpec((rows, width), lambda i: (i, 0)),
            pl.BlockSpec((rows, width), lambda i: (i, 0)),
            pl.BlockSpec((head_count, lanes, lanes), lambda i: (0, 0, 0)),
            pl.BlockSpec((rows, width), lambda i: (i, 3)),
            pl.BlockSpec((1, lanes), lambda i: (0, 0)),
            pl.BlockSpec((rows, 1), lambda i: (i, 0)),
        ],
        out_specs=[
            pl.BlockSpec((rows, width), lambda i: (i, 0)),
            pl.BlockSpec((rows, width), lambda i: (i, 0)),
        ],
        out_shape=[
            jax.ShapeDtypeStruct((tokens, width), F32),
            jax.ShapeDtypeStruct((tokens, width), BF16),
        ],
        compiler_params=pltpu.CompilerParams(
            dimension_semantics=("arbitrary",), vmem_limit_bytes=40 << 20
        ),
        cost_estimate=pl.CostEstimate(
            flops=tokens * width * 300,
            bytes_accessed=tokens * width * 16,
            transcendentals=tokens * width,
        ),
        name="gate_forward",
    )(local, lead, carry, pre, gain, keep)


def gate_backward_kernel(
    head_count,
    key_scale,
    grad_ref,
    mixed_ref,
    lead_ref,
    gate_ref,
    gain_ref,
    keep_ref,
    grad_mixed_ref,
    grad_gate_ref,
    grad_gain_ref,
    back_ref,
):
    lanes = gain_ref.shape[1]

    @pl.when(pl.program_id(0) == 0)
    def _():
        grad_gain_ref[...] = jnp.zeros_like(grad_gain_ref)
        back_ref[...] = jnp.zeros_like(back_ref)

    gain = gain_ref[...]
    total = jnp.zeros_like(gain)
    for head in range(head_count):
        part = slice(head * lanes, (head + 1) * lanes)
        mixed, gate, grad = mixed_ref[:, part], gate_ref[:, part], grad_ref[:, part]
        inverse = lax.rsqrt(jnp.mean(mixed * mixed, axis=-1, keepdims=True) + EPSILON)
        unit = mixed * inverse
        sigma = jax.nn.sigmoid(gate)
        scaled = grad * unit
        total = total + jnp.sum(scaled * (gate * sigma), axis=0, keepdims=True)
        grad_gate = scaled * gain * sigma * (1.0 + gate * (1.0 - sigma))
        grad_gate_ref[:, part] = grad_gate.astype(BF16)
        lifted = grad * gain * (gate * sigma)
        mean = jnp.mean(lifted * unit, axis=-1, keepdims=True)
        grad_mixed = inverse * (lifted - unit * mean) * (key_scale * keep_ref[...])
        grad_mixed = grad_mixed.astype(BF16)
        grad_mixed_ref[:, part] = grad_mixed
        back_ref[head] += mm_tn(grad_mixed, lead_ref[:, part])
    grad_gain_ref[...] += total


def gate_backward(grad, mixed, lead, pre, gain, keep, head_count, key_scale):
    tokens, width = mixed.shape
    lanes = gain.shape[1]
    rows = 2 * BLOCK
    return pl.pallas_call(
        partial(gate_backward_kernel, head_count, key_scale),
        grid=(tokens // rows,),
        in_specs=[
            pl.BlockSpec((rows, width), lambda i: (i, 0)),
            pl.BlockSpec((rows, width), lambda i: (i, 0)),
            pl.BlockSpec((rows, width), lambda i: (i, 0)),
            pl.BlockSpec((rows, width), lambda i: (i, 3)),
            pl.BlockSpec((1, lanes), lambda i: (0, 0)),
            pl.BlockSpec((rows, 1), lambda i: (i, 0)),
        ],
        out_specs=[
            pl.BlockSpec((rows, width), lambda i: (i, 0)),
            pl.BlockSpec((rows, width), lambda i: (i, 0)),
            pl.BlockSpec((1, lanes), lambda i: (0, 0)),
            pl.BlockSpec((head_count, lanes, lanes), lambda i: (0, 0, 0)),
        ],
        out_shape=[
            jax.ShapeDtypeStruct((tokens, width), BF16),
            jax.ShapeDtypeStruct((tokens, width), BF16),
            jax.ShapeDtypeStruct((1, lanes), F32),
            jax.ShapeDtypeStruct((head_count, lanes, lanes), F32),
        ],
        compiler_params=pltpu.CompilerParams(
            dimension_semantics=("arbitrary",), vmem_limit_bytes=40 << 20
        ),
        cost_estimate=pl.CostEstimate(
            flops=tokens * width * 300,
            bytes_accessed=tokens * width * 18,
            transcendentals=tokens * width,
        ),
        name="gate_backward",
    )(grad, mixed, lead, pre, gain, keep)


def mixer_backward_kernel(
    head_count,
    pre_ref,
    grad_mixed_ref,
    grad_gate_ref,
    start_ref,
    run_ref,
    carry_ref,
    after_ref,
    open_ref,
    count_ref,
    keep_ref,
    flags_ref,
    grads_ref,
    floor_ref,
    grad_scr,
    lifted_scr,
    lowered_scr,
    moved_scr,
    value_scr,
):
    width = open_ref.shape[1]
    lanes = width // head_count

    @pl.when(pl.program_id(0) == 0)
    def _():
        grad_scr[...] = after_ref[...]
        floor_ref[...] = jnp.zeros_like(floor_ref)

    counts, keep = count_ref[...], keep_ref[...]
    flags = flags_ref[0]
    row_ids, col_ids, linked, fresh, tail, closing = block_masks(counts, flags)
    tri = (row_ids >= col_ids).astype(BF16)
    tri_back = (row_ids <= col_ids).astype(BF16)
    query_pre = pre_ref[:, :width]
    values = pre_ref[:, 2 * width : 3 * width].astype(BF16)
    opened = open_ref[...]
    closed = jax.nn.sigmoid(-pre_ref[:, width : 2 * width])
    keys = opened * closed
    cum = split_sum(tri, jnp.log1p(-keys))
    rows = cum.shape[0]
    ending = cum[rows - 1 : rows, :]
    rise, fall = jnp.exp(cum), jnp.exp(-cum) * keep
    shift = jnp.exp(ending - cum) * (keep * tail)
    sigma_query = jax.nn.sigmoid(query_pre)
    lifted = (query_pre * sigma_query * rise).astype(BF16)
    lowered = (keys * fall).astype(BF16)
    moved = (keys * shift).astype(BF16)
    fresh_lifted = (lifted.astype(F32) * fresh).astype(BF16)
    end_decay = jnp.exp(ending) * closing
    lead_in = jnp.exp(run_ref[0]) * (flags[1:2, 0:1] == 0).astype(F32)
    for head in range(head_count):
        part = slice(head * lanes, (head + 1) * lanes)
        grad_out, value = grad_mixed_ref[:, part], values[:, part]
        lift, lower, move = lifted[:, part], lowered[:, part], moved[:, part]
        scores = jnp.where(linked, mm_nt(lift, lower), 0.0).astype(BF16)
        pulls = jnp.where(linked, mm_nt(grad_out, value), 0.0).astype(BF16)
        state = start_ref[0, head] + lead_in[:, part] * carry_ref[head]
        grad_state = grad_scr[head]
        grad_low = grad_state.astype(BF16)
        lifted_scr[:, part] = mm_nn(pulls, lower) + fresh * mm_nn(grad_out, state.astype(BF16))
        lowered_scr[:, part] = mm_tn(pulls, lift)
        grad_moved = mm_nn(value, grad_low)
        moved_scr[:, part] = grad_moved
        grads_ref[:, 2 * width + head * lanes : 2 * width + (head + 1) * lanes] = (
            mm_tn(scores, grad_out) + mm_nt(move, grad_low)
        ).astype(BF16)
        value_scr[:, part] = jnp.sum(
            grad_moved * move.astype(F32), axis=0, keepdims=True
        ) + end_decay[:, part] * jnp.sum(state * grad_state, axis=0, keepdims=True)
        grad_scr[head] = grad_state * end_decay[:, part] + mm_tn(grad_out, fresh_lifted[:, part])
    grad_lifted, grad_lowered, grad_moved = lifted_scr[...], lowered_scr[...], moved_scr[...]
    grad_cum = (
        grad_lifted * lifted.astype(F32)
        - grad_lowered * lowered.astype(F32)
        - grad_moved * moved.astype(F32)
    )
    grad_decay = split_sum(tri_back, grad_cum) + value_scr[...]
    key_total = grad_lowered * fall + grad_moved * shift - grad_decay / (1.0 - keys)
    floor_ref[...] -= jnp.sum(key_total * closed, axis=0, keepdims=True)
    grads_ref[:, :width] = (
        grad_lifted * rise * sigma_query * (1.0 + query_pre * (1.0 - sigma_query))
    ).astype(BF16)
    grads_ref[:, width : 2 * width] = (-key_total * opened * closed * (1.0 - closed)).astype(BF16)
    grads_ref[:, 3 * width :] = grad_gate_ref[...]


def mixer_backward(
    pre, grad_mixed, grad_gate, starts, runs, carry, after, open_part, counts, keep, flags
):
    tokens, all_width = pre.shape
    width = open_part.shape[1]
    head_count, lanes = carry.shape[0], carry.shape[2]
    blocks = tokens // BLOCK
    last = blocks - 1
    return pl.pallas_call(
        partial(mixer_backward_kernel, head_count),
        grid=(blocks,),
        in_specs=[
            pl.BlockSpec((BLOCK, all_width), lambda i: (last - i, 0)),
            pl.BlockSpec((BLOCK, width), lambda i: (last - i, 0)),
            pl.BlockSpec((BLOCK, width), lambda i: (last - i, 0)),
            pl.BlockSpec((1, head_count, lanes, lanes), lambda i: (last - i, 0, 0, 0)),
            pl.BlockSpec((1, 1, width), lambda i: (last - i, 0, 0)),
            pl.BlockSpec((head_count, lanes, lanes), lambda i: (0, 0, 0)),
            pl.BlockSpec((head_count, lanes, lanes), lambda i: (0, 0, 0)),
            pl.BlockSpec((1, width), lambda i: (0, 0)),
            pl.BlockSpec((BLOCK, 1), lambda i: (last - i, 0)),
            pl.BlockSpec((BLOCK, 1), lambda i: (last - i, 0)),
            pl.BlockSpec((1, 8, BLOCK), lambda i: (last - i, 0, 0)),
        ],
        out_specs=[
            pl.BlockSpec((BLOCK, all_width), lambda i: (last - i, 0)),
            pl.BlockSpec((1, width), lambda i: (0, 0)),
        ],
        out_shape=[
            jax.ShapeDtypeStruct((tokens, all_width), BF16),
            jax.ShapeDtypeStruct((1, width), F32),
        ],
        scratch_shapes=[
            pltpu.VMEM((head_count, lanes, lanes), F32),
            pltpu.VMEM((BLOCK, width), F32),
            pltpu.VMEM((BLOCK, width), F32),
            pltpu.VMEM((BLOCK, width), F32),
            pltpu.VMEM((1, width), F32),
        ],
        compiler_params=pltpu.CompilerParams(
            dimension_semantics=("arbitrary",), vmem_limit_bytes=40 << 20
        ),
        cost_estimate=pl.CostEstimate(
            flops=tokens * width * BLOCK * 30,
            bytes_accessed=tokens * width * 36,
            transcendentals=tokens * width * 9,
        ),
        name="mixer_backward",
    )(pre, grad_mixed, grad_gate, starts, runs, carry, after, open_part, counts, keep, flags)


def row_flags(segment_ids):
    ids = segment_ids.reshape(-1)
    tokens = ids.shape[0]
    starts = jnp.concatenate([jnp.zeros((1,), F32), (ids[1:] != ids[:-1]).astype(F32)])
    positions = jnp.arange(tokens)
    counts = jnp.sum(
        jnp.where(positions[None, :] <= positions[:, None], starts[None, :], 0.0), axis=1
    )
    keep = (ids > 0).astype(F32)
    blocks = tokens // BLOCK
    by_block = counts.reshape(blocks, BLOCK)
    lasts = by_block[:, -1]
    before = jnp.concatenate([jnp.zeros((1,), F32), lasts[:-1]])
    wide = (blocks, BLOCK)
    flags = jnp.stack(
        [by_block, jnp.broadcast_to(before[:, None], wide), jnp.broadcast_to(lasts[:, None], wide)]
        + [jnp.zeros(wide, F32)] * 5,
        axis=1,
    )
    return counts[:, None], keep[:, None], flags, lasts[-1]


def from_earlier(values, axis, shift):
    count = lax.axis_size(axis)
    return lax.ppermute(values, axis, [(i, i + shift) for i in range(count - shift)])


def from_later(values, axis, shift):
    count = lax.axis_size(axis)
    return lax.ppermute(values, axis, [(i + shift, i) for i in range(count - shift)])


def state_before(state, decay, first_id, last_id, axis):
    head_count, lanes, _ = state.shape
    ids = jnp.stack([first_id, last_id, jnp.float32(1.0)] + [jnp.float32(0.0)] * 5)
    message = jnp.concatenate(
        [
            state.reshape(head_count * lanes, lanes),
            decay.reshape(head_count, lanes),
            jnp.broadcast_to(ids[:, None], (8, lanes)),
        ]
    )
    rows = head_count * lanes
    total = jnp.zeros_like(state)
    factor = jnp.ones((head_count, 1, lanes), F32)
    follower = first_id
    link_in = jnp.float32(0.0)
    for shift in range(1, lax.axis_size(axis)):
        got = from_earlier(message, axis, shift)
        got_ids = got[rows + head_count :, 0]
        linked = (got_ids[1] == follower).astype(F32) * got_ids[2]
        if shift == 1:
            link_in = linked
        factor = factor * linked
        total = total + factor * got[:rows].reshape(state.shape)
        factor = factor * got[rows : rows + head_count].reshape(head_count, 1, lanes)
        follower = got_ids[0]
    return total, link_in


def grad_after(back, decay, link_in, axis):
    head_count, lanes, _ = back.shape
    rows = head_count * lanes
    message = (
        jnp.concatenate([back.reshape(rows, lanes), decay.reshape(head_count, lanes)]) * link_in
    )
    message = jnp.pad(message, ((0, 8 - head_count % 8 if head_count % 8 else 0), (0, 0)))
    total = jnp.zeros_like(back)
    factor = jnp.ones((head_count, 1, lanes), F32)
    for shift in range(1, lax.axis_size(axis)):
        got = from_later(message, axis, shift)
        total = total + factor * got[:rows].reshape(back.shape)
        factor = factor * got[rows : rows + head_count].reshape(head_count, 1, lanes)
    return total


CHUNK = 32
LAG = 2


def line_exchange_kernel(transform, mesh_axes, n_in, n_out, *refs):
    part, extra_in = refs[0], refs[1 : 1 + n_in]
    out, extra_out = refs[1 + n_in], refs[2 + n_in : 2 + n_in + n_out]
    arrived, passed, sum_send, sum_recv, back_send, back_recv = refs[2 + n_in + n_out :]
    half = part.shape[0] // 2
    chunks = half // CHUNK
    size = lax.axis_size("tensor")
    place = lax.axis_index("tensor")
    others = {axis: lax.axis_index(axis) for axis in mesh_axes}

    def device(position):
        return tuple(
            jnp.clip(position, 0, size - 1) if axis == "tensor" else others[axis]
            for axis in mesh_axes
        )

    barrier = pltpu.get_barrier_semaphore()
    for step in (-1, 1):
        inside = jnp.logical_and(place + step >= 0, place + step < size)

        @pl.when(inside)
        def _(step=step):
            pl.semaphore_signal(
                barrier, inc=1, device_id=device(place + step), device_id_type=pl.DeviceIdType.MESH
            )

    at_end = jnp.logical_or(place == 0, place == size - 1)
    pl.semaphore_wait(barrier, jnp.where(at_end, 1, 2))

    transform(None, None, None, extra_in, out, extra_out)

    lines = ((size - 1 - place, -1), (place, 1))

    def rows_of(side, index):
        return pl.ds(pl.multiple_of(side * half + index * CHUNK, CHUNK), CHUNK)

    def sum_copy(side, index, source):
        rows = rows_of(side, index)
        return pltpu.make_async_remote_copy(
            source.at[rows],
            arrived.at[rows],
            sum_send.at[side, index],
            sum_recv.at[side, index],
            device_id=device(place + lines[side][1]),
            device_id_type=pl.DeviceIdType.MESH,
        )

    def back_copy(side, index):
        rows = rows_of(side, index)
        return pltpu.make_async_remote_copy(
            out.at[rows],
            out.at[rows],
            back_send.at[side, index],
            back_recv.at[side, index],
            device_id=device(place - lines[side][1]),
            device_id_type=pl.DeviceIdType.MESH,
        )

    def step(time, _):
        for side in (0, 1):
            hops = lines[side][0]
            index = time - LAG * hops
            valid = jnp.logical_and(index >= 0, index < chunks)
            at_source, at_owner = hops == 0, hops == size - 1
            index = jnp.clip(index, 0, chunks - 1)

            @pl.when(jnp.logical_and(valid, at_source))
            def _(side=side, index=index):
                sum_copy(side, index, part).start()

            @pl.when(jnp.logical_and(valid, jnp.logical_not(at_source)))
            def _(side=side, index=index):
                sum_copy(side, index, passed).wait_recv()

            @pl.when(
                jnp.logical_and(
                    valid, jnp.logical_and(jnp.logical_not(at_source), jnp.logical_not(at_owner))
                )
            )
            def _(side=side, index=index):
                rows = rows_of(side, index)
                passed[rows] = (part[rows].astype(F32) + arrived[rows].astype(F32)).astype(BF16)
                sum_copy(side, index, passed).start()

            @pl.when(jnp.logical_and(valid, at_owner))
            def _(side=side, index=index):
                rows = rows_of(side, index)
                total = part[rows].astype(F32) + arrived[rows].astype(F32)
                own = pl.ds(pl.multiple_of(index * CHUNK, CHUNK), CHUNK)
                transform(total, rows, own, extra_in, out, extra_out)
                back_copy(side, index).start()

            away = size - 1 - hops
            index = time - LAG * (size - 1 + away)
            valid = jnp.logical_and(jnp.logical_and(index >= 0, index < chunks), away > 0)
            index = jnp.clip(index, 0, chunks - 1)

            @pl.when(valid)
            def _(side=side, index=index):
                back_copy(side, index).wait_recv()

            @pl.when(jnp.logical_and(valid, away < size - 1))
            def _(side=side, index=index):
                back_copy(side, index).start()

        return 0

    lax.fori_loop(0, chunks + 2 * LAG * (size - 1), step, 0)

    def finish(index, _):
        for side in (0, 1):
            hops = lines[side][0]

            @pl.when(hops < size - 1)
            def _(side=side):
                sum_copy(side, index, passed).wait_send()

            @pl.when(hops > 0)
            def _(side=side):
                back_copy(side, index).wait_send()

        return 0

    lax.fori_loop(0, chunks, finish, 0)


def line_exchange(transform, mesh_axes, collective, part, extras, extra_shapes, name):
    tokens, width = part.shape
    chunks = tokens // 2 // CHUNK
    whole = pl.BlockSpec(memory_space=pltpu.VMEM)
    return pl.pallas_call(
        partial(
            line_exchange_kernel, transform, mesh_axes, len(extras), len(extra_shapes)
        ),
        in_specs=[whole] * (1 + len(extras)),
        out_specs=[whole] * (1 + len(extra_shapes)),
        out_shape=[jax.ShapeDtypeStruct((tokens, width), BF16)] + list(extra_shapes),
        scratch_shapes=[
            pltpu.VMEM((tokens, width), BF16),
            pltpu.VMEM((tokens, width), BF16),
            pltpu.SemaphoreType.DMA((2, chunks)),
            pltpu.SemaphoreType.DMA((2, chunks)),
            pltpu.SemaphoreType.DMA((2, chunks)),
            pltpu.SemaphoreType.DMA((2, chunks)),
        ],
        compiler_params=pltpu.CompilerParams(
            collective_id=collective, has_side_effects=True, vmem_limit_bytes=52 << 20
        ),
        cost_estimate=pl.CostEstimate(
            flops=tokens * width * 8, bytes_accessed=360_000_000, transcendentals=0
        ),
        name=name,
    )(part, *extras)


def inverse_rms(values):
    return lax.rsqrt(jnp.mean(values * values, axis=-1, keepdims=True) + EPSILON)


def residual_norm(total, rows, own, extra_in, out, extra_out):
    hidden, gain = extra_in
    if total is None:
        return
    residual = hidden[rows].astype(F32) + total
    extra_out[0][own] = residual
    out[rows] = (residual * inverse_rms(residual) * gain[...]).astype(BF16)


def residual_out(total, rows, own, extra_in, out, extra_out):
    if total is None:
        return
    out[rows] = (extra_in[0][own] + total).astype(BF16)


def norm_two_back(total, rows, own, extra_in, out, extra_out):
    residual_ref, cotangent_ref, gain = extra_in
    grad_ref, gain_grad = extra_out
    if total is None:
        gain_grad[...] = jnp.zeros_like(gain_grad)
        return
    residual = residual_ref[own]
    inverse = inverse_rms(residual)
    unit = residual * inverse
    gain_grad[...] += jnp.sum(total * unit, axis=0, keepdims=True)
    lifted = total * gain[...]
    mean = jnp.mean(lifted * unit, axis=-1, keepdims=True)
    grad = cotangent_ref[rows].astype(F32) + inverse * (lifted - unit * mean)
    grad_ref[own] = grad
    out[rows] = grad.astype(BF16)


def norm_one_back(total, rows, own, extra_in, out, extra_out):
    hidden, residual_grad, gain = extra_in
    gain_grad = extra_out[0]
    if total is None:
        gain_grad[...] = jnp.zeros_like(gain_grad)
        return
    values = hidden[rows].astype(F32)
    inverse = inverse_rms(values)
    unit = values * inverse
    gain_grad[...] += jnp.sum(total * unit, axis=0, keepdims=True)
    lifted = total * gain[...]
    mean = jnp.mean(lifted * unit, axis=-1, keepdims=True)
    grad = residual_grad[own] + inverse * (lifted - unit * mean)
    out[rows] = grad.astype(BF16)


def rms_parts(values):
    inverse = lax.rsqrt(jnp.mean(values * values, axis=-1, keepdims=True) + EPSILON)
    return (values * inverse, inverse)


def local(
    mesh_axes,
    hidden,
    segment_ids,
    norm1_gain,
    w_query,
    w_forget,
    w_input,
    w_gate_out,
    forget_floor,
    head_gain,
    w_out,
    norm2_gain,
    w_ffn_gate,
    w_ffn_up,
    w_ffn_down,
    out_grad,
):
    sequences, span_len, model_width = hidden.shape
    tokens = sequences * span_len
    head_count, key_dim = forget_floor.shape
    width = head_count * key_dim
    key_scale = key_dim ** (-0.5)
    both = ("shard", "context")
    mixer_full = lax.all_gather(
        jnp.concatenate([w_query, w_forget, w_input, w_gate_out], axis=1), both, axis=0, tiled=True
    )
    out_full = lax.all_gather(w_out, both, axis=1, tiled=True)
    gate_full = lax.all_gather(w_ffn_gate, both, axis=0, tiled=True)
    up_full = lax.all_gather(w_ffn_up, both, axis=0, tiled=True)
    down_full = lax.all_gather(w_ffn_down, both, axis=1, tiled=True)
    gain_one, gain_two = norm1_gain.reshape(1, -1), norm2_gain.reshape(1, -1)
    half_wide = jax.ShapeDtypeStruct((tokens // 2, model_width), F32)
    one_row = jax.ShapeDtypeStruct((1, model_width), F32)
    hidden_rows = hidden.reshape(tokens, model_width)
    unit_rows, _ = rms_parts(hidden_rows.astype(F32))
    normed_one = (unit_rows * norm1_gain).astype(BF16)
    pre = jnp.dot(normed_one, mixer_full, preferred_element_type=F32)
    open_part = (1.0 - forget_floor).reshape(1, width)
    counts, keep, flags, last_count = row_flags(segment_ids)
    mixed_local, lead, starts, runs, state_end, run_end = mixer_forward(
        pre, open_part, counts, keep, flags, head_count, key_scale
    )
    decay = (jnp.exp(run_end) * (last_count == 0).astype(F32)).reshape(head_count, 1, key_dim)
    ids = segment_ids.reshape(-1).astype(F32)
    carry, link_in = state_before(state_end, decay, ids[0], ids[-1], "context")
    gain_row = head_gain.reshape(1, -1)
    mixed, gated_low = gate_forward(
        mixed_local, lead, carry.astype(BF16), pre, gain_row, keep, key_scale
    )
    mix_part = jnp.dot(gated_low, out_full, preferred_element_type=F32).astype(BF16)
    normed_two, residual = line_exchange(
        residual_norm, mesh_axes, 0, mix_part, (hidden_rows, gain_two), [half_wide], "mix_line"
    )
    gate_ffn = jnp.dot(normed_two, gate_full, preferred_element_type=F32)
    up_ffn = jnp.dot(normed_two, up_full, preferred_element_type=F32)
    sigma_gate = jax.nn.sigmoid(gate_ffn)
    active = gate_ffn * sigma_gate
    hidden_low = (active * up_ffn).astype(BF16)
    feed_part = jnp.dot(hidden_low, down_full, preferred_element_type=F32).astype(BF16)
    (output_rows,) = line_exchange(
        residual_out, mesh_axes, 1, feed_part, (residual,), [], "feed_line"
    )
    grad_rows = out_grad.reshape(tokens, model_width)
    grad_down = jnp.einsum("tf,td->fd", hidden_low, grad_rows, preferred_element_type=F32)
    grad_hidden = jnp.einsum("td,fd->tf", grad_rows, down_full, preferred_element_type=F32)
    grad_gate_low = (
        grad_hidden * up_ffn * sigma_gate * (1.0 + gate_ffn * (1.0 - sigma_gate))
    ).astype(BF16)
    grad_up_low = (grad_hidden * active).astype(BF16)
    grad_gate = jnp.einsum("td,tf->df", normed_two, grad_gate_low, preferred_element_type=F32)
    grad_up = jnp.einsum("td,tf->df", normed_two, grad_up_low, preferred_element_type=F32)
    back_two = jnp.einsum("tf,df->td", grad_gate_low, gate_full, preferred_element_type=F32)
    back_two = back_two + jnp.einsum(
        "tf,df->td", grad_up_low, up_full, preferred_element_type=F32
    )
    grad_mix_low, grad_residual, grad_norm_two = line_exchange(
        norm_two_back,
        mesh_axes,
        2,
        back_two.astype(BF16),
        (residual, grad_rows, gain_two),
        [half_wide, one_row],
        "norm_two_line",
    )
    grad_out = jnp.einsum("tv,td->vd", gated_low, grad_mix_low, preferred_element_type=F32)
    grad_gated = jnp.einsum("td,vd->tv", grad_mix_low, out_full, preferred_element_type=F32)
    grad_mixed, grad_gate_pre, grad_head_part, back = gate_backward(
        grad_gated, mixed, lead, pre, gain_row, keep, head_count, key_scale
    )
    after = grad_after(back, decay, link_in, "context")
    grad_pre, grad_floor_part = mixer_backward(
        pre,
        grad_mixed,
        grad_gate_pre,
        starts,
        runs,
        carry,
        after,
        open_part,
        counts,
        keep,
        flags,
    )
    grad_mixer = jnp.einsum("td,tk->dk", normed_one, grad_pre, preferred_element_type=F32)
    back_one = jnp.einsum("tk,dk->td", grad_pre, mixer_full, preferred_element_type=F32)
    input_rows, grad_norm_one = line_exchange(
        norm_one_back,
        mesh_axes,
        3,
        back_one.astype(BF16),
        (hidden_rows, grad_residual, gain_one),
        [one_row],
        "norm_one_line",
    )
    grad_norm_one, grad_norm_two, head_total = lax.psum(
        (grad_norm_one.reshape(-1), grad_norm_two.reshape(-1), grad_head_part.reshape(-1)),
        "tensor",
    )

    def share(values, dim):
        return lax.psum_scatter(
            values.astype(BF16), both, scatter_dimension=dim, tiled=True
        ).astype(F32)

    share_mixer = share(grad_mixer, 0)
    return (
        output_rows.reshape(hidden.shape),
        input_rows.reshape(hidden.shape),
        share(grad_norm_one, 0),
        share_mixer[:, :width],
        share_mixer[:, width : 2 * width],
        share_mixer[:, 2 * width : 3 * width],
        share_mixer[:, 3 * width :],
        share(grad_floor_part.reshape(head_count, key_dim), 1),
        share(head_total, 0),
        share(grad_out, 1),
        share(grad_norm_two, 0),
        share(grad_gate, 0),
        share(grad_up, 0),
        share(grad_down, 1),
    )


def solution(mesh):
    in_specs = (
        P("shard", "context", None),
        P("shard", "context"),
        P(),
        P(("shard", "context"), "tensor"),
        P(("shard", "context"), "tensor"),
        P(("shard", "context"), "tensor"),
        P(("shard", "context"), "tensor"),
        P("tensor", None),
        P(),
        P("tensor", ("shard", "context")),
        P(),
        P(("shard", "context"), "tensor"),
        P(("shard", "context"), "tensor"),
        P("tensor", ("shard", "context")),
        P("shard", "context", None),
    )
    out_specs = (
        P("shard", "context", None),
        P("shard", "context", None),
        P(("shard", "context")),
        P(("shard", "context"), "tensor"),
        P(("shard", "context"), "tensor"),
        P(("shard", "context"), "tensor"),
        P(("shard", "context"), "tensor"),
        P("tensor", ("shard", "context")),
        P(("shard", "context")),
        P("tensor", ("shard", "context")),
        P(("shard", "context")),
        P(("shard", "context"), "tensor"),
        P(("shard", "context"), "tensor"),
        P("tensor", ("shard", "context")),
    )
    return jax.shard_map(
        partial(local, mesh.axis_names), mesh=mesh, in_specs=in_specs, out_specs=out_specs, check_vma=False)
```

```python
from functools import partial

import jax
import jax.numpy as jnp
from jax import lax
from jax.experimental import pallas as pl
from jax.experimental.pallas import tpu as pltpu
from jax.sharding import PartitionSpec as P

EPSILON = 1e-05


BLOCK = 128
F32 = jnp.float32
BF16 = jnp.bfloat16


def mm(a, b, dims):
    return lax.dot_general(a, b, (dims, ((), ())), preferred_element_type=F32)


def mm_nn(a, b):
    return mm(a, b, ((1,), (0,)))


def mm_nt(a, b):
    return mm(a, b, ((1,), (1,)))


def mm_tn(a, b):
    return mm(a, b, ((0,), (0,)))


def split_sum(tri, values):
    high = values.astype(BF16)
    low = (values - high.astype(F32)).astype(BF16)
    return mm_nn(tri, high) + mm_nn(tri, low)


def block_masks(counts, flags_row):
    rows = counts.shape[0]
    row_ids = lax.broadcasted_iota(jnp.int32, (rows, rows), 0)
    col_ids = lax.broadcasted_iota(jnp.int32, (rows, rows), 1)
    linked = jnp.logical_and(counts == flags_row[0:1], row_ids >= col_ids)
    fresh = (counts == flags_row[1:2, 0:1]).astype(F32)
    tail = (counts == flags_row[2:3, 0:1]).astype(F32)
    closing = (flags_row[1:2, 0:1] == flags_row[2:3, 0:1]).astype(F32)
    return row_ids, col_ids, linked, fresh, tail, closing


def mixer_forward_kernel(
    head_count,
    key_scale,
    pre_ref,
    open_ref,
    count_ref,
    keep_ref,
    flags_ref,
    mixed_ref,
    lead_ref,
    start_ref,
    run_ref,
    end_ref,
    total_ref,
    state_scr,
    run_scr,
):
    step = pl.program_id(0)
    width = open_ref.shape[1]
    lanes = width // head_count

    @pl.when(step == 0)
    def _():
        state_scr[...] = jnp.zeros_like(state_scr)
        run_scr[...] = jnp.zeros_like(run_scr)

    counts, keep = count_ref[...], keep_ref[...]
    row_ids, col_ids, linked, fresh, tail, closing = block_masks(counts, flags_ref[0])
    tri = (row_ids >= col_ids).astype(BF16)
    query_pre = pre_ref[:, :width]
    values = pre_ref[:, 2 * width : 3 * width].astype(BF16)
    keys = open_ref[...] * jax.nn.sigmoid(-pre_ref[:, width : 2 * width])
    cum = split_sum(tri, jnp.log1p(-keys))
    rows = cum.shape[0]
    ending = cum[rows - 1 : rows, :]
    lifted = query_pre * jax.nn.sigmoid(query_pre) * jnp.exp(cum)
    lowered = (keys * jnp.exp(-cum) * keep).astype(BF16)
    moved = (keys * jnp.exp(ending - cum) * (keep * tail)).astype(BF16)
    run = run_scr[...]
    lead_ref[...] = (lifted * jnp.exp(run) * (counts == 0).astype(F32)).astype(BF16)
    run_ref[0] = run
    run_scr[...] = run + ending
    total_ref[...] = run + ending
    fresh_lifted = (lifted * fresh).astype(BF16)
    lifted = lifted.astype(BF16)
    end_decay = jnp.exp(ending) * closing
    for head in range(head_count):
        part = slice(head * lanes, (head + 1) * lanes)
        state = state_scr[head]
        start_ref[0, head] = state
        scores = jnp.where(linked, mm_nt(lifted[:, part], lowered[:, part]), 0.0)
        results = mm_nn(scores.astype(BF16), values[:, part])
        results = results + mm_nt(fresh_lifted[:, part], state.astype(BF16))
        mixed_ref[:, part] = results * (key_scale * keep)
        state = state * end_decay[:, part] + mm_tn(values[:, part], moved[:, part])
        state_scr[head] = state
        end_ref[head] = state


def mixer_forward(pre, open_part, counts, keep, flags, head_count, key_scale):
    tokens, all_width = pre.shape
    width = open_part.shape[1]
    lanes = width // head_count
    blocks = tokens // BLOCK
    return pl.pallas_call(
        partial(mixer_forward_kernel, head_count, key_scale),
        grid=(blocks,),
        in_specs=[
            pl.BlockSpec((BLOCK, all_width), lambda i: (i, 0)),
            pl.BlockSpec((1, width), lambda i: (0, 0)),
            pl.BlockSpec((BLOCK, 1), lambda i: (i, 0)),
            pl.BlockSpec((BLOCK, 1), lambda i: (i, 0)),
            pl.BlockSpec((1, 8, BLOCK), lambda i: (i, 0, 0)),
        ],
        out_specs=[
            pl.BlockSpec((BLOCK, width), lambda i: (i, 0)),
            pl.BlockSpec((BLOCK, width), lambda i: (i, 0)),
            pl.BlockSpec((1, head_count, lanes, lanes), lambda i: (i, 0, 0, 0)),
            pl.BlockSpec((1, 1, width), lambda i: (i, 0, 0)),
            pl.BlockSpec((head_count, lanes, lanes), lambda i: (0, 0, 0)),
            pl.BlockSpec((1, width), lambda i: (0, 0)),
        ],
        out_shape=[
            jax.ShapeDtypeStruct((tokens, width), F32),
            jax.ShapeDtypeStruct((tokens, width), BF16),
            jax.ShapeDtypeStruct((blocks, head_count, lanes, lanes), F32),
            jax.ShapeDtypeStruct((blocks, 1, width), F32),
            jax.ShapeDtypeStruct((head_count, lanes, lanes), F32),
            jax.ShapeDtypeStruct((1, width), F32),
        ],
        scratch_shapes=[
            pltpu.VMEM((head_count, lanes, lanes), F32),
            pltpu.VMEM((1, width), F32),
        ],
        compiler_params=pltpu.CompilerParams(
            dimension_semantics=("arbitrary",), vmem_limit_bytes=40 << 20
        ),
        cost_estimate=pl.CostEstimate(
            flops=tokens * width * BLOCK * 12,
            bytes_accessed=tokens * width * 30,
            transcendentals=tokens * width * 7,
        ),
        name="mixer_forward",
    )(pre, open_part, counts, keep, flags)


def gate_forward_kernel(
    head_count,
    key_scale,
    local_ref,
    lead_ref,
    carry_ref,
    gate_ref,
    gain_ref,
    keep_ref,
    mixed_ref,
    gated_ref,
):
    lanes = gain_ref.shape[1]
    for head in range(head_count):
        part = slice(head * lanes, (head + 1) * lanes)
        carried = mm_nt(lead_ref[:, part], carry_ref[head])
        mixed = local_ref[:, part] + carried * (key_scale * keep_ref[...])
        mixed_ref[:, part] = mixed
        inverse = lax.rsqrt(jnp.mean(mixed * mixed, axis=-1, keepdims=True) + EPSILON)
        gate = gate_ref[:, part]
        gated = mixed * inverse * gain_ref[...] * (gate * jax.nn.sigmoid(gate))
        gated_ref[:, part] = gated.astype(BF16)


def gate_forward(local, lead, carry, pre, gain, keep, key_scale):
    tokens, width = local.shape
    head_count, lanes = carry.shape[0], carry.shape[2]
    rows = 2 * BLOCK
    return pl.pallas_call(
        partial(gate_forward_kernel, head_count, key_scale),
        grid=(tokens // rows,),
        in_specs=[
            pl.BlockSpec((rows, width), lambda i: (i, 0)),
            pl.BlockSpec((rows, width), lambda i: (i, 0)),
            pl.BlockSpec((head_count, lanes, lanes), lambda i: (0, 0, 0)),
            pl.BlockSpec((rows, width), lambda i: (i, 3)),
            pl.BlockSpec((1, lanes), lambda i: (0, 0)),
            pl.BlockSpec((rows, 1), lambda i: (i, 0)),
        ],
        out_specs=[
            pl.BlockSpec((rows, width), lambda i: (i, 0)),
            pl.BlockSpec((rows, width), lambda i: (i, 0)),
        ],
        out_shape=[
            jax.ShapeDtypeStruct((tokens, width), F32),
            jax.ShapeDtypeStruct((tokens, width), BF16),
        ],
        compiler_params=pltpu.CompilerParams(
            dimension_semantics=("arbitrary",), vmem_limit_bytes=40 << 20
        ),
        cost_estimate=pl.CostEstimate(
            flops=tokens * width * 300,
            bytes_accessed=tokens * width * 16,
            transcendentals=tokens * width,
        ),
        name="gate_forward",
    )(local, lead, carry, pre, gain, keep)


def gate_backward_kernel(
    head_count,
    key_scale,
    grad_ref,
    mixed_ref,
    lead_ref,
    gate_ref,
    gain_ref,
    keep_ref,
    grad_mixed_ref,
    grad_gate_ref,
    grad_gain_ref,
    back_ref,
):
    lanes = gain_ref.shape[1]

    @pl.when(pl.program_id(0) == 0)
    def _():
        grad_gain_ref[...] = jnp.zeros_like(grad_gain_ref)
        back_ref[...] = jnp.zeros_like(back_ref)

    gain = gain_ref[...]
    total = jnp.zeros_like(gain)
    for head in range(head_count):
        part = slice(head * lanes, (head + 1) * lanes)
        mixed, gate, grad = mixed_ref[:, part], gate_ref[:, part], grad_ref[:, part]
        inverse = lax.rsqrt(jnp.mean(mixed * mixed, axis=-1, keepdims=True) + EPSILON)
        unit = mixed * inverse
        sigma = jax.nn.sigmoid(gate)
        scaled = grad * unit
        total = total + jnp.sum(scaled * (gate * sigma), axis=0, keepdims=True)
        grad_gate = scaled * gain * sigma * (1.0 + gate * (1.0 - sigma))
        grad_gate_ref[:, part] = grad_gate.astype(BF16)
        lifted = grad * gain * (gate * sigma)
        mean = jnp.mean(lifted * unit, axis=-1, keepdims=True)
        grad_mixed = inverse * (lifted - unit * mean) * (key_scale * keep_ref[...])
        grad_mixed = grad_mixed.astype(BF16)
        grad_mixed_ref[:, part] = grad_mixed
        back_ref[head] += mm_tn(grad_mixed, lead_ref[:, part])
    grad_gain_ref[...] += total


def gate_backward(grad, mixed, lead, pre, gain, keep, head_count, key_scale):
    tokens, width = mixed.shape
    lanes = gain.shape[1]
    rows = 2 * BLOCK
    return pl.pallas_call(
        partial(gate_backward_kernel, head_count, key_scale),
        grid=(tokens // rows,),
        in_specs=[
            pl.BlockSpec((rows, width), lambda i: (i, 0)),
            pl.BlockSpec((rows, width), lambda i: (i, 0)),
            pl.BlockSpec((rows, width), lambda i: (i, 0)),
            pl.BlockSpec((rows, width), lambda i: (i, 3)),
            pl.BlockSpec((1, lanes), lambda i: (0, 0)),
            pl.BlockSpec((rows, 1), lambda i: (i, 0)),
        ],
        out_specs=[
            pl.BlockSpec((rows, width), lambda i: (i, 0)),
            pl.BlockSpec((rows, width), lambda i: (i, 0)),
            pl.BlockSpec((1, lanes), lambda i: (0, 0)),
            pl.BlockSpec((head_count, lanes, lanes), lambda i: (0, 0, 0)),
        ],
        out_shape=[
            jax.ShapeDtypeStruct((tokens, width), BF16),
            jax.ShapeDtypeStruct((tokens, width), BF16),
            jax.ShapeDtypeStruct((1, lanes), F32),
            jax.ShapeDtypeStruct((head_count, lanes, lanes), F32),
        ],
        compiler_params=pltpu.CompilerParams(
            dimension_semantics=("arbitrary",), vmem_limit_bytes=40 << 20
        ),
        cost_estimate=pl.CostEstimate(
            flops=tokens * width * 300,
            bytes_accessed=tokens * width * 18,
            transcendentals=tokens * width,
        ),
        name="gate_backward",
    )(grad, mixed, lead, pre, gain, keep)


def mixer_backward_kernel(
    head_count,
    pre_ref,
    grad_mixed_ref,
    grad_gate_ref,
    start_ref,
    run_ref,
    carry_ref,
    after_ref,
    open_ref,
    count_ref,
    keep_ref,
    flags_ref,
    grads_ref,
    floor_ref,
    grad_scr,
    lifted_scr,
    lowered_scr,
    moved_scr,
    value_scr,
):
    width = open_ref.shape[1]
    lanes = width // head_count

    @pl.when(pl.program_id(0) == 0)
    def _():
        grad_scr[...] = after_ref[...]
        floor_ref[...] = jnp.zeros_like(floor_ref)

    counts, keep = count_ref[...], keep_ref[...]
    flags = flags_ref[0]
    row_ids, col_ids, linked, fresh, tail, closing = block_masks(counts, flags)
    tri = (row_ids >= col_ids).astype(BF16)
    tri_back = (row_ids <= col_ids).astype(BF16)
    query_pre = pre_ref[:, :width]
    values = pre_ref[:, 2 * width : 3 * width].astype(BF16)
    opened = open_ref[...]
    closed = jax.nn.sigmoid(-pre_ref[:, width : 2 * width])
    keys = opened * closed
    cum = split_sum(tri, jnp.log1p(-keys))
    rows = cum.shape[0]
    ending = cum[rows - 1 : rows, :]
    rise, fall = jnp.exp(cum), jnp.exp(-cum) * keep
    shift = jnp.exp(ending - cum) * (keep * tail)
    sigma_query = jax.nn.sigmoid(query_pre)
    lifted = (query_pre * sigma_query * rise).astype(BF16)
    lowered = (keys * fall).astype(BF16)
    moved = (keys * shift).astype(BF16)
    fresh_lifted = (lifted.astype(F32) * fresh).astype(BF16)
    end_decay = jnp.exp(ending) * closing
    lead_in = jnp.exp(run_ref[0]) * (flags[1:2, 0:1] == 0).astype(F32)
    for head in range(head_count):
        part = slice(head * lanes, (head + 1) * lanes)
        grad_out, value = grad_mixed_ref[:, part], values[:, part]
        lift, lower, move = lifted[:, part], lowered[:, part], moved[:, part]
        scores = jnp.where(linked, mm_nt(lift, lower), 0.0).astype(BF16)
        pulls = jnp.where(linked, mm_nt(grad_out, value), 0.0).astype(BF16)
        state = start_ref[0, head] + lead_in[:, part] * carry_ref[head]
        grad_state = grad_scr[head]
        grad_low = grad_state.astype(BF16)
        lifted_scr[:, part] = mm_nn(pulls, lower) + fresh * mm_nn(grad_out, state.astype(BF16))
        lowered_scr[:, part] = mm_tn(pulls, lift)
        grad_moved = mm_nn(value, grad_low)
        moved_scr[:, part] = grad_moved
        grads_ref[:, 2 * width + head * lanes : 2 * width + (head + 1) * lanes] = (
            mm_tn(scores, grad_out) + mm_nt(move, grad_low)
        ).astype(BF16)
        value_scr[:, part] = jnp.sum(
            grad_moved * move.astype(F32), axis=0, keepdims=True
        ) + end_decay[:, part] * jnp.sum(state * grad_state, axis=0, keepdims=True)
        grad_scr[head] = grad_state * end_decay[:, part] + mm_tn(grad_out, fresh_lifted[:, part])
    grad_lifted, grad_lowered, grad_moved = lifted_scr[...], lowered_scr[...], moved_scr[...]
    grad_cum = (
        grad_lifted * lifted.astype(F32)
        - grad_lowered * lowered.astype(F32)
        - grad_moved * moved.astype(F32)
    )
    grad_decay = split_sum(tri_back, grad_cum) + value_scr[...]
    key_total = grad_lowered * fall + grad_moved * shift - grad_decay / (1.0 - keys)
    floor_ref[...] -= jnp.sum(key_total * closed, axis=0, keepdims=True)
    grads_ref[:, :width] = (
        grad_lifted * rise * sigma_query * (1.0 + query_pre * (1.0 - sigma_query))
    ).astype(BF16)
    grads_ref[:, width : 2 * width] = (-key_total * opened * closed * (1.0 - closed)).astype(BF16)
    grads_ref[:, 3 * width :] = grad_gate_ref[...]


def mixer_backward(
    pre, grad_mixed, grad_gate, starts, runs, carry, after, open_part, counts, keep, flags
):
    tokens, all_width = pre.shape
    width = open_part.shape[1]
    head_count, lanes = carry.shape[0], carry.shape[2]
    blocks = tokens // BLOCK
    last = blocks - 1
    return pl.pallas_call(
        partial(mixer_backward_kernel, head_count),
        grid=(blocks,),
        in_specs=[
            pl.BlockSpec((BLOCK, all_width), lambda i: (last - i, 0)),
            pl.BlockSpec((BLOCK, width), lambda i: (last - i, 0)),
            pl.BlockSpec((BLOCK, width), lambda i: (last - i, 0)),
            pl.BlockSpec((1, head_count, lanes, lanes), lambda i: (last - i, 0, 0, 0)),
            pl.BlockSpec((1, 1, width), lambda i: (last - i, 0, 0)),
            pl.BlockSpec((head_count, lanes, lanes), lambda i: (0, 0, 0)),
            pl.BlockSpec((head_count, lanes, lanes), lambda i: (0, 0, 0)),
            pl.BlockSpec((1, width), lambda i: (0, 0)),
            pl.BlockSpec((BLOCK, 1), lambda i: (last - i, 0)),
            pl.BlockSpec((BLOCK, 1), lambda i: (last - i, 0)),
            pl.BlockSpec((1, 8, BLOCK), lambda i: (last - i, 0, 0)),
        ],
        out_specs=[
            pl.BlockSpec((BLOCK, all_width), lambda i: (last - i, 0)),
            pl.BlockSpec((1, width), lambda i: (0, 0)),
        ],
        out_shape=[
            jax.ShapeDtypeStruct((tokens, all_width), BF16),
            jax.ShapeDtypeStruct((1, width), F32),
        ],
        scratch_shapes=[
            pltpu.VMEM((head_count, lanes, lanes), F32),
            pltpu.VMEM((BLOCK, width), F32),
            pltpu.VMEM((BLOCK, width), F32),
            pltpu.VMEM((BLOCK, width), F32),
            pltpu.VMEM((1, width), F32),
        ],
        compiler_params=pltpu.CompilerParams(
            dimension_semantics=("arbitrary",), vmem_limit_bytes=40 << 20
        ),
        cost_estimate=pl.CostEstimate(
            flops=tokens * width * BLOCK * 30,
            bytes_accessed=tokens * width * 36,
            transcendentals=tokens * width * 9,
        ),
        name="mixer_backward",
    )(pre, grad_mixed, grad_gate, starts, runs, carry, after, open_part, counts, keep, flags)


def row_flags(segment_ids):
    ids = segment_ids.reshape(-1)
    tokens = ids.shape[0]
    starts = jnp.concatenate([jnp.zeros((1,), F32), (ids[1:] != ids[:-1]).astype(F32)])
    positions = jnp.arange(tokens)
    counts = jnp.sum(
        jnp.where(positions[None, :] <= positions[:, None], starts[None, :], 0.0), axis=1
    )
    keep = (ids > 0).astype(F32)
    blocks = tokens // BLOCK
    by_block = counts.reshape(blocks, BLOCK)
    lasts = by_block[:, -1]
    before = jnp.concatenate([jnp.zeros((1,), F32), lasts[:-1]])
    wide = (blocks, BLOCK)
    flags = jnp.stack(
        [by_block, jnp.broadcast_to(before[:, None], wide), jnp.broadcast_to(lasts[:, None], wide)]
        + [jnp.zeros(wide, F32)] * 5,
        axis=1,
    )
    return counts[:, None], keep[:, None], flags, lasts[-1]


def from_earlier(values, axis, shift):
    count = lax.axis_size(axis)
    return lax.ppermute(values, axis, [(i, i + shift) for i in range(count - shift)])


def from_later(values, axis, shift):
    count = lax.axis_size(axis)
    return lax.ppermute(values, axis, [(i + shift, i) for i in range(count - shift)])


def state_before(state, decay, first_id, last_id, axis):
    head_count, lanes, _ = state.shape
    ids = jnp.stack([first_id, last_id, jnp.float32(1.0)] + [jnp.float32(0.0)] * 5)
    message = jnp.concatenate(
        [
            state.reshape(head_count * lanes, lanes),
            decay.reshape(head_count, lanes),
            jnp.broadcast_to(ids[:, None], (8, lanes)),
        ]
    )
    rows = head_count * lanes
    total = jnp.zeros_like(state)
    factor = jnp.ones((head_count, 1, lanes), F32)
    follower = first_id
    link_in = jnp.float32(0.0)
    for shift in range(1, lax.axis_size(axis)):
        got = from_earlier(message, axis, shift)
        got_ids = got[rows + head_count :, 0]
        linked = (got_ids[1] == follower).astype(F32) * got_ids[2]
        if shift == 1:
            link_in = linked
        factor = factor * linked
        total = total + factor * got[:rows].reshape(state.shape)
        factor = factor * got[rows : rows + head_count].reshape(head_count, 1, lanes)
        follower = got_ids[0]
    return total, link_in


def grad_after(back, decay, link_in, axis):
    head_count, lanes, _ = back.shape
    rows = head_count * lanes
    message = (
        jnp.concatenate([back.reshape(rows, lanes), decay.reshape(head_count, lanes)]) * link_in
    )
    message = jnp.pad(message, ((0, 8 - head_count % 8 if head_count % 8 else 0), (0, 0)))
    total = jnp.zeros_like(back)
    factor = jnp.ones((head_count, 1, lanes), F32)
    for shift in range(1, lax.axis_size(axis)):
        got = from_later(message, axis, shift)
        total = total + factor * got[:rows].reshape(back.shape)
        factor = factor * got[rows : rows + head_count].reshape(head_count, 1, lanes)
    return total


CHUNK = 32
LAG = 2
MESH_ID = pl.DeviceIdType.MESH


class Line:
    def __init__(self, mesh_axes, part, arrived, out, sems, transform):
        self.mesh_axes = mesh_axes
        self.part, self.arrived, self.out = part, arrived, out
        self.sum_send, self.sum_recv, self.back_send, self.back_recv = sems
        self.transform = transform
        self.half = part.shape[0] // 2
        self.chunks = self.half // CHUNK
        self.size = lax.axis_size("tensor")
        self.place = lax.axis_index("tensor")
        self.lines = ((self.size - 1 - self.place, -1), (self.place, 1))
        self.steps = self.chunks + 2 * LAG * (self.size - 1)

    def device(self, position):
        return tuple(
            jnp.clip(position, 0, self.size - 1) if axis == "tensor" else lax.axis_index(axis)
            for axis in self.mesh_axes
        )

    def greet(self, barrier):
        for step in (-1, 1):
            inside = jnp.logical_and(self.place + step >= 0, self.place + step < self.size)

            @pl.when(inside)
            def _(step=step):
                pl.semaphore_signal(
                    barrier, inc=1, device_id=self.device(self.place + step), device_id_type=MESH_ID
                )

        at_end = jnp.logical_or(self.place == 0, self.place == self.size - 1)
        return jnp.where(at_end, 1, 2)

    def rows_of(self, side, index):
        return pl.ds(pl.multiple_of(side * self.half + index * CHUNK, CHUNK), CHUNK)

    def sum_copy(self, side, index, source):
        rows = self.rows_of(side, index)
        return pltpu.make_async_remote_copy(
            source.at[rows],
            self.arrived.at[rows],
            self.sum_send.at[side, index],
            self.sum_recv.at[side, index],
            device_id=self.device(self.place + self.lines[side][1]),
            device_id_type=MESH_ID,
        )

    def back_copy(self, side, index):
        rows = self.rows_of(side, index)
        return pltpu.make_async_remote_copy(
            self.out.at[rows],
            self.out.at[rows],
            self.back_send.at[side, index],
            self.back_recv.at[side, index],
            device_id=self.device(self.place - self.lines[side][1]),
            device_id_type=MESH_ID,
        )

    def step(self, time):
        for side in (0, 1):
            hops = self.lines[side][0]
            index = time - LAG * hops
            valid = jnp.logical_and(index >= 0, index < self.chunks)
            at_source, at_owner = hops == 0, hops == self.size - 1
            index = jnp.clip(index, 0, self.chunks - 1)
            rows = self.rows_of(side, index)

            @pl.when(jnp.logical_and(valid, at_source))
            def _(side=side, index=index):
                self.sum_copy(side, index, self.part).start()

            @pl.when(jnp.logical_and(valid, jnp.logical_not(at_source)))
            def _(side=side, index=index):
                self.sum_copy(side, index, self.arrived).wait_recv()

            between = jnp.logical_and(jnp.logical_not(at_source), jnp.logical_not(at_owner))

            @pl.when(jnp.logical_and(valid, between))
            def _(side=side, index=index, rows=rows):
                total = self.part[rows].astype(F32) + self.arrived[rows].astype(F32)
                self.arrived[rows] = total.astype(BF16)
                self.sum_copy(side, index, self.arrived).start()

            @pl.when(jnp.logical_and(valid, at_owner))
            def _(side=side, index=index, rows=rows):
                total = self.part[rows].astype(F32) + self.arrived[rows].astype(F32)
                own = pl.ds(pl.multiple_of(index * CHUNK, CHUNK), CHUNK)
                self.transform(total, rows, own)
                self.back_copy(side, index).start()

            away = self.size - 1 - hops
            index = time - LAG * (self.size - 1 + away)
            valid = jnp.logical_and(jnp.logical_and(index >= 0, index < self.chunks), away > 0)
            index = jnp.clip(index, 0, self.chunks - 1)

            @pl.when(valid)
            def _(side=side, index=index):
                self.back_copy(side, index).wait_recv()

            @pl.when(jnp.logical_and(valid, away < self.size - 1))
            def _(side=side, index=index):
                self.back_copy(side, index).start()

    def run(self, first, last):
        def body(time, _):
            self.step(time)
            return 0

        lax.fori_loop(first, last, body, 0)

    def finish(self):
        def body(index, _):
            for side in (0, 1):
                hops = self.lines[side][0]

                @pl.when(hops < self.size - 1)
                def _(side=side):
                    self.sum_copy(side, index, self.arrived).wait_send()

                @pl.when(hops > 0)
                def _(side=side):
                    self.back_copy(side, index).wait_send()

            return 0

        lax.fori_loop(0, self.chunks, body, 0)


def line_sems(tokens):
    return [pltpu.SemaphoreType.DMA((2, tokens // 2 // CHUNK))] * 4


def line_exchange_kernel(transform, mesh_axes, n_in, n_out, *refs):
    part, extra_in = refs[0], refs[1 : 1 + n_in]
    out, extra_out = refs[1 + n_in], refs[2 + n_in : 2 + n_in + n_out]
    arrived, *sems = refs[2 + n_in + n_out :]
    if transform is norm_one_back:
        extra_out[0][...] = jnp.zeros_like(extra_out[0])

    def turn(total, rows, own):
        transform(total, rows, own, extra_in, out, extra_out)

    line = Line(mesh_axes, part, arrived, out, sems, turn)
    barrier = pltpu.get_barrier_semaphore()
    pl.semaphore_wait(barrier, line.greet(barrier))
    line.run(0, line.steps)
    line.finish()


def line_exchange(transform, mesh_axes, collective, part, extras, extra_shapes, name):
    tokens, width = part.shape
    whole = pl.BlockSpec(memory_space=pltpu.VMEM)
    return pl.pallas_call(
        partial(line_exchange_kernel, transform, mesh_axes, len(extras), len(extra_shapes)),
        in_specs=[whole] * (1 + len(extras)),
        out_specs=[whole] * (1 + len(extra_shapes)),
        out_shape=[jax.ShapeDtypeStruct((tokens, width), BF16)] + list(extra_shapes),
        scratch_shapes=[pltpu.VMEM((tokens, width), BF16)] + line_sems(tokens),
        compiler_params=pltpu.CompilerParams(
            collective_id=collective, has_side_effects=True, vmem_limit_bytes=52 << 20
        ),
        cost_estimate=pl.CostEstimate(
            flops=tokens * width * 8, bytes_accessed=360_000_000, transcendentals=0
        ),
        name=name,
    )(part, *extras)


def inverse_rms(values):
    return lax.rsqrt(jnp.mean(values * values, axis=-1, keepdims=True) + EPSILON)


def residual_norm(total, rows, own, extra_in, out, extra_out):
    hidden, gain = extra_in
    residual = hidden[rows].astype(F32) + total
    extra_out[0][own] = residual
    out[rows] = (residual * inverse_rms(residual) * gain[...]).astype(BF16)


def residual_out(total, rows, own, extra_in, out, extra_out):
    out[rows] = (extra_in[0][own] + total).astype(BF16)


def norm_one_back(total, rows, own, extra_in, out, extra_out):
    hidden, residual_grad, gain = extra_in
    gain_grad = extra_out[0]
    values = hidden[rows].astype(F32)
    inverse = inverse_rms(values)
    unit = values * inverse
    gain_grad[...] += jnp.sum(total * unit, axis=0, keepdims=True)
    lifted = total * gain[...]
    mean = jnp.mean(lifted * unit, axis=-1, keepdims=True)
    grad = residual_grad[own] + inverse * (lifted - unit * mean)
    out[rows] = grad.astype(BF16)


GROUP = 128
TILE = 256


def feed_kernel(
    mesh_axes,
    normed_ref,
    cotangent_ref,
    residual_hbm,
    gain_ref,
    gate_hbm,
    up_hbm,
    down_hbm,
    out_ref,
    gain_grad,
    hidden_hbm,
    grad_gate_hbm,
    grad_up_hbm,
    feed_hbm,
    grad_hbm,
    gate_w,
    up_w,
    down_w,
    part,
    arrived,
    residual,
    stage_hidden,
    stage_gate,
    stage_up,
    stage_feed,
    weight_sem,
    residual_sem,
    stage_sem,
    grad_sem,
    *sems,
):
    tokens, model_width = normed_ref.shape
    half = tokens // 2
    hidden_width = gate_hbm.shape[1]
    padded = gate_w.shape[1]
    groups = half // GROUP
    loads = [
        pltpu.make_async_copy(gate_hbm, gate_w.at[:, pl.ds(0, hidden_width)], weight_sem.at[0]),
        pltpu.make_async_copy(up_hbm, up_w.at[:, pl.ds(0, hidden_width)], weight_sem.at[1]),
        pltpu.make_async_copy(down_hbm, down_w.at[pl.ds(0, hidden_width)], weight_sem.at[2]),
    ]
    for load in loads:
        load.start()
    residual_load = pltpu.make_async_copy(residual_hbm, residual, residual_sem.at[0])
    residual_load.start()
    if padded > hidden_width:
        spare = slice(hidden_width, padded)
        gate_w[:, spare] = jnp.zeros((model_width, padded - hidden_width), BF16)
        up_w[:, spare] = jnp.zeros((model_width, padded - hidden_width), BF16)
        down_w[spare, :] = jnp.zeros((padded - hidden_width, model_width), BF16)
    gain_grad[...] = jnp.zeros_like(gain_grad)

    def turn(total, rows, own):
        values = residual[own]
        inverse = inverse_rms(values)
        unit = values * inverse
        gain_grad[...] += jnp.sum(total * unit, axis=0, keepdims=True)
        lifted = total * gain_ref[...]
        mean = jnp.mean(lifted * unit, axis=-1, keepdims=True)
        grad = cotangent_ref[rows].astype(F32) + inverse * (lifted - unit * mean)
        residual[own] = grad
        out_ref[rows] = grad.astype(BF16)

    line = Line(mesh_axes, part, arrived, out_ref, sems, turn)
    barrier = pltpu.get_barrier_semaphore()
    pl.semaphore_wait(barrier, line.greet(barrier))
    residual_load.wait()
    for load in loads:
        load.wait()

    def both(ref, group):
        first = pl.ds(pl.multiple_of(group * GROUP, GROUP), GROUP)
        second = pl.ds(pl.multiple_of(half + group * GROUP, GROUP), GROUP)
        return first, second

    def stage_copies(group):
        slot = lax.rem(group, 2)
        copies = []
        for side, rows in enumerate(both(None, group)):
            from_rows = pl.ds(side * GROUP, GROUP)
            columns = pl.ds(0, hidden_width)
            for which, (stage, target) in enumerate(
                (
                    (stage_hidden, hidden_hbm),
                    (stage_gate, grad_gate_hbm),
                    (stage_up, grad_up_hbm),
                )
            ):
                copies.append(
                    pltpu.make_async_copy(
                        stage.at[slot, from_rows, columns],
                        target.at[rows],
                        stage_sem.at[slot, which, side],
                    )
                )
            copies.append(
                pltpu.make_async_copy(
                    stage_feed.at[slot, from_rows], feed_hbm.at[rows], stage_sem.at[slot, 3, side]
                )
            )
        return copies

    def hidden_tile(group, tile):
        first, second = both(normed_ref, group)
        slot = lax.rem(group, 2)
        columns = pl.ds(pl.multiple_of(tile * TILE, TILE), TILE)
        rows = jnp.concatenate([normed_ref[first], normed_ref[second]], axis=0)
        gate = mm_nn(rows, gate_w[:, columns])
        up = mm_nn(rows, up_w[:, columns])
        grads = jnp.concatenate([cotangent_ref[first], cotangent_ref[second]], axis=0)
        grad = mm_nt(grads, down_w[columns, :])
        sigma = jax.nn.sigmoid(gate)
        active = gate * sigma
        stage_hidden[slot, :, columns] = (active * up).astype(BF16)
        stage_gate[slot, :, columns] = (grad * up * sigma * (1.0 + gate * (1.0 - sigma))).astype(
            BF16
        )
        stage_up[slot, :, columns] = (grad * active).astype(BF16)

    def model_tile(group, tile):
        first, second = both(part, group)
        slot = lax.rem(group, 2)
        columns = pl.ds(pl.multiple_of(tile * TILE, TILE), TILE)
        back = mm_nt(stage_gate[slot], gate_w[columns, :])
        back = (back + mm_nt(stage_up[slot], up_w[columns, :])).astype(BF16)
        part[first, columns] = back[:GROUP]
        part[second, columns] = back[GROUP:]
        stage_feed[slot, :, columns] = mm_nn(stage_hidden[slot], down_w[:, columns]).astype(BF16)

    hidden_tiles, model_tiles = padded // TILE, model_width // TILE
    ticks = hidden_tiles + model_tiles
    pace = GROUP // CHUNK
    piece = -(-ticks // pace)

    def group_body(group, _):
        @pl.when(group >= 2)
        def _():
            for copy in stage_copies(group - 2):
                copy.wait()

        def piece_body(index, _):
            def tick_body(offset, _):
                tick = index * piece + offset

                @pl.when(tick < hidden_tiles)
                def _():
                    hidden_tile(group, tick)

                @pl.when(jnp.logical_and(tick >= hidden_tiles, tick < ticks))
                def _():
                    model_tile(group, tick - hidden_tiles)

                return 0

            lax.fori_loop(0, piece, tick_body, 0)

            @pl.when(group >= 1)
            def _():
                line.step((group - 1) * pace + index)

            return 0

        lax.fori_loop(0, pace, piece_body, 0)
        for copy in stage_copies(group):
            copy.start()
        return 0

    lax.fori_loop(0, groups, group_body, 0)
    line.run((groups - 1) * pace, line.steps)
    save = pltpu.make_async_copy(residual, grad_hbm, grad_sem.at[0])
    save.start()
    for group in range(max(groups - 2, 0), groups):
        for copy in stage_copies(group):
            copy.wait()
    line.finish()
    save.wait()


def feed_line(mesh_axes, collective, normed, cotangent, residual, gain, gate_w, up_w, down_w):
    tokens, model_width = normed.shape
    hidden_width = gate_w.shape[1]
    padded = -(-hidden_width // TILE) * TILE
    whole = pl.BlockSpec(memory_space=pltpu.VMEM)
    remote = pl.BlockSpec(memory_space=pl.ANY)
    group_rows = 2 * GROUP
    return pl.pallas_call(
        partial(feed_kernel, mesh_axes),
        in_specs=[whole, whole, remote, whole, remote, remote, remote],
        out_specs=[whole, whole] + [remote] * 5,
        out_shape=[
            jax.ShapeDtypeStruct((tokens, model_width), BF16),
            jax.ShapeDtypeStruct((1, model_width), F32),
            jax.ShapeDtypeStruct((tokens, hidden_width), BF16),
            jax.ShapeDtypeStruct((tokens, hidden_width), BF16),
            jax.ShapeDtypeStruct((tokens, hidden_width), BF16),
            jax.ShapeDtypeStruct((tokens, model_width), BF16),
            jax.ShapeDtypeStruct((tokens // 2, model_width), F32),
        ],
        scratch_shapes=[
            pltpu.VMEM((model_width, padded), BF16),
            pltpu.VMEM((model_width, padded), BF16),
            pltpu.VMEM((padded, model_width), BF16),
            pltpu.VMEM((tokens, model_width), BF16),
            pltpu.VMEM((tokens, model_width), BF16),
            pltpu.VMEM((tokens // 2, model_width), F32),
            pltpu.VMEM((2, group_rows, padded), BF16),
            pltpu.VMEM((2, group_rows, padded), BF16),
            pltpu.VMEM((2, group_rows, padded), BF16),
            pltpu.VMEM((2, group_rows, model_width), BF16),
            pltpu.SemaphoreType.DMA((3,)),
            pltpu.SemaphoreType.DMA((1,)),
            pltpu.SemaphoreType.DMA((2, 4, 2)),
            pltpu.SemaphoreType.DMA((1,)),
        ]
        + line_sems(tokens),
        compiler_params=pltpu.CompilerParams(
            collective_id=collective, has_side_effects=True, vmem_limit_bytes=58 << 20
        ),
        cost_estimate=pl.CostEstimate(
            flops=tokens * model_width * hidden_width * 12,
            bytes_accessed=360_000_000,
            transcendentals=tokens * hidden_width,
        ),
        name="feed_and_norm_two_line",
    )(normed, cotangent, residual, gain, gate_w, up_w, down_w)


def rms_parts(values):
    inverse = lax.rsqrt(jnp.mean(values * values, axis=-1, keepdims=True) + EPSILON)
    return (values * inverse, inverse)


def local(
    mesh_axes,
    hidden,
    segment_ids,
    norm1_gain,
    w_query,
    w_forget,
    w_input,
    w_gate_out,
    forget_floor,
    head_gain,
    w_out,
    norm2_gain,
    w_ffn_gate,
    w_ffn_up,
    w_ffn_down,
    out_grad,
):
    sequences, span_len, model_width = hidden.shape
    tokens = sequences * span_len
    head_count, key_dim = forget_floor.shape
    width = head_count * key_dim
    key_scale = key_dim ** (-0.5)
    both = ("shard", "context")
    mixer_full = lax.all_gather(
        jnp.concatenate([w_query, w_forget, w_input, w_gate_out], axis=1), both, axis=0, tiled=True
    )
    out_full = lax.all_gather(w_out, both, axis=1, tiled=True)
    gate_full = lax.all_gather(w_ffn_gate, both, axis=0, tiled=True)
    up_full = lax.all_gather(w_ffn_up, both, axis=0, tiled=True)
    down_full = lax.all_gather(w_ffn_down, both, axis=1, tiled=True)
    gain_one, gain_two = norm1_gain.reshape(1, -1), norm2_gain.reshape(1, -1)
    half_wide = jax.ShapeDtypeStruct((tokens // 2, model_width), F32)
    one_row = jax.ShapeDtypeStruct((1, model_width), F32)
    hidden_rows = hidden.reshape(tokens, model_width)
    unit_rows, _ = rms_parts(hidden_rows.astype(F32))
    normed_one = (unit_rows * norm1_gain).astype(BF16)
    pre = jnp.dot(normed_one, mixer_full, preferred_element_type=F32)
    open_part = (1.0 - forget_floor).reshape(1, width)
    counts, keep, flags, last_count = row_flags(segment_ids)
    mixed_local, lead, starts, runs, state_end, run_end = mixer_forward(
        pre, open_part, counts, keep, flags, head_count, key_scale
    )
    decay = (jnp.exp(run_end) * (last_count == 0).astype(F32)).reshape(head_count, 1, key_dim)
    ids = segment_ids.reshape(-1).astype(F32)
    carry, link_in = state_before(state_end, decay, ids[0], ids[-1], "context")
    gain_row = head_gain.reshape(1, -1)
    mixed, gated_low = gate_forward(
        mixed_local, lead, carry.astype(BF16), pre, gain_row, keep, key_scale
    )
    mix_part = jnp.dot(gated_low, out_full, preferred_element_type=F32).astype(BF16)
    normed_two, residual = line_exchange(
        residual_norm, mesh_axes, 0, mix_part, (hidden_rows, gain_two), [half_wide], "mix_line"
    )
    grad_rows = out_grad.reshape(tokens, model_width)
    grad_mix_low, grad_norm_two, hidden_low, grad_gate_low, grad_up_low, feed_part, grad_residual = (
        feed_line(
            mesh_axes, 2, normed_two, grad_rows, residual, gain_two, gate_full, up_full, down_full
        )
    )
    (output_rows,) = line_exchange(
        residual_out, mesh_axes, 1, feed_part, (residual,), [], "feed_line"
    )
    grad_down = jnp.einsum("tf,td->fd", hidden_low, grad_rows, preferred_element_type=F32)
    grad_gate = jnp.einsum("td,tf->df", normed_two, grad_gate_low, preferred_element_type=F32)
    grad_up = jnp.einsum("td,tf->df", normed_two, grad_up_low, preferred_element_type=F32)
    grad_out = jnp.einsum("tv,td->vd", gated_low, grad_mix_low, preferred_element_type=F32)
    grad_gated = jnp.einsum("td,vd->tv", grad_mix_low, out_full, preferred_element_type=F32)
    grad_mixed, grad_gate_pre, grad_head_part, back = gate_backward(
        grad_gated, mixed, lead, pre, gain_row, keep, head_count, key_scale
    )
    after = grad_after(back, decay, link_in, "context")
    grad_pre, grad_floor_part = mixer_backward(
        pre,
        grad_mixed,
        grad_gate_pre,
        starts,
        runs,
        carry,
        after,
        open_part,
        counts,
        keep,
        flags,
    )
    grad_mixer = jnp.einsum("td,tk->dk", normed_one, grad_pre, preferred_element_type=F32)
    back_one = jnp.einsum("tk,dk->td", grad_pre, mixer_full, preferred_element_type=F32)
    input_rows, grad_norm_one = line_exchange(
        norm_one_back,
        mesh_axes,
        3,
        back_one.astype(BF16),
        (hidden_rows, grad_residual, gain_one),
        [one_row],
        "norm_one_line",
    )
    grad_norm_one, grad_norm_two, head_total = lax.psum(
        (grad_norm_one.reshape(-1), grad_norm_two.reshape(-1), grad_head_part.reshape(-1)),
        "tensor",
    )

    def share(values, dim):
        return lax.psum_scatter(
            values.astype(BF16), both, scatter_dimension=dim, tiled=True
        ).astype(F32)

    share_mixer = share(grad_mixer, 0)
    return (
        output_rows.reshape(hidden.shape),
        input_rows.reshape(hidden.shape),
        share(grad_norm_one, 0),
        share_mixer[:, :width],
        share_mixer[:, width : 2 * width],
        share_mixer[:, 2 * width : 3 * width],
        share_mixer[:, 3 * width :],
        share(grad_floor_part.reshape(head_count, key_dim), 1),
        share(head_total, 0),
        share(grad_out, 1),
        share(grad_norm_two, 0),
        share(grad_gate, 0),
        share(grad_up, 0),
        share(grad_down, 1),
    )


def solution(mesh):
    in_specs = (
        P("shard", "context", None),
        P("shard", "context"),
        P(),
        P(("shard", "context"), "tensor"),
        P(("shard", "context"), "tensor"),
        P(("shard", "context"), "tensor"),
        P(("shard", "context"), "tensor"),
        P("tensor", None),
        P(),
        P("tensor", ("shard", "context")),
        P(),
        P(("shard", "context"), "tensor"),
        P(("shard", "context"), "tensor"),
        P("tensor", ("shard", "context")),
        P("shard", "context", None),
    )
    out_specs = (
        P("shard", "context", None),
        P("shard", "context", None),
        P(("shard", "context")),
        P(("shard", "context"), "tensor"),
        P(("shard", "context"), "tensor"),
        P(("shard", "context"), "tensor"),
        P(("shard", "context"), "tensor"),
        P("tensor", ("shard", "context")),
        P(("shard", "context")),
        P("tensor", ("shard", "context")),
        P(("shard", "context")),
        P(("shard", "context"), "tensor"),
        P(("shard", "context"), "tensor"),
        P("tensor", ("shard", "context")),
    )
    return jax.shard_map(
        partial(local, mesh.axis_names), mesh=mesh, in_specs=in_specs, out_specs=out_specs, check_vma=False)
```

```python
from functools import partial

import jax
import jax.numpy as jnp
from jax import lax
from jax.experimental import pallas as pl
from jax.experimental.pallas import tpu as pltpu
from jax.sharding import PartitionSpec as P

EPSILON = 1e-05


BLOCK = 128
F32 = jnp.float32
BF16 = jnp.bfloat16


def mm(a, b, dims):
    return lax.dot_general(a, b, (dims, ((), ())), preferred_element_type=F32)


def mm_nn(a, b):
    return mm(a, b, ((1,), (0,)))


def mm_nt(a, b):
    return mm(a, b, ((1,), (1,)))


def mm_tn(a, b):
    return mm(a, b, ((0,), (0,)))


def split_sum(tri, values):
    high = values.astype(BF16)
    low = (values - high.astype(F32)).astype(BF16)
    return mm_nn(tri, high) + mm_nn(tri, low)


def block_masks(counts, flags_row):
    rows = counts.shape[0]
    row_ids = lax.broadcasted_iota(jnp.int32, (rows, rows), 0)
    col_ids = lax.broadcasted_iota(jnp.int32, (rows, rows), 1)
    linked = jnp.logical_and(counts == flags_row[0:1], row_ids >= col_ids)
    fresh = (counts == flags_row[1:2, 0:1]).astype(F32)
    tail = (counts == flags_row[2:3, 0:1]).astype(F32)
    closing = (flags_row[1:2, 0:1] == flags_row[2:3, 0:1]).astype(F32)
    return row_ids, col_ids, linked, fresh, tail, closing


def mixer_forward_kernel(
    head_count,
    key_scale,
    pre_ref,
    open_ref,
    count_ref,
    keep_ref,
    flags_ref,
    mixed_ref,
    lead_ref,
    start_ref,
    run_ref,
    end_ref,
    total_ref,
    state_scr,
    run_scr,
):
    step = pl.program_id(0)
    width = open_ref.shape[1]
    lanes = width // head_count

    @pl.when(step == 0)
    def _():
        state_scr[...] = jnp.zeros_like(state_scr)
        run_scr[...] = jnp.zeros_like(run_scr)

    counts, keep = count_ref[...], keep_ref[...]
    row_ids, col_ids, linked, fresh, tail, closing = block_masks(counts, flags_ref[0])
    tri = (row_ids >= col_ids).astype(BF16)
    query_pre = pre_ref[:, :width]
    values = pre_ref[:, 2 * width : 3 * width].astype(BF16)
    keys = open_ref[...] * jax.nn.sigmoid(-pre_ref[:, width : 2 * width])
    cum = split_sum(tri, jnp.log1p(-keys))
    rows = cum.shape[0]
    ending = cum[rows - 1 : rows, :]
    lifted = query_pre * jax.nn.sigmoid(query_pre) * jnp.exp(cum)
    lowered = (keys * jnp.exp(-cum) * keep).astype(BF16)
    moved = (keys * jnp.exp(ending - cum) * (keep * tail)).astype(BF16)
    run = run_scr[...]
    lead_ref[...] = (lifted * jnp.exp(run) * (counts == 0).astype(F32)).astype(BF16)
    run_ref[0] = run
    run_scr[...] = run + ending
    total_ref[...] = run + ending
    fresh_lifted = (lifted * fresh).astype(BF16)
    lifted = lifted.astype(BF16)
    end_decay = jnp.exp(ending) * closing
    for head in range(head_count):
        part = slice(head * lanes, (head + 1) * lanes)
        state = state_scr[head]
        start_ref[0, head] = state
        scores = jnp.where(linked, mm_nt(lifted[:, part], lowered[:, part]), 0.0)
        results = mm_nn(scores.astype(BF16), values[:, part])
        results = results + mm_nt(fresh_lifted[:, part], state.astype(BF16))
        mixed_ref[:, part] = results * (key_scale * keep)
        state = state * end_decay[:, part] + mm_tn(values[:, part], moved[:, part])
        state_scr[head] = state
        end_ref[head] = state


def mixer_forward(pre, open_part, counts, keep, flags, head_count, key_scale):
    tokens, all_width = pre.shape
    width = open_part.shape[1]
    lanes = width // head_count
    blocks = tokens // BLOCK
    return pl.pallas_call(
        partial(mixer_forward_kernel, head_count, key_scale),
        grid=(blocks,),
        in_specs=[
            pl.BlockSpec((BLOCK, all_width), lambda i: (i, 0)),
            pl.BlockSpec((1, width), lambda i: (0, 0)),
            pl.BlockSpec((BLOCK, 1), lambda i: (i, 0)),
            pl.BlockSpec((BLOCK, 1), lambda i: (i, 0)),
            pl.BlockSpec((1, 8, BLOCK), lambda i: (i, 0, 0)),
        ],
        out_specs=[
            pl.BlockSpec((BLOCK, width), lambda i: (i, 0)),
            pl.BlockSpec((BLOCK, width), lambda i: (i, 0)),
            pl.BlockSpec((1, head_count, lanes, lanes), lambda i: (i, 0, 0, 0)),
            pl.BlockSpec((1, 1, width), lambda i: (i, 0, 0)),
            pl.BlockSpec((head_count, lanes, lanes), lambda i: (0, 0, 0)),
            pl.BlockSpec((1, width), lambda i: (0, 0)),
        ],
        out_shape=[
            jax.ShapeDtypeStruct((tokens, width), F32),
            jax.ShapeDtypeStruct((tokens, width), BF16),
            jax.ShapeDtypeStruct((blocks, head_count, lanes, lanes), F32),
            jax.ShapeDtypeStruct((blocks, 1, width), F32),
            jax.ShapeDtypeStruct((head_count, lanes, lanes), F32),
            jax.ShapeDtypeStruct((1, width), F32),
        ],
        scratch_shapes=[
            pltpu.VMEM((head_count, lanes, lanes), F32),
            pltpu.VMEM((1, width), F32),
        ],
        compiler_params=pltpu.CompilerParams(
            dimension_semantics=("arbitrary",), vmem_limit_bytes=40 << 20
        ),
        cost_estimate=pl.CostEstimate(
            flops=tokens * width * BLOCK * 12,
            bytes_accessed=tokens * width * 30,
            transcendentals=tokens * width * 7,
        ),
        name="mixer_forward",
    )(pre, open_part, counts, keep, flags)


def gate_forward_kernel(
    head_count,
    key_scale,
    local_ref,
    lead_ref,
    carry_ref,
    gate_ref,
    gain_ref,
    keep_ref,
    mixed_ref,
    gated_ref,
):
    lanes = gain_ref.shape[1]
    for head in range(head_count):
        part = slice(head * lanes, (head + 1) * lanes)
        carried = mm_nt(lead_ref[:, part], carry_ref[head])
        mixed = local_ref[:, part] + carried * (key_scale * keep_ref[...])
        mixed_ref[:, part] = mixed
        inverse = lax.rsqrt(jnp.mean(mixed * mixed, axis=-1, keepdims=True) + EPSILON)
        gate = gate_ref[:, part]
        gated = mixed * inverse * gain_ref[...] * (gate * jax.nn.sigmoid(gate))
        gated_ref[:, part] = gated.astype(BF16)


def gate_forward(local, lead, carry, pre, gain, keep, key_scale):
    tokens, width = local.shape
    head_count, lanes = carry.shape[0], carry.shape[2]
    rows = 2 * BLOCK
    return pl.pallas_call(
        partial(gate_forward_kernel, head_count, key_scale),
        grid=(tokens // rows,),
        in_specs=[
            pl.BlockSpec((rows, width), lambda i: (i, 0)),
            pl.BlockSpec((rows, width), lambda i: (i, 0)),
            pl.BlockSpec((head_count, lanes, lanes), lambda i: (0, 0, 0)),
            pl.BlockSpec((rows, width), lambda i: (i, 3)),
            pl.BlockSpec((1, lanes), lambda i: (0, 0)),
            pl.BlockSpec((rows, 1), lambda i: (i, 0)),
        ],
        out_specs=[
            pl.BlockSpec((rows, width), lambda i: (i, 0)),
            pl.BlockSpec((rows, width), lambda i: (i, 0)),
        ],
        out_shape=[
            jax.ShapeDtypeStruct((tokens, width), F32),
            jax.ShapeDtypeStruct((tokens, width), BF16),
        ],
        compiler_params=pltpu.CompilerParams(
            dimension_semantics=("arbitrary",), vmem_limit_bytes=40 << 20
        ),
        cost_estimate=pl.CostEstimate(
            flops=tokens * width * 300,
            bytes_accessed=tokens * width * 16,
            transcendentals=tokens * width,
        ),
        name="gate_forward",
    )(local, lead, carry, pre, gain, keep)


def gate_backward_kernel(
    head_count,
    key_scale,
    grad_ref,
    mixed_ref,
    lead_ref,
    gate_ref,
    gain_ref,
    keep_ref,
    grad_mixed_ref,
    grad_gate_ref,
    grad_gain_ref,
    back_ref,
):
    lanes = gain_ref.shape[1]

    @pl.when(pl.program_id(0) == 0)
    def _():
        grad_gain_ref[...] = jnp.zeros_like(grad_gain_ref)
        back_ref[...] = jnp.zeros_like(back_ref)

    gain = gain_ref[...]
    total = jnp.zeros_like(gain)
    for head in range(head_count):
        part = slice(head * lanes, (head + 1) * lanes)
        mixed, gate, grad = mixed_ref[:, part], gate_ref[:, part], grad_ref[:, part]
        inverse = lax.rsqrt(jnp.mean(mixed * mixed, axis=-1, keepdims=True) + EPSILON)
        unit = mixed * inverse
        sigma = jax.nn.sigmoid(gate)
        scaled = grad * unit
        total = total + jnp.sum(scaled * (gate * sigma), axis=0, keepdims=True)
        grad_gate = scaled * gain * sigma * (1.0 + gate * (1.0 - sigma))
        grad_gate_ref[:, part] = grad_gate.astype(BF16)
        lifted = grad * gain * (gate * sigma)
        mean = jnp.mean(lifted * unit, axis=-1, keepdims=True)
        grad_mixed = inverse * (lifted - unit * mean) * (key_scale * keep_ref[...])
        grad_mixed = grad_mixed.astype(BF16)
        grad_mixed_ref[:, part] = grad_mixed
        back_ref[head] += mm_tn(grad_mixed, lead_ref[:, part])
    grad_gain_ref[...] += total


def gate_backward(grad, mixed, lead, pre, gain, keep, head_count, key_scale):
    tokens, width = mixed.shape
    lanes = gain.shape[1]
    rows = 2 * BLOCK
    return pl.pallas_call(
        partial(gate_backward_kernel, head_count, key_scale),
        grid=(tokens // rows,),
        in_specs=[
            pl.BlockSpec((rows, width), lambda i: (i, 0)),
            pl.BlockSpec((rows, width), lambda i: (i, 0)),
            pl.BlockSpec((rows, width), lambda i: (i, 0)),
            pl.BlockSpec((rows, width), lambda i: (i, 3)),
            pl.BlockSpec((1, lanes), lambda i: (0, 0)),
            pl.BlockSpec((rows, 1), lambda i: (i, 0)),
        ],
        out_specs=[
            pl.BlockSpec((rows, width), lambda i: (i, 0)),
            pl.BlockSpec((rows, width), lambda i: (i, 0)),
            pl.BlockSpec((1, lanes), lambda i: (0, 0)),
            pl.BlockSpec((head_count, lanes, lanes), lambda i: (0, 0, 0)),
        ],
        out_shape=[
            jax.ShapeDtypeStruct((tokens, width), BF16),
            jax.ShapeDtypeStruct((tokens, width), BF16),
            jax.ShapeDtypeStruct((1, lanes), F32),
            jax.ShapeDtypeStruct((head_count, lanes, lanes), F32),
        ],
        compiler_params=pltpu.CompilerParams(
            dimension_semantics=("arbitrary",), vmem_limit_bytes=40 << 20
        ),
        cost_estimate=pl.CostEstimate(
            flops=tokens * width * 300,
            bytes_accessed=tokens * width * 18,
            transcendentals=tokens * width,
        ),
        name="gate_backward",
    )(grad, mixed, lead, pre, gain, keep)


def mixer_backward_kernel(
    head_count,
    pre_ref,
    grad_mixed_ref,
    grad_gate_ref,
    start_ref,
    run_ref,
    carry_ref,
    after_ref,
    open_ref,
    count_ref,
    keep_ref,
    flags_ref,
    grads_ref,
    floor_ref,
    grad_scr,
    lifted_scr,
    lowered_scr,
    moved_scr,
    value_scr,
):
    width = open_ref.shape[1]
    lanes = width // head_count

    @pl.when(pl.program_id(0) == 0)
    def _():
        grad_scr[...] = after_ref[...]
        floor_ref[...] = jnp.zeros_like(floor_ref)

    counts, keep = count_ref[...], keep_ref[...]
    flags = flags_ref[0]
    row_ids, col_ids, linked, fresh, tail, closing = block_masks(counts, flags)
    tri = (row_ids >= col_ids).astype(BF16)
    tri_back = (row_ids <= col_ids).astype(BF16)
    query_pre = pre_ref[:, :width]
    values = pre_ref[:, 2 * width : 3 * width].astype(BF16)
    opened = open_ref[...]
    closed = jax.nn.sigmoid(-pre_ref[:, width : 2 * width])
    keys = opened * closed
    cum = split_sum(tri, jnp.log1p(-keys))
    rows = cum.shape[0]
    ending = cum[rows - 1 : rows, :]
    rise, fall = jnp.exp(cum), jnp.exp(-cum) * keep
    shift = jnp.exp(ending - cum) * (keep * tail)
    sigma_query = jax.nn.sigmoid(query_pre)
    lifted = (query_pre * sigma_query * rise).astype(BF16)
    lowered = (keys * fall).astype(BF16)
    moved = (keys * shift).astype(BF16)
    fresh_lifted = (lifted.astype(F32) * fresh).astype(BF16)
    end_decay = jnp.exp(ending) * closing
    lead_in = jnp.exp(run_ref[0]) * (flags[1:2, 0:1] == 0).astype(F32)
    for head in range(head_count):
        part = slice(head * lanes, (head + 1) * lanes)
        grad_out, value = grad_mixed_ref[:, part], values[:, part]
        lift, lower, move = lifted[:, part], lowered[:, part], moved[:, part]
        scores = jnp.where(linked, mm_nt(lift, lower), 0.0).astype(BF16)
        pulls = jnp.where(linked, mm_nt(grad_out, value), 0.0).astype(BF16)
        state = start_ref[0, head] + lead_in[:, part] * carry_ref[head]
        grad_state = grad_scr[head]
        grad_low = grad_state.astype(BF16)
        lifted_scr[:, part] = mm_nn(pulls, lower) + fresh * mm_nn(grad_out, state.astype(BF16))
        lowered_scr[:, part] = mm_tn(pulls, lift)
        grad_moved = mm_nn(value, grad_low)
        moved_scr[:, part] = grad_moved
        grads_ref[:, 2 * width + head * lanes : 2 * width + (head + 1) * lanes] = (
            mm_tn(scores, grad_out) + mm_nt(move, grad_low)
        ).astype(BF16)
        value_scr[:, part] = jnp.sum(
            grad_moved * move.astype(F32), axis=0, keepdims=True
        ) + end_decay[:, part] * jnp.sum(state * grad_state, axis=0, keepdims=True)
        grad_scr[head] = grad_state * end_decay[:, part] + mm_tn(grad_out, fresh_lifted[:, part])
    grad_lifted, grad_lowered, grad_moved = lifted_scr[...], lowered_scr[...], moved_scr[...]
    grad_cum = (
        grad_lifted * lifted.astype(F32)
        - grad_lowered * lowered.astype(F32)
        - grad_moved * moved.astype(F32)
    )
    grad_decay = split_sum(tri_back, grad_cum) + value_scr[...]
    key_total = grad_lowered * fall + grad_moved * shift - grad_decay / (1.0 - keys)
    floor_ref[...] -= jnp.sum(key_total * closed, axis=0, keepdims=True)
    grads_ref[:, :width] = (
        grad_lifted * rise * sigma_query * (1.0 + query_pre * (1.0 - sigma_query))
    ).astype(BF16)
    grads_ref[:, width : 2 * width] = (-key_total * opened * closed * (1.0 - closed)).astype(BF16)
    grads_ref[:, 3 * width :] = grad_gate_ref[...]


def mixer_backward(
    pre, grad_mixed, grad_gate, starts, runs, carry, after, open_part, counts, keep, flags
):
    tokens, all_width = pre.shape
    width = open_part.shape[1]
    head_count, lanes = carry.shape[0], carry.shape[2]
    blocks = tokens // BLOCK
    last = blocks - 1
    return pl.pallas_call(
        partial(mixer_backward_kernel, head_count),
        grid=(blocks,),
        in_specs=[
            pl.BlockSpec((BLOCK, all_width), lambda i: (last - i, 0)),
            pl.BlockSpec((BLOCK, width), lambda i: (last - i, 0)),
            pl.BlockSpec((BLOCK, width), lambda i: (last - i, 0)),
            pl.BlockSpec((1, head_count, lanes, lanes), lambda i: (last - i, 0, 0, 0)),
            pl.BlockSpec((1, 1, width), lambda i: (last - i, 0, 0)),
            pl.BlockSpec((head_count, lanes, lanes), lambda i: (0, 0, 0)),
            pl.BlockSpec((head_count, lanes, lanes), lambda i: (0, 0, 0)),
            pl.BlockSpec((1, width), lambda i: (0, 0)),
            pl.BlockSpec((BLOCK, 1), lambda i: (last - i, 0)),
            pl.BlockSpec((BLOCK, 1), lambda i: (last - i, 0)),
            pl.BlockSpec((1, 8, BLOCK), lambda i: (last - i, 0, 0)),
        ],
        out_specs=[
            pl.BlockSpec((BLOCK, all_width), lambda i: (last - i, 0)),
            pl.BlockSpec((1, width), lambda i: (0, 0)),
        ],
        out_shape=[
            jax.ShapeDtypeStruct((tokens, all_width), BF16),
            jax.ShapeDtypeStruct((1, width), F32),
        ],
        scratch_shapes=[
            pltpu.VMEM((head_count, lanes, lanes), F32),
            pltpu.VMEM((BLOCK, width), F32),
            pltpu.VMEM((BLOCK, width), F32),
            pltpu.VMEM((BLOCK, width), F32),
            pltpu.VMEM((1, width), F32),
        ],
        compiler_params=pltpu.CompilerParams(
            dimension_semantics=("arbitrary",), vmem_limit_bytes=40 << 20
        ),
        cost_estimate=pl.CostEstimate(
            flops=tokens * width * BLOCK * 30,
            bytes_accessed=tokens * width * 36,
            transcendentals=tokens * width * 9,
        ),
        name="mixer_backward",
    )(pre, grad_mixed, grad_gate, starts, runs, carry, after, open_part, counts, keep, flags)


def row_flags(segment_ids):
    ids = segment_ids.reshape(-1)
    tokens = ids.shape[0]
    starts = jnp.concatenate([jnp.zeros((1,), F32), (ids[1:] != ids[:-1]).astype(F32)])
    positions = jnp.arange(tokens)
    counts = jnp.sum(
        jnp.where(positions[None, :] <= positions[:, None], starts[None, :], 0.0), axis=1
    )
    keep = (ids > 0).astype(F32)
    blocks = tokens // BLOCK
    by_block = counts.reshape(blocks, BLOCK)
    lasts = by_block[:, -1]
    before = jnp.concatenate([jnp.zeros((1,), F32), lasts[:-1]])
    wide = (blocks, BLOCK)
    flags = jnp.stack(
        [by_block, jnp.broadcast_to(before[:, None], wide), jnp.broadcast_to(lasts[:, None], wide)]
        + [jnp.zeros(wide, F32)] * 5,
        axis=1,
    )
    return counts[:, None], keep[:, None], flags, lasts[-1]


def from_earlier(values, axis, shift):
    count = lax.axis_size(axis)
    return lax.ppermute(values, axis, [(i, i + shift) for i in range(count - shift)])


def from_later(values, axis, shift):
    count = lax.axis_size(axis)
    return lax.ppermute(values, axis, [(i + shift, i) for i in range(count - shift)])


def state_before(state, decay, first_id, last_id, axis):
    head_count, lanes, _ = state.shape
    ids = jnp.stack([first_id, last_id, jnp.float32(1.0)] + [jnp.float32(0.0)] * 5)
    message = jnp.concatenate(
        [
            state.reshape(head_count * lanes, lanes),
            decay.reshape(head_count, lanes),
            jnp.broadcast_to(ids[:, None], (8, lanes)),
        ]
    )
    rows = head_count * lanes
    total = jnp.zeros_like(state)
    factor = jnp.ones((head_count, 1, lanes), F32)
    follower = first_id
    link_in = jnp.float32(0.0)
    for shift in range(1, lax.axis_size(axis)):
        got = from_earlier(message, axis, shift)
        got_ids = got[rows + head_count :, 0]
        linked = (got_ids[1] == follower).astype(F32) * got_ids[2]
        if shift == 1:
            link_in = linked
        factor = factor * linked
        total = total + factor * got[:rows].reshape(state.shape)
        factor = factor * got[rows : rows + head_count].reshape(head_count, 1, lanes)
        follower = got_ids[0]
    return total, link_in


def grad_after(back, decay, link_in, axis):
    head_count, lanes, _ = back.shape
    rows = head_count * lanes
    message = (
        jnp.concatenate([back.reshape(rows, lanes), decay.reshape(head_count, lanes)]) * link_in
    )
    message = jnp.pad(message, ((0, 8 - head_count % 8 if head_count % 8 else 0), (0, 0)))
    total = jnp.zeros_like(back)
    factor = jnp.ones((head_count, 1, lanes), F32)
    for shift in range(1, lax.axis_size(axis)):
        got = from_later(message, axis, shift)
        total = total + factor * got[:rows].reshape(back.shape)
        factor = factor * got[rows : rows + head_count].reshape(head_count, 1, lanes)
    return total


CHUNK = 32
LAG = 2
MESH_ID = pl.DeviceIdType.MESH


class Line:
    def __init__(self, mesh_axes, part, arrived, out, sems, transform):
        self.mesh_axes = mesh_axes
        self.part, self.arrived, self.out = part, arrived, out
        self.sum_send, self.sum_recv, self.back_send, self.back_recv = sems
        self.transform = transform
        self.half = part.shape[0] // 2
        self.chunks = self.half // CHUNK
        self.size = lax.axis_size("tensor")
        self.place = lax.axis_index("tensor")
        self.lines = ((self.size - 1 - self.place, -1), (self.place, 1))
        self.steps = self.chunks + 2 * LAG * (self.size - 1)

    def device(self, position):
        return tuple(
            jnp.clip(position, 0, self.size - 1) if axis == "tensor" else lax.axis_index(axis)
            for axis in self.mesh_axes
        )

    def greet(self, barrier):
        for step in (-1, 1):
            inside = jnp.logical_and(self.place + step >= 0, self.place + step < self.size)

            @pl.when(inside)
            def _(step=step):
                pl.semaphore_signal(
                    barrier, inc=1, device_id=self.device(self.place + step), device_id_type=MESH_ID
                )

        at_end = jnp.logical_or(self.place == 0, self.place == self.size - 1)
        return jnp.where(at_end, 1, 2)

    def rows_of(self, side, index):
        return pl.ds(pl.multiple_of(side * self.half + index * CHUNK, CHUNK), CHUNK)

    def sum_copy(self, side, index, source):
        rows = self.rows_of(side, index)
        return pltpu.make_async_remote_copy(
            source.at[rows],
            self.arrived.at[rows],
            self.sum_send.at[side, index],
            self.sum_recv.at[side, index],
            device_id=self.device(self.place + self.lines[side][1]),
            device_id_type=MESH_ID,
        )

    def back_copy(self, side, index):
        rows = self.rows_of(side, index)
        return pltpu.make_async_remote_copy(
            self.out.at[rows],
            self.out.at[rows],
            self.back_send.at[side, index],
            self.back_recv.at[side, index],
            device_id=self.device(self.place - self.lines[side][1]),
            device_id_type=MESH_ID,
        )

    def step(self, time):
        for side in (0, 1):
            hops = self.lines[side][0]
            index = time - LAG * hops
            valid = jnp.logical_and(index >= 0, index < self.chunks)
            at_source, at_owner = hops == 0, hops == self.size - 1
            index = jnp.clip(index, 0, self.chunks - 1)
            rows = self.rows_of(side, index)

            @pl.when(jnp.logical_and(valid, at_source))
            def _(side=side, index=index):
                self.sum_copy(side, index, self.part).start()

            @pl.when(jnp.logical_and(valid, jnp.logical_not(at_source)))
            def _(side=side, index=index):
                self.sum_copy(side, index, self.arrived).wait_recv()

            between = jnp.logical_and(jnp.logical_not(at_source), jnp.logical_not(at_owner))

            @pl.when(jnp.logical_and(valid, between))
            def _(side=side, index=index, rows=rows):
                total = self.part[rows].astype(F32) + self.arrived[rows].astype(F32)
                self.arrived[rows] = total.astype(BF16)
                self.sum_copy(side, index, self.arrived).start()

            @pl.when(jnp.logical_and(valid, at_owner))
            def _(side=side, index=index, rows=rows):
                total = self.part[rows].astype(F32) + self.arrived[rows].astype(F32)
                own = pl.ds(pl.multiple_of(index * CHUNK, CHUNK), CHUNK)
                self.transform(total, rows, own)
                self.back_copy(side, index).start()

            away = self.size - 1 - hops
            index = time - LAG * (self.size - 1 + away)
            valid = jnp.logical_and(jnp.logical_and(index >= 0, index < self.chunks), away > 0)
            index = jnp.clip(index, 0, self.chunks - 1)

            @pl.when(valid)
            def _(side=side, index=index):
                self.back_copy(side, index).wait_recv()

            @pl.when(jnp.logical_and(valid, away < self.size - 1))
            def _(side=side, index=index):
                self.back_copy(side, index).start()

    def run(self, first, last, beside=None):
        def body(time, _):
            self.step(time)
            if beside is not None:
                beside(time)
            return 0

        lax.fori_loop(first, last, body, 0)

    def finish(self):
        def body(index, _):
            for side in (0, 1):
                hops = self.lines[side][0]

                @pl.when(hops < self.size - 1)
                def _(side=side):
                    self.sum_copy(side, index, self.arrived).wait_send()

                @pl.when(hops > 0)
                def _(side=side):
                    self.back_copy(side, index).wait_send()

            return 0

        lax.fori_loop(0, self.chunks, body, 0)


def line_sems(tokens):
    return [pltpu.SemaphoreType.DMA((2, tokens // 2 // CHUNK))] * 4


def line_exchange_kernel(transform, mesh_axes, n_in, n_out, *refs):
    part, extra_in = refs[0], refs[1 : 1 + n_in]
    out, extra_out = refs[1 + n_in], refs[2 + n_in : 2 + n_in + n_out]
    arrived, *sems = refs[2 + n_in + n_out :]
    def turn(total, rows, own):
        transform(total, rows, own, extra_in, out, extra_out)

    line = Line(mesh_axes, part, arrived, out, sems, turn)
    barrier = pltpu.get_barrier_semaphore()
    pl.semaphore_wait(barrier, line.greet(barrier))
    line.run(0, line.steps)
    line.finish()


def line_exchange(transform, mesh_axes, collective, part, extras, extra_shapes, name):
    tokens, width = part.shape
    whole = pl.BlockSpec(memory_space=pltpu.VMEM)
    return pl.pallas_call(
        partial(line_exchange_kernel, transform, mesh_axes, len(extras), len(extra_shapes)),
        in_specs=[whole] * (1 + len(extras)),
        out_specs=[whole] * (1 + len(extra_shapes)),
        out_shape=[jax.ShapeDtypeStruct((tokens, width), BF16)] + list(extra_shapes),
        scratch_shapes=[pltpu.VMEM((tokens, width), BF16)] + line_sems(tokens),
        compiler_params=pltpu.CompilerParams(
            collective_id=collective, has_side_effects=True, vmem_limit_bytes=52 << 20
        ),
        cost_estimate=pl.CostEstimate(
            flops=tokens * width * 8, bytes_accessed=360_000_000, transcendentals=0
        ),
        name=name,
    )(part, *extras)


def inverse_rms(values):
    return lax.rsqrt(jnp.mean(values * values, axis=-1, keepdims=True) + EPSILON)


def residual_norm(total, rows, own, extra_in, out, extra_out):
    hidden, gain = extra_in
    residual = hidden[rows].astype(F32) + total
    extra_out[0][own] = residual
    out[rows] = (residual * inverse_rms(residual) * gain[...]).astype(BF16)


GROUP = 128
TILE = 256


def feed_kernel(
    mesh_axes,
    normed_ref,
    cotangent_ref,
    residual_hbm,
    gain_ref,
    gate_hbm,
    up_hbm,
    down_hbm,
    out_ref,
    gain_grad,
    hidden_hbm,
    grad_gate_hbm,
    grad_up_hbm,
    feed_hbm,
    grad_hbm,
    gate_w,
    up_w,
    down_w,
    part,
    arrived,
    residual,
    stage_hidden,
    stage_gate,
    stage_up,
    stage_feed,
    weight_sem,
    residual_sem,
    stage_sem,
    grad_sem,
    *sems,
):
    tokens, model_width = normed_ref.shape
    half = tokens // 2
    hidden_width = gate_hbm.shape[1]
    padded = gate_w.shape[1]
    groups = half // GROUP
    loads = [
        pltpu.make_async_copy(gate_hbm, gate_w.at[:, pl.ds(0, hidden_width)], weight_sem.at[0]),
        pltpu.make_async_copy(up_hbm, up_w.at[:, pl.ds(0, hidden_width)], weight_sem.at[1]),
        pltpu.make_async_copy(down_hbm, down_w.at[pl.ds(0, hidden_width)], weight_sem.at[2]),
    ]
    for load in loads:
        load.start()
    residual_load = pltpu.make_async_copy(residual_hbm, residual, residual_sem.at[0])
    residual_load.start()
    if padded > hidden_width:
        spare = slice(hidden_width, padded)
        gate_w[:, spare] = jnp.zeros((model_width, padded - hidden_width), BF16)
        up_w[:, spare] = jnp.zeros((model_width, padded - hidden_width), BF16)
        down_w[spare, :] = jnp.zeros((padded - hidden_width, model_width), BF16)
    gain_grad[...] = jnp.zeros_like(gain_grad)

    def turn(total, rows, own):
        values = residual[own]
        inverse = inverse_rms(values)
        unit = values * inverse
        gain_grad[...] += jnp.sum(total * unit, axis=0, keepdims=True)
        lifted = total * gain_ref[...]
        mean = jnp.mean(lifted * unit, axis=-1, keepdims=True)
        grad = cotangent_ref[rows].astype(F32) + inverse * (lifted - unit * mean)
        residual[own] = grad
        out_ref[rows] = grad.astype(BF16)

    line = Line(mesh_axes, part, arrived, out_ref, sems, turn)
    barrier = pltpu.get_barrier_semaphore()
    pl.semaphore_wait(barrier, line.greet(barrier))
    residual_load.wait()
    for load in loads:
        load.wait()

    def both(ref, group):
        first = pl.ds(pl.multiple_of(group * GROUP, GROUP), GROUP)
        second = pl.ds(pl.multiple_of(half + group * GROUP, GROUP), GROUP)
        return first, second

    def stage_copies(group):
        slot = lax.rem(group, 2)
        copies = []
        for side, rows in enumerate(both(None, group)):
            from_rows = pl.ds(side * GROUP, GROUP)
            columns = pl.ds(0, hidden_width)
            for which, (stage, target) in enumerate(
                (
                    (stage_hidden, hidden_hbm),
                    (stage_gate, grad_gate_hbm),
                    (stage_up, grad_up_hbm),
                )
            ):
                copies.append(
                    pltpu.make_async_copy(
                        stage.at[slot, from_rows, columns],
                        target.at[rows],
                        stage_sem.at[slot, which, side],
                    )
                )
            copies.append(
                pltpu.make_async_copy(
                    stage_feed.at[slot, from_rows], feed_hbm.at[rows], stage_sem.at[slot, 3, side]
                )
            )
        return copies

    def hidden_tile(group, tile):
        first, second = both(normed_ref, group)
        slot = lax.rem(group, 2)
        columns = pl.ds(pl.multiple_of(tile * TILE, TILE), TILE)
        rows = jnp.concatenate([normed_ref[first], normed_ref[second]], axis=0)
        gate = mm_nn(rows, gate_w[:, columns])
        up = mm_nn(rows, up_w[:, columns])
        grads = jnp.concatenate([cotangent_ref[first], cotangent_ref[second]], axis=0)
        grad = mm_nt(grads, down_w[columns, :])
        sigma = jax.nn.sigmoid(gate)
        active = gate * sigma
        stage_hidden[slot, :, columns] = (active * up).astype(BF16)
        stage_gate[slot, :, columns] = (grad * up * sigma * (1.0 + gate * (1.0 - sigma))).astype(
            BF16
        )
        stage_up[slot, :, columns] = (grad * active).astype(BF16)

    def model_tile(group, tile):
        first, second = both(part, group)
        slot = lax.rem(group, 2)
        columns = pl.ds(pl.multiple_of(tile * TILE, TILE), TILE)
        back = mm_nt(stage_gate[slot], gate_w[columns, :])
        back = (back + mm_nt(stage_up[slot], up_w[columns, :])).astype(BF16)
        part[first, columns] = back[:GROUP]
        part[second, columns] = back[GROUP:]
        stage_feed[slot, :, columns] = mm_nn(stage_hidden[slot], down_w[:, columns]).astype(BF16)

    hidden_tiles, model_tiles = padded // TILE, model_width // TILE
    ticks = hidden_tiles + model_tiles
    pace = GROUP // CHUNK
    piece = -(-ticks // pace)

    def group_body(group, _):
        @pl.when(group >= 2)
        def _():
            for copy in stage_copies(group - 2):
                copy.wait()

        def piece_body(index, _):
            def tick_body(offset, _):
                tick = index * piece + offset

                @pl.when(tick < hidden_tiles)
                def _():
                    hidden_tile(group, tick)

                @pl.when(jnp.logical_and(tick >= hidden_tiles, tick < ticks))
                def _():
                    model_tile(group, tick - hidden_tiles)

                return 0

            lax.fori_loop(0, piece, tick_body, 0)

            @pl.when(group >= 1)
            def _():
                line.step((group - 1) * pace + index)

            return 0

        lax.fori_loop(0, pace, piece_body, 0)
        for copy in stage_copies(group):
            copy.start()
        return 0

    lax.fori_loop(0, groups, group_body, 0)
    line.run((groups - 1) * pace, line.steps)
    save = pltpu.make_async_copy(residual, grad_hbm, grad_sem.at[0])
    save.start()
    for group in range(max(groups - 2, 0), groups):
        for copy in stage_copies(group):
            copy.wait()
    line.finish()
    save.wait()


def feed_line(mesh_axes, collective, normed, cotangent, residual, gain, gate_w, up_w, down_w):
    tokens, model_width = normed.shape
    hidden_width = gate_w.shape[1]
    padded = -(-hidden_width // TILE) * TILE
    whole = pl.BlockSpec(memory_space=pltpu.VMEM)
    remote = pl.BlockSpec(memory_space=pl.ANY)
    group_rows = 2 * GROUP
    return pl.pallas_call(
        partial(feed_kernel, mesh_axes),
        in_specs=[whole, whole, remote, whole, remote, remote, remote],
        out_specs=[whole, whole] + [remote] * 5,
        out_shape=[
            jax.ShapeDtypeStruct((tokens, model_width), BF16),
            jax.ShapeDtypeStruct((1, model_width), F32),
            jax.ShapeDtypeStruct((tokens, hidden_width), BF16),
            jax.ShapeDtypeStruct((tokens, hidden_width), BF16),
            jax.ShapeDtypeStruct((tokens, hidden_width), BF16),
            jax.ShapeDtypeStruct((tokens, model_width), BF16),
            jax.ShapeDtypeStruct((tokens // 2, model_width), F32),
        ],
        scratch_shapes=[
            pltpu.VMEM((model_width, padded), BF16),
            pltpu.VMEM((model_width, padded), BF16),
            pltpu.VMEM((padded, model_width), BF16),
            pltpu.VMEM((tokens, model_width), BF16),
            pltpu.VMEM((tokens, model_width), BF16),
            pltpu.VMEM((tokens // 2, model_width), F32),
            pltpu.VMEM((2, group_rows, padded), BF16),
            pltpu.VMEM((2, group_rows, padded), BF16),
            pltpu.VMEM((2, group_rows, padded), BF16),
            pltpu.VMEM((2, group_rows, model_width), BF16),
            pltpu.SemaphoreType.DMA((3,)),
            pltpu.SemaphoreType.DMA((1,)),
            pltpu.SemaphoreType.DMA((2, 4, 2)),
            pltpu.SemaphoreType.DMA((1,)),
        ]
        + line_sems(tokens),
        compiler_params=pltpu.CompilerParams(
            collective_id=collective, has_side_effects=True, vmem_limit_bytes=58 << 20
        ),
        cost_estimate=pl.CostEstimate(
            flops=tokens * model_width * hidden_width * 12,
            bytes_accessed=360_000_000,
            transcendentals=tokens * hidden_width,
        ),
        name="feed_and_norm_two_line",
    )(normed, cotangent, residual, gain, gate_w, up_w, down_w)


def output_kernel(
    mesh_axes,
    part,
    residual,
    normed_ref,
    cotangent_ref,
    hidden_ref,
    grad_gate_ref,
    grad_up_ref,
    out_ref,
    grads_hbm,
    arrived,
    stage,
    stage_sem,
    *sems,
):
    model_width = normed_ref.shape[1]
    tiles = model_width // TILE

    def turn(total, rows, own):
        out_ref[rows] = (residual[own] + total).astype(BF16)

    line = Line(mesh_axes, part, arrived, out_ref, sems, turn)
    barrier = pltpu.get_barrier_semaphore()
    pl.semaphore_wait(barrier, line.greet(barrier))

    def stage_copy(tile):
        rows = pl.ds(pl.multiple_of(tile * TILE, TILE), TILE)
        slot = lax.rem(tile, 2)
        return pltpu.make_async_copy(stage.at[slot], grads_hbm.at[:, rows], stage_sem.at[slot])

    def weight_tile(time):
        tile = jnp.clip(time, 0, tiles - 1)
        slot = lax.rem(tile, 2)
        columns = pl.ds(pl.multiple_of(tile * TILE, TILE), TILE)

        @pl.when(jnp.logical_and(time < tiles, time >= 2))
        def _():
            stage_copy(tile - 2).wait()

        @pl.when(time < tiles)
        def _():
            rows = normed_ref[:, columns]
            stage[slot, 0] = mm_tn(rows, grad_gate_ref[...]).astype(BF16)
            stage[slot, 1] = mm_tn(rows, grad_up_ref[...]).astype(BF16)
            stage[slot, 2] = mm_tn(cotangent_ref[:, columns], hidden_ref[...]).astype(BF16)
            stage_copy(tile).start()

    line.run(0, line.steps, weight_tile)
    for tile in range(max(tiles - 2, 0), tiles):
        stage_copy(tile).wait()
    line.finish()


def output_line(
    mesh_axes, collective, part, residual, normed, cotangent, hidden_low, grad_gate, grad_up
):
    tokens, model_width = part.shape
    hidden_width = hidden_low.shape[1]
    whole = pl.BlockSpec(memory_space=pltpu.VMEM)
    return pl.pallas_call(
        partial(output_kernel, mesh_axes),
        in_specs=[whole] * 7,
        out_specs=[whole, pl.BlockSpec(memory_space=pl.ANY)],
        out_shape=[
            jax.ShapeDtypeStruct((tokens, model_width), BF16),
            jax.ShapeDtypeStruct((3, model_width, hidden_width), BF16),
        ],
        scratch_shapes=[
            pltpu.VMEM((tokens, model_width), BF16),
            pltpu.VMEM((2, 3, TILE, hidden_width), BF16),
            pltpu.SemaphoreType.DMA((2,)),
        ]
        + line_sems(tokens),
        compiler_params=pltpu.CompilerParams(
            collective_id=collective, has_side_effects=True, vmem_limit_bytes=56 << 20
        ),
        cost_estimate=pl.CostEstimate(
            flops=tokens * model_width * hidden_width * 6,
            bytes_accessed=360_000_000,
            transcendentals=0,
        ),
        name="output_line",
    )(part, residual, normed, cotangent, hidden_low, grad_gate, grad_up)


class Plane:
    def __init__(self, mesh_axes):
        self.mesh_axes = mesh_axes
        self.context = lax.axis_size("context")
        self.per_row = self.context // 2
        self.chips = lax.axis_size("shard") * self.per_row
        context_place = lax.axis_index("context")
        self.core = lax.rem(context_place, 2)
        self.chip = lax.axis_index("shard") * self.per_row + context_place // 2

    def device(self, chip, core):
        places = {
            "shard": chip // self.per_row,
            "context": 2 * lax.rem(chip, self.per_row) + core,
            "tensor": lax.axis_index("tensor"),
        }
        return tuple(places[axis] for axis in self.mesh_axes)

    def ahead(self, distance):
        return lax.rem(self.chip + distance, self.chips)

    def greet(self, barrier):
        targets = [self.device(self.chip, 1 - self.core)]
        targets += [self.device(self.ahead(step), self.core) for step in range(1, self.chips)]
        for target in targets:
            pl.semaphore_signal(barrier, inc=1, device_id=target, device_id_type=MESH_ID)
        return len(targets)


def input_kernel(
    mesh_axes,
    part,
    hidden_ref,
    residual_grad,
    gain_ref,
    grads_hbm,
    out_ref,
    gain_grad,
    share_gate,
    share_up,
    share_down,
    arrived,
    own,
    other,
    remote,
    load_sem,
    pair_send,
    pair_recv,
    chip_send,
    chip_recv,
    *sems,
):
    plane = Plane(mesh_axes)
    chips = plane.chips
    block = own.shape[2]
    gain_grad[...] = jnp.zeros_like(gain_grad)

    def turn(total, rows, own_rows):
        values = hidden_ref[rows].astype(F32)
        inverse = inverse_rms(values)
        unit = values * inverse
        gain_grad[...] += jnp.sum(total * unit, axis=0, keepdims=True)
        lifted = total * gain_ref[...]
        mean = jnp.mean(lifted * unit, axis=-1, keepdims=True)
        grad = residual_grad[own_rows] + inverse * (lifted - unit * mean)
        out_ref[rows] = grad.astype(BF16)

    line = Line(mesh_axes, part, arrived, out_ref, sems, turn)
    barrier = pltpu.get_barrier_semaphore()
    expected = line.greet(barrier) + plane.greet(barrier)
    pl.semaphore_wait(barrier, expected)

    def rows_of(slot, core):
        return pl.ds(pl.multiple_of((2 * plane.ahead(slot) + core) * block, block), block)

    def load(slot):
        return pltpu.make_async_copy(
            grads_hbm.at[:, rows_of(slot, plane.core)], own.at[slot], load_sem.at[slot]
        )

    def pair_copy(slot):
        return pltpu.make_async_remote_copy(
            grads_hbm.at[:, rows_of(slot, 1 - plane.core)],
            other.at[slot],
            pair_send.at[slot],
            pair_recv.at[slot],
            device_id=plane.device(plane.chip, 1 - plane.core),
            device_id_type=MESH_ID,
        )

    def chip_copy(slot):
        return pltpu.make_async_remote_copy(
            own.at[slot],
            remote.at[slot - 1],
            chip_send.at[slot - 1],
            chip_recv.at[slot - 1],
            device_id=plane.device(plane.ahead(slot), plane.core),
            device_id_type=MESH_ID,
        )

    def start(index, _):
        slot = lax.rem(index + 1, chips)
        pair_copy(slot).start()
        load(slot).start()
        return 0

    lax.fori_loop(0, chips, start, 0)
    strip = 32

    def combine(time):
        slot = lax.rem(jnp.clip(time, 0, chips - 1) + 1, chips)

        @pl.when(time < chips)
        def _():
            load(slot).wait()
            pair_copy(slot).wait_recv()

            def add(index, _):
                rows = pl.ds(pl.multiple_of(index * strip, strip), strip)
                for which in range(3):
                    total = own[slot, which, rows].astype(F32) + other[slot, which, rows].astype(F32)
                    own[slot, which, rows] = total.astype(BF16)
                return 0

            lax.fori_loop(0, block // strip, add, 0)

        @pl.when(time < chips - 1)
        def _():
            chip_copy(slot).start()

    line.run(0, line.steps, combine)

    def arrive(index, _):
        chip_copy(index).wait_recv()
        return 0

    lax.fori_loop(1, chips, arrive, 0)

    def total(index, _):
        rows = pl.ds(pl.multiple_of(index * strip, strip), strip)

        def whole(which):
            def add(slot, value):
                return value + remote[slot, which, rows].astype(F32)

            return lax.fori_loop(0, chips - 1, add, own[0, which, rows].astype(F32))

        share_gate[rows] = whole(0)
        share_up[rows] = whole(1)
        share_down[rows] = whole(2)
        return 0

    lax.fori_loop(0, block // strip, total, 0)

    def sent(index, _):
        pair_copy(index).wait_send()
        return 0

    lax.fori_loop(0, chips, sent, 0)

    def chip_sent(index, _):
        chip_copy(index).wait_send()
        return 0

    lax.fori_loop(1, chips, chip_sent, 0)
    line.finish()


def input_line(mesh_axes, collective, part, hidden, residual_grad, gain, grads):
    tokens, model_width = part.shape
    hidden_width = grads.shape[2]
    chips = lax.axis_size("shard") * lax.axis_size("context") // 2
    block = model_width // (2 * chips)
    whole = pl.BlockSpec(memory_space=pltpu.VMEM)
    return pl.pallas_call(
        partial(input_kernel, mesh_axes),
        in_specs=[whole] * 4 + [pl.BlockSpec(memory_space=pl.ANY)],
        out_specs=[whole] * 5,
        out_shape=[
            jax.ShapeDtypeStruct((tokens, model_width), BF16),
            jax.ShapeDtypeStruct((1, model_width), F32),
        ]
        + [jax.ShapeDtypeStruct((block, hidden_width), F32)] * 3,
        scratch_shapes=[
            pltpu.VMEM((tokens, model_width), BF16),
            pltpu.VMEM((chips, 3, block, hidden_width), BF16),
            pltpu.VMEM((chips, 3, block, hidden_width), BF16),
            pltpu.VMEM((chips - 1, 3, block, hidden_width), BF16),
            pltpu.SemaphoreType.DMA((chips,)),
            pltpu.SemaphoreType.DMA((chips,)),
            pltpu.SemaphoreType.DMA((chips,)),
            pltpu.SemaphoreType.DMA((chips - 1,)),
            pltpu.SemaphoreType.DMA((chips - 1,)),
        ]
        + line_sems(tokens),
        compiler_params=pltpu.CompilerParams(
            collective_id=collective, has_side_effects=True, vmem_limit_bytes=58 << 20
        ),
        cost_estimate=pl.CostEstimate(
            flops=tokens * model_width * 8, bytes_accessed=360_000_000, transcendentals=0
        ),
        name="input_line",
    )(part, hidden, residual_grad, gain, grads)


def rms_parts(values):
    inverse = lax.rsqrt(jnp.mean(values * values, axis=-1, keepdims=True) + EPSILON)
    return (values * inverse, inverse)


def local(
    mesh_axes,
    hidden,
    segment_ids,
    norm1_gain,
    w_query,
    w_forget,
    w_input,
    w_gate_out,
    forget_floor,
    head_gain,
    w_out,
    norm2_gain,
    w_ffn_gate,
    w_ffn_up,
    w_ffn_down,
    out_grad,
):
    sequences, span_len, model_width = hidden.shape
    tokens = sequences * span_len
    head_count, key_dim = forget_floor.shape
    width = head_count * key_dim
    key_scale = key_dim ** (-0.5)
    both = ("shard", "context")
    mixer_full = lax.all_gather(
        jnp.concatenate([w_query, w_forget, w_input, w_gate_out], axis=1), both, axis=0, tiled=True
    )
    out_full = lax.all_gather(w_out, both, axis=1, tiled=True)
    gate_full = lax.all_gather(w_ffn_gate, both, axis=0, tiled=True)
    up_full = lax.all_gather(w_ffn_up, both, axis=0, tiled=True)
    down_full = lax.all_gather(w_ffn_down, both, axis=1, tiled=True)
    gain_one, gain_two = norm1_gain.reshape(1, -1), norm2_gain.reshape(1, -1)
    half_wide = jax.ShapeDtypeStruct((tokens // 2, model_width), F32)
    hidden_rows = hidden.reshape(tokens, model_width)
    unit_rows, _ = rms_parts(hidden_rows.astype(F32))
    normed_one = (unit_rows * norm1_gain).astype(BF16)
    pre = jnp.dot(normed_one, mixer_full, preferred_element_type=F32)
    open_part = (1.0 - forget_floor).reshape(1, width)
    counts, keep, flags, last_count = row_flags(segment_ids)
    mixed_local, lead, starts, runs, state_end, run_end = mixer_forward(
        pre, open_part, counts, keep, flags, head_count, key_scale
    )
    decay = (jnp.exp(run_end) * (last_count == 0).astype(F32)).reshape(head_count, 1, key_dim)
    ids = segment_ids.reshape(-1).astype(F32)
    carry, link_in = state_before(state_end, decay, ids[0], ids[-1], "context")
    gain_row = head_gain.reshape(1, -1)
    mixed, gated_low = gate_forward(
        mixed_local, lead, carry.astype(BF16), pre, gain_row, keep, key_scale
    )
    mix_part = jnp.dot(gated_low, out_full, preferred_element_type=F32).astype(BF16)
    normed_two, residual = line_exchange(
        residual_norm, mesh_axes, 0, mix_part, (hidden_rows, gain_two), [half_wide], "mix_line"
    )
    grad_rows = out_grad.reshape(tokens, model_width)
    grad_mix_low, grad_norm_two, hidden_low, grad_gate_low, grad_up_low, feed_part, grad_residual = (
        feed_line(
            mesh_axes, 2, normed_two, grad_rows, residual, gain_two, gate_full, up_full, down_full
        )
    )
    output_rows, grads_ffn = output_line(
        mesh_axes,
        1,
        feed_part,
        residual,
        normed_two,
        grad_rows,
        hidden_low,
        grad_gate_low,
        grad_up_low,
    )
    grad_out = jnp.einsum("tv,td->vd", gated_low, grad_mix_low, preferred_element_type=F32)
    grad_gated = jnp.einsum("td,vd->tv", grad_mix_low, out_full, preferred_element_type=F32)
    grad_mixed, grad_gate_pre, grad_head_part, back = gate_backward(
        grad_gated, mixed, lead, pre, gain_row, keep, head_count, key_scale
    )
    after = grad_after(back, decay, link_in, "context")
    grad_pre, grad_floor_part = mixer_backward(
        pre,
        grad_mixed,
        grad_gate_pre,
        starts,
        runs,
        carry,
        after,
        open_part,
        counts,
        keep,
        flags,
    )
    grad_mixer = jnp.einsum("td,tk->dk", normed_one, grad_pre, preferred_element_type=F32)
    back_one = jnp.einsum("tk,dk->td", grad_pre, mixer_full, preferred_element_type=F32)
    input_rows, grad_norm_one, share_gate, share_up, share_down = input_line(
        mesh_axes, 3, back_one.astype(BF16), hidden_rows, grad_residual, gain_one, grads_ffn
    )
    grad_norm_one, grad_norm_two, head_total = lax.psum(
        (grad_norm_one.reshape(-1), grad_norm_two.reshape(-1), grad_head_part.reshape(-1)),
        "tensor",
    )

    def share(values, dim):
        return lax.psum_scatter(
            values.astype(BF16), both, scatter_dimension=dim, tiled=True
        ).astype(F32)

    share_mixer = share(grad_mixer, 0)
    return (
        output_rows.reshape(hidden.shape),
        input_rows.reshape(hidden.shape),
        share(grad_norm_one, 0),
        share_mixer[:, :width],
        share_mixer[:, width : 2 * width],
        share_mixer[:, 2 * width : 3 * width],
        share_mixer[:, 3 * width :],
        share(grad_floor_part.reshape(head_count, key_dim), 1),
        share(head_total, 0),
        share(grad_out, 1),
        share(grad_norm_two, 0),
        share_gate,
        share_up,
        share_down.T,
    )


def solution(mesh):
    in_specs = (
        P("shard", "context", None),
        P("shard", "context"),
        P(),
        P(("shard", "context"), "tensor"),
        P(("shard", "context"), "tensor"),
        P(("shard", "context"), "tensor"),
        P(("shard", "context"), "tensor"),
        P("tensor", None),
        P(),
        P("tensor", ("shard", "context")),
        P(),
        P(("shard", "context"), "tensor"),
        P(("shard", "context"), "tensor"),
        P("tensor", ("shard", "context")),
        P("shard", "context", None),
    )
    out_specs = (
        P("shard", "context", None),
        P("shard", "context", None),
        P(("shard", "context")),
        P(("shard", "context"), "tensor"),
        P(("shard", "context"), "tensor"),
        P(("shard", "context"), "tensor"),
        P(("shard", "context"), "tensor"),
        P("tensor", ("shard", "context")),
        P(("shard", "context")),
        P("tensor", ("shard", "context")),
        P(("shard", "context")),
        P(("shard", "context"), "tensor"),
        P(("shard", "context"), "tensor"),
        P("tensor", ("shard", "context")),
    )
    return jax.shard_map(
        partial(local, mesh.axis_names), mesh=mesh, in_specs=in_specs, out_specs=out_specs, check_vma=False)
```

```python
from functools import partial

import jax
import jax.numpy as jnp
from jax import lax
from jax.experimental import pallas as pl
from jax.experimental.pallas import tpu as pltpu
from jax.sharding import PartitionSpec as P

EPSILON = 1e-05


BLOCK = 128
F32 = jnp.float32
BF16 = jnp.bfloat16


def mm(a, b, dims):
    return lax.dot_general(a, b, (dims, ((), ())), preferred_element_type=F32)


def mm_nn(a, b):
    return mm(a, b, ((1,), (0,)))


def mm_nt(a, b):
    return mm(a, b, ((1,), (1,)))


def mm_tn(a, b):
    return mm(a, b, ((0,), (0,)))


def split_sum(tri, values):
    high = values.astype(BF16)
    low = (values - high.astype(F32)).astype(BF16)
    return mm_nn(tri, high) + mm_nn(tri, low)


def block_masks(counts, flags_row):
    rows = counts.shape[0]
    row_ids = lax.broadcasted_iota(jnp.int32, (rows, rows), 0)
    col_ids = lax.broadcasted_iota(jnp.int32, (rows, rows), 1)
    linked = jnp.logical_and(counts == flags_row[0:1], row_ids >= col_ids)
    fresh = (counts == flags_row[1:2, 0:1]).astype(F32)
    tail = (counts == flags_row[2:3, 0:1]).astype(F32)
    closing = (flags_row[1:2, 0:1] == flags_row[2:3, 0:1]).astype(F32)
    return row_ids, col_ids, linked, fresh, tail, closing


def mixer_forward_kernel(
    head_count,
    key_scale,
    pre_ref,
    open_ref,
    count_ref,
    keep_ref,
    flags_ref,
    mixed_ref,
    lead_ref,
    start_ref,
    run_ref,
    end_ref,
    total_ref,
    state_scr,
    run_scr,
):
    step = pl.program_id(0)
    width = open_ref.shape[1]
    lanes = width // head_count

    @pl.when(step == 0)
    def _():
        state_scr[...] = jnp.zeros_like(state_scr)
        run_scr[...] = jnp.zeros_like(run_scr)

    counts, keep = count_ref[...], keep_ref[...]
    row_ids, col_ids, linked, fresh, tail, closing = block_masks(counts, flags_ref[0])
    tri = (row_ids >= col_ids).astype(BF16)
    query_pre = pre_ref[:, :width]
    values = pre_ref[:, 2 * width : 3 * width].astype(BF16)
    keys = open_ref[...] * jax.nn.sigmoid(-pre_ref[:, width : 2 * width])
    cum = split_sum(tri, jnp.log1p(-keys))
    rows = cum.shape[0]
    ending = cum[rows - 1 : rows, :]
    lifted = query_pre * jax.nn.sigmoid(query_pre) * jnp.exp(cum)
    lowered = (keys * jnp.exp(-cum) * keep).astype(BF16)
    moved = (keys * jnp.exp(ending - cum) * (keep * tail)).astype(BF16)
    run = run_scr[...]
    lead_ref[...] = (lifted * jnp.exp(run) * (counts == 0).astype(F32)).astype(BF16)
    run_ref[0] = run
    run_scr[...] = run + ending
    total_ref[...] = run + ending
    fresh_lifted = (lifted * fresh).astype(BF16)
    lifted = lifted.astype(BF16)
    end_decay = jnp.exp(ending) * closing
    for head in range(head_count):
        part = slice(head * lanes, (head + 1) * lanes)
        state = state_scr[head]
        start_ref[0, head] = state
        scores = jnp.where(linked, mm_nt(lifted[:, part], lowered[:, part]), 0.0)
        results = mm_nn(scores.astype(BF16), values[:, part])
        results = results + mm_nt(fresh_lifted[:, part], state.astype(BF16))
        mixed_ref[:, part] = results * (key_scale * keep)
        state = state * end_decay[:, part] + mm_tn(values[:, part], moved[:, part])
        state_scr[head] = state
        end_ref[head] = state


def mixer_forward(pre, open_part, counts, keep, flags, head_count, key_scale):
    tokens, all_width = pre.shape
    width = open_part.shape[1]
    lanes = width // head_count
    blocks = tokens // BLOCK
    return pl.pallas_call(
        partial(mixer_forward_kernel, head_count, key_scale),
        grid=(blocks,),
        in_specs=[
            pl.BlockSpec((BLOCK, all_width), lambda i: (i, 0)),
            pl.BlockSpec((1, width), lambda i: (0, 0)),
            pl.BlockSpec((BLOCK, 1), lambda i: (i, 0)),
            pl.BlockSpec((BLOCK, 1), lambda i: (i, 0)),
            pl.BlockSpec((1, 8, BLOCK), lambda i: (i, 0, 0)),
        ],
        out_specs=[
            pl.BlockSpec((BLOCK, width), lambda i: (i, 0)),
            pl.BlockSpec((BLOCK, width), lambda i: (i, 0)),
            pl.BlockSpec((1, head_count, lanes, lanes), lambda i: (i, 0, 0, 0)),
            pl.BlockSpec((1, 1, width), lambda i: (i, 0, 0)),
            pl.BlockSpec((head_count, lanes, lanes), lambda i: (0, 0, 0)),
            pl.BlockSpec((1, width), lambda i: (0, 0)),
        ],
        out_shape=[
            jax.ShapeDtypeStruct((tokens, width), F32),
            jax.ShapeDtypeStruct((tokens, width), BF16),
            jax.ShapeDtypeStruct((blocks, head_count, lanes, lanes), F32),
            jax.ShapeDtypeStruct((blocks, 1, width), F32),
            jax.ShapeDtypeStruct((head_count, lanes, lanes), F32),
            jax.ShapeDtypeStruct((1, width), F32),
        ],
        scratch_shapes=[
            pltpu.VMEM((head_count, lanes, lanes), F32),
            pltpu.VMEM((1, width), F32),
        ],
        compiler_params=pltpu.CompilerParams(
            dimension_semantics=("arbitrary",), vmem_limit_bytes=40 << 20
        ),
        cost_estimate=pl.CostEstimate(
            flops=tokens * width * BLOCK * 12,
            bytes_accessed=tokens * width * 30,
            transcendentals=tokens * width * 7,
        ),
        name="mixer_forward",
    )(pre, open_part, counts, keep, flags)


def gate_forward_kernel(
    head_count,
    key_scale,
    local_ref,
    lead_ref,
    carry_ref,
    gate_ref,
    gain_ref,
    keep_ref,
    mixed_ref,
    gated_ref,
):
    lanes = gain_ref.shape[1]
    for head in range(head_count):
        part = slice(head * lanes, (head + 1) * lanes)
        carried = mm_nt(lead_ref[:, part], carry_ref[head])
        mixed = local_ref[:, part] + carried * (key_scale * keep_ref[...])
        mixed_ref[:, part] = mixed
        inverse = lax.rsqrt(jnp.mean(mixed * mixed, axis=-1, keepdims=True) + EPSILON)
        gate = gate_ref[:, part]
        gated = mixed * inverse * gain_ref[...] * (gate * jax.nn.sigmoid(gate))
        gated_ref[:, part] = gated.astype(BF16)


def gate_forward(local, lead, carry, pre, gain, keep, key_scale):
    tokens, width = local.shape
    head_count, lanes = carry.shape[0], carry.shape[2]
    rows = 2 * BLOCK
    return pl.pallas_call(
        partial(gate_forward_kernel, head_count, key_scale),
        grid=(tokens // rows,),
        in_specs=[
            pl.BlockSpec((rows, width), lambda i: (i, 0)),
            pl.BlockSpec((rows, width), lambda i: (i, 0)),
            pl.BlockSpec((head_count, lanes, lanes), lambda i: (0, 0, 0)),
            pl.BlockSpec((rows, width), lambda i: (i, 3)),
            pl.BlockSpec((1, lanes), lambda i: (0, 0)),
            pl.BlockSpec((rows, 1), lambda i: (i, 0)),
        ],
        out_specs=[
            pl.BlockSpec((rows, width), lambda i: (i, 0)),
            pl.BlockSpec((rows, width), lambda i: (i, 0)),
        ],
        out_shape=[
            jax.ShapeDtypeStruct((tokens, width), F32),
            jax.ShapeDtypeStruct((tokens, width), BF16),
        ],
        compiler_params=pltpu.CompilerParams(
            dimension_semantics=("arbitrary",), vmem_limit_bytes=40 << 20
        ),
        cost_estimate=pl.CostEstimate(
            flops=tokens * width * 300,
            bytes_accessed=tokens * width * 16,
            transcendentals=tokens * width,
        ),
        name="gate_forward",
    )(local, lead, carry, pre, gain, keep)


def gate_backward_kernel(
    head_count,
    key_scale,
    grad_ref,
    mixed_ref,
    lead_ref,
    gate_ref,
    gain_ref,
    keep_ref,
    grad_mixed_ref,
    grad_gate_ref,
    grad_gain_ref,
    back_ref,
):
    lanes = gain_ref.shape[1]

    @pl.when(pl.program_id(0) == 0)
    def _():
        grad_gain_ref[...] = jnp.zeros_like(grad_gain_ref)
        back_ref[...] = jnp.zeros_like(back_ref)

    gain = gain_ref[...]
    total = jnp.zeros_like(gain)
    for head in range(head_count):
        part = slice(head * lanes, (head + 1) * lanes)
        mixed, gate, grad = mixed_ref[:, part], gate_ref[:, part], grad_ref[:, part]
        inverse = lax.rsqrt(jnp.mean(mixed * mixed, axis=-1, keepdims=True) + EPSILON)
        unit = mixed * inverse
        sigma = jax.nn.sigmoid(gate)
        scaled = grad * unit
        total = total + jnp.sum(scaled * (gate * sigma), axis=0, keepdims=True)
        grad_gate = scaled * gain * sigma * (1.0 + gate * (1.0 - sigma))
        grad_gate_ref[:, part] = grad_gate.astype(BF16)
        lifted = grad * gain * (gate * sigma)
        mean = jnp.mean(lifted * unit, axis=-1, keepdims=True)
        grad_mixed = inverse * (lifted - unit * mean) * (key_scale * keep_ref[...])
        grad_mixed = grad_mixed.astype(BF16)
        grad_mixed_ref[:, part] = grad_mixed
        back_ref[head] += mm_tn(grad_mixed, lead_ref[:, part])
    grad_gain_ref[...] += total


def gate_backward(grad, mixed, lead, pre, gain, keep, head_count, key_scale):
    tokens, width = mixed.shape
    lanes = gain.shape[1]
    rows = 2 * BLOCK
    return pl.pallas_call(
        partial(gate_backward_kernel, head_count, key_scale),
        grid=(tokens // rows,),
        in_specs=[
            pl.BlockSpec((rows, width), lambda i: (i, 0)),
            pl.BlockSpec((rows, width), lambda i: (i, 0)),
            pl.BlockSpec((rows, width), lambda i: (i, 0)),
            pl.BlockSpec((rows, width), lambda i: (i, 3)),
            pl.BlockSpec((1, lanes), lambda i: (0, 0)),
            pl.BlockSpec((rows, 1), lambda i: (i, 0)),
        ],
        out_specs=[
            pl.BlockSpec((rows, width), lambda i: (i, 0)),
            pl.BlockSpec((rows, width), lambda i: (i, 0)),
            pl.BlockSpec((1, lanes), lambda i: (0, 0)),
            pl.BlockSpec((head_count, lanes, lanes), lambda i: (0, 0, 0)),
        ],
        out_shape=[
            jax.ShapeDtypeStruct((tokens, width), BF16),
            jax.ShapeDtypeStruct((tokens, width), BF16),
            jax.ShapeDtypeStruct((1, lanes), F32),
            jax.ShapeDtypeStruct((head_count, lanes, lanes), F32),
        ],
        compiler_params=pltpu.CompilerParams(
            dimension_semantics=("arbitrary",), vmem_limit_bytes=40 << 20
        ),
        cost_estimate=pl.CostEstimate(
            flops=tokens * width * 300,
            bytes_accessed=tokens * width * 18,
            transcendentals=tokens * width,
        ),
        name="gate_backward",
    )(grad, mixed, lead, pre, gain, keep)


def mixer_backward_kernel(
    head_count,
    pre_ref,
    grad_mixed_ref,
    grad_gate_ref,
    start_ref,
    run_ref,
    carry_ref,
    after_ref,
    open_ref,
    count_ref,
    keep_ref,
    flags_ref,
    grads_ref,
    floor_ref,
    grad_scr,
    lifted_scr,
    lowered_scr,
    moved_scr,
    value_scr,
):
    width = open_ref.shape[1]
    lanes = width // head_count

    @pl.when(pl.program_id(0) == 0)
    def _():
        grad_scr[...] = after_ref[...]
        floor_ref[...] = jnp.zeros_like(floor_ref)

    counts, keep = count_ref[...], keep_ref[...]
    flags = flags_ref[0]
    row_ids, col_ids, linked, fresh, tail, closing = block_masks(counts, flags)
    tri = (row_ids >= col_ids).astype(BF16)
    tri_back = (row_ids <= col_ids).astype(BF16)
    query_pre = pre_ref[:, :width]
    values = pre_ref[:, 2 * width : 3 * width].astype(BF16)
    opened = open_ref[...]
    closed = jax.nn.sigmoid(-pre_ref[:, width : 2 * width])
    keys = opened * closed
    cum = split_sum(tri, jnp.log1p(-keys))
    rows = cum.shape[0]
    ending = cum[rows - 1 : rows, :]
    rise, fall = jnp.exp(cum), jnp.exp(-cum) * keep
    shift = jnp.exp(ending - cum) * (keep * tail)
    sigma_query = jax.nn.sigmoid(query_pre)
    lifted = (query_pre * sigma_query * rise).astype(BF16)
    lowered = (keys * fall).astype(BF16)
    moved = (keys * shift).astype(BF16)
    fresh_lifted = (lifted.astype(F32) * fresh).astype(BF16)
    end_decay = jnp.exp(ending) * closing
    lead_in = jnp.exp(run_ref[0]) * (flags[1:2, 0:1] == 0).astype(F32)
    for head in range(head_count):
        part = slice(head * lanes, (head + 1) * lanes)
        grad_out, value = grad_mixed_ref[:, part], values[:, part]
        lift, lower, move = lifted[:, part], lowered[:, part], moved[:, part]
        scores = jnp.where(linked, mm_nt(lift, lower), 0.0).astype(BF16)
        pulls = jnp.where(linked, mm_nt(grad_out, value), 0.0).astype(BF16)
        state = start_ref[0, head] + lead_in[:, part] * carry_ref[head]
        grad_state = grad_scr[head]
        grad_low = grad_state.astype(BF16)
        lifted_scr[:, part] = mm_nn(pulls, lower) + fresh * mm_nn(grad_out, state.astype(BF16))
        lowered_scr[:, part] = mm_tn(pulls, lift)
        grad_moved = mm_nn(value, grad_low)
        moved_scr[:, part] = grad_moved
        grads_ref[:, 2 * width + head * lanes : 2 * width + (head + 1) * lanes] = (
            mm_tn(scores, grad_out) + mm_nt(move, grad_low)
        ).astype(BF16)
        value_scr[:, part] = jnp.sum(
            grad_moved * move.astype(F32), axis=0, keepdims=True
        ) + end_decay[:, part] * jnp.sum(state * grad_state, axis=0, keepdims=True)
        grad_scr[head] = grad_state * end_decay[:, part] + mm_tn(grad_out, fresh_lifted[:, part])
    grad_lifted, grad_lowered, grad_moved = lifted_scr[...], lowered_scr[...], moved_scr[...]
    grad_cum = (
        grad_lifted * lifted.astype(F32)
        - grad_lowered * lowered.astype(F32)
        - grad_moved * moved.astype(F32)
    )
    grad_decay = split_sum(tri_back, grad_cum) + value_scr[...]
    key_total = grad_lowered * fall + grad_moved * shift - grad_decay / (1.0 - keys)
    floor_ref[...] -= jnp.sum(key_total * closed, axis=0, keepdims=True)
    grads_ref[:, :width] = (
        grad_lifted * rise * sigma_query * (1.0 + query_pre * (1.0 - sigma_query))
    ).astype(BF16)
    grads_ref[:, width : 2 * width] = (-key_total * opened * closed * (1.0 - closed)).astype(BF16)
    grads_ref[:, 3 * width :] = grad_gate_ref[...]


def mixer_backward(
    pre, grad_mixed, grad_gate, starts, runs, carry, after, open_part, counts, keep, flags
):
    tokens, all_width = pre.shape
    width = open_part.shape[1]
    head_count, lanes = carry.shape[0], carry.shape[2]
    blocks = tokens // BLOCK
    last = blocks - 1
    return pl.pallas_call(
        partial(mixer_backward_kernel, head_count),
        grid=(blocks,),
        in_specs=[
            pl.BlockSpec((BLOCK, all_width), lambda i: (last - i, 0)),
            pl.BlockSpec((BLOCK, width), lambda i: (last - i, 0)),
            pl.BlockSpec((BLOCK, width), lambda i: (last - i, 0)),
            pl.BlockSpec((1, head_count, lanes, lanes), lambda i: (last - i, 0, 0, 0)),
            pl.BlockSpec((1, 1, width), lambda i: (last - i, 0, 0)),
            pl.BlockSpec((head_count, lanes, lanes), lambda i: (0, 0, 0)),
            pl.BlockSpec((head_count, lanes, lanes), lambda i: (0, 0, 0)),
            pl.BlockSpec((1, width), lambda i: (0, 0)),
            pl.BlockSpec((BLOCK, 1), lambda i: (last - i, 0)),
            pl.BlockSpec((BLOCK, 1), lambda i: (last - i, 0)),
            pl.BlockSpec((1, 8, BLOCK), lambda i: (last - i, 0, 0)),
        ],
        out_specs=[
            pl.BlockSpec((BLOCK, all_width), lambda i: (last - i, 0)),
            pl.BlockSpec((1, width), lambda i: (0, 0)),
        ],
        out_shape=[
            jax.ShapeDtypeStruct((tokens, all_width), BF16),
            jax.ShapeDtypeStruct((1, width), F32),
        ],
        scratch_shapes=[
            pltpu.VMEM((head_count, lanes, lanes), F32),
            pltpu.VMEM((BLOCK, width), F32),
            pltpu.VMEM((BLOCK, width), F32),
            pltpu.VMEM((BLOCK, width), F32),
            pltpu.VMEM((1, width), F32),
        ],
        compiler_params=pltpu.CompilerParams(
            dimension_semantics=("arbitrary",), vmem_limit_bytes=40 << 20
        ),
        cost_estimate=pl.CostEstimate(
            flops=tokens * width * BLOCK * 30,
            bytes_accessed=tokens * width * 36,
            transcendentals=tokens * width * 9,
        ),
        name="mixer_backward",
    )(pre, grad_mixed, grad_gate, starts, runs, carry, after, open_part, counts, keep, flags)


def row_flags(segment_ids):
    ids = segment_ids.reshape(-1)
    tokens = ids.shape[0]
    starts = jnp.concatenate([jnp.zeros((1,), F32), (ids[1:] != ids[:-1]).astype(F32)])
    positions = jnp.arange(tokens)
    counts = jnp.sum(
        jnp.where(positions[None, :] <= positions[:, None], starts[None, :], 0.0), axis=1
    )
    keep = (ids > 0).astype(F32)
    blocks = tokens // BLOCK
    by_block = counts.reshape(blocks, BLOCK)
    lasts = by_block[:, -1]
    before = jnp.concatenate([jnp.zeros((1,), F32), lasts[:-1]])
    wide = (blocks, BLOCK)
    flags = jnp.stack(
        [by_block, jnp.broadcast_to(before[:, None], wide), jnp.broadcast_to(lasts[:, None], wide)]
        + [jnp.zeros(wide, F32)] * 5,
        axis=1,
    )
    return counts[:, None], keep[:, None], flags, lasts[-1]


def from_earlier(values, axis, shift):
    count = lax.axis_size(axis)
    return lax.ppermute(values, axis, [(i, i + shift) for i in range(count - shift)])


def from_later(values, axis, shift):
    count = lax.axis_size(axis)
    return lax.ppermute(values, axis, [(i + shift, i) for i in range(count - shift)])


def state_before(state, decay, first_id, last_id, axis):
    head_count, lanes, _ = state.shape
    ids = jnp.stack([first_id, last_id, jnp.float32(1.0)] + [jnp.float32(0.0)] * 5)
    message = jnp.concatenate(
        [
            state.reshape(head_count * lanes, lanes),
            decay.reshape(head_count, lanes),
            jnp.broadcast_to(ids[:, None], (8, lanes)),
        ]
    )
    rows = head_count * lanes
    total = jnp.zeros_like(state)
    factor = jnp.ones((head_count, 1, lanes), F32)
    follower = first_id
    link_in = jnp.float32(0.0)
    for shift in range(1, lax.axis_size(axis)):
        got = from_earlier(message, axis, shift)
        got_ids = got[rows + head_count :, 0]
        linked = (got_ids[1] == follower).astype(F32) * got_ids[2]
        if shift == 1:
            link_in = linked
        factor = factor * linked
        total = total + factor * got[:rows].reshape(state.shape)
        factor = factor * got[rows : rows + head_count].reshape(head_count, 1, lanes)
        follower = got_ids[0]
    return total, link_in


def grad_after(back, decay, link_in, axis):
    head_count, lanes, _ = back.shape
    rows = head_count * lanes
    message = (
        jnp.concatenate([back.reshape(rows, lanes), decay.reshape(head_count, lanes)]) * link_in
    )
    message = jnp.pad(message, ((0, 8 - head_count % 8 if head_count % 8 else 0), (0, 0)))
    total = jnp.zeros_like(back)
    factor = jnp.ones((head_count, 1, lanes), F32)
    for shift in range(1, lax.axis_size(axis)):
        got = from_later(message, axis, shift)
        total = total + factor * got[:rows].reshape(back.shape)
        factor = factor * got[rows : rows + head_count].reshape(head_count, 1, lanes)
    return total


CHUNK = 32
LAG = 2
MESH_ID = pl.DeviceIdType.MESH


class Line:
    def __init__(self, mesh_axes, part, arrived, out, sems, transform):
        self.mesh_axes = mesh_axes
        self.part, self.arrived, self.out = part, arrived, out
        self.sum_send, self.sum_recv, self.back_send, self.back_recv = sems
        self.transform = transform
        self.half = part.shape[0] // 2
        self.chunks = self.half // CHUNK
        self.size = lax.axis_size("tensor")
        self.place = lax.axis_index("tensor")
        self.lines = ((self.size - 1 - self.place, -1), (self.place, 1))
        self.steps = self.chunks + 2 * LAG * (self.size - 1)

    def device(self, position):
        return tuple(
            jnp.clip(position, 0, self.size - 1) if axis == "tensor" else lax.axis_index(axis)
            for axis in self.mesh_axes
        )

    def greet(self, barrier):
        for step in (-1, 1):
            inside = jnp.logical_and(self.place + step >= 0, self.place + step < self.size)

            @pl.when(inside)
            def _(step=step):
                pl.semaphore_signal(
                    barrier, inc=1, device_id=self.device(self.place + step), device_id_type=MESH_ID
                )

        at_end = jnp.logical_or(self.place == 0, self.place == self.size - 1)
        return jnp.where(at_end, 1, 2)

    def rows_of(self, side, index):
        return pl.ds(pl.multiple_of(side * self.half + index * CHUNK, CHUNK), CHUNK)

    def sum_copy(self, side, index, source):
        rows = self.rows_of(side, index)
        return pltpu.make_async_remote_copy(
            source.at[rows],
            self.arrived.at[rows],
            self.sum_send.at[side, index],
            self.sum_recv.at[side, index],
            device_id=self.device(self.place + self.lines[side][1]),
            device_id_type=MESH_ID,
        )

    def back_copy(self, side, index):
        rows = self.rows_of(side, index)
        return pltpu.make_async_remote_copy(
            self.out.at[rows],
            self.out.at[rows],
            self.back_send.at[side, index],
            self.back_recv.at[side, index],
            device_id=self.device(self.place - self.lines[side][1]),
            device_id_type=MESH_ID,
        )

    def step(self, time):
        for side in (0, 1):
            hops = self.lines[side][0]
            index = time - LAG * hops
            valid = jnp.logical_and(index >= 0, index < self.chunks)
            at_source, at_owner = hops == 0, hops == self.size - 1
            index = jnp.clip(index, 0, self.chunks - 1)
            rows = self.rows_of(side, index)

            @pl.when(jnp.logical_and(valid, at_source))
            def _(side=side, index=index):
                self.sum_copy(side, index, self.part).start()

            @pl.when(jnp.logical_and(valid, jnp.logical_not(at_source)))
            def _(side=side, index=index):
                self.sum_copy(side, index, self.arrived).wait_recv()

            between = jnp.logical_and(jnp.logical_not(at_source), jnp.logical_not(at_owner))

            @pl.when(jnp.logical_and(valid, between))
            def _(side=side, index=index, rows=rows):
                total = self.part[rows].astype(F32) + self.arrived[rows].astype(F32)
                self.arrived[rows] = total.astype(BF16)
                self.sum_copy(side, index, self.arrived).start()

            @pl.when(jnp.logical_and(valid, at_owner))
            def _(side=side, index=index, rows=rows):
                total = self.part[rows].astype(F32) + self.arrived[rows].astype(F32)
                own = pl.ds(pl.multiple_of(index * CHUNK, CHUNK), CHUNK)
                self.transform(total, rows, own)
                self.back_copy(side, index).start()

            away = self.size - 1 - hops
            index = time - LAG * (self.size - 1 + away)
            valid = jnp.logical_and(jnp.logical_and(index >= 0, index < self.chunks), away > 0)
            index = jnp.clip(index, 0, self.chunks - 1)

            @pl.when(valid)
            def _(side=side, index=index):
                self.back_copy(side, index).wait_recv()

            @pl.when(jnp.logical_and(valid, away < self.size - 1))
            def _(side=side, index=index):
                self.back_copy(side, index).start()

    def run(self, first, last, beside=None):
        def body(time, _):
            self.step(time)
            if beside is not None:
                beside(time)
            return 0

        lax.fori_loop(first, last, body, 0)

    def finish(self):
        def body(index, _):
            for side in (0, 1):
                hops = self.lines[side][0]

                @pl.when(hops < self.size - 1)
                def _(side=side):
                    self.sum_copy(side, index, self.arrived).wait_send()

                @pl.when(hops > 0)
                def _(side=side):
                    self.back_copy(side, index).wait_send()

            return 0

        lax.fori_loop(0, self.chunks, body, 0)


def line_sems(tokens):
    return [pltpu.SemaphoreType.DMA((2, tokens // 2 // CHUNK))] * 4


def line_exchange_kernel(transform, mesh_axes, n_in, n_out, *refs):
    part, extra_in = refs[0], refs[1 : 1 + n_in]
    out, extra_out = refs[1 + n_in], refs[2 + n_in : 2 + n_in + n_out]
    arrived, *sems = refs[2 + n_in + n_out :]
    def turn(total, rows, own):
        transform(total, rows, own, extra_in, out, extra_out)

    line = Line(mesh_axes, part, arrived, out, sems, turn)
    barrier = pltpu.get_barrier_semaphore()
    pl.semaphore_wait(barrier, line.greet(barrier))
    line.run(0, line.steps)
    line.finish()


def line_exchange(transform, mesh_axes, collective, part, extras, extra_shapes, name):
    tokens, width = part.shape
    whole = pl.BlockSpec(memory_space=pltpu.VMEM)
    return pl.pallas_call(
        partial(line_exchange_kernel, transform, mesh_axes, len(extras), len(extra_shapes)),
        in_specs=[whole] * (1 + len(extras)),
        out_specs=[whole] * (1 + len(extra_shapes)),
        out_shape=[jax.ShapeDtypeStruct((tokens, width), BF16)] + list(extra_shapes),
        scratch_shapes=[pltpu.VMEM((tokens, width), BF16)] + line_sems(tokens),
        compiler_params=pltpu.CompilerParams(
            collective_id=collective, has_side_effects=True, vmem_limit_bytes=52 << 20
        ),
        cost_estimate=pl.CostEstimate(
            flops=tokens * width * 8, bytes_accessed=360_000_000, transcendentals=0
        ),
        name=name,
    )(part, *extras)


def inverse_rms(values):
    return lax.rsqrt(jnp.mean(values * values, axis=-1, keepdims=True) + EPSILON)


def residual_norm(total, rows, own, extra_in, out, extra_out):
    hidden, gain = extra_in
    residual = hidden[rows].astype(F32) + total
    extra_out[0][own] = residual
    out[rows] = (residual * inverse_rms(residual) * gain[...]).astype(BF16)


GROUP = 128
TILE = 256


def feed_kernel(
    mesh_axes,
    normed_ref,
    cotangent_ref,
    residual_hbm,
    gain_ref,
    gate_hbm,
    up_hbm,
    down_hbm,
    out_ref,
    gain_grad,
    hidden_hbm,
    grad_gate_hbm,
    grad_up_hbm,
    feed_hbm,
    grad_hbm,
    gate_w,
    up_w,
    down_w,
    part,
    arrived,
    residual,
    stage_hidden,
    stage_gate,
    stage_up,
    stage_feed,
    weight_sem,
    residual_sem,
    stage_sem,
    grad_sem,
    *sems,
):
    tokens, model_width = normed_ref.shape
    half = tokens // 2
    hidden_width = gate_hbm.shape[1]
    padded = gate_w.shape[1]
    groups = half // GROUP
    loads = [
        pltpu.make_async_copy(gate_hbm, gate_w.at[:, pl.ds(0, hidden_width)], weight_sem.at[0]),
        pltpu.make_async_copy(up_hbm, up_w.at[:, pl.ds(0, hidden_width)], weight_sem.at[1]),
        pltpu.make_async_copy(down_hbm, down_w.at[pl.ds(0, hidden_width)], weight_sem.at[2]),
    ]
    for load in loads:
        load.start()
    residual_load = pltpu.make_async_copy(residual_hbm, residual, residual_sem.at[0])
    residual_load.start()
    if padded > hidden_width:
        spare = slice(hidden_width, padded)
        gate_w[:, spare] = jnp.zeros((model_width, padded - hidden_width), BF16)
        up_w[:, spare] = jnp.zeros((model_width, padded - hidden_width), BF16)
        down_w[spare, :] = jnp.zeros((padded - hidden_width, model_width), BF16)
    gain_grad[...] = jnp.zeros_like(gain_grad)

    def turn(total, rows, own):
        values = residual[own]
        inverse = inverse_rms(values)
        unit = values * inverse
        gain_grad[...] += jnp.sum(total * unit, axis=0, keepdims=True)
        lifted = total * gain_ref[...]
        mean = jnp.mean(lifted * unit, axis=-1, keepdims=True)
        grad = cotangent_ref[rows].astype(F32) + inverse * (lifted - unit * mean)
        residual[own] = grad
        out_ref[rows] = grad.astype(BF16)

    line = Line(mesh_axes, part, arrived, out_ref, sems, turn)
    barrier = pltpu.get_barrier_semaphore()
    pl.semaphore_wait(barrier, line.greet(barrier))
    residual_load.wait()
    for load in loads:
        load.wait()

    def both(ref, group):
        first = pl.ds(pl.multiple_of(group * GROUP, GROUP), GROUP)
        second = pl.ds(pl.multiple_of(half + group * GROUP, GROUP), GROUP)
        return first, second

    def stage_copies(group):
        slot = lax.rem(group, 2)
        copies = []
        for side, rows in enumerate(both(None, group)):
            from_rows = pl.ds(side * GROUP, GROUP)
            columns = pl.ds(0, hidden_width)
            for which, (stage, target) in enumerate(
                (
                    (stage_hidden, hidden_hbm),
                    (stage_gate, grad_gate_hbm),
                    (stage_up, grad_up_hbm),
                )
            ):
                copies.append(
                    pltpu.make_async_copy(
                        stage.at[slot, from_rows, columns],
                        target.at[rows],
                        stage_sem.at[slot, which, side],
                    )
                )
            copies.append(
                pltpu.make_async_copy(
                    stage_feed.at[slot, from_rows], feed_hbm.at[rows], stage_sem.at[slot, 3, side]
                )
            )
        return copies

    def hidden_tile(group, tile):
        first, second = both(normed_ref, group)
        slot = lax.rem(group, 2)
        columns = pl.ds(pl.multiple_of(tile * TILE, TILE), TILE)
        rows = jnp.concatenate([normed_ref[first], normed_ref[second]], axis=0)
        gate = mm_nn(rows, gate_w[:, columns])
        up = mm_nn(rows, up_w[:, columns])
        grads = jnp.concatenate([cotangent_ref[first], cotangent_ref[second]], axis=0)
        grad = mm_nt(grads, down_w[columns, :])
        sigma = jax.nn.sigmoid(gate)
        active = gate * sigma
        stage_hidden[slot, :, columns] = (active * up).astype(BF16)
        stage_gate[slot, :, columns] = (grad * up * sigma * (1.0 + gate * (1.0 - sigma))).astype(
            BF16
        )
        stage_up[slot, :, columns] = (grad * active).astype(BF16)

    def model_tile(group, tile):
        first, second = both(part, group)
        slot = lax.rem(group, 2)
        columns = pl.ds(pl.multiple_of(tile * TILE, TILE), TILE)
        back = mm_nt(stage_gate[slot], gate_w[columns, :])
        back = (back + mm_nt(stage_up[slot], up_w[columns, :])).astype(BF16)
        part[first, columns] = back[:GROUP]
        part[second, columns] = back[GROUP:]
        stage_feed[slot, :, columns] = mm_nn(stage_hidden[slot], down_w[:, columns]).astype(BF16)

    hidden_tiles, model_tiles = padded // TILE, model_width // TILE
    ticks = hidden_tiles + model_tiles
    pace = GROUP // CHUNK
    piece = -(-ticks // pace)

    def group_body(group, _):
        @pl.when(group >= 2)
        def _():
            for copy in stage_copies(group - 2):
                copy.wait()

        def piece_body(index, _):
            def tick_body(offset, _):
                tick = index * piece + offset

                @pl.when(tick < hidden_tiles)
                def _():
                    hidden_tile(group, tick)

                @pl.when(jnp.logical_and(tick >= hidden_tiles, tick < ticks))
                def _():
                    model_tile(group, tick - hidden_tiles)

                return 0

            lax.fori_loop(0, piece, tick_body, 0)

            @pl.when(group >= 1)
            def _():
                line.step((group - 1) * pace + index)

            return 0

        lax.fori_loop(0, pace, piece_body, 0)
        for copy in stage_copies(group):
            copy.start()
        return 0

    lax.fori_loop(0, groups, group_body, 0)
    line.run((groups - 1) * pace, line.steps)
    save = pltpu.make_async_copy(residual, grad_hbm, grad_sem.at[0])
    save.start()
    for group in range(max(groups - 2, 0), groups):
        for copy in stage_copies(group):
            copy.wait()
    line.finish()
    save.wait()


def feed_line(mesh_axes, collective, normed, cotangent, residual, gain, gate_w, up_w, down_w):
    tokens, model_width = normed.shape
    hidden_width = gate_w.shape[1]
    padded = -(-hidden_width // TILE) * TILE
    whole = pl.BlockSpec(memory_space=pltpu.VMEM)
    remote = pl.BlockSpec(memory_space=pl.ANY)
    group_rows = 2 * GROUP
    return pl.pallas_call(
        partial(feed_kernel, mesh_axes),
        in_specs=[whole, whole, remote, whole, remote, remote, remote],
        out_specs=[whole, whole] + [remote] * 5,
        out_shape=[
            jax.ShapeDtypeStruct((tokens, model_width), BF16),
            jax.ShapeDtypeStruct((1, model_width), F32),
            jax.ShapeDtypeStruct((tokens, hidden_width), BF16),
            jax.ShapeDtypeStruct((tokens, hidden_width), BF16),
            jax.ShapeDtypeStruct((tokens, hidden_width), BF16),
            jax.ShapeDtypeStruct((tokens, model_width), BF16),
            jax.ShapeDtypeStruct((tokens // 2, model_width), F32),
        ],
        scratch_shapes=[
            pltpu.VMEM((model_width, padded), BF16),
            pltpu.VMEM((model_width, padded), BF16),
            pltpu.VMEM((padded, model_width), BF16),
            pltpu.VMEM((tokens, model_width), BF16),
            pltpu.VMEM((tokens, model_width), BF16),
            pltpu.VMEM((tokens // 2, model_width), F32),
            pltpu.VMEM((2, group_rows, padded), BF16),
            pltpu.VMEM((2, group_rows, padded), BF16),
            pltpu.VMEM((2, group_rows, padded), BF16),
            pltpu.VMEM((2, group_rows, model_width), BF16),
            pltpu.SemaphoreType.DMA((3,)),
            pltpu.SemaphoreType.DMA((1,)),
            pltpu.SemaphoreType.DMA((2, 4, 2)),
            pltpu.SemaphoreType.DMA((1,)),
        ]
        + line_sems(tokens),
        compiler_params=pltpu.CompilerParams(
            collective_id=collective, has_side_effects=True, vmem_limit_bytes=58 << 20
        ),
        cost_estimate=pl.CostEstimate(
            flops=tokens * model_width * hidden_width * 12,
            bytes_accessed=360_000_000,
            transcendentals=tokens * hidden_width,
        ),
        name="feed_and_norm_two_line",
    )(normed, cotangent, residual, gain, gate_w, up_w, down_w)


def output_kernel(
    mesh_axes,
    part,
    residual,
    normed_ref,
    cotangent_ref,
    hidden_ref,
    grad_gate_ref,
    grad_up_ref,
    out_ref,
    grads_hbm,
    arrived,
    stage,
    stage_sem,
    *sems,
):
    model_width = normed_ref.shape[1]
    tiles = model_width // TILE

    def turn(total, rows, own):
        out_ref[rows] = (residual[own] + total).astype(BF16)

    line = Line(mesh_axes, part, arrived, out_ref, sems, turn)
    barrier = pltpu.get_barrier_semaphore()
    pl.semaphore_wait(barrier, line.greet(barrier))

    def stage_copy(tile):
        rows = pl.ds(pl.multiple_of(tile * TILE, TILE), TILE)
        slot = lax.rem(tile, 2)
        return pltpu.make_async_copy(stage.at[slot], grads_hbm.at[:, rows], stage_sem.at[slot])

    def weight_tile(time):
        tile = jnp.clip(time, 0, tiles - 1)
        slot = lax.rem(tile, 2)
        columns = pl.ds(pl.multiple_of(tile * TILE, TILE), TILE)

        @pl.when(jnp.logical_and(time < tiles, time >= 2))
        def _():
            stage_copy(tile - 2).wait()

        @pl.when(time < tiles)
        def _():
            rows = normed_ref[:, columns]
            stage[slot, 0] = mm_tn(rows, grad_gate_ref[...]).astype(BF16)
            stage[slot, 1] = mm_tn(rows, grad_up_ref[...]).astype(BF16)
            stage[slot, 2] = mm_tn(cotangent_ref[:, columns], hidden_ref[...]).astype(BF16)
            stage_copy(tile).start()

    line.run(0, line.steps, weight_tile)
    for tile in range(max(tiles - 2, 0), tiles):
        stage_copy(tile).wait()
    line.finish()


def output_line(
    mesh_axes, collective, part, residual, normed, cotangent, hidden_low, grad_gate, grad_up
):
    tokens, model_width = part.shape
    hidden_width = hidden_low.shape[1]
    whole = pl.BlockSpec(memory_space=pltpu.VMEM)
    return pl.pallas_call(
        partial(output_kernel, mesh_axes),
        in_specs=[whole] * 7,
        out_specs=[whole, pl.BlockSpec(memory_space=pl.ANY)],
        out_shape=[
            jax.ShapeDtypeStruct((tokens, model_width), BF16),
            jax.ShapeDtypeStruct((3, model_width, hidden_width), BF16),
        ],
        scratch_shapes=[
            pltpu.VMEM((tokens, model_width), BF16),
            pltpu.VMEM((2, 3, TILE, hidden_width), BF16),
            pltpu.SemaphoreType.DMA((2,)),
        ]
        + line_sems(tokens),
        compiler_params=pltpu.CompilerParams(
            collective_id=collective, has_side_effects=True, vmem_limit_bytes=56 << 20
        ),
        cost_estimate=pl.CostEstimate(
            flops=tokens * model_width * hidden_width * 6,
            bytes_accessed=360_000_000,
            transcendentals=0,
        ),
        name="output_line",
    )(part, residual, normed, cotangent, hidden_low, grad_gate, grad_up)


class Plane:
    def __init__(self, mesh_axes):
        self.mesh_axes = mesh_axes
        self.context = lax.axis_size("context")
        self.per_row = self.context // 2
        self.chips = lax.axis_size("shard") * self.per_row
        context_place = lax.axis_index("context")
        self.core = lax.rem(context_place, 2)
        self.chip = lax.axis_index("shard") * self.per_row + context_place // 2

    def device(self, chip, core):
        places = {
            "shard": chip // self.per_row,
            "context": 2 * lax.rem(chip, self.per_row) + core,
            "tensor": lax.axis_index("tensor"),
        }
        return tuple(places[axis] for axis in self.mesh_axes)

    def ahead(self, distance):
        return lax.rem(self.chip + distance, self.chips)

    def greet(self, barrier):
        targets = [self.device(self.chip, 1 - self.core)]
        targets += [self.device(self.ahead(step), self.core) for step in range(1, self.chips)]
        for target in targets:
            pl.semaphore_signal(barrier, inc=1, device_id=target, device_id_type=MESH_ID)
        return len(targets)


def input_kernel(
    mesh_axes,
    part,
    hidden_ref,
    residual_grad,
    gain_ref,
    grads_hbm,
    out_ref,
    gain_grad,
    share_gate,
    share_up,
    share_down,
    arrived,
    own,
    other,
    remote,
    load_sem,
    pair_send,
    pair_recv,
    chip_send,
    chip_recv,
    *sems,
):
    plane = Plane(mesh_axes)
    chips = plane.chips
    block = own.shape[2]
    gain_grad[...] = jnp.zeros_like(gain_grad)

    def turn(total, rows, own_rows):
        values = hidden_ref[rows].astype(F32)
        inverse = inverse_rms(values)
        unit = values * inverse
        gain_grad[...] += jnp.sum(total * unit, axis=0, keepdims=True)
        lifted = total * gain_ref[...]
        mean = jnp.mean(lifted * unit, axis=-1, keepdims=True)
        grad = residual_grad[own_rows] + inverse * (lifted - unit * mean)
        out_ref[rows] = grad.astype(BF16)

    line = Line(mesh_axes, part, arrived, out_ref, sems, turn)
    barrier = pltpu.get_barrier_semaphore()
    expected = line.greet(barrier) + plane.greet(barrier)
    pl.semaphore_wait(barrier, expected)

    def rows_of(slot, core):
        return pl.ds(pl.multiple_of((2 * plane.ahead(slot) + core) * block, block), block)

    def load(slot):
        return pltpu.make_async_copy(
            grads_hbm.at[:, rows_of(slot, plane.core)], own.at[slot], load_sem.at[slot]
        )

    def pair_copy(slot):
        return pltpu.make_async_remote_copy(
            grads_hbm.at[:, rows_of(slot, 1 - plane.core)],
            other.at[slot],
            pair_send.at[slot],
            pair_recv.at[slot],
            device_id=plane.device(plane.chip, 1 - plane.core),
            device_id_type=MESH_ID,
        )

    def chip_copy(slot):
        return pltpu.make_async_remote_copy(
            own.at[slot],
            remote.at[slot - 1],
            chip_send.at[slot - 1],
            chip_recv.at[slot - 1],
            device_id=plane.device(plane.ahead(slot), plane.core),
            device_id_type=MESH_ID,
        )

    def start(index, _):
        slot = lax.rem(index + 1, chips)
        pair_copy(slot).start()
        load(slot).start()
        return 0

    lax.fori_loop(0, chips, start, 0)
    strip = 32

    def combine(time):
        slot = lax.rem(jnp.clip(time, 0, chips - 1) + 1, chips)

        @pl.when(time < chips)
        def _():
            load(slot).wait()
            pair_copy(slot).wait_recv()

            def add(index, _):
                rows = pl.ds(pl.multiple_of(index * strip, strip), strip)
                for which in range(3):
                    total = own[slot, which, rows].astype(F32) + other[slot, which, rows].astype(F32)
                    own[slot, which, rows] = total.astype(BF16)
                return 0

            lax.fori_loop(0, block // strip, add, 0)

        @pl.when(time < chips - 1)
        def _():
            chip_copy(slot).start()

    line.run(0, line.steps, combine)

    def arrive(index, _):
        chip_copy(index).wait_recv()
        return 0

    lax.fori_loop(1, chips, arrive, 0)

    def total(index, _):
        rows = pl.ds(pl.multiple_of(index * strip, strip), strip)

        def whole(which):
            def add(slot, value):
                return value + remote[slot, which, rows].astype(F32)

            return lax.fori_loop(0, chips - 1, add, own[0, which, rows].astype(F32))

        share_gate[rows] = whole(0)
        share_up[rows] = whole(1)
        share_down[rows] = whole(2)
        return 0

    lax.fori_loop(0, block // strip, total, 0)

    def sent(index, _):
        pair_copy(index).wait_send()
        return 0

    lax.fori_loop(0, chips, sent, 0)

    def chip_sent(index, _):
        chip_copy(index).wait_send()
        return 0

    lax.fori_loop(1, chips, chip_sent, 0)
    line.finish()


def input_line(mesh_axes, collective, part, hidden, residual_grad, gain, grads):
    tokens, model_width = part.shape
    hidden_width = grads.shape[2]
    chips = lax.axis_size("shard") * lax.axis_size("context") // 2
    block = model_width // (2 * chips)
    whole = pl.BlockSpec(memory_space=pltpu.VMEM)
    return pl.pallas_call(
        partial(input_kernel, mesh_axes),
        in_specs=[whole] * 4 + [pl.BlockSpec(memory_space=pl.ANY)],
        out_specs=[whole] * 5,
        out_shape=[
            jax.ShapeDtypeStruct((tokens, model_width), BF16),
            jax.ShapeDtypeStruct((1, model_width), F32),
        ]
        + [jax.ShapeDtypeStruct((block, hidden_width), F32)] * 3,
        scratch_shapes=[
            pltpu.VMEM((tokens, model_width), BF16),
            pltpu.VMEM((chips, 3, block, hidden_width), BF16),
            pltpu.VMEM((chips, 3, block, hidden_width), BF16),
            pltpu.VMEM((chips - 1, 3, block, hidden_width), BF16),
            pltpu.SemaphoreType.DMA((chips,)),
            pltpu.SemaphoreType.DMA((chips,)),
            pltpu.SemaphoreType.DMA((chips,)),
            pltpu.SemaphoreType.DMA((chips - 1,)),
            pltpu.SemaphoreType.DMA((chips - 1,)),
        ]
        + line_sems(tokens),
        compiler_params=pltpu.CompilerParams(
            collective_id=collective, has_side_effects=True, vmem_limit_bytes=58 << 20
        ),
        cost_estimate=pl.CostEstimate(
            flops=tokens * model_width * 8, bytes_accessed=360_000_000, transcendentals=0
        ),
        name="input_line",
    )(part, hidden, residual_grad, gain, grads)


def front_kernel(
    mesh_axes,
    hidden_ref,
    gain_ref,
    query_ref,
    forget_ref,
    input_ref,
    gate_ref,
    normed_hbm,
    pre_hbm,
    full_hbm,
    normed,
    pre,
    full,
    save_sem,
    normed_sem,
    pre_sem,
    send_sem,
    recv_sem,
    pair_send,
    pair_recv,
):
    plane = Plane(mesh_axes)
    chips = plane.chips
    tokens, model_width = hidden_ref.shape
    block, width = query_ref.shape
    part = block // 2
    relayed = chips == 4

    def partner(distance):
        return jnp.bitwise_xor(plane.chip, distance)

    def rows_of(chip, core, half):
        return pl.ds(pl.multiple_of((2 * chip + core) * block + half * part, part), part)

    def copy(rows, distance, half, chip):
        return pltpu.make_async_remote_copy(
            full.at[rows],
            full.at[rows],
            send_sem.at[distance - 1, half],
            recv_sem.at[distance - 1, half],
            device_id=plane.device(chip, plane.core),
            device_id_type=MESH_ID,
        )

    def send(distance, half):
        if relayed and distance == 3:
            through, target = (2, 1) if half == 0 else (1, 2)
            return copy(
                rows_of(partner(through), plane.core, half), 3, half, partner(target)
            )
        return copy(rows_of(plane.chip, plane.core, half), distance, half, partner(distance))

    def forward(distance, half):
        rows = rows_of(partner(distance), plane.core, half)
        return pltpu.make_async_remote_copy(
            full.at[rows],
            full.at[rows],
            pair_send.at[distance, half],
            pair_recv.at[distance, half],
            device_id=plane.device(plane.chip, 1 - plane.core),
            device_id_type=MESH_ID,
        )

    own = pl.ds(pl.multiple_of((2 * plane.chip + plane.core) * block, block), block)
    for which, ref in enumerate((query_ref, forget_ref, input_ref, gate_ref)):
        full[own, which * width : (which + 1) * width] = ref[...]
    barrier = pltpu.get_barrier_semaphore()
    targets = [plane.device(plane.chip, 1 - plane.core)]
    targets += [
        plane.device(partner(step), plane.core)
        for step in range(1, 3 if relayed else chips)
    ]
    for target in targets:
        pl.semaphore_signal(barrier, inc=1, device_id=target, device_id_type=MESH_ID)
    pl.semaphore_wait(barrier, len(targets))
    if relayed:
        for distance, half in ((1, 1), (2, 0), (1, 0), (2, 1)):
            send(distance, half).start()
    else:
        for distance in range(1, chips):
            send(distance, 0).start()
            send(distance, 1).start()
    for half in range(2):
        forward(0, half).start()

    def norm(index, _):
        rows = pl.ds(pl.multiple_of(index * 128, 128), 128)
        values = hidden_ref[rows].astype(F32)
        normed[rows] = (values * inverse_rms(values) * gain_ref[...]).astype(BF16)
        return 0

    lax.fori_loop(0, tokens // 128, norm, 0)
    normed_save = pltpu.make_async_copy(normed, normed_hbm, normed_sem.at[0])
    normed_save.start()
    row_tile, column_tile = 256, 512

    def pre_save(index):
        rows = pl.ds(pl.multiple_of(index * row_tile, row_tile), row_tile)
        return pltpu.make_async_copy(pre.at[rows], pre_hbm.at[rows], pre_sem.at[index])

    def product(distance):
        depth = pl.ds(pl.multiple_of(2 * partner(distance) * block, 2 * block), 2 * block)

        def row_body(index, _):
            rows = pl.ds(pl.multiple_of(index * row_tile, row_tile), row_tile)
            left = normed[rows, depth]

            def column_body(column, _):
                columns = pl.ds(pl.multiple_of(column * column_tile, column_tile), column_tile)
                value = mm_nn(left, full[depth, columns])
                if distance > 0:
                    value = value + pre[rows, columns]
                pre[rows, columns] = value
                return 0

            lax.fori_loop(0, full.shape[1] // column_tile, column_body, 0)
            if distance == chips - 1:
                pre_save(index).start()
            return 0

        lax.fori_loop(0, tokens // row_tile, row_body, 0)

    def full_save(distance):
        depth = pl.ds(pl.multiple_of(2 * partner(distance) * block, 2 * block), 2 * block)
        return pltpu.make_async_copy(full.at[depth], full_hbm.at[depth], save_sem.at[distance])

    def use(distance):
        for half in range(2):
            forward(distance, half).wait_recv()
        full_save(distance).start()
        product(distance)

    use(0)
    if relayed:
        for distance, half in ((1, 1), (2, 0), (1, 0), (2, 1)):
            send(distance, half).wait_recv()
            if (distance, half) in ((1, 1), (2, 0)):
                send(3, half).start()
            forward(distance, half).start()
        use(1)
        use(2)
        for half in range(2):
            send(3, half).wait_recv()
            forward(3, half).start()
        use(3)
    else:
        for distance in range(1, chips):
            for half in range(2):
                send(distance, half).wait_recv()
                forward(distance, half).start()
            if distance > 1:
                use(distance - 1)
        use(chips - 1)
    for distance in range(chips):
        for half in range(2):
            if distance > 0:
                send(distance, half).wait_send()
            forward(distance, half).wait_send()
        full_save(distance).wait()
    normed_save.wait()
    for index in range(tokens // row_tile):
        pre_save(index).wait()


def front(mesh_axes, collective, hidden, gain, shards):
    tokens, model_width = hidden.shape
    block, width = shards[0].shape
    all_width = width * len(shards)
    chips = lax.axis_size("shard") * lax.axis_size("context") // 2
    whole = pl.BlockSpec(memory_space=pltpu.VMEM)
    remote = pl.BlockSpec(memory_space=pl.ANY)
    return pl.pallas_call(
        partial(front_kernel, mesh_axes),
        in_specs=[whole] * 6,
        out_specs=[remote] * 3,
        out_shape=[
            jax.ShapeDtypeStruct((tokens, model_width), BF16),
            jax.ShapeDtypeStruct((tokens, all_width), F32),
            jax.ShapeDtypeStruct((model_width, all_width), BF16),
        ],
        scratch_shapes=[
            pltpu.VMEM((tokens, model_width), BF16),
            pltpu.VMEM((tokens, all_width), F32),
            pltpu.VMEM((model_width, all_width), BF16),
            pltpu.SemaphoreType.DMA((chips,)),
            pltpu.SemaphoreType.DMA((1,)),
            pltpu.SemaphoreType.DMA((tokens // 256,)),
            pltpu.SemaphoreType.DMA((chips - 1, 2)),
            pltpu.SemaphoreType.DMA((chips - 1, 2)),
            pltpu.SemaphoreType.DMA((chips, 2)),
            pltpu.SemaphoreType.DMA((chips, 2)),
        ],
        compiler_params=pltpu.CompilerParams(
            collective_id=collective, has_side_effects=True, vmem_limit_bytes=48 << 20
        ),
        cost_estimate=pl.CostEstimate(
            flops=2 * tokens * model_width * all_width,
            bytes_accessed=160_000_000,
            transcendentals=0,
        ),
        name="front",
    )(hidden, gain, *shards)


def small_sum_kernel(
    mesh_axes, value, local_ref, total_ref, near, far, near_send, near_recv, far_send, far_recv
):
    shard_size, context_size = lax.axis_size("shard"), lax.axis_size("context")
    line_size = lax.axis_size("tensor")
    group = shard_size * context_size
    place = lax.axis_index("shard") * context_size + lax.axis_index("context")
    line_place = lax.axis_index("tensor")

    def device(position, line_position):
        places = {
            "shard": position // context_size,
            "context": lax.rem(position, context_size),
            "tensor": line_position,
        }
        return tuple(places[axis] for axis in mesh_axes)

    def near_target(step):
        return device(lax.rem(place + step, group), line_place)

    def far_target(step):
        return device(place, lax.rem(line_place + step, line_size))

    def near_copy(step):
        return pltpu.make_async_remote_copy(
            value,
            near.at[step - 1],
            near_send.at[step - 1],
            near_recv.at[step - 1],
            device_id=near_target(step),
            device_id_type=MESH_ID,
        )

    def far_copy(step):
        return pltpu.make_async_remote_copy(
            local_ref,
            far.at[step - 1],
            far_send.at[step - 1],
            far_recv.at[step - 1],
            device_id=far_target(step),
            device_id_type=MESH_ID,
        )

    barrier = pltpu.get_barrier_semaphore()
    for step in range(1, group):
        pl.semaphore_signal(barrier, inc=1, device_id=near_target(step), device_id_type=MESH_ID)
    for step in range(1, line_size):
        pl.semaphore_signal(barrier, inc=1, device_id=far_target(step), device_id_type=MESH_ID)
    pl.semaphore_wait(barrier, group + line_size - 2)
    for step in range(1, group):
        near_copy(step).start()
    total = value[...]
    for step in range(1, group):
        near_copy(step).wait_recv()
        total = total + near[step - 1]
    local_ref[...] = total
    for step in range(1, line_size):
        far_copy(step).start()
    for step in range(1, line_size):
        far_copy(step).wait_recv()
        total = total + far[step - 1]
    total_ref[...] = total
    for step in range(1, group):
        near_copy(step).wait_send()
    for step in range(1, line_size):
        far_copy(step).wait_send()


def small_sum(mesh_axes, collective, values):
    flat = jnp.concatenate([value.reshape(-1) for value in values])
    lanes = -(-flat.shape[0] // 1024) * 128
    flat = jnp.pad(flat, (0, 8 * lanes - flat.shape[0])).reshape(8, lanes)
    group = lax.axis_size("shard") * lax.axis_size("context")
    line_size = lax.axis_size("tensor")
    whole = pl.BlockSpec(memory_space=pltpu.VMEM)
    local, total = pl.pallas_call(
        partial(small_sum_kernel, mesh_axes),
        in_specs=[whole],
        out_specs=[whole] * 2,
        out_shape=[jax.ShapeDtypeStruct((8, lanes), F32)] * 2,
        scratch_shapes=[
            pltpu.VMEM((group - 1, 8, lanes), F32),
            pltpu.VMEM((line_size - 1, 8, lanes), F32),
            pltpu.SemaphoreType.DMA((group - 1,)),
            pltpu.SemaphoreType.DMA((group - 1,)),
            pltpu.SemaphoreType.DMA((line_size - 1,)),
            pltpu.SemaphoreType.DMA((line_size - 1,)),
        ],
        compiler_params=pltpu.CompilerParams(collective_id=collective, has_side_effects=True),
        cost_estimate=pl.CostEstimate(
            flops=8 * lanes * group, bytes_accessed=20_000_000, transcendentals=0
        ),
        name="small_sum",
    )(flat)
    return local.reshape(-1), total.reshape(-1)


def local(
    mesh_axes,
    hidden,
    segment_ids,
    norm1_gain,
    w_query,
    w_forget,
    w_input,
    w_gate_out,
    forget_floor,
    head_gain,
    w_out,
    norm2_gain,
    w_ffn_gate,
    w_ffn_up,
    w_ffn_down,
    out_grad,
):
    sequences, span_len, model_width = hidden.shape
    tokens = sequences * span_len
    head_count, key_dim = forget_floor.shape
    width = head_count * key_dim
    key_scale = key_dim ** (-0.5)
    both = ("shard", "context")
    gain_one, gain_two = norm1_gain.reshape(1, -1), norm2_gain.reshape(1, -1)
    half_wide = jax.ShapeDtypeStruct((tokens // 2, model_width), F32)
    hidden_rows = hidden.reshape(tokens, model_width)
    normed_one, pre, mixer_full = front(
        mesh_axes, 4, hidden_rows, gain_one, (w_query, w_forget, w_input, w_gate_out)
    )
    pre, w_out, w_ffn_gate, w_ffn_up, w_ffn_down = lax.optimization_barrier(
        (pre, w_out, w_ffn_gate, w_ffn_up, w_ffn_down)
    )
    out_full = lax.all_gather(w_out, both, axis=1, tiled=True)
    gate_full = lax.all_gather(w_ffn_gate, both, axis=0, tiled=True)
    up_full = lax.all_gather(w_ffn_up, both, axis=0, tiled=True)
    down_full = lax.all_gather(w_ffn_down, both, axis=1, tiled=True)
    open_part = (1.0 - forget_floor).reshape(1, width)
    counts, keep, flags, last_count = row_flags(segment_ids)
    mixed_local, lead, starts, runs, state_end, run_end = mixer_forward(
        pre, open_part, counts, keep, flags, head_count, key_scale
    )
    decay = (jnp.exp(run_end) * (last_count == 0).astype(F32)).reshape(head_count, 1, key_dim)
    ids = segment_ids.reshape(-1).astype(F32)
    carry, link_in = state_before(state_end, decay, ids[0], ids[-1], "context")
    gain_row = head_gain.reshape(1, -1)
    mixed, gated_low = gate_forward(
        mixed_local, lead, carry.astype(BF16), pre, gain_row, keep, key_scale
    )
    mix_part = jnp.dot(gated_low, out_full, preferred_element_type=F32).astype(BF16)
    normed_two, residual = line_exchange(
        residual_norm, mesh_axes, 0, mix_part, (hidden_rows, gain_two), [half_wide], "mix_line"
    )
    grad_rows = out_grad.reshape(tokens, model_width)
    grad_mix_low, grad_norm_two, hidden_low, grad_gate_low, grad_up_low, feed_part, grad_residual = (
        feed_line(
            mesh_axes, 2, normed_two, grad_rows, residual, gain_two, gate_full, up_full, down_full
        )
    )
    output_rows, grads_ffn = output_line(
        mesh_axes,
        1,
        feed_part,
        residual,
        normed_two,
        grad_rows,
        hidden_low,
        grad_gate_low,
        grad_up_low,
    )
    grad_out = jnp.einsum("tv,td->vd", gated_low, grad_mix_low, preferred_element_type=F32)
    grad_gated = jnp.einsum("td,vd->tv", grad_mix_low, out_full, preferred_element_type=F32)
    grad_mixed, grad_gate_pre, grad_head_part, back = gate_backward(
        grad_gated, mixed, lead, pre, gain_row, keep, head_count, key_scale
    )
    after = grad_after(back, decay, link_in, "context")
    grad_pre, grad_floor_part = mixer_backward(
        pre,
        grad_mixed,
        grad_gate_pre,
        starts,
        runs,
        carry,
        after,
        open_part,
        counts,
        keep,
        flags,
    )
    grad_mixer = jnp.einsum("td,tk->dk", normed_one, grad_pre, preferred_element_type=F32)
    back_one = jnp.einsum("tk,dk->td", grad_pre, mixer_full, preferred_element_type=F32)
    input_rows, grad_norm_one, share_gate, share_up, share_down = input_line(
        mesh_axes, 3, back_one.astype(BF16), hidden_rows, grad_residual, gain_one, grads_ffn
    )
    near, total = small_sum(
        mesh_axes, 5, (grad_norm_one, grad_norm_two, grad_head_part, grad_floor_part)
    )
    shares = lax.axis_size("shard") * lax.axis_size("context")
    position = lax.axis_index("shard") * lax.axis_size("context") + lax.axis_index("context")

    def own_slice(values, first, length):
        values = values[first : first + length].reshape(shares, length // shares)
        return lax.dynamic_index_in_dim(values, position, 0, False)

    floor_total = near[2 * model_width + key_dim : 2 * model_width + key_dim + width]
    floor_total = floor_total.reshape(head_count, shares, key_dim // shares)

    def share(values, dim):
        return lax.psum_scatter(
            values.astype(BF16), both, scatter_dimension=dim, tiled=True
        ).astype(F32)

    share_mixer = share(grad_mixer, 0)
    return (
        output_rows.reshape(hidden.shape),
        input_rows.reshape(hidden.shape),
        own_slice(total, 0, model_width),
        share_mixer[:, :width],
        share_mixer[:, width : 2 * width],
        share_mixer[:, 2 * width : 3 * width],
        share_mixer[:, 3 * width :],
        lax.dynamic_index_in_dim(floor_total, position, 1, False),
        own_slice(total, 2 * model_width, key_dim),
        share(grad_out, 1),
        own_slice(total, model_width, model_width),
        share_gate,
        share_up,
        share_down.T,
    )


def solution(mesh):
    in_specs = (
        P("shard", "context", None),
        P("shard", "context"),
        P(),
        P(("shard", "context"), "tensor"),
        P(("shard", "context"), "tensor"),
        P(("shard", "context"), "tensor"),
        P(("shard", "context"), "tensor"),
        P("tensor", None),
        P(),
        P("tensor", ("shard", "context")),
        P(),
        P(("shard", "context"), "tensor"),
        P(("shard", "context"), "tensor"),
        P("tensor", ("shard", "context")),
        P("shard", "context", None),
    )
    out_specs = (
        P("shard", "context", None),
        P("shard", "context", None),
        P(("shard", "context")),
        P(("shard", "context"), "tensor"),
        P(("shard", "context"), "tensor"),
        P(("shard", "context"), "tensor"),
        P(("shard", "context"), "tensor"),
        P("tensor", ("shard", "context")),
        P(("shard", "context")),
        P("tensor", ("shard", "context")),
        P(("shard", "context")),
        P(("shard", "context"), "tensor"),
        P(("shard", "context"), "tensor"),
        P("tensor", ("shard", "context")),
    )
    return jax.shard_map(
        partial(local, mesh.axis_names), mesh=mesh, in_specs=in_specs, out_specs=out_specs, check_vma=False)
```

```python
from functools import partial

import jax
import jax.numpy as jnp
from jax import lax
from jax.experimental import pallas as pl
from jax.experimental.pallas import tpu as pltpu
from jax.sharding import PartitionSpec as P

EPSILON = 1e-05


BLOCK = 128
F32 = jnp.float32
BF16 = jnp.bfloat16


def mm(a, b, dims):
    return lax.dot_general(a, b, (dims, ((), ())), preferred_element_type=F32)


def mm_nn(a, b):
    return mm(a, b, ((1,), (0,)))


def mm_nt(a, b):
    return mm(a, b, ((1,), (1,)))


def mm_tn(a, b):
    return mm(a, b, ((0,), (0,)))


def split_sum(tri, values):
    high = values.astype(BF16)
    low = (values - high.astype(F32)).astype(BF16)
    return mm_nn(tri, high) + mm_nn(tri, low)


def block_masks(counts, flags_row):
    rows = counts.shape[0]
    row_ids = lax.broadcasted_iota(jnp.int32, (rows, rows), 0)
    col_ids = lax.broadcasted_iota(jnp.int32, (rows, rows), 1)
    linked = jnp.logical_and(counts == flags_row[0:1], row_ids >= col_ids)
    fresh = (counts == flags_row[1:2, 0:1]).astype(F32)
    tail = (counts == flags_row[2:3, 0:1]).astype(F32)
    closing = (flags_row[1:2, 0:1] == flags_row[2:3, 0:1]).astype(F32)
    return row_ids, col_ids, linked, fresh, tail, closing


def mixer_forward_kernel(
    head_count,
    key_scale,
    pre_ref,
    open_ref,
    count_ref,
    keep_ref,
    flags_ref,
    mixed_ref,
    lead_ref,
    start_ref,
    run_ref,
    end_ref,
    total_ref,
    state_scr,
    run_scr,
):
    step = pl.program_id(0)
    width = open_ref.shape[1]
    lanes = width // head_count

    @pl.when(step == 0)
    def _():
        state_scr[...] = jnp.zeros_like(state_scr)
        run_scr[...] = jnp.zeros_like(run_scr)

    counts, keep = count_ref[...], keep_ref[...]
    row_ids, col_ids, linked, fresh, tail, closing = block_masks(counts, flags_ref[0])
    tri = (row_ids >= col_ids).astype(BF16)
    query_pre = pre_ref[:, :width]
    values = pre_ref[:, 2 * width : 3 * width].astype(BF16)
    keys = open_ref[...] * jax.nn.sigmoid(-pre_ref[:, width : 2 * width])
    cum = split_sum(tri, jnp.log1p(-keys))
    rows = cum.shape[0]
    ending = cum[rows - 1 : rows, :]
    lifted = query_pre * jax.nn.sigmoid(query_pre) * jnp.exp(cum)
    lowered = (keys * jnp.exp(-cum) * keep).astype(BF16)
    moved = (keys * jnp.exp(ending - cum) * (keep * tail)).astype(BF16)
    run = run_scr[...]
    lead_ref[...] = (lifted * jnp.exp(run) * (counts == 0).astype(F32)).astype(BF16)
    run_ref[0] = run
    run_scr[...] = run + ending
    total_ref[...] = run + ending
    fresh_lifted = (lifted * fresh).astype(BF16)
    lifted = lifted.astype(BF16)
    end_decay = jnp.exp(ending) * closing
    for head in range(head_count):
        part = slice(head * lanes, (head + 1) * lanes)
        state = state_scr[head]
        start_ref[0, head] = state
        scores = jnp.where(linked, mm_nt(lifted[:, part], lowered[:, part]), 0.0)
        results = mm_nn(scores.astype(BF16), values[:, part])
        results = results + mm_nt(fresh_lifted[:, part], state.astype(BF16))
        mixed_ref[:, part] = results * (key_scale * keep)
        state = state * end_decay[:, part] + mm_tn(values[:, part], moved[:, part])
        state_scr[head] = state
        end_ref[head] = state


def mixer_forward(pre, open_part, counts, keep, flags, head_count, key_scale):
    tokens, all_width = pre.shape
    width = open_part.shape[1]
    lanes = width // head_count
    blocks = tokens // BLOCK
    return pl.pallas_call(
        partial(mixer_forward_kernel, head_count, key_scale),
        grid=(blocks,),
        in_specs=[
            pl.BlockSpec((BLOCK, all_width), lambda i: (i, 0)),
            pl.BlockSpec((1, width), lambda i: (0, 0)),
            pl.BlockSpec((BLOCK, 1), lambda i: (i, 0)),
            pl.BlockSpec((BLOCK, 1), lambda i: (i, 0)),
            pl.BlockSpec((1, 8, BLOCK), lambda i: (i, 0, 0)),
        ],
        out_specs=[
            pl.BlockSpec((BLOCK, width), lambda i: (i, 0)),
            pl.BlockSpec((BLOCK, width), lambda i: (i, 0)),
            pl.BlockSpec((1, head_count, lanes, lanes), lambda i: (i, 0, 0, 0)),
            pl.BlockSpec((1, 1, width), lambda i: (i, 0, 0)),
            pl.BlockSpec((head_count, lanes, lanes), lambda i: (0, 0, 0)),
            pl.BlockSpec((1, width), lambda i: (0, 0)),
        ],
        out_shape=[
            jax.ShapeDtypeStruct((tokens, width), F32),
            jax.ShapeDtypeStruct((tokens, width), BF16),
            jax.ShapeDtypeStruct((blocks, head_count, lanes, lanes), F32),
            jax.ShapeDtypeStruct((blocks, 1, width), F32),
            jax.ShapeDtypeStruct((head_count, lanes, lanes), F32),
            jax.ShapeDtypeStruct((1, width), F32),
        ],
        scratch_shapes=[
            pltpu.VMEM((head_count, lanes, lanes), F32),
            pltpu.VMEM((1, width), F32),
        ],
        compiler_params=pltpu.CompilerParams(
            dimension_semantics=("arbitrary",), vmem_limit_bytes=40 << 20
        ),
        cost_estimate=pl.CostEstimate(
            flops=tokens * width * BLOCK * 12,
            bytes_accessed=tokens * width * 30,
            transcendentals=tokens * width * 7,
        ),
        name="mixer_forward",
    )(pre, open_part, counts, keep, flags)


def gate_forward_kernel(
    head_count,
    key_scale,
    local_ref,
    lead_ref,
    carry_ref,
    gate_ref,
    gain_ref,
    keep_ref,
    mixed_ref,
    gated_ref,
):
    lanes = gain_ref.shape[1]
    for head in range(head_count):
        part = slice(head * lanes, (head + 1) * lanes)
        carried = mm_nt(lead_ref[:, part], carry_ref[head])
        mixed = local_ref[:, part] + carried * (key_scale * keep_ref[...])
        mixed_ref[:, part] = mixed
        inverse = lax.rsqrt(jnp.mean(mixed * mixed, axis=-1, keepdims=True) + EPSILON)
        gate = gate_ref[:, part]
        gated = mixed * inverse * gain_ref[...] * (gate * jax.nn.sigmoid(gate))
        gated_ref[:, part] = gated.astype(BF16)


def gate_forward(local, lead, carry, pre, gain, keep, key_scale):
    tokens, width = local.shape
    head_count, lanes = carry.shape[0], carry.shape[2]
    rows = 2 * BLOCK
    return pl.pallas_call(
        partial(gate_forward_kernel, head_count, key_scale),
        grid=(tokens // rows,),
        in_specs=[
            pl.BlockSpec((rows, width), lambda i: (i, 0)),
            pl.BlockSpec((rows, width), lambda i: (i, 0)),
            pl.BlockSpec((head_count, lanes, lanes), lambda i: (0, 0, 0)),
            pl.BlockSpec((rows, width), lambda i: (i, 3)),
            pl.BlockSpec((1, lanes), lambda i: (0, 0)),
            pl.BlockSpec((rows, 1), lambda i: (i, 0)),
        ],
        out_specs=[
            pl.BlockSpec((rows, width), lambda i: (i, 0)),
            pl.BlockSpec((rows, width), lambda i: (i, 0)),
        ],
        out_shape=[
            jax.ShapeDtypeStruct((tokens, width), F32),
            jax.ShapeDtypeStruct((tokens, width), BF16),
        ],
        compiler_params=pltpu.CompilerParams(
            dimension_semantics=("arbitrary",), vmem_limit_bytes=40 << 20
        ),
        cost_estimate=pl.CostEstimate(
            flops=tokens * width * 300,
            bytes_accessed=tokens * width * 16,
            transcendentals=tokens * width,
        ),
        name="gate_forward",
    )(local, lead, carry, pre, gain, keep)


def gate_backward_kernel(
    head_count,
    key_scale,
    grad_ref,
    mixed_ref,
    lead_ref,
    gate_ref,
    gain_ref,
    keep_ref,
    grad_mixed_ref,
    grad_gate_ref,
    grad_gain_ref,
    back_ref,
):
    lanes = gain_ref.shape[1]

    @pl.when(pl.program_id(0) == 0)
    def _():
        grad_gain_ref[...] = jnp.zeros_like(grad_gain_ref)
        back_ref[...] = jnp.zeros_like(back_ref)

    gain = gain_ref[...]
    total = jnp.zeros_like(gain)
    for head in range(head_count):
        part = slice(head * lanes, (head + 1) * lanes)
        mixed, gate, grad = mixed_ref[:, part], gate_ref[:, part], grad_ref[:, part]
        inverse = lax.rsqrt(jnp.mean(mixed * mixed, axis=-1, keepdims=True) + EPSILON)
        unit = mixed * inverse
        sigma = jax.nn.sigmoid(gate)
        scaled = grad * unit
        total = total + jnp.sum(scaled * (gate * sigma), axis=0, keepdims=True)
        grad_gate = scaled * gain * sigma * (1.0 + gate * (1.0 - sigma))
        grad_gate_ref[:, part] = grad_gate.astype(BF16)
        lifted = grad * gain * (gate * sigma)
        mean = jnp.mean(lifted * unit, axis=-1, keepdims=True)
        grad_mixed = inverse * (lifted - unit * mean) * (key_scale * keep_ref[...])
        grad_mixed = grad_mixed.astype(BF16)
        grad_mixed_ref[:, part] = grad_mixed
        back_ref[head] += mm_tn(grad_mixed, lead_ref[:, part])
    grad_gain_ref[...] += total


def gate_backward(grad, mixed, lead, pre, gain, keep, head_count, key_scale):
    tokens, width = mixed.shape
    lanes = gain.shape[1]
    rows = 2 * BLOCK
    return pl.pallas_call(
        partial(gate_backward_kernel, head_count, key_scale),
        grid=(tokens // rows,),
        in_specs=[
            pl.BlockSpec((rows, width), lambda i: (i, 0)),
            pl.BlockSpec((rows, width), lambda i: (i, 0)),
            pl.BlockSpec((rows, width), lambda i: (i, 0)),
            pl.BlockSpec((rows, width), lambda i: (i, 3)),
            pl.BlockSpec((1, lanes), lambda i: (0, 0)),
            pl.BlockSpec((rows, 1), lambda i: (i, 0)),
        ],
        out_specs=[
            pl.BlockSpec((rows, width), lambda i: (i, 0)),
            pl.BlockSpec((rows, width), lambda i: (i, 0)),
            pl.BlockSpec((1, lanes), lambda i: (0, 0)),
            pl.BlockSpec((head_count, lanes, lanes), lambda i: (0, 0, 0)),
        ],
        out_shape=[
            jax.ShapeDtypeStruct((tokens, width), BF16),
            jax.ShapeDtypeStruct((tokens, width), BF16),
            jax.ShapeDtypeStruct((1, lanes), F32),
            jax.ShapeDtypeStruct((head_count, lanes, lanes), F32),
        ],
        compiler_params=pltpu.CompilerParams(
            dimension_semantics=("arbitrary",), vmem_limit_bytes=40 << 20
        ),
        cost_estimate=pl.CostEstimate(
            flops=tokens * width * 300,
            bytes_accessed=tokens * width * 18,
            transcendentals=tokens * width,
        ),
        name="gate_backward",
    )(grad, mixed, lead, pre, gain, keep)


def mixer_backward_kernel(
    head_count,
    pre_ref,
    grad_mixed_ref,
    grad_gate_ref,
    start_ref,
    run_ref,
    carry_ref,
    after_ref,
    open_ref,
    count_ref,
    keep_ref,
    flags_ref,
    grads_ref,
    floor_ref,
    grad_scr,
    lifted_scr,
    lowered_scr,
    moved_scr,
    value_scr,
):
    width = open_ref.shape[1]
    lanes = width // head_count

    @pl.when(pl.program_id(0) == 0)
    def _():
        grad_scr[...] = after_ref[...]
        floor_ref[...] = jnp.zeros_like(floor_ref)

    counts, keep = count_ref[...], keep_ref[...]
    flags = flags_ref[0]
    row_ids, col_ids, linked, fresh, tail, closing = block_masks(counts, flags)
    tri = (row_ids >= col_ids).astype(BF16)
    tri_back = (row_ids <= col_ids).astype(BF16)
    query_pre = pre_ref[:, :width]
    values = pre_ref[:, 2 * width : 3 * width].astype(BF16)
    opened = open_ref[...]
    closed = jax.nn.sigmoid(-pre_ref[:, width : 2 * width])
    keys = opened * closed
    cum = split_sum(tri, jnp.log1p(-keys))
    rows = cum.shape[0]
    ending = cum[rows - 1 : rows, :]
    rise, fall = jnp.exp(cum), jnp.exp(-cum) * keep
    shift = jnp.exp(ending - cum) * (keep * tail)
    sigma_query = jax.nn.sigmoid(query_pre)
    lifted = (query_pre * sigma_query * rise).astype(BF16)
    lowered = (keys * fall).astype(BF16)
    moved = (keys * shift).astype(BF16)
    fresh_lifted = (lifted.astype(F32) * fresh).astype(BF16)
    end_decay = jnp.exp(ending) * closing
    lead_in = jnp.exp(run_ref[0]) * (flags[1:2, 0:1] == 0).astype(F32)
    for head in range(head_count):
        part = slice(head * lanes, (head + 1) * lanes)
        grad_out, value = grad_mixed_ref[:, part], values[:, part]
        lift, lower, move = lifted[:, part], lowered[:, part], moved[:, part]
        scores = jnp.where(linked, mm_nt(lift, lower), 0.0).astype(BF16)
        pulls = jnp.where(linked, mm_nt(grad_out, value), 0.0).astype(BF16)
        state = start_ref[0, head] + lead_in[:, part] * carry_ref[head]
        grad_state = grad_scr[head]
        grad_low = grad_state.astype(BF16)
        lifted_scr[:, part] = mm_nn(pulls, lower) + fresh * mm_nn(grad_out, state.astype(BF16))
        lowered_scr[:, part] = mm_tn(pulls, lift)
        grad_moved = mm_nn(value, grad_low)
        moved_scr[:, part] = grad_moved
        grads_ref[:, 2 * width + head * lanes : 2 * width + (head + 1) * lanes] = (
            mm_tn(scores, grad_out) + mm_nt(move, grad_low)
        ).astype(BF16)
        value_scr[:, part] = jnp.sum(
            grad_moved * move.astype(F32), axis=0, keepdims=True
        ) + end_decay[:, part] * jnp.sum(state * grad_state, axis=0, keepdims=True)
        grad_scr[head] = grad_state * end_decay[:, part] + mm_tn(grad_out, fresh_lifted[:, part])
    grad_lifted, grad_lowered, grad_moved = lifted_scr[...], lowered_scr[...], moved_scr[...]
    grad_cum = (
        grad_lifted * lifted.astype(F32)
        - grad_lowered * lowered.astype(F32)
        - grad_moved * moved.astype(F32)
    )
    grad_decay = split_sum(tri_back, grad_cum) + value_scr[...]
    key_total = grad_lowered * fall + grad_moved * shift - grad_decay / (1.0 - keys)
    floor_ref[...] -= jnp.sum(key_total * closed, axis=0, keepdims=True)
    grads_ref[:, :width] = (
        grad_lifted * rise * sigma_query * (1.0 + query_pre * (1.0 - sigma_query))
    ).astype(BF16)
    grads_ref[:, width : 2 * width] = (-key_total * opened * closed * (1.0 - closed)).astype(BF16)
    grads_ref[:, 3 * width :] = grad_gate_ref[...]


def mixer_backward(
    pre, grad_mixed, grad_gate, starts, runs, carry, after, open_part, counts, keep, flags
):
    tokens, all_width = pre.shape
    width = open_part.shape[1]
    head_count, lanes = carry.shape[0], carry.shape[2]
    blocks = tokens // BLOCK
    last = blocks - 1
    return pl.pallas_call(
        partial(mixer_backward_kernel, head_count),
        grid=(blocks,),
        in_specs=[
            pl.BlockSpec((BLOCK, all_width), lambda i: (last - i, 0)),
            pl.BlockSpec((BLOCK, width), lambda i: (last - i, 0)),
            pl.BlockSpec((BLOCK, width), lambda i: (last - i, 0)),
            pl.BlockSpec((1, head_count, lanes, lanes), lambda i: (last - i, 0, 0, 0)),
            pl.BlockSpec((1, 1, width), lambda i: (last - i, 0, 0)),
            pl.BlockSpec((head_count, lanes, lanes), lambda i: (0, 0, 0)),
            pl.BlockSpec((head_count, lanes, lanes), lambda i: (0, 0, 0)),
            pl.BlockSpec((1, width), lambda i: (0, 0)),
            pl.BlockSpec((BLOCK, 1), lambda i: (last - i, 0)),
            pl.BlockSpec((BLOCK, 1), lambda i: (last - i, 0)),
            pl.BlockSpec((1, 8, BLOCK), lambda i: (last - i, 0, 0)),
        ],
        out_specs=[
            pl.BlockSpec((BLOCK, all_width), lambda i: (last - i, 0)),
            pl.BlockSpec((1, width), lambda i: (0, 0)),
        ],
        out_shape=[
            jax.ShapeDtypeStruct((tokens, all_width), BF16),
            jax.ShapeDtypeStruct((1, width), F32),
        ],
        scratch_shapes=[
            pltpu.VMEM((head_count, lanes, lanes), F32),
            pltpu.VMEM((BLOCK, width), F32),
            pltpu.VMEM((BLOCK, width), F32),
            pltpu.VMEM((BLOCK, width), F32),
            pltpu.VMEM((1, width), F32),
        ],
        compiler_params=pltpu.CompilerParams(
            dimension_semantics=("arbitrary",), vmem_limit_bytes=40 << 20
        ),
        cost_estimate=pl.CostEstimate(
            flops=tokens * width * BLOCK * 30,
            bytes_accessed=tokens * width * 36,
            transcendentals=tokens * width * 9,
        ),
        name="mixer_backward",
    )(pre, grad_mixed, grad_gate, starts, runs, carry, after, open_part, counts, keep, flags)


def row_flags(segment_ids):
    ids = segment_ids.reshape(-1)
    tokens = ids.shape[0]
    starts = jnp.concatenate([jnp.zeros((1,), F32), (ids[1:] != ids[:-1]).astype(F32)])
    positions = jnp.arange(tokens)
    counts = jnp.sum(
        jnp.where(positions[None, :] <= positions[:, None], starts[None, :], 0.0), axis=1
    )
    keep = (ids > 0).astype(F32)
    blocks = tokens // BLOCK
    by_block = counts.reshape(blocks, BLOCK)
    lasts = by_block[:, -1]
    before = jnp.concatenate([jnp.zeros((1,), F32), lasts[:-1]])
    wide = (blocks, BLOCK)
    flags = jnp.stack(
        [by_block, jnp.broadcast_to(before[:, None], wide), jnp.broadcast_to(lasts[:, None], wide)]
        + [jnp.zeros(wide, F32)] * 5,
        axis=1,
    )
    return counts[:, None], keep[:, None], flags, lasts[-1]


def from_earlier(values, axis, shift):
    count = lax.axis_size(axis)
    return lax.ppermute(values, axis, [(i, i + shift) for i in range(count - shift)])


def from_later(values, axis, shift):
    count = lax.axis_size(axis)
    return lax.ppermute(values, axis, [(i + shift, i) for i in range(count - shift)])


def state_before(state, decay, first_id, last_id, axis):
    head_count, lanes, _ = state.shape
    ids = jnp.stack([first_id, last_id, jnp.float32(1.0)] + [jnp.float32(0.0)] * 5)
    message = jnp.concatenate(
        [
            state.reshape(head_count * lanes, lanes),
            decay.reshape(head_count, lanes),
            jnp.broadcast_to(ids[:, None], (8, lanes)),
        ]
    )
    rows = head_count * lanes
    total = jnp.zeros_like(state)
    factor = jnp.ones((head_count, 1, lanes), F32)
    follower = first_id
    link_in = jnp.float32(0.0)
    for shift in range(1, lax.axis_size(axis)):
        got = from_earlier(message, axis, shift)
        got_ids = got[rows + head_count :, 0]
        linked = (got_ids[1] == follower).astype(F32) * got_ids[2]
        if shift == 1:
            link_in = linked
        factor = factor * linked
        total = total + factor * got[:rows].reshape(state.shape)
        factor = factor * got[rows : rows + head_count].reshape(head_count, 1, lanes)
        follower = got_ids[0]
    return total, link_in


def grad_after(back, decay, link_in, axis):
    head_count, lanes, _ = back.shape
    rows = head_count * lanes
    message = (
        jnp.concatenate([back.reshape(rows, lanes), decay.reshape(head_count, lanes)]) * link_in
    )
    message = jnp.pad(message, ((0, 8 - head_count % 8 if head_count % 8 else 0), (0, 0)))
    total = jnp.zeros_like(back)
    factor = jnp.ones((head_count, 1, lanes), F32)
    for shift in range(1, lax.axis_size(axis)):
        got = from_later(message, axis, shift)
        total = total + factor * got[:rows].reshape(back.shape)
        factor = factor * got[rows : rows + head_count].reshape(head_count, 1, lanes)
    return total


CHUNK = 32
LAG = 2
MESH_ID = pl.DeviceIdType.MESH


class Line:
    def __init__(self, mesh_axes, part, arrived, out, sems, transform):
        self.mesh_axes = mesh_axes
        self.part, self.arrived, self.out = part, arrived, out
        self.sum_send, self.sum_recv, self.back_send, self.back_recv = sems
        self.transform = transform
        self.half = part.shape[0] // 2
        self.chunks = self.half // CHUNK
        self.size = lax.axis_size("tensor")
        self.place = lax.axis_index("tensor")
        self.lines = ((self.size - 1 - self.place, -1), (self.place, 1))
        self.steps = self.chunks + 2 * LAG * (self.size - 1)

    def device(self, position):
        return tuple(
            jnp.clip(position, 0, self.size - 1) if axis == "tensor" else lax.axis_index(axis)
            for axis in self.mesh_axes
        )

    def greet(self, barrier):
        for step in (-1, 1):
            inside = jnp.logical_and(self.place + step >= 0, self.place + step < self.size)

            @pl.when(inside)
            def _(step=step):
                pl.semaphore_signal(
                    barrier, inc=1, device_id=self.device(self.place + step), device_id_type=MESH_ID
                )

        at_end = jnp.logical_or(self.place == 0, self.place == self.size - 1)
        return jnp.where(at_end, 1, 2)

    def rows_of(self, side, index):
        return pl.ds(pl.multiple_of(side * self.half + index * CHUNK, CHUNK), CHUNK)

    def sum_copy(self, side, index, source):
        rows = self.rows_of(side, index)
        return pltpu.make_async_remote_copy(
            source.at[rows],
            self.arrived.at[rows],
            self.sum_send.at[side, index],
            self.sum_recv.at[side, index],
            device_id=self.device(self.place + self.lines[side][1]),
            device_id_type=MESH_ID,
        )

    def back_copy(self, side, index):
        rows = self.rows_of(side, index)
        return pltpu.make_async_remote_copy(
            self.out.at[rows],
            self.out.at[rows],
            self.back_send.at[side, index],
            self.back_recv.at[side, index],
            device_id=self.device(self.place - self.lines[side][1]),
            device_id_type=MESH_ID,
        )

    def step(self, time):
        for side in (0, 1):
            hops = self.lines[side][0]
            index = time - LAG * hops
            valid = jnp.logical_and(index >= 0, index < self.chunks)
            at_source, at_owner = hops == 0, hops == self.size - 1
            index = jnp.clip(index, 0, self.chunks - 1)
            rows = self.rows_of(side, index)

            @pl.when(jnp.logical_and(valid, at_source))
            def _(side=side, index=index):
                self.sum_copy(side, index, self.part).start()

            @pl.when(jnp.logical_and(valid, jnp.logical_not(at_source)))
            def _(side=side, index=index):
                self.sum_copy(side, index, self.arrived).wait_recv()

            between = jnp.logical_and(jnp.logical_not(at_source), jnp.logical_not(at_owner))

            @pl.when(jnp.logical_and(valid, between))
            def _(side=side, index=index, rows=rows):
                total = self.part[rows].astype(F32) + self.arrived[rows].astype(F32)
                self.arrived[rows] = total.astype(BF16)
                self.sum_copy(side, index, self.arrived).start()

            @pl.when(jnp.logical_and(valid, at_owner))
            def _(side=side, index=index, rows=rows):
                total = self.part[rows].astype(F32) + self.arrived[rows].astype(F32)
                own = pl.ds(pl.multiple_of(index * CHUNK, CHUNK), CHUNK)
                self.transform(total, rows, own)
                self.back_copy(side, index).start()

            away = self.size - 1 - hops
            index = time - LAG * (self.size - 1 + away)
            valid = jnp.logical_and(jnp.logical_and(index >= 0, index < self.chunks), away > 0)
            index = jnp.clip(index, 0, self.chunks - 1)

            @pl.when(valid)
            def _(side=side, index=index):
                self.back_copy(side, index).wait_recv()

            @pl.when(jnp.logical_and(valid, away < self.size - 1))
            def _(side=side, index=index):
                self.back_copy(side, index).start()

    def run(self, first, last, beside=None):
        def body(time, _):
            self.step(time)
            if beside is not None:
                beside(time)
            return 0

        lax.fori_loop(first, last, body, 0)

    def source_sent(self, first, last):
        def body(index, _):
            for side in (0, 1):

                @pl.when(self.lines[side][0] == 0)
                def _(side=side):
                    self.sum_copy(side, index, self.part).wait_send()

            return 0

        lax.fori_loop(first, last, body, 0)

    def finish(self, source_waits=True):
        def body(index, _):
            for side in (0, 1):
                hops = self.lines[side][0]
                passed = hops < self.size - 1
                if not source_waits:
                    passed = jnp.logical_and(passed, hops > 0)

                @pl.when(passed)
                def _(side=side):
                    self.sum_copy(side, index, self.arrived).wait_send()

                @pl.when(hops > 0)
                def _(side=side):
                    self.back_copy(side, index).wait_send()

            return 0

        lax.fori_loop(0, self.chunks, body, 0)


def line_sems(tokens):
    return [pltpu.SemaphoreType.DMA((2, tokens // 2 // CHUNK))] * 4


def inverse_rms(values):
    return lax.rsqrt(jnp.mean(values * values, axis=-1, keepdims=True) + EPSILON)


class Plane:
    def __init__(self, mesh_axes):
        self.mesh_axes = mesh_axes
        self.context = lax.axis_size("context")
        self.per_row = self.context // 2
        self.chips = lax.axis_size("shard") * self.per_row
        context_place = lax.axis_index("context")
        self.core = lax.rem(context_place, 2)
        self.chip = lax.axis_index("shard") * self.per_row + context_place // 2

    def device(self, chip, core):
        places = {
            "shard": chip // self.per_row,
            "context": 2 * lax.rem(chip, self.per_row) + core,
            "tensor": lax.axis_index("tensor"),
        }
        return tuple(places[axis] for axis in self.mesh_axes)

    def ahead(self, distance):
        return lax.rem(self.chip + distance, self.chips)

    def greet(self, barrier):
        targets = [self.device(self.chip, 1 - self.core)]
        targets += [self.device(self.ahead(step), self.core) for step in range(1, self.chips)]
        for target in targets:
            pl.semaphore_signal(barrier, inc=1, device_id=target, device_id_type=MESH_ID)
        return len(targets)


class Gather:
    def __init__(self, plane, sources, targets, sems):
        self.plane, self.sources, self.targets = plane, sources, targets
        self.load_sem, self.send_sem, self.recv_sem, self.pair_send, self.pair_recv = sems
        self.block = sources[0].shape[0]
        self.part = self.block // 2
        self.relayed = plane.chips == 4
        self.arrays = range(len(sources))

    def partner(self, distance):
        return jnp.bitwise_xor(self.plane.chip, distance)

    def greet(self, barrier):
        plane = self.plane
        targets = [plane.device(plane.chip, 1 - plane.core)]
        targets += [
            plane.device(self.partner(step), plane.core)
            for step in range(1, 3 if self.relayed else plane.chips)
        ]
        for target in targets:
            pl.semaphore_signal(barrier, inc=1, device_id=target, device_id_type=MESH_ID)
        return len(targets)

    def place(self, array, chip, core, half):
        first = (2 * chip + core) * self.block + half * self.part
        rows = pl.ds(pl.multiple_of(first, self.part), self.part)
        return self.targets[array].at[rows, pl.ds(0, self.sources[array].shape[1])]

    def mine(self, array, half):
        return self.sources[array].at[pl.ds(half * self.part, self.part)]

    def loads(self):
        plane = self.plane
        return [
            pltpu.make_async_copy(
                self.mine(array, half),
                self.place(array, plane.chip, plane.core, half),
                self.load_sem.at[array, half],
            )
            for array in self.arrays
            for half in range(2)
        ]

    def send(self, distance, half):
        plane = self.plane
        copies = []
        for array in self.arrays:
            chip, target = plane.chip, self.partner(distance)
            source = self.mine(array, half)
            if self.relayed and distance == 3:
                chip = self.partner(2 if half == 0 else 1)
                target = self.partner(1 if half == 0 else 2)
                source = self.place(array, chip, plane.core, half)
            copies.append(
                pltpu.make_async_remote_copy(
                    source,
                    self.place(array, chip, plane.core, half),
                    self.send_sem.at[array, distance - 1, half],
                    self.recv_sem.at[array, distance - 1, half],
                    device_id=plane.device(target, plane.core),
                    device_id_type=MESH_ID,
                )
            )
        return copies

    def forward(self, distance, half):
        plane = self.plane
        copies = []
        for array in self.arrays:
            place = self.place(array, self.partner(distance), plane.core, half)
            copies.append(
                pltpu.make_async_remote_copy(
                    self.mine(array, half) if distance == 0 else place,
                    place,
                    self.pair_send.at[array, distance, half],
                    self.pair_recv.at[array, distance, half],
                    device_id=plane.device(plane.chip, 1 - plane.core),
                    device_id_type=MESH_ID,
                )
            )
        return copies

    def start(self):
        if self.relayed:
            order = ((1, 1), (2, 0), (1, 0), (2, 1))
        else:
            order = [(step, half) for step in range(1, self.plane.chips) for half in range(2)]
        for distance, half in order:
            for copy in self.send(distance, half):
                copy.start()
        for copy in self.loads():
            copy.start()
        for half in range(2):
            for copy in self.forward(0, half):
                copy.start()

    def take(self, distance, half, relay):
        for copy in self.send(distance, half):
            copy.wait_recv()
        if relay:
            for copy in self.send(3, half):
                copy.start()
        for copy in self.forward(distance, half):
            copy.start()

    def stage(self, number):
        if self.relayed:
            if number == 0:
                self.take(1, 1, True)
                self.take(2, 0, True)
            elif number == 1:
                self.take(1, 0, False)
                self.take(2, 1, False)
            else:
                self.take(3, 0, False)
                self.take(3, 1, False)
        elif number == 2:
            for distance in range(1, self.plane.chips):
                for half in range(2):
                    self.take(distance, half, False)

    def arrive(self):
        for copy in self.loads():
            copy.wait()
        for distance in range(self.plane.chips):
            for half in range(2):
                for copy in self.forward(distance, half):
                    copy.wait_recv()

    def finish(self):
        for distance in range(self.plane.chips):
            for half in range(2):
                for copy in self.forward(distance, half):
                    copy.wait_send()
                if distance > 0:
                    for copy in self.send(distance, half):
                        copy.wait_send()


def gather_sems(arrays):
    chips = lax.axis_size("shard") * lax.axis_size("context") // 2
    return [
        pltpu.SemaphoreType.DMA((arrays, 2)),
        pltpu.SemaphoreType.DMA((arrays, chips - 1, 2)),
        pltpu.SemaphoreType.DMA((arrays, chips - 1, 2)),
        pltpu.SemaphoreType.DMA((arrays, chips, 2)),
        pltpu.SemaphoreType.DMA((arrays, chips, 2)),
    ]


GROUP = 128
TILE = 256


def middle_kernel(
    mesh_axes,
    mix_hbm,
    cotangent_ref,
    input_hbm,
    gain_ref,
    gate_hbm,
    up_hbm,
    down_hbm,
    normed_ref,
    out_ref,
    gain_grad,
    residual_hbm,
    hidden_hbm,
    grad_gate_hbm,
    grad_up_hbm,
    feed_hbm,
    grad_hbm,
    gate_w,
    up_w,
    down_w,
    part,
    mix_arrived,
    arrived,
    inputs,
    residual,
    stage_hidden,
    stage_gate,
    stage_up,
    stage_feed,
    part_sem,
    input_sem,
    save_sem,
    stage_sem,
    grad_sem,
    *sems,
):
    tokens, model_width = normed_ref.shape
    half = tokens // 2
    hidden_width = gate_hbm.shape[1]
    padded = gate_w.shape[1]
    groups = half // GROUP
    place, line_size = lax.axis_index("tensor"), lax.axis_size("tensor")
    own_half = pl.ds(pl.multiple_of(jnp.where(place == 0, 0, half), half), half)
    part_load = pltpu.make_async_copy(mix_hbm, part, part_sem.at[0])
    part_load.start()
    input_load = pltpu.make_async_copy(input_hbm.at[own_half], inputs, input_sem.at[0])
    input_load.start()
    if padded > hidden_width:
        spare = slice(hidden_width, padded)
        gate_w[:, spare] = jnp.zeros((model_width, padded - hidden_width), BF16)
        up_w[:, spare] = jnp.zeros((model_width, padded - hidden_width), BF16)
        down_w[:, spare] = jnp.zeros((model_width, padded - hidden_width), BF16)
    gain_grad[...] = jnp.zeros_like(gain_grad)

    def mix_turn(total, rows, own):
        values = inputs[own].astype(F32) + total
        residual[own] = values
        normed_ref[rows] = (values * inverse_rms(values) * gain_ref[...]).astype(BF16)

    def turn(total, rows, own):
        values = residual[own]
        inverse = inverse_rms(values)
        unit = values * inverse
        gain_grad[...] += jnp.sum(total * unit, axis=0, keepdims=True)
        lifted = total * gain_ref[...]
        mean = jnp.mean(lifted * unit, axis=-1, keepdims=True)
        grad = cotangent_ref[rows].astype(F32) + inverse * (lifted - unit * mean)
        residual[own] = grad
        out_ref[rows] = grad.astype(BF16)

    mix_line = Line(mesh_axes, part, mix_arrived, normed_ref, sems[:4], mix_turn)
    line = Line(mesh_axes, part, arrived, out_ref, sems[4:8], turn)
    gather = Gather(
        Plane(mesh_axes), (gate_hbm, up_hbm, down_hbm), (gate_w, up_w, down_w), sems[8:]
    )
    barrier = pltpu.get_barrier_semaphore()
    expected = mix_line.greet(barrier) + gather.greet(barrier)
    pl.semaphore_wait(barrier, expected)
    gather.start()
    part_load.wait()
    input_load.wait()
    pace = GROUP // CHUNK
    begin = pace + 2 * LAG * (line_size - 1) + 4
    mix_line.run(0, begin - 10)
    gather.stage(0)
    mix_line.run(begin - 10, begin - 4)
    gather.stage(1)
    mix_line.run(begin - 4, begin)
    gather.stage(2)
    gather.arrive()

    def both(ref, group):
        first = pl.ds(pl.multiple_of(group * GROUP, GROUP), GROUP)
        second = pl.ds(pl.multiple_of(half + group * GROUP, GROUP), GROUP)
        return first, second

    def stage_copies(group):
        slot = lax.rem(group, 2)
        copies = []
        for side, rows in enumerate(both(None, group)):
            from_rows = pl.ds(side * GROUP, GROUP)
            columns = pl.ds(0, hidden_width)
            for which, (stage, target) in enumerate(
                (
                    (stage_hidden, hidden_hbm),
                    (stage_gate, grad_gate_hbm),
                    (stage_up, grad_up_hbm),
                )
            ):
                copies.append(
                    pltpu.make_async_copy(
                        stage.at[slot, from_rows, columns],
                        target.at[rows],
                        stage_sem.at[slot, which, side],
                    )
                )
            copies.append(
                pltpu.make_async_copy(
                    stage_feed.at[slot, from_rows], feed_hbm.at[rows], stage_sem.at[slot, 3, side]
                )
            )
        return copies

    def hidden_tile(group, tile):
        first, second = both(normed_ref, group)
        slot = lax.rem(group, 2)
        columns = pl.ds(pl.multiple_of(tile * TILE, TILE), TILE)
        rows = jnp.concatenate([normed_ref[first], normed_ref[second]], axis=0)
        gate = mm_nn(rows, gate_w[:, columns])
        up = mm_nn(rows, up_w[:, columns])
        grads = jnp.concatenate([cotangent_ref[first], cotangent_ref[second]], axis=0)
        grad = mm_nn(grads, down_w[:, columns])
        sigma = jax.nn.sigmoid(gate)
        active = gate * sigma
        stage_hidden[slot, :, columns] = (active * up).astype(BF16)
        stage_gate[slot, :, columns] = (grad * up * sigma * (1.0 + gate * (1.0 - sigma))).astype(
            BF16
        )
        stage_up[slot, :, columns] = (grad * active).astype(BF16)

    def model_tile(group, tile):
        first, second = both(part, group)
        slot = lax.rem(group, 2)
        columns = pl.ds(pl.multiple_of(tile * TILE, TILE), TILE)
        back = mm_nt(stage_gate[slot], gate_w[columns, :])
        back = (back + mm_nt(stage_up[slot], up_w[columns, :])).astype(BF16)
        part[first, columns] = back[:GROUP]
        part[second, columns] = back[GROUP:]
        stage_feed[slot, :, columns] = mm_nt(stage_hidden[slot], down_w[columns, :]).astype(BF16)

    hidden_tiles, model_tiles = padded // TILE, model_width // TILE
    ticks = hidden_tiles + model_tiles
    piece = -(-ticks // pace)
    save = pltpu.make_async_copy(residual, residual_hbm, save_sem.at[0])

    def group_body(group, _):
        mix_line.source_sent(group * pace, (group + 1) * pace)

        @pl.when(group == 1)
        def _():
            save.start()

        @pl.when(group == 2)
        def _():
            save.wait()

        @pl.when(group >= 2)
        def _():
            for copy in stage_copies(group - 2):
                copy.wait()

        def piece_body(index, _):
            def tick_body(offset, _):
                tick = index * piece + offset

                @pl.when(tick < hidden_tiles)
                def _():
                    hidden_tile(group, tick)

                @pl.when(jnp.logical_and(tick >= hidden_tiles, tick < ticks))
                def _():
                    model_tile(group, tick - hidden_tiles)

                return 0

            lax.fori_loop(0, piece, tick_body, 0)

            mix_time = begin + group * pace + index

            @pl.when(mix_time < mix_line.steps)
            def _():
                mix_line.step(mix_time)

            @pl.when(group >= 1)
            def _():
                line.step((group - 1) * pace + index)

            return 0

        lax.fori_loop(0, pace, piece_body, 0)
        for copy in stage_copies(group):
            copy.start()
        return 0

    lax.fori_loop(0, groups, group_body, 0)
    line.run((groups - 1) * pace, line.steps)
    grad_save = pltpu.make_async_copy(residual, grad_hbm, grad_sem.at[0])
    grad_save.start()
    for group in range(max(groups - 2, 0), groups):
        for copy in stage_copies(group):
            copy.wait()
    gather.finish()
    mix_line.finish(source_waits=False)
    line.finish()
    grad_save.wait()


def middle(mesh_axes, collective, mix, cotangent, inputs, gain, gate_w, up_w, down_w):
    tokens, model_width = mix.shape
    hidden_width = gate_w.shape[1]
    padded = -(-hidden_width // TILE) * TILE
    whole = pl.BlockSpec(memory_space=pltpu.VMEM)
    remote = pl.BlockSpec(memory_space=pl.ANY)
    group_rows = 2 * GROUP
    return pl.pallas_call(
        partial(middle_kernel, mesh_axes),
        in_specs=[remote, whole, remote, whole, remote, remote, remote],
        out_specs=[whole, whole, whole] + [remote] * 6,
        out_shape=[
            jax.ShapeDtypeStruct((tokens, model_width), BF16),
            jax.ShapeDtypeStruct((tokens, model_width), BF16),
            jax.ShapeDtypeStruct((1, model_width), F32),
            jax.ShapeDtypeStruct((tokens // 2, model_width), F32),
            jax.ShapeDtypeStruct((tokens, hidden_width), BF16),
            jax.ShapeDtypeStruct((tokens, hidden_width), BF16),
            jax.ShapeDtypeStruct((tokens, hidden_width), BF16),
            jax.ShapeDtypeStruct((tokens, model_width), BF16),
            jax.ShapeDtypeStruct((tokens // 2, model_width), F32),
        ],
        scratch_shapes=[
            pltpu.VMEM((model_width, padded), BF16),
            pltpu.VMEM((model_width, padded), BF16),
            pltpu.VMEM((model_width, padded), BF16),
            pltpu.VMEM((tokens, model_width), BF16),
            pltpu.VMEM((tokens, model_width), BF16),
            pltpu.VMEM((tokens, model_width), BF16),
            pltpu.VMEM((tokens // 2, model_width), BF16),
            pltpu.VMEM((tokens // 2, model_width), F32),
            pltpu.VMEM((2, group_rows, padded), BF16),
            pltpu.VMEM((2, group_rows, padded), BF16),
            pltpu.VMEM((2, group_rows, padded), BF16),
            pltpu.VMEM((2, group_rows, model_width), BF16),
            pltpu.SemaphoreType.DMA((1,)),
            pltpu.SemaphoreType.DMA((1,)),
            pltpu.SemaphoreType.DMA((1,)),
            pltpu.SemaphoreType.DMA((2, 4, 2)),
            pltpu.SemaphoreType.DMA((1,)),
        ]
        + line_sems(tokens)
        + line_sems(tokens)
        + gather_sems(3),
        compiler_params=pltpu.CompilerParams(
            collective_id=collective, has_side_effects=True, vmem_limit_bytes=61 << 20
        ),
        cost_estimate=pl.CostEstimate(
            flops=tokens * model_width * hidden_width * 12,
            bytes_accessed=360_000_000,
            transcendentals=tokens * hidden_width,
        ),
        name="middle",
    )(mix, cotangent, inputs, gain, gate_w, up_w, down_w)


def output_kernel(
    mesh_axes,
    part,
    residual,
    normed_ref,
    cotangent_ref,
    hidden_ref,
    grad_gate_ref,
    grad_up_ref,
    out_ref,
    grads_hbm,
    arrived,
    stage,
    stage_sem,
    *sems,
):
    model_width = normed_ref.shape[1]
    tiles = model_width // TILE

    def turn(total, rows, own):
        out_ref[rows] = (residual[own] + total).astype(BF16)

    line = Line(mesh_axes, part, arrived, out_ref, sems, turn)
    barrier = pltpu.get_barrier_semaphore()
    pl.semaphore_wait(barrier, line.greet(barrier))

    def stage_copy(tile):
        rows = pl.ds(pl.multiple_of(tile * TILE, TILE), TILE)
        slot = lax.rem(tile, 2)
        return pltpu.make_async_copy(stage.at[slot], grads_hbm.at[:, rows], stage_sem.at[slot])

    def weight_tile(time):
        tile = jnp.clip(time, 0, tiles - 1)
        slot = lax.rem(tile, 2)
        columns = pl.ds(pl.multiple_of(tile * TILE, TILE), TILE)

        @pl.when(jnp.logical_and(time < tiles, time >= 2))
        def _():
            stage_copy(tile - 2).wait()

        @pl.when(time < tiles)
        def _():
            rows = normed_ref[:, columns]
            stage[slot, 0] = mm_tn(rows, grad_gate_ref[...]).astype(BF16)
            stage[slot, 1] = mm_tn(rows, grad_up_ref[...]).astype(BF16)
            stage[slot, 2] = mm_tn(cotangent_ref[:, columns], hidden_ref[...]).astype(BF16)
            stage_copy(tile).start()

    line.run(0, line.steps, weight_tile)
    for tile in range(max(tiles - 2, 0), tiles):
        stage_copy(tile).wait()
    line.finish()


def output_line(
    mesh_axes, collective, part, residual, normed, cotangent, hidden_low, grad_gate, grad_up
):
    tokens, model_width = part.shape
    hidden_width = hidden_low.shape[1]
    whole = pl.BlockSpec(memory_space=pltpu.VMEM)
    return pl.pallas_call(
        partial(output_kernel, mesh_axes),
        in_specs=[whole] * 7,
        out_specs=[whole, pl.BlockSpec(memory_space=pl.ANY)],
        out_shape=[
            jax.ShapeDtypeStruct((tokens, model_width), BF16),
            jax.ShapeDtypeStruct((3, model_width, hidden_width), BF16),
        ],
        scratch_shapes=[
            pltpu.VMEM((tokens, model_width), BF16),
            pltpu.VMEM((2, 3, TILE, hidden_width), BF16),
            pltpu.SemaphoreType.DMA((2,)),
        ]
        + line_sems(tokens),
        compiler_params=pltpu.CompilerParams(
            collective_id=collective, has_side_effects=True, vmem_limit_bytes=56 << 20
        ),
        cost_estimate=pl.CostEstimate(
            flops=tokens * model_width * hidden_width * 6,
            bytes_accessed=360_000_000,
            transcendentals=0,
        ),
        name="output_line",
    )(part, residual, normed, cotangent, hidden_low, grad_gate, grad_up)


def input_kernel(
    mesh_axes,
    part,
    hidden_ref,
    residual_grad,
    gain_ref,
    grads_hbm,
    out_ref,
    gain_grad,
    share_gate,
    share_up,
    share_down,
    arrived,
    own,
    other,
    remote,
    load_sem,
    pair_send,
    pair_recv,
    chip_send,
    chip_recv,
    *sems,
):
    plane = Plane(mesh_axes)
    chips = plane.chips
    block = own.shape[2]
    gain_grad[...] = jnp.zeros_like(gain_grad)

    def turn(total, rows, own_rows):
        values = hidden_ref[rows].astype(F32)
        inverse = inverse_rms(values)
        unit = values * inverse
        gain_grad[...] += jnp.sum(total * unit, axis=0, keepdims=True)
        lifted = total * gain_ref[...]
        mean = jnp.mean(lifted * unit, axis=-1, keepdims=True)
        grad = residual_grad[own_rows] + inverse * (lifted - unit * mean)
        out_ref[rows] = grad.astype(BF16)

    line = Line(mesh_axes, part, arrived, out_ref, sems, turn)
    barrier = pltpu.get_barrier_semaphore()
    expected = line.greet(barrier) + plane.greet(barrier)
    pl.semaphore_wait(barrier, expected)

    def rows_of(slot, core):
        return pl.ds(pl.multiple_of((2 * plane.ahead(slot) + core) * block, block), block)

    def load(slot):
        return pltpu.make_async_copy(
            grads_hbm.at[:, rows_of(slot, plane.core)], own.at[slot], load_sem.at[slot]
        )

    def pair_copy(slot):
        return pltpu.make_async_remote_copy(
            grads_hbm.at[:, rows_of(slot, 1 - plane.core)],
            other.at[slot],
            pair_send.at[slot],
            pair_recv.at[slot],
            device_id=plane.device(plane.chip, 1 - plane.core),
            device_id_type=MESH_ID,
        )

    def chip_copy(slot):
        return pltpu.make_async_remote_copy(
            own.at[slot],
            remote.at[slot - 1],
            chip_send.at[slot - 1],
            chip_recv.at[slot - 1],
            device_id=plane.device(plane.ahead(slot), plane.core),
            device_id_type=MESH_ID,
        )

    def start(index, _):
        slot = lax.rem(index + 1, chips)
        pair_copy(slot).start()
        load(slot).start()
        return 0

    lax.fori_loop(0, chips, start, 0)
    strip = 32

    def combine(time):
        slot = lax.rem(jnp.clip(time, 0, chips - 1) + 1, chips)

        @pl.when(time < chips)
        def _():
            load(slot).wait()
            pair_copy(slot).wait_recv()

            def add(index, _):
                rows = pl.ds(pl.multiple_of(index * strip, strip), strip)
                for which in range(3):
                    total = own[slot, which, rows].astype(F32) + other[slot, which, rows].astype(F32)
                    own[slot, which, rows] = total.astype(BF16)
                return 0

            lax.fori_loop(0, block // strip, add, 0)

        @pl.when(time < chips - 1)
        def _():
            chip_copy(slot).start()

    line.run(0, line.steps, combine)

    def arrive(index, _):
        chip_copy(index).wait_recv()
        return 0

    lax.fori_loop(1, chips, arrive, 0)

    def total(index, _):
        rows = pl.ds(pl.multiple_of(index * strip, strip), strip)

        def whole(which):
            def add(slot, value):
                return value + remote[slot, which, rows].astype(F32)

            return lax.fori_loop(0, chips - 1, add, own[0, which, rows].astype(F32))

        share_gate[rows] = whole(0)
        share_up[rows] = whole(1)
        share_down[rows] = whole(2)
        return 0

    lax.fori_loop(0, block // strip, total, 0)

    def sent(index, _):
        pair_copy(index).wait_send()
        return 0

    lax.fori_loop(0, chips, sent, 0)

    def chip_sent(index, _):
        chip_copy(index).wait_send()
        return 0

    lax.fori_loop(1, chips, chip_sent, 0)
    line.finish()


def input_line(mesh_axes, collective, part, hidden, residual_grad, gain, grads):
    tokens, model_width = part.shape
    hidden_width = grads.shape[2]
    chips = lax.axis_size("shard") * lax.axis_size("context") // 2
    block = model_width // (2 * chips)
    whole = pl.BlockSpec(memory_space=pltpu.VMEM)
    return pl.pallas_call(
        partial(input_kernel, mesh_axes),
        in_specs=[whole] * 4 + [pl.BlockSpec(memory_space=pl.ANY)],
        out_specs=[whole] * 5,
        out_shape=[
            jax.ShapeDtypeStruct((tokens, model_width), BF16),
            jax.ShapeDtypeStruct((1, model_width), F32),
        ]
        + [jax.ShapeDtypeStruct((block, hidden_width), F32)] * 3,
        scratch_shapes=[
            pltpu.VMEM((tokens, model_width), BF16),
            pltpu.VMEM((chips, 3, block, hidden_width), BF16),
            pltpu.VMEM((chips, 3, block, hidden_width), BF16),
            pltpu.VMEM((chips - 1, 3, block, hidden_width), BF16),
            pltpu.SemaphoreType.DMA((chips,)),
            pltpu.SemaphoreType.DMA((chips,)),
            pltpu.SemaphoreType.DMA((chips,)),
            pltpu.SemaphoreType.DMA((chips - 1,)),
            pltpu.SemaphoreType.DMA((chips - 1,)),
        ]
        + line_sems(tokens),
        compiler_params=pltpu.CompilerParams(
            collective_id=collective, has_side_effects=True, vmem_limit_bytes=58 << 20
        ),
        cost_estimate=pl.CostEstimate(
            flops=tokens * model_width * 8, bytes_accessed=360_000_000, transcendentals=0
        ),
        name="input_line",
    )(part, hidden, residual_grad, gain, grads)


def front_kernel(
    mesh_axes,
    hidden_ref,
    gain_ref,
    query_ref,
    forget_ref,
    input_ref,
    gate_ref,
    normed_hbm,
    pre_hbm,
    full_hbm,
    normed,
    pre,
    full,
    save_sem,
    normed_sem,
    pre_sem,
    send_sem,
    recv_sem,
    pair_send,
    pair_recv,
):
    plane = Plane(mesh_axes)
    chips = plane.chips
    tokens, model_width = hidden_ref.shape
    block, width = query_ref.shape
    part = block // 2
    relayed = chips == 4

    def partner(distance):
        return jnp.bitwise_xor(plane.chip, distance)

    def rows_of(chip, core, half):
        return pl.ds(pl.multiple_of((2 * chip + core) * block + half * part, part), part)

    def copy(rows, distance, half, chip):
        return pltpu.make_async_remote_copy(
            full.at[rows],
            full.at[rows],
            send_sem.at[distance - 1, half],
            recv_sem.at[distance - 1, half],
            device_id=plane.device(chip, plane.core),
            device_id_type=MESH_ID,
        )

    def send(distance, half):
        if relayed and distance == 3:
            through, target = (2, 1) if half == 0 else (1, 2)
            return copy(
                rows_of(partner(through), plane.core, half), 3, half, partner(target)
            )
        return copy(rows_of(plane.chip, plane.core, half), distance, half, partner(distance))

    def forward(distance, half):
        rows = rows_of(partner(distance), plane.core, half)
        return pltpu.make_async_remote_copy(
            full.at[rows],
            full.at[rows],
            pair_send.at[distance, half],
            pair_recv.at[distance, half],
            device_id=plane.device(plane.chip, 1 - plane.core),
            device_id_type=MESH_ID,
        )

    own = pl.ds(pl.multiple_of((2 * plane.chip + plane.core) * block, block), block)
    for which, ref in enumerate((query_ref, forget_ref, input_ref, gate_ref)):
        full[own, which * width : (which + 1) * width] = ref[...]
    barrier = pltpu.get_barrier_semaphore()
    targets = [plane.device(plane.chip, 1 - plane.core)]
    targets += [
        plane.device(partner(step), plane.core)
        for step in range(1, 3 if relayed else chips)
    ]
    for target in targets:
        pl.semaphore_signal(barrier, inc=1, device_id=target, device_id_type=MESH_ID)
    pl.semaphore_wait(barrier, len(targets))
    if relayed:
        for distance, half in ((1, 1), (2, 0), (1, 0), (2, 1)):
            send(distance, half).start()
    else:
        for distance in range(1, chips):
            send(distance, 0).start()
            send(distance, 1).start()
    for half in range(2):
        forward(0, half).start()

    def norm(index, _):
        rows = pl.ds(pl.multiple_of(index * 128, 128), 128)
        values = hidden_ref[rows].astype(F32)
        normed[rows] = (values * inverse_rms(values) * gain_ref[...]).astype(BF16)
        return 0

    lax.fori_loop(0, tokens // 128, norm, 0)
    normed_save = pltpu.make_async_copy(normed, normed_hbm, normed_sem.at[0])
    normed_save.start()
    row_tile, column_tile = 256, 512

    def pre_save(index):
        rows = pl.ds(pl.multiple_of(index * row_tile, row_tile), row_tile)
        return pltpu.make_async_copy(pre.at[rows], pre_hbm.at[rows], pre_sem.at[index])

    def product(distance):
        depth = pl.ds(pl.multiple_of(2 * partner(distance) * block, 2 * block), 2 * block)

        def row_body(index, _):
            rows = pl.ds(pl.multiple_of(index * row_tile, row_tile), row_tile)
            left = normed[rows, depth]

            def column_body(column, _):
                columns = pl.ds(pl.multiple_of(column * column_tile, column_tile), column_tile)
                value = mm_nn(left, full[depth, columns])
                if distance > 0:
                    value = value + pre[rows, columns]
                pre[rows, columns] = value
                return 0

            lax.fori_loop(0, full.shape[1] // column_tile, column_body, 0)
            if distance == chips - 1:
                pre_save(index).start()
            return 0

        lax.fori_loop(0, tokens // row_tile, row_body, 0)

    def full_save(distance):
        depth = pl.ds(pl.multiple_of(2 * partner(distance) * block, 2 * block), 2 * block)
        return pltpu.make_async_copy(full.at[depth], full_hbm.at[depth], save_sem.at[distance])

    def use(distance):
        for half in range(2):
            forward(distance, half).wait_recv()
        full_save(distance).start()
        product(distance)

    use(0)
    if relayed:
        for distance, half in ((1, 1), (2, 0), (1, 0), (2, 1)):
            send(distance, half).wait_recv()
            if (distance, half) in ((1, 1), (2, 0)):
                send(3, half).start()
            forward(distance, half).start()
        use(1)
        use(2)
        for half in range(2):
            send(3, half).wait_recv()
            forward(3, half).start()
        use(3)
    else:
        for distance in range(1, chips):
            for half in range(2):
                send(distance, half).wait_recv()
                forward(distance, half).start()
            if distance > 1:
                use(distance - 1)
        use(chips - 1)
    for distance in range(chips):
        for half in range(2):
            if distance > 0:
                send(distance, half).wait_send()
            forward(distance, half).wait_send()
        full_save(distance).wait()
    normed_save.wait()
    for index in range(tokens // row_tile):
        pre_save(index).wait()


def front(mesh_axes, collective, hidden, gain, shards):
    tokens, model_width = hidden.shape
    block, width = shards[0].shape
    all_width = width * len(shards)
    chips = lax.axis_size("shard") * lax.axis_size("context") // 2
    whole = pl.BlockSpec(memory_space=pltpu.VMEM)
    remote = pl.BlockSpec(memory_space=pl.ANY)
    return pl.pallas_call(
        partial(front_kernel, mesh_axes),
        in_specs=[whole] * 6,
        out_specs=[remote] * 3,
        out_shape=[
            jax.ShapeDtypeStruct((tokens, model_width), BF16),
            jax.ShapeDtypeStruct((tokens, all_width), F32),
            jax.ShapeDtypeStruct((model_width, all_width), BF16),
        ],
        scratch_shapes=[
            pltpu.VMEM((tokens, model_width), BF16),
            pltpu.VMEM((tokens, all_width), F32),
            pltpu.VMEM((model_width, all_width), BF16),
            pltpu.SemaphoreType.DMA((chips,)),
            pltpu.SemaphoreType.DMA((1,)),
            pltpu.SemaphoreType.DMA((tokens // 256,)),
            pltpu.SemaphoreType.DMA((chips - 1, 2)),
            pltpu.SemaphoreType.DMA((chips - 1, 2)),
            pltpu.SemaphoreType.DMA((chips, 2)),
            pltpu.SemaphoreType.DMA((chips, 2)),
        ],
        compiler_params=pltpu.CompilerParams(
            collective_id=collective, has_side_effects=True, vmem_limit_bytes=48 << 20
        ),
        cost_estimate=pl.CostEstimate(
            flops=2 * tokens * model_width * all_width,
            bytes_accessed=160_000_000,
            transcendentals=0,
        ),
        name="front",
    )(hidden, gain, *shards)


def small_sum_kernel(
    mesh_axes, value, local_ref, total_ref, near, far, near_send, near_recv, far_send, far_recv
):
    shard_size, context_size = lax.axis_size("shard"), lax.axis_size("context")
    line_size = lax.axis_size("tensor")
    group = shard_size * context_size
    place = lax.axis_index("shard") * context_size + lax.axis_index("context")
    line_place = lax.axis_index("tensor")

    def device(position, line_position):
        places = {
            "shard": position // context_size,
            "context": lax.rem(position, context_size),
            "tensor": line_position,
        }
        return tuple(places[axis] for axis in mesh_axes)

    def near_target(step):
        return device(lax.rem(place + step, group), line_place)

    def far_target(step):
        return device(place, lax.rem(line_place + step, line_size))

    def near_copy(step):
        return pltpu.make_async_remote_copy(
            value,
            near.at[step - 1],
            near_send.at[step - 1],
            near_recv.at[step - 1],
            device_id=near_target(step),
            device_id_type=MESH_ID,
        )

    def far_copy(step):
        return pltpu.make_async_remote_copy(
            local_ref,
            far.at[step - 1],
            far_send.at[step - 1],
            far_recv.at[step - 1],
            device_id=far_target(step),
            device_id_type=MESH_ID,
        )

    barrier = pltpu.get_barrier_semaphore()
    for step in range(1, group):
        pl.semaphore_signal(barrier, inc=1, device_id=near_target(step), device_id_type=MESH_ID)
    for step in range(1, line_size):
        pl.semaphore_signal(barrier, inc=1, device_id=far_target(step), device_id_type=MESH_ID)
    pl.semaphore_wait(barrier, group + line_size - 2)
    for step in range(1, group):
        near_copy(step).start()
    total = value[...]
    for step in range(1, group):
        near_copy(step).wait_recv()
        total = total + near[step - 1]
    local_ref[...] = total
    for step in range(1, line_size):
        far_copy(step).start()
    for step in range(1, line_size):
        far_copy(step).wait_recv()
        total = total + far[step - 1]
    total_ref[...] = total
    for step in range(1, group):
        near_copy(step).wait_send()
    for step in range(1, line_size):
        far_copy(step).wait_send()


def small_sum(mesh_axes, collective, values):
    flat = jnp.concatenate([value.reshape(-1) for value in values])
    lanes = -(-flat.shape[0] // 1024) * 128
    flat = jnp.pad(flat, (0, 8 * lanes - flat.shape[0])).reshape(8, lanes)
    group = lax.axis_size("shard") * lax.axis_size("context")
    line_size = lax.axis_size("tensor")
    whole = pl.BlockSpec(memory_space=pltpu.VMEM)
    local, total = pl.pallas_call(
        partial(small_sum_kernel, mesh_axes),
        in_specs=[whole],
        out_specs=[whole] * 2,
        out_shape=[jax.ShapeDtypeStruct((8, lanes), F32)] * 2,
        scratch_shapes=[
            pltpu.VMEM((group - 1, 8, lanes), F32),
            pltpu.VMEM((line_size - 1, 8, lanes), F32),
            pltpu.SemaphoreType.DMA((group - 1,)),
            pltpu.SemaphoreType.DMA((group - 1,)),
            pltpu.SemaphoreType.DMA((line_size - 1,)),
            pltpu.SemaphoreType.DMA((line_size - 1,)),
        ],
        compiler_params=pltpu.CompilerParams(collective_id=collective, has_side_effects=True),
        cost_estimate=pl.CostEstimate(
            flops=8 * lanes * group, bytes_accessed=20_000_000, transcendentals=0
        ),
        name="small_sum",
    )(flat)
    return local.reshape(-1), total.reshape(-1)


def local(
    mesh_axes,
    hidden,
    segment_ids,
    norm1_gain,
    w_query,
    w_forget,
    w_input,
    w_gate_out,
    forget_floor,
    head_gain,
    w_out,
    norm2_gain,
    w_ffn_gate,
    w_ffn_up,
    w_ffn_down,
    out_grad,
):
    sequences, span_len, model_width = hidden.shape
    tokens = sequences * span_len
    head_count, key_dim = forget_floor.shape
    width = head_count * key_dim
    key_scale = key_dim ** (-0.5)
    both = ("shard", "context")
    gain_one, gain_two = norm1_gain.reshape(1, -1), norm2_gain.reshape(1, -1)
    hidden_rows = hidden.reshape(tokens, model_width)
    normed_one, pre, mixer_full = front(
        mesh_axes, 4, hidden_rows, gain_one, (w_query, w_forget, w_input, w_gate_out)
    )
    pre, w_out = lax.optimization_barrier((pre, w_out))
    out_full = lax.all_gather(w_out, both, axis=1, tiled=True)
    open_part = (1.0 - forget_floor).reshape(1, width)
    counts, keep, flags, last_count = row_flags(segment_ids)
    mixed_local, lead, starts, runs, state_end, run_end = mixer_forward(
        pre, open_part, counts, keep, flags, head_count, key_scale
    )
    decay = (jnp.exp(run_end) * (last_count == 0).astype(F32)).reshape(head_count, 1, key_dim)
    ids = segment_ids.reshape(-1).astype(F32)
    carry, link_in = state_before(state_end, decay, ids[0], ids[-1], "context")
    gain_row = head_gain.reshape(1, -1)
    mixed, gated_low = gate_forward(
        mixed_local, lead, carry.astype(BF16), pre, gain_row, keep, key_scale
    )
    mix_part = jnp.dot(gated_low, out_full, preferred_element_type=F32).astype(BF16)
    grad_rows = out_grad.reshape(tokens, model_width)
    (
        normed_two,
        grad_mix_low,
        grad_norm_two,
        residual,
        hidden_low,
        grad_gate_low,
        grad_up_low,
        feed_part,
        grad_residual,
    ) = middle(
        mesh_axes,
        2,
        mix_part,
        grad_rows,
        hidden_rows,
        gain_two,
        w_ffn_gate,
        w_ffn_up,
        w_ffn_down.T,
    )
    output_rows, grads_ffn = output_line(
        mesh_axes,
        1,
        feed_part,
        residual,
        normed_two,
        grad_rows,
        hidden_low,
        grad_gate_low,
        grad_up_low,
    )
    grad_out = jnp.einsum("tv,td->vd", gated_low, grad_mix_low, preferred_element_type=F32)
    grad_gated = jnp.einsum("td,vd->tv", grad_mix_low, out_full, preferred_element_type=F32)
    grad_mixed, grad_gate_pre, grad_head_part, back = gate_backward(
        grad_gated, mixed, lead, pre, gain_row, keep, head_count, key_scale
    )
    after = grad_after(back, decay, link_in, "context")
    grad_pre, grad_floor_part = mixer_backward(
        pre,
        grad_mixed,
        grad_gate_pre,
        starts,
        runs,
        carry,
        after,
        open_part,
        counts,
        keep,
        flags,
    )
    grad_mixer = jnp.einsum("td,tk->dk", normed_one, grad_pre, preferred_element_type=F32)
    back_one = jnp.einsum("tk,dk->td", grad_pre, mixer_full, preferred_element_type=F32)
    input_rows, grad_norm_one, share_gate, share_up, share_down = input_line(
        mesh_axes, 3, back_one.astype(BF16), hidden_rows, grad_residual, gain_one, grads_ffn
    )
    near, total = small_sum(
        mesh_axes, 5, (grad_norm_one, grad_norm_two, grad_head_part, grad_floor_part)
    )
    shares = lax.axis_size("shard") * lax.axis_size("context")
    position = lax.axis_index("shard") * lax.axis_size("context") + lax.axis_index("context")

    def own_slice(values, first, length):
        values = values[first : first + length].reshape(shares, length // shares)
        return lax.dynamic_index_in_dim(values, position, 0, False)

    floor_total = near[2 * model_width + key_dim : 2 * model_width + key_dim + width]
    floor_total = floor_total.reshape(head_count, shares, key_dim // shares)

    def share(values, dim):
        return lax.psum_scatter(
            values.astype(BF16), both, scatter_dimension=dim, tiled=True
        ).astype(F32)

    share_mixer = share(grad_mixer, 0)
    return (
        output_rows.reshape(hidden.shape),
        input_rows.reshape(hidden.shape),
        own_slice(total, 0, model_width),
        share_mixer[:, :width],
        share_mixer[:, width : 2 * width],
        share_mixer[:, 2 * width : 3 * width],
        share_mixer[:, 3 * width :],
        lax.dynamic_index_in_dim(floor_total, position, 1, False),
        own_slice(total, 2 * model_width, key_dim),
        share(grad_out, 1),
        own_slice(total, model_width, model_width),
        share_gate,
        share_up,
        share_down.T,
    )


def solution(mesh):
    in_specs = (
        P("shard", "context", None),
        P("shard", "context"),
        P(),
        P(("shard", "context"), "tensor"),
        P(("shard", "context"), "tensor"),
        P(("shard", "context"), "tensor"),
        P(("shard", "context"), "tensor"),
        P("tensor", None),
        P(),
        P("tensor", ("shard", "context")),
        P(),
        P(("shard", "context"), "tensor"),
        P(("shard", "context"), "tensor"),
        P("tensor", ("shard", "context")),
        P("shard", "context", None),
    )
    out_specs = (
        P("shard", "context", None),
        P("shard", "context", None),
        P(("shard", "context")),
        P(("shard", "context"), "tensor"),
        P(("shard", "context"), "tensor"),
        P(("shard", "context"), "tensor"),
        P(("shard", "context"), "tensor"),
        P("tensor", ("shard", "context")),
        P(("shard", "context")),
        P("tensor", ("shard", "context")),
        P(("shard", "context")),
        P(("shard", "context"), "tensor"),
        P(("shard", "context"), "tensor"),
        P("tensor", ("shard", "context")),
    )
    return jax.shard_map(
        partial(local, mesh.axis_names), mesh=mesh, in_specs=in_specs, out_specs=out_specs, check_vma=False)
```

```python
from functools import partial

import jax
import jax.numpy as jnp
from jax import lax
from jax.experimental import pallas as pl
from jax.experimental.pallas import tpu as pltpu
from jax.sharding import PartitionSpec as P

EPSILON = 1e-05


BLOCK = 128
F32 = jnp.float32
BF16 = jnp.bfloat16


def mm(a, b, dims):
    return lax.dot_general(a, b, (dims, ((), ())), preferred_element_type=F32)


def mm_nn(a, b):
    return mm(a, b, ((1,), (0,)))


def mm_nt(a, b):
    return mm(a, b, ((1,), (1,)))


def mm_tn(a, b):
    return mm(a, b, ((0,), (0,)))


def split_sum(tri, values):
    high = values.astype(BF16)
    low = (values - high.astype(F32)).astype(BF16)
    return mm_nn(tri, high) + mm_nn(tri, low)


def block_masks(counts, flags_row):
    rows = counts.shape[0]
    row_ids = lax.broadcasted_iota(jnp.int32, (rows, rows), 0)
    col_ids = lax.broadcasted_iota(jnp.int32, (rows, rows), 1)
    linked = jnp.logical_and(counts == flags_row[0:1], row_ids >= col_ids)
    fresh = (counts == flags_row[1:2, 0:1]).astype(F32)
    tail = (counts == flags_row[2:3, 0:1]).astype(F32)
    closing = (flags_row[1:2, 0:1] == flags_row[2:3, 0:1]).astype(F32)
    return row_ids, col_ids, linked, fresh, tail, closing


def gate_backward_kernel(
    head_count,
    key_scale,
    grad_ref,
    mixed_ref,
    lead_ref,
    gate_ref,
    gain_ref,
    keep_ref,
    grad_mixed_ref,
    grad_gate_ref,
    grad_gain_ref,
    back_ref,
):
    lanes = gain_ref.shape[1]

    @pl.when(pl.program_id(0) == 0)
    def _():
        grad_gain_ref[...] = jnp.zeros_like(grad_gain_ref)
        back_ref[...] = jnp.zeros_like(back_ref)

    gain = gain_ref[...]
    total = jnp.zeros_like(gain)
    for head in range(head_count):
        part = slice(head * lanes, (head + 1) * lanes)
        mixed, gate, grad = mixed_ref[:, part], gate_ref[:, part], grad_ref[:, part]
        inverse = lax.rsqrt(jnp.mean(mixed * mixed, axis=-1, keepdims=True) + EPSILON)
        unit = mixed * inverse
        sigma = jax.nn.sigmoid(gate)
        scaled = grad * unit
        total = total + jnp.sum(scaled * (gate * sigma), axis=0, keepdims=True)
        grad_gate = scaled * gain * sigma * (1.0 + gate * (1.0 - sigma))
        grad_gate_ref[:, part] = grad_gate.astype(BF16)
        lifted = grad * gain * (gate * sigma)
        mean = jnp.mean(lifted * unit, axis=-1, keepdims=True)
        grad_mixed = inverse * (lifted - unit * mean) * (key_scale * keep_ref[...])
        grad_mixed = grad_mixed.astype(BF16)
        grad_mixed_ref[:, part] = grad_mixed
        back_ref[head] += mm_tn(grad_mixed, lead_ref[:, part])
    grad_gain_ref[...] += total


def gate_backward(grad, mixed, lead, pre, gain, keep, head_count, key_scale):
    tokens, width = mixed.shape
    lanes = gain.shape[1]
    rows = 2 * BLOCK
    return pl.pallas_call(
        partial(gate_backward_kernel, head_count, key_scale),
        grid=(tokens // rows,),
        in_specs=[
            pl.BlockSpec((rows, width), lambda i: (i, 0)),
            pl.BlockSpec((rows, width), lambda i: (i, 0)),
            pl.BlockSpec((rows, width), lambda i: (i, 0)),
            pl.BlockSpec((rows, width), lambda i: (i, 3)),
            pl.BlockSpec((1, lanes), lambda i: (0, 0)),
            pl.BlockSpec((rows, 1), lambda i: (i, 0)),
        ],
        out_specs=[
            pl.BlockSpec((rows, width), lambda i: (i, 0)),
            pl.BlockSpec((rows, width), lambda i: (i, 0)),
            pl.BlockSpec((1, lanes), lambda i: (0, 0)),
            pl.BlockSpec((head_count, lanes, lanes), lambda i: (0, 0, 0)),
        ],
        out_shape=[
            jax.ShapeDtypeStruct((tokens, width), BF16),
            jax.ShapeDtypeStruct((tokens, width), BF16),
            jax.ShapeDtypeStruct((1, lanes), F32),
            jax.ShapeDtypeStruct((head_count, lanes, lanes), F32),
        ],
        compiler_params=pltpu.CompilerParams(
            dimension_semantics=("arbitrary",), vmem_limit_bytes=40 << 20
        ),
        cost_estimate=pl.CostEstimate(
            flops=tokens * width * 300,
            bytes_accessed=tokens * width * 18,
            transcendentals=tokens * width,
        ),
        name="gate_backward",
    )(grad, mixed, lead, pre, gain, keep)


def mixer_backward_kernel(
    head_count,
    pre_ref,
    grad_mixed_ref,
    grad_gate_ref,
    start_ref,
    run_ref,
    carry_ref,
    after_ref,
    open_ref,
    count_ref,
    keep_ref,
    flags_ref,
    grads_ref,
    floor_ref,
    grad_scr,
    lifted_scr,
    lowered_scr,
    moved_scr,
    value_scr,
):
    width = open_ref.shape[1]
    lanes = width // head_count

    @pl.when(pl.program_id(0) == 0)
    def _():
        grad_scr[...] = after_ref[...]
        floor_ref[...] = jnp.zeros_like(floor_ref)

    counts, keep = count_ref[...], keep_ref[...]
    flags = flags_ref[0]
    row_ids, col_ids, linked, fresh, tail, closing = block_masks(counts, flags)
    tri = (row_ids >= col_ids).astype(BF16)
    tri_back = (row_ids <= col_ids).astype(BF16)
    query_pre = pre_ref[:, :width]
    values = pre_ref[:, 2 * width : 3 * width].astype(BF16)
    opened = open_ref[...]
    closed = jax.nn.sigmoid(-pre_ref[:, width : 2 * width])
    keys = opened * closed
    cum = split_sum(tri, jnp.log1p(-keys))
    rows = cum.shape[0]
    ending = cum[rows - 1 : rows, :]
    rise, fall = jnp.exp(cum), jnp.exp(-cum) * keep
    shift = jnp.exp(ending - cum) * (keep * tail)
    sigma_query = jax.nn.sigmoid(query_pre)
    lifted = (query_pre * sigma_query * rise).astype(BF16)
    lowered = (keys * fall).astype(BF16)
    moved = (keys * shift).astype(BF16)
    fresh_lifted = (lifted.astype(F32) * fresh).astype(BF16)
    end_decay = jnp.exp(ending) * closing
    lead_in = jnp.exp(run_ref[0]) * (flags[1:2, 0:1] == 0).astype(F32)
    for head in range(head_count):
        part = slice(head * lanes, (head + 1) * lanes)
        grad_out, value = grad_mixed_ref[:, part], values[:, part]
        lift, lower, move = lifted[:, part], lowered[:, part], moved[:, part]
        scores = jnp.where(linked, mm_nt(lift, lower), 0.0).astype(BF16)
        pulls = jnp.where(linked, mm_nt(grad_out, value), 0.0).astype(BF16)
        state = start_ref[0, head] + lead_in[:, part] * carry_ref[head]
        grad_state = grad_scr[head]
        grad_low = grad_state.astype(BF16)
        lifted_scr[:, part] = mm_nn(pulls, lower) + fresh * mm_nn(grad_out, state.astype(BF16))
        lowered_scr[:, part] = mm_tn(pulls, lift)
        grad_moved = mm_nn(value, grad_low)
        moved_scr[:, part] = grad_moved
        grads_ref[:, 2 * width + head * lanes : 2 * width + (head + 1) * lanes] = (
            mm_tn(scores, grad_out) + mm_nt(move, grad_low)
        ).astype(BF16)
        value_scr[:, part] = jnp.sum(
            grad_moved * move.astype(F32), axis=0, keepdims=True
        ) + end_decay[:, part] * jnp.sum(state * grad_state, axis=0, keepdims=True)
        grad_scr[head] = grad_state * end_decay[:, part] + mm_tn(grad_out, fresh_lifted[:, part])
    grad_lifted, grad_lowered, grad_moved = lifted_scr[...], lowered_scr[...], moved_scr[...]
    grad_cum = (
        grad_lifted * lifted.astype(F32)
        - grad_lowered * lowered.astype(F32)
        - grad_moved * moved.astype(F32)
    )
    grad_decay = split_sum(tri_back, grad_cum) + value_scr[...]
    key_total = grad_lowered * fall + grad_moved * shift - grad_decay / (1.0 - keys)
    floor_ref[...] -= jnp.sum(key_total * closed, axis=0, keepdims=True)
    grads_ref[:, :width] = (
        grad_lifted * rise * sigma_query * (1.0 + query_pre * (1.0 - sigma_query))
    ).astype(BF16)
    grads_ref[:, width : 2 * width] = (-key_total * opened * closed * (1.0 - closed)).astype(BF16)
    grads_ref[:, 3 * width :] = grad_gate_ref[...]


def mixer_backward(
    pre, grad_mixed, grad_gate, starts, runs, carry, after, open_part, counts, keep, flags
):
    tokens, all_width = pre.shape
    width = open_part.shape[1]
    head_count, lanes = carry.shape[0], carry.shape[2]
    blocks = tokens // BLOCK
    last = blocks - 1
    return pl.pallas_call(
        partial(mixer_backward_kernel, head_count),
        grid=(blocks,),
        in_specs=[
            pl.BlockSpec((BLOCK, all_width), lambda i: (last - i, 0)),
            pl.BlockSpec((BLOCK, width), lambda i: (last - i, 0)),
            pl.BlockSpec((BLOCK, width), lambda i: (last - i, 0)),
            pl.BlockSpec((1, head_count, lanes, lanes), lambda i: (last - i, 0, 0, 0)),
            pl.BlockSpec((1, 1, width), lambda i: (last - i, 0, 0)),
            pl.BlockSpec((head_count, lanes, lanes), lambda i: (0, 0, 0)),
            pl.BlockSpec((head_count, lanes, lanes), lambda i: (0, 0, 0)),
            pl.BlockSpec((1, width), lambda i: (0, 0)),
            pl.BlockSpec((BLOCK, 1), lambda i: (last - i, 0)),
            pl.BlockSpec((BLOCK, 1), lambda i: (last - i, 0)),
            pl.BlockSpec((1, 8, BLOCK), lambda i: (last - i, 0, 0)),
        ],
        out_specs=[
            pl.BlockSpec((BLOCK, all_width), lambda i: (last - i, 0)),
            pl.BlockSpec((1, width), lambda i: (0, 0)),
        ],
        out_shape=[
            jax.ShapeDtypeStruct((tokens, all_width), BF16),
            jax.ShapeDtypeStruct((1, width), F32),
        ],
        scratch_shapes=[
            pltpu.VMEM((head_count, lanes, lanes), F32),
            pltpu.VMEM((BLOCK, width), F32),
            pltpu.VMEM((BLOCK, width), F32),
            pltpu.VMEM((BLOCK, width), F32),
            pltpu.VMEM((1, width), F32),
        ],
        compiler_params=pltpu.CompilerParams(
            dimension_semantics=("arbitrary",), vmem_limit_bytes=40 << 20
        ),
        cost_estimate=pl.CostEstimate(
            flops=tokens * width * BLOCK * 30,
            bytes_accessed=tokens * width * 36,
            transcendentals=tokens * width * 9,
        ),
        name="mixer_backward",
    )(pre, grad_mixed, grad_gate, starts, runs, carry, after, open_part, counts, keep, flags)


def row_flags(segment_ids):
    ids = segment_ids.reshape(-1)
    tokens = ids.shape[0]
    starts = jnp.concatenate([jnp.zeros((1,), F32), (ids[1:] != ids[:-1]).astype(F32)])
    positions = jnp.arange(tokens)
    counts = jnp.sum(
        jnp.where(positions[None, :] <= positions[:, None], starts[None, :], 0.0), axis=1
    )
    keep = (ids > 0).astype(F32)
    blocks = tokens // BLOCK
    by_block = counts.reshape(blocks, BLOCK)
    lasts = by_block[:, -1]
    before = jnp.concatenate([jnp.zeros((1,), F32), lasts[:-1]])
    wide = (blocks, BLOCK)
    flags = jnp.stack(
        [by_block, jnp.broadcast_to(before[:, None], wide), jnp.broadcast_to(lasts[:, None], wide)]
        + [jnp.zeros(wide, F32)] * 5,
        axis=1,
    )
    return counts[:, None], keep[:, None], flags


def from_later(values, axis, shift):
    count = lax.axis_size(axis)
    return lax.ppermute(values, axis, [(i + shift, i) for i in range(count - shift)])


def grad_after(back, decay, link_in, axis):
    head_count, lanes, _ = back.shape
    rows = head_count * lanes
    message = (
        jnp.concatenate([back.reshape(rows, lanes), decay.reshape(head_count, lanes)]) * link_in
    )
    message = jnp.pad(message, ((0, 8 - head_count % 8 if head_count % 8 else 0), (0, 0)))
    total = jnp.zeros_like(back)
    factor = jnp.ones((head_count, 1, lanes), F32)
    for shift in range(1, lax.axis_size(axis)):
        got = from_later(message, axis, shift)
        total = total + factor * got[:rows].reshape(back.shape)
        factor = factor * got[rows : rows + head_count].reshape(head_count, 1, lanes)
    return total


CHUNK = 32
LAG = 2
MESH_ID = pl.DeviceIdType.MESH


class Line:
    def __init__(self, mesh_axes, part, arrived, out, sems, transform):
        self.mesh_axes = mesh_axes
        self.part, self.arrived, self.out = part, arrived, out
        self.sum_send, self.sum_recv, self.back_send, self.back_recv = sems
        self.transform = transform
        self.half = part.shape[0] // 2
        self.chunks = self.half // CHUNK
        self.size = lax.axis_size("tensor")
        self.place = lax.axis_index("tensor")
        self.lines = ((self.size - 1 - self.place, -1), (self.place, 1))
        self.steps = self.chunks + 2 * LAG * (self.size - 1)

    def device(self, position):
        return tuple(
            jnp.clip(position, 0, self.size - 1) if axis == "tensor" else lax.axis_index(axis)
            for axis in self.mesh_axes
        )

    def greet(self, barrier):
        for step in (-1, 1):
            inside = jnp.logical_and(self.place + step >= 0, self.place + step < self.size)

            @pl.when(inside)
            def _(step=step):
                pl.semaphore_signal(
                    barrier, inc=1, device_id=self.device(self.place + step), device_id_type=MESH_ID
                )

        at_end = jnp.logical_or(self.place == 0, self.place == self.size - 1)
        return jnp.where(at_end, 1, 2)

    def rows_of(self, side, index):
        return pl.ds(pl.multiple_of(side * self.half + index * CHUNK, CHUNK), CHUNK)

    def sum_copy(self, side, index, source):
        rows = self.rows_of(side, index)
        return pltpu.make_async_remote_copy(
            source.at[rows],
            self.arrived.at[rows],
            self.sum_send.at[side, index],
            self.sum_recv.at[side, index],
            device_id=self.device(self.place + self.lines[side][1]),
            device_id_type=MESH_ID,
        )

    def back_copy(self, side, index):
        rows = self.rows_of(side, index)
        return pltpu.make_async_remote_copy(
            self.out.at[rows],
            self.out.at[rows],
            self.back_send.at[side, index],
            self.back_recv.at[side, index],
            device_id=self.device(self.place - self.lines[side][1]),
            device_id_type=MESH_ID,
        )

    def step(self, time):
        for side in (0, 1):
            hops = self.lines[side][0]
            index = time - LAG * hops
            valid = jnp.logical_and(index >= 0, index < self.chunks)
            at_source, at_owner = hops == 0, hops == self.size - 1
            index = jnp.clip(index, 0, self.chunks - 1)
            rows = self.rows_of(side, index)

            @pl.when(jnp.logical_and(valid, at_source))
            def _(side=side, index=index):
                self.sum_copy(side, index, self.part).start()

            @pl.when(jnp.logical_and(valid, jnp.logical_not(at_source)))
            def _(side=side, index=index):
                self.sum_copy(side, index, self.arrived).wait_recv()

            between = jnp.logical_and(jnp.logical_not(at_source), jnp.logical_not(at_owner))

            @pl.when(jnp.logical_and(valid, between))
            def _(side=side, index=index, rows=rows):
                total = self.part[rows].astype(F32) + self.arrived[rows].astype(F32)
                self.arrived[rows] = total.astype(BF16)
                self.sum_copy(side, index, self.arrived).start()

            @pl.when(jnp.logical_and(valid, at_owner))
            def _(side=side, index=index, rows=rows):
                total = self.part[rows].astype(F32) + self.arrived[rows].astype(F32)
                own = pl.ds(pl.multiple_of(index * CHUNK, CHUNK), CHUNK)
                self.transform(total, rows, own)
                self.back_copy(side, index).start()

            away = self.size - 1 - hops
            index = time - LAG * (self.size - 1 + away)
            valid = jnp.logical_and(jnp.logical_and(index >= 0, index < self.chunks), away > 0)
            index = jnp.clip(index, 0, self.chunks - 1)

            @pl.when(valid)
            def _(side=side, index=index):
                self.back_copy(side, index).wait_recv()

            @pl.when(jnp.logical_and(valid, away < self.size - 1))
            def _(side=side, index=index):
                self.back_copy(side, index).start()

    def run(self, first, last, beside=None):
        def body(time, _):
            self.step(time)
            if beside is not None:
                beside(time)
            return 0

        lax.fori_loop(first, last, body, 0)

    def source_sent(self, first, last):
        def body(index, _):
            for side in (0, 1):

                @pl.when(self.lines[side][0] == 0)
                def _(side=side):
                    self.sum_copy(side, index, self.part).wait_send()

            return 0

        lax.fori_loop(first, last, body, 0)

    def finish(self, source_waits=True):
        def body(index, _):
            for side in (0, 1):
                hops = self.lines[side][0]
                passed = hops < self.size - 1
                if not source_waits:
                    passed = jnp.logical_and(passed, hops > 0)

                @pl.when(passed)
                def _(side=side):
                    self.sum_copy(side, index, self.arrived).wait_send()

                @pl.when(hops > 0)
                def _(side=side):
                    self.back_copy(side, index).wait_send()

            return 0

        lax.fori_loop(0, self.chunks, body, 0)


def line_sems(tokens):
    return [pltpu.SemaphoreType.DMA((2, tokens // 2 // CHUNK))] * 4


def inverse_rms(values):
    return lax.rsqrt(jnp.mean(values * values, axis=-1, keepdims=True) + EPSILON)


class Plane:
    def __init__(self, mesh_axes):
        self.mesh_axes = mesh_axes
        self.context = lax.axis_size("context")
        self.per_row = self.context // 2
        self.chips = lax.axis_size("shard") * self.per_row
        context_place = lax.axis_index("context")
        self.core = lax.rem(context_place, 2)
        self.chip = lax.axis_index("shard") * self.per_row + context_place // 2

    def device(self, chip, core):
        places = {
            "shard": chip // self.per_row,
            "context": 2 * lax.rem(chip, self.per_row) + core,
            "tensor": lax.axis_index("tensor"),
        }
        return tuple(places[axis] for axis in self.mesh_axes)

    def ahead(self, distance):
        return lax.rem(self.chip + distance, self.chips)

    def greet(self, barrier):
        targets = [self.device(self.chip, 1 - self.core)]
        targets += [self.device(self.ahead(step), self.core) for step in range(1, self.chips)]
        for target in targets:
            pl.semaphore_signal(barrier, inc=1, device_id=target, device_id_type=MESH_ID)
        return len(targets)


class Gather:
    def __init__(self, plane, sources, targets, sems):
        self.plane, self.sources, self.targets = plane, sources, targets
        self.load_sem, self.send_sem, self.recv_sem, self.pair_send, self.pair_recv = sems
        self.block = sources[0].shape[0]
        self.part = self.block // 2
        self.relayed = plane.chips == 4
        self.arrays = range(len(sources))

    def partner(self, distance):
        return jnp.bitwise_xor(self.plane.chip, distance)

    def greet(self, barrier):
        plane = self.plane
        targets = [plane.device(plane.chip, 1 - plane.core)]
        targets += [
            plane.device(self.partner(step), plane.core)
            for step in range(1, 3 if self.relayed else plane.chips)
        ]
        for target in targets:
            pl.semaphore_signal(barrier, inc=1, device_id=target, device_id_type=MESH_ID)
        return len(targets)

    def place(self, array, chip, core, half):
        first = (2 * chip + core) * self.block + half * self.part
        rows = pl.ds(pl.multiple_of(first, self.part), self.part)
        return self.targets[array].at[rows, pl.ds(0, self.sources[array].shape[1])]

    def mine(self, array, half):
        return self.sources[array].at[pl.ds(half * self.part, self.part)]

    def loads(self):
        plane = self.plane
        return [
            pltpu.make_async_copy(
                self.mine(array, half),
                self.place(array, plane.chip, plane.core, half),
                self.load_sem.at[array, half],
            )
            for array in self.arrays
            for half in range(2)
        ]

    def send(self, distance, half):
        plane = self.plane
        copies = []
        for array in self.arrays:
            chip, target = plane.chip, self.partner(distance)
            source = self.mine(array, half)
            if self.relayed and distance == 3:
                chip = self.partner(2 if half == 0 else 1)
                target = self.partner(1 if half == 0 else 2)
                source = self.place(array, chip, plane.core, half)
            copies.append(
                pltpu.make_async_remote_copy(
                    source,
                    self.place(array, chip, plane.core, half),
                    self.send_sem.at[array, distance - 1, half],
                    self.recv_sem.at[array, distance - 1, half],
                    device_id=plane.device(target, plane.core),
                    device_id_type=MESH_ID,
                )
            )
        return copies

    def forward(self, distance, half):
        plane = self.plane
        copies = []
        for array in self.arrays:
            place = self.place(array, self.partner(distance), plane.core, half)
            copies.append(
                pltpu.make_async_remote_copy(
                    self.mine(array, half) if distance == 0 else place,
                    place,
                    self.pair_send.at[array, distance, half],
                    self.pair_recv.at[array, distance, half],
                    device_id=plane.device(plane.chip, 1 - plane.core),
                    device_id_type=MESH_ID,
                )
            )
        return copies

    def start(self):
        if self.relayed:
            order = ((1, 1), (2, 0), (1, 0), (2, 1))
        else:
            order = [(step, half) for step in range(1, self.plane.chips) for half in range(2)]
        for distance, half in order:
            for copy in self.send(distance, half):
                copy.start()
        for copy in self.loads():
            copy.start()
        for half in range(2):
            for copy in self.forward(0, half):
                copy.start()

    def take(self, distance, half, relay):
        for copy in self.send(distance, half):
            copy.wait_recv()
        if relay:
            for copy in self.send(3, half):
                copy.start()
        for copy in self.forward(distance, half):
            copy.start()

    def stage(self, number):
        if self.relayed:
            if number == 0:
                self.take(1, 1, True)
                self.take(2, 0, True)
            elif number == 1:
                self.take(1, 0, False)
                self.take(2, 1, False)
            else:
                self.take(3, 0, False)
                self.take(3, 1, False)
        elif number == 2:
            for distance in range(1, self.plane.chips):
                for half in range(2):
                    self.take(distance, half, False)

    def arrive_from(self, distance):
        if distance == 0:
            for copy in self.loads():
                copy.wait()
        for half in range(2):
            for copy in self.forward(distance, half):
                copy.wait_recv()

    def arrive(self):
        for distance in range(self.plane.chips):
            self.arrive_from(distance)

    def finish(self):
        for distance in range(self.plane.chips):
            for half in range(2):
                for copy in self.forward(distance, half):
                    copy.wait_send()
                if distance > 0:
                    for copy in self.send(distance, half):
                        copy.wait_send()


def gather_sems(arrays):
    chips = lax.axis_size("shard") * lax.axis_size("context") // 2
    return [
        pltpu.SemaphoreType.DMA((arrays, 2)),
        pltpu.SemaphoreType.DMA((arrays, chips - 1, 2)),
        pltpu.SemaphoreType.DMA((arrays, chips - 1, 2)),
        pltpu.SemaphoreType.DMA((arrays, chips, 2)),
        pltpu.SemaphoreType.DMA((arrays, chips, 2)),
    ]


GROUP = 128
TILE = 256
WIDE = 512


def middle_kernel(
    mesh_axes,
    mix_hbm,
    cotangent_ref,
    input_hbm,
    gain_ref,
    gate_hbm,
    up_hbm,
    down_hbm,
    normed_ref,
    out_ref,
    gain_grad,
    residual_hbm,
    hidden_hbm,
    grad_gate_hbm,
    grad_up_hbm,
    feed_hbm,
    grad_hbm,
    gate_w,
    up_w,
    down_w,
    part,
    mix_arrived,
    arrived,
    inputs,
    residual,
    stage_hidden,
    stage_gate,
    stage_up,
    stage_feed,
    part_sem,
    input_sem,
    save_sem,
    stage_sem,
    grad_sem,
    *sems,
):
    tokens, model_width = normed_ref.shape
    half = tokens // 2
    hidden_width = gate_hbm.shape[1]
    padded = gate_w.shape[1]
    groups = half // GROUP
    place, line_size = lax.axis_index("tensor"), lax.axis_size("tensor")
    own_half = pl.ds(pl.multiple_of(jnp.where(place == 0, 0, half), half), half)
    part_load = pltpu.make_async_copy(mix_hbm, part, part_sem.at[0])
    part_load.start()
    input_load = pltpu.make_async_copy(input_hbm.at[own_half], inputs, input_sem.at[0])
    input_load.start()
    if padded > hidden_width:
        spare = slice(hidden_width, padded)
        gate_w[:, spare] = jnp.zeros((model_width, padded - hidden_width), BF16)
        up_w[:, spare] = jnp.zeros((model_width, padded - hidden_width), BF16)
        down_w[:, spare] = jnp.zeros((model_width, padded - hidden_width), BF16)
    gain_grad[...] = jnp.zeros_like(gain_grad)

    def mix_turn(total, rows, own):
        values = inputs[own].astype(F32) + total
        residual[own] = values
        normed_ref[rows] = (values * inverse_rms(values) * gain_ref[...]).astype(BF16)

    def turn(total, rows, own):
        values = residual[own]
        inverse = inverse_rms(values)
        unit = values * inverse
        gain_grad[...] += jnp.sum(total * unit, axis=0, keepdims=True)
        lifted = total * gain_ref[...]
        mean = jnp.mean(lifted * unit, axis=-1, keepdims=True)
        grad = cotangent_ref[rows].astype(F32) + inverse * (lifted - unit * mean)
        residual[own] = grad
        out_ref[rows] = grad.astype(BF16)

    mix_line = Line(mesh_axes, part, mix_arrived, normed_ref, sems[:4], mix_turn)
    line = Line(mesh_axes, part, arrived, out_ref, sems[4:8], turn)
    gather = Gather(
        Plane(mesh_axes), (gate_hbm, up_hbm, down_hbm), (gate_w, up_w, down_w), sems[8:]
    )
    barrier = pltpu.get_barrier_semaphore()
    expected = mix_line.greet(barrier) + gather.greet(barrier)
    pl.semaphore_wait(barrier, expected)
    gather.start()
    part_load.wait()
    input_load.wait()
    pace = GROUP // CHUNK
    begin = pace + 2 * LAG * (line_size - 1) + 4
    mix_line.run(0, begin - 10)
    gather.stage(0)
    mix_line.run(begin - 10, begin - 4)
    gather.stage(1)
    mix_line.run(begin - 4, begin)
    gather.stage(2)
    gather.arrive()

    def both(ref, group):
        first = pl.ds(pl.multiple_of(group * GROUP, GROUP), GROUP)
        second = pl.ds(pl.multiple_of(half + group * GROUP, GROUP), GROUP)
        return first, second

    def stage_copies(group):
        slot = lax.rem(group, 2)
        copies = []
        for side, rows in enumerate(both(None, group)):
            from_rows = pl.ds(side * GROUP, GROUP)
            columns = pl.ds(0, hidden_width)
            for which, (stage, target) in enumerate(
                (
                    (stage_hidden, hidden_hbm),
                    (stage_gate, grad_gate_hbm),
                    (stage_up, grad_up_hbm),
                )
            ):
                copies.append(
                    pltpu.make_async_copy(
                        stage.at[slot, from_rows, columns],
                        target.at[rows],
                        stage_sem.at[slot, which, side],
                    )
                )
            copies.append(
                pltpu.make_async_copy(
                    stage_feed.at[slot, from_rows], feed_hbm.at[rows], stage_sem.at[slot, 3, side]
                )
            )
        return copies

    def hidden_tile(group, tile):
        first, second = both(normed_ref, group)
        slot = lax.rem(group, 2)
        columns = pl.ds(pl.multiple_of(tile * WIDE, WIDE), WIDE)
        rows = jnp.concatenate([normed_ref[first], normed_ref[second]], axis=0)
        gate = mm_nn(rows, gate_w[:, columns])
        up = mm_nn(rows, up_w[:, columns])
        grads = jnp.concatenate([cotangent_ref[first], cotangent_ref[second]], axis=0)
        grad = mm_nn(grads, down_w[:, columns])
        sigma = jax.nn.sigmoid(gate)
        active = gate * sigma
        stage_hidden[slot, :, columns] = (active * up).astype(BF16)
        stage_gate[slot, :, columns] = (grad * up * sigma * (1.0 + gate * (1.0 - sigma))).astype(
            BF16
        )
        stage_up[slot, :, columns] = (grad * active).astype(BF16)

    def model_tile(group, tile):
        first, second = both(part, group)
        slot = lax.rem(group, 2)
        columns = pl.ds(pl.multiple_of(tile * WIDE, WIDE), WIDE)
        back = mm_nt(stage_gate[slot], gate_w[columns, :])
        back = (back + mm_nt(stage_up[slot], up_w[columns, :])).astype(BF16)
        part[first, columns] = back[:GROUP]
        part[second, columns] = back[GROUP:]
        stage_feed[slot, :, columns] = mm_nt(stage_hidden[slot], down_w[columns, :]).astype(BF16)

    hidden_tiles, model_tiles = padded // WIDE, model_width // WIDE
    ticks = hidden_tiles + model_tiles
    piece = -(-ticks // pace)
    save = pltpu.make_async_copy(residual, residual_hbm, save_sem.at[0])

    def group_body(group, _):
        mix_line.source_sent(group * pace, (group + 1) * pace)

        @pl.when(group == 1)
        def _():
            save.start()

        @pl.when(group == 2)
        def _():
            save.wait()

        @pl.when(group >= 2)
        def _():
            for copy in stage_copies(group - 2):
                copy.wait()

        def piece_body(index, _):
            def tick_body(offset, _):
                tick = index * piece + offset

                @pl.when(tick < hidden_tiles)
                def _():
                    hidden_tile(group, tick)

                @pl.when(jnp.logical_and(tick >= hidden_tiles, tick < ticks))
                def _():
                    model_tile(group, tick - hidden_tiles)

                return 0

            lax.fori_loop(0, piece, tick_body, 0)

            mix_time = begin + group * pace + index

            @pl.when(mix_time < mix_line.steps)
            def _():
                mix_line.step(mix_time)

            @pl.when(group >= 1)
            def _():
                line.step((group - 1) * pace + index)

            return 0

        lax.fori_loop(0, pace, piece_body, 0)
        for copy in stage_copies(group):
            copy.start()
        return 0

    lax.fori_loop(0, groups, group_body, 0)
    line.run((groups - 1) * pace, line.steps)
    grad_save = pltpu.make_async_copy(residual, grad_hbm, grad_sem.at[0])
    grad_save.start()
    for group in range(max(groups - 2, 0), groups):
        for copy in stage_copies(group):
            copy.wait()
    gather.finish()
    mix_line.finish(source_waits=False)
    line.finish()
    grad_save.wait()


def middle(mesh_axes, collective, mix, cotangent, inputs, gain, gate_w, up_w, down_w):
    tokens, model_width = mix.shape
    hidden_width = gate_w.shape[1]
    padded = -(-hidden_width // WIDE) * WIDE
    whole = pl.BlockSpec(memory_space=pltpu.VMEM)
    remote = pl.BlockSpec(memory_space=pl.ANY)
    group_rows = 2 * GROUP
    return pl.pallas_call(
        partial(middle_kernel, mesh_axes),
        in_specs=[remote, whole, remote, whole, remote, remote, remote],
        out_specs=[whole, whole, whole] + [remote] * 6,
        out_shape=[
            jax.ShapeDtypeStruct((tokens, model_width), BF16),
            jax.ShapeDtypeStruct((tokens, model_width), BF16),
            jax.ShapeDtypeStruct((1, model_width), F32),
            jax.ShapeDtypeStruct((tokens // 2, model_width), F32),
            jax.ShapeDtypeStruct((tokens, hidden_width), BF16),
            jax.ShapeDtypeStruct((tokens, hidden_width), BF16),
            jax.ShapeDtypeStruct((tokens, hidden_width), BF16),
            jax.ShapeDtypeStruct((tokens, model_width), BF16),
            jax.ShapeDtypeStruct((tokens // 2, model_width), F32),
        ],
        scratch_shapes=[
            pltpu.VMEM((model_width, padded), BF16),
            pltpu.VMEM((model_width, padded), BF16),
            pltpu.VMEM((model_width, padded), BF16),
            pltpu.VMEM((tokens, model_width), BF16),
            pltpu.VMEM((tokens, model_width), BF16),
            pltpu.VMEM((tokens, model_width), BF16),
            pltpu.VMEM((tokens // 2, model_width), BF16),
            pltpu.VMEM((tokens // 2, model_width), F32),
            pltpu.VMEM((2, group_rows, padded), BF16),
            pltpu.VMEM((2, group_rows, padded), BF16),
            pltpu.VMEM((2, group_rows, padded), BF16),
            pltpu.VMEM((2, group_rows, model_width), BF16),
            pltpu.SemaphoreType.DMA((1,)),
            pltpu.SemaphoreType.DMA((1,)),
            pltpu.SemaphoreType.DMA((1,)),
            pltpu.SemaphoreType.DMA((2, 4, 2)),
            pltpu.SemaphoreType.DMA((1,)),
        ]
        + line_sems(tokens)
        + line_sems(tokens)
        + gather_sems(3),
        compiler_params=pltpu.CompilerParams(
            collective_id=collective, has_side_effects=True, vmem_limit_bytes=61 << 20
        ),
        cost_estimate=pl.CostEstimate(
            flops=tokens * model_width * hidden_width * 12,
            bytes_accessed=360_000_000,
            transcendentals=tokens * hidden_width,
        ),
        name="middle",
    )(mix, cotangent, inputs, gain, gate_w, up_w, down_w)


def output_kernel(
    mesh_axes,
    part,
    residual,
    normed_ref,
    cotangent_ref,
    hidden_ref,
    grad_gate_ref,
    grad_up_ref,
    gated_ref,
    mix_grad_ref,
    out_ref,
    grads_hbm,
    out_grads_hbm,
    arrived,
    stage,
    out_stage,
    stage_sem,
    out_sem,
    *sems,
):
    model_width = normed_ref.shape[1]
    tiles = model_width // TILE

    def turn(total, rows, own):
        out_ref[rows] = (residual[own] + total).astype(BF16)

    line = Line(mesh_axes, part, arrived, out_ref, sems, turn)
    barrier = pltpu.get_barrier_semaphore()
    pl.semaphore_wait(barrier, line.greet(barrier))

    def stage_copies(tile):
        rows = pl.ds(pl.multiple_of(tile * TILE, TILE), TILE)
        slot = lax.rem(tile, 2)
        return (
            pltpu.make_async_copy(stage.at[slot], grads_hbm.at[:, rows], stage_sem.at[slot]),
            pltpu.make_async_copy(out_stage.at[slot], out_grads_hbm.at[rows], out_sem.at[slot]),
        )

    def weight_tile(time):
        tile = jnp.clip(time, 0, tiles - 1)
        slot = lax.rem(tile, 2)
        columns = pl.ds(pl.multiple_of(tile * TILE, TILE), TILE)

        @pl.when(jnp.logical_and(time < tiles, time >= 2))
        def _():
            for copy in stage_copies(tile - 2):
                copy.wait()

        @pl.when(time < tiles)
        def _():
            rows = normed_ref[:, columns]
            stage[slot, 0] = mm_tn(rows, grad_gate_ref[...]).astype(BF16)
            stage[slot, 1] = mm_tn(rows, grad_up_ref[...]).astype(BF16)
            stage[slot, 2] = mm_tn(cotangent_ref[:, columns], hidden_ref[...]).astype(BF16)
            out_stage[slot] = mm_tn(mix_grad_ref[:, columns], gated_ref[...]).astype(BF16)
            for copy in stage_copies(tile):
                copy.start()

    line.run(0, line.steps, weight_tile)
    for tile in range(max(tiles - 2, 0), tiles):
        for copy in stage_copies(tile):
            copy.wait()
    line.finish()


def output_line(
    mesh_axes,
    collective,
    part,
    residual,
    normed,
    cotangent,
    hidden_low,
    grad_gate,
    grad_up,
    gated,
    mix_grad,
):
    tokens, model_width = part.shape
    width = gated.shape[1]
    hidden_width = hidden_low.shape[1]
    whole = pl.BlockSpec(memory_space=pltpu.VMEM)
    return pl.pallas_call(
        partial(output_kernel, mesh_axes),
        in_specs=[whole] * 9,
        out_specs=[whole] + [pl.BlockSpec(memory_space=pl.ANY)] * 2,
        out_shape=[
            jax.ShapeDtypeStruct((tokens, model_width), BF16),
            jax.ShapeDtypeStruct((3, model_width, hidden_width), BF16),
            jax.ShapeDtypeStruct((model_width, width), BF16),
        ],
        scratch_shapes=[
            pltpu.VMEM((tokens, model_width), BF16),
            pltpu.VMEM((2, 3, TILE, hidden_width), BF16),
            pltpu.VMEM((2, TILE, width), BF16),
            pltpu.SemaphoreType.DMA((2,)),
            pltpu.SemaphoreType.DMA((2,)),
        ]
        + line_sems(tokens),
        compiler_params=pltpu.CompilerParams(
            collective_id=collective, has_side_effects=True, vmem_limit_bytes=56 << 20
        ),
        cost_estimate=pl.CostEstimate(
            flops=tokens * model_width * hidden_width * 6,
            bytes_accessed=360_000_000,
            transcendentals=0,
        ),
        name="output_line",
    )(
        part, residual, normed, cotangent, hidden_low, grad_gate, grad_up, gated, mix_grad
    )


def input_kernel(
    mesh_axes,
    part,
    hidden_ref,
    residual_grad,
    gain_ref,
    grads_hbm,
    out_ref,
    gain_grad,
    share_gate,
    share_up,
    share_down,
    arrived,
    own,
    other,
    remote,
    load_sem,
    pair_send,
    pair_recv,
    chip_send,
    chip_recv,
    *sems,
):
    plane = Plane(mesh_axes)
    chips = plane.chips
    block = own.shape[2]
    gain_grad[...] = jnp.zeros_like(gain_grad)

    def turn(total, rows, own_rows):
        values = hidden_ref[rows].astype(F32)
        inverse = inverse_rms(values)
        unit = values * inverse
        gain_grad[...] += jnp.sum(total * unit, axis=0, keepdims=True)
        lifted = total * gain_ref[...]
        mean = jnp.mean(lifted * unit, axis=-1, keepdims=True)
        grad = residual_grad[own_rows] + inverse * (lifted - unit * mean)
        out_ref[rows] = grad.astype(BF16)

    line = Line(mesh_axes, part, arrived, out_ref, sems, turn)
    barrier = pltpu.get_barrier_semaphore()
    expected = line.greet(barrier) + plane.greet(barrier)
    pl.semaphore_wait(barrier, expected)

    def rows_of(slot, core):
        return pl.ds(pl.multiple_of((2 * plane.ahead(slot) + core) * block, block), block)

    def load(slot):
        return pltpu.make_async_copy(
            grads_hbm.at[:, rows_of(slot, plane.core)], own.at[slot], load_sem.at[slot]
        )

    def pair_copy(slot):
        return pltpu.make_async_remote_copy(
            grads_hbm.at[:, rows_of(slot, 1 - plane.core)],
            other.at[slot],
            pair_send.at[slot],
            pair_recv.at[slot],
            device_id=plane.device(plane.chip, 1 - plane.core),
            device_id_type=MESH_ID,
        )

    def chip_copy(slot):
        return pltpu.make_async_remote_copy(
            own.at[slot],
            remote.at[slot - 1],
            chip_send.at[slot - 1],
            chip_recv.at[slot - 1],
            device_id=plane.device(plane.ahead(slot), plane.core),
            device_id_type=MESH_ID,
        )

    def start(index, _):
        slot = lax.rem(index + 1, chips)
        pair_copy(slot).start()
        load(slot).start()
        return 0

    lax.fori_loop(0, chips, start, 0)
    strip = 32

    def combine(time):
        slot = lax.rem(jnp.clip(time, 0, chips - 1) + 1, chips)

        @pl.when(time < chips)
        def _():
            load(slot).wait()
            pair_copy(slot).wait_recv()

            def add(index, _):
                rows = pl.ds(pl.multiple_of(index * strip, strip), strip)
                for which in range(3):
                    total = own[slot, which, rows].astype(F32) + other[slot, which, rows].astype(F32)
                    own[slot, which, rows] = total.astype(BF16)
                return 0

            lax.fori_loop(0, block // strip, add, 0)

        @pl.when(time < chips - 1)
        def _():
            chip_copy(slot).start()

    line.run(0, line.steps, combine)

    def arrive(index, _):
        chip_copy(index).wait_recv()
        return 0

    lax.fori_loop(1, chips, arrive, 0)

    def total(index, _):
        rows = pl.ds(pl.multiple_of(index * strip, strip), strip)

        def whole(which):
            def add(slot, value):
                return value + remote[slot, which, rows].astype(F32)

            return lax.fori_loop(0, chips - 1, add, own[0, which, rows].astype(F32))

        share_gate[rows] = whole(0)
        share_up[rows] = whole(1)
        share_down[rows] = whole(2)
        return 0

    lax.fori_loop(0, block // strip, total, 0)

    def sent(index, _):
        pair_copy(index).wait_send()
        return 0

    lax.fori_loop(0, chips, sent, 0)

    def chip_sent(index, _):
        chip_copy(index).wait_send()
        return 0

    lax.fori_loop(1, chips, chip_sent, 0)
    line.finish()


def input_line(mesh_axes, collective, part, hidden, residual_grad, gain, grads):
    tokens, model_width = part.shape
    hidden_width = grads.shape[2]
    chips = lax.axis_size("shard") * lax.axis_size("context") // 2
    block = model_width // (2 * chips)
    whole = pl.BlockSpec(memory_space=pltpu.VMEM)
    return pl.pallas_call(
        partial(input_kernel, mesh_axes),
        in_specs=[whole] * 4 + [pl.BlockSpec(memory_space=pl.ANY)],
        out_specs=[whole] * 5,
        out_shape=[
            jax.ShapeDtypeStruct((tokens, model_width), BF16),
            jax.ShapeDtypeStruct((1, model_width), F32),
        ]
        + [jax.ShapeDtypeStruct((block, hidden_width), F32)] * 3,
        scratch_shapes=[
            pltpu.VMEM((tokens, model_width), BF16),
            pltpu.VMEM((chips, 3, block, hidden_width), BF16),
            pltpu.VMEM((chips, 3, block, hidden_width), BF16),
            pltpu.VMEM((chips - 1, 3, block, hidden_width), BF16),
            pltpu.SemaphoreType.DMA((chips,)),
            pltpu.SemaphoreType.DMA((chips,)),
            pltpu.SemaphoreType.DMA((chips,)),
            pltpu.SemaphoreType.DMA((chips - 1,)),
            pltpu.SemaphoreType.DMA((chips - 1,)),
        ]
        + line_sems(tokens),
        compiler_params=pltpu.CompilerParams(
            collective_id=collective, has_side_effects=True, vmem_limit_bytes=58 << 20
        ),
        cost_estimate=pl.CostEstimate(
            flops=tokens * model_width * 8, bytes_accessed=360_000_000, transcendentals=0
        ),
        name="input_line",
    )(part, hidden, residual_grad, gain, grads)


def forward_kernel(
    mesh_axes,
    head_count,
    key_scale,
    hidden_ref,
    gain_ref,
    query_hbm,
    forget_hbm,
    input_hbm,
    gate_hbm,
    out_shard_hbm,
    open_ref,
    count_ref,
    keep_ref,
    flags_ref,
    ids_ref,
    head_gain_ref,
    normed_hbm,
    pre_hbm,
    full_hbm,
    out_full_hbm,
    mixed_hbm,
    lead_hbm,
    start_hbm,
    gated_hbm,
    mix_hbm,
    run_ref,
    carry_ref,
    decay_ref,
    link_ref,
    normed,
    pre,
    mine,
    full,
    out_full,
    mixed,
    lead,
    starts,
    gated,
    mix,
    state_scr,
    run_scr,
    message,
    received,
    mine_sem,
    full_sem,
    save_sem,
    pre_sem,
    mix_sem,
    state_send,
    state_recv,
    *sems,
):
    plane = Plane(mesh_axes)
    chips = plane.chips
    tokens, model_width = hidden_ref.shape
    block, width = query_hbm.shape
    lanes = width // head_count
    state_rows = head_count * lanes
    context, context_size = lax.axis_index("context"), lax.axis_size("context")

    mine_loads = [
        pltpu.make_async_copy(
            ref, mine.at[:, pl.ds(which * width, width)], mine_sem.at[which]
        )
        for which, ref in enumerate((query_hbm, forget_hbm, input_hbm, gate_hbm))
    ]
    for load in mine_loads:
        load.start()
    gather = Gather(plane, (mine,), (full,), sems[:5])
    out_gather = Gather(plane, (out_shard_hbm,), (out_full,), sems[5:])

    def later(shift):
        places = {axis: lax.axis_index(axis) for axis in mesh_axes}
        places["context"] = lax.rem(context + shift, context_size)
        return tuple(places[axis] for axis in mesh_axes)

    barrier = pltpu.get_barrier_semaphore()
    expected = gather.greet(barrier)
    for shift in range(1, context_size):
        pl.semaphore_signal(barrier, inc=1, device_id=later(shift), device_id_type=MESH_ID)
    pl.semaphore_wait(barrier, expected + context_size - 1)
    for load in mine_loads:
        load.wait()
    gather.start()
    out_gather.start()

    def norm(index, _):
        rows = pl.ds(pl.multiple_of(index * 128, 128), 128)
        values = hidden_ref[rows].astype(F32)
        normed[rows] = (values * inverse_rms(values) * gain_ref[...]).astype(BF16)
        return 0

    lax.fori_loop(0, tokens // 128, norm, 0)

    saves = [
        pltpu.make_async_copy(source, target, save_sem.at[which])
        for which, (source, target) in enumerate(
            (
                (normed, normed_hbm),
                (out_full, out_full_hbm),
                (mixed, mixed_hbm),
                (lead, lead_hbm),
                (starts, start_hbm),
                (gated, gated_hbm),
            )
        )
    ]
    saves[0].start()
    row_tile, column_tile = 256, 512

    def pre_save(index):
        rows = pl.ds(pl.multiple_of(index * row_tile, row_tile), row_tile)
        return pltpu.make_async_copy(pre.at[rows], pre_hbm.at[rows], pre_sem.at[index])

    def depth_of(distance):
        first = 2 * gather.partner(distance) * block
        return pl.ds(pl.multiple_of(first, 2 * block), 2 * block)

    def product(distance):
        depth = depth_of(distance)

        def row_body(index, _):
            rows = pl.ds(pl.multiple_of(index * row_tile, row_tile), row_tile)
            left = normed[rows, depth]

            def column_body(column, _):
                columns = pl.ds(pl.multiple_of(column * column_tile, column_tile), column_tile)
                value = mm_nn(left, full[depth, columns])
                if distance > 0:
                    value = value + pre[rows, columns]
                pre[rows, columns] = value
                return 0

            lax.fori_loop(0, full.shape[1] // column_tile, column_body, 0)
            if distance == chips - 1:
                pre_save(index).start()
            return 0

        lax.fori_loop(0, tokens // row_tile, row_body, 0)

    def full_save(distance):
        depth = depth_of(distance)
        return pltpu.make_async_copy(full.at[depth], full_hbm.at[depth], full_sem.at[distance])

    def use(distance):
        gather.arrive_from(distance)
        full_save(distance).start()
        product(distance)

    use(0)
    gather.stage(0)
    gather.stage(1)
    if gather.relayed:
        use(1)
        use(2)
    gather.stage(2)
    if gather.relayed:
        use(3)
    else:
        for distance in range(1, chips):
            use(distance)
    out_gather.stage(0)
    out_gather.stage(1)

    state_scr[...] = jnp.zeros_like(state_scr)
    run_scr[...] = jnp.zeros_like(run_scr)

    def recur(step, _):
        rows = pl.ds(pl.multiple_of(step * BLOCK, BLOCK), BLOCK)
        counts, keep = count_ref[rows], keep_ref[rows]
        row_ids, col_ids, linked, fresh, tail, closing = block_masks(counts, flags_ref[step])
        tri = (row_ids >= col_ids).astype(BF16)
        query_pre = pre[rows, :width]
        values = pre[rows, 2 * width : 3 * width].astype(BF16)
        keys = open_ref[...] * jax.nn.sigmoid(-pre[rows, width : 2 * width])
        cum = split_sum(tri, jnp.log1p(-keys))
        ending = cum[BLOCK - 1 : BLOCK, :]
        lifted = query_pre * jax.nn.sigmoid(query_pre) * jnp.exp(cum)
        lowered = (keys * jnp.exp(-cum) * keep).astype(BF16)
        moved = (keys * jnp.exp(ending - cum) * (keep * tail)).astype(BF16)
        run = run_scr[...]
        lead[rows] = (lifted * jnp.exp(run) * (counts == 0).astype(F32)).astype(BF16)
        run_ref[step] = run
        run_scr[...] = run + ending
        fresh_lifted = (lifted * fresh).astype(BF16)
        lifted = lifted.astype(BF16)
        end_decay = jnp.exp(ending) * closing
        for head in range(head_count):
            part = slice(head * lanes, (head + 1) * lanes)
            state = state_scr[head]
            starts[step, head] = state
            scores = jnp.where(linked, mm_nt(lifted[:, part], lowered[:, part]), 0.0)
            results = mm_nn(scores.astype(BF16), values[:, part])
            results = results + mm_nt(fresh_lifted[:, part], state.astype(BF16))
            mixed[rows, part] = results * (key_scale * keep)
            state_scr[head] = state * end_decay[:, part] + mm_tn(values[:, part], moved[:, part])
        return 0

    lax.fori_loop(0, tokens // BLOCK, recur, 0)
    saves[3].start()
    saves[4].start()

    last_count = flags_ref[tokens // BLOCK - 1][2:3, 0:1]
    for head in range(head_count):
        part = slice(head * lanes, (head + 1) * lanes)
        message[head * lanes : (head + 1) * lanes] = state_scr[head]
        decay = jnp.exp(run_scr[:, part]) * (last_count == 0).astype(F32)
        decay_ref[head] = decay
        message[state_rows + 8 + head : state_rows + 9 + head] = decay
    message[state_rows : state_rows + 8] = ids_ref[...]

    def state_copy(shift):
        return pltpu.make_async_remote_copy(
            message,
            received.at[shift - 1],
            state_send.at[shift - 1],
            state_recv.at[shift - 1],
            device_id=later(shift),
            device_id_type=MESH_ID,
        )

    for shift in range(1, context_size):

        @pl.when(context + shift < context_size)
        def _(shift=shift):
            state_copy(shift).start()

    out_gather.stage(2)
    carry_ref[...] = jnp.zeros_like(carry_ref)
    link_ref[...] = jnp.zeros_like(link_ref)
    for shift in range(1, context_size):

        @pl.when(context >= shift)
        def _(shift=shift):
            state_copy(shift).wait_recv()
            linked = jnp.ones((1, lanes), F32)
            follower = ids_ref[0:1]
            factors = [jnp.ones((1, lanes), F32)] * head_count
            for near in range(shift):
                got = received.at[near]
                linked = (got[state_rows + 1 : state_rows + 2] == follower).astype(F32)
                follower = got[state_rows : state_rows + 1]
                factors = [factor * linked for factor in factors]
                if near < shift - 1:
                    factors = [
                        factor * got[state_rows + 8 + head : state_rows + 9 + head]
                        for head, factor in enumerate(factors)
                    ]
            if shift == 1:
                link_ref[0:1] = linked
            for head in range(head_count):
                rows = slice(head * lanes, (head + 1) * lanes)
                carry_ref[head] += factors[head] * received[shift - 1, rows]

    for shift in range(1, context_size):

        @pl.when(context + shift < context_size)
        def _(shift=shift):
            state_copy(shift).wait_send()

    for distance in range(chips):
        out_gather.arrive_from(distance)
    saves[1].start()

    def mix_save(index):
        rows = pl.ds(pl.multiple_of(index * row_tile, row_tile), row_tile)
        return pltpu.make_async_copy(mix.at[rows], mix_hbm.at[rows], mix_sem.at[index])

    def project(index, _):
        rows = pl.ds(pl.multiple_of(index * row_tile, row_tile), row_tile)
        for head in range(head_count):
            part = slice(head * lanes, (head + 1) * lanes)
            carried = mm_nt(lead[rows, part], carry_ref[head].astype(BF16))
            value = mixed[rows, part] + carried * (key_scale * keep_ref[rows])
            mixed[rows, part] = value
            gate = pre[rows, 3 * width + head * lanes : 3 * width + (head + 1) * lanes]
            unit = value * inverse_rms(value)
            gated[rows, part] = (
                unit * head_gain_ref[...] * (gate * jax.nn.sigmoid(gate))
            ).astype(BF16)
        left = gated[rows]

        def column_body(column, _):
            columns = pl.ds(pl.multiple_of(column * column_tile, column_tile), column_tile)
            mix[rows, columns] = mm_nt(left, out_full[columns, :]).astype(BF16)
            return 0

        lax.fori_loop(0, model_width // column_tile, column_body, 0)
        mix_save(index).start()
        return 0

    lax.fori_loop(0, tokens // row_tile, project, 0)
    saves[2].start()
    saves[5].start()
    gather.finish()
    out_gather.finish()
    for distance in range(chips):
        full_save(distance).wait()
    for save in saves:
        save.wait()
    for index in range(tokens // row_tile):
        pre_save(index).wait()
        mix_save(index).wait()


def forward(
    mesh_axes, collective, hidden, gain, shards, out_shard, open_part, masks, ids, head_gain
):
    counts, keep, flags = masks
    tokens, model_width = hidden.shape
    block, width = shards[0].shape
    lanes = head_gain.shape[1]
    head_count = width // lanes
    all_width = width * len(shards)
    blocks = tokens // BLOCK
    context_size = lax.axis_size("context")
    chips = lax.axis_size("shard") * context_size // 2
    messages = head_count * lanes + 8 + -(-head_count // 8) * 8
    whole = pl.BlockSpec(memory_space=pltpu.VMEM)
    remote = pl.BlockSpec(memory_space=pl.ANY)
    stored = [
        ((tokens, model_width), BF16),
        ((tokens, all_width), F32),
        ((model_width, all_width), BF16),
        ((model_width, width), BF16),
        ((tokens, width), F32),
        ((tokens, width), BF16),
        ((blocks, head_count, lanes, lanes), F32),
        ((tokens, width), BF16),
        ((tokens, model_width), BF16),
    ]
    kept = [
        ((blocks, 1, width), F32),
        ((head_count, lanes, lanes), F32),
        ((head_count, 1, lanes), F32),
        ((8, lanes), F32),
    ]
    return pl.pallas_call(
        partial(forward_kernel, mesh_axes, head_count, lanes ** (-0.5)),
        in_specs=[whole] * 2 + [remote] * 5 + [whole] * 6,
        out_specs=[remote] * len(stored) + [whole] * len(kept),
        out_shape=[jax.ShapeDtypeStruct(shape, kind) for shape, kind in stored + kept],
        scratch_shapes=[
            pltpu.VMEM((tokens, model_width), BF16),
            pltpu.VMEM((tokens, all_width), F32),
            pltpu.VMEM((block, all_width), BF16),
            pltpu.VMEM((model_width, all_width), BF16),
            pltpu.VMEM((model_width, width), BF16),
            pltpu.VMEM((tokens, width), F32),
            pltpu.VMEM((tokens, width), BF16),
            pltpu.VMEM((blocks, head_count, lanes, lanes), F32),
            pltpu.VMEM((tokens, width), BF16),
            pltpu.VMEM((tokens, model_width), BF16),
            pltpu.VMEM((head_count, lanes, lanes), F32),
            pltpu.VMEM((1, width), F32),
            pltpu.VMEM((messages, lanes), F32),
            pltpu.VMEM((context_size - 1, messages, lanes), F32),
            pltpu.SemaphoreType.DMA((4,)),
            pltpu.SemaphoreType.DMA((chips,)),
            pltpu.SemaphoreType.DMA((6,)),
            pltpu.SemaphoreType.DMA((tokens // 256,)),
            pltpu.SemaphoreType.DMA((tokens // 256,)),
            pltpu.SemaphoreType.DMA((context_size - 1,)),
            pltpu.SemaphoreType.DMA((context_size - 1,)),
        ]
        + gather_sems(1)
        + gather_sems(1),
        compiler_params=pltpu.CompilerParams(
            collective_id=collective, has_side_effects=True, vmem_limit_bytes=56 << 20
        ),
        cost_estimate=pl.CostEstimate(
            flops=2 * tokens * model_width * all_width,
            bytes_accessed=200_000_000,
            transcendentals=tokens * width * 9,
        ),
        name="forward",
    )(hidden, gain, *shards, out_shard, open_part, counts, keep, flags, ids, head_gain)


def small_sum_kernel(
    mesh_axes, value, local_ref, total_ref, near, far, near_send, near_recv, far_send, far_recv
):
    shard_size, context_size = lax.axis_size("shard"), lax.axis_size("context")
    line_size = lax.axis_size("tensor")
    group = shard_size * context_size
    place = lax.axis_index("shard") * context_size + lax.axis_index("context")
    line_place = lax.axis_index("tensor")

    def device(position, line_position):
        places = {
            "shard": position // context_size,
            "context": lax.rem(position, context_size),
            "tensor": line_position,
        }
        return tuple(places[axis] for axis in mesh_axes)

    def near_target(step):
        return device(lax.rem(place + step, group), line_place)

    def far_target(step):
        return device(place, lax.rem(line_place + step, line_size))

    def near_copy(step):
        return pltpu.make_async_remote_copy(
            value,
            near.at[step - 1],
            near_send.at[step - 1],
            near_recv.at[step - 1],
            device_id=near_target(step),
            device_id_type=MESH_ID,
        )

    def far_copy(step):
        return pltpu.make_async_remote_copy(
            local_ref,
            far.at[step - 1],
            far_send.at[step - 1],
            far_recv.at[step - 1],
            device_id=far_target(step),
            device_id_type=MESH_ID,
        )

    barrier = pltpu.get_barrier_semaphore()
    for step in range(1, group):
        pl.semaphore_signal(barrier, inc=1, device_id=near_target(step), device_id_type=MESH_ID)
    for step in range(1, line_size):
        pl.semaphore_signal(barrier, inc=1, device_id=far_target(step), device_id_type=MESH_ID)
    pl.semaphore_wait(barrier, group + line_size - 2)
    for step in range(1, group):
        near_copy(step).start()
    total = value[...]
    for step in range(1, group):
        near_copy(step).wait_recv()
        total = total + near[step - 1]
    local_ref[...] = total
    for step in range(1, line_size):
        far_copy(step).start()
    for step in range(1, line_size):
        far_copy(step).wait_recv()
        total = total + far[step - 1]
    total_ref[...] = total
    for step in range(1, group):
        near_copy(step).wait_send()
    for step in range(1, line_size):
        far_copy(step).wait_send()


def small_sum(mesh_axes, collective, values):
    flat = jnp.concatenate([value.reshape(-1) for value in values])
    lanes = -(-flat.shape[0] // 1024) * 128
    flat = jnp.pad(flat, (0, 8 * lanes - flat.shape[0])).reshape(8, lanes)
    group = lax.axis_size("shard") * lax.axis_size("context")
    line_size = lax.axis_size("tensor")
    whole = pl.BlockSpec(memory_space=pltpu.VMEM)
    local, total = pl.pallas_call(
        partial(small_sum_kernel, mesh_axes),
        in_specs=[whole],
        out_specs=[whole] * 2,
        out_shape=[jax.ShapeDtypeStruct((8, lanes), F32)] * 2,
        scratch_shapes=[
            pltpu.VMEM((group - 1, 8, lanes), F32),
            pltpu.VMEM((line_size - 1, 8, lanes), F32),
            pltpu.SemaphoreType.DMA((group - 1,)),
            pltpu.SemaphoreType.DMA((group - 1,)),
            pltpu.SemaphoreType.DMA((line_size - 1,)),
            pltpu.SemaphoreType.DMA((line_size - 1,)),
        ],
        compiler_params=pltpu.CompilerParams(collective_id=collective, has_side_effects=True),
        cost_estimate=pl.CostEstimate(
            flops=8 * lanes * group, bytes_accessed=20_000_000, transcendentals=0
        ),
        name="small_sum",
    )(flat)
    return local.reshape(-1), total.reshape(-1)


def local(
    mesh_axes,
    hidden,
    segment_ids,
    norm1_gain,
    w_query,
    w_forget,
    w_input,
    w_gate_out,
    forget_floor,
    head_gain,
    w_out,
    norm2_gain,
    w_ffn_gate,
    w_ffn_up,
    w_ffn_down,
    out_grad,
):
    sequences, span_len, model_width = hidden.shape
    tokens = sequences * span_len
    head_count, key_dim = forget_floor.shape
    width = head_count * key_dim
    key_scale = key_dim ** (-0.5)
    both = ("shard", "context")
    gain_one, gain_two = norm1_gain.reshape(1, -1), norm2_gain.reshape(1, -1)
    hidden_rows = hidden.reshape(tokens, model_width)
    open_part = (1.0 - forget_floor).reshape(1, width)
    counts, keep, flags = row_flags(segment_ids)
    ends = segment_ids.reshape(-1).astype(F32)
    ids = jnp.where(lax.broadcasted_iota(jnp.int32, (8, key_dim), 0) == 1, ends[-1], ends[0])
    gain_row = head_gain.reshape(1, -1)
    (
        normed_one,
        pre,
        mixer_full,
        out_full,
        mixed,
        lead,
        starts,
        gated_low,
        mix_part,
        runs,
        carry,
        decay,
        link,
    ) = forward(
        mesh_axes,
        4,
        hidden_rows,
        gain_one,
        (w_query, w_forget, w_input, w_gate_out),
        w_out.T,
        open_part,
        (counts, keep, flags),
        ids,
        gain_row,
    )
    grad_rows = out_grad.reshape(tokens, model_width)
    (
        normed_two,
        grad_mix_low,
        grad_norm_two,
        residual,
        hidden_low,
        grad_gate_low,
        grad_up_low,
        feed_part,
        grad_residual,
    ) = middle(
        mesh_axes,
        2,
        mix_part,
        grad_rows,
        hidden_rows,
        gain_two,
        w_ffn_gate,
        w_ffn_up,
        w_ffn_down.T,
    )
    output_rows, grads_ffn, grad_out = output_line(
        mesh_axes,
        1,
        feed_part,
        residual,
        normed_two,
        grad_rows,
        hidden_low,
        grad_gate_low,
        grad_up_low,
        gated_low,
        grad_mix_low,
    )
    grad_gated = jnp.dot(grad_mix_low, out_full, preferred_element_type=F32)
    grad_mixed, grad_gate_pre, grad_head_part, back = gate_backward(
        grad_gated, mixed, lead, pre, gain_row, keep, head_count, key_scale
    )
    after = grad_after(back, decay, link[0, 0], "context")
    grad_pre, grad_floor_part = mixer_backward(
        pre,
        grad_mixed,
        grad_gate_pre,
        starts,
        runs,
        carry,
        after,
        open_part,
        counts,
        keep,
        flags,
    )
    grad_mixer = jnp.einsum("td,tk->dk", normed_one, grad_pre, preferred_element_type=F32)
    back_one = jnp.einsum("tk,dk->td", grad_pre, mixer_full, preferred_element_type=F32)
    input_rows, grad_norm_one, share_gate, share_up, share_down = input_line(
        mesh_axes, 3, back_one.astype(BF16), hidden_rows, grad_residual, gain_one, grads_ffn
    )
    near, total = small_sum(
        mesh_axes, 5, (grad_norm_one, grad_norm_two, grad_head_part, grad_floor_part)
    )
    shares = lax.axis_size("shard") * lax.axis_size("context")
    position = lax.axis_index("shard") * lax.axis_size("context") + lax.axis_index("context")

    def own_slice(values, first, length):
        values = values[first : first + length].reshape(shares, length // shares)
        return lax.dynamic_index_in_dim(values, position, 0, False)

    floor_total = near[2 * model_width + key_dim : 2 * model_width + key_dim + width]
    floor_total = floor_total.reshape(head_count, shares, key_dim // shares)

    def share(values, dim):
        return lax.psum_scatter(
            values.astype(BF16), both, scatter_dimension=dim, tiled=True
        ).astype(F32)

    share_mixer = share(grad_mixer, 0)
    return (
        output_rows.reshape(hidden.shape),
        input_rows.reshape(hidden.shape),
        own_slice(total, 0, model_width),
        share_mixer[:, :width],
        share_mixer[:, width : 2 * width],
        share_mixer[:, 2 * width : 3 * width],
        share_mixer[:, 3 * width :],
        lax.dynamic_index_in_dim(floor_total, position, 1, False),
        own_slice(total, 2 * model_width, key_dim),
        share(grad_out, 0).T,
        own_slice(total, model_width, model_width),
        share_gate,
        share_up,
        share_down.T,
    )


def solution(mesh):
    in_specs = (
        P("shard", "context", None),
        P("shard", "context"),
        P(),
        P(("shard", "context"), "tensor"),
        P(("shard", "context"), "tensor"),
        P(("shard", "context"), "tensor"),
        P(("shard", "context"), "tensor"),
        P("tensor", None),
        P(),
        P("tensor", ("shard", "context")),
        P(),
        P(("shard", "context"), "tensor"),
        P(("shard", "context"), "tensor"),
        P("tensor", ("shard", "context")),
        P("shard", "context", None),
    )
    out_specs = (
        P("shard", "context", None),
        P("shard", "context", None),
        P(("shard", "context")),
        P(("shard", "context"), "tensor"),
        P(("shard", "context"), "tensor"),
        P(("shard", "context"), "tensor"),
        P(("shard", "context"), "tensor"),
        P("tensor", ("shard", "context")),
        P(("shard", "context")),
        P("tensor", ("shard", "context")),
        P(("shard", "context")),
        P(("shard", "context"), "tensor"),
        P(("shard", "context"), "tensor"),
        P("tensor", ("shard", "context")),
    )
    return jax.shard_map(
        partial(local, mesh.axis_names), mesh=mesh, in_specs=in_specs, out_specs=out_specs, check_vma=False)
```

```python
from functools import partial

import jax
import jax.numpy as jnp
from jax import lax
from jax.experimental import pallas as pl
from jax.experimental.pallas import tpu as pltpu
from jax.sharding import PartitionSpec as P

EPSILON = 1e-05


BLOCK = 128
F32 = jnp.float32
BF16 = jnp.bfloat16


def mm(a, b, dims):
    return lax.dot_general(a, b, (dims, ((), ())), preferred_element_type=F32)


def mm_nn(a, b):
    return mm(a, b, ((1,), (0,)))


def mm_nt(a, b):
    return mm(a, b, ((1,), (1,)))


def mm_tn(a, b):
    return mm(a, b, ((0,), (0,)))


def split_sum(tri, values):
    high = values.astype(BF16)
    low = (values - high.astype(F32)).astype(BF16)
    return mm_nn(tri, high) + mm_nn(tri, low)


def block_masks(counts, flags_row):
    rows = counts.shape[0]
    row_ids = lax.broadcasted_iota(jnp.int32, (rows, rows), 0)
    col_ids = lax.broadcasted_iota(jnp.int32, (rows, rows), 1)
    linked = jnp.logical_and(counts == flags_row[0:1], row_ids >= col_ids)
    fresh = (counts == flags_row[1:2, 0:1]).astype(F32)
    tail = (counts == flags_row[2:3, 0:1]).astype(F32)
    closing = (flags_row[1:2, 0:1] == flags_row[2:3, 0:1]).astype(F32)
    return row_ids, col_ids, linked, fresh, tail, closing


def gate_backward_kernel(
    head_count,
    key_scale,
    grad_ref,
    mixed_ref,
    lead_ref,
    gate_ref,
    gain_ref,
    keep_ref,
    grad_mixed_ref,
    grad_gate_ref,
    grad_gain_ref,
    back_ref,
):
    lanes = gain_ref.shape[1]

    @pl.when(pl.program_id(0) == 0)
    def _():
        grad_gain_ref[...] = jnp.zeros_like(grad_gain_ref)
        back_ref[...] = jnp.zeros_like(back_ref)

    gain = gain_ref[...]
    total = jnp.zeros_like(gain)
    for head in range(head_count):
        part = slice(head * lanes, (head + 1) * lanes)
        mixed, gate, grad = mixed_ref[:, part], gate_ref[:, part], grad_ref[:, part]
        inverse = lax.rsqrt(jnp.mean(mixed * mixed, axis=-1, keepdims=True) + EPSILON)
        unit = mixed * inverse
        sigma = jax.nn.sigmoid(gate)
        scaled = grad * unit
        total = total + jnp.sum(scaled * (gate * sigma), axis=0, keepdims=True)
        grad_gate = scaled * gain * sigma * (1.0 + gate * (1.0 - sigma))
        grad_gate_ref[:, part] = grad_gate.astype(BF16)
        lifted = grad * gain * (gate * sigma)
        mean = jnp.mean(lifted * unit, axis=-1, keepdims=True)
        grad_mixed = inverse * (lifted - unit * mean) * (key_scale * keep_ref[...])
        grad_mixed = grad_mixed.astype(BF16)
        grad_mixed_ref[:, part] = grad_mixed
        back_ref[head] += mm_tn(grad_mixed, lead_ref[:, part])
    grad_gain_ref[...] += total


def gate_backward(grad, mixed, lead, pre, gain, keep, head_count, key_scale):
    tokens, width = mixed.shape
    lanes = gain.shape[1]
    rows = 2 * BLOCK
    return pl.pallas_call(
        partial(gate_backward_kernel, head_count, key_scale),
        grid=(tokens // rows,),
        in_specs=[
            pl.BlockSpec((rows, width), lambda i: (i, 0)),
            pl.BlockSpec((rows, width), lambda i: (i, 0)),
            pl.BlockSpec((rows, width), lambda i: (i, 0)),
            pl.BlockSpec((rows, width), lambda i: (i, 3)),
            pl.BlockSpec((1, lanes), lambda i: (0, 0)),
            pl.BlockSpec((rows, 1), lambda i: (i, 0)),
        ],
        out_specs=[
            pl.BlockSpec((rows, width), lambda i: (i, 0)),
            pl.BlockSpec((rows, width), lambda i: (i, 0)),
            pl.BlockSpec((1, lanes), lambda i: (0, 0)),
            pl.BlockSpec((head_count, lanes, lanes), lambda i: (0, 0, 0)),
        ],
        out_shape=[
            jax.ShapeDtypeStruct((tokens, width), BF16),
            jax.ShapeDtypeStruct((tokens, width), BF16),
            jax.ShapeDtypeStruct((1, lanes), F32),
            jax.ShapeDtypeStruct((head_count, lanes, lanes), F32),
        ],
        compiler_params=pltpu.CompilerParams(
            dimension_semantics=("arbitrary",), vmem_limit_bytes=40 << 20
        ),
        cost_estimate=pl.CostEstimate(
            flops=tokens * width * 300,
            bytes_accessed=tokens * width * 18,
            transcendentals=tokens * width,
        ),
        name="gate_backward",
    )(grad, mixed, lead, pre, gain, keep)


def mixer_backward_kernel(
    head_count,
    pre_ref,
    grad_mixed_ref,
    grad_gate_ref,
    start_ref,
    run_ref,
    carry_ref,
    after_ref,
    open_ref,
    count_ref,
    keep_ref,
    flags_ref,
    grads_ref,
    floor_ref,
    grad_scr,
    lifted_scr,
    lowered_scr,
    moved_scr,
    value_scr,
):
    width = open_ref.shape[1]
    lanes = width // head_count

    @pl.when(pl.program_id(0) == 0)
    def _():
        grad_scr[...] = after_ref[...]
        floor_ref[...] = jnp.zeros_like(floor_ref)

    counts, keep = count_ref[...], keep_ref[...]
    flags = flags_ref[0]
    row_ids, col_ids, linked, fresh, tail, closing = block_masks(counts, flags)
    tri = (row_ids >= col_ids).astype(BF16)
    tri_back = (row_ids <= col_ids).astype(BF16)
    query_pre = pre_ref[:, :width]
    values = pre_ref[:, 2 * width : 3 * width].astype(BF16)
    opened = open_ref[...]
    closed = jax.nn.sigmoid(-pre_ref[:, width : 2 * width])
    keys = opened * closed
    cum = split_sum(tri, jnp.log1p(-keys))
    rows = cum.shape[0]
    ending = cum[rows - 1 : rows, :]
    rise, fall = jnp.exp(cum), jnp.exp(-cum) * keep
    shift = jnp.exp(ending - cum) * (keep * tail)
    sigma_query = jax.nn.sigmoid(query_pre)
    lifted = (query_pre * sigma_query * rise).astype(BF16)
    lowered = (keys * fall).astype(BF16)
    moved = (keys * shift).astype(BF16)
    fresh_lifted = (lifted.astype(F32) * fresh).astype(BF16)
    end_decay = jnp.exp(ending) * closing
    lead_in = jnp.exp(run_ref[0]) * (flags[1:2, 0:1] == 0).astype(F32)
    for head in range(head_count):
        part = slice(head * lanes, (head + 1) * lanes)
        grad_out, value = grad_mixed_ref[:, part], values[:, part]
        lift, lower, move = lifted[:, part], lowered[:, part], moved[:, part]
        scores = jnp.where(linked, mm_nt(lift, lower), 0.0).astype(BF16)
        pulls = jnp.where(linked, mm_nt(grad_out, value), 0.0).astype(BF16)
        state = start_ref[0, head] + lead_in[:, part] * carry_ref[head]
        grad_state = grad_scr[head]
        grad_low = grad_state.astype(BF16)
        lifted_scr[:, part] = mm_nn(pulls, lower) + fresh * mm_nn(grad_out, state.astype(BF16))
        lowered_scr[:, part] = mm_tn(pulls, lift)
        grad_moved = mm_nn(value, grad_low)
        moved_scr[:, part] = grad_moved
        grads_ref[:, 2 * width + head * lanes : 2 * width + (head + 1) * lanes] = (
            mm_tn(scores, grad_out) + mm_nt(move, grad_low)
        ).astype(BF16)
        value_scr[:, part] = jnp.sum(
            grad_moved * move.astype(F32), axis=0, keepdims=True
        ) + end_decay[:, part] * jnp.sum(state * grad_state, axis=0, keepdims=True)
        grad_scr[head] = grad_state * end_decay[:, part] + mm_tn(grad_out, fresh_lifted[:, part])
    grad_lifted, grad_lowered, grad_moved = lifted_scr[...], lowered_scr[...], moved_scr[...]
    grad_cum = (
        grad_lifted * lifted.astype(F32)
        - grad_lowered * lowered.astype(F32)
        - grad_moved * moved.astype(F32)
    )
    grad_decay = split_sum(tri_back, grad_cum) + value_scr[...]
    key_total = grad_lowered * fall + grad_moved * shift - grad_decay / (1.0 - keys)
    floor_ref[...] -= jnp.sum(key_total * closed, axis=0, keepdims=True)
    grads_ref[:, :width] = (
        grad_lifted * rise * sigma_query * (1.0 + query_pre * (1.0 - sigma_query))
    ).astype(BF16)
    grads_ref[:, width : 2 * width] = (-key_total * opened * closed * (1.0 - closed)).astype(BF16)
    grads_ref[:, 3 * width :] = grad_gate_ref[...]


def mixer_backward(
    pre, grad_mixed, grad_gate, starts, runs, carry, after, open_part, counts, keep, flags
):
    tokens, all_width = pre.shape
    width = open_part.shape[1]
    head_count, lanes = carry.shape[0], carry.shape[2]
    blocks = tokens // BLOCK
    last = blocks - 1
    return pl.pallas_call(
        partial(mixer_backward_kernel, head_count),
        grid=(blocks,),
        in_specs=[
            pl.BlockSpec((BLOCK, all_width), lambda i: (last - i, 0)),
            pl.BlockSpec((BLOCK, width), lambda i: (last - i, 0)),
            pl.BlockSpec((BLOCK, width), lambda i: (last - i, 0)),
            pl.BlockSpec((1, head_count, lanes, lanes), lambda i: (last - i, 0, 0, 0)),
            pl.BlockSpec((1, 1, width), lambda i: (last - i, 0, 0)),
            pl.BlockSpec((head_count, lanes, lanes), lambda i: (0, 0, 0)),
            pl.BlockSpec((head_count, lanes, lanes), lambda i: (0, 0, 0)),
            pl.BlockSpec((1, width), lambda i: (0, 0)),
            pl.BlockSpec((BLOCK, 1), lambda i: (last - i, 0)),
            pl.BlockSpec((BLOCK, 1), lambda i: (last - i, 0)),
            pl.BlockSpec((1, 8, BLOCK), lambda i: (last - i, 0, 0)),
        ],
        out_specs=[
            pl.BlockSpec((BLOCK, all_width), lambda i: (last - i, 0)),
            pl.BlockSpec((1, width), lambda i: (0, 0)),
        ],
        out_shape=[
            jax.ShapeDtypeStruct((tokens, all_width), BF16),
            jax.ShapeDtypeStruct((1, width), F32),
        ],
        scratch_shapes=[
            pltpu.VMEM((head_count, lanes, lanes), F32),
            pltpu.VMEM((BLOCK, width), F32),
            pltpu.VMEM((BLOCK, width), F32),
            pltpu.VMEM((BLOCK, width), F32),
            pltpu.VMEM((1, width), F32),
        ],
        compiler_params=pltpu.CompilerParams(
            dimension_semantics=("arbitrary",), vmem_limit_bytes=40 << 20
        ),
        cost_estimate=pl.CostEstimate(
            flops=tokens * width * BLOCK * 30,
            bytes_accessed=tokens * width * 36,
            transcendentals=tokens * width * 9,
        ),
        name="mixer_backward",
    )(pre, grad_mixed, grad_gate, starts, runs, carry, after, open_part, counts, keep, flags)


def from_later(values, axis, shift):
    count = lax.axis_size(axis)
    return lax.ppermute(values, axis, [(i + shift, i) for i in range(count - shift)])


def grad_after(back, decay, link_in, axis):
    head_count, lanes, _ = back.shape
    rows = head_count * lanes
    message = (
        jnp.concatenate([back.reshape(rows, lanes), decay.reshape(head_count, lanes)]) * link_in
    )
    message = jnp.pad(message, ((0, 8 - head_count % 8 if head_count % 8 else 0), (0, 0)))
    total = jnp.zeros_like(back)
    factor = jnp.ones((head_count, 1, lanes), F32)
    for shift in range(1, lax.axis_size(axis)):
        got = from_later(message, axis, shift)
        total = total + factor * got[:rows].reshape(back.shape)
        factor = factor * got[rows : rows + head_count].reshape(head_count, 1, lanes)
    return total


CHUNK = 32
LAG = 2
MESH_ID = pl.DeviceIdType.MESH


class Line:
    def __init__(self, mesh_axes, part, arrived, out, sems, transform):
        self.mesh_axes = mesh_axes
        self.part, self.arrived, self.out = part, arrived, out
        self.sum_send, self.sum_recv, self.back_send, self.back_recv = sems
        self.transform = transform
        self.half = part.shape[0] // 2
        self.chunks = self.half // CHUNK
        self.size = lax.axis_size("tensor")
        self.place = lax.axis_index("tensor")
        self.lines = ((self.size - 1 - self.place, -1), (self.place, 1))
        self.steps = self.chunks + 2 * LAG * (self.size - 1)

    def device(self, position):
        return tuple(
            jnp.clip(position, 0, self.size - 1) if axis == "tensor" else lax.axis_index(axis)
            for axis in self.mesh_axes
        )

    def greet(self, barrier):
        for step in (-1, 1):
            inside = jnp.logical_and(self.place + step >= 0, self.place + step < self.size)

            @pl.when(inside)
            def _(step=step):
                pl.semaphore_signal(
                    barrier, inc=1, device_id=self.device(self.place + step), device_id_type=MESH_ID
                )

        at_end = jnp.logical_or(self.place == 0, self.place == self.size - 1)
        return jnp.where(at_end, 1, 2)

    def rows_of(self, side, index):
        return pl.ds(pl.multiple_of(side * self.half + index * CHUNK, CHUNK), CHUNK)

    def sum_copy(self, side, index, source):
        rows = self.rows_of(side, index)
        return pltpu.make_async_remote_copy(
            source.at[rows],
            self.arrived.at[rows],
            self.sum_send.at[side, index],
            self.sum_recv.at[side, index],
            device_id=self.device(self.place + self.lines[side][1]),
            device_id_type=MESH_ID,
        )

    def back_copy(self, side, index):
        rows = self.rows_of(side, index)
        return pltpu.make_async_remote_copy(
            self.out.at[rows],
            self.out.at[rows],
            self.back_send.at[side, index],
            self.back_recv.at[side, index],
            device_id=self.device(self.place - self.lines[side][1]),
            device_id_type=MESH_ID,
        )

    def step(self, time):
        for side in (0, 1):
            hops = self.lines[side][0]
            index = time - LAG * hops
            valid = jnp.logical_and(index >= 0, index < self.chunks)
            at_source, at_owner = hops == 0, hops == self.size - 1
            index = jnp.clip(index, 0, self.chunks - 1)
            rows = self.rows_of(side, index)

            @pl.when(jnp.logical_and(valid, at_source))
            def _(side=side, index=index):
                self.sum_copy(side, index, self.part).start()

            @pl.when(jnp.logical_and(valid, jnp.logical_not(at_source)))
            def _(side=side, index=index):
                self.sum_copy(side, index, self.arrived).wait_recv()

            between = jnp.logical_and(jnp.logical_not(at_source), jnp.logical_not(at_owner))

            @pl.when(jnp.logical_and(valid, between))
            def _(side=side, index=index, rows=rows):
                total = self.part[rows].astype(F32) + self.arrived[rows].astype(F32)
                self.arrived[rows] = total.astype(BF16)
                self.sum_copy(side, index, self.arrived).start()

            @pl.when(jnp.logical_and(valid, at_owner))
            def _(side=side, index=index, rows=rows):
                total = self.part[rows].astype(F32) + self.arrived[rows].astype(F32)
                own = pl.ds(pl.multiple_of(index * CHUNK, CHUNK), CHUNK)
                self.transform(total, rows, own)
                self.back_copy(side, index).start()

            away = self.size - 1 - hops
            index = time - LAG * (self.size - 1 + away)
            valid = jnp.logical_and(jnp.logical_and(index >= 0, index < self.chunks), away > 0)
            index = jnp.clip(index, 0, self.chunks - 1)

            @pl.when(valid)
            def _(side=side, index=index):
                self.back_copy(side, index).wait_recv()

            @pl.when(jnp.logical_and(valid, away < self.size - 1))
            def _(side=side, index=index):
                self.back_copy(side, index).start()

    def run(self, first, last, beside=None):
        def body(time, _):
            self.step(time)
            if beside is not None:
                beside(time)
            return 0

        lax.fori_loop(first, last, body, 0)

    def source_sent(self, first, last):
        def body(index, _):
            for side in (0, 1):

                @pl.when(self.lines[side][0] == 0)
                def _(side=side):
                    self.sum_copy(side, index, self.part).wait_send()

            return 0

        lax.fori_loop(first, last, body, 0)

    def finish(self, source_waits=True):
        def body(index, _):
            for side in (0, 1):
                hops = self.lines[side][0]
                passed = hops < self.size - 1
                if not source_waits:
                    passed = jnp.logical_and(passed, hops > 0)

                @pl.when(passed)
                def _(side=side):
                    self.sum_copy(side, index, self.arrived).wait_send()

                @pl.when(hops > 0)
                def _(side=side):
                    self.back_copy(side, index).wait_send()

            return 0

        lax.fori_loop(0, self.chunks, body, 0)


def line_sems(tokens):
    return [pltpu.SemaphoreType.DMA((2, tokens // 2 // CHUNK))] * 4


def inverse_rms(values):
    return lax.rsqrt(jnp.mean(values * values, axis=-1, keepdims=True) + EPSILON)


class Plane:
    def __init__(self, mesh_axes):
        self.mesh_axes = mesh_axes
        self.context = lax.axis_size("context")
        self.per_row = self.context // 2
        self.chips = lax.axis_size("shard") * self.per_row
        context_place = lax.axis_index("context")
        self.core = lax.rem(context_place, 2)
        self.chip = lax.axis_index("shard") * self.per_row + context_place // 2

    def device(self, chip, core):
        places = {
            "shard": chip // self.per_row,
            "context": 2 * lax.rem(chip, self.per_row) + core,
            "tensor": lax.axis_index("tensor"),
        }
        return tuple(places[axis] for axis in self.mesh_axes)

    def ahead(self, distance):
        return lax.rem(self.chip + distance, self.chips)

    def greet(self, barrier):
        targets = [self.device(self.chip, 1 - self.core)]
        targets += [self.device(self.ahead(step), self.core) for step in range(1, self.chips)]
        for target in targets:
            pl.semaphore_signal(barrier, inc=1, device_id=target, device_id_type=MESH_ID)
        return len(targets)


class Gather:
    def __init__(self, plane, sources, targets, sems):
        self.plane, self.sources, self.targets = plane, sources, targets
        self.load_sem, self.send_sem, self.recv_sem, self.pair_send, self.pair_recv = sems
        self.block = sources[0].shape[0]
        self.part = self.block // 2
        self.relayed = plane.chips == 4
        self.arrays = range(len(sources))

    def partner(self, distance):
        return jnp.bitwise_xor(self.plane.chip, distance)

    def greet(self, barrier):
        plane = self.plane
        targets = [plane.device(plane.chip, 1 - plane.core)]
        targets += [
            plane.device(self.partner(step), plane.core)
            for step in range(1, 3 if self.relayed else plane.chips)
        ]
        for target in targets:
            pl.semaphore_signal(barrier, inc=1, device_id=target, device_id_type=MESH_ID)
        return len(targets)

    def place(self, array, chip, core, half):
        first = (2 * chip + core) * self.block + half * self.part
        rows = pl.ds(pl.multiple_of(first, self.part), self.part)
        return self.targets[array].at[rows, pl.ds(0, self.sources[array].shape[1])]

    def mine(self, array, half):
        return self.sources[array].at[pl.ds(half * self.part, self.part)]

    def loads(self):
        plane = self.plane
        return [
            pltpu.make_async_copy(
                self.mine(array, half),
                self.place(array, plane.chip, plane.core, half),
                self.load_sem.at[array, half],
            )
            for array in self.arrays
            for half in range(2)
        ]

    def send(self, distance, half):
        plane = self.plane
        copies = []
        for array in self.arrays:
            chip, target = plane.chip, self.partner(distance)
            source = self.mine(array, half)
            if self.relayed and distance == 3:
                chip = self.partner(2 if half == 0 else 1)
                target = self.partner(1 if half == 0 else 2)
                source = self.place(array, chip, plane.core, half)
            copies.append(
                pltpu.make_async_remote_copy(
                    source,
                    self.place(array, chip, plane.core, half),
                    self.send_sem.at[array, distance - 1, half],
                    self.recv_sem.at[array, distance - 1, half],
                    device_id=plane.device(target, plane.core),
                    device_id_type=MESH_ID,
                )
            )
        return copies

    def forward(self, distance, half):
        plane = self.plane
        copies = []
        for array in self.arrays:
            place = self.place(array, self.partner(distance), plane.core, half)
            copies.append(
                pltpu.make_async_remote_copy(
                    self.mine(array, half) if distance == 0 else place,
                    place,
                    self.pair_send.at[array, distance, half],
                    self.pair_recv.at[array, distance, half],
                    device_id=plane.device(plane.chip, 1 - plane.core),
                    device_id_type=MESH_ID,
                )
            )
        return copies

    def start(self):
        if self.relayed:
            order = ((1, 1), (2, 0), (1, 0), (2, 1))
        else:
            order = [(step, half) for step in range(1, self.plane.chips) for half in range(2)]
        for distance, half in order:
            for copy in self.send(distance, half):
                copy.start()
        for copy in self.loads():
            copy.start()
        for half in range(2):
            for copy in self.forward(0, half):
                copy.start()

    def take(self, distance, half, relay):
        for copy in self.send(distance, half):
            copy.wait_recv()
        if relay:
            for copy in self.send(3, half):
                copy.start()
        for copy in self.forward(distance, half):
            copy.start()

    def stage(self, number):
        if self.relayed:
            if number == 0:
                self.take(1, 1, True)
                self.take(2, 0, True)
            elif number == 1:
                self.take(1, 0, False)
                self.take(2, 1, False)
            else:
                self.take(3, 0, False)
                self.take(3, 1, False)
        elif number == 2:
            for distance in range(1, self.plane.chips):
                for half in range(2):
                    self.take(distance, half, False)

    def arrive_from(self, distance):
        if distance == 0:
            for copy in self.loads():
                copy.wait()
        for half in range(2):
            for copy in self.forward(distance, half):
                copy.wait_recv()

    def arrive(self):
        for distance in range(self.plane.chips):
            self.arrive_from(distance)

    def finish(self):
        for distance in range(self.plane.chips):
            for half in range(2):
                for copy in self.forward(distance, half):
                    copy.wait_send()
                if distance > 0:
                    for copy in self.send(distance, half):
                        copy.wait_send()


def gather_sems(arrays):
    chips = lax.axis_size("shard") * lax.axis_size("context") // 2
    return [
        pltpu.SemaphoreType.DMA((arrays, 2)),
        pltpu.SemaphoreType.DMA((arrays, chips - 1, 2)),
        pltpu.SemaphoreType.DMA((arrays, chips - 1, 2)),
        pltpu.SemaphoreType.DMA((arrays, chips, 2)),
        pltpu.SemaphoreType.DMA((arrays, chips, 2)),
    ]


GROUP = 128
TILE = 256
WIDE = 512


def middle_kernel(
    mesh_axes,
    mix_hbm,
    cotangent_ref,
    input_hbm,
    gain_ref,
    gate_hbm,
    up_hbm,
    down_hbm,
    normed_ref,
    out_ref,
    gain_grad,
    residual_hbm,
    hidden_hbm,
    grad_gate_hbm,
    grad_up_hbm,
    feed_hbm,
    grad_hbm,
    gate_w,
    up_w,
    down_w,
    part,
    mix_arrived,
    arrived,
    inputs,
    residual,
    stage_hidden,
    stage_gate,
    stage_up,
    stage_feed,
    part_sem,
    input_sem,
    save_sem,
    stage_sem,
    grad_sem,
    *sems,
):
    tokens, model_width = normed_ref.shape
    half = tokens // 2
    hidden_width = gate_hbm.shape[1]
    padded = gate_w.shape[1]
    groups = half // GROUP
    place, line_size = lax.axis_index("tensor"), lax.axis_size("tensor")
    own_half = pl.ds(pl.multiple_of(jnp.where(place == 0, 0, half), half), half)
    part_load = pltpu.make_async_copy(mix_hbm, part, part_sem.at[0])
    part_load.start()
    input_load = pltpu.make_async_copy(input_hbm.at[own_half], inputs, input_sem.at[0])
    input_load.start()
    if padded > hidden_width:
        spare = slice(hidden_width, padded)
        gate_w[:, spare] = jnp.zeros((model_width, padded - hidden_width), BF16)
        up_w[:, spare] = jnp.zeros((model_width, padded - hidden_width), BF16)
        down_w[:, spare] = jnp.zeros((model_width, padded - hidden_width), BF16)
    gain_grad[...] = jnp.zeros_like(gain_grad)

    def mix_turn(total, rows, own):
        values = inputs[own].astype(F32) + total
        residual[own] = values
        normed_ref[rows] = (values * inverse_rms(values) * gain_ref[...]).astype(BF16)

    def turn(total, rows, own):
        values = residual[own]
        inverse = inverse_rms(values)
        unit = values * inverse
        gain_grad[...] += jnp.sum(total * unit, axis=0, keepdims=True)
        lifted = total * gain_ref[...]
        mean = jnp.mean(lifted * unit, axis=-1, keepdims=True)
        grad = cotangent_ref[rows].astype(F32) + inverse * (lifted - unit * mean)
        residual[own] = grad
        out_ref[rows] = grad.astype(BF16)

    mix_line = Line(mesh_axes, part, mix_arrived, normed_ref, sems[:4], mix_turn)
    line = Line(mesh_axes, part, arrived, out_ref, sems[4:8], turn)
    gather = Gather(
        Plane(mesh_axes), (gate_hbm, up_hbm, down_hbm), (gate_w, up_w, down_w), sems[8:]
    )
    barrier = pltpu.get_barrier_semaphore()
    expected = mix_line.greet(barrier) + gather.greet(barrier)
    pl.semaphore_wait(barrier, expected)
    gather.start()
    part_load.wait()
    input_load.wait()
    pace = GROUP // CHUNK
    begin = pace + 2 * LAG * (line_size - 1) + 4
    mix_line.run(0, begin - 10)
    gather.stage(0)
    mix_line.run(begin - 10, begin - 4)
    gather.stage(1)
    mix_line.run(begin - 4, begin)
    gather.stage(2)
    gather.arrive()

    def both(ref, group):
        first = pl.ds(pl.multiple_of(group * GROUP, GROUP), GROUP)
        second = pl.ds(pl.multiple_of(half + group * GROUP, GROUP), GROUP)
        return first, second

    def stage_copies(group):
        slot = lax.rem(group, 2)
        copies = []
        for side, rows in enumerate(both(None, group)):
            from_rows = pl.ds(side * GROUP, GROUP)
            columns = pl.ds(0, hidden_width)
            for which, (stage, target) in enumerate(
                (
                    (stage_hidden, hidden_hbm),
                    (stage_gate, grad_gate_hbm),
                    (stage_up, grad_up_hbm),
                )
            ):
                copies.append(
                    pltpu.make_async_copy(
                        stage.at[slot, from_rows, columns],
                        target.at[rows],
                        stage_sem.at[slot, which, side],
                    )
                )
            copies.append(
                pltpu.make_async_copy(
                    stage_feed.at[slot, from_rows], feed_hbm.at[rows], stage_sem.at[slot, 3, side]
                )
            )
        return copies

    def hidden_tile(group, tile):
        first, second = both(normed_ref, group)
        slot = lax.rem(group, 2)
        columns = pl.ds(pl.multiple_of(tile * WIDE, WIDE), WIDE)
        rows = jnp.concatenate([normed_ref[first], normed_ref[second]], axis=0)
        gate = mm_nn(rows, gate_w[:, columns])
        up = mm_nn(rows, up_w[:, columns])
        grads = jnp.concatenate([cotangent_ref[first], cotangent_ref[second]], axis=0)
        grad = mm_nn(grads, down_w[:, columns])
        sigma = jax.nn.sigmoid(gate)
        active = gate * sigma
        stage_hidden[slot, :, columns] = (active * up).astype(BF16)
        stage_gate[slot, :, columns] = (grad * up * sigma * (1.0 + gate * (1.0 - sigma))).astype(
            BF16
        )
        stage_up[slot, :, columns] = (grad * active).astype(BF16)

    def model_tile(group, tile):
        first, second = both(part, group)
        slot = lax.rem(group, 2)
        columns = pl.ds(pl.multiple_of(tile * WIDE, WIDE), WIDE)
        back = mm_nt(stage_gate[slot], gate_w[columns, :])
        back = (back + mm_nt(stage_up[slot], up_w[columns, :])).astype(BF16)
        part[first, columns] = back[:GROUP]
        part[second, columns] = back[GROUP:]
        stage_feed[slot, :, columns] = mm_nt(stage_hidden[slot], down_w[columns, :]).astype(BF16)

    hidden_tiles, model_tiles = padded // WIDE, model_width // WIDE
    ticks = hidden_tiles + model_tiles
    piece = -(-ticks // pace)
    save = pltpu.make_async_copy(residual, residual_hbm, save_sem.at[0])

    def group_body(group, _):
        mix_line.source_sent(group * pace, (group + 1) * pace)

        @pl.when(group == 1)
        def _():
            save.start()

        @pl.when(group == 2)
        def _():
            save.wait()

        @pl.when(group >= 2)
        def _():
            for copy in stage_copies(group - 2):
                copy.wait()

        def piece_body(index, _):
            def tick_body(offset, _):
                tick = index * piece + offset

                @pl.when(tick < hidden_tiles)
                def _():
                    hidden_tile(group, tick)

                @pl.when(jnp.logical_and(tick >= hidden_tiles, tick < ticks))
                def _():
                    model_tile(group, tick - hidden_tiles)

                return 0

            lax.fori_loop(0, piece, tick_body, 0)

            mix_time = begin + group * pace + index

            @pl.when(mix_time < mix_line.steps)
            def _():
                mix_line.step(mix_time)

            @pl.when(group >= 1)
            def _():
                line.step((group - 1) * pace + index)

            return 0

        lax.fori_loop(0, pace, piece_body, 0)
        for copy in stage_copies(group):
            copy.start()
        return 0

    lax.fori_loop(0, groups, group_body, 0)
    line.run((groups - 1) * pace, line.steps)
    grad_save = pltpu.make_async_copy(residual, grad_hbm, grad_sem.at[0])
    grad_save.start()
    for group in range(max(groups - 2, 0), groups):
        for copy in stage_copies(group):
            copy.wait()
    gather.finish()
    mix_line.finish(source_waits=False)
    line.finish()
    grad_save.wait()


def middle(mesh_axes, collective, mix, cotangent, inputs, gain, gate_w, up_w, down_w):
    tokens, model_width = mix.shape
    hidden_width = gate_w.shape[1]
    padded = -(-hidden_width // WIDE) * WIDE
    whole = pl.BlockSpec(memory_space=pltpu.VMEM)
    remote = pl.BlockSpec(memory_space=pl.ANY)
    group_rows = 2 * GROUP
    return pl.pallas_call(
        partial(middle_kernel, mesh_axes),
        in_specs=[remote, whole, remote, whole, remote, remote, remote],
        out_specs=[whole, whole, whole] + [remote] * 6,
        out_shape=[
            jax.ShapeDtypeStruct((tokens, model_width), BF16),
            jax.ShapeDtypeStruct((tokens, model_width), BF16),
            jax.ShapeDtypeStruct((1, model_width), F32),
            jax.ShapeDtypeStruct((tokens // 2, model_width), F32),
            jax.ShapeDtypeStruct((tokens, hidden_width), BF16),
            jax.ShapeDtypeStruct((tokens, hidden_width), BF16),
            jax.ShapeDtypeStruct((tokens, hidden_width), BF16),
            jax.ShapeDtypeStruct((tokens, model_width), BF16),
            jax.ShapeDtypeStruct((tokens // 2, model_width), F32),
        ],
        scratch_shapes=[
            pltpu.VMEM((model_width, padded), BF16),
            pltpu.VMEM((model_width, padded), BF16),
            pltpu.VMEM((model_width, padded), BF16),
            pltpu.VMEM((tokens, model_width), BF16),
            pltpu.VMEM((tokens, model_width), BF16),
            pltpu.VMEM((tokens, model_width), BF16),
            pltpu.VMEM((tokens // 2, model_width), BF16),
            pltpu.VMEM((tokens // 2, model_width), F32),
            pltpu.VMEM((2, group_rows, padded), BF16),
            pltpu.VMEM((2, group_rows, padded), BF16),
            pltpu.VMEM((2, group_rows, padded), BF16),
            pltpu.VMEM((2, group_rows, model_width), BF16),
            pltpu.SemaphoreType.DMA((1,)),
            pltpu.SemaphoreType.DMA((1,)),
            pltpu.SemaphoreType.DMA((1,)),
            pltpu.SemaphoreType.DMA((2, 4, 2)),
            pltpu.SemaphoreType.DMA((1,)),
        ]
        + line_sems(tokens)
        + line_sems(tokens)
        + gather_sems(3),
        compiler_params=pltpu.CompilerParams(
            collective_id=collective, has_side_effects=True, vmem_limit_bytes=61 << 20
        ),
        cost_estimate=pl.CostEstimate(
            flops=tokens * model_width * hidden_width * 12,
            bytes_accessed=360_000_000,
            transcendentals=tokens * hidden_width,
        ),
        name="middle",
    )(mix, cotangent, inputs, gain, gate_w, up_w, down_w)


def output_kernel(
    mesh_axes,
    part,
    residual,
    normed_ref,
    cotangent_ref,
    hidden_ref,
    grad_gate_ref,
    grad_up_ref,
    gated_ref,
    mix_grad_ref,
    out_ref,
    grads_hbm,
    out_grads_hbm,
    arrived,
    stage,
    out_stage,
    stage_sem,
    out_sem,
    *sems,
):
    model_width = normed_ref.shape[1]
    tiles = model_width // TILE

    def turn(total, rows, own):
        out_ref[rows] = (residual[own] + total).astype(BF16)

    line = Line(mesh_axes, part, arrived, out_ref, sems, turn)
    barrier = pltpu.get_barrier_semaphore()
    pl.semaphore_wait(barrier, line.greet(barrier))

    def stage_copies(tile):
        rows = pl.ds(pl.multiple_of(tile * TILE, TILE), TILE)
        slot = lax.rem(tile, 2)
        return (
            pltpu.make_async_copy(stage.at[slot], grads_hbm.at[:, rows], stage_sem.at[slot]),
            pltpu.make_async_copy(out_stage.at[slot], out_grads_hbm.at[rows], out_sem.at[slot]),
        )

    def weight_tile(time):
        tile = jnp.clip(time, 0, tiles - 1)
        slot = lax.rem(tile, 2)
        columns = pl.ds(pl.multiple_of(tile * TILE, TILE), TILE)

        @pl.when(jnp.logical_and(time < tiles, time >= 2))
        def _():
            for copy in stage_copies(tile - 2):
                copy.wait()

        @pl.when(time < tiles)
        def _():
            rows = normed_ref[:, columns]
            stage[slot, 0] = mm_tn(rows, grad_gate_ref[...]).astype(BF16)
            stage[slot, 1] = mm_tn(rows, grad_up_ref[...]).astype(BF16)
            stage[slot, 2] = mm_tn(cotangent_ref[:, columns], hidden_ref[...]).astype(BF16)
            out_stage[slot] = mm_tn(mix_grad_ref[:, columns], gated_ref[...]).astype(BF16)
            for copy in stage_copies(tile):
                copy.start()

    line.run(0, line.steps, weight_tile)
    for tile in range(max(tiles - 2, 0), tiles):
        for copy in stage_copies(tile):
            copy.wait()
    line.finish()


def output_line(
    mesh_axes,
    collective,
    part,
    residual,
    normed,
    cotangent,
    hidden_low,
    grad_gate,
    grad_up,
    gated,
    mix_grad,
):
    tokens, model_width = part.shape
    width = gated.shape[1]
    hidden_width = hidden_low.shape[1]
    whole = pl.BlockSpec(memory_space=pltpu.VMEM)
    return pl.pallas_call(
        partial(output_kernel, mesh_axes),
        in_specs=[whole] * 9,
        out_specs=[whole] + [pl.BlockSpec(memory_space=pl.ANY)] * 2,
        out_shape=[
            jax.ShapeDtypeStruct((tokens, model_width), BF16),
            jax.ShapeDtypeStruct((3, model_width, hidden_width), BF16),
            jax.ShapeDtypeStruct((model_width, width), BF16),
        ],
        scratch_shapes=[
            pltpu.VMEM((tokens, model_width), BF16),
            pltpu.VMEM((2, 3, TILE, hidden_width), BF16),
            pltpu.VMEM((2, TILE, width), BF16),
            pltpu.SemaphoreType.DMA((2,)),
            pltpu.SemaphoreType.DMA((2,)),
        ]
        + line_sems(tokens),
        compiler_params=pltpu.CompilerParams(
            collective_id=collective, has_side_effects=True, vmem_limit_bytes=56 << 20
        ),
        cost_estimate=pl.CostEstimate(
            flops=tokens * model_width * hidden_width * 6,
            bytes_accessed=360_000_000,
            transcendentals=0,
        ),
        name="output_line",
    )(
        part, residual, normed, cotangent, hidden_low, grad_gate, grad_up, gated, mix_grad
    )


def input_kernel(
    mesh_axes,
    part,
    hidden_ref,
    residual_grad,
    gain_ref,
    grads_hbm,
    out_ref,
    gain_grad,
    share_gate,
    share_up,
    share_down,
    arrived,
    own,
    other,
    remote,
    load_sem,
    pair_send,
    pair_recv,
    chip_send,
    chip_recv,
    *sems,
):
    plane = Plane(mesh_axes)
    chips = plane.chips
    block = own.shape[2]
    gain_grad[...] = jnp.zeros_like(gain_grad)

    def turn(total, rows, own_rows):
        values = hidden_ref[rows].astype(F32)
        inverse = inverse_rms(values)
        unit = values * inverse
        gain_grad[...] += jnp.sum(total * unit, axis=0, keepdims=True)
        lifted = total * gain_ref[...]
        mean = jnp.mean(lifted * unit, axis=-1, keepdims=True)
        grad = residual_grad[own_rows] + inverse * (lifted - unit * mean)
        out_ref[rows] = grad.astype(BF16)

    line = Line(mesh_axes, part, arrived, out_ref, sems, turn)
    barrier = pltpu.get_barrier_semaphore()
    expected = line.greet(barrier) + plane.greet(barrier)
    pl.semaphore_wait(barrier, expected)

    def rows_of(slot, core):
        return pl.ds(pl.multiple_of((2 * plane.ahead(slot) + core) * block, block), block)

    def load(slot):
        return pltpu.make_async_copy(
            grads_hbm.at[:, rows_of(slot, plane.core)], own.at[slot], load_sem.at[slot]
        )

    def pair_copy(slot):
        return pltpu.make_async_remote_copy(
            grads_hbm.at[:, rows_of(slot, 1 - plane.core)],
            other.at[slot],
            pair_send.at[slot],
            pair_recv.at[slot],
            device_id=plane.device(plane.chip, 1 - plane.core),
            device_id_type=MESH_ID,
        )

    def chip_copy(slot):
        return pltpu.make_async_remote_copy(
            own.at[slot],
            remote.at[slot - 1],
            chip_send.at[slot - 1],
            chip_recv.at[slot - 1],
            device_id=plane.device(plane.ahead(slot), plane.core),
            device_id_type=MESH_ID,
        )

    def start(index, _):
        slot = lax.rem(index + 1, chips)
        pair_copy(slot).start()
        load(slot).start()
        return 0

    lax.fori_loop(0, chips, start, 0)
    strip = 32

    def combine(time):
        slot = lax.rem(jnp.clip(time, 0, chips - 1) + 1, chips)

        @pl.when(time < chips)
        def _():
            load(slot).wait()
            pair_copy(slot).wait_recv()

            def add(index, _):
                rows = pl.ds(pl.multiple_of(index * strip, strip), strip)
                for which in range(3):
                    total = own[slot, which, rows].astype(F32) + other[slot, which, rows].astype(F32)
                    own[slot, which, rows] = total.astype(BF16)
                return 0

            lax.fori_loop(0, block // strip, add, 0)

        @pl.when(time < chips - 1)
        def _():
            chip_copy(slot).start()

    line.run(0, line.steps, combine)

    def arrive(index, _):
        chip_copy(index).wait_recv()
        return 0

    lax.fori_loop(1, chips, arrive, 0)

    def total(index, _):
        rows = pl.ds(pl.multiple_of(index * strip, strip), strip)

        def whole(which):
            def add(slot, value):
                return value + remote[slot, which, rows].astype(F32)

            return lax.fori_loop(0, chips - 1, add, own[0, which, rows].astype(F32))

        share_gate[rows] = whole(0)
        share_up[rows] = whole(1)
        share_down[rows] = whole(2)
        return 0

    lax.fori_loop(0, block // strip, total, 0)

    def sent(index, _):
        pair_copy(index).wait_send()
        return 0

    lax.fori_loop(0, chips, sent, 0)

    def chip_sent(index, _):
        chip_copy(index).wait_send()
        return 0

    lax.fori_loop(1, chips, chip_sent, 0)
    line.finish()


def input_line(mesh_axes, collective, part, hidden, residual_grad, gain, grads):
    tokens, model_width = part.shape
    hidden_width = grads.shape[2]
    chips = lax.axis_size("shard") * lax.axis_size("context") // 2
    block = model_width // (2 * chips)
    whole = pl.BlockSpec(memory_space=pltpu.VMEM)
    return pl.pallas_call(
        partial(input_kernel, mesh_axes),
        in_specs=[whole] * 4 + [pl.BlockSpec(memory_space=pl.ANY)],
        out_specs=[whole] * 5,
        out_shape=[
            jax.ShapeDtypeStruct((tokens, model_width), BF16),
            jax.ShapeDtypeStruct((1, model_width), F32),
        ]
        + [jax.ShapeDtypeStruct((block, hidden_width), F32)] * 3,
        scratch_shapes=[
            pltpu.VMEM((tokens, model_width), BF16),
            pltpu.VMEM((chips, 3, block, hidden_width), BF16),
            pltpu.VMEM((chips, 3, block, hidden_width), BF16),
            pltpu.VMEM((chips - 1, 3, block, hidden_width), BF16),
            pltpu.SemaphoreType.DMA((chips,)),
            pltpu.SemaphoreType.DMA((chips,)),
            pltpu.SemaphoreType.DMA((chips,)),
            pltpu.SemaphoreType.DMA((chips - 1,)),
            pltpu.SemaphoreType.DMA((chips - 1,)),
        ]
        + line_sems(tokens),
        compiler_params=pltpu.CompilerParams(
            collective_id=collective, has_side_effects=True, vmem_limit_bytes=58 << 20
        ),
        cost_estimate=pl.CostEstimate(
            flops=tokens * model_width * 8, bytes_accessed=360_000_000, transcendentals=0
        ),
        name="input_line",
    )(part, hidden, residual_grad, gain, grads)


def forward_kernel(
    mesh_axes,
    head_count,
    key_scale,
    hidden_ref,
    gain_ref,
    query_hbm,
    forget_hbm,
    input_hbm,
    gate_hbm,
    out_shard_ref,
    down_shard_ref,
    floor_ref,
    segments_ref,
    head_gain_ref,
    normed_hbm,
    pre_hbm,
    full_hbm,
    out_full_hbm,
    mixed_hbm,
    lead_hbm,
    start_hbm,
    gated_hbm,
    mix_hbm,
    down_turned,
    open_ref,
    count_ref,
    keep_ref,
    flags_ref,
    run_ref,
    carry_ref,
    decay_ref,
    link_ref,
    normed,
    pre,
    mine,
    out_turned,
    full,
    out_full,
    mixed,
    lead,
    starts,
    gated,
    mix,
    state_scr,
    run_scr,
    message,
    received,
    mine_sem,
    full_sem,
    save_sem,
    pre_sem,
    mix_sem,
    state_send,
    state_recv,
    *sems,
):
    plane = Plane(mesh_axes)
    chips = plane.chips
    tokens, model_width = hidden_ref.shape
    block, width = query_hbm.shape
    lanes = width // head_count
    state_rows = head_count * lanes
    context, context_size = lax.axis_index("context"), lax.axis_size("context")

    mine_loads = [
        pltpu.make_async_copy(
            ref, mine.at[:, pl.ds(which * width, width)], mine_sem.at[which]
        )
        for which, ref in enumerate((query_hbm, forget_hbm, input_hbm, gate_hbm))
    ]
    for load in mine_loads:
        load.start()
    gather = Gather(plane, (mine,), (full,), sems[:5])
    out_gather = Gather(plane, (out_turned,), (out_full,), sems[5:])

    def later(shift):
        places = {axis: lax.axis_index(axis) for axis in mesh_axes}
        places["context"] = lax.rem(context + shift, context_size)
        return tuple(places[axis] for axis in mesh_axes)

    out_turned[...] = out_shard_ref[...].T
    barrier = pltpu.get_barrier_semaphore()
    expected = gather.greet(barrier)
    for shift in range(1, context_size):
        pl.semaphore_signal(barrier, inc=1, device_id=later(shift), device_id_type=MESH_ID)
    pl.semaphore_wait(barrier, expected + context_size - 1)
    for load in mine_loads:
        load.wait()
    gather.start()
    out_gather.start()
    down_turned[...] = down_shard_ref[...].T
    for head in range(head_count):
        open_ref[:, head * lanes : (head + 1) * lanes] = 1.0 - floor_ref[head : head + 1]

    segments = segments_ref[...]
    blocks = segments.shape[0]
    block_ids = lax.broadcasted_iota(jnp.int32, segments.shape, 0)
    slot_ids = lax.broadcasted_iota(jnp.int32, segments.shape, 1)
    before = pltpu.roll(segments, 1, 1)
    wrapped = pltpu.roll(before, 1, 0)
    before = jnp.where(slot_ids == 0, wrapped, before)
    first_slot = jnp.logical_and(slot_ids == 0, block_ids == 0)
    begins = jnp.where(jnp.logical_or(first_slot, segments == before), 0.0, 1.0)
    wide_rows = lax.broadcasted_iota(jnp.int32, (BLOCK, BLOCK), 0)
    wide_columns = lax.broadcasted_iota(jnp.int32, (BLOCK, BLOCK), 1)
    within = mm_nn(begins.astype(BF16), (wide_rows <= wide_columns).astype(BF16))
    count_rows = []
    running = jnp.zeros((1, 1), F32)
    flags_ref[...] = jnp.zeros_like(flags_ref)
    for index in range(blocks):
        row = within[index : index + 1] + running
        flags_ref[index, 0:1] = row
        flags_ref[index, 1:2] = jnp.broadcast_to(running, (1, BLOCK))
        running = row[:, BLOCK - 1 : BLOCK]
        flags_ref[index, 2:3] = jnp.broadcast_to(running, (1, BLOCK))
        count_rows.append(row)
    turned_counts = jnp.concatenate(count_rows, axis=0).T
    turned_keep = (segments > 0).astype(F32).T
    for index in range(blocks):
        rows = slice(index * BLOCK, (index + 1) * BLOCK)
        count_ref[rows] = turned_counts[:, index : index + 1]
        keep_ref[rows] = turned_keep[:, index : index + 1]
    first_id = jnp.broadcast_to(segments[0:1, 0:1], (1, lanes))
    last_id = jnp.broadcast_to(segments[blocks - 1 : blocks, BLOCK - 1 : BLOCK], (1, lanes))

    def norm(index, _):
        rows = pl.ds(pl.multiple_of(index * 128, 128), 128)
        values = hidden_ref[rows].astype(F32)
        normed[rows] = (values * inverse_rms(values) * gain_ref[...]).astype(BF16)
        return 0

    lax.fori_loop(0, tokens // 128, norm, 0)

    saves = [
        pltpu.make_async_copy(source, target, save_sem.at[which])
        for which, (source, target) in enumerate(
            (
                (normed, normed_hbm),
                (out_full, out_full_hbm),
                (mixed, mixed_hbm),
                (lead, lead_hbm),
                (starts, start_hbm),
                (gated, gated_hbm),
            )
        )
    ]
    saves[0].start()
    row_tile, column_tile = 256, 512

    def pre_save(index):
        rows = pl.ds(pl.multiple_of(index * row_tile, row_tile), row_tile)
        return pltpu.make_async_copy(pre.at[rows], pre_hbm.at[rows], pre_sem.at[index])

    def depth_of(distance):
        first = 2 * gather.partner(distance) * block
        return pl.ds(pl.multiple_of(first, 2 * block), 2 * block)

    def product(distance):
        depth = depth_of(distance)

        def row_body(index, _):
            rows = pl.ds(pl.multiple_of(index * row_tile, row_tile), row_tile)
            left = normed[rows, depth]

            def column_body(column, _):
                columns = pl.ds(pl.multiple_of(column * column_tile, column_tile), column_tile)
                value = mm_nn(left, full[depth, columns])
                if distance > 0:
                    value = value + pre[rows, columns]
                pre[rows, columns] = value
                return 0

            lax.fori_loop(0, full.shape[1] // column_tile, column_body, 0)
            if distance == chips - 1:
                pre_save(index).start()
            return 0

        lax.fori_loop(0, tokens // row_tile, row_body, 0)

    def full_save(distance):
        depth = depth_of(distance)
        return pltpu.make_async_copy(full.at[depth], full_hbm.at[depth], full_sem.at[distance])

    def use(distance):
        gather.arrive_from(distance)
        full_save(distance).start()
        product(distance)

    use(0)
    gather.stage(0)
    gather.stage(1)
    if gather.relayed:
        use(1)
        use(2)
    gather.stage(2)
    if gather.relayed:
        use(3)
    else:
        for distance in range(1, chips):
            use(distance)
    out_gather.stage(0)
    out_gather.stage(1)

    state_scr[...] = jnp.zeros_like(state_scr)
    run_scr[...] = jnp.zeros_like(run_scr)

    def recur(step, _):
        rows = pl.ds(pl.multiple_of(step * BLOCK, BLOCK), BLOCK)
        counts, keep = count_ref[rows], keep_ref[rows]
        row_ids, col_ids, linked, fresh, tail, closing = block_masks(counts, flags_ref[step])
        tri = (row_ids >= col_ids).astype(BF16)
        query_pre = pre[rows, :width]
        values = pre[rows, 2 * width : 3 * width].astype(BF16)
        keys = open_ref[...] * jax.nn.sigmoid(-pre[rows, width : 2 * width])
        cum = split_sum(tri, jnp.log1p(-keys))
        ending = cum[BLOCK - 1 : BLOCK, :]
        lifted = query_pre * jax.nn.sigmoid(query_pre) * jnp.exp(cum)
        lowered = (keys * jnp.exp(-cum) * keep).astype(BF16)
        moved = (keys * jnp.exp(ending - cum) * (keep * tail)).astype(BF16)
        run = run_scr[...]
        lead[rows] = (lifted * jnp.exp(run) * (counts == 0).astype(F32)).astype(BF16)
        run_ref[step] = run
        run_scr[...] = run + ending
        fresh_lifted = (lifted * fresh).astype(BF16)
        lifted = lifted.astype(BF16)
        end_decay = jnp.exp(ending) * closing
        for head in range(head_count):
            part = slice(head * lanes, (head + 1) * lanes)
            state = state_scr[head]
            starts[step, head] = state
            scores = jnp.where(linked, mm_nt(lifted[:, part], lowered[:, part]), 0.0)
            results = mm_nn(scores.astype(BF16), values[:, part])
            results = results + mm_nt(fresh_lifted[:, part], state.astype(BF16))
            mixed[rows, part] = results * (key_scale * keep)
            state_scr[head] = state * end_decay[:, part] + mm_tn(values[:, part], moved[:, part])
        return 0

    lax.fori_loop(0, tokens // BLOCK, recur, 0)
    saves[3].start()
    saves[4].start()

    last_count = flags_ref[tokens // BLOCK - 1][2:3, 0:1]
    for head in range(head_count):
        part = slice(head * lanes, (head + 1) * lanes)
        message[head * lanes : (head + 1) * lanes] = state_scr[head]
        decay = jnp.exp(run_scr[:, part]) * (last_count == 0).astype(F32)
        decay_ref[head] = decay
        message[state_rows + 8 + head : state_rows + 9 + head] = decay
    message[state_rows : state_rows + 1] = first_id
    message[state_rows + 1 : state_rows + 2] = last_id

    def state_copy(shift):
        return pltpu.make_async_remote_copy(
            message,
            received.at[shift - 1],
            state_send.at[shift - 1],
            state_recv.at[shift - 1],
            device_id=later(shift),
            device_id_type=MESH_ID,
        )

    for shift in range(1, context_size):

        @pl.when(context + shift < context_size)
        def _(shift=shift):
            state_copy(shift).start()

    out_gather.stage(2)
    carry_ref[...] = jnp.zeros_like(carry_ref)
    link_ref[...] = jnp.zeros_like(link_ref)
    for shift in range(1, context_size):

        @pl.when(context >= shift)
        def _(shift=shift):
            state_copy(shift).wait_recv()
            linked = jnp.ones((1, lanes), F32)
            follower = first_id
            factors = [jnp.ones((1, lanes), F32)] * head_count
            for near in range(shift):
                got = received.at[near]
                linked = (got[state_rows + 1 : state_rows + 2] == follower).astype(F32)
                follower = got[state_rows : state_rows + 1]
                factors = [factor * linked for factor in factors]
                if near < shift - 1:
                    factors = [
                        factor * got[state_rows + 8 + head : state_rows + 9 + head]
                        for head, factor in enumerate(factors)
                    ]
            if shift == 1:
                link_ref[0:1] = linked
            for head in range(head_count):
                rows = slice(head * lanes, (head + 1) * lanes)
                carry_ref[head] += factors[head] * received[shift - 1, rows]

    for shift in range(1, context_size):

        @pl.when(context + shift < context_size)
        def _(shift=shift):
            state_copy(shift).wait_send()

    for distance in range(chips):
        out_gather.arrive_from(distance)
    saves[1].start()

    def mix_save(index):
        rows = pl.ds(pl.multiple_of(index * row_tile, row_tile), row_tile)
        return pltpu.make_async_copy(mix.at[rows], mix_hbm.at[rows], mix_sem.at[index])

    def project(index, _):
        rows = pl.ds(pl.multiple_of(index * row_tile, row_tile), row_tile)
        for head in range(head_count):
            part = slice(head * lanes, (head + 1) * lanes)
            carried = mm_nt(lead[rows, part], carry_ref[head].astype(BF16))
            value = mixed[rows, part] + carried * (key_scale * keep_ref[rows])
            mixed[rows, part] = value
            gate = pre[rows, 3 * width + head * lanes : 3 * width + (head + 1) * lanes]
            unit = value * inverse_rms(value)
            gated[rows, part] = (
                unit * head_gain_ref[...] * (gate * jax.nn.sigmoid(gate))
            ).astype(BF16)
        left = gated[rows]

        def column_body(column, _):
            columns = pl.ds(pl.multiple_of(column * column_tile, column_tile), column_tile)
            mix[rows, columns] = mm_nt(left, out_full[columns, :]).astype(BF16)
            return 0

        lax.fori_loop(0, model_width // column_tile, column_body, 0)
        mix_save(index).start()
        return 0

    lax.fori_loop(0, tokens // row_tile, project, 0)
    saves[2].start()
    saves[5].start()
    gather.finish()
    out_gather.finish()
    for distance in range(chips):
        full_save(distance).wait()
    for save in saves:
        save.wait()
    for index in range(tokens // row_tile):
        pre_save(index).wait()
        mix_save(index).wait()


def forward(
    mesh_axes, collective, hidden, gain, shards, out_shard, down_shard, floor, segments, head_gain
):
    tokens, model_width = hidden.shape
    block, width = shards[0].shape
    lanes = head_gain.shape[1]
    head_count = width // lanes
    all_width = width * len(shards)
    blocks = tokens // BLOCK
    context_size = lax.axis_size("context")
    chips = lax.axis_size("shard") * context_size // 2
    messages = head_count * lanes + 8 + -(-head_count // 8) * 8
    whole = pl.BlockSpec(memory_space=pltpu.VMEM)
    remote = pl.BlockSpec(memory_space=pl.ANY)
    stored = [
        ((tokens, model_width), BF16),
        ((tokens, all_width), F32),
        ((model_width, all_width), BF16),
        ((model_width, width), BF16),
        ((tokens, width), F32),
        ((tokens, width), BF16),
        ((blocks, head_count, lanes, lanes), F32),
        ((tokens, width), BF16),
        ((tokens, model_width), BF16),
    ]
    kept = [
        (down_shard.shape[::-1], BF16),
        ((1, width), F32),
        ((tokens, 1), F32),
        ((tokens, 1), F32),
        ((blocks, 8, BLOCK), F32),
        ((blocks, 1, width), F32),
        ((head_count, lanes, lanes), F32),
        ((head_count, 1, lanes), F32),
        ((8, lanes), F32),
    ]
    return pl.pallas_call(
        partial(forward_kernel, mesh_axes, head_count, lanes ** (-0.5)),
        in_specs=[whole] * 2 + [remote] * 4 + [whole] * 5,
        out_specs=[remote] * len(stored) + [whole] * len(kept),
        out_shape=[jax.ShapeDtypeStruct(shape, kind) for shape, kind in stored + kept],
        scratch_shapes=[
            pltpu.VMEM((tokens, model_width), BF16),
            pltpu.VMEM((tokens, all_width), F32),
            pltpu.VMEM((block, all_width), BF16),
            pltpu.VMEM((block, width), BF16),
            pltpu.VMEM((model_width, all_width), BF16),
            pltpu.VMEM((model_width, width), BF16),
            pltpu.VMEM((tokens, width), F32),
            pltpu.VMEM((tokens, width), BF16),
            pltpu.VMEM((blocks, head_count, lanes, lanes), F32),
            pltpu.VMEM((tokens, width), BF16),
            pltpu.VMEM((tokens, model_width), BF16),
            pltpu.VMEM((head_count, lanes, lanes), F32),
            pltpu.VMEM((1, width), F32),
            pltpu.VMEM((messages, lanes), F32),
            pltpu.VMEM((context_size - 1, messages, lanes), F32),
            pltpu.SemaphoreType.DMA((4,)),
            pltpu.SemaphoreType.DMA((chips,)),
            pltpu.SemaphoreType.DMA((6,)),
            pltpu.SemaphoreType.DMA((tokens // 256,)),
            pltpu.SemaphoreType.DMA((tokens // 256,)),
            pltpu.SemaphoreType.DMA((context_size - 1,)),
            pltpu.SemaphoreType.DMA((context_size - 1,)),
        ]
        + gather_sems(1)
        + gather_sems(1),
        compiler_params=pltpu.CompilerParams(
            collective_id=collective, has_side_effects=True, vmem_limit_bytes=56 << 20
        ),
        cost_estimate=pl.CostEstimate(
            flops=2 * tokens * model_width * all_width,
            bytes_accessed=200_000_000,
            transcendentals=tokens * width * 9,
        ),
        name="forward",
    )(hidden, gain, *shards, out_shard, down_shard, floor, segments, head_gain)


def small_sum_kernel(
    mesh_axes, value, local_ref, total_ref, near, far, near_send, near_recv, far_send, far_recv
):
    shard_size, context_size = lax.axis_size("shard"), lax.axis_size("context")
    line_size = lax.axis_size("tensor")
    group = shard_size * context_size
    place = lax.axis_index("shard") * context_size + lax.axis_index("context")
    line_place = lax.axis_index("tensor")

    def device(position, line_position):
        places = {
            "shard": position // context_size,
            "context": lax.rem(position, context_size),
            "tensor": line_position,
        }
        return tuple(places[axis] for axis in mesh_axes)

    def near_target(step):
        return device(lax.rem(place + step, group), line_place)

    def far_target(step):
        return device(place, lax.rem(line_place + step, line_size))

    def near_copy(step):
        return pltpu.make_async_remote_copy(
            value,
            near.at[step - 1],
            near_send.at[step - 1],
            near_recv.at[step - 1],
            device_id=near_target(step),
            device_id_type=MESH_ID,
        )

    def far_copy(step):
        return pltpu.make_async_remote_copy(
            local_ref,
            far.at[step - 1],
            far_send.at[step - 1],
            far_recv.at[step - 1],
            device_id=far_target(step),
            device_id_type=MESH_ID,
        )

    barrier = pltpu.get_barrier_semaphore()
    for step in range(1, group):
        pl.semaphore_signal(barrier, inc=1, device_id=near_target(step), device_id_type=MESH_ID)
    for step in range(1, line_size):
        pl.semaphore_signal(barrier, inc=1, device_id=far_target(step), device_id_type=MESH_ID)
    pl.semaphore_wait(barrier, group + line_size - 2)
    for step in range(1, group):
        near_copy(step).start()
    total = value[...]
    for step in range(1, group):
        near_copy(step).wait_recv()
        total = total + near[step - 1]
    local_ref[...] = total
    for step in range(1, line_size):
        far_copy(step).start()
    for step in range(1, line_size):
        far_copy(step).wait_recv()
        total = total + far[step - 1]
    total_ref[...] = total
    for step in range(1, group):
        near_copy(step).wait_send()
    for step in range(1, line_size):
        far_copy(step).wait_send()


def small_sum(mesh_axes, collective, values):
    flat = jnp.concatenate([value.reshape(-1) for value in values])
    lanes = -(-flat.shape[0] // 1024) * 128
    flat = jnp.pad(flat, (0, 8 * lanes - flat.shape[0])).reshape(8, lanes)
    group = lax.axis_size("shard") * lax.axis_size("context")
    line_size = lax.axis_size("tensor")
    whole = pl.BlockSpec(memory_space=pltpu.VMEM)
    local, total = pl.pallas_call(
        partial(small_sum_kernel, mesh_axes),
        in_specs=[whole],
        out_specs=[whole] * 2,
        out_shape=[jax.ShapeDtypeStruct((8, lanes), F32)] * 2,
        scratch_shapes=[
            pltpu.VMEM((group - 1, 8, lanes), F32),
            pltpu.VMEM((line_size - 1, 8, lanes), F32),
            pltpu.SemaphoreType.DMA((group - 1,)),
            pltpu.SemaphoreType.DMA((group - 1,)),
            pltpu.SemaphoreType.DMA((line_size - 1,)),
            pltpu.SemaphoreType.DMA((line_size - 1,)),
        ],
        compiler_params=pltpu.CompilerParams(collective_id=collective, has_side_effects=True),
        cost_estimate=pl.CostEstimate(
            flops=8 * lanes * group, bytes_accessed=20_000_000, transcendentals=0
        ),
        name="small_sum",
    )(flat)
    return local.reshape(-1), total.reshape(-1)


def local(
    mesh_axes,
    hidden,
    segment_ids,
    norm1_gain,
    w_query,
    w_forget,
    w_input,
    w_gate_out,
    forget_floor,
    head_gain,
    w_out,
    norm2_gain,
    w_ffn_gate,
    w_ffn_up,
    w_ffn_down,
    out_grad,
):
    sequences, span_len, model_width = hidden.shape
    tokens = sequences * span_len
    head_count, key_dim = forget_floor.shape
    width = head_count * key_dim
    key_scale = key_dim ** (-0.5)
    both = ("shard", "context")
    gain_one, gain_two = norm1_gain.reshape(1, -1), norm2_gain.reshape(1, -1)
    hidden_rows = hidden.reshape(tokens, model_width)
    gain_row = head_gain.reshape(1, -1)
    segments = segment_ids.reshape(tokens // BLOCK, BLOCK).astype(F32)
    (
        normed_one,
        pre,
        mixer_full,
        out_full,
        mixed,
        lead,
        starts,
        gated_low,
        mix_part,
        down_turned,
        open_part,
        counts,
        keep,
        flags,
        runs,
        carry,
        decay,
        link,
    ) = forward(
        mesh_axes,
        4,
        hidden_rows,
        gain_one,
        (w_query, w_forget, w_input, w_gate_out),
        w_out,
        w_ffn_down,
        forget_floor,
        segments,
        gain_row,
    )
    grad_rows = out_grad.reshape(tokens, model_width)
    (
        normed_two,
        grad_mix_low,
        grad_norm_two,
        residual,
        hidden_low,
        grad_gate_low,
        grad_up_low,
        feed_part,
        grad_residual,
    ) = middle(
        mesh_axes,
        2,
        mix_part,
        grad_rows,
        hidden_rows,
        gain_two,
        w_ffn_gate,
        w_ffn_up,
        down_turned,
    )
    grad_gated = jnp.dot(grad_mix_low, out_full, preferred_element_type=F32)
    grad_mixed, grad_gate_pre, grad_head_part, back = gate_backward(
        grad_gated, mixed, lead, pre, gain_row, keep, head_count, key_scale
    )
    after = grad_after(back, decay, link[0, 0], "context")
    grad_pre, grad_floor_part = mixer_backward(
        pre,
        grad_mixed,
        grad_gate_pre,
        starts,
        runs,
        carry,
        after,
        open_part,
        counts,
        keep,
        flags,
    )
    grad_mixer = jnp.einsum(
        "td,tk->dk", normed_one, grad_pre, preferred_element_type=F32
    ).astype(BF16)
    feed_part, grad_mixer = lax.optimization_barrier((feed_part, grad_mixer))
    output_rows, grads_ffn, grad_out = output_line(
        mesh_axes,
        1,
        feed_part,
        residual,
        normed_two,
        grad_rows,
        hidden_low,
        grad_gate_low,
        grad_up_low,
        gated_low,
        grad_mix_low,
    )
    back_one = jnp.einsum("tk,dk->td", grad_pre, mixer_full, preferred_element_type=F32)
    input_rows, grad_norm_one, share_gate, share_up, share_down = input_line(
        mesh_axes, 3, back_one.astype(BF16), hidden_rows, grad_residual, gain_one, grads_ffn
    )
    near, total = small_sum(
        mesh_axes, 5, (grad_norm_one, grad_norm_two, grad_head_part, grad_floor_part)
    )
    shares = lax.axis_size("shard") * lax.axis_size("context")
    position = lax.axis_index("shard") * lax.axis_size("context") + lax.axis_index("context")

    def own_slice(values, first, length):
        values = values[first : first + length].reshape(shares, length // shares)
        return lax.dynamic_index_in_dim(values, position, 0, False)

    floor_total = near[2 * model_width + key_dim : 2 * model_width + key_dim + width]
    floor_total = floor_total.reshape(head_count, shares, key_dim // shares)

    def share(values, dim):
        return lax.psum_scatter(
            values.astype(BF16), both, scatter_dimension=dim, tiled=True
        ).astype(F32)

    share_mixer = share(grad_mixer, 0)
    return (
        output_rows.reshape(hidden.shape),
        input_rows.reshape(hidden.shape),
        own_slice(total, 0, model_width),
        share_mixer[:, :width],
        share_mixer[:, width : 2 * width],
        share_mixer[:, 2 * width : 3 * width],
        share_mixer[:, 3 * width :],
        lax.dynamic_index_in_dim(floor_total, position, 1, False),
        own_slice(total, 2 * model_width, key_dim),
        share(grad_out, 0).T,
        own_slice(total, model_width, model_width),
        share_gate,
        share_up,
        share_down.T,
    )


def solution(mesh):
    in_specs = (
        P("shard", "context", None),
        P("shard", "context"),
        P(),
        P(("shard", "context"), "tensor"),
        P(("shard", "context"), "tensor"),
        P(("shard", "context"), "tensor"),
        P(("shard", "context"), "tensor"),
        P("tensor", None),
        P(),
        P("tensor", ("shard", "context")),
        P(),
        P(("shard", "context"), "tensor"),
        P(("shard", "context"), "tensor"),
        P("tensor", ("shard", "context")),
        P("shard", "context", None),
    )
    out_specs = (
        P("shard", "context", None),
        P("shard", "context", None),
        P(("shard", "context")),
        P(("shard", "context"), "tensor"),
        P(("shard", "context"), "tensor"),
        P(("shard", "context"), "tensor"),
        P(("shard", "context"), "tensor"),
        P("tensor", ("shard", "context")),
        P(("shard", "context")),
        P("tensor", ("shard", "context")),
        P(("shard", "context")),
        P(("shard", "context"), "tensor"),
        P(("shard", "context"), "tensor"),
        P("tensor", ("shard", "context")),
    )
    return jax.shard_map(
        partial(local, mesh.axis_names), mesh=mesh, in_specs=in_specs, out_specs=out_specs, check_vma=False)
```

```python
from functools import partial

import jax
import jax.numpy as jnp
from jax import lax
from jax.experimental import pallas as pl
from jax.experimental.pallas import tpu as pltpu
from jax.sharding import PartitionSpec as P

EPSILON = 1e-05


BLOCK = 128
F32 = jnp.float32
BF16 = jnp.bfloat16


def mm(a, b, dims):
    return lax.dot_general(a, b, (dims, ((), ())), preferred_element_type=F32)


def mm_nn(a, b):
    return mm(a, b, ((1,), (0,)))


def mm_nt(a, b):
    return mm(a, b, ((1,), (1,)))


def mm_tn(a, b):
    return mm(a, b, ((0,), (0,)))


def split_sum(tri, values):
    high = values.astype(BF16)
    low = (values - high.astype(F32)).astype(BF16)
    return mm_nn(tri, high) + mm_nn(tri, low)


def block_masks(counts, flags_row):
    rows = counts.shape[0]
    row_ids = lax.broadcasted_iota(jnp.int32, (rows, rows), 0)
    col_ids = lax.broadcasted_iota(jnp.int32, (rows, rows), 1)
    linked = jnp.logical_and(counts == flags_row[0:1], row_ids >= col_ids)
    fresh = (counts == flags_row[1:2, 0:1]).astype(F32)
    tail = (counts == flags_row[2:3, 0:1]).astype(F32)
    closing = (flags_row[1:2, 0:1] == flags_row[2:3, 0:1]).astype(F32)
    return row_ids, col_ids, linked, fresh, tail, closing


CHUNK = 32
LAG = 2
MESH_ID = pl.DeviceIdType.MESH


class Line:
    def __init__(self, mesh_axes, part, arrived, out, sems, transform):
        self.mesh_axes = mesh_axes
        self.part, self.arrived, self.out = part, arrived, out
        self.sum_send, self.sum_recv, self.back_send, self.back_recv = sems
        self.transform = transform
        self.half = part.shape[0] // 2
        self.chunks = self.half // CHUNK
        self.size = lax.axis_size("tensor")
        self.place = lax.axis_index("tensor")
        self.lines = ((self.size - 1 - self.place, -1), (self.place, 1))
        self.steps = self.chunks + 2 * LAG * (self.size - 1)

    def device(self, position):
        return tuple(
            jnp.clip(position, 0, self.size - 1) if axis == "tensor" else lax.axis_index(axis)
            for axis in self.mesh_axes
        )

    def greet(self, barrier):
        for step in (-1, 1):
            inside = jnp.logical_and(self.place + step >= 0, self.place + step < self.size)

            @pl.when(inside)
            def _(step=step):
                pl.semaphore_signal(
                    barrier, inc=1, device_id=self.device(self.place + step), device_id_type=MESH_ID
                )

        at_end = jnp.logical_or(self.place == 0, self.place == self.size - 1)
        return jnp.where(at_end, 1, 2)

    def rows_of(self, side, index):
        return pl.ds(pl.multiple_of(side * self.half + index * CHUNK, CHUNK), CHUNK)

    def sum_copy(self, side, index, source):
        rows = self.rows_of(side, index)
        return pltpu.make_async_remote_copy(
            source.at[rows],
            self.arrived.at[rows],
            self.sum_send.at[side, index],
            self.sum_recv.at[side, index],
            device_id=self.device(self.place + self.lines[side][1]),
            device_id_type=MESH_ID,
        )

    def back_copy(self, side, index):
        rows = self.rows_of(side, index)
        return pltpu.make_async_remote_copy(
            self.out.at[rows],
            self.out.at[rows],
            self.back_send.at[side, index],
            self.back_recv.at[side, index],
            device_id=self.device(self.place - self.lines[side][1]),
            device_id_type=MESH_ID,
        )

    def step(self, time):
        for side in (0, 1):
            hops = self.lines[side][0]
            index = time - LAG * hops
            valid = jnp.logical_and(index >= 0, index < self.chunks)
            at_source, at_owner = hops == 0, hops == self.size - 1
            index = jnp.clip(index, 0, self.chunks - 1)
            rows = self.rows_of(side, index)

            @pl.when(jnp.logical_and(valid, at_source))
            def _(side=side, index=index):
                self.sum_copy(side, index, self.part).start()

            @pl.when(jnp.logical_and(valid, jnp.logical_not(at_source)))
            def _(side=side, index=index):
                self.sum_copy(side, index, self.arrived).wait_recv()

            between = jnp.logical_and(jnp.logical_not(at_source), jnp.logical_not(at_owner))

            @pl.when(jnp.logical_and(valid, between))
            def _(side=side, index=index, rows=rows):
                total = self.part[rows].astype(F32) + self.arrived[rows].astype(F32)
                self.arrived[rows] = total.astype(BF16)
                self.sum_copy(side, index, self.arrived).start()

            @pl.when(jnp.logical_and(valid, at_owner))
            def _(side=side, index=index, rows=rows):
                total = self.part[rows].astype(F32) + self.arrived[rows].astype(F32)
                own = pl.ds(pl.multiple_of(index * CHUNK, CHUNK), CHUNK)
                self.transform(total, rows, own)
                self.back_copy(side, index).start()

            away = self.size - 1 - hops
            index = time - LAG * (self.size - 1 + away)
            valid = jnp.logical_and(jnp.logical_and(index >= 0, index < self.chunks), away > 0)
            index = jnp.clip(index, 0, self.chunks - 1)

            @pl.when(valid)
            def _(side=side, index=index):
                self.back_copy(side, index).wait_recv()

            @pl.when(jnp.logical_and(valid, away < self.size - 1))
            def _(side=side, index=index):
                self.back_copy(side, index).start()

    def run(self, first, last, beside=None):
        def body(time, _):
            self.step(time)
            if beside is not None:
                beside(time)
            return 0

        lax.fori_loop(first, last, body, 0)

    def source_sent(self, first, last):
        def body(index, _):
            for side in (0, 1):

                @pl.when(self.lines[side][0] == 0)
                def _(side=side):
                    self.sum_copy(side, index, self.part).wait_send()

            return 0

        lax.fori_loop(first, last, body, 0)

    def finish(self, source_waits=True):
        def body(index, _):
            for side in (0, 1):
                hops = self.lines[side][0]
                passed = hops < self.size - 1
                if not source_waits:
                    passed = jnp.logical_and(passed, hops > 0)

                @pl.when(passed)
                def _(side=side):
                    self.sum_copy(side, index, self.arrived).wait_send()

                @pl.when(hops > 0)
                def _(side=side):
                    self.back_copy(side, index).wait_send()

            return 0

        lax.fori_loop(0, self.chunks, body, 0)


def line_sems(tokens):
    return [pltpu.SemaphoreType.DMA((2, tokens // 2 // CHUNK))] * 4


def inverse_rms(values):
    return lax.rsqrt(jnp.mean(values * values, axis=-1, keepdims=True) + EPSILON)


class Plane:
    def __init__(self, mesh_axes):
        self.mesh_axes = mesh_axes
        self.context = lax.axis_size("context")
        self.per_row = self.context // 2
        self.chips = lax.axis_size("shard") * self.per_row
        context_place = lax.axis_index("context")
        self.core = lax.rem(context_place, 2)
        self.chip = lax.axis_index("shard") * self.per_row + context_place // 2

    def device(self, chip, core):
        places = {
            "shard": chip // self.per_row,
            "context": 2 * lax.rem(chip, self.per_row) + core,
            "tensor": lax.axis_index("tensor"),
        }
        return tuple(places[axis] for axis in self.mesh_axes)

    def ahead(self, distance):
        return lax.rem(self.chip + distance, self.chips)

    def greet(self, barrier):
        targets = [self.device(self.chip, 1 - self.core)]
        targets += [self.device(self.ahead(step), self.core) for step in range(1, self.chips)]
        for target in targets:
            pl.semaphore_signal(barrier, inc=1, device_id=target, device_id_type=MESH_ID)
        return len(targets)


class Gather:
    def __init__(self, plane, sources, targets, sems):
        self.plane, self.sources, self.targets = plane, sources, targets
        self.load_sem, self.send_sem, self.recv_sem, self.pair_send, self.pair_recv = sems
        self.block = sources[0].shape[0]
        self.part = self.block // 2
        self.relayed = plane.chips == 4
        self.arrays = range(len(sources))

    def partner(self, distance):
        return jnp.bitwise_xor(self.plane.chip, distance)

    def greet(self, barrier):
        plane = self.plane
        targets = [plane.device(plane.chip, 1 - plane.core)]
        targets += [
            plane.device(self.partner(step), plane.core)
            for step in range(1, 3 if self.relayed else plane.chips)
        ]
        for target in targets:
            pl.semaphore_signal(barrier, inc=1, device_id=target, device_id_type=MESH_ID)
        return len(targets)

    def place(self, array, chip, core, half):
        first = (2 * chip + core) * self.block + half * self.part
        rows = pl.ds(pl.multiple_of(first, self.part), self.part)
        return self.targets[array].at[rows, pl.ds(0, self.sources[array].shape[1])]

    def mine(self, array, half):
        return self.sources[array].at[pl.ds(half * self.part, self.part)]

    def loads(self):
        plane = self.plane
        return [
            pltpu.make_async_copy(
                self.mine(array, half),
                self.place(array, plane.chip, plane.core, half),
                self.load_sem.at[array, half],
            )
            for array in self.arrays
            for half in range(2)
        ]

    def send(self, distance, half):
        plane = self.plane
        copies = []
        for array in self.arrays:
            chip, target = plane.chip, self.partner(distance)
            source = self.mine(array, half)
            if self.relayed and distance == 3:
                chip = self.partner(2 if half == 0 else 1)
                target = self.partner(1 if half == 0 else 2)
                source = self.place(array, chip, plane.core, half)
            copies.append(
                pltpu.make_async_remote_copy(
                    source,
                    self.place(array, chip, plane.core, half),
                    self.send_sem.at[array, distance - 1, half],
                    self.recv_sem.at[array, distance - 1, half],
                    device_id=plane.device(target, plane.core),
                    device_id_type=MESH_ID,
                )
            )
        return copies

    def forward(self, distance, half):
        plane = self.plane
        copies = []
        for array in self.arrays:
            place = self.place(array, self.partner(distance), plane.core, half)
            copies.append(
                pltpu.make_async_remote_copy(
                    self.mine(array, half) if distance == 0 else place,
                    place,
                    self.pair_send.at[array, distance, half],
                    self.pair_recv.at[array, distance, half],
                    device_id=plane.device(plane.chip, 1 - plane.core),
                    device_id_type=MESH_ID,
                )
            )
        return copies

    def start(self):
        if self.relayed:
            order = ((1, 1), (2, 0), (1, 0), (2, 1))
        else:
            order = [(step, half) for step in range(1, self.plane.chips) for half in range(2)]
        for distance, half in order:
            for copy in self.send(distance, half):
                copy.start()
        for copy in self.loads():
            copy.start()
        for half in range(2):
            for copy in self.forward(0, half):
                copy.start()

    def take(self, distance, half, relay):
        for copy in self.send(distance, half):
            copy.wait_recv()
        if relay:
            for copy in self.send(3, half):
                copy.start()
        for copy in self.forward(distance, half):
            copy.start()

    def stage(self, number):
        if self.relayed:
            if number == 0:
                self.take(1, 1, True)
                self.take(2, 0, True)
            elif number == 1:
                self.take(1, 0, False)
                self.take(2, 1, False)
            else:
                self.take(3, 0, False)
                self.take(3, 1, False)
        elif number == 2:
            for distance in range(1, self.plane.chips):
                for half in range(2):
                    self.take(distance, half, False)

    def arrive_from(self, distance):
        if distance == 0:
            for copy in self.loads():
                copy.wait()
        for half in range(2):
            for copy in self.forward(distance, half):
                copy.wait_recv()

    def arrive(self):
        for distance in range(self.plane.chips):
            self.arrive_from(distance)

    def finish(self):
        for distance in range(self.plane.chips):
            for half in range(2):
                for copy in self.forward(distance, half):
                    copy.wait_send()
                if distance > 0:
                    for copy in self.send(distance, half):
                        copy.wait_send()


def gather_sems(arrays):
    chips = lax.axis_size("shard") * lax.axis_size("context") // 2
    return [
        pltpu.SemaphoreType.DMA((arrays, 2)),
        pltpu.SemaphoreType.DMA((arrays, chips - 1, 2)),
        pltpu.SemaphoreType.DMA((arrays, chips - 1, 2)),
        pltpu.SemaphoreType.DMA((arrays, chips, 2)),
        pltpu.SemaphoreType.DMA((arrays, chips, 2)),
    ]


GROUP = 128
TILE = 256
WIDE = 512


def middle_kernel(
    mesh_axes,
    mix_hbm,
    cotangent_ref,
    input_hbm,
    gain_ref,
    gate_hbm,
    up_hbm,
    down_hbm,
    normed_ref,
    out_ref,
    gain_grad,
    residual_hbm,
    hidden_hbm,
    grad_gate_hbm,
    grad_up_hbm,
    feed_hbm,
    grad_hbm,
    gate_w,
    up_w,
    down_w,
    part,
    mix_arrived,
    arrived,
    inputs,
    residual,
    stage_hidden,
    stage_gate,
    stage_up,
    stage_feed,
    part_sem,
    input_sem,
    save_sem,
    stage_sem,
    grad_sem,
    *sems,
):
    tokens, model_width = normed_ref.shape
    half = tokens // 2
    hidden_width = gate_hbm.shape[1]
    padded = gate_w.shape[1]
    groups = half // GROUP
    place, line_size = lax.axis_index("tensor"), lax.axis_size("tensor")
    own_half = pl.ds(pl.multiple_of(jnp.where(place == 0, 0, half), half), half)
    part_load = pltpu.make_async_copy(mix_hbm, part, part_sem.at[0])
    part_load.start()
    input_load = pltpu.make_async_copy(input_hbm.at[own_half], inputs, input_sem.at[0])
    input_load.start()
    if padded > hidden_width:
        spare = slice(hidden_width, padded)
        gate_w[:, spare] = jnp.zeros((model_width, padded - hidden_width), BF16)
        up_w[:, spare] = jnp.zeros((model_width, padded - hidden_width), BF16)
        down_w[:, spare] = jnp.zeros((model_width, padded - hidden_width), BF16)
    gain_grad[...] = jnp.zeros_like(gain_grad)

    def mix_turn(total, rows, own):
        values = inputs[own].astype(F32) + total
        residual[own] = values
        normed_ref[rows] = (values * inverse_rms(values) * gain_ref[...]).astype(BF16)

    def turn(total, rows, own):
        values = residual[own]
        inverse = inverse_rms(values)
        unit = values * inverse
        gain_grad[...] += jnp.sum(total * unit, axis=0, keepdims=True)
        lifted = total * gain_ref[...]
        mean = jnp.mean(lifted * unit, axis=-1, keepdims=True)
        grad = cotangent_ref[rows].astype(F32) + inverse * (lifted - unit * mean)
        residual[own] = grad
        out_ref[rows] = grad.astype(BF16)

    mix_line = Line(mesh_axes, part, mix_arrived, normed_ref, sems[:4], mix_turn)
    line = Line(mesh_axes, part, arrived, out_ref, sems[4:8], turn)
    gather = Gather(
        Plane(mesh_axes), (gate_hbm, up_hbm, down_hbm), (gate_w, up_w, down_w), sems[8:]
    )
    barrier = pltpu.get_barrier_semaphore()
    expected = mix_line.greet(barrier) + gather.greet(barrier)
    pl.semaphore_wait(barrier, expected)
    gather.start()
    part_load.wait()
    input_load.wait()
    pace = GROUP // CHUNK
    begin = pace + 2 * LAG * (line_size - 1) + 4
    mix_line.run(0, begin - 10)
    gather.stage(0)
    mix_line.run(begin - 10, begin - 4)
    gather.stage(1)
    mix_line.run(begin - 4, begin)
    gather.stage(2)
    gather.arrive()

    def both(ref, group):
        first = pl.ds(pl.multiple_of(group * GROUP, GROUP), GROUP)
        second = pl.ds(pl.multiple_of(half + group * GROUP, GROUP), GROUP)
        return first, second

    def stage_copies(group):
        slot = lax.rem(group, 2)
        copies = []
        for side, rows in enumerate(both(None, group)):
            from_rows = pl.ds(side * GROUP, GROUP)
            columns = pl.ds(0, hidden_width)
            for which, (stage, target) in enumerate(
                (
                    (stage_hidden, hidden_hbm),
                    (stage_gate, grad_gate_hbm),
                    (stage_up, grad_up_hbm),
                )
            ):
                copies.append(
                    pltpu.make_async_copy(
                        stage.at[slot, from_rows, columns],
                        target.at[rows],
                        stage_sem.at[slot, which, side],
                    )
                )
            copies.append(
                pltpu.make_async_copy(
                    stage_feed.at[slot, from_rows], feed_hbm.at[rows], stage_sem.at[slot, 3, side]
                )
            )
        return copies

    def hidden_tile(group, tile):
        first, second = both(normed_ref, group)
        slot = lax.rem(group, 2)
        columns = pl.ds(pl.multiple_of(tile * WIDE, WIDE), WIDE)
        rows = jnp.concatenate([normed_ref[first], normed_ref[second]], axis=0)
        gate = mm_nn(rows, gate_w[:, columns])
        up = mm_nn(rows, up_w[:, columns])
        grads = jnp.concatenate([cotangent_ref[first], cotangent_ref[second]], axis=0)
        grad = mm_nn(grads, down_w[:, columns])
        sigma = jax.nn.sigmoid(gate)
        active = gate * sigma
        stage_hidden[slot, :, columns] = (active * up).astype(BF16)
        stage_gate[slot, :, columns] = (grad * up * sigma * (1.0 + gate * (1.0 - sigma))).astype(
            BF16
        )
        stage_up[slot, :, columns] = (grad * active).astype(BF16)

    def model_tile(group, tile):
        first, second = both(part, group)
        slot = lax.rem(group, 2)
        columns = pl.ds(pl.multiple_of(tile * WIDE, WIDE), WIDE)
        back = mm_nt(stage_gate[slot], gate_w[columns, :])
        back = (back + mm_nt(stage_up[slot], up_w[columns, :])).astype(BF16)
        part[first, columns] = back[:GROUP]
        part[second, columns] = back[GROUP:]
        stage_feed[slot, :, columns] = mm_nt(stage_hidden[slot], down_w[columns, :]).astype(BF16)

    hidden_tiles, model_tiles = padded // WIDE, model_width // WIDE
    ticks = hidden_tiles + model_tiles
    piece = -(-ticks // pace)
    save = pltpu.make_async_copy(residual, residual_hbm, save_sem.at[0])

    def group_body(group, _):
        mix_line.source_sent(group * pace, (group + 1) * pace)

        @pl.when(group == 1)
        def _():
            save.start()

        @pl.when(group == 2)
        def _():
            save.wait()

        @pl.when(group >= 2)
        def _():
            for copy in stage_copies(group - 2):
                copy.wait()

        def piece_body(index, _):
            def tick_body(offset, _):
                tick = index * piece + offset

                @pl.when(tick < hidden_tiles)
                def _():
                    hidden_tile(group, tick)

                @pl.when(jnp.logical_and(tick >= hidden_tiles, tick < ticks))
                def _():
                    model_tile(group, tick - hidden_tiles)

                return 0

            lax.fori_loop(0, piece, tick_body, 0)

            mix_time = begin + group * pace + index

            @pl.when(mix_time < mix_line.steps)
            def _():
                mix_line.step(mix_time)

            @pl.when(group >= 1)
            def _():
                line.step((group - 1) * pace + index)

            return 0

        lax.fori_loop(0, pace, piece_body, 0)
        for copy in stage_copies(group):
            copy.start()
        return 0

    lax.fori_loop(0, groups, group_body, 0)
    line.run((groups - 1) * pace, line.steps)
    grad_save = pltpu.make_async_copy(residual, grad_hbm, grad_sem.at[0])
    grad_save.start()
    for group in range(max(groups - 2, 0), groups):
        for copy in stage_copies(group):
            copy.wait()
    gather.finish()
    mix_line.finish(source_waits=False)
    line.finish()
    grad_save.wait()


def middle(mesh_axes, collective, mix, cotangent, inputs, gain, gate_w, up_w, down_w):
    tokens, model_width = mix.shape
    hidden_width = gate_w.shape[1]
    padded = -(-hidden_width // WIDE) * WIDE
    whole = pl.BlockSpec(memory_space=pltpu.VMEM)
    remote = pl.BlockSpec(memory_space=pl.ANY)
    group_rows = 2 * GROUP
    return pl.pallas_call(
        partial(middle_kernel, mesh_axes),
        in_specs=[remote, whole, remote, whole, remote, remote, remote],
        out_specs=[whole, whole, whole] + [remote] * 6,
        out_shape=[
            jax.ShapeDtypeStruct((tokens, model_width), BF16),
            jax.ShapeDtypeStruct((tokens, model_width), BF16),
            jax.ShapeDtypeStruct((1, model_width), F32),
            jax.ShapeDtypeStruct((tokens // 2, model_width), F32),
            jax.ShapeDtypeStruct((tokens, hidden_width), BF16),
            jax.ShapeDtypeStruct((tokens, hidden_width), BF16),
            jax.ShapeDtypeStruct((tokens, hidden_width), BF16),
            jax.ShapeDtypeStruct((tokens, model_width), BF16),
            jax.ShapeDtypeStruct((tokens // 2, model_width), F32),
        ],
        scratch_shapes=[
            pltpu.VMEM((model_width, padded), BF16),
            pltpu.VMEM((model_width, padded), BF16),
            pltpu.VMEM((model_width, padded), BF16),
            pltpu.VMEM((tokens, model_width), BF16),
            pltpu.VMEM((tokens, model_width), BF16),
            pltpu.VMEM((tokens, model_width), BF16),
            pltpu.VMEM((tokens // 2, model_width), BF16),
            pltpu.VMEM((tokens // 2, model_width), F32),
            pltpu.VMEM((2, group_rows, padded), BF16),
            pltpu.VMEM((2, group_rows, padded), BF16),
            pltpu.VMEM((2, group_rows, padded), BF16),
            pltpu.VMEM((2, group_rows, model_width), BF16),
            pltpu.SemaphoreType.DMA((1,)),
            pltpu.SemaphoreType.DMA((1,)),
            pltpu.SemaphoreType.DMA((1,)),
            pltpu.SemaphoreType.DMA((2, 4, 2)),
            pltpu.SemaphoreType.DMA((1,)),
        ]
        + line_sems(tokens)
        + line_sems(tokens)
        + gather_sems(3),
        compiler_params=pltpu.CompilerParams(
            collective_id=collective, has_side_effects=True, vmem_limit_bytes=61 << 20
        ),
        cost_estimate=pl.CostEstimate(
            flops=tokens * model_width * hidden_width * 12,
            bytes_accessed=360_000_000,
            transcendentals=tokens * hidden_width,
        ),
        name="middle",
    )(mix, cotangent, inputs, gain, gate_w, up_w, down_w)


def output_kernel(
    mesh_axes,
    head_count,
    key_scale,
    part,
    residual,
    hidden_ref,
    grad_gate_ref,
    grad_up_ref,
    gated_ref,
    mix_grad_ref,
    out_full,
    mixed_ref,
    lead_ref,
    starts_ref,
    run_ref,
    carry_ref,
    decay_ref,
    link_ref,
    open_ref,
    count_ref,
    keep_ref,
    flags_ref,
    gain_ref,
    normed_two_hbm,
    cotangent_hbm,
    normed_one_hbm,
    pre_hbm,
    out_ref,
    gain_grad,
    floor_grad,
    grads_hbm,
    out_grads_hbm,
    mixer_grads_hbm,
    grad_pre_hbm,
    arrived,
    left,
    right,
    stage,
    out_stage,
    mixer_stage,
    gates,
    pre,
    grad_mixed,
    back_scr,
    message,
    received,
    grad_scr,
    lifted_scr,
    lowered_scr,
    moved_scr,
    value_scr,
    load_sem,
    pre_sem,
    stage_sem,
    save_sem,
    grad_send,
    grad_recv,
    *sems,
):
    tokens, model_width = left.shape
    width = gated_ref.shape[1]
    lanes = width // head_count
    state_rows = head_count * lanes
    tiles, blocks = model_width // TILE, tokens // BLOCK
    piece_rows = 2 * BLOCK
    context, context_size = lax.axis_index("context"), lax.axis_size("context")

    left_load = pltpu.make_async_copy(normed_two_hbm, left, load_sem.at[0])
    right_load = pltpu.make_async_copy(cotangent_hbm, right, load_sem.at[1])
    gate_load = pltpu.make_async_copy(
        pre_hbm.at[:, pl.ds(3 * width, width)], gates, load_sem.at[2]
    )
    next_load = pltpu.make_async_copy(normed_one_hbm, left, load_sem.at[3])
    for load in (left_load, right_load, gate_load):
        load.start()
    gain_grad[...] = jnp.zeros_like(gain_grad)
    floor_grad[...] = jnp.zeros_like(floor_grad)
    back_scr[...] = jnp.zeros_like(back_scr)

    def turn(total, rows, own):
        out_ref[rows] = (residual[own] + total).astype(BF16)

    def earlier(shift):
        places = {axis: lax.axis_index(axis) for axis in mesh_axes}
        places["context"] = lax.rem(context + context_size - shift, context_size)
        return tuple(places[axis] for axis in mesh_axes)

    line = Line(mesh_axes, part, arrived, out_ref, sems, turn)
    barrier = pltpu.get_barrier_semaphore()
    expected = line.greet(barrier)
    for shift in range(1, context_size):
        pl.semaphore_signal(barrier, inc=1, device_id=earlier(shift), device_id_type=MESH_ID)
    pl.semaphore_wait(barrier, expected + context_size - 1)
    for load in (left_load, right_load, gate_load):
        load.wait()

    def tile_columns(tile):
        return pl.ds(pl.multiple_of(tile * TILE, TILE), TILE)

    def stage_copies(tile):
        rows = tile_columns(tile)
        return (
            pltpu.make_async_copy(stage, grads_hbm.at[:, rows], stage_sem.at[0]),
            pltpu.make_async_copy(out_stage, out_grads_hbm.at[rows], stage_sem.at[1]),
        )

    def mixer_copy(tile):
        rows = tile_columns(tile)
        return pltpu.make_async_copy(mixer_stage, mixer_grads_hbm.at[rows], stage_sem.at[2])

    grad_save = pltpu.make_async_copy(right, grad_pre_hbm, save_sem.at[0])

    def feed_tile(tile):
        columns = tile_columns(tile)

        @pl.when(tile > 0)
        def _():
            for copy in stage_copies(tile - 1):
                copy.wait()

        rows = left[:, columns]
        stage[0] = mm_tn(rows, grad_gate_ref[...]).astype(BF16)
        stage[1] = mm_tn(rows, grad_up_ref[...]).astype(BF16)
        stage[2] = mm_tn(right[:, columns], hidden_ref[...]).astype(BF16)
        out_stage[...] = mm_tn(mix_grad_ref[:, columns], gated_ref[...]).astype(BF16)
        for copy in stage_copies(tile):
            copy.start()

    def gate_piece(index):
        rows = pl.ds(pl.multiple_of(index * piece_rows, piece_rows), piece_rows)
        grads = mm_nn(mix_grad_ref[rows], out_full[...])
        gain = gain_ref[...]
        total = jnp.zeros_like(gain)
        for head in range(head_count):
            part_of = slice(head * lanes, (head + 1) * lanes)
            mixed, gate, grad = mixed_ref[rows, part_of], gates[rows, part_of], grads[:, part_of]
            inverse = inverse_rms(mixed)
            unit = mixed * inverse
            sigma = jax.nn.sigmoid(gate)
            scaled = grad * unit
            total = total + jnp.sum(scaled * (gate * sigma), axis=0, keepdims=True)
            grad_gate = scaled * gain * sigma * (1.0 + gate * (1.0 - sigma))
            first = 3 * width + head * lanes
            right[rows, first : first + lanes] = grad_gate.astype(BF16)
            lifted = grad * gain * (gate * sigma)
            mean = jnp.mean(lifted * unit, axis=-1, keepdims=True)
            grad_in = inverse * (lifted - unit * mean) * (key_scale * keep_ref[rows])
            grad_in = grad_in.astype(BF16)
            grad_mixed[rows, part_of] = grad_in
            back_scr[head] += mm_tn(grad_in, lead_ref[rows, part_of])
        gain_grad[...] += total

    def state_copy(shift):
        return pltpu.make_async_remote_copy(
            message,
            received.at[shift - 1],
            grad_send.at[shift - 1],
            grad_recv.at[shift - 1],
            device_id=earlier(shift),
            device_id_type=MESH_ID,
        )

    def block_of(index):
        return blocks - 1 - index

    def pre_load(index):
        rows = pl.ds(pl.multiple_of(block_of(index) * BLOCK, BLOCK), BLOCK)
        slot = lax.rem(index, 2)
        return pltpu.make_async_copy(
            pre_hbm.at[rows, pl.ds(0, 3 * width)], pre.at[slot], pre_sem.at[slot]
        )

    def send_back():
        for head in range(head_count):
            rows = slice(head * lanes, (head + 1) * lanes)
            message[rows] = back_scr[head] * link_ref[0:1]
            message[state_rows + head : state_rows + head + 1] = decay_ref[head] * link_ref[0:1]
        for shift in range(1, context_size):

            @pl.when(context >= shift)
            def _(shift=shift):
                state_copy(shift).start()

        pre_load(0).start()

    def take_back():
        grad_scr[...] = jnp.zeros_like(grad_scr)
        for shift in range(1, context_size):

            @pl.when(context + shift < context_size)
            def _(shift=shift):
                state_copy(shift).wait_recv()
                for head in range(head_count):
                    value = received[shift - 1, head * lanes : (head + 1) * lanes]
                    for near in range(shift - 1):
                        value = value * received[near, state_rows + head : state_rows + head + 1]
                    grad_scr[head] += value

        for shift in range(1, context_size):

            @pl.when(context >= shift)
            def _(shift=shift):
                state_copy(shift).wait_send()

    def mixer_block(index):
        block = block_of(index)
        slot = lax.rem(index, 2)
        block_rows = pl.ds(pl.multiple_of(block * BLOCK, BLOCK), BLOCK)

        @pl.when(index + 1 < blocks)
        def _():
            pre_load(index + 1).start()

        pre_load(index).wait()
        counts, keep, flags = count_ref[block_rows], keep_ref[block_rows], flags_ref[block]
        row_ids, col_ids, linked, fresh, tail, closing = block_masks(counts, flags)
        tri = (row_ids >= col_ids).astype(BF16)
        tri_back = (row_ids <= col_ids).astype(BF16)
        query_pre = pre[slot, :, :width]
        values = pre[slot, :, 2 * width : 3 * width].astype(BF16)
        opened = open_ref[...]
        closed = jax.nn.sigmoid(-pre[slot, :, width : 2 * width])
        keys = opened * closed
        cum = split_sum(tri, jnp.log1p(-keys))
        ending = cum[BLOCK - 1 : BLOCK, :]
        rise, fall = jnp.exp(cum), jnp.exp(-cum) * keep
        shift = jnp.exp(ending - cum) * (keep * tail)
        sigma_query = jax.nn.sigmoid(query_pre)
        lifted = (query_pre * sigma_query * rise).astype(BF16)
        lowered = (keys * fall).astype(BF16)
        moved = (keys * shift).astype(BF16)
        fresh_lifted = (lifted.astype(F32) * fresh).astype(BF16)
        end_decay = jnp.exp(ending) * closing
        lead_in = jnp.exp(run_ref[block]) * (flags[1:2, 0:1] == 0).astype(F32)
        for head in range(head_count):
            part_of = slice(head * lanes, (head + 1) * lanes)
            grad_out, value = grad_mixed[block_rows, part_of], values[:, part_of]
            lift, lower, move = lifted[:, part_of], lowered[:, part_of], moved[:, part_of]
            scores = jnp.where(linked, mm_nt(lift, lower), 0.0).astype(BF16)
            pulls = jnp.where(linked, mm_nt(grad_out, value), 0.0).astype(BF16)
            state = starts_ref[block, head] + lead_in[:, part_of] * carry_ref[head]
            grad_state = grad_scr[head]
            grad_low = grad_state.astype(BF16)
            lifted_scr[:, part_of] = mm_nn(pulls, lower) + fresh * mm_nn(
                grad_out, state.astype(BF16)
            )
            lowered_scr[:, part_of] = mm_tn(pulls, lift)
            grad_moved = mm_nn(value, grad_low)
            moved_scr[:, part_of] = grad_moved
            first = 2 * width + head * lanes
            right[block_rows, first : first + lanes] = (
                mm_tn(scores, grad_out) + mm_nt(move, grad_low)
            ).astype(BF16)
            value_scr[:, part_of] = jnp.sum(
                grad_moved * move.astype(F32), axis=0, keepdims=True
            ) + end_decay[:, part_of] * jnp.sum(state * grad_state, axis=0, keepdims=True)
            grad_scr[head] = grad_state * end_decay[:, part_of] + mm_tn(
                grad_out, fresh_lifted[:, part_of]
            )
        grad_lifted, grad_lowered, grad_moved = lifted_scr[...], lowered_scr[...], moved_scr[...]
        grad_cum = (
            grad_lifted * lifted.astype(F32)
            - grad_lowered * lowered.astype(F32)
            - grad_moved * moved.astype(F32)
        )
        grad_decay = split_sum(tri_back, grad_cum) + value_scr[...]
        key_total = grad_lowered * fall + grad_moved * shift - grad_decay / (1.0 - keys)
        floor_grad[...] -= jnp.sum(key_total * closed, axis=0, keepdims=True)
        right[block_rows, :width] = (
            grad_lifted * rise * sigma_query * (1.0 + query_pre * (1.0 - sigma_query))
        ).astype(BF16)
        right[block_rows, width : 2 * width] = (
            -key_total * opened * closed * (1.0 - closed)
        ).astype(BF16)

    def mixer_tile(tile):
        @pl.when(tile > 0)
        def _():
            mixer_copy(tile - 1).wait()

        rows = left[:, tile_columns(tile)]
        for first in range(0, 4 * width, 1024):
            columns = slice(first, min(first + 1024, 4 * width))
            mixer_stage[:, columns] = mm_tn(rows, right[:, columns]).astype(BF16)
        mixer_copy(tile).start()

    gate_time = tiles
    send_time = gate_time + tokens // piece_rows
    block_time = send_time + 1
    tile_time = block_time + blocks
    end_time = tile_time + tiles

    def beside(time):
        @pl.when(time < tiles)
        def _():
            feed_tile(time)

        @pl.when(time == gate_time)
        def _():
            next_load.start()

        @pl.when(jnp.logical_and(time >= gate_time, time < send_time))
        def _():
            gate_piece(time - gate_time)

        @pl.when(time == send_time)
        def _():
            send_back()

        @pl.when(time == block_time)
        def _():
            take_back()

        @pl.when(jnp.logical_and(time >= block_time, time < tile_time))
        def _():
            mixer_block(time - block_time)

        @pl.when(time == tile_time)
        def _():
            grad_save.start()
            next_load.wait()

        @pl.when(jnp.logical_and(time >= tile_time, time < end_time))
        def _():
            mixer_tile(time - tile_time)

    steps = max(line.steps, end_time)

    def body(time, _):
        @pl.when(time < line.steps)
        def _():
            line.step(time)

        beside(time)
        return 0

    lax.fori_loop(0, steps, body, 0)
    for copy in stage_copies(tiles - 1):
        copy.wait()
    mixer_copy(tiles - 1).wait()
    grad_save.wait()
    line.finish()


def output_line(mesh_axes, collective, in_vmem, in_hbm, head_count):
    part, _, hidden_low, _, _, gated = in_vmem[:6]
    tokens, model_width = part.shape
    hidden_width, width = hidden_low.shape[1], gated.shape[1]
    lanes = width // head_count
    context_size = lax.axis_size("context")
    messages = head_count * lanes + -(-head_count // 8) * 8
    whole = pl.BlockSpec(memory_space=pltpu.VMEM)
    remote = pl.BlockSpec(memory_space=pl.ANY)
    return pl.pallas_call(
        partial(output_kernel, mesh_axes, head_count, lanes ** (-0.5)),
        in_specs=[whole] * len(in_vmem) + [remote] * len(in_hbm),
        out_specs=[whole] * 3 + [remote] * 4,
        out_shape=[
            jax.ShapeDtypeStruct((tokens, model_width), BF16),
            jax.ShapeDtypeStruct((1, lanes), F32),
            jax.ShapeDtypeStruct((1, width), F32),
            jax.ShapeDtypeStruct((3, model_width, hidden_width), BF16),
            jax.ShapeDtypeStruct((model_width, width), BF16),
            jax.ShapeDtypeStruct((model_width, 4 * width), BF16),
            jax.ShapeDtypeStruct((tokens, 4 * width), BF16),
        ],
        scratch_shapes=[
            pltpu.VMEM((tokens, model_width), BF16),
            pltpu.VMEM((tokens, model_width), BF16),
            pltpu.VMEM((tokens, model_width), BF16),
            pltpu.VMEM((3, TILE, hidden_width), BF16),
            pltpu.VMEM((TILE, width), BF16),
            pltpu.VMEM((TILE, 4 * width), BF16),
            pltpu.VMEM((tokens, width), F32),
            pltpu.VMEM((2, BLOCK, 3 * width), F32),
            pltpu.VMEM((tokens, width), BF16),
            pltpu.VMEM((head_count, lanes, lanes), F32),
            pltpu.VMEM((messages, lanes), F32),
            pltpu.VMEM((context_size - 1, messages, lanes), F32),
            pltpu.VMEM((head_count, lanes, lanes), F32),
            pltpu.VMEM((BLOCK, width), F32),
            pltpu.VMEM((BLOCK, width), F32),
            pltpu.VMEM((BLOCK, width), F32),
            pltpu.VMEM((1, width), F32),
            pltpu.SemaphoreType.DMA((4,)),
            pltpu.SemaphoreType.DMA((2,)),
            pltpu.SemaphoreType.DMA((3,)),
            pltpu.SemaphoreType.DMA((1,)),
            pltpu.SemaphoreType.DMA((context_size - 1,)),
            pltpu.SemaphoreType.DMA((context_size - 1,)),
        ]
        + line_sems(tokens),
        compiler_params=pltpu.CompilerParams(
            collective_id=collective, has_side_effects=True, vmem_limit_bytes=61 << 20
        ),
        cost_estimate=pl.CostEstimate(
            flops=tokens * model_width * hidden_width * 6,
            bytes_accessed=360_000_000,
            transcendentals=0,
        ),
        name="output_line",
    )(*in_vmem, *in_hbm)


def input_kernel(
    mesh_axes,
    part,
    hidden_ref,
    residual_grad,
    gain_ref,
    grads_hbm,
    out_ref,
    gain_grad,
    share_gate,
    share_up,
    share_down,
    arrived,
    own,
    other,
    remote,
    load_sem,
    pair_send,
    pair_recv,
    chip_send,
    chip_recv,
    *sems,
):
    plane = Plane(mesh_axes)
    chips = plane.chips
    block = own.shape[2]
    gain_grad[...] = jnp.zeros_like(gain_grad)

    def turn(total, rows, own_rows):
        values = hidden_ref[rows].astype(F32)
        inverse = inverse_rms(values)
        unit = values * inverse
        gain_grad[...] += jnp.sum(total * unit, axis=0, keepdims=True)
        lifted = total * gain_ref[...]
        mean = jnp.mean(lifted * unit, axis=-1, keepdims=True)
        grad = residual_grad[own_rows] + inverse * (lifted - unit * mean)
        out_ref[rows] = grad.astype(BF16)

    line = Line(mesh_axes, part, arrived, out_ref, sems, turn)
    barrier = pltpu.get_barrier_semaphore()
    expected = line.greet(barrier) + plane.greet(barrier)
    pl.semaphore_wait(barrier, expected)

    def rows_of(slot, core):
        return pl.ds(pl.multiple_of((2 * plane.ahead(slot) + core) * block, block), block)

    def load(slot):
        return pltpu.make_async_copy(
            grads_hbm.at[:, rows_of(slot, plane.core)], own.at[slot], load_sem.at[slot]
        )

    def pair_copy(slot):
        return pltpu.make_async_remote_copy(
            grads_hbm.at[:, rows_of(slot, 1 - plane.core)],
            other.at[slot],
            pair_send.at[slot],
            pair_recv.at[slot],
            device_id=plane.device(plane.chip, 1 - plane.core),
            device_id_type=MESH_ID,
        )

    def chip_copy(slot):
        return pltpu.make_async_remote_copy(
            own.at[slot],
            remote.at[slot - 1],
            chip_send.at[slot - 1],
            chip_recv.at[slot - 1],
            device_id=plane.device(plane.ahead(slot), plane.core),
            device_id_type=MESH_ID,
        )

    def start(index, _):
        slot = lax.rem(index + 1, chips)
        pair_copy(slot).start()
        load(slot).start()
        return 0

    lax.fori_loop(0, chips, start, 0)
    strip = 32

    def combine(time):
        slot = lax.rem(jnp.clip(time, 0, chips - 1) + 1, chips)

        @pl.when(time < chips)
        def _():
            load(slot).wait()
            pair_copy(slot).wait_recv()

            def add(index, _):
                rows = pl.ds(pl.multiple_of(index * strip, strip), strip)
                for which in range(3):
                    total = own[slot, which, rows].astype(F32) + other[slot, which, rows].astype(F32)
                    own[slot, which, rows] = total.astype(BF16)
                return 0

            lax.fori_loop(0, block // strip, add, 0)

        @pl.when(time < chips - 1)
        def _():
            chip_copy(slot).start()

    line.run(0, line.steps, combine)

    def arrive(index, _):
        chip_copy(index).wait_recv()
        return 0

    lax.fori_loop(1, chips, arrive, 0)

    def total(index, _):
        rows = pl.ds(pl.multiple_of(index * strip, strip), strip)

        def whole(which):
            def add(slot, value):
                return value + remote[slot, which, rows].astype(F32)

            return lax.fori_loop(0, chips - 1, add, own[0, which, rows].astype(F32))

        share_gate[rows] = whole(0)
        share_up[rows] = whole(1)
        share_down[rows] = whole(2)
        return 0

    lax.fori_loop(0, block // strip, total, 0)

    def sent(index, _):
        pair_copy(index).wait_send()
        return 0

    lax.fori_loop(0, chips, sent, 0)

    def chip_sent(index, _):
        chip_copy(index).wait_send()
        return 0

    lax.fori_loop(1, chips, chip_sent, 0)
    line.finish()


def input_line(mesh_axes, collective, part, hidden, residual_grad, gain, grads):
    tokens, model_width = part.shape
    hidden_width = grads.shape[2]
    chips = lax.axis_size("shard") * lax.axis_size("context") // 2
    block = model_width // (2 * chips)
    whole = pl.BlockSpec(memory_space=pltpu.VMEM)
    return pl.pallas_call(
        partial(input_kernel, mesh_axes),
        in_specs=[whole] * 4 + [pl.BlockSpec(memory_space=pl.ANY)],
        out_specs=[whole] * 5,
        out_shape=[
            jax.ShapeDtypeStruct((tokens, model_width), BF16),
            jax.ShapeDtypeStruct((1, model_width), F32),
        ]
        + [jax.ShapeDtypeStruct((block, hidden_width), F32)] * 3,
        scratch_shapes=[
            pltpu.VMEM((tokens, model_width), BF16),
            pltpu.VMEM((chips, 3, block, hidden_width), BF16),
            pltpu.VMEM((chips, 3, block, hidden_width), BF16),
            pltpu.VMEM((chips - 1, 3, block, hidden_width), BF16),
            pltpu.SemaphoreType.DMA((chips,)),
            pltpu.SemaphoreType.DMA((chips,)),
            pltpu.SemaphoreType.DMA((chips,)),
            pltpu.SemaphoreType.DMA((chips - 1,)),
            pltpu.SemaphoreType.DMA((chips - 1,)),
        ]
        + line_sems(tokens),
        compiler_params=pltpu.CompilerParams(
            collective_id=collective, has_side_effects=True, vmem_limit_bytes=58 << 20
        ),
        cost_estimate=pl.CostEstimate(
            flops=tokens * model_width * 8, bytes_accessed=360_000_000, transcendentals=0
        ),
        name="input_line",
    )(part, hidden, residual_grad, gain, grads)


def forward_kernel(
    mesh_axes,
    head_count,
    key_scale,
    hidden_ref,
    gain_ref,
    query_hbm,
    forget_hbm,
    input_hbm,
    gate_hbm,
    out_shard_ref,
    down_shard_ref,
    floor_ref,
    segments_ref,
    head_gain_ref,
    normed_hbm,
    pre_hbm,
    full_hbm,
    out_full_hbm,
    mixed_hbm,
    lead_hbm,
    start_hbm,
    gated_hbm,
    mix_hbm,
    down_turned,
    open_ref,
    count_ref,
    keep_ref,
    flags_ref,
    run_ref,
    carry_ref,
    decay_ref,
    link_ref,
    normed,
    pre,
    mine,
    out_turned,
    full,
    out_full,
    mixed,
    lead,
    starts,
    gated,
    mix,
    state_scr,
    run_scr,
    message,
    received,
    mine_sem,
    full_sem,
    save_sem,
    pre_sem,
    mix_sem,
    state_send,
    state_recv,
    *sems,
):
    plane = Plane(mesh_axes)
    chips = plane.chips
    tokens, model_width = hidden_ref.shape
    block, width = query_hbm.shape
    lanes = width // head_count
    state_rows = head_count * lanes
    context, context_size = lax.axis_index("context"), lax.axis_size("context")

    mine_loads = [
        pltpu.make_async_copy(
            ref, mine.at[:, pl.ds(which * width, width)], mine_sem.at[which]
        )
        for which, ref in enumerate((query_hbm, forget_hbm, input_hbm, gate_hbm))
    ]
    for load in mine_loads:
        load.start()
    gather = Gather(plane, (mine,), (full,), sems[:5])
    out_gather = Gather(plane, (out_turned,), (out_full,), sems[5:])

    def later(shift):
        places = {axis: lax.axis_index(axis) for axis in mesh_axes}
        places["context"] = lax.rem(context + shift, context_size)
        return tuple(places[axis] for axis in mesh_axes)

    out_turned[...] = out_shard_ref[...].T
    barrier = pltpu.get_barrier_semaphore()
    expected = gather.greet(barrier)
    for shift in range(1, context_size):
        pl.semaphore_signal(barrier, inc=1, device_id=later(shift), device_id_type=MESH_ID)
    pl.semaphore_wait(barrier, expected + context_size - 1)
    for load in mine_loads:
        load.wait()
    gather.start()
    out_gather.start()
    down_turned[...] = down_shard_ref[...].T
    for head in range(head_count):
        open_ref[:, head * lanes : (head + 1) * lanes] = 1.0 - floor_ref[head : head + 1]

    segments = segments_ref[...]
    blocks = segments.shape[0]
    block_ids = lax.broadcasted_iota(jnp.int32, segments.shape, 0)
    slot_ids = lax.broadcasted_iota(jnp.int32, segments.shape, 1)
    before = pltpu.roll(segments, 1, 1)
    wrapped = pltpu.roll(before, 1, 0)
    before = jnp.where(slot_ids == 0, wrapped, before)
    first_slot = jnp.logical_and(slot_ids == 0, block_ids == 0)
    begins = jnp.where(jnp.logical_or(first_slot, segments == before), 0.0, 1.0)
    wide_rows = lax.broadcasted_iota(jnp.int32, (BLOCK, BLOCK), 0)
    wide_columns = lax.broadcasted_iota(jnp.int32, (BLOCK, BLOCK), 1)
    within = mm_nn(begins.astype(BF16), (wide_rows <= wide_columns).astype(BF16))
    count_rows = []
    running = jnp.zeros((1, 1), F32)
    flags_ref[...] = jnp.zeros_like(flags_ref)
    for index in range(blocks):
        row = within[index : index + 1] + running
        flags_ref[index, 0:1] = row
        flags_ref[index, 1:2] = jnp.broadcast_to(running, (1, BLOCK))
        running = row[:, BLOCK - 1 : BLOCK]
        flags_ref[index, 2:3] = jnp.broadcast_to(running, (1, BLOCK))
        count_rows.append(row)
    turned_counts = jnp.concatenate(count_rows, axis=0).T
    turned_keep = (segments > 0).astype(F32).T
    for index in range(blocks):
        rows = slice(index * BLOCK, (index + 1) * BLOCK)
        count_ref[rows] = turned_counts[:, index : index + 1]
        keep_ref[rows] = turned_keep[:, index : index + 1]
    first_id = jnp.broadcast_to(segments[0:1, 0:1], (1, lanes))
    last_id = jnp.broadcast_to(segments[blocks - 1 : blocks, BLOCK - 1 : BLOCK], (1, lanes))

    def norm(index, _):
        rows = pl.ds(pl.multiple_of(index * 128, 128), 128)
        values = hidden_ref[rows].astype(F32)
        normed[rows] = (values * inverse_rms(values) * gain_ref[...]).astype(BF16)
        return 0

    lax.fori_loop(0, tokens // 128, norm, 0)

    saves = [
        pltpu.make_async_copy(source, target, save_sem.at[which])
        for which, (source, target) in enumerate(
            (
                (normed, normed_hbm),
                (out_full, out_full_hbm),
                (mixed, mixed_hbm),
                (lead, lead_hbm),
                (starts, start_hbm),
                (gated, gated_hbm),
            )
        )
    ]
    saves[0].start()
    row_tile, column_tile = 256, 512

    def pre_save(index):
        rows = pl.ds(pl.multiple_of(index * row_tile, row_tile), row_tile)
        return pltpu.make_async_copy(pre.at[rows], pre_hbm.at[rows], pre_sem.at[index])

    def depth_of(distance):
        first = 2 * gather.partner(distance) * block
        return pl.ds(pl.multiple_of(first, 2 * block), 2 * block)

    def product(distance):
        depth = depth_of(distance)

        def row_body(index, _):
            rows = pl.ds(pl.multiple_of(index * row_tile, row_tile), row_tile)
            left = normed[rows, depth]

            def column_body(column, _):
                columns = pl.ds(pl.multiple_of(column * column_tile, column_tile), column_tile)
                value = mm_nn(left, full[depth, columns])
                if distance > 0:
                    value = value + pre[rows, columns]
                pre[rows, columns] = value
                return 0

            lax.fori_loop(0, full.shape[1] // column_tile, column_body, 0)
            if distance == chips - 1:
                pre_save(index).start()
            return 0

        lax.fori_loop(0, tokens // row_tile, row_body, 0)

    def full_save(distance):
        depth = depth_of(distance)
        return pltpu.make_async_copy(full.at[depth], full_hbm.at[depth], full_sem.at[distance])

    def use(distance):
        gather.arrive_from(distance)
        full_save(distance).start()
        product(distance)

    use(0)
    gather.stage(0)
    gather.stage(1)
    if gather.relayed:
        use(1)
        use(2)
    gather.stage(2)
    if gather.relayed:
        use(3)
    else:
        for distance in range(1, chips):
            use(distance)
    out_gather.stage(0)
    out_gather.stage(1)

    state_scr[...] = jnp.zeros_like(state_scr)
    run_scr[...] = jnp.zeros_like(run_scr)

    def recur(step, _):
        rows = pl.ds(pl.multiple_of(step * BLOCK, BLOCK), BLOCK)
        counts, keep = count_ref[rows], keep_ref[rows]
        row_ids, col_ids, linked, fresh, tail, closing = block_masks(counts, flags_ref[step])
        tri = (row_ids >= col_ids).astype(BF16)
        query_pre = pre[rows, :width]
        values = pre[rows, 2 * width : 3 * width].astype(BF16)
        keys = open_ref[...] * jax.nn.sigmoid(-pre[rows, width : 2 * width])
        cum = split_sum(tri, jnp.log1p(-keys))
        ending = cum[BLOCK - 1 : BLOCK, :]
        lifted = query_pre * jax.nn.sigmoid(query_pre) * jnp.exp(cum)
        lowered = (keys * jnp.exp(-cum) * keep).astype(BF16)
        moved = (keys * jnp.exp(ending - cum) * (keep * tail)).astype(BF16)
        run = run_scr[...]
        lead[rows] = (lifted * jnp.exp(run) * (counts == 0).astype(F32)).astype(BF16)
        run_ref[step] = run
        run_scr[...] = run + ending
        fresh_lifted = (lifted * fresh).astype(BF16)
        lifted = lifted.astype(BF16)
        end_decay = jnp.exp(ending) * closing
        for head in range(head_count):
            part = slice(head * lanes, (head + 1) * lanes)
            state = state_scr[head]
            starts[step, head] = state
            scores = jnp.where(linked, mm_nt(lifted[:, part], lowered[:, part]), 0.0)
            results = mm_nn(scores.astype(BF16), values[:, part])
            results = results + mm_nt(fresh_lifted[:, part], state.astype(BF16))
            mixed[rows, part] = results * (key_scale * keep)
            state_scr[head] = state * end_decay[:, part] + mm_tn(values[:, part], moved[:, part])
        return 0

    lax.fori_loop(0, tokens // BLOCK, recur, 0)
    saves[3].start()
    saves[4].start()

    last_count = flags_ref[tokens // BLOCK - 1][2:3, 0:1]
    for head in range(head_count):
        part = slice(head * lanes, (head + 1) * lanes)
        message[head * lanes : (head + 1) * lanes] = state_scr[head]
        decay = jnp.exp(run_scr[:, part]) * (last_count == 0).astype(F32)
        decay_ref[head] = decay
        message[state_rows + 8 + head : state_rows + 9 + head] = decay
    message[state_rows : state_rows + 1] = first_id
    message[state_rows + 1 : state_rows + 2] = last_id

    def state_copy(shift):
        return pltpu.make_async_remote_copy(
            message,
            received.at[shift - 1],
            state_send.at[shift - 1],
            state_recv.at[shift - 1],
            device_id=later(shift),
            device_id_type=MESH_ID,
        )

    for shift in range(1, context_size):

        @pl.when(context + shift < context_size)
        def _(shift=shift):
            state_copy(shift).start()

    out_gather.stage(2)
    carry_ref[...] = jnp.zeros_like(carry_ref)
    link_ref[...] = jnp.zeros_like(link_ref)
    for shift in range(1, context_size):

        @pl.when(context >= shift)
        def _(shift=shift):
            state_copy(shift).wait_recv()
            linked = jnp.ones((1, lanes), F32)
            follower = first_id
            factors = [jnp.ones((1, lanes), F32)] * head_count
            for near in range(shift):
                got = received.at[near]
                linked = (got[state_rows + 1 : state_rows + 2] == follower).astype(F32)
                follower = got[state_rows : state_rows + 1]
                factors = [factor * linked for factor in factors]
                if near < shift - 1:
                    factors = [
                        factor * got[state_rows + 8 + head : state_rows + 9 + head]
                        for head, factor in enumerate(factors)
                    ]
            if shift == 1:
                link_ref[0:1] = linked
            for head in range(head_count):
                rows = slice(head * lanes, (head + 1) * lanes)
                carry_ref[head] += factors[head] * received[shift - 1, rows]

    for shift in range(1, context_size):

        @pl.when(context + shift < context_size)
        def _(shift=shift):
            state_copy(shift).wait_send()

    for distance in range(chips):
        out_gather.arrive_from(distance)
    saves[1].start()

    def mix_save(index):
        rows = pl.ds(pl.multiple_of(index * row_tile, row_tile), row_tile)
        return pltpu.make_async_copy(mix.at[rows], mix_hbm.at[rows], mix_sem.at[index])

    def project(index, _):
        rows = pl.ds(pl.multiple_of(index * row_tile, row_tile), row_tile)
        for head in range(head_count):
            part = slice(head * lanes, (head + 1) * lanes)
            carried = mm_nt(lead[rows, part], carry_ref[head].astype(BF16))
            value = mixed[rows, part] + carried * (key_scale * keep_ref[rows])
            mixed[rows, part] = value
            gate = pre[rows, 3 * width + head * lanes : 3 * width + (head + 1) * lanes]
            unit = value * inverse_rms(value)
            gated[rows, part] = (
                unit * head_gain_ref[...] * (gate * jax.nn.sigmoid(gate))
            ).astype(BF16)
        left = gated[rows]

        def column_body(column, _):
            columns = pl.ds(pl.multiple_of(column * column_tile, column_tile), column_tile)
            mix[rows, columns] = mm_nt(left, out_full[columns, :]).astype(BF16)
            return 0

        lax.fori_loop(0, model_width // column_tile, column_body, 0)
        mix_save(index).start()
        return 0

    lax.fori_loop(0, tokens // row_tile, project, 0)
    saves[2].start()
    saves[5].start()
    gather.finish()
    out_gather.finish()
    for distance in range(chips):
        full_save(distance).wait()
    for save in saves:
        save.wait()
    for index in range(tokens // row_tile):
        pre_save(index).wait()
        mix_save(index).wait()


def forward(
    mesh_axes, collective, hidden, gain, shards, out_shard, down_shard, floor, segments, head_gain
):
    tokens, model_width = hidden.shape
    block, width = shards[0].shape
    lanes = head_gain.shape[1]
    head_count = width // lanes
    all_width = width * len(shards)
    blocks = tokens // BLOCK
    context_size = lax.axis_size("context")
    chips = lax.axis_size("shard") * context_size // 2
    messages = head_count * lanes + 8 + -(-head_count // 8) * 8
    whole = pl.BlockSpec(memory_space=pltpu.VMEM)
    remote = pl.BlockSpec(memory_space=pl.ANY)
    stored = [
        ((tokens, model_width), BF16),
        ((tokens, all_width), F32),
        ((model_width, all_width), BF16),
        ((model_width, width), BF16),
        ((tokens, width), F32),
        ((tokens, width), BF16),
        ((blocks, head_count, lanes, lanes), F32),
        ((tokens, width), BF16),
        ((tokens, model_width), BF16),
    ]
    kept = [
        (down_shard.shape[::-1], BF16),
        ((1, width), F32),
        ((tokens, 1), F32),
        ((tokens, 1), F32),
        ((blocks, 8, BLOCK), F32),
        ((blocks, 1, width), F32),
        ((head_count, lanes, lanes), F32),
        ((head_count, 1, lanes), F32),
        ((8, lanes), F32),
    ]
    return pl.pallas_call(
        partial(forward_kernel, mesh_axes, head_count, lanes ** (-0.5)),
        in_specs=[whole] * 2 + [remote] * 4 + [whole] * 5,
        out_specs=[remote] * len(stored) + [whole] * len(kept),
        out_shape=[jax.ShapeDtypeStruct(shape, kind) for shape, kind in stored + kept],
        scratch_shapes=[
            pltpu.VMEM((tokens, model_width), BF16),
            pltpu.VMEM((tokens, all_width), F32),
            pltpu.VMEM((block, all_width), BF16),
            pltpu.VMEM((block, width), BF16),
            pltpu.VMEM((model_width, all_width), BF16),
            pltpu.VMEM((model_width, width), BF16),
            pltpu.VMEM((tokens, width), F32),
            pltpu.VMEM((tokens, width), BF16),
            pltpu.VMEM((blocks, head_count, lanes, lanes), F32),
            pltpu.VMEM((tokens, width), BF16),
            pltpu.VMEM((tokens, model_width), BF16),
            pltpu.VMEM((head_count, lanes, lanes), F32),
            pltpu.VMEM((1, width), F32),
            pltpu.VMEM((messages, lanes), F32),
            pltpu.VMEM((context_size - 1, messages, lanes), F32),
            pltpu.SemaphoreType.DMA((4,)),
            pltpu.SemaphoreType.DMA((chips,)),
            pltpu.SemaphoreType.DMA((6,)),
            pltpu.SemaphoreType.DMA((tokens // 256,)),
            pltpu.SemaphoreType.DMA((tokens // 256,)),
            pltpu.SemaphoreType.DMA((context_size - 1,)),
            pltpu.SemaphoreType.DMA((context_size - 1,)),
        ]
        + gather_sems(1)
        + gather_sems(1),
        compiler_params=pltpu.CompilerParams(
            collective_id=collective, has_side_effects=True, vmem_limit_bytes=56 << 20
        ),
        cost_estimate=pl.CostEstimate(
            flops=2 * tokens * model_width * all_width,
            bytes_accessed=200_000_000,
            transcendentals=tokens * width * 9,
        ),
        name="forward",
    )(hidden, gain, *shards, out_shard, down_shard, floor, segments, head_gain)


def small_sum_kernel(
    mesh_axes, value, local_ref, total_ref, near, far, near_send, near_recv, far_send, far_recv
):
    shard_size, context_size = lax.axis_size("shard"), lax.axis_size("context")
    line_size = lax.axis_size("tensor")
    group = shard_size * context_size
    place = lax.axis_index("shard") * context_size + lax.axis_index("context")
    line_place = lax.axis_index("tensor")

    def device(position, line_position):
        places = {
            "shard": position // context_size,
            "context": lax.rem(position, context_size),
            "tensor": line_position,
        }
        return tuple(places[axis] for axis in mesh_axes)

    def near_target(step):
        return device(lax.rem(place + step, group), line_place)

    def far_target(step):
        return device(place, lax.rem(line_place + step, line_size))

    def near_copy(step):
        return pltpu.make_async_remote_copy(
            value,
            near.at[step - 1],
            near_send.at[step - 1],
            near_recv.at[step - 1],
            device_id=near_target(step),
            device_id_type=MESH_ID,
        )

    def far_copy(step):
        return pltpu.make_async_remote_copy(
            local_ref,
            far.at[step - 1],
            far_send.at[step - 1],
            far_recv.at[step - 1],
            device_id=far_target(step),
            device_id_type=MESH_ID,
        )

    barrier = pltpu.get_barrier_semaphore()
    for step in range(1, group):
        pl.semaphore_signal(barrier, inc=1, device_id=near_target(step), device_id_type=MESH_ID)
    for step in range(1, line_size):
        pl.semaphore_signal(barrier, inc=1, device_id=far_target(step), device_id_type=MESH_ID)
    pl.semaphore_wait(barrier, group + line_size - 2)
    for step in range(1, group):
        near_copy(step).start()
    total = value[...]
    for step in range(1, group):
        near_copy(step).wait_recv()
        total = total + near[step - 1]
    local_ref[...] = total
    for step in range(1, line_size):
        far_copy(step).start()
    for step in range(1, line_size):
        far_copy(step).wait_recv()
        total = total + far[step - 1]
    total_ref[...] = total
    for step in range(1, group):
        near_copy(step).wait_send()
    for step in range(1, line_size):
        far_copy(step).wait_send()


def small_sum(mesh_axes, collective, values):
    flat = jnp.concatenate([value.reshape(-1) for value in values])
    lanes = -(-flat.shape[0] // 1024) * 128
    flat = jnp.pad(flat, (0, 8 * lanes - flat.shape[0])).reshape(8, lanes)
    group = lax.axis_size("shard") * lax.axis_size("context")
    line_size = lax.axis_size("tensor")
    whole = pl.BlockSpec(memory_space=pltpu.VMEM)
    local, total = pl.pallas_call(
        partial(small_sum_kernel, mesh_axes),
        in_specs=[whole],
        out_specs=[whole] * 2,
        out_shape=[jax.ShapeDtypeStruct((8, lanes), F32)] * 2,
        scratch_shapes=[
            pltpu.VMEM((group - 1, 8, lanes), F32),
            pltpu.VMEM((line_size - 1, 8, lanes), F32),
            pltpu.SemaphoreType.DMA((group - 1,)),
            pltpu.SemaphoreType.DMA((group - 1,)),
            pltpu.SemaphoreType.DMA((line_size - 1,)),
            pltpu.SemaphoreType.DMA((line_size - 1,)),
        ],
        compiler_params=pltpu.CompilerParams(collective_id=collective, has_side_effects=True),
        cost_estimate=pl.CostEstimate(
            flops=8 * lanes * group, bytes_accessed=20_000_000, transcendentals=0
        ),
        name="small_sum",
    )(flat)
    return local.reshape(-1), total.reshape(-1)


def local(
    mesh_axes,
    hidden,
    segment_ids,
    norm1_gain,
    w_query,
    w_forget,
    w_input,
    w_gate_out,
    forget_floor,
    head_gain,
    w_out,
    norm2_gain,
    w_ffn_gate,
    w_ffn_up,
    w_ffn_down,
    out_grad,
):
    sequences, span_len, model_width = hidden.shape
    tokens = sequences * span_len
    head_count, key_dim = forget_floor.shape
    width = head_count * key_dim
    key_scale = key_dim ** (-0.5)
    both = ("shard", "context")
    gain_one, gain_two = norm1_gain.reshape(1, -1), norm2_gain.reshape(1, -1)
    hidden_rows = hidden.reshape(tokens, model_width)
    gain_row = head_gain.reshape(1, -1)
    segments = segment_ids.reshape(tokens // BLOCK, BLOCK).astype(F32)
    (
        normed_one,
        pre,
        mixer_full,
        out_full,
        mixed,
        lead,
        starts,
        gated_low,
        mix_part,
        down_turned,
        open_part,
        counts,
        keep,
        flags,
        runs,
        carry,
        decay,
        link,
    ) = forward(
        mesh_axes,
        4,
        hidden_rows,
        gain_one,
        (w_query, w_forget, w_input, w_gate_out),
        w_out,
        w_ffn_down,
        forget_floor,
        segments,
        gain_row,
    )
    grad_rows = out_grad.reshape(tokens, model_width)
    (
        normed_two,
        grad_mix_low,
        grad_norm_two,
        residual,
        hidden_low,
        grad_gate_low,
        grad_up_low,
        feed_part,
        grad_residual,
    ) = middle(
        mesh_axes,
        2,
        mix_part,
        grad_rows,
        hidden_rows,
        gain_two,
        w_ffn_gate,
        w_ffn_up,
        down_turned,
    )
    (
        output_rows,
        grad_head_part,
        grad_floor_part,
        grads_ffn,
        grad_out,
        grad_mixer,
        grad_pre,
    ) = output_line(
        mesh_axes,
        1,
        (
            feed_part,
            residual,
            hidden_low,
            grad_gate_low,
            grad_up_low,
            gated_low,
            grad_mix_low,
            out_full,
            mixed,
            lead,
            starts,
            runs,
            carry,
            decay,
            link,
            open_part,
            counts,
            keep,
            flags,
            gain_row,
        ),
        (normed_two, grad_rows, normed_one, pre),
        head_count,
    )
    back_one = jnp.einsum("tk,dk->td", grad_pre, mixer_full, preferred_element_type=F32)
    input_rows, grad_norm_one, share_gate, share_up, share_down = input_line(
        mesh_axes, 3, back_one.astype(BF16), hidden_rows, grad_residual, gain_one, grads_ffn
    )
    near, total = small_sum(
        mesh_axes, 5, (grad_norm_one, grad_norm_two, grad_head_part, grad_floor_part)
    )
    shares = lax.axis_size("shard") * lax.axis_size("context")
    position = lax.axis_index("shard") * lax.axis_size("context") + lax.axis_index("context")

    def own_slice(values, first, length):
        values = values[first : first + length].reshape(shares, length // shares)
        return lax.dynamic_index_in_dim(values, position, 0, False)

    floor_total = near[2 * model_width + key_dim : 2 * model_width + key_dim + width]
    floor_total = floor_total.reshape(head_count, shares, key_dim // shares)

    def share(values, dim):
        return lax.psum_scatter(
            values.astype(BF16), both, scatter_dimension=dim, tiled=True
        ).astype(F32)

    share_mixer = share(grad_mixer, 0)
    return (
        output_rows.reshape(hidden.shape),
        input_rows.reshape(hidden.shape),
        own_slice(total, 0, model_width),
        share_mixer[:, :width],
        share_mixer[:, width : 2 * width],
        share_mixer[:, 2 * width : 3 * width],
        share_mixer[:, 3 * width :],
        lax.dynamic_index_in_dim(floor_total, position, 1, False),
        own_slice(total, 2 * model_width, key_dim),
        share(grad_out, 0).T,
        own_slice(total, model_width, model_width),
        share_gate,
        share_up,
        share_down.T,
    )


def solution(mesh):
    in_specs = (
        P("shard", "context", None),
        P("shard", "context"),
        P(),
        P(("shard", "context"), "tensor"),
        P(("shard", "context"), "tensor"),
        P(("shard", "context"), "tensor"),
        P(("shard", "context"), "tensor"),
        P("tensor", None),
        P(),
        P("tensor", ("shard", "context")),
        P(),
        P(("shard", "context"), "tensor"),
        P(("shard", "context"), "tensor"),
        P("tensor", ("shard", "context")),
        P("shard", "context", None),
    )
    out_specs = (
        P("shard", "context", None),
        P("shard", "context", None),
        P(("shard", "context")),
        P(("shard", "context"), "tensor"),
        P(("shard", "context"), "tensor"),
        P(("shard", "context"), "tensor"),
        P(("shard", "context"), "tensor"),
        P("tensor", ("shard", "context")),
        P(("shard", "context")),
        P("tensor", ("shard", "context")),
        P(("shard", "context")),
        P(("shard", "context"), "tensor"),
        P(("shard", "context"), "tensor"),
        P("tensor", ("shard", "context")),
    )
    return jax.shard_map(
        partial(local, mesh.axis_names), mesh=mesh, in_specs=in_specs, out_specs=out_specs, check_vma=False)
```

```python
from functools import partial

import jax
import jax.numpy as jnp
from jax import lax
from jax.experimental import pallas as pl
from jax.experimental.pallas import tpu as pltpu
from jax.sharding import PartitionSpec as P

EPSILON = 1e-05


BLOCK = 128
F32 = jnp.float32
BF16 = jnp.bfloat16


def mm(a, b, dims):
    return lax.dot_general(a, b, (dims, ((), ())), preferred_element_type=F32)


def mm_nn(a, b):
    return mm(a, b, ((1,), (0,)))


def mm_nt(a, b):
    return mm(a, b, ((1,), (1,)))


def mm_tn(a, b):
    return mm(a, b, ((0,), (0,)))


def split_sum(tri, values):
    high = values.astype(BF16)
    low = (values - high.astype(F32)).astype(BF16)
    return mm_nn(tri, high) + mm_nn(tri, low)


def block_masks(counts, flags_row):
    rows = counts.shape[0]
    row_ids = lax.broadcasted_iota(jnp.int32, (rows, rows), 0)
    col_ids = lax.broadcasted_iota(jnp.int32, (rows, rows), 1)
    linked = jnp.logical_and(counts == flags_row[0:1], row_ids >= col_ids)
    fresh = (counts == flags_row[1:2, 0:1]).astype(F32)
    tail = (counts == flags_row[2:3, 0:1]).astype(F32)
    closing = (flags_row[1:2, 0:1] == flags_row[2:3, 0:1]).astype(F32)
    return row_ids, col_ids, linked, fresh, tail, closing


CHUNK = 32
LAG = 2
MESH_ID = pl.DeviceIdType.MESH


class Line:
    def __init__(self, mesh_axes, part, arrived, out, sems, transform):
        self.mesh_axes = mesh_axes
        self.part, self.arrived, self.out = part, arrived, out
        self.sum_send, self.sum_recv, self.back_send, self.back_recv = sems
        self.transform = transform
        self.half = part.shape[0] // 2
        self.chunks = self.half // CHUNK
        self.size = lax.axis_size("tensor")
        self.place = lax.axis_index("tensor")
        self.lines = ((self.size - 1 - self.place, -1), (self.place, 1))
        self.steps = self.chunks + 2 * LAG * (self.size - 1)

    def device(self, position):
        return tuple(
            jnp.clip(position, 0, self.size - 1) if axis == "tensor" else lax.axis_index(axis)
            for axis in self.mesh_axes
        )

    def greet(self, barrier):
        for step in (-1, 1):
            inside = jnp.logical_and(self.place + step >= 0, self.place + step < self.size)

            @pl.when(inside)
            def _(step=step):
                pl.semaphore_signal(
                    barrier, inc=1, device_id=self.device(self.place + step), device_id_type=MESH_ID
                )

        at_end = jnp.logical_or(self.place == 0, self.place == self.size - 1)
        return jnp.where(at_end, 1, 2)

    def rows_of(self, side, index):
        return pl.ds(pl.multiple_of(side * self.half + index * CHUNK, CHUNK), CHUNK)

    def sum_copy(self, side, index, source):
        rows = self.rows_of(side, index)
        return pltpu.make_async_remote_copy(
            source.at[rows],
            self.arrived.at[rows],
            self.sum_send.at[side, index],
            self.sum_recv.at[side, index],
            device_id=self.device(self.place + self.lines[side][1]),
            device_id_type=MESH_ID,
        )

    def back_copy(self, side, index):
        rows = self.rows_of(side, index)
        return pltpu.make_async_remote_copy(
            self.out.at[rows],
            self.out.at[rows],
            self.back_send.at[side, index],
            self.back_recv.at[side, index],
            device_id=self.device(self.place - self.lines[side][1]),
            device_id_type=MESH_ID,
        )

    def step(self, time):
        for side in (0, 1):
            hops = self.lines[side][0]
            index = time - LAG * hops
            valid = jnp.logical_and(index >= 0, index < self.chunks)
            at_source, at_owner = hops == 0, hops == self.size - 1
            index = jnp.clip(index, 0, self.chunks - 1)
            rows = self.rows_of(side, index)

            @pl.when(jnp.logical_and(valid, at_source))
            def _(side=side, index=index):
                self.sum_copy(side, index, self.part).start()

            @pl.when(jnp.logical_and(valid, jnp.logical_not(at_source)))
            def _(side=side, index=index):
                self.sum_copy(side, index, self.arrived).wait_recv()

            between = jnp.logical_and(jnp.logical_not(at_source), jnp.logical_not(at_owner))

            @pl.when(jnp.logical_and(valid, between))
            def _(side=side, index=index, rows=rows):
                total = self.part[rows].astype(F32) + self.arrived[rows].astype(F32)
                self.arrived[rows] = total.astype(BF16)
                self.sum_copy(side, index, self.arrived).start()

            @pl.when(jnp.logical_and(valid, at_owner))
            def _(side=side, index=index, rows=rows):
                total = self.part[rows].astype(F32) + self.arrived[rows].astype(F32)
                own = pl.ds(pl.multiple_of(index * CHUNK, CHUNK), CHUNK)
                self.transform(total, rows, own)
                self.back_copy(side, index).start()

            away = self.size - 1 - hops
            index = time - LAG * (self.size - 1 + away)
            valid = jnp.logical_and(jnp.logical_and(index >= 0, index < self.chunks), away > 0)
            index = jnp.clip(index, 0, self.chunks - 1)

            @pl.when(valid)
            def _(side=side, index=index):
                self.back_copy(side, index).wait_recv()

            @pl.when(jnp.logical_and(valid, away < self.size - 1))
            def _(side=side, index=index):
                self.back_copy(side, index).start()

    def run(self, first, last, beside=None):
        def body(time, _):
            self.step(time)
            if beside is not None:
                beside(time)
            return 0

        lax.fori_loop(first, last, body, 0)

    def source_sent(self, first, last):
        def body(index, _):
            for side in (0, 1):

                @pl.when(self.lines[side][0] == 0)
                def _(side=side):
                    self.sum_copy(side, index, self.part).wait_send()

            return 0

        lax.fori_loop(first, last, body, 0)

    def finish(self, source_waits=True):
        def body(index, _):
            for side in (0, 1):
                hops = self.lines[side][0]
                passed = hops < self.size - 1
                if not source_waits:
                    passed = jnp.logical_and(passed, hops > 0)

                @pl.when(passed)
                def _(side=side):
                    self.sum_copy(side, index, self.arrived).wait_send()

                @pl.when(hops > 0)
                def _(side=side):
                    self.back_copy(side, index).wait_send()

            return 0

        lax.fori_loop(0, self.chunks, body, 0)


def line_sems(tokens):
    return [pltpu.SemaphoreType.DMA((2, tokens // 2 // CHUNK))] * 4


def inverse_rms(values):
    return lax.rsqrt(jnp.mean(values * values, axis=-1, keepdims=True) + EPSILON)


class Plane:
    def __init__(self, mesh_axes):
        self.mesh_axes = mesh_axes
        self.context = lax.axis_size("context")
        self.per_row = self.context // 2
        self.chips = lax.axis_size("shard") * self.per_row
        context_place = lax.axis_index("context")
        self.core = lax.rem(context_place, 2)
        self.chip = lax.axis_index("shard") * self.per_row + context_place // 2

    def device(self, chip, core):
        places = {
            "shard": chip // self.per_row,
            "context": 2 * lax.rem(chip, self.per_row) + core,
            "tensor": lax.axis_index("tensor"),
        }
        return tuple(places[axis] for axis in self.mesh_axes)

    def ahead(self, distance):
        return lax.rem(self.chip + distance, self.chips)

    def greet(self, barrier):
        targets = [self.device(self.chip, 1 - self.core)]
        targets += [self.device(self.ahead(step), self.core) for step in range(1, self.chips)]
        for target in targets:
            pl.semaphore_signal(barrier, inc=1, device_id=target, device_id_type=MESH_ID)
        return len(targets)


class Gather:
    def __init__(self, plane, sources, targets, sems):
        self.plane, self.sources, self.targets = plane, sources, targets
        self.load_sem, self.send_sem, self.recv_sem, self.pair_send, self.pair_recv = sems
        self.block = sources[0].shape[0]
        self.part = self.block // 2
        self.relayed = plane.chips == 4
        self.arrays = range(len(sources))

    def partner(self, distance):
        return jnp.bitwise_xor(self.plane.chip, distance)

    def greet(self, barrier):
        plane = self.plane
        targets = [plane.device(plane.chip, 1 - plane.core)]
        targets += [
            plane.device(self.partner(step), plane.core)
            for step in range(1, 3 if self.relayed else plane.chips)
        ]
        for target in targets:
            pl.semaphore_signal(barrier, inc=1, device_id=target, device_id_type=MESH_ID)
        return len(targets)

    def place(self, array, chip, core, half):
        first = (2 * chip + core) * self.block + half * self.part
        rows = pl.ds(pl.multiple_of(first, self.part), self.part)
        return self.targets[array].at[rows, pl.ds(0, self.sources[array].shape[1])]

    def mine(self, array, half):
        return self.sources[array].at[pl.ds(half * self.part, self.part)]

    def loads(self):
        plane = self.plane
        return [
            pltpu.make_async_copy(
                self.mine(array, half),
                self.place(array, plane.chip, plane.core, half),
                self.load_sem.at[array, half],
            )
            for array in self.arrays
            for half in range(2)
        ]

    def send(self, distance, half):
        plane = self.plane
        copies = []
        for array in self.arrays:
            chip, target = plane.chip, self.partner(distance)
            source = self.mine(array, half)
            if self.relayed and distance == 3:
                chip = self.partner(2 if half == 0 else 1)
                target = self.partner(1 if half == 0 else 2)
                source = self.place(array, chip, plane.core, half)
            copies.append(
                pltpu.make_async_remote_copy(
                    source,
                    self.place(array, chip, plane.core, half),
                    self.send_sem.at[array, distance - 1, half],
                    self.recv_sem.at[array, distance - 1, half],
                    device_id=plane.device(target, plane.core),
                    device_id_type=MESH_ID,
                )
            )
        return copies

    def forward(self, distance, half):
        plane = self.plane
        copies = []
        for array in self.arrays:
            place = self.place(array, self.partner(distance), plane.core, half)
            copies.append(
                pltpu.make_async_remote_copy(
                    self.mine(array, half) if distance == 0 else place,
                    place,
                    self.pair_send.at[array, distance, half],
                    self.pair_recv.at[array, distance, half],
                    device_id=plane.device(plane.chip, 1 - plane.core),
                    device_id_type=MESH_ID,
                )
            )
        return copies

    def start(self):
        if self.relayed:
            order = ((1, 1), (2, 0), (1, 0), (2, 1))
        else:
            order = [(step, half) for step in range(1, self.plane.chips) for half in range(2)]
        for distance, half in order:
            for copy in self.send(distance, half):
                copy.start()
        for copy in self.loads():
            copy.start()
        for half in range(2):
            for copy in self.forward(0, half):
                copy.start()

    def take(self, distance, half, relay):
        for copy in self.send(distance, half):
            copy.wait_recv()
        if relay:
            for copy in self.send(3, half):
                copy.start()
        for copy in self.forward(distance, half):
            copy.start()

    def stage(self, number):
        if self.relayed:
            if number == 0:
                self.take(1, 1, True)
                self.take(2, 0, True)
            elif number == 1:
                self.take(1, 0, False)
                self.take(2, 1, False)
            else:
                self.take(3, 0, False)
                self.take(3, 1, False)
        elif number == 2:
            for distance in range(1, self.plane.chips):
                for half in range(2):
                    self.take(distance, half, False)

    def arrive_from(self, distance):
        if distance == 0:
            for copy in self.loads():
                copy.wait()
        for half in range(2):
            for copy in self.forward(distance, half):
                copy.wait_recv()

    def arrive(self):
        for distance in range(self.plane.chips):
            self.arrive_from(distance)

    def finish(self):
        for distance in range(self.plane.chips):
            for half in range(2):
                for copy in self.forward(distance, half):
                    copy.wait_send()
                if distance > 0:
                    for copy in self.send(distance, half):
                        copy.wait_send()


def gather_sems(arrays):
    chips = lax.axis_size("shard") * lax.axis_size("context") // 2
    return [
        pltpu.SemaphoreType.DMA((arrays, 2)),
        pltpu.SemaphoreType.DMA((arrays, chips - 1, 2)),
        pltpu.SemaphoreType.DMA((arrays, chips - 1, 2)),
        pltpu.SemaphoreType.DMA((arrays, chips, 2)),
        pltpu.SemaphoreType.DMA((arrays, chips, 2)),
    ]


GROUP = 128
TILE = 256
WIDE = 512


def middle_kernel(
    mesh_axes,
    mix_hbm,
    cotangent_ref,
    input_hbm,
    gain_ref,
    gate_hbm,
    up_hbm,
    down_hbm,
    normed_ref,
    out_ref,
    gain_grad,
    residual_hbm,
    hidden_hbm,
    grad_gate_hbm,
    grad_up_hbm,
    feed_hbm,
    grad_hbm,
    grads_hbm,
    gate_w,
    up_w,
    down_w,
    part,
    mix_arrived,
    arrived,
    inputs,
    residual,
    stage_hidden,
    stage_gate,
    stage_up,
    stage_feed,
    part_sem,
    input_sem,
    save_sem,
    stage_sem,
    grad_sem,
    back_sem,
    tile_sem,
    *sems,
):
    tokens, model_width = normed_ref.shape
    half = tokens // 2
    hidden_width = gate_hbm.shape[1]
    padded = gate_w.shape[1]
    groups = half // GROUP
    place, line_size = lax.axis_index("tensor"), lax.axis_size("tensor")
    own_half = pl.ds(pl.multiple_of(jnp.where(place == 0, 0, half), half), half)
    part_load = pltpu.make_async_copy(mix_hbm, part, part_sem.at[0])
    part_load.start()
    input_load = pltpu.make_async_copy(input_hbm.at[own_half], inputs, input_sem.at[0])
    input_load.start()
    if padded > hidden_width:
        spare = slice(hidden_width, padded)
        gate_w[:, spare] = jnp.zeros((model_width, padded - hidden_width), BF16)
        up_w[:, spare] = jnp.zeros((model_width, padded - hidden_width), BF16)
        down_w[:, spare] = jnp.zeros((model_width, padded - hidden_width), BF16)
    gain_grad[...] = jnp.zeros_like(gain_grad)

    def mix_turn(total, rows, own):
        values = inputs[own].astype(F32) + total
        residual[own] = values
        normed_ref[rows] = (values * inverse_rms(values) * gain_ref[...]).astype(BF16)

    def turn(total, rows, own):
        values = residual[own]
        inverse = inverse_rms(values)
        unit = values * inverse
        gain_grad[...] += jnp.sum(total * unit, axis=0, keepdims=True)
        lifted = total * gain_ref[...]
        mean = jnp.mean(lifted * unit, axis=-1, keepdims=True)
        grad = cotangent_ref[rows].astype(F32) + inverse * (lifted - unit * mean)
        residual[own] = grad
        out_ref[rows] = grad.astype(BF16)

    mix_line = Line(mesh_axes, part, mix_arrived, normed_ref, sems[:4], mix_turn)
    line = Line(mesh_axes, part, arrived, out_ref, sems[4:8], turn)
    gather = Gather(
        Plane(mesh_axes), (gate_hbm, up_hbm, down_hbm), (gate_w, up_w, down_w), sems[8:]
    )
    barrier = pltpu.get_barrier_semaphore()
    expected = mix_line.greet(barrier) + gather.greet(barrier)
    pl.semaphore_wait(barrier, expected)
    gather.start()
    part_load.wait()
    input_load.wait()
    pace = GROUP // CHUNK
    begin = pace + 2 * LAG * (line_size - 1) + 4
    mix_line.run(0, begin - 10)
    gather.stage(0)
    mix_line.run(begin - 10, begin - 4)
    gather.stage(1)
    mix_line.run(begin - 4, begin)
    gather.stage(2)
    gather.arrive()

    def both(ref, group):
        first = pl.ds(pl.multiple_of(group * GROUP, GROUP), GROUP)
        second = pl.ds(pl.multiple_of(half + group * GROUP, GROUP), GROUP)
        return first, second

    def stage_copies(group):
        slot = lax.rem(group, 2)
        copies = []
        for side, rows in enumerate(both(None, group)):
            from_rows = pl.ds(side * GROUP, GROUP)
            columns = pl.ds(0, hidden_width)
            for which, (stage, target) in enumerate(
                (
                    (stage_hidden, hidden_hbm),
                    (stage_gate, grad_gate_hbm),
                    (stage_up, grad_up_hbm),
                )
            ):
                copies.append(
                    pltpu.make_async_copy(
                        stage.at[slot, from_rows, columns],
                        target.at[rows],
                        stage_sem.at[slot, which, side],
                    )
                )
            copies.append(
                pltpu.make_async_copy(
                    stage_feed.at[slot, from_rows], feed_hbm.at[rows], stage_sem.at[slot, 3, side]
                )
            )
        return copies

    def hidden_tile(group, tile):
        first, second = both(normed_ref, group)
        slot = lax.rem(group, 2)
        columns = pl.ds(pl.multiple_of(tile * WIDE, WIDE), WIDE)
        rows = jnp.concatenate([normed_ref[first], normed_ref[second]], axis=0)
        gate = mm_nn(rows, gate_w[:, columns])
        up = mm_nn(rows, up_w[:, columns])
        grads = jnp.concatenate([cotangent_ref[first], cotangent_ref[second]], axis=0)
        grad = mm_nn(grads, down_w[:, columns])
        sigma = jax.nn.sigmoid(gate)
        active = gate * sigma
        stage_hidden[slot, :, columns] = (active * up).astype(BF16)
        stage_gate[slot, :, columns] = (grad * up * sigma * (1.0 + gate * (1.0 - sigma))).astype(
            BF16
        )
        stage_up[slot, :, columns] = (grad * active).astype(BF16)

    def model_tile(group, tile):
        first, second = both(part, group)
        slot = lax.rem(group, 2)
        columns = pl.ds(pl.multiple_of(tile * WIDE, WIDE), WIDE)
        back = mm_nt(stage_gate[slot], gate_w[columns, :])
        back = (back + mm_nt(stage_up[slot], up_w[columns, :])).astype(BF16)
        part[first, columns] = back[:GROUP]
        part[second, columns] = back[GROUP:]
        stage_feed[slot, :, columns] = mm_nt(stage_hidden[slot], down_w[columns, :]).astype(BF16)

    hidden_tiles, model_tiles = padded // WIDE, model_width // WIDE
    ticks = hidden_tiles + model_tiles
    piece = -(-ticks // pace)
    save = pltpu.make_async_copy(residual, residual_hbm, save_sem.at[0])

    def group_body(group, _):
        mix_line.source_sent(group * pace, (group + 1) * pace)

        @pl.when(group == 1)
        def _():
            save.start()

        @pl.when(group == 2)
        def _():
            save.wait()

        @pl.when(group >= 2)
        def _():
            for copy in stage_copies(group - 2):
                copy.wait()

        def piece_body(index, _):
            def tick_body(offset, _):
                tick = index * piece + offset

                @pl.when(tick < hidden_tiles)
                def _():
                    hidden_tile(group, tick)

                @pl.when(jnp.logical_and(tick >= hidden_tiles, tick < ticks))
                def _():
                    model_tile(group, tick - hidden_tiles)

                return 0

            lax.fori_loop(0, piece, tick_body, 0)

            mix_time = begin + group * pace + index

            @pl.when(mix_time < mix_line.steps)
            def _():
                mix_line.step(mix_time)

            @pl.when(group >= 1)
            def _():
                line.step((group - 1) * pace + index)

            return 0

        lax.fori_loop(0, pace, piece_body, 0)
        for copy in stage_copies(group):
            copy.start()
        return 0

    lax.fori_loop(0, groups, group_body, 0)
    for group in range(max(groups - 2, 0), groups):
        for copy in stage_copies(group):
            copy.wait()
    gather.finish()

    token_rows, hidden_columns = pl.ds(0, tokens), pl.ds(0, hidden_width)
    returned = [
        pltpu.make_async_copy(
            source, target.at[token_rows, hidden_columns], back_sem.at[which]
        )
        for which, (source, target) in enumerate(
            ((grad_gate_hbm, gate_w), (grad_up_hbm, up_w), (hidden_hbm, down_w))
        )
    ]
    for copy in returned:
        copy.start()
    tiles = model_width // TILE
    first_time = (groups - 1) * pace + 1
    stages = (stage_gate, stage_up, stage_hidden)

    def tile_copies(tile):
        rows = pl.ds(pl.multiple_of(tile * TILE, TILE), TILE)
        slot = lax.rem(tile, 2)
        return [
            pltpu.make_async_copy(
                stage.at[slot, pl.ds(0, TILE), hidden_columns],
                grads_hbm.at[which, rows],
                tile_sem.at[slot, which],
            )
            for which, stage in enumerate(stages)
        ]

    def weight_tile(time):
        tile = time - first_time

        @pl.when(tile == 0)
        def _():
            for copy in returned:
                copy.wait()

        @pl.when(jnp.logical_and(tile >= 2, tile < tiles))
        def _():
            for copy in tile_copies(tile - 2):
                copy.wait()

        @pl.when(jnp.logical_and(tile >= 0, tile < tiles))
        def _():
            slot = lax.rem(tile, 2)
            columns = pl.ds(pl.multiple_of(tile * TILE, TILE), TILE)
            rows = normed_ref[:, columns]
            for source, right, stage in (
                (rows, gate_w, stage_gate),
                (rows, up_w, stage_up),
                (cotangent_ref[:, columns], down_w, stage_hidden),
            ):
                product = mm_tn(source, right[:tokens, :hidden_width])
                stage[slot, :TILE, :hidden_width] = product.astype(BF16)
            for copy in tile_copies(tile):
                copy.start()

    line.run((groups - 1) * pace, line.steps, weight_tile)
    grad_save = pltpu.make_async_copy(residual, grad_hbm, grad_sem.at[0])
    grad_save.start()
    for tile in range(max(tiles - 2, 0), tiles):
        for copy in tile_copies(tile):
            copy.wait()
    mix_line.finish(source_waits=False)
    line.finish()
    grad_save.wait()


def middle(mesh_axes, collective, mix, cotangent, inputs, gain, gate_w, up_w, down_w):
    tokens, model_width = mix.shape
    hidden_width = gate_w.shape[1]
    padded = -(-hidden_width // WIDE) * WIDE
    whole = pl.BlockSpec(memory_space=pltpu.VMEM)
    remote = pl.BlockSpec(memory_space=pl.ANY)
    group_rows = 2 * GROUP
    return pl.pallas_call(
        partial(middle_kernel, mesh_axes),
        in_specs=[remote, whole, remote, whole, remote, remote, remote],
        out_specs=[whole, whole, whole] + [remote] * 7,
        out_shape=[
            jax.ShapeDtypeStruct((tokens, model_width), BF16),
            jax.ShapeDtypeStruct((tokens, model_width), BF16),
            jax.ShapeDtypeStruct((1, model_width), F32),
            jax.ShapeDtypeStruct((tokens // 2, model_width), F32),
            jax.ShapeDtypeStruct((tokens, hidden_width), BF16),
            jax.ShapeDtypeStruct((tokens, hidden_width), BF16),
            jax.ShapeDtypeStruct((tokens, hidden_width), BF16),
            jax.ShapeDtypeStruct((tokens, model_width), BF16),
            jax.ShapeDtypeStruct((tokens // 2, model_width), F32),
            jax.ShapeDtypeStruct((3, model_width, hidden_width), BF16),
        ],
        scratch_shapes=[
            pltpu.VMEM((model_width, padded), BF16),
            pltpu.VMEM((model_width, padded), BF16),
            pltpu.VMEM((model_width, padded), BF16),
            pltpu.VMEM((tokens, model_width), BF16),
            pltpu.VMEM((tokens, model_width), BF16),
            pltpu.VMEM((tokens, model_width), BF16),
            pltpu.VMEM((tokens // 2, model_width), BF16),
            pltpu.VMEM((tokens // 2, model_width), F32),
            pltpu.VMEM((2, group_rows, padded), BF16),
            pltpu.VMEM((2, group_rows, padded), BF16),
            pltpu.VMEM((2, group_rows, padded), BF16),
            pltpu.VMEM((2, group_rows, model_width), BF16),
            pltpu.SemaphoreType.DMA((1,)),
            pltpu.SemaphoreType.DMA((1,)),
            pltpu.SemaphoreType.DMA((1,)),
            pltpu.SemaphoreType.DMA((2, 4, 2)),
            pltpu.SemaphoreType.DMA((1,)),
            pltpu.SemaphoreType.DMA((3,)),
            pltpu.SemaphoreType.DMA((2, 3)),
        ]
        + line_sems(tokens)
        + line_sems(tokens)
        + gather_sems(3),
        compiler_params=pltpu.CompilerParams(
            collective_id=collective, has_side_effects=True, vmem_limit_bytes=61 << 20
        ),
        cost_estimate=pl.CostEstimate(
            flops=tokens * model_width * hidden_width * 12,
            bytes_accessed=360_000_000,
            transcendentals=tokens * hidden_width,
        ),
        name="middle",
    )(mix, cotangent, inputs, gain, gate_w, up_w, down_w)


def output_kernel(
    mesh_axes,
    head_count,
    key_scale,
    part,
    residual,
    gated_ref,
    mix_grad_ref,
    out_full,
    mixed_ref,
    lead_ref,
    starts_ref,
    run_ref,
    carry_ref,
    decay_ref,
    link_ref,
    open_ref,
    count_ref,
    keep_ref,
    flags_ref,
    gain_ref,
    normed_hbm,
    pre_hbm,
    full_hbm,
    out_ref,
    gain_grad,
    floor_grad,
    back_ref,
    out_grads_hbm,
    mixer_grads_hbm,
    arrived,
    left,
    right,
    full,
    out_stage,
    mixer_stage,
    gates,
    pre,
    grad_mixed,
    back_scr,
    message,
    received,
    grad_scr,
    lifted_scr,
    lowered_scr,
    moved_scr,
    value_scr,
    load_sem,
    pre_sem,
    stage_sem,
    grad_send,
    grad_recv,
    *sems,
):
    tokens, model_width = left.shape
    width = gated_ref.shape[1]
    lanes = width // head_count
    state_rows = head_count * lanes
    tiles, blocks = model_width // TILE, tokens // BLOCK
    piece_rows = 2 * BLOCK
    context, context_size = lax.axis_index("context"), lax.axis_size("context")

    left_load = pltpu.make_async_copy(normed_hbm, left, load_sem.at[0])
    full_load = pltpu.make_async_copy(full_hbm, full, load_sem.at[1])
    gate_load = pltpu.make_async_copy(
        pre_hbm.at[:, pl.ds(3 * width, width)], gates, load_sem.at[2]
    )
    for load in (gate_load, left_load, full_load):
        load.start()
    gain_grad[...] = jnp.zeros_like(gain_grad)
    floor_grad[...] = jnp.zeros_like(floor_grad)
    back_scr[...] = jnp.zeros_like(back_scr)

    def turn(total, rows, own):
        out_ref[rows] = (residual[own] + total).astype(BF16)

    def earlier(shift):
        places = {axis: lax.axis_index(axis) for axis in mesh_axes}
        places["context"] = lax.rem(context + context_size - shift, context_size)
        return tuple(places[axis] for axis in mesh_axes)

    line = Line(mesh_axes, part, arrived, out_ref, sems, turn)
    barrier = pltpu.get_barrier_semaphore()
    expected = line.greet(barrier)
    for shift in range(1, context_size):
        pl.semaphore_signal(barrier, inc=1, device_id=earlier(shift), device_id_type=MESH_ID)
    pl.semaphore_wait(barrier, expected + context_size - 1)
    gate_load.wait()

    def tile_columns(tile):
        return pl.ds(pl.multiple_of(tile * TILE, TILE), TILE)

    def stage_copies(tile):
        rows = tile_columns(tile)
        return (
            pltpu.make_async_copy(out_stage, out_grads_hbm.at[rows], stage_sem.at[0]),
            pltpu.make_async_copy(mixer_stage, mixer_grads_hbm.at[rows], stage_sem.at[1]),
        )

    def gate_piece(index):
        rows = pl.ds(pl.multiple_of(index * piece_rows, piece_rows), piece_rows)
        grads = mm_nn(mix_grad_ref[rows], out_full[...])
        gain = gain_ref[...]
        total = jnp.zeros_like(gain)
        for head in range(head_count):
            part_of = slice(head * lanes, (head + 1) * lanes)
            mixed, gate, grad = mixed_ref[rows, part_of], gates[rows, part_of], grads[:, part_of]
            inverse = inverse_rms(mixed)
            unit = mixed * inverse
            sigma = jax.nn.sigmoid(gate)
            scaled = grad * unit
            total = total + jnp.sum(scaled * (gate * sigma), axis=0, keepdims=True)
            grad_gate = scaled * gain * sigma * (1.0 + gate * (1.0 - sigma))
            first = 3 * width + head * lanes
            right[rows, first : first + lanes] = grad_gate.astype(BF16)
            lifted = grad * gain * (gate * sigma)
            mean = jnp.mean(lifted * unit, axis=-1, keepdims=True)
            grad_in = inverse * (lifted - unit * mean) * (key_scale * keep_ref[rows])
            grad_in = grad_in.astype(BF16)
            grad_mixed[rows, part_of] = grad_in
            back_scr[head] += mm_tn(grad_in, lead_ref[rows, part_of])
        gain_grad[...] += total

    def state_copy(shift):
        return pltpu.make_async_remote_copy(
            message,
            received.at[shift - 1],
            grad_send.at[shift - 1],
            grad_recv.at[shift - 1],
            device_id=earlier(shift),
            device_id_type=MESH_ID,
        )

    def block_of(index):
        return blocks - 1 - index

    def pre_load(index):
        rows = pl.ds(pl.multiple_of(block_of(index) * BLOCK, BLOCK), BLOCK)
        slot = lax.rem(index, 2)
        return pltpu.make_async_copy(
            pre_hbm.at[rows, pl.ds(0, 3 * width)], pre.at[slot], pre_sem.at[slot]
        )

    def send_back():
        for head in range(head_count):
            rows = slice(head * lanes, (head + 1) * lanes)
            message[rows] = back_scr[head] * link_ref[0:1]
            message[state_rows + head : state_rows + head + 1] = decay_ref[head] * link_ref[0:1]
        for shift in range(1, context_size):

            @pl.when(context >= shift)
            def _(shift=shift):
                state_copy(shift).start()

        pre_load(0).start()

    def take_back():
        grad_scr[...] = jnp.zeros_like(grad_scr)
        for shift in range(1, context_size):

            @pl.when(context + shift < context_size)
            def _(shift=shift):
                state_copy(shift).wait_recv()
                for head in range(head_count):
                    value = received[shift - 1, head * lanes : (head + 1) * lanes]
                    for near in range(shift - 1):
                        value = value * received[near, state_rows + head : state_rows + head + 1]
                    grad_scr[head] += value

        for shift in range(1, context_size):

            @pl.when(context >= shift)
            def _(shift=shift):
                state_copy(shift).wait_send()

    def mixer_block(index):
        block = block_of(index)
        slot = lax.rem(index, 2)
        block_rows = pl.ds(pl.multiple_of(block * BLOCK, BLOCK), BLOCK)

        @pl.when(index + 1 < blocks)
        def _():
            pre_load(index + 1).start()

        pre_load(index).wait()
        counts, keep, flags = count_ref[block_rows], keep_ref[block_rows], flags_ref[block]
        row_ids, col_ids, linked, fresh, tail, closing = block_masks(counts, flags)
        tri = (row_ids >= col_ids).astype(BF16)
        tri_back = (row_ids <= col_ids).astype(BF16)
        query_pre = pre[slot, :, :width]
        values = pre[slot, :, 2 * width : 3 * width].astype(BF16)
        opened = open_ref[...]
        closed = jax.nn.sigmoid(-pre[slot, :, width : 2 * width])
        keys = opened * closed
        cum = split_sum(tri, jnp.log1p(-keys))
        ending = cum[BLOCK - 1 : BLOCK, :]
        rise, fall = jnp.exp(cum), jnp.exp(-cum) * keep
        shift = jnp.exp(ending - cum) * (keep * tail)
        sigma_query = jax.nn.sigmoid(query_pre)
        lifted = (query_pre * sigma_query * rise).astype(BF16)
        lowered = (keys * fall).astype(BF16)
        moved = (keys * shift).astype(BF16)
        fresh_lifted = (lifted.astype(F32) * fresh).astype(BF16)
        end_decay = jnp.exp(ending) * closing
        lead_in = jnp.exp(run_ref[block]) * (flags[1:2, 0:1] == 0).astype(F32)
        for head in range(head_count):
            part_of = slice(head * lanes, (head + 1) * lanes)
            grad_out, value = grad_mixed[block_rows, part_of], values[:, part_of]
            lift, lower, move = lifted[:, part_of], lowered[:, part_of], moved[:, part_of]
            scores = jnp.where(linked, mm_nt(lift, lower), 0.0).astype(BF16)
            pulls = jnp.where(linked, mm_nt(grad_out, value), 0.0).astype(BF16)
            state = starts_ref[block, head] + lead_in[:, part_of] * carry_ref[head]
            grad_state = grad_scr[head]
            grad_low = grad_state.astype(BF16)
            lifted_scr[:, part_of] = mm_nn(pulls, lower) + fresh * mm_nn(
                grad_out, state.astype(BF16)
            )
            lowered_scr[:, part_of] = mm_tn(pulls, lift)
            grad_moved = mm_nn(value, grad_low)
            moved_scr[:, part_of] = grad_moved
            first = 2 * width + head * lanes
            right[block_rows, first : first + lanes] = (
                mm_tn(scores, grad_out) + mm_nt(move, grad_low)
            ).astype(BF16)
            value_scr[:, part_of] = jnp.sum(
                grad_moved * move.astype(F32), axis=0, keepdims=True
            ) + end_decay[:, part_of] * jnp.sum(state * grad_state, axis=0, keepdims=True)
            grad_scr[head] = grad_state * end_decay[:, part_of] + mm_tn(
                grad_out, fresh_lifted[:, part_of]
            )
        grad_lifted, grad_lowered, grad_moved = lifted_scr[...], lowered_scr[...], moved_scr[...]
        grad_cum = (
            grad_lifted * lifted.astype(F32)
            - grad_lowered * lowered.astype(F32)
            - grad_moved * moved.astype(F32)
        )
        grad_decay = split_sum(tri_back, grad_cum) + value_scr[...]
        key_total = grad_lowered * fall + grad_moved * shift - grad_decay / (1.0 - keys)
        floor_grad[...] -= jnp.sum(key_total * closed, axis=0, keepdims=True)
        right[block_rows, :width] = (
            grad_lifted * rise * sigma_query * (1.0 + query_pre * (1.0 - sigma_query))
        ).astype(BF16)
        right[block_rows, width : 2 * width] = (
            -key_total * opened * closed * (1.0 - closed)
        ).astype(BF16)

    def back_tile(tile):
        columns = tile_columns(tile)
        back_ref[:, columns] = mm_nt(right[...], full[columns, :]).astype(BF16)

    def mixer_tile(tile):
        @pl.when(tile > 0)
        def _():
            for copy in stage_copies(tile - 1):
                copy.wait()

        columns = tile_columns(tile)
        rows = left[:, columns]
        for first in range(0, 4 * width, 1024):
            some = slice(first, min(first + 1024, 4 * width))
            mixer_stage[:, some] = mm_tn(rows, right[:, some]).astype(BF16)
        out_stage[...] = mm_tn(mix_grad_ref[:, columns], gated_ref[...]).astype(BF16)
        for copy in stage_copies(tile):
            copy.start()

    send_time = tokens // piece_rows
    block_time = send_time + 1
    back_time = block_time + blocks
    tile_time = back_time + tiles
    end_time = tile_time + tiles

    def beside(time):
        @pl.when(time < send_time)
        def _():
            gate_piece(time)

        @pl.when(time == send_time)
        def _():
            send_back()

        @pl.when(time == block_time)
        def _():
            take_back()

        @pl.when(jnp.logical_and(time >= block_time, time < back_time))
        def _():
            mixer_block(time - block_time)

        @pl.when(time == back_time)
        def _():
            full_load.wait()

        @pl.when(jnp.logical_and(time >= back_time, time < tile_time))
        def _():
            back_tile(time - back_time)

        @pl.when(time == tile_time)
        def _():
            left_load.wait()

        @pl.when(jnp.logical_and(time >= tile_time, time < end_time))
        def _():
            mixer_tile(time - tile_time)

    steps = max(line.steps, end_time)

    def body(time, _):
        @pl.when(time < line.steps)
        def _():
            line.step(time)

        beside(time)
        return 0

    lax.fori_loop(0, steps, body, 0)
    for copy in stage_copies(tiles - 1):
        copy.wait()
    line.finish()


def output_line(mesh_axes, collective, in_vmem, in_hbm, head_count):
    part, _, gated = in_vmem[:3]
    tokens, model_width = part.shape
    width = gated.shape[1]
    lanes = width // head_count
    context_size = lax.axis_size("context")
    messages = head_count * lanes + -(-head_count // 8) * 8
    whole = pl.BlockSpec(memory_space=pltpu.VMEM)
    remote = pl.BlockSpec(memory_space=pl.ANY)
    return pl.pallas_call(
        partial(output_kernel, mesh_axes, head_count, lanes ** (-0.5)),
        in_specs=[whole] * len(in_vmem) + [remote] * len(in_hbm),
        out_specs=[whole] * 4 + [remote] * 2,
        out_shape=[
            jax.ShapeDtypeStruct((tokens, model_width), BF16),
            jax.ShapeDtypeStruct((1, lanes), F32),
            jax.ShapeDtypeStruct((1, width), F32),
            jax.ShapeDtypeStruct((tokens, model_width), BF16),
            jax.ShapeDtypeStruct((model_width, width), BF16),
            jax.ShapeDtypeStruct((model_width, 4 * width), BF16),
        ],
        scratch_shapes=[
            pltpu.VMEM((tokens, model_width), BF16),
            pltpu.VMEM((tokens, model_width), BF16),
            pltpu.VMEM((tokens, 4 * width), BF16),
            pltpu.VMEM((model_width, 4 * width), BF16),
            pltpu.VMEM((TILE, width), BF16),
            pltpu.VMEM((TILE, 4 * width), BF16),
            pltpu.VMEM((tokens, width), F32),
            pltpu.VMEM((2, BLOCK, 3 * width), F32),
            pltpu.VMEM((tokens, width), BF16),
            pltpu.VMEM((head_count, lanes, lanes), F32),
            pltpu.VMEM((messages, lanes), F32),
            pltpu.VMEM((context_size - 1, messages, lanes), F32),
            pltpu.VMEM((head_count, lanes, lanes), F32),
            pltpu.VMEM((BLOCK, width), F32),
            pltpu.VMEM((BLOCK, width), F32),
            pltpu.VMEM((BLOCK, width), F32),
            pltpu.VMEM((1, width), F32),
            pltpu.SemaphoreType.DMA((3,)),
            pltpu.SemaphoreType.DMA((2,)),
            pltpu.SemaphoreType.DMA((2,)),
            pltpu.SemaphoreType.DMA((context_size - 1,)),
            pltpu.SemaphoreType.DMA((context_size - 1,)),
        ]
        + line_sems(tokens),
        compiler_params=pltpu.CompilerParams(
            collective_id=collective, has_side_effects=True, vmem_limit_bytes=61 << 20
        ),
        cost_estimate=pl.CostEstimate(
            flops=tokens * model_width * width * 24,
            bytes_accessed=360_000_000,
            transcendentals=tokens * width * 12,
        ),
        name="output_line",
    )(*in_vmem, *in_hbm)


def input_kernel(
    mesh_axes,
    part,
    hidden_ref,
    residual_grad,
    gain_ref,
    grads_hbm,
    out_ref,
    gain_grad,
    share_gate,
    share_up,
    share_down,
    arrived,
    own,
    other,
    remote,
    load_sem,
    pair_send,
    pair_recv,
    chip_send,
    chip_recv,
    *sems,
):
    plane = Plane(mesh_axes)
    chips = plane.chips
    block = own.shape[2]
    gain_grad[...] = jnp.zeros_like(gain_grad)

    def turn(total, rows, own_rows):
        values = hidden_ref[rows].astype(F32)
        inverse = inverse_rms(values)
        unit = values * inverse
        gain_grad[...] += jnp.sum(total * unit, axis=0, keepdims=True)
        lifted = total * gain_ref[...]
        mean = jnp.mean(lifted * unit, axis=-1, keepdims=True)
        grad = residual_grad[own_rows] + inverse * (lifted - unit * mean)
        out_ref[rows] = grad.astype(BF16)

    line = Line(mesh_axes, part, arrived, out_ref, sems, turn)
    barrier = pltpu.get_barrier_semaphore()
    expected = line.greet(barrier) + plane.greet(barrier)
    pl.semaphore_wait(barrier, expected)

    def rows_of(slot, core):
        return pl.ds(pl.multiple_of((2 * plane.ahead(slot) + core) * block, block), block)

    def load(slot):
        return pltpu.make_async_copy(
            grads_hbm.at[:, rows_of(slot, plane.core)], own.at[slot], load_sem.at[slot]
        )

    def pair_copy(slot):
        return pltpu.make_async_remote_copy(
            grads_hbm.at[:, rows_of(slot, 1 - plane.core)],
            other.at[slot],
            pair_send.at[slot],
            pair_recv.at[slot],
            device_id=plane.device(plane.chip, 1 - plane.core),
            device_id_type=MESH_ID,
        )

    def chip_copy(slot):
        return pltpu.make_async_remote_copy(
            own.at[slot],
            remote.at[slot - 1],
            chip_send.at[slot - 1],
            chip_recv.at[slot - 1],
            device_id=plane.device(plane.ahead(slot), plane.core),
            device_id_type=MESH_ID,
        )

    def start(index, _):
        slot = lax.rem(index + 1, chips)
        pair_copy(slot).start()
        load(slot).start()
        return 0

    lax.fori_loop(0, chips, start, 0)
    strip = 32

    def combine(time):
        slot = lax.rem(jnp.clip(time, 0, chips - 1) + 1, chips)

        @pl.when(time < chips)
        def _():
            load(slot).wait()
            pair_copy(slot).wait_recv()

            def add(index, _):
                rows = pl.ds(pl.multiple_of(index * strip, strip), strip)
                for which in range(3):
                    total = own[slot, which, rows].astype(F32) + other[slot, which, rows].astype(F32)
                    own[slot, which, rows] = total.astype(BF16)
                return 0

            lax.fori_loop(0, block // strip, add, 0)

        @pl.when(time < chips - 1)
        def _():
            chip_copy(slot).start()

    line.run(0, line.steps, combine)

    def arrive(index, _):
        chip_copy(index).wait_recv()
        return 0

    lax.fori_loop(1, chips, arrive, 0)

    def total(index, _):
        rows = pl.ds(pl.multiple_of(index * strip, strip), strip)

        def whole(which):
            def add(slot, value):
                return value + remote[slot, which, rows].astype(F32)

            return lax.fori_loop(0, chips - 1, add, own[0, which, rows].astype(F32))

        share_gate[rows] = whole(0)
        share_up[rows] = whole(1)
        share_down[rows] = whole(2)
        return 0

    lax.fori_loop(0, block // strip, total, 0)

    def sent(index, _):
        pair_copy(index).wait_send()
        return 0

    lax.fori_loop(0, chips, sent, 0)

    def chip_sent(index, _):
        chip_copy(index).wait_send()
        return 0

    lax.fori_loop(1, chips, chip_sent, 0)
    line.finish()


def input_line(mesh_axes, collective, part, hidden, residual_grad, gain, grads):
    tokens, model_width = part.shape
    hidden_width = grads.shape[2]
    chips = lax.axis_size("shard") * lax.axis_size("context") // 2
    block = model_width // (2 * chips)
    whole = pl.BlockSpec(memory_space=pltpu.VMEM)
    return pl.pallas_call(
        partial(input_kernel, mesh_axes),
        in_specs=[whole] * 4 + [pl.BlockSpec(memory_space=pl.ANY)],
        out_specs=[whole] * 5,
        out_shape=[
            jax.ShapeDtypeStruct((tokens, model_width), BF16),
            jax.ShapeDtypeStruct((1, model_width), F32),
        ]
        + [jax.ShapeDtypeStruct((block, hidden_width), F32)] * 3,
        scratch_shapes=[
            pltpu.VMEM((tokens, model_width), BF16),
            pltpu.VMEM((chips, 3, block, hidden_width), BF16),
            pltpu.VMEM((chips, 3, block, hidden_width), BF16),
            pltpu.VMEM((chips - 1, 3, block, hidden_width), BF16),
            pltpu.SemaphoreType.DMA((chips,)),
            pltpu.SemaphoreType.DMA((chips,)),
            pltpu.SemaphoreType.DMA((chips,)),
            pltpu.SemaphoreType.DMA((chips - 1,)),
            pltpu.SemaphoreType.DMA((chips - 1,)),
        ]
        + line_sems(tokens),
        compiler_params=pltpu.CompilerParams(
            collective_id=collective, has_side_effects=True, vmem_limit_bytes=58 << 20
        ),
        cost_estimate=pl.CostEstimate(
            flops=tokens * model_width * 8, bytes_accessed=360_000_000, transcendentals=0
        ),
        name="input_line",
    )(part, hidden, residual_grad, gain, grads)


def forward_kernel(
    mesh_axes,
    head_count,
    key_scale,
    hidden_ref,
    gain_ref,
    query_hbm,
    forget_hbm,
    input_hbm,
    gate_hbm,
    out_shard_ref,
    down_shard_ref,
    floor_ref,
    segments_ref,
    head_gain_ref,
    normed_hbm,
    pre_hbm,
    full_hbm,
    out_full_hbm,
    mixed_hbm,
    lead_hbm,
    start_hbm,
    gated_hbm,
    mix_hbm,
    down_turned,
    open_ref,
    count_ref,
    keep_ref,
    flags_ref,
    run_ref,
    carry_ref,
    decay_ref,
    link_ref,
    normed,
    pre,
    mine,
    out_turned,
    full,
    out_full,
    mixed,
    lead,
    starts,
    gated,
    mix,
    state_scr,
    run_scr,
    message,
    received,
    mine_sem,
    full_sem,
    save_sem,
    pre_sem,
    mix_sem,
    state_send,
    state_recv,
    *sems,
):
    plane = Plane(mesh_axes)
    chips = plane.chips
    tokens, model_width = hidden_ref.shape
    block, width = query_hbm.shape
    lanes = width // head_count
    state_rows = head_count * lanes
    context, context_size = lax.axis_index("context"), lax.axis_size("context")

    mine_loads = [
        pltpu.make_async_copy(
            ref, mine.at[:, pl.ds(which * width, width)], mine_sem.at[which]
        )
        for which, ref in enumerate((query_hbm, forget_hbm, input_hbm, gate_hbm))
    ]
    for load in mine_loads:
        load.start()
    gather = Gather(plane, (mine,), (full,), sems[:5])
    out_gather = Gather(plane, (out_turned,), (out_full,), sems[5:])

    def later(shift):
        places = {axis: lax.axis_index(axis) for axis in mesh_axes}
        places["context"] = lax.rem(context + shift, context_size)
        return tuple(places[axis] for axis in mesh_axes)

    out_turned[...] = out_shard_ref[...].T
    barrier = pltpu.get_barrier_semaphore()
    expected = gather.greet(barrier)
    for shift in range(1, context_size):
        pl.semaphore_signal(barrier, inc=1, device_id=later(shift), device_id_type=MESH_ID)
    pl.semaphore_wait(barrier, expected + context_size - 1)
    for load in mine_loads:
        load.wait()
    gather.start()
    out_gather.start()
    down_turned[...] = down_shard_ref[...].T
    for head in range(head_count):
        open_ref[:, head * lanes : (head + 1) * lanes] = 1.0 - floor_ref[head : head + 1]

    segments = segments_ref[...]
    blocks = segments.shape[0]
    block_ids = lax.broadcasted_iota(jnp.int32, segments.shape, 0)
    slot_ids = lax.broadcasted_iota(jnp.int32, segments.shape, 1)
    before = pltpu.roll(segments, 1, 1)
    wrapped = pltpu.roll(before, 1, 0)
    before = jnp.where(slot_ids == 0, wrapped, before)
    first_slot = jnp.logical_and(slot_ids == 0, block_ids == 0)
    begins = jnp.where(jnp.logical_or(first_slot, segments == before), 0.0, 1.0)
    wide_rows = lax.broadcasted_iota(jnp.int32, (BLOCK, BLOCK), 0)
    wide_columns = lax.broadcasted_iota(jnp.int32, (BLOCK, BLOCK), 1)
    within = mm_nn(begins.astype(BF16), (wide_rows <= wide_columns).astype(BF16))
    count_rows = []
    running = jnp.zeros((1, 1), F32)
    flags_ref[...] = jnp.zeros_like(flags_ref)
    for index in range(blocks):
        row = within[index : index + 1] + running
        flags_ref[index, 0:1] = row
        flags_ref[index, 1:2] = jnp.broadcast_to(running, (1, BLOCK))
        running = row[:, BLOCK - 1 : BLOCK]
        flags_ref[index, 2:3] = jnp.broadcast_to(running, (1, BLOCK))
        count_rows.append(row)
    turned_counts = jnp.concatenate(count_rows, axis=0).T
    turned_keep = (segments > 0).astype(F32).T
    for index in range(blocks):
        rows = slice(index * BLOCK, (index + 1) * BLOCK)
        count_ref[rows] = turned_counts[:, index : index + 1]
        keep_ref[rows] = turned_keep[:, index : index + 1]
    first_id = jnp.broadcast_to(segments[0:1, 0:1], (1, lanes))
    last_id = jnp.broadcast_to(segments[blocks - 1 : blocks, BLOCK - 1 : BLOCK], (1, lanes))

    def norm(index, _):
        rows = pl.ds(pl.multiple_of(index * 128, 128), 128)
        values = hidden_ref[rows].astype(F32)
        normed[rows] = (values * inverse_rms(values) * gain_ref[...]).astype(BF16)
        return 0

    lax.fori_loop(0, tokens // 128, norm, 0)

    saves = [
        pltpu.make_async_copy(source, target, save_sem.at[which])
        for which, (source, target) in enumerate(
            (
                (normed, normed_hbm),
                (out_full, out_full_hbm),
                (mixed, mixed_hbm),
                (lead, lead_hbm),
                (starts, start_hbm),
                (gated, gated_hbm),
            )
        )
    ]
    saves[0].start()
    row_tile, column_tile = 256, 512

    def pre_save(index):
        rows = pl.ds(pl.multiple_of(index * row_tile, row_tile), row_tile)
        return pltpu.make_async_copy(pre.at[rows], pre_hbm.at[rows], pre_sem.at[index])

    def depth_of(distance):
        first = 2 * gather.partner(distance) * block
        return pl.ds(pl.multiple_of(first, 2 * block), 2 * block)

    def product(distance):
        depth = depth_of(distance)

        def row_body(index, _):
            rows = pl.ds(pl.multiple_of(index * row_tile, row_tile), row_tile)
            left = normed[rows, depth]

            def column_body(column, _):
                columns = pl.ds(pl.multiple_of(column * column_tile, column_tile), column_tile)
                value = mm_nn(left, full[depth, columns])
                if distance > 0:
                    value = value + pre[rows, columns]
                pre[rows, columns] = value
                return 0

            lax.fori_loop(0, full.shape[1] // column_tile, column_body, 0)
            if distance == chips - 1:
                pre_save(index).start()
            return 0

        lax.fori_loop(0, tokens // row_tile, row_body, 0)

    def full_save(distance):
        depth = depth_of(distance)
        return pltpu.make_async_copy(full.at[depth], full_hbm.at[depth], full_sem.at[distance])

    def use(distance):
        gather.arrive_from(distance)
        full_save(distance).start()
        product(distance)

    use(0)
    gather.stage(0)
    gather.stage(1)
    if gather.relayed:
        use(1)
        use(2)
    gather.stage(2)
    if gather.relayed:
        use(3)
    else:
        for distance in range(1, chips):
            use(distance)
    out_gather.stage(0)
    out_gather.stage(1)

    state_scr[...] = jnp.zeros_like(state_scr)
    run_scr[...] = jnp.zeros_like(run_scr)

    def recur(step, _):
        rows = pl.ds(pl.multiple_of(step * BLOCK, BLOCK), BLOCK)
        counts, keep = count_ref[rows], keep_ref[rows]
        row_ids, col_ids, linked, fresh, tail, closing = block_masks(counts, flags_ref[step])
        tri = (row_ids >= col_ids).astype(BF16)
        query_pre = pre[rows, :width]
        values = pre[rows, 2 * width : 3 * width].astype(BF16)
        keys = open_ref[...] * jax.nn.sigmoid(-pre[rows, width : 2 * width])
        cum = split_sum(tri, jnp.log1p(-keys))
        ending = cum[BLOCK - 1 : BLOCK, :]
        lifted = query_pre * jax.nn.sigmoid(query_pre) * jnp.exp(cum)
        lowered = (keys * jnp.exp(-cum) * keep).astype(BF16)
        moved = (keys * jnp.exp(ending - cum) * (keep * tail)).astype(BF16)
        run = run_scr[...]
        lead[rows] = (lifted * jnp.exp(run) * (counts == 0).astype(F32)).astype(BF16)
        run_ref[step] = run
        run_scr[...] = run + ending
        fresh_lifted = (lifted * fresh).astype(BF16)
        lifted = lifted.astype(BF16)
        end_decay = jnp.exp(ending) * closing
        for head in range(head_count):
            part = slice(head * lanes, (head + 1) * lanes)
            state = state_scr[head]
            starts[step, head] = state
            scores = jnp.where(linked, mm_nt(lifted[:, part], lowered[:, part]), 0.0)
            results = mm_nn(scores.astype(BF16), values[:, part])
            results = results + mm_nt(fresh_lifted[:, part], state.astype(BF16))
            mixed[rows, part] = results * (key_scale * keep)
            state_scr[head] = state * end_decay[:, part] + mm_tn(values[:, part], moved[:, part])
        return 0

    lax.fori_loop(0, tokens // BLOCK, recur, 0)
    saves[3].start()
    saves[4].start()

    last_count = flags_ref[tokens // BLOCK - 1][2:3, 0:1]
    for head in range(head_count):
        part = slice(head * lanes, (head + 1) * lanes)
        message[head * lanes : (head + 1) * lanes] = state_scr[head]
        decay = jnp.exp(run_scr[:, part]) * (last_count == 0).astype(F32)
        decay_ref[head] = decay
        message[state_rows + 8 + head : state_rows + 9 + head] = decay
    message[state_rows : state_rows + 1] = first_id
    message[state_rows + 1 : state_rows + 2] = last_id

    def state_copy(shift):
        return pltpu.make_async_remote_copy(
            message,
            received.at[shift - 1],
            state_send.at[shift - 1],
            state_recv.at[shift - 1],
            device_id=later(shift),
            device_id_type=MESH_ID,
        )

    for shift in range(1, context_size):

        @pl.when(context + shift < context_size)
        def _(shift=shift):
            state_copy(shift).start()

    out_gather.stage(2)
    carry_ref[...] = jnp.zeros_like(carry_ref)
    link_ref[...] = jnp.zeros_like(link_ref)
    for shift in range(1, context_size):

        @pl.when(context >= shift)
        def _(shift=shift):
            state_copy(shift).wait_recv()
            linked = jnp.ones((1, lanes), F32)
            follower = first_id
            factors = [jnp.ones((1, lanes), F32)] * head_count
            for near in range(shift):
                got = received.at[near]
                linked = (got[state_rows + 1 : state_rows + 2] == follower).astype(F32)
                follower = got[state_rows : state_rows + 1]
                factors = [factor * linked for factor in factors]
                if near < shift - 1:
                    factors = [
                        factor * got[state_rows + 8 + head : state_rows + 9 + head]
                        for head, factor in enumerate(factors)
                    ]
            if shift == 1:
                link_ref[0:1] = linked
            for head in range(head_count):
                rows = slice(head * lanes, (head + 1) * lanes)
                carry_ref[head] += factors[head] * received[shift - 1, rows]

    for shift in range(1, context_size):

        @pl.when(context + shift < context_size)
        def _(shift=shift):
            state_copy(shift).wait_send()

    for distance in range(chips):
        out_gather.arrive_from(distance)
    saves[1].start()

    def mix_save(index):
        rows = pl.ds(pl.multiple_of(index * row_tile, row_tile), row_tile)
        return pltpu.make_async_copy(mix.at[rows], mix_hbm.at[rows], mix_sem.at[index])

    def project(index, _):
        rows = pl.ds(pl.multiple_of(index * row_tile, row_tile), row_tile)
        for head in range(head_count):
            part = slice(head * lanes, (head + 1) * lanes)
            carried = mm_nt(lead[rows, part], carry_ref[head].astype(BF16))
            value = mixed[rows, part] + carried * (key_scale * keep_ref[rows])
            mixed[rows, part] = value
            gate = pre[rows, 3 * width + head * lanes : 3 * width + (head + 1) * lanes]
            unit = value * inverse_rms(value)
            gated[rows, part] = (
                unit * head_gain_ref[...] * (gate * jax.nn.sigmoid(gate))
            ).astype(BF16)
        left = gated[rows]

        def column_body(column, _):
            columns = pl.ds(pl.multiple_of(column * column_tile, column_tile), column_tile)
            mix[rows, columns] = mm_nt(left, out_full[columns, :]).astype(BF16)
            return 0

        lax.fori_loop(0, model_width // column_tile, column_body, 0)
        mix_save(index).start()
        return 0

    lax.fori_loop(0, tokens // row_tile, project, 0)
    saves[2].start()
    saves[5].start()
    gather.finish()
    out_gather.finish()
    for distance in range(chips):
        full_save(distance).wait()
    for save in saves:
        save.wait()
    for index in range(tokens // row_tile):
        pre_save(index).wait()
        mix_save(index).wait()


def forward(
    mesh_axes, collective, hidden, gain, shards, out_shard, down_shard, floor, segments, head_gain
):
    tokens, model_width = hidden.shape
    block, width = shards[0].shape
    lanes = head_gain.shape[1]
    head_count = width // lanes
    all_width = width * len(shards)
    blocks = tokens // BLOCK
    context_size = lax.axis_size("context")
    chips = lax.axis_size("shard") * context_size // 2
    messages = head_count * lanes + 8 + -(-head_count // 8) * 8
    whole = pl.BlockSpec(memory_space=pltpu.VMEM)
    remote = pl.BlockSpec(memory_space=pl.ANY)
    stored = [
        ((tokens, model_width), BF16),
        ((tokens, all_width), F32),
        ((model_width, all_width), BF16),
        ((model_width, width), BF16),
        ((tokens, width), F32),
        ((tokens, width), BF16),
        ((blocks, head_count, lanes, lanes), F32),
        ((tokens, width), BF16),
        ((tokens, model_width), BF16),
    ]
    kept = [
        (down_shard.shape[::-1], BF16),
        ((1, width), F32),
        ((tokens, 1), F32),
        ((tokens, 1), F32),
        ((blocks, 8, BLOCK), F32),
        ((blocks, 1, width), F32),
        ((head_count, lanes, lanes), F32),
        ((head_count, 1, lanes), F32),
        ((8, lanes), F32),
    ]
    return pl.pallas_call(
        partial(forward_kernel, mesh_axes, head_count, lanes ** (-0.5)),
        in_specs=[whole] * 2 + [remote] * 4 + [whole] * 5,
        out_specs=[remote] * len(stored) + [whole] * len(kept),
        out_shape=[jax.ShapeDtypeStruct(shape, kind) for shape, kind in stored + kept],
        scratch_shapes=[
            pltpu.VMEM((tokens, model_width), BF16),
            pltpu.VMEM((tokens, all_width), F32),
            pltpu.VMEM((block, all_width), BF16),
            pltpu.VMEM((block, width), BF16),
            pltpu.VMEM((model_width, all_width), BF16),
            pltpu.VMEM((model_width, width), BF16),
            pltpu.VMEM((tokens, width), F32),
            pltpu.VMEM((tokens, width), BF16),
            pltpu.VMEM((blocks, head_count, lanes, lanes), F32),
            pltpu.VMEM((tokens, width), BF16),
            pltpu.VMEM((tokens, model_width), BF16),
            pltpu.VMEM((head_count, lanes, lanes), F32),
            pltpu.VMEM((1, width), F32),
            pltpu.VMEM((messages, lanes), F32),
            pltpu.VMEM((context_size - 1, messages, lanes), F32),
            pltpu.SemaphoreType.DMA((4,)),
            pltpu.SemaphoreType.DMA((chips,)),
            pltpu.SemaphoreType.DMA((6,)),
            pltpu.SemaphoreType.DMA((tokens // 256,)),
            pltpu.SemaphoreType.DMA((tokens // 256,)),
            pltpu.SemaphoreType.DMA((context_size - 1,)),
            pltpu.SemaphoreType.DMA((context_size - 1,)),
        ]
        + gather_sems(1)
        + gather_sems(1),
        compiler_params=pltpu.CompilerParams(
            collective_id=collective, has_side_effects=True, vmem_limit_bytes=56 << 20
        ),
        cost_estimate=pl.CostEstimate(
            flops=2 * tokens * model_width * all_width,
            bytes_accessed=200_000_000,
            transcendentals=tokens * width * 9,
        ),
        name="forward",
    )(hidden, gain, *shards, out_shard, down_shard, floor, segments, head_gain)


def small_sum_kernel(
    mesh_axes, value, local_ref, total_ref, near, far, near_send, near_recv, far_send, far_recv
):
    shard_size, context_size = lax.axis_size("shard"), lax.axis_size("context")
    line_size = lax.axis_size("tensor")
    group = shard_size * context_size
    place = lax.axis_index("shard") * context_size + lax.axis_index("context")
    line_place = lax.axis_index("tensor")

    def device(position, line_position):
        places = {
            "shard": position // context_size,
            "context": lax.rem(position, context_size),
            "tensor": line_position,
        }
        return tuple(places[axis] for axis in mesh_axes)

    def near_target(step):
        return device(lax.rem(place + step, group), line_place)

    def far_target(step):
        return device(place, lax.rem(line_place + step, line_size))

    def near_copy(step):
        return pltpu.make_async_remote_copy(
            value,
            near.at[step - 1],
            near_send.at[step - 1],
            near_recv.at[step - 1],
            device_id=near_target(step),
            device_id_type=MESH_ID,
        )

    def far_copy(step):
        return pltpu.make_async_remote_copy(
            local_ref,
            far.at[step - 1],
            far_send.at[step - 1],
            far_recv.at[step - 1],
            device_id=far_target(step),
            device_id_type=MESH_ID,
        )

    barrier = pltpu.get_barrier_semaphore()
    for step in range(1, group):
        pl.semaphore_signal(barrier, inc=1, device_id=near_target(step), device_id_type=MESH_ID)
    for step in range(1, line_size):
        pl.semaphore_signal(barrier, inc=1, device_id=far_target(step), device_id_type=MESH_ID)
    pl.semaphore_wait(barrier, group + line_size - 2)
    for step in range(1, group):
        near_copy(step).start()
    total = value[...]
    for step in range(1, group):
        near_copy(step).wait_recv()
        total = total + near[step - 1]
    local_ref[...] = total
    for step in range(1, line_size):
        far_copy(step).start()
    for step in range(1, line_size):
        far_copy(step).wait_recv()
        total = total + far[step - 1]
    total_ref[...] = total
    for step in range(1, group):
        near_copy(step).wait_send()
    for step in range(1, line_size):
        far_copy(step).wait_send()


def small_sum(mesh_axes, collective, values):
    flat = jnp.concatenate([value.reshape(-1) for value in values])
    lanes = -(-flat.shape[0] // 1024) * 128
    flat = jnp.pad(flat, (0, 8 * lanes - flat.shape[0])).reshape(8, lanes)
    group = lax.axis_size("shard") * lax.axis_size("context")
    line_size = lax.axis_size("tensor")
    whole = pl.BlockSpec(memory_space=pltpu.VMEM)
    local, total = pl.pallas_call(
        partial(small_sum_kernel, mesh_axes),
        in_specs=[whole],
        out_specs=[whole] * 2,
        out_shape=[jax.ShapeDtypeStruct((8, lanes), F32)] * 2,
        scratch_shapes=[
            pltpu.VMEM((group - 1, 8, lanes), F32),
            pltpu.VMEM((line_size - 1, 8, lanes), F32),
            pltpu.SemaphoreType.DMA((group - 1,)),
            pltpu.SemaphoreType.DMA((group - 1,)),
            pltpu.SemaphoreType.DMA((line_size - 1,)),
            pltpu.SemaphoreType.DMA((line_size - 1,)),
        ],
        compiler_params=pltpu.CompilerParams(collective_id=collective, has_side_effects=True),
        cost_estimate=pl.CostEstimate(
            flops=8 * lanes * group, bytes_accessed=20_000_000, transcendentals=0
        ),
        name="small_sum",
    )(flat)
    return local.reshape(-1), total.reshape(-1)


def local(
    mesh_axes,
    hidden,
    segment_ids,
    norm1_gain,
    w_query,
    w_forget,
    w_input,
    w_gate_out,
    forget_floor,
    head_gain,
    w_out,
    norm2_gain,
    w_ffn_gate,
    w_ffn_up,
    w_ffn_down,
    out_grad,
):
    sequences, span_len, model_width = hidden.shape
    tokens = sequences * span_len
    head_count, key_dim = forget_floor.shape
    width = head_count * key_dim
    key_scale = key_dim ** (-0.5)
    both = ("shard", "context")
    gain_one, gain_two = norm1_gain.reshape(1, -1), norm2_gain.reshape(1, -1)
    hidden_rows = hidden.reshape(tokens, model_width)
    gain_row = head_gain.reshape(1, -1)
    segments = segment_ids.reshape(tokens // BLOCK, BLOCK).astype(F32)
    (
        normed_one,
        pre,
        mixer_full,
        out_full,
        mixed,
        lead,
        starts,
        gated_low,
        mix_part,
        down_turned,
        open_part,
        counts,
        keep,
        flags,
        runs,
        carry,
        decay,
        link,
    ) = forward(
        mesh_axes,
        4,
        hidden_rows,
        gain_one,
        (w_query, w_forget, w_input, w_gate_out),
        w_out,
        w_ffn_down,
        forget_floor,
        segments,
        gain_row,
    )
    grad_rows = out_grad.reshape(tokens, model_width)
    (
        _,
        grad_mix_low,
        grad_norm_two,
        residual,
        _,
        _,
        _,
        feed_part,
        grad_residual,
        grads_ffn,
    ) = middle(
        mesh_axes,
        2,
        mix_part,
        grad_rows,
        hidden_rows,
        gain_two,
        w_ffn_gate,
        w_ffn_up,
        down_turned,
    )
    (
        output_rows,
        grad_head_part,
        grad_floor_part,
        back_one,
        grad_out,
        grad_mixer,
    ) = output_line(
        mesh_axes,
        1,
        (
            feed_part,
            residual,
            gated_low,
            grad_mix_low,
            out_full,
            mixed,
            lead,
            starts,
            runs,
            carry,
            decay,
            link,
            open_part,
            counts,
            keep,
            flags,
            gain_row,
        ),
        (normed_one, pre, mixer_full),
        head_count,
    )
    input_rows, grad_norm_one, share_gate, share_up, share_down = input_line(
        mesh_axes, 3, back_one, hidden_rows, grad_residual, gain_one, grads_ffn
    )
    near, total = small_sum(
        mesh_axes, 5, (grad_norm_one, grad_norm_two, grad_head_part, grad_floor_part)
    )
    shares = lax.axis_size("shard") * lax.axis_size("context")
    position = lax.axis_index("shard") * lax.axis_size("context") + lax.axis_index("context")

    def own_slice(values, first, length):
        values = values[first : first + length].reshape(shares, length // shares)
        return lax.dynamic_index_in_dim(values, position, 0, False)

    floor_total = near[2 * model_width + key_dim : 2 * model_width + key_dim + width]
    floor_total = floor_total.reshape(head_count, shares, key_dim // shares)

    def share(values, dim):
        return lax.psum_scatter(
            values.astype(BF16), both, scatter_dimension=dim, tiled=True
        ).astype(F32)

    share_mixer = share(grad_mixer, 0)
    return (
        output_rows.reshape(hidden.shape),
        input_rows.reshape(hidden.shape),
        own_slice(total, 0, model_width),
        share_mixer[:, :width],
        share_mixer[:, width : 2 * width],
        share_mixer[:, 2 * width : 3 * width],
        share_mixer[:, 3 * width :],
        lax.dynamic_index_in_dim(floor_total, position, 1, False),
        own_slice(total, 2 * model_width, key_dim),
        share(grad_out, 0).T,
        own_slice(total, model_width, model_width),
        share_gate,
        share_up,
        share_down.T,
    )


def solution(mesh):
    in_specs = (
        P("shard", "context", None),
        P("shard", "context"),
        P(),
        P(("shard", "context"), "tensor"),
        P(("shard", "context"), "tensor"),
        P(("shard", "context"), "tensor"),
        P(("shard", "context"), "tensor"),
        P("tensor", None),
        P(),
        P("tensor", ("shard", "context")),
        P(),
        P(("shard", "context"), "tensor"),
        P(("shard", "context"), "tensor"),
        P("tensor", ("shard", "context")),
        P("shard", "context", None),
    )
    out_specs = (
        P("shard", "context", None),
        P("shard", "context", None),
        P(("shard", "context")),
        P(("shard", "context"), "tensor"),
        P(("shard", "context"), "tensor"),
        P(("shard", "context"), "tensor"),
        P(("shard", "context"), "tensor"),
        P("tensor", ("shard", "context")),
        P(("shard", "context")),
        P("tensor", ("shard", "context")),
        P(("shard", "context")),
        P(("shard", "context"), "tensor"),
        P(("shard", "context"), "tensor"),
        P("tensor", ("shard", "context")),
    )
    return jax.shard_map(
        partial(local, mesh.axis_names), mesh=mesh, in_specs=in_specs, out_specs=out_specs, check_vma=False)
```

```python
from functools import partial

import jax
import jax.numpy as jnp
from jax import lax
from jax.experimental import pallas as pl
from jax.experimental.pallas import tpu as pltpu
from jax.sharding import PartitionSpec as P

EPSILON = 1e-05


BLOCK = 128
F32 = jnp.float32
BF16 = jnp.bfloat16


def mm(a, b, dims):
    return lax.dot_general(a, b, (dims, ((), ())), preferred_element_type=F32)


def mm_nn(a, b):
    return mm(a, b, ((1,), (0,)))


def mm_nt(a, b):
    return mm(a, b, ((1,), (1,)))


def mm_tn(a, b):
    return mm(a, b, ((0,), (0,)))


def split_sum(tri, values):
    high = values.astype(BF16)
    low = (values - high.astype(F32)).astype(BF16)
    return mm_nn(tri, high) + mm_nn(tri, low)


def block_masks(counts, flags_row):
    rows = counts.shape[0]
    row_ids = lax.broadcasted_iota(jnp.int32, (rows, rows), 0)
    col_ids = lax.broadcasted_iota(jnp.int32, (rows, rows), 1)
    linked = jnp.logical_and(counts == flags_row[0:1], row_ids >= col_ids)
    fresh = (counts == flags_row[1:2, 0:1]).astype(F32)
    tail = (counts == flags_row[2:3, 0:1]).astype(F32)
    closing = (flags_row[1:2, 0:1] == flags_row[2:3, 0:1]).astype(F32)
    return row_ids, col_ids, linked, fresh, tail, closing


CHUNK = 32
LAG = 2
MESH_ID = pl.DeviceIdType.MESH


class Line:
    def __init__(self, mesh_axes, part, arrived, out, sems, transform):
        self.mesh_axes = mesh_axes
        self.part, self.arrived, self.out = part, arrived, out
        self.sum_send, self.sum_recv, self.back_send, self.back_recv = sems
        self.transform = transform
        self.half = part.shape[0] // 2
        self.chunks = self.half // CHUNK
        self.size = lax.axis_size("tensor")
        self.place = lax.axis_index("tensor")
        self.lines = ((self.size - 1 - self.place, -1), (self.place, 1))
        self.steps = self.chunks + 2 * LAG * (self.size - 1)

    def device(self, position):
        return tuple(
            jnp.clip(position, 0, self.size - 1) if axis == "tensor" else lax.axis_index(axis)
            for axis in self.mesh_axes
        )

    def greet(self, barrier):
        for step in (-1, 1):
            inside = jnp.logical_and(self.place + step >= 0, self.place + step < self.size)

            @pl.when(inside)
            def _(step=step):
                pl.semaphore_signal(
                    barrier, inc=1, device_id=self.device(self.place + step), device_id_type=MESH_ID
                )

        at_end = jnp.logical_or(self.place == 0, self.place == self.size - 1)
        return jnp.where(at_end, 1, 2)

    def rows_of(self, side, index):
        return pl.ds(pl.multiple_of(side * self.half + index * CHUNK, CHUNK), CHUNK)

    def sum_copy(self, side, index, source):
        rows = self.rows_of(side, index)
        return pltpu.make_async_remote_copy(
            source.at[rows],
            self.arrived.at[rows],
            self.sum_send.at[side, index],
            self.sum_recv.at[side, index],
            device_id=self.device(self.place + self.lines[side][1]),
            device_id_type=MESH_ID,
        )

    def back_copy(self, side, index):
        rows = self.rows_of(side, index)
        return pltpu.make_async_remote_copy(
            self.out.at[rows],
            self.out.at[rows],
            self.back_send.at[side, index],
            self.back_recv.at[side, index],
            device_id=self.device(self.place - self.lines[side][1]),
            device_id_type=MESH_ID,
        )

    def step(self, time):
        for side in (0, 1):
            hops = self.lines[side][0]
            index = time - LAG * hops
            valid = jnp.logical_and(index >= 0, index < self.chunks)
            at_source, at_owner = hops == 0, hops == self.size - 1
            index = jnp.clip(index, 0, self.chunks - 1)
            rows = self.rows_of(side, index)

            @pl.when(jnp.logical_and(valid, at_source))
            def _(side=side, index=index):
                self.sum_copy(side, index, self.part).start()

            @pl.when(jnp.logical_and(valid, jnp.logical_not(at_source)))
            def _(side=side, index=index):
                self.sum_copy(side, index, self.arrived).wait_recv()

            between = jnp.logical_and(jnp.logical_not(at_source), jnp.logical_not(at_owner))

            @pl.when(jnp.logical_and(valid, between))
            def _(side=side, index=index, rows=rows):
                total = self.part[rows].astype(F32) + self.arrived[rows].astype(F32)
                self.arrived[rows] = total.astype(BF16)
                self.sum_copy(side, index, self.arrived).start()

            @pl.when(jnp.logical_and(valid, at_owner))
            def _(side=side, index=index, rows=rows):
                total = self.part[rows].astype(F32) + self.arrived[rows].astype(F32)
                own = pl.ds(pl.multiple_of(index * CHUNK, CHUNK), CHUNK)
                self.transform(total, rows, own)
                self.back_copy(side, index).start()

            away = self.size - 1 - hops
            index = time - LAG * (self.size - 1 + away)
            valid = jnp.logical_and(jnp.logical_and(index >= 0, index < self.chunks), away > 0)
            index = jnp.clip(index, 0, self.chunks - 1)

            @pl.when(valid)
            def _(side=side, index=index):
                self.back_copy(side, index).wait_recv()

            @pl.when(jnp.logical_and(valid, away < self.size - 1))
            def _(side=side, index=index):
                self.back_copy(side, index).start()

    def run(self, first, last, beside=None):
        def body(time, _):
            self.step(time)
            if beside is not None:
                beside(time)
            return 0

        lax.fori_loop(first, last, body, 0)

    def source_sent(self, first, last):
        def body(index, _):
            for side in (0, 1):

                @pl.when(self.lines[side][0] == 0)
                def _(side=side):
                    self.sum_copy(side, index, self.part).wait_send()

            return 0

        lax.fori_loop(first, last, body, 0)

    def finish(self, source_waits=True):
        def body(index, _):
            for side in (0, 1):
                hops = self.lines[side][0]
                passed = hops < self.size - 1
                if not source_waits:
                    passed = jnp.logical_and(passed, hops > 0)

                @pl.when(passed)
                def _(side=side):
                    self.sum_copy(side, index, self.arrived).wait_send()

                @pl.when(hops > 0)
                def _(side=side):
                    self.back_copy(side, index).wait_send()

            return 0

        lax.fori_loop(0, self.chunks, body, 0)


def line_sems(tokens):
    return [pltpu.SemaphoreType.DMA((2, tokens // 2 // CHUNK))] * 4


def inverse_rms(values):
    return lax.rsqrt(jnp.mean(values * values, axis=-1, keepdims=True) + EPSILON)


class Plane:
    def __init__(self, mesh_axes):
        self.mesh_axes = mesh_axes
        self.context = lax.axis_size("context")
        self.per_row = self.context // 2
        self.chips = lax.axis_size("shard") * self.per_row
        context_place = lax.axis_index("context")
        self.core = lax.rem(context_place, 2)
        self.chip = lax.axis_index("shard") * self.per_row + context_place // 2

    def device(self, chip, core):
        places = {
            "shard": chip // self.per_row,
            "context": 2 * lax.rem(chip, self.per_row) + core,
            "tensor": lax.axis_index("tensor"),
        }
        return tuple(places[axis] for axis in self.mesh_axes)

    def ahead(self, distance):
        return lax.rem(self.chip + distance, self.chips)

    def greet(self, barrier):
        targets = [self.device(self.chip, 1 - self.core)]
        targets += [self.device(self.ahead(step), self.core) for step in range(1, self.chips)]
        for target in targets:
            pl.semaphore_signal(barrier, inc=1, device_id=target, device_id_type=MESH_ID)
        return len(targets)


class Gather:
    def __init__(self, plane, sources, targets, sems):
        self.plane, self.sources, self.targets = plane, sources, targets
        self.load_sem, self.send_sem, self.recv_sem, self.pair_send, self.pair_recv = sems
        self.block = sources[0].shape[0]
        self.part = self.block // 2
        self.relayed = plane.chips == 4
        self.arrays = range(len(sources))

    def partner(self, distance):
        return jnp.bitwise_xor(self.plane.chip, distance)

    def greet(self, barrier):
        plane = self.plane
        targets = [plane.device(plane.chip, 1 - plane.core)]
        targets += [
            plane.device(self.partner(step), plane.core)
            for step in range(1, 3 if self.relayed else plane.chips)
        ]
        for target in targets:
            pl.semaphore_signal(barrier, inc=1, device_id=target, device_id_type=MESH_ID)
        return len(targets)

    def place(self, array, chip, core, half):
        first = (2 * chip + core) * self.block + half * self.part
        rows = pl.ds(pl.multiple_of(first, self.part), self.part)
        return self.targets[array].at[rows, pl.ds(0, self.sources[array].shape[1])]

    def mine(self, array, half):
        return self.sources[array].at[pl.ds(half * self.part, self.part)]

    def loads(self):
        plane = self.plane
        return [
            pltpu.make_async_copy(
                self.mine(array, half),
                self.place(array, plane.chip, plane.core, half),
                self.load_sem.at[array, half],
            )
            for array in self.arrays
            for half in range(2)
        ]

    def send(self, distance, half):
        plane = self.plane
        copies = []
        for array in self.arrays:
            chip, target = plane.chip, self.partner(distance)
            source = self.mine(array, half)
            if self.relayed and distance == 3:
                chip = self.partner(2 if half == 0 else 1)
                target = self.partner(1 if half == 0 else 2)
                source = self.place(array, chip, plane.core, half)
            copies.append(
                pltpu.make_async_remote_copy(
                    source,
                    self.place(array, chip, plane.core, half),
                    self.send_sem.at[array, distance - 1, half],
                    self.recv_sem.at[array, distance - 1, half],
                    device_id=plane.device(target, plane.core),
                    device_id_type=MESH_ID,
                )
            )
        return copies

    def forward(self, distance, half):
        plane = self.plane
        copies = []
        for array in self.arrays:
            place = self.place(array, self.partner(distance), plane.core, half)
            copies.append(
                pltpu.make_async_remote_copy(
                    self.mine(array, half) if distance == 0 else place,
                    place,
                    self.pair_send.at[array, distance, half],
                    self.pair_recv.at[array, distance, half],
                    device_id=plane.device(plane.chip, 1 - plane.core),
                    device_id_type=MESH_ID,
                )
            )
        return copies

    def start(self):
        if self.relayed:
            order = ((1, 1), (2, 0), (1, 0), (2, 1))
        else:
            order = [(step, half) for step in range(1, self.plane.chips) for half in range(2)]
        for distance, half in order:
            for copy in self.send(distance, half):
                copy.start()
        for copy in self.loads():
            copy.start()
        for half in range(2):
            for copy in self.forward(0, half):
                copy.start()

    def take(self, distance, half, relay):
        for copy in self.send(distance, half):
            copy.wait_recv()
        if relay:
            for copy in self.send(3, half):
                copy.start()
        for copy in self.forward(distance, half):
            copy.start()

    def stage(self, number):
        if self.relayed:
            if number == 0:
                self.take(1, 1, True)
                self.take(2, 0, True)
            elif number == 1:
                self.take(1, 0, False)
                self.take(2, 1, False)
            else:
                self.take(3, 0, False)
                self.take(3, 1, False)
        elif number == 2:
            for distance in range(1, self.plane.chips):
                for half in range(2):
                    self.take(distance, half, False)

    def arrive_from(self, distance):
        if distance == 0:
            for copy in self.loads():
                copy.wait()
        for half in range(2):
            for copy in self.forward(distance, half):
                copy.wait_recv()

    def arrive(self):
        for distance in range(self.plane.chips):
            self.arrive_from(distance)

    def finish(self):
        for distance in range(self.plane.chips):
            for half in range(2):
                for copy in self.forward(distance, half):
                    copy.wait_send()
                if distance > 0:
                    for copy in self.send(distance, half):
                        copy.wait_send()


def gather_sems(arrays):
    chips = lax.axis_size("shard") * lax.axis_size("context") // 2
    return [
        pltpu.SemaphoreType.DMA((arrays, 2)),
        pltpu.SemaphoreType.DMA((arrays, chips - 1, 2)),
        pltpu.SemaphoreType.DMA((arrays, chips - 1, 2)),
        pltpu.SemaphoreType.DMA((arrays, chips, 2)),
        pltpu.SemaphoreType.DMA((arrays, chips, 2)),
    ]


GROUP = 128
TILE = 256
WIDE = 512


def middle_kernel(
    mesh_axes,
    mix_hbm,
    cotangent_ref,
    input_hbm,
    gain_ref,
    gate_hbm,
    up_hbm,
    down_hbm,
    normed_ref,
    out_ref,
    gain_grad,
    residual_hbm,
    hidden_hbm,
    grad_gate_hbm,
    grad_up_hbm,
    feed_hbm,
    grad_hbm,
    grads_hbm,
    gate_w,
    up_w,
    down_w,
    part,
    mix_arrived,
    arrived,
    inputs,
    residual,
    stage_hidden,
    stage_gate,
    stage_up,
    stage_feed,
    part_sem,
    input_sem,
    save_sem,
    stage_sem,
    grad_sem,
    back_sem,
    tile_sem,
    *sems,
):
    tokens, model_width = normed_ref.shape
    half = tokens // 2
    hidden_width = gate_hbm.shape[1]
    padded = gate_w.shape[1]
    groups = half // GROUP
    place, line_size = lax.axis_index("tensor"), lax.axis_size("tensor")
    own_half = pl.ds(pl.multiple_of(jnp.where(place == 0, 0, half), half), half)
    part_load = pltpu.make_async_copy(mix_hbm, part, part_sem.at[0])
    part_load.start()
    input_load = pltpu.make_async_copy(input_hbm.at[own_half], inputs, input_sem.at[0])
    input_load.start()
    if padded > hidden_width:
        spare = slice(hidden_width, padded)
        gate_w[:, spare] = jnp.zeros((model_width, padded - hidden_width), BF16)
        up_w[:, spare] = jnp.zeros((model_width, padded - hidden_width), BF16)
        down_w[:, spare] = jnp.zeros((model_width, padded - hidden_width), BF16)
    gain_grad[...] = jnp.zeros_like(gain_grad)

    def mix_turn(total, rows, own):
        values = inputs[own].astype(F32) + total
        residual[own] = values
        normed_ref[rows] = (values * inverse_rms(values) * gain_ref[...]).astype(BF16)

    def turn(total, rows, own):
        values = residual[own]
        inverse = inverse_rms(values)
        unit = values * inverse
        gain_grad[...] += jnp.sum(total * unit, axis=0, keepdims=True)
        lifted = total * gain_ref[...]
        mean = jnp.mean(lifted * unit, axis=-1, keepdims=True)
        grad = cotangent_ref[rows].astype(F32) + inverse * (lifted - unit * mean)
        residual[own] = grad
        out_ref[rows] = grad.astype(BF16)

    mix_line = Line(mesh_axes, part, mix_arrived, normed_ref, sems[:4], mix_turn)
    line = Line(mesh_axes, part, arrived, out_ref, sems[4:8], turn)
    gather = Gather(
        Plane(mesh_axes), (gate_hbm, up_hbm, down_hbm), (gate_w, up_w, down_w), sems[8:]
    )
    barrier = pltpu.get_barrier_semaphore()
    expected = mix_line.greet(barrier) + gather.greet(barrier)
    pl.semaphore_wait(barrier, expected)
    gather.start()
    part_load.wait()
    input_load.wait()
    pace = GROUP // CHUNK
    begin = pace + 2 * LAG * (line_size - 1) + 4
    mix_line.run(0, begin - 10)
    gather.stage(0)
    mix_line.run(begin - 10, begin - 4)
    gather.stage(1)
    mix_line.run(begin - 4, begin)
    gather.stage(2)
    gather.arrive()

    def both(ref, group):
        first = pl.ds(pl.multiple_of(group * GROUP, GROUP), GROUP)
        second = pl.ds(pl.multiple_of(half + group * GROUP, GROUP), GROUP)
        return first, second

    def stage_copies(group):
        slot = lax.rem(group, 2)
        copies = []
        for side, rows in enumerate(both(None, group)):
            from_rows = pl.ds(side * GROUP, GROUP)
            columns = pl.ds(0, hidden_width)
            for which, (stage, target) in enumerate(
                (
                    (stage_hidden, hidden_hbm),
                    (stage_gate, grad_gate_hbm),
                    (stage_up, grad_up_hbm),
                )
            ):
                copies.append(
                    pltpu.make_async_copy(
                        stage.at[slot, from_rows, columns],
                        target.at[rows],
                        stage_sem.at[slot, which, side],
                    )
                )
            copies.append(
                pltpu.make_async_copy(
                    stage_feed.at[slot, from_rows], feed_hbm.at[rows], stage_sem.at[slot, 3, side]
                )
            )
        return copies

    def hidden_tile(group, tile):
        first, second = both(normed_ref, group)
        slot = lax.rem(group, 2)
        columns = pl.ds(pl.multiple_of(tile * WIDE, WIDE), WIDE)
        rows = jnp.concatenate([normed_ref[first], normed_ref[second]], axis=0)
        gate = mm_nn(rows, gate_w[:, columns])
        up = mm_nn(rows, up_w[:, columns])
        grads = jnp.concatenate([cotangent_ref[first], cotangent_ref[second]], axis=0)
        grad = mm_nn(grads, down_w[:, columns])
        sigma = jax.nn.sigmoid(gate)
        active = gate * sigma
        stage_hidden[slot, :, columns] = (active * up).astype(BF16)
        stage_gate[slot, :, columns] = (grad * up * sigma * (1.0 + gate * (1.0 - sigma))).astype(
            BF16
        )
        stage_up[slot, :, columns] = (grad * active).astype(BF16)

    def model_tile(group, tile):
        first, second = both(part, group)
        slot = lax.rem(group, 2)
        columns = pl.ds(pl.multiple_of(tile * WIDE, WIDE), WIDE)
        back = mm_nt(stage_gate[slot], gate_w[columns, :])
        back = (back + mm_nt(stage_up[slot], up_w[columns, :])).astype(BF16)
        part[first, columns] = back[:GROUP]
        part[second, columns] = back[GROUP:]
        stage_feed[slot, :, columns] = mm_nt(stage_hidden[slot], down_w[columns, :]).astype(BF16)

    hidden_tiles, model_tiles = padded // WIDE, model_width // WIDE
    ticks = hidden_tiles + model_tiles
    piece = -(-ticks // pace)
    save = pltpu.make_async_copy(residual, residual_hbm, save_sem.at[0])

    def group_body(group, _):
        mix_line.source_sent(group * pace, (group + 1) * pace)

        @pl.when(group == 1)
        def _():
            save.start()

        @pl.when(group == 2)
        def _():
            save.wait()

        @pl.when(group >= 2)
        def _():
            for copy in stage_copies(group - 2):
                copy.wait()

        def piece_body(index, _):
            def tick_body(offset, _):
                tick = index * piece + offset

                @pl.when(tick < hidden_tiles)
                def _():
                    hidden_tile(group, tick)

                @pl.when(jnp.logical_and(tick >= hidden_tiles, tick < ticks))
                def _():
                    model_tile(group, tick - hidden_tiles)

                return 0

            lax.fori_loop(0, piece, tick_body, 0)

            mix_time = begin + group * pace + index

            @pl.when(mix_time < mix_line.steps)
            def _():
                mix_line.step(mix_time)

            @pl.when(group >= 1)
            def _():
                line.step((group - 1) * pace + index)

            return 0

        lax.fori_loop(0, pace, piece_body, 0)
        for copy in stage_copies(group):
            copy.start()
        return 0

    lax.fori_loop(0, groups, group_body, 0)
    for group in range(max(groups - 2, 0), groups):
        for copy in stage_copies(group):
            copy.wait()
    gather.finish()

    token_rows, hidden_columns = pl.ds(0, tokens), pl.ds(0, hidden_width)
    returned = [
        pltpu.make_async_copy(
            source, target.at[token_rows, hidden_columns], back_sem.at[which]
        )
        for which, (source, target) in enumerate(
            ((grad_gate_hbm, gate_w), (grad_up_hbm, up_w), (hidden_hbm, down_w))
        )
    ]
    for copy in returned:
        copy.start()
    tiles = model_width // TILE
    first_time = (groups - 1) * pace + 1
    stages = (stage_gate, stage_up, stage_hidden)

    def tile_copies(tile):
        rows = pl.ds(pl.multiple_of(tile * TILE, TILE), TILE)
        slot = lax.rem(tile, 2)
        return [
            pltpu.make_async_copy(
                stage.at[slot, pl.ds(0, TILE), hidden_columns],
                grads_hbm.at[rows, pl.ds(which * hidden_width, hidden_width)],
                tile_sem.at[slot, which],
            )
            for which, stage in enumerate(stages)
        ]

    def weight_tile(time):
        tile = time - first_time

        @pl.when(tile == 0)
        def _():
            for copy in returned:
                copy.wait()

        @pl.when(jnp.logical_and(tile >= 2, tile < tiles))
        def _():
            for copy in tile_copies(tile - 2):
                copy.wait()

        @pl.when(jnp.logical_and(tile >= 0, tile < tiles))
        def _():
            slot = lax.rem(tile, 2)
            columns = pl.ds(pl.multiple_of(tile * TILE, TILE), TILE)
            rows = normed_ref[:, columns]
            for source, right, stage in (
                (rows, gate_w, stage_gate),
                (rows, up_w, stage_up),
                (cotangent_ref[:, columns], down_w, stage_hidden),
            ):
                product = mm_tn(source, right[:tokens, :hidden_width])
                stage[slot, :TILE, :hidden_width] = product.astype(BF16)
            for copy in tile_copies(tile):
                copy.start()

    line.run((groups - 1) * pace, line.steps, weight_tile)
    grad_save = pltpu.make_async_copy(residual, grad_hbm, grad_sem.at[0])
    grad_save.start()
    for tile in range(max(tiles - 2, 0), tiles):
        for copy in tile_copies(tile):
            copy.wait()
    mix_line.finish(source_waits=False)
    line.finish()
    grad_save.wait()


def middle(mesh_axes, collective, mix, cotangent, inputs, gain, gate_w, up_w, down_w):
    tokens, model_width = mix.shape
    hidden_width = gate_w.shape[1]
    padded = -(-hidden_width // WIDE) * WIDE
    whole = pl.BlockSpec(memory_space=pltpu.VMEM)
    remote = pl.BlockSpec(memory_space=pl.ANY)
    group_rows = 2 * GROUP
    return pl.pallas_call(
        partial(middle_kernel, mesh_axes),
        in_specs=[remote, whole, remote, whole, remote, remote, remote],
        out_specs=[whole, whole, whole] + [remote] * 7,
        out_shape=[
            jax.ShapeDtypeStruct((tokens, model_width), BF16),
            jax.ShapeDtypeStruct((tokens, model_width), BF16),
            jax.ShapeDtypeStruct((1, model_width), F32),
            jax.ShapeDtypeStruct((tokens // 2, model_width), F32),
            jax.ShapeDtypeStruct((tokens, hidden_width), BF16),
            jax.ShapeDtypeStruct((tokens, hidden_width), BF16),
            jax.ShapeDtypeStruct((tokens, hidden_width), BF16),
            jax.ShapeDtypeStruct((tokens, model_width), BF16),
            jax.ShapeDtypeStruct((tokens // 2, model_width), F32),
            jax.ShapeDtypeStruct((model_width, 3 * hidden_width), BF16),
        ],
        scratch_shapes=[
            pltpu.VMEM((model_width, padded), BF16),
            pltpu.VMEM((model_width, padded), BF16),
            pltpu.VMEM((model_width, padded), BF16),
            pltpu.VMEM((tokens, model_width), BF16),
            pltpu.VMEM((tokens, model_width), BF16),
            pltpu.VMEM((tokens, model_width), BF16),
            pltpu.VMEM((tokens // 2, model_width), BF16),
            pltpu.VMEM((tokens // 2, model_width), F32),
            pltpu.VMEM((2, group_rows, padded), BF16),
            pltpu.VMEM((2, group_rows, padded), BF16),
            pltpu.VMEM((2, group_rows, padded), BF16),
            pltpu.VMEM((2, group_rows, model_width), BF16),
            pltpu.SemaphoreType.DMA((1,)),
            pltpu.SemaphoreType.DMA((1,)),
            pltpu.SemaphoreType.DMA((1,)),
            pltpu.SemaphoreType.DMA((2, 4, 2)),
            pltpu.SemaphoreType.DMA((1,)),
            pltpu.SemaphoreType.DMA((3,)),
            pltpu.SemaphoreType.DMA((2, 3)),
        ]
        + line_sems(tokens)
        + line_sems(tokens)
        + gather_sems(3),
        compiler_params=pltpu.CompilerParams(
            collective_id=collective, has_side_effects=True, vmem_limit_bytes=61 << 20
        ),
        cost_estimate=pl.CostEstimate(
            flops=tokens * model_width * hidden_width * 12,
            bytes_accessed=360_000_000,
            transcendentals=tokens * hidden_width,
        ),
        name="middle",
    )(mix, cotangent, inputs, gain, gate_w, up_w, down_w)


def output_kernel(
    mesh_axes,
    head_count,
    key_scale,
    part,
    residual,
    gated_ref,
    mix_grad_ref,
    out_full,
    mixed_ref,
    lead_ref,
    starts_ref,
    run_ref,
    carry_ref,
    decay_ref,
    link_ref,
    open_ref,
    count_ref,
    keep_ref,
    flags_ref,
    gain_ref,
    normed_hbm,
    pre_hbm,
    full_hbm,
    out_ref,
    gain_grad,
    floor_grad,
    back_ref,
    mixer_grads_hbm,
    arrived,
    left,
    right,
    full,
    mixer_stage,
    gates,
    pre,
    grad_mixed,
    back_scr,
    message,
    received,
    grad_scr,
    lifted_scr,
    lowered_scr,
    moved_scr,
    value_scr,
    load_sem,
    pre_sem,
    stage_sem,
    grad_send,
    grad_recv,
    *sems,
):
    tokens, model_width = left.shape
    width = gated_ref.shape[1]
    lanes = width // head_count
    state_rows = head_count * lanes
    tiles, blocks = model_width // TILE, tokens // BLOCK
    piece_rows = 2 * BLOCK
    context, context_size = lax.axis_index("context"), lax.axis_size("context")

    left_load = pltpu.make_async_copy(normed_hbm, left, load_sem.at[0])
    full_load = pltpu.make_async_copy(full_hbm, full, load_sem.at[1])
    gate_load = pltpu.make_async_copy(
        pre_hbm.at[:, pl.ds(3 * width, width)], gates, load_sem.at[2]
    )
    for load in (gate_load, left_load, full_load):
        load.start()
    gain_grad[...] = jnp.zeros_like(gain_grad)
    floor_grad[...] = jnp.zeros_like(floor_grad)
    back_scr[...] = jnp.zeros_like(back_scr)

    def turn(total, rows, own):
        out_ref[rows] = (residual[own] + total).astype(BF16)

    def earlier(shift):
        places = {axis: lax.axis_index(axis) for axis in mesh_axes}
        places["context"] = lax.rem(context + context_size - shift, context_size)
        return tuple(places[axis] for axis in mesh_axes)

    line = Line(mesh_axes, part, arrived, out_ref, sems, turn)
    barrier = pltpu.get_barrier_semaphore()
    expected = line.greet(barrier)
    for shift in range(1, context_size):
        pl.semaphore_signal(barrier, inc=1, device_id=earlier(shift), device_id_type=MESH_ID)
    pl.semaphore_wait(barrier, expected + context_size - 1)
    gate_load.wait()

    def tile_columns(tile):
        return pl.ds(pl.multiple_of(tile * TILE, TILE), TILE)

    def stage_copy(tile):
        rows = tile_columns(tile)
        return pltpu.make_async_copy(mixer_stage, mixer_grads_hbm.at[rows], stage_sem.at[0])

    def gate_piece(index):
        rows = pl.ds(pl.multiple_of(index * piece_rows, piece_rows), piece_rows)
        grads = mm_nn(mix_grad_ref[rows], out_full[...])
        gain = gain_ref[...]
        total = jnp.zeros_like(gain)
        for head in range(head_count):
            part_of = slice(head * lanes, (head + 1) * lanes)
            mixed, gate, grad = mixed_ref[rows, part_of], gates[rows, part_of], grads[:, part_of]
            inverse = inverse_rms(mixed)
            unit = mixed * inverse
            sigma = jax.nn.sigmoid(gate)
            scaled = grad * unit
            total = total + jnp.sum(scaled * (gate * sigma), axis=0, keepdims=True)
            grad_gate = scaled * gain * sigma * (1.0 + gate * (1.0 - sigma))
            first = 3 * width + head * lanes
            right[rows, first : first + lanes] = grad_gate.astype(BF16)
            lifted = grad * gain * (gate * sigma)
            mean = jnp.mean(lifted * unit, axis=-1, keepdims=True)
            grad_in = inverse * (lifted - unit * mean) * (key_scale * keep_ref[rows])
            grad_in = grad_in.astype(BF16)
            grad_mixed[rows, part_of] = grad_in
            back_scr[head] += mm_tn(grad_in, lead_ref[rows, part_of])
        gain_grad[...] += total

    def state_copy(shift):
        return pltpu.make_async_remote_copy(
            message,
            received.at[shift - 1],
            grad_send.at[shift - 1],
            grad_recv.at[shift - 1],
            device_id=earlier(shift),
            device_id_type=MESH_ID,
        )

    def block_of(index):
        return blocks - 1 - index

    def pre_load(index):
        rows = pl.ds(pl.multiple_of(block_of(index) * BLOCK, BLOCK), BLOCK)
        slot = lax.rem(index, 2)
        return pltpu.make_async_copy(
            pre_hbm.at[rows, pl.ds(0, 3 * width)], pre.at[slot], pre_sem.at[slot]
        )

    def send_back():
        for head in range(head_count):
            rows = slice(head * lanes, (head + 1) * lanes)
            message[rows] = back_scr[head] * link_ref[0:1]
            message[state_rows + head : state_rows + head + 1] = decay_ref[head] * link_ref[0:1]
        for shift in range(1, context_size):

            @pl.when(context >= shift)
            def _(shift=shift):
                state_copy(shift).start()

        pre_load(0).start()

    def take_back():
        grad_scr[...] = jnp.zeros_like(grad_scr)
        for shift in range(1, context_size):

            @pl.when(context + shift < context_size)
            def _(shift=shift):
                state_copy(shift).wait_recv()
                for head in range(head_count):
                    value = received[shift - 1, head * lanes : (head + 1) * lanes]
                    for near in range(shift - 1):
                        value = value * received[near, state_rows + head : state_rows + head + 1]
                    grad_scr[head] += value

        for shift in range(1, context_size):

            @pl.when(context >= shift)
            def _(shift=shift):
                state_copy(shift).wait_send()

    def mixer_block(index):
        block = block_of(index)
        slot = lax.rem(index, 2)
        block_rows = pl.ds(pl.multiple_of(block * BLOCK, BLOCK), BLOCK)

        @pl.when(index + 1 < blocks)
        def _():
            pre_load(index + 1).start()

        pre_load(index).wait()
        counts, keep, flags = count_ref[block_rows], keep_ref[block_rows], flags_ref[block]
        row_ids, col_ids, linked, fresh, tail, closing = block_masks(counts, flags)
        tri = (row_ids >= col_ids).astype(BF16)
        tri_back = (row_ids <= col_ids).astype(BF16)
        query_pre = pre[slot, :, :width]
        values = pre[slot, :, 2 * width : 3 * width].astype(BF16)
        opened = open_ref[...]
        closed = jax.nn.sigmoid(-pre[slot, :, width : 2 * width])
        keys = opened * closed
        cum = split_sum(tri, jnp.log1p(-keys))
        ending = cum[BLOCK - 1 : BLOCK, :]
        rise, fall = jnp.exp(cum), jnp.exp(-cum) * keep
        shift = jnp.exp(ending - cum) * (keep * tail)
        sigma_query = jax.nn.sigmoid(query_pre)
        lifted = (query_pre * sigma_query * rise).astype(BF16)
        lowered = (keys * fall).astype(BF16)
        moved = (keys * shift).astype(BF16)
        fresh_lifted = (lifted.astype(F32) * fresh).astype(BF16)
        end_decay = jnp.exp(ending) * closing
        lead_in = jnp.exp(run_ref[block]) * (flags[1:2, 0:1] == 0).astype(F32)
        for head in range(head_count):
            part_of = slice(head * lanes, (head + 1) * lanes)
            grad_out, value = grad_mixed[block_rows, part_of], values[:, part_of]
            lift, lower, move = lifted[:, part_of], lowered[:, part_of], moved[:, part_of]
            scores = jnp.where(linked, mm_nt(lift, lower), 0.0).astype(BF16)
            pulls = jnp.where(linked, mm_nt(grad_out, value), 0.0).astype(BF16)
            state = starts_ref[block, head] + lead_in[:, part_of] * carry_ref[head]
            grad_state = grad_scr[head]
            grad_low = grad_state.astype(BF16)
            lifted_scr[:, part_of] = mm_nn(pulls, lower) + fresh * mm_nn(
                grad_out, state.astype(BF16)
            )
            lowered_scr[:, part_of] = mm_tn(pulls, lift)
            grad_moved = mm_nn(value, grad_low)
            moved_scr[:, part_of] = grad_moved
            first = 2 * width + head * lanes
            right[block_rows, first : first + lanes] = (
                mm_tn(scores, grad_out) + mm_nt(move, grad_low)
            ).astype(BF16)
            value_scr[:, part_of] = jnp.sum(
                grad_moved * move.astype(F32), axis=0, keepdims=True
            ) + end_decay[:, part_of] * jnp.sum(state * grad_state, axis=0, keepdims=True)
            grad_scr[head] = grad_state * end_decay[:, part_of] + mm_tn(
                grad_out, fresh_lifted[:, part_of]
            )
        grad_lifted, grad_lowered, grad_moved = lifted_scr[...], lowered_scr[...], moved_scr[...]
        grad_cum = (
            grad_lifted * lifted.astype(F32)
            - grad_lowered * lowered.astype(F32)
            - grad_moved * moved.astype(F32)
        )
        grad_decay = split_sum(tri_back, grad_cum) + value_scr[...]
        key_total = grad_lowered * fall + grad_moved * shift - grad_decay / (1.0 - keys)
        floor_grad[...] -= jnp.sum(key_total * closed, axis=0, keepdims=True)
        right[block_rows, :width] = (
            grad_lifted * rise * sigma_query * (1.0 + query_pre * (1.0 - sigma_query))
        ).astype(BF16)
        right[block_rows, width : 2 * width] = (
            -key_total * opened * closed * (1.0 - closed)
        ).astype(BF16)

    def back_tile(tile):
        columns = tile_columns(tile)
        back_ref[:, columns] = mm_nt(right[...], full[columns, :]).astype(BF16)

    def mixer_tile(tile):
        @pl.when(tile > 0)
        def _():
            stage_copy(tile - 1).wait()

        columns = tile_columns(tile)
        rows = left[:, columns]
        for first in range(0, 4 * width, 1024):
            some = slice(first, min(first + 1024, 4 * width))
            mixer_stage[:, some] = mm_tn(rows, right[:, some]).astype(BF16)
        product = mm_tn(mix_grad_ref[:, columns], gated_ref[...])
        mixer_stage[:, 4 * width :] = product.astype(BF16)
        stage_copy(tile).start()

    send_time = tokens // piece_rows
    block_time = send_time + 1
    back_time = block_time + blocks
    tile_time = back_time + tiles
    end_time = tile_time + tiles

    def beside(time):
        @pl.when(time < send_time)
        def _():
            gate_piece(time)

        @pl.when(time == send_time)
        def _():
            send_back()

        @pl.when(time == block_time)
        def _():
            take_back()

        @pl.when(jnp.logical_and(time >= block_time, time < back_time))
        def _():
            mixer_block(time - block_time)

        @pl.when(time == back_time)
        def _():
            full_load.wait()

        @pl.when(jnp.logical_and(time >= back_time, time < tile_time))
        def _():
            back_tile(time - back_time)

        @pl.when(time == tile_time)
        def _():
            left_load.wait()

        @pl.when(jnp.logical_and(time >= tile_time, time < end_time))
        def _():
            mixer_tile(time - tile_time)

    steps = max(line.steps, end_time)

    def body(time, _):
        @pl.when(time < line.steps)
        def _():
            line.step(time)

        beside(time)
        return 0

    lax.fori_loop(0, steps, body, 0)
    stage_copy(tiles - 1).wait()
    line.finish()


def output_line(mesh_axes, collective, in_vmem, in_hbm, head_count):
    part, _, gated = in_vmem[:3]
    tokens, model_width = part.shape
    width = gated.shape[1]
    lanes = width // head_count
    context_size = lax.axis_size("context")
    messages = head_count * lanes + -(-head_count // 8) * 8
    whole = pl.BlockSpec(memory_space=pltpu.VMEM)
    remote = pl.BlockSpec(memory_space=pl.ANY)
    return pl.pallas_call(
        partial(output_kernel, mesh_axes, head_count, lanes ** (-0.5)),
        in_specs=[whole] * len(in_vmem) + [remote] * len(in_hbm),
        out_specs=[whole] * 4 + [remote],
        out_shape=[
            jax.ShapeDtypeStruct((tokens, model_width), BF16),
            jax.ShapeDtypeStruct((1, lanes), F32),
            jax.ShapeDtypeStruct((1, width), F32),
            jax.ShapeDtypeStruct((tokens, model_width), BF16),
            jax.ShapeDtypeStruct((model_width, 5 * width), BF16),
        ],
        scratch_shapes=[
            pltpu.VMEM((tokens, model_width), BF16),
            pltpu.VMEM((tokens, model_width), BF16),
            pltpu.VMEM((tokens, 4 * width), BF16),
            pltpu.VMEM((model_width, 4 * width), BF16),
            pltpu.VMEM((TILE, 5 * width), BF16),
            pltpu.VMEM((tokens, width), F32),
            pltpu.VMEM((2, BLOCK, 3 * width), F32),
            pltpu.VMEM((tokens, width), BF16),
            pltpu.VMEM((head_count, lanes, lanes), F32),
            pltpu.VMEM((messages, lanes), F32),
            pltpu.VMEM((context_size - 1, messages, lanes), F32),
            pltpu.VMEM((head_count, lanes, lanes), F32),
            pltpu.VMEM((BLOCK, width), F32),
            pltpu.VMEM((BLOCK, width), F32),
            pltpu.VMEM((BLOCK, width), F32),
            pltpu.VMEM((1, width), F32),
            pltpu.SemaphoreType.DMA((3,)),
            pltpu.SemaphoreType.DMA((2,)),
            pltpu.SemaphoreType.DMA((1,)),
            pltpu.SemaphoreType.DMA((context_size - 1,)),
            pltpu.SemaphoreType.DMA((context_size - 1,)),
        ]
        + line_sems(tokens),
        compiler_params=pltpu.CompilerParams(
            collective_id=collective, has_side_effects=True, vmem_limit_bytes=61 << 20
        ),
        cost_estimate=pl.CostEstimate(
            flops=tokens * model_width * width * 24,
            bytes_accessed=360_000_000,
            transcendentals=tokens * width * 12,
        ),
        name="output_line",
    )(*in_vmem, *in_hbm)


def input_kernel(
    mesh_axes,
    part,
    hidden_ref,
    residual_grad,
    gain_ref,
    grads_hbm,
    out_ref,
    gain_grad,
    share_query,
    share_forget,
    share_input,
    share_gate,
    share_out,
    arrived,
    own,
    other,
    remote,
    load_sem,
    pair_send,
    pair_recv,
    chip_send,
    chip_recv,
    *sems,
):
    plane = Plane(mesh_axes)
    chips = plane.chips
    block = own.shape[1]
    gain_grad[...] = jnp.zeros_like(gain_grad)

    def turn(total, rows, own_rows):
        values = hidden_ref[rows].astype(F32)
        inverse = inverse_rms(values)
        unit = values * inverse
        gain_grad[...] += jnp.sum(total * unit, axis=0, keepdims=True)
        lifted = total * gain_ref[...]
        mean = jnp.mean(lifted * unit, axis=-1, keepdims=True)
        grad = residual_grad[own_rows] + inverse * (lifted - unit * mean)
        out_ref[rows] = grad.astype(BF16)

    line = Line(mesh_axes, part, arrived, out_ref, sems, turn)
    barrier = pltpu.get_barrier_semaphore()
    expected = line.greet(barrier) + plane.greet(barrier)
    pl.semaphore_wait(barrier, expected)

    def rows_of(slot, core):
        return pl.ds(pl.multiple_of((2 * plane.ahead(slot) + core) * block, block), block)

    def load(slot):
        return pltpu.make_async_copy(
            grads_hbm.at[rows_of(slot, plane.core)], own.at[slot], load_sem.at[slot]
        )

    def pair_copy(slot):
        return pltpu.make_async_remote_copy(
            grads_hbm.at[rows_of(slot, 1 - plane.core)],
            other.at[slot],
            pair_send.at[slot],
            pair_recv.at[slot],
            device_id=plane.device(plane.chip, 1 - plane.core),
            device_id_type=MESH_ID,
        )

    def chip_copy(slot):
        return pltpu.make_async_remote_copy(
            own.at[slot],
            remote.at[slot - 1],
            chip_send.at[slot - 1],
            chip_recv.at[slot - 1],
            device_id=plane.device(plane.ahead(slot), plane.core),
            device_id_type=MESH_ID,
        )

    def start(index, _):
        slot = lax.rem(index + 1, chips)
        pair_copy(slot).start()
        load(slot).start()
        return 0

    lax.fori_loop(0, chips, start, 0)
    strip = 32

    def combine(time):
        slot = lax.rem(jnp.clip(time, 0, chips - 1) + 1, chips)

        @pl.when(time < chips)
        def _():
            load(slot).wait()
            pair_copy(slot).wait_recv()

            def add(index, _):
                rows = pl.ds(pl.multiple_of(index * strip, strip), strip)
                total = own[slot, rows].astype(F32) + other[slot, rows].astype(F32)
                own[slot, rows] = total.astype(BF16)
                return 0

            lax.fori_loop(0, block // strip, add, 0)

        @pl.when(time < chips - 1)
        def _():
            chip_copy(slot).start()

    line.run(0, line.steps, combine)

    def arrive(index, _):
        chip_copy(index).wait_recv()
        return 0

    lax.fori_loop(1, chips, arrive, 0)

    def total(index, _):
        rows = pl.ds(pl.multiple_of(index * strip, strip), strip)

        for which, share in enumerate(
            (share_query, share_forget, share_input, share_gate, share_out)
        ):
            columns = pl.ds(which * share.shape[1], share.shape[1])

            def add(slot, value, columns=columns):
                return value + remote[slot, rows, columns].astype(F32)

            share[rows] = lax.fori_loop(0, chips - 1, add, own[0, rows, columns].astype(F32))
        return 0

    lax.fori_loop(0, block // strip, total, 0)

    def sent(index, _):
        pair_copy(index).wait_send()
        return 0

    lax.fori_loop(0, chips, sent, 0)

    def chip_sent(index, _):
        chip_copy(index).wait_send()
        return 0

    lax.fori_loop(1, chips, chip_sent, 0)
    line.finish()


def input_line(mesh_axes, collective, part, hidden, residual_grad, gain, grads):
    tokens, model_width = part.shape
    all_width = grads.shape[1]
    chips = lax.axis_size("shard") * lax.axis_size("context") // 2
    block = model_width // (2 * chips)
    whole = pl.BlockSpec(memory_space=pltpu.VMEM)
    return pl.pallas_call(
        partial(input_kernel, mesh_axes),
        in_specs=[whole] * 4 + [pl.BlockSpec(memory_space=pl.ANY)],
        out_specs=[whole] * 7,
        out_shape=[
            jax.ShapeDtypeStruct((tokens, model_width), BF16),
            jax.ShapeDtypeStruct((1, model_width), F32),
        ]
        + [jax.ShapeDtypeStruct((block, all_width // 5), F32)] * 5,
        scratch_shapes=[
            pltpu.VMEM((tokens, model_width), BF16),
            pltpu.VMEM((chips, block, all_width), BF16),
            pltpu.VMEM((chips, block, all_width), BF16),
            pltpu.VMEM((chips - 1, block, all_width), BF16),
            pltpu.SemaphoreType.DMA((chips,)),
            pltpu.SemaphoreType.DMA((chips,)),
            pltpu.SemaphoreType.DMA((chips,)),
            pltpu.SemaphoreType.DMA((chips - 1,)),
            pltpu.SemaphoreType.DMA((chips - 1,)),
        ]
        + line_sems(tokens),
        compiler_params=pltpu.CompilerParams(
            collective_id=collective, has_side_effects=True, vmem_limit_bytes=58 << 20
        ),
        cost_estimate=pl.CostEstimate(
            flops=tokens * model_width * 8, bytes_accessed=360_000_000, transcendentals=0
        ),
        name="input_line",
    )(part, hidden, residual_grad, gain, grads)


def forward_kernel(
    mesh_axes,
    head_count,
    key_scale,
    hidden_ref,
    gain_ref,
    query_hbm,
    forget_hbm,
    input_hbm,
    gate_hbm,
    out_shard_ref,
    down_shard_ref,
    floor_ref,
    segments_ref,
    head_gain_ref,
    normed_hbm,
    pre_hbm,
    full_hbm,
    out_full_hbm,
    mixed_hbm,
    lead_hbm,
    start_hbm,
    gated_hbm,
    mix_hbm,
    down_turned,
    open_ref,
    count_ref,
    keep_ref,
    flags_ref,
    run_ref,
    carry_ref,
    decay_ref,
    link_ref,
    normed,
    pre,
    mine,
    out_turned,
    full,
    out_full,
    mixed,
    lead,
    starts,
    gated,
    mix,
    state_scr,
    run_scr,
    message,
    received,
    mine_sem,
    full_sem,
    save_sem,
    pre_sem,
    mix_sem,
    state_send,
    state_recv,
    *sems,
):
    plane = Plane(mesh_axes)
    chips = plane.chips
    tokens, model_width = hidden_ref.shape
    block, width = query_hbm.shape
    lanes = width // head_count
    state_rows = head_count * lanes
    context, context_size = lax.axis_index("context"), lax.axis_size("context")

    mine_loads = [
        pltpu.make_async_copy(
            ref, mine.at[:, pl.ds(which * width, width)], mine_sem.at[which]
        )
        for which, ref in enumerate((query_hbm, forget_hbm, input_hbm, gate_hbm))
    ]
    for load in mine_loads:
        load.start()
    gather = Gather(plane, (mine,), (full,), sems[:5])
    out_gather = Gather(plane, (out_turned,), (out_full,), sems[5:])

    def later(shift):
        places = {axis: lax.axis_index(axis) for axis in mesh_axes}
        places["context"] = lax.rem(context + shift, context_size)
        return tuple(places[axis] for axis in mesh_axes)

    out_turned[...] = out_shard_ref[...].T
    barrier = pltpu.get_barrier_semaphore()
    expected = gather.greet(barrier)
    for shift in range(1, context_size):
        pl.semaphore_signal(barrier, inc=1, device_id=later(shift), device_id_type=MESH_ID)
    pl.semaphore_wait(barrier, expected + context_size - 1)
    for load in mine_loads:
        load.wait()
    gather.start()
    out_gather.start()
    down_turned[...] = down_shard_ref[...].T
    for head in range(head_count):
        open_ref[:, head * lanes : (head + 1) * lanes] = 1.0 - floor_ref[head : head + 1]

    segments = segments_ref[...]
    blocks = segments.shape[0]
    block_ids = lax.broadcasted_iota(jnp.int32, segments.shape, 0)
    slot_ids = lax.broadcasted_iota(jnp.int32, segments.shape, 1)
    before = pltpu.roll(segments, 1, 1)
    wrapped = pltpu.roll(before, 1, 0)
    before = jnp.where(slot_ids == 0, wrapped, before)
    first_slot = jnp.logical_and(slot_ids == 0, block_ids == 0)
    begins = jnp.where(jnp.logical_or(first_slot, segments == before), 0.0, 1.0)
    wide_rows = lax.broadcasted_iota(jnp.int32, (BLOCK, BLOCK), 0)
    wide_columns = lax.broadcasted_iota(jnp.int32, (BLOCK, BLOCK), 1)
    within = mm_nn(begins.astype(BF16), (wide_rows <= wide_columns).astype(BF16))
    count_rows = []
    running = jnp.zeros((1, 1), F32)
    flags_ref[...] = jnp.zeros_like(flags_ref)
    for index in range(blocks):
        row = within[index : index + 1] + running
        flags_ref[index, 0:1] = row
        flags_ref[index, 1:2] = jnp.broadcast_to(running, (1, BLOCK))
        running = row[:, BLOCK - 1 : BLOCK]
        flags_ref[index, 2:3] = jnp.broadcast_to(running, (1, BLOCK))
        count_rows.append(row)
    turned_counts = jnp.concatenate(count_rows, axis=0).T
    turned_keep = (segments > 0).astype(F32).T
    for index in range(blocks):
        rows = slice(index * BLOCK, (index + 1) * BLOCK)
        count_ref[rows] = turned_counts[:, index : index + 1]
        keep_ref[rows] = turned_keep[:, index : index + 1]
    first_id = jnp.broadcast_to(segments[0:1, 0:1], (1, lanes))
    last_id = jnp.broadcast_to(segments[blocks - 1 : blocks, BLOCK - 1 : BLOCK], (1, lanes))

    def norm(index, _):
        rows = pl.ds(pl.multiple_of(index * 128, 128), 128)
        values = hidden_ref[rows].astype(F32)
        normed[rows] = (values * inverse_rms(values) * gain_ref[...]).astype(BF16)
        return 0

    lax.fori_loop(0, tokens // 128, norm, 0)

    saves = [
        pltpu.make_async_copy(source, target, save_sem.at[which])
        for which, (source, target) in enumerate(
            (
                (normed, normed_hbm),
                (out_full, out_full_hbm),
                (mixed, mixed_hbm),
                (lead, lead_hbm),
                (starts, start_hbm),
                (gated, gated_hbm),
            )
        )
    ]
    saves[0].start()
    row_tile, column_tile = 256, 512

    def pre_save(index):
        rows = pl.ds(pl.multiple_of(index * row_tile, row_tile), row_tile)
        return pltpu.make_async_copy(pre.at[rows], pre_hbm.at[rows], pre_sem.at[index])

    def depth_of(distance):
        first = 2 * gather.partner(distance) * block
        return pl.ds(pl.multiple_of(first, 2 * block), 2 * block)

    def product(distance):
        depth = depth_of(distance)

        def row_body(index, _):
            rows = pl.ds(pl.multiple_of(index * row_tile, row_tile), row_tile)
            left = normed[rows, depth]

            def column_body(column, _):
                columns = pl.ds(pl.multiple_of(column * column_tile, column_tile), column_tile)
                value = mm_nn(left, full[depth, columns])
                if distance > 0:
                    value = value + pre[rows, columns]
                pre[rows, columns] = value
                return 0

            lax.fori_loop(0, full.shape[1] // column_tile, column_body, 0)
            if distance == chips - 1:
                pre_save(index).start()
            return 0

        lax.fori_loop(0, tokens // row_tile, row_body, 0)

    def full_save(distance):
        depth = depth_of(distance)
        return pltpu.make_async_copy(full.at[depth], full_hbm.at[depth], full_sem.at[distance])

    def use(distance):
        gather.arrive_from(distance)
        full_save(distance).start()
        product(distance)

    use(0)
    gather.stage(0)
    gather.stage(1)
    if gather.relayed:
        use(1)
        use(2)
    gather.stage(2)
    if gather.relayed:
        use(3)
    else:
        for distance in range(1, chips):
            use(distance)
    out_gather.stage(0)
    out_gather.stage(1)

    state_scr[...] = jnp.zeros_like(state_scr)
    run_scr[...] = jnp.zeros_like(run_scr)

    def recur(step, _):
        rows = pl.ds(pl.multiple_of(step * BLOCK, BLOCK), BLOCK)
        counts, keep = count_ref[rows], keep_ref[rows]
        row_ids, col_ids, linked, fresh, tail, closing = block_masks(counts, flags_ref[step])
        tri = (row_ids >= col_ids).astype(BF16)
        query_pre = pre[rows, :width]
        values = pre[rows, 2 * width : 3 * width].astype(BF16)
        keys = open_ref[...] * jax.nn.sigmoid(-pre[rows, width : 2 * width])
        cum = split_sum(tri, jnp.log1p(-keys))
        ending = cum[BLOCK - 1 : BLOCK, :]
        lifted = query_pre * jax.nn.sigmoid(query_pre) * jnp.exp(cum)
        lowered = (keys * jnp.exp(-cum) * keep).astype(BF16)
        moved = (keys * jnp.exp(ending - cum) * (keep * tail)).astype(BF16)
        run = run_scr[...]
        lead[rows] = (lifted * jnp.exp(run) * (counts == 0).astype(F32)).astype(BF16)
        run_ref[step] = run
        run_scr[...] = run + ending
        fresh_lifted = (lifted * fresh).astype(BF16)
        lifted = lifted.astype(BF16)
        end_decay = jnp.exp(ending) * closing
        for head in range(head_count):
            part = slice(head * lanes, (head + 1) * lanes)
            state = state_scr[head]
            starts[step, head] = state
            scores = jnp.where(linked, mm_nt(lifted[:, part], lowered[:, part]), 0.0)
            results = mm_nn(scores.astype(BF16), values[:, part])
            results = results + mm_nt(fresh_lifted[:, part], state.astype(BF16))
            mixed[rows, part] = results * (key_scale * keep)
            state_scr[head] = state * end_decay[:, part] + mm_tn(values[:, part], moved[:, part])
        return 0

    lax.fori_loop(0, tokens // BLOCK, recur, 0)
    saves[3].start()
    saves[4].start()

    last_count = flags_ref[tokens // BLOCK - 1][2:3, 0:1]
    for head in range(head_count):
        part = slice(head * lanes, (head + 1) * lanes)
        message[head * lanes : (head + 1) * lanes] = state_scr[head]
        decay = jnp.exp(run_scr[:, part]) * (last_count == 0).astype(F32)
        decay_ref[head] = decay
        message[state_rows + 8 + head : state_rows + 9 + head] = decay
    message[state_rows : state_rows + 1] = first_id
    message[state_rows + 1 : state_rows + 2] = last_id

    def state_copy(shift):
        return pltpu.make_async_remote_copy(
            message,
            received.at[shift - 1],
            state_send.at[shift - 1],
            state_recv.at[shift - 1],
            device_id=later(shift),
            device_id_type=MESH_ID,
        )

    for shift in range(1, context_size):

        @pl.when(context + shift < context_size)
        def _(shift=shift):
            state_copy(shift).start()

    out_gather.stage(2)
    carry_ref[...] = jnp.zeros_like(carry_ref)
    link_ref[...] = jnp.zeros_like(link_ref)
    for shift in range(1, context_size):

        @pl.when(context >= shift)
        def _(shift=shift):
            state_copy(shift).wait_recv()
            linked = jnp.ones((1, lanes), F32)
            follower = first_id
            factors = [jnp.ones((1, lanes), F32)] * head_count
            for near in range(shift):
                got = received.at[near]
                linked = (got[state_rows + 1 : state_rows + 2] == follower).astype(F32)
                follower = got[state_rows : state_rows + 1]
                factors = [factor * linked for factor in factors]
                if near < shift - 1:
                    factors = [
                        factor * got[state_rows + 8 + head : state_rows + 9 + head]
                        for head, factor in enumerate(factors)
                    ]
            if shift == 1:
                link_ref[0:1] = linked
            for head in range(head_count):
                rows = slice(head * lanes, (head + 1) * lanes)
                carry_ref[head] += factors[head] * received[shift - 1, rows]

    for shift in range(1, context_size):

        @pl.when(context + shift < context_size)
        def _(shift=shift):
            state_copy(shift).wait_send()

    for distance in range(chips):
        out_gather.arrive_from(distance)
    saves[1].start()

    def mix_save(index):
        rows = pl.ds(pl.multiple_of(index * row_tile, row_tile), row_tile)
        return pltpu.make_async_copy(mix.at[rows], mix_hbm.at[rows], mix_sem.at[index])

    def project(index, _):
        rows = pl.ds(pl.multiple_of(index * row_tile, row_tile), row_tile)
        for head in range(head_count):
            part = slice(head * lanes, (head + 1) * lanes)
            carried = mm_nt(lead[rows, part], carry_ref[head].astype(BF16))
            value = mixed[rows, part] + carried * (key_scale * keep_ref[rows])
            mixed[rows, part] = value
            gate = pre[rows, 3 * width + head * lanes : 3 * width + (head + 1) * lanes]
            unit = value * inverse_rms(value)
            gated[rows, part] = (
                unit * head_gain_ref[...] * (gate * jax.nn.sigmoid(gate))
            ).astype(BF16)
        left = gated[rows]

        def column_body(column, _):
            columns = pl.ds(pl.multiple_of(column * column_tile, column_tile), column_tile)
            mix[rows, columns] = mm_nt(left, out_full[columns, :]).astype(BF16)
            return 0

        lax.fori_loop(0, model_width // column_tile, column_body, 0)
        mix_save(index).start()
        return 0

    lax.fori_loop(0, tokens // row_tile, project, 0)
    saves[2].start()
    saves[5].start()
    gather.finish()
    out_gather.finish()
    for distance in range(chips):
        full_save(distance).wait()
    for save in saves:
        save.wait()
    for index in range(tokens // row_tile):
        pre_save(index).wait()
        mix_save(index).wait()


def forward(
    mesh_axes, collective, hidden, gain, shards, out_shard, down_shard, floor, segments, head_gain
):
    tokens, model_width = hidden.shape
    block, width = shards[0].shape
    lanes = head_gain.shape[1]
    head_count = width // lanes
    all_width = width * len(shards)
    blocks = tokens // BLOCK
    context_size = lax.axis_size("context")
    chips = lax.axis_size("shard") * context_size // 2
    messages = head_count * lanes + 8 + -(-head_count // 8) * 8
    whole = pl.BlockSpec(memory_space=pltpu.VMEM)
    remote = pl.BlockSpec(memory_space=pl.ANY)
    stored = [
        ((tokens, model_width), BF16),
        ((tokens, all_width), F32),
        ((model_width, all_width), BF16),
        ((model_width, width), BF16),
        ((tokens, width), F32),
        ((tokens, width), BF16),
        ((blocks, head_count, lanes, lanes), F32),
        ((tokens, width), BF16),
        ((tokens, model_width), BF16),
    ]
    kept = [
        (down_shard.shape[::-1], BF16),
        ((1, width), F32),
        ((tokens, 1), F32),
        ((tokens, 1), F32),
        ((blocks, 8, BLOCK), F32),
        ((blocks, 1, width), F32),
        ((head_count, lanes, lanes), F32),
        ((head_count, 1, lanes), F32),
        ((8, lanes), F32),
    ]
    return pl.pallas_call(
        partial(forward_kernel, mesh_axes, head_count, lanes ** (-0.5)),
        in_specs=[whole] * 2 + [remote] * 4 + [whole] * 5,
        out_specs=[remote] * len(stored) + [whole] * len(kept),
        out_shape=[jax.ShapeDtypeStruct(shape, kind) for shape, kind in stored + kept],
        scratch_shapes=[
            pltpu.VMEM((tokens, model_width), BF16),
            pltpu.VMEM((tokens, all_width), F32),
            pltpu.VMEM((block, all_width), BF16),
            pltpu.VMEM((block, width), BF16),
            pltpu.VMEM((model_width, all_width), BF16),
            pltpu.VMEM((model_width, width), BF16),
            pltpu.VMEM((tokens, width), F32),
            pltpu.VMEM((tokens, width), BF16),
            pltpu.VMEM((blocks, head_count, lanes, lanes), F32),
            pltpu.VMEM((tokens, width), BF16),
            pltpu.VMEM((tokens, model_width), BF16),
            pltpu.VMEM((head_count, lanes, lanes), F32),
            pltpu.VMEM((1, width), F32),
            pltpu.VMEM((messages, lanes), F32),
            pltpu.VMEM((context_size - 1, messages, lanes), F32),
            pltpu.SemaphoreType.DMA((4,)),
            pltpu.SemaphoreType.DMA((chips,)),
            pltpu.SemaphoreType.DMA((6,)),
            pltpu.SemaphoreType.DMA((tokens // 256,)),
            pltpu.SemaphoreType.DMA((tokens // 256,)),
            pltpu.SemaphoreType.DMA((context_size - 1,)),
            pltpu.SemaphoreType.DMA((context_size - 1,)),
        ]
        + gather_sems(1)
        + gather_sems(1),
        compiler_params=pltpu.CompilerParams(
            collective_id=collective, has_side_effects=True, vmem_limit_bytes=56 << 20
        ),
        cost_estimate=pl.CostEstimate(
            flops=2 * tokens * model_width * all_width,
            bytes_accessed=200_000_000,
            transcendentals=tokens * width * 9,
        ),
        name="forward",
    )(hidden, gain, *shards, out_shard, down_shard, floor, segments, head_gain)


def small_sum_kernel(
    mesh_axes, value, local_ref, total_ref, near, far, near_send, near_recv, far_send, far_recv
):
    shard_size, context_size = lax.axis_size("shard"), lax.axis_size("context")
    line_size = lax.axis_size("tensor")
    group = shard_size * context_size
    place = lax.axis_index("shard") * context_size + lax.axis_index("context")
    line_place = lax.axis_index("tensor")

    def device(position, line_position):
        places = {
            "shard": position // context_size,
            "context": lax.rem(position, context_size),
            "tensor": line_position,
        }
        return tuple(places[axis] for axis in mesh_axes)

    def near_target(step):
        return device(lax.rem(place + step, group), line_place)

    def far_target(step):
        return device(place, lax.rem(line_place + step, line_size))

    def near_copy(step):
        return pltpu.make_async_remote_copy(
            value,
            near.at[step - 1],
            near_send.at[step - 1],
            near_recv.at[step - 1],
            device_id=near_target(step),
            device_id_type=MESH_ID,
        )

    def far_copy(step):
        return pltpu.make_async_remote_copy(
            local_ref,
            far.at[step - 1],
            far_send.at[step - 1],
            far_recv.at[step - 1],
            device_id=far_target(step),
            device_id_type=MESH_ID,
        )

    barrier = pltpu.get_barrier_semaphore()
    for step in range(1, group):
        pl.semaphore_signal(barrier, inc=1, device_id=near_target(step), device_id_type=MESH_ID)
    for step in range(1, line_size):
        pl.semaphore_signal(barrier, inc=1, device_id=far_target(step), device_id_type=MESH_ID)
    pl.semaphore_wait(barrier, group + line_size - 2)
    for step in range(1, group):
        near_copy(step).start()
    total = value[...]
    for step in range(1, group):
        near_copy(step).wait_recv()
        total = total + near[step - 1]
    local_ref[...] = total
    for step in range(1, line_size):
        far_copy(step).start()
    for step in range(1, line_size):
        far_copy(step).wait_recv()
        total = total + far[step - 1]
    total_ref[...] = total
    for step in range(1, group):
        near_copy(step).wait_send()
    for step in range(1, line_size):
        far_copy(step).wait_send()


def small_sum(mesh_axes, collective, values):
    flat = jnp.concatenate([value.reshape(-1) for value in values])
    lanes = -(-flat.shape[0] // 1024) * 128
    flat = jnp.pad(flat, (0, 8 * lanes - flat.shape[0])).reshape(8, lanes)
    group = lax.axis_size("shard") * lax.axis_size("context")
    line_size = lax.axis_size("tensor")
    whole = pl.BlockSpec(memory_space=pltpu.VMEM)
    local, total = pl.pallas_call(
        partial(small_sum_kernel, mesh_axes),
        in_specs=[whole],
        out_specs=[whole] * 2,
        out_shape=[jax.ShapeDtypeStruct((8, lanes), F32)] * 2,
        scratch_shapes=[
            pltpu.VMEM((group - 1, 8, lanes), F32),
            pltpu.VMEM((line_size - 1, 8, lanes), F32),
            pltpu.SemaphoreType.DMA((group - 1,)),
            pltpu.SemaphoreType.DMA((group - 1,)),
            pltpu.SemaphoreType.DMA((line_size - 1,)),
            pltpu.SemaphoreType.DMA((line_size - 1,)),
        ],
        compiler_params=pltpu.CompilerParams(collective_id=collective, has_side_effects=True),
        cost_estimate=pl.CostEstimate(
            flops=8 * lanes * group, bytes_accessed=20_000_000, transcendentals=0
        ),
        name="small_sum",
    )(flat)
    return local.reshape(-1), total.reshape(-1)


def local(
    mesh_axes,
    hidden,
    segment_ids,
    norm1_gain,
    w_query,
    w_forget,
    w_input,
    w_gate_out,
    forget_floor,
    head_gain,
    w_out,
    norm2_gain,
    w_ffn_gate,
    w_ffn_up,
    w_ffn_down,
    out_grad,
):
    sequences, span_len, model_width = hidden.shape
    tokens = sequences * span_len
    head_count, key_dim = forget_floor.shape
    width = head_count * key_dim
    key_scale = key_dim ** (-0.5)
    both = ("shard", "context")
    gain_one, gain_two = norm1_gain.reshape(1, -1), norm2_gain.reshape(1, -1)
    hidden_rows = hidden.reshape(tokens, model_width)
    gain_row = head_gain.reshape(1, -1)
    segments = segment_ids.reshape(tokens // BLOCK, BLOCK).astype(F32)
    (
        normed_one,
        pre,
        mixer_full,
        out_full,
        mixed,
        lead,
        starts,
        gated_low,
        mix_part,
        down_turned,
        open_part,
        counts,
        keep,
        flags,
        runs,
        carry,
        decay,
        link,
    ) = forward(
        mesh_axes,
        4,
        hidden_rows,
        gain_one,
        (w_query, w_forget, w_input, w_gate_out),
        w_out,
        w_ffn_down,
        forget_floor,
        segments,
        gain_row,
    )
    grad_rows = out_grad.reshape(tokens, model_width)
    (
        _,
        grad_mix_low,
        grad_norm_two,
        residual,
        _,
        _,
        _,
        feed_part,
        grad_residual,
        grads_ffn,
    ) = middle(
        mesh_axes,
        2,
        mix_part,
        grad_rows,
        hidden_rows,
        gain_two,
        w_ffn_gate,
        w_ffn_up,
        down_turned,
    )
    (
        output_rows,
        grad_head_part,
        grad_floor_part,
        back_one,
        grads_mixer,
    ) = output_line(
        mesh_axes,
        1,
        (
            feed_part,
            residual,
            gated_low,
            grad_mix_low,
            out_full,
            mixed,
            lead,
            starts,
            runs,
            carry,
            decay,
            link,
            open_part,
            counts,
            keep,
            flags,
            gain_row,
        ),
        (normed_one, pre, mixer_full),
        head_count,
    )
    share_ffn = lax.psum_scatter(grads_ffn, both, scatter_dimension=0, tiled=True)
    hidden_width = w_ffn_gate.shape[1]

    def ffn_share(which):
        return share_ffn[:, which * hidden_width : (which + 1) * hidden_width].astype(F32)

    input_rows, grad_norm_one, *mixer_shares, share_out = input_line(
        mesh_axes, 3, back_one, hidden_rows, grad_residual, gain_one, grads_mixer
    )
    near, total = small_sum(
        mesh_axes, 5, (grad_norm_one, grad_norm_two, grad_head_part, grad_floor_part)
    )
    shares = lax.axis_size("shard") * lax.axis_size("context")
    position = lax.axis_index("shard") * lax.axis_size("context") + lax.axis_index("context")

    def own_slice(values, first, length):
        values = values[first : first + length].reshape(shares, length // shares)
        return lax.dynamic_index_in_dim(values, position, 0, False)

    floor_total = near[2 * model_width + key_dim : 2 * model_width + key_dim + width]
    floor_total = floor_total.reshape(head_count, shares, key_dim // shares)

    return (
        output_rows.reshape(hidden.shape),
        input_rows.reshape(hidden.shape),
        own_slice(total, 0, model_width),
        *mixer_shares,
        lax.dynamic_index_in_dim(floor_total, position, 1, False),
        own_slice(total, 2 * model_width, key_dim),
        share_out.T,
        own_slice(total, model_width, model_width),
        ffn_share(0),
        ffn_share(1),
        ffn_share(2).T,
    )


def solution(mesh):
    in_specs = (
        P("shard", "context", None),
        P("shard", "context"),
        P(),
        P(("shard", "context"), "tensor"),
        P(("shard", "context"), "tensor"),
        P(("shard", "context"), "tensor"),
        P(("shard", "context"), "tensor"),
        P("tensor", None),
        P(),
        P("tensor", ("shard", "context")),
        P(),
        P(("shard", "context"), "tensor"),
        P(("shard", "context"), "tensor"),
        P("tensor", ("shard", "context")),
        P("shard", "context", None),
    )
    out_specs = (
        P("shard", "context", None),
        P("shard", "context", None),
        P(("shard", "context")),
        P(("shard", "context"), "tensor"),
        P(("shard", "context"), "tensor"),
        P(("shard", "context"), "tensor"),
        P(("shard", "context"), "tensor"),
        P("tensor", ("shard", "context")),
        P(("shard", "context")),
        P("tensor", ("shard", "context")),
        P(("shard", "context")),
        P(("shard", "context"), "tensor"),
        P(("shard", "context"), "tensor"),
        P("tensor", ("shard", "context")),
    )
    return jax.shard_map(
        partial(local, mesh.axis_names), mesh=mesh, in_specs=in_specs, out_specs=out_specs, check_vma=False)
```

```python
from functools import partial

import jax
import jax.numpy as jnp
from jax import lax
from jax.experimental import pallas as pl
from jax.experimental.pallas import tpu as pltpu
from jax.sharding import PartitionSpec as P

EPSILON = 1e-05


BLOCK = 128
F32 = jnp.float32
BF16 = jnp.bfloat16


def mm(a, b, dims):
    return lax.dot_general(a, b, (dims, ((), ())), preferred_element_type=F32)


def mm_nn(a, b):
    return mm(a, b, ((1,), (0,)))


def mm_nt(a, b):
    return mm(a, b, ((1,), (1,)))


def mm_tn(a, b):
    return mm(a, b, ((0,), (0,)))


def split_sum(tri, values):
    high = values.astype(BF16)
    low = (values - high.astype(F32)).astype(BF16)
    return mm_nn(tri, high) + mm_nn(tri, low)


def block_masks(counts, flags_row):
    rows = counts.shape[0]
    row_ids = lax.broadcasted_iota(jnp.int32, (rows, rows), 0)
    col_ids = lax.broadcasted_iota(jnp.int32, (rows, rows), 1)
    linked = jnp.logical_and(counts == flags_row[0:1], row_ids >= col_ids)
    fresh = (counts == flags_row[1:2, 0:1]).astype(F32)
    tail = (counts == flags_row[2:3, 0:1]).astype(F32)
    closing = (flags_row[1:2, 0:1] == flags_row[2:3, 0:1]).astype(F32)
    return row_ids, col_ids, linked, fresh, tail, closing


CHUNK = 32
LAG = 2
MESH_ID = pl.DeviceIdType.MESH


class Line:
    def __init__(self, mesh_axes, part, arrived, out, sems, transform, sums=True, backs=True):
        self.mesh_axes = mesh_axes
        self.sums, self.backs = sums, backs
        self.part, self.arrived, self.out = part, arrived, out
        if sums:
            self.sum_send, self.sum_recv = sems[:2]
        if backs:
            self.back_send, self.back_recv = sems[-2:]
        self.transform = transform
        self.half = (part if sums else out).shape[0] // 2
        self.chunks = self.half // CHUNK
        self.size = lax.axis_size("tensor")
        self.place = lax.axis_index("tensor")
        self.lines = ((self.size - 1 - self.place, -1), (self.place, 1))
        self.offset = LAG * (self.size - 1) if sums else 0
        self.steps = self.chunks + self.offset + (LAG * (self.size - 1) if backs else 0)

    def device(self, position):
        return tuple(
            jnp.clip(position, 0, self.size - 1) if axis == "tensor" else lax.axis_index(axis)
            for axis in self.mesh_axes
        )

    def greet(self, barrier):
        for step in (-1, 1):
            inside = jnp.logical_and(self.place + step >= 0, self.place + step < self.size)

            @pl.when(inside)
            def _(step=step):
                pl.semaphore_signal(
                    barrier, inc=1, device_id=self.device(self.place + step), device_id_type=MESH_ID
                )

        at_end = jnp.logical_or(self.place == 0, self.place == self.size - 1)
        return jnp.where(at_end, 1, 2)

    def rows_of(self, side, index):
        return pl.ds(pl.multiple_of(side * self.half + index * CHUNK, CHUNK), CHUNK)

    def sum_copy(self, side, index, source):
        rows = self.rows_of(side, index)
        return pltpu.make_async_remote_copy(
            source.at[rows],
            self.arrived.at[rows],
            self.sum_send.at[side, index],
            self.sum_recv.at[side, index],
            device_id=self.device(self.place + self.lines[side][1]),
            device_id_type=MESH_ID,
        )

    def back_copy(self, side, index):
        rows = self.rows_of(side, index)
        return pltpu.make_async_remote_copy(
            self.out.at[rows],
            self.out.at[rows],
            self.back_send.at[side, index],
            self.back_recv.at[side, index],
            device_id=self.device(self.place - self.lines[side][1]),
            device_id_type=MESH_ID,
        )

    def step(self, time):
        for side in (0, 1):
            hops = self.lines[side][0]
            at_source, at_owner = hops == 0, hops == self.size - 1
            if self.sums:
                self.sum_step(time, side, hops, at_source, at_owner)
            if self.backs:
                self.back_step(time, side, hops, at_owner)

    def sum_step(self, time, side, hops, at_source, at_owner):
        index = time - LAG * hops
        valid = jnp.logical_and(index >= 0, index < self.chunks)
        index = jnp.clip(index, 0, self.chunks - 1)
        rows = self.rows_of(side, index)

        @pl.when(jnp.logical_and(valid, at_source))
        def _():
            self.sum_copy(side, index, self.part).start()

        @pl.when(jnp.logical_and(valid, jnp.logical_not(at_source)))
        def _():
            self.sum_copy(side, index, self.arrived).wait_recv()

        between = jnp.logical_and(jnp.logical_not(at_source), jnp.logical_not(at_owner))

        @pl.when(jnp.logical_and(valid, between))
        def _():
            total = self.part[rows].astype(F32) + self.arrived[rows].astype(F32)
            self.arrived[rows] = total.astype(BF16)
            self.sum_copy(side, index, self.arrived).start()

        @pl.when(jnp.logical_and(valid, at_owner))
        def _():
            total = self.part[rows].astype(F32) + self.arrived[rows].astype(F32)
            self.turn(total, side, index)

    def turn(self, total, side, index):
        own = pl.ds(pl.multiple_of(index * CHUNK, CHUNK), CHUNK)
        self.transform(total, self.rows_of(side, index), own)
        if self.backs:
            self.back_copy(side, index).start()

    def back_step(self, time, side, hops, at_owner):
        if not self.sums:

            @pl.when(jnp.logical_and(at_owner, time < self.chunks))
            def _():
                self.turn(None, side, jnp.clip(time, 0, self.chunks - 1))

        away = self.size - 1 - hops
        index = time - self.offset - LAG * away
        valid = jnp.logical_and(jnp.logical_and(index >= 0, index < self.chunks), away > 0)
        index = jnp.clip(index, 0, self.chunks - 1)

        @pl.when(valid)
        def _():
            self.back_copy(side, index).wait_recv()

        @pl.when(jnp.logical_and(valid, away < self.size - 1))
        def _():
            self.back_copy(side, index).start()

    def run(self, first, last, beside=None):
        def body(time, _):
            self.step(time)
            if beside is not None:
                beside(time)
            return 0

        lax.fori_loop(first, last, body, 0)

    def source_sent(self, first, last):
        def body(index, _):
            for side in (0, 1):

                @pl.when(self.lines[side][0] == 0)
                def _(side=side):
                    self.sum_copy(side, index, self.part).wait_send()

            return 0

        lax.fori_loop(first, last, body, 0)

    def finish(self, source_waits=True):
        def body(index, _):
            for side in (0, 1):
                hops = self.lines[side][0]
                passed = hops < self.size - 1
                if not source_waits:
                    passed = jnp.logical_and(passed, hops > 0)

                if self.sums:

                    @pl.when(passed)
                    def _(side=side):
                        self.sum_copy(side, index, self.arrived).wait_send()

                if self.backs:

                    @pl.when(hops > 0)
                    def _(side=side):
                        self.back_copy(side, index).wait_send()

            return 0

        lax.fori_loop(0, self.chunks, body, 0)


def line_sems(tokens, count=4):
    return [pltpu.SemaphoreType.DMA((2, tokens // 2 // CHUNK))] * count


def inverse_rms(values):
    return lax.rsqrt(jnp.mean(values * values, axis=-1, keepdims=True) + EPSILON)


class Plane:
    def __init__(self, mesh_axes):
        self.mesh_axes = mesh_axes
        self.context = lax.axis_size("context")
        self.per_row = self.context // 2
        self.chips = lax.axis_size("shard") * self.per_row
        context_place = lax.axis_index("context")
        self.core = lax.rem(context_place, 2)
        self.chip = lax.axis_index("shard") * self.per_row + context_place // 2

    def device(self, chip, core):
        places = {
            "shard": chip // self.per_row,
            "context": 2 * lax.rem(chip, self.per_row) + core,
            "tensor": lax.axis_index("tensor"),
        }
        return tuple(places[axis] for axis in self.mesh_axes)

    def ahead(self, distance):
        return lax.rem(self.chip + distance, self.chips)

    def greet(self, barrier):
        targets = [self.device(self.chip, 1 - self.core)]
        targets += [self.device(self.ahead(step), self.core) for step in range(1, self.chips)]
        for target in targets:
            pl.semaphore_signal(barrier, inc=1, device_id=target, device_id_type=MESH_ID)
        return len(targets)


class Gather:
    def __init__(self, plane, sources, targets, sems):
        self.plane, self.sources, self.targets = plane, sources, targets
        self.load_sem, self.send_sem, self.recv_sem, self.pair_send, self.pair_recv = sems
        self.block = sources[0].shape[0]
        self.part = self.block // 2
        self.relayed = plane.chips == 4
        self.arrays = range(len(sources))

    def partner(self, distance):
        return jnp.bitwise_xor(self.plane.chip, distance)

    def greet(self, barrier):
        plane = self.plane
        targets = [plane.device(plane.chip, 1 - plane.core)]
        targets += [
            plane.device(self.partner(step), plane.core)
            for step in range(1, 3 if self.relayed else plane.chips)
        ]
        for target in targets:
            pl.semaphore_signal(barrier, inc=1, device_id=target, device_id_type=MESH_ID)
        return len(targets)

    def place(self, array, chip, core, half):
        first = (2 * chip + core) * self.block + half * self.part
        rows = pl.ds(pl.multiple_of(first, self.part), self.part)
        return self.targets[array].at[rows, pl.ds(0, self.sources[array].shape[1])]

    def mine(self, array, half):
        return self.sources[array].at[pl.ds(half * self.part, self.part)]

    def loads(self):
        plane = self.plane
        return [
            pltpu.make_async_copy(
                self.mine(array, half),
                self.place(array, plane.chip, plane.core, half),
                self.load_sem.at[array, half],
            )
            for array in self.arrays
            for half in range(2)
        ]

    def send(self, distance, half):
        plane = self.plane
        copies = []
        for array in self.arrays:
            chip, target = plane.chip, self.partner(distance)
            source = self.mine(array, half)
            if self.relayed and distance == 3:
                chip = self.partner(2 if half == 0 else 1)
                target = self.partner(1 if half == 0 else 2)
                source = self.place(array, chip, plane.core, half)
            copies.append(
                pltpu.make_async_remote_copy(
                    source,
                    self.place(array, chip, plane.core, half),
                    self.send_sem.at[array, distance - 1, half],
                    self.recv_sem.at[array, distance - 1, half],
                    device_id=plane.device(target, plane.core),
                    device_id_type=MESH_ID,
                )
            )
        return copies

    def forward(self, distance, half):
        plane = self.plane
        copies = []
        for array in self.arrays:
            place = self.place(array, self.partner(distance), plane.core, half)
            copies.append(
                pltpu.make_async_remote_copy(
                    self.mine(array, half) if distance == 0 else place,
                    place,
                    self.pair_send.at[array, distance, half],
                    self.pair_recv.at[array, distance, half],
                    device_id=plane.device(plane.chip, 1 - plane.core),
                    device_id_type=MESH_ID,
                )
            )
        return copies

    def start(self):
        if self.relayed:
            order = ((1, 1), (2, 0), (1, 0), (2, 1))
        else:
            order = [(step, half) for step in range(1, self.plane.chips) for half in range(2)]
        for distance, half in order:
            for copy in self.send(distance, half):
                copy.start()
        for copy in self.loads():
            copy.start()
        for half in range(2):
            for copy in self.forward(0, half):
                copy.start()

    def take(self, distance, half, relay):
        for copy in self.send(distance, half):
            copy.wait_recv()
        if relay:
            for copy in self.send(3, half):
                copy.start()
        for copy in self.forward(distance, half):
            copy.start()

    def stage(self, number):
        if self.relayed:
            if number == 0:
                self.take(1, 1, True)
                self.take(2, 0, True)
            elif number == 1:
                self.take(1, 0, False)
                self.take(2, 1, False)
            else:
                self.take(3, 0, False)
                self.take(3, 1, False)
        elif number == 2:
            for distance in range(1, self.plane.chips):
                for half in range(2):
                    self.take(distance, half, False)

    def arrive_from(self, distance):
        if distance == 0:
            for copy in self.loads():
                copy.wait()
        for half in range(2):
            for copy in self.forward(distance, half):
                copy.wait_recv()

    def arrive(self):
        for distance in range(self.plane.chips):
            self.arrive_from(distance)

    def finish(self):
        for distance in range(self.plane.chips):
            for half in range(2):
                for copy in self.forward(distance, half):
                    copy.wait_send()
                if distance > 0:
                    for copy in self.send(distance, half):
                        copy.wait_send()


def gather_sems(arrays):
    chips = lax.axis_size("shard") * lax.axis_size("context") // 2
    return [
        pltpu.SemaphoreType.DMA((arrays, 2)),
        pltpu.SemaphoreType.DMA((arrays, chips - 1, 2)),
        pltpu.SemaphoreType.DMA((arrays, chips - 1, 2)),
        pltpu.SemaphoreType.DMA((arrays, chips, 2)),
        pltpu.SemaphoreType.DMA((arrays, chips, 2)),
    ]


GROUP = 128
TILE = 256
WIDE = 512


def middle_kernel(
    mesh_axes,
    mix_hbm,
    cotangent_ref,
    input_hbm,
    gain_ref,
    gate_hbm,
    up_hbm,
    down_hbm,
    normed_ref,
    out_ref,
    gain_grad,
    residual_hbm,
    hidden_hbm,
    grad_gate_hbm,
    grad_up_hbm,
    feed_hbm,
    grad_hbm,
    grads_hbm,
    gate_w,
    up_w,
    down_w,
    part,
    mix_arrived,
    arrived,
    inputs,
    residual,
    stage_hidden,
    stage_gate,
    stage_up,
    stage_feed,
    part_sem,
    input_sem,
    save_sem,
    stage_sem,
    grad_sem,
    back_sem,
    tile_sem,
    *sems,
):
    tokens, model_width = normed_ref.shape
    half = tokens // 2
    hidden_width = gate_hbm.shape[1]
    padded = gate_w.shape[1]
    groups = half // GROUP
    place, line_size = lax.axis_index("tensor"), lax.axis_size("tensor")
    own_half = pl.ds(pl.multiple_of(jnp.where(place == 0, 0, half), half), half)
    part_load = pltpu.make_async_copy(mix_hbm, part, part_sem.at[0])
    part_load.start()
    input_load = pltpu.make_async_copy(input_hbm.at[own_half], inputs, input_sem.at[0])
    input_load.start()
    if padded > hidden_width:
        spare = slice(hidden_width, padded)
        gate_w[:, spare] = jnp.zeros((model_width, padded - hidden_width), BF16)
        up_w[:, spare] = jnp.zeros((model_width, padded - hidden_width), BF16)
        down_w[:, spare] = jnp.zeros((model_width, padded - hidden_width), BF16)
    gain_grad[...] = jnp.zeros_like(gain_grad)

    def mix_turn(total, rows, own):
        values = inputs[own].astype(F32) + total
        residual[own] = values
        normed_ref[rows] = (values * inverse_rms(values) * gain_ref[...]).astype(BF16)

    def turn(total, rows, own):
        values = residual[own]
        inverse = inverse_rms(values)
        unit = values * inverse
        gain_grad[...] += jnp.sum(total * unit, axis=0, keepdims=True)
        lifted = total * gain_ref[...]
        mean = jnp.mean(lifted * unit, axis=-1, keepdims=True)
        grad = cotangent_ref[rows].astype(F32) + inverse * (lifted - unit * mean)
        residual[own] = grad
        out_ref[rows] = grad.astype(BF16)

    mix_line = Line(mesh_axes, part, mix_arrived, normed_ref, sems[:4], mix_turn)
    line = Line(mesh_axes, part, arrived, out_ref, sems[4:8], turn)
    gather = Gather(
        Plane(mesh_axes), (gate_hbm, up_hbm, down_hbm), (gate_w, up_w, down_w), sems[8:]
    )
    barrier = pltpu.get_barrier_semaphore()
    expected = mix_line.greet(barrier) + gather.greet(barrier)
    pl.semaphore_wait(barrier, expected)
    gather.start()
    part_load.wait()
    input_load.wait()
    pace = GROUP // CHUNK
    begin = pace + 2 * LAG * (line_size - 1) + 4
    mix_line.run(0, begin - 10)
    gather.stage(0)
    mix_line.run(begin - 10, begin - 4)
    gather.stage(1)
    mix_line.run(begin - 4, begin)
    gather.stage(2)
    gather.arrive()

    def both(ref, group):
        first = pl.ds(pl.multiple_of(group * GROUP, GROUP), GROUP)
        second = pl.ds(pl.multiple_of(half + group * GROUP, GROUP), GROUP)
        return first, second

    def stage_copies(group):
        slot = lax.rem(group, 2)
        copies = []
        for side, rows in enumerate(both(None, group)):
            from_rows = pl.ds(side * GROUP, GROUP)
            columns = pl.ds(0, hidden_width)
            for which, (stage, target) in enumerate(
                (
                    (stage_hidden, hidden_hbm),
                    (stage_gate, grad_gate_hbm),
                    (stage_up, grad_up_hbm),
                )
            ):
                copies.append(
                    pltpu.make_async_copy(
                        stage.at[slot, from_rows, columns],
                        target.at[rows],
                        stage_sem.at[slot, which, side],
                    )
                )
            copies.append(
                pltpu.make_async_copy(
                    stage_feed.at[slot, from_rows], feed_hbm.at[rows], stage_sem.at[slot, 3, side]
                )
            )
        return copies

    def hidden_tile(group, tile):
        first, second = both(normed_ref, group)
        slot = lax.rem(group, 2)
        columns = pl.ds(pl.multiple_of(tile * WIDE, WIDE), WIDE)
        rows = jnp.concatenate([normed_ref[first], normed_ref[second]], axis=0)
        gate = mm_nn(rows, gate_w[:, columns])
        up = mm_nn(rows, up_w[:, columns])
        grads = jnp.concatenate([cotangent_ref[first], cotangent_ref[second]], axis=0)
        grad = mm_nn(grads, down_w[:, columns])
        sigma = jax.nn.sigmoid(gate)
        active = gate * sigma
        stage_hidden[slot, :, columns] = (active * up).astype(BF16)
        stage_gate[slot, :, columns] = (grad * up * sigma * (1.0 + gate * (1.0 - sigma))).astype(
            BF16
        )
        stage_up[slot, :, columns] = (grad * active).astype(BF16)

    def model_tile(group, tile):
        first, second = both(part, group)
        slot = lax.rem(group, 2)
        columns = pl.ds(pl.multiple_of(tile * WIDE, WIDE), WIDE)
        back = mm_nt(stage_gate[slot], gate_w[columns, :])
        back = (back + mm_nt(stage_up[slot], up_w[columns, :])).astype(BF16)
        part[first, columns] = back[:GROUP]
        part[second, columns] = back[GROUP:]
        stage_feed[slot, :, columns] = mm_nt(stage_hidden[slot], down_w[columns, :]).astype(BF16)

    hidden_tiles, model_tiles = padded // WIDE, model_width // WIDE
    ticks = hidden_tiles + model_tiles
    piece = -(-ticks // pace)
    save = pltpu.make_async_copy(residual, residual_hbm, save_sem.at[0])

    def group_body(group, _):
        mix_line.source_sent(group * pace, (group + 1) * pace)

        @pl.when(group == 1)
        def _():
            save.start()

        @pl.when(group == 2)
        def _():
            save.wait()

        @pl.when(group >= 2)
        def _():
            for copy in stage_copies(group - 2):
                copy.wait()

        def piece_body(index, _):
            def tick_body(offset, _):
                tick = index * piece + offset

                @pl.when(tick < hidden_tiles)
                def _():
                    hidden_tile(group, tick)

                @pl.when(jnp.logical_and(tick >= hidden_tiles, tick < ticks))
                def _():
                    model_tile(group, tick - hidden_tiles)

                return 0

            lax.fori_loop(0, piece, tick_body, 0)

            mix_time = begin + group * pace + index

            @pl.when(mix_time < mix_line.steps)
            def _():
                mix_line.step(mix_time)

            @pl.when(group >= 1)
            def _():
                line.step((group - 1) * pace + index)

            return 0

        lax.fori_loop(0, pace, piece_body, 0)
        for copy in stage_copies(group):
            copy.start()
        return 0

    lax.fori_loop(0, groups, group_body, 0)
    for group in range(max(groups - 2, 0), groups):
        for copy in stage_copies(group):
            copy.wait()
    gather.finish()

    token_rows, hidden_columns = pl.ds(0, tokens), pl.ds(0, hidden_width)
    returned = [
        pltpu.make_async_copy(
            source, target.at[token_rows, hidden_columns], back_sem.at[which]
        )
        for which, (source, target) in enumerate(
            ((grad_gate_hbm, gate_w), (grad_up_hbm, up_w), (hidden_hbm, down_w))
        )
    ]
    for copy in returned:
        copy.start()
    tiles = model_width // TILE
    first_time = (groups - 1) * pace + 1
    stages = (stage_gate, stage_up, stage_hidden)

    def tile_copies(tile):
        rows = pl.ds(pl.multiple_of(tile * TILE, TILE), TILE)
        slot = lax.rem(tile, 2)
        return [
            pltpu.make_async_copy(
                stage.at[slot, pl.ds(0, TILE), hidden_columns],
                grads_hbm.at[rows, pl.ds(which * hidden_width, hidden_width)],
                tile_sem.at[slot, which],
            )
            for which, stage in enumerate(stages)
        ]

    def weight_tile(time):
        tile = time - first_time

        @pl.when(tile == 0)
        def _():
            for copy in returned:
                copy.wait()

        @pl.when(jnp.logical_and(tile >= 2, tile < tiles))
        def _():
            for copy in tile_copies(tile - 2):
                copy.wait()

        @pl.when(jnp.logical_and(tile >= 0, tile < tiles))
        def _():
            slot = lax.rem(tile, 2)
            columns = pl.ds(pl.multiple_of(tile * TILE, TILE), TILE)
            rows = normed_ref[:, columns]
            for source, right, stage in (
                (rows, gate_w, stage_gate),
                (rows, up_w, stage_up),
                (cotangent_ref[:, columns], down_w, stage_hidden),
            ):
                product = mm_tn(source, right[:tokens, :hidden_width])
                stage[slot, :TILE, :hidden_width] = product.astype(BF16)
            for copy in tile_copies(tile):
                copy.start()

    line.run((groups - 1) * pace, line.steps, weight_tile)
    grad_save = pltpu.make_async_copy(residual, grad_hbm, grad_sem.at[0])
    grad_save.start()
    for tile in range(max(tiles - 2, 0), tiles):
        for copy in tile_copies(tile):
            copy.wait()
    mix_line.finish(source_waits=False)
    line.finish()
    grad_save.wait()


def middle(mesh_axes, collective, mix, cotangent, inputs, gain, gate_w, up_w, down_w):
    tokens, model_width = mix.shape
    hidden_width = gate_w.shape[1]
    padded = -(-hidden_width // WIDE) * WIDE
    whole = pl.BlockSpec(memory_space=pltpu.VMEM)
    remote = pl.BlockSpec(memory_space=pl.ANY)
    group_rows = 2 * GROUP
    return pl.pallas_call(
        partial(middle_kernel, mesh_axes),
        in_specs=[remote, whole, remote, whole, remote, remote, remote],
        out_specs=[whole, whole, whole] + [remote] * 7,
        out_shape=[
            jax.ShapeDtypeStruct((tokens, model_width), BF16),
            jax.ShapeDtypeStruct((tokens, model_width), BF16),
            jax.ShapeDtypeStruct((1, model_width), F32),
            jax.ShapeDtypeStruct((tokens // 2, model_width), F32),
            jax.ShapeDtypeStruct((tokens, hidden_width), BF16),
            jax.ShapeDtypeStruct((tokens, hidden_width), BF16),
            jax.ShapeDtypeStruct((tokens, hidden_width), BF16),
            jax.ShapeDtypeStruct((tokens, model_width), BF16),
            jax.ShapeDtypeStruct((tokens // 2, model_width), F32),
            jax.ShapeDtypeStruct((model_width, 3 * hidden_width), BF16),
        ],
        scratch_shapes=[
            pltpu.VMEM((model_width, padded), BF16),
            pltpu.VMEM((model_width, padded), BF16),
            pltpu.VMEM((model_width, padded), BF16),
            pltpu.VMEM((tokens, model_width), BF16),
            pltpu.VMEM((tokens, model_width), BF16),
            pltpu.VMEM((tokens, model_width), BF16),
            pltpu.VMEM((tokens // 2, model_width), BF16),
            pltpu.VMEM((tokens // 2, model_width), F32),
            pltpu.VMEM((2, group_rows, padded), BF16),
            pltpu.VMEM((2, group_rows, padded), BF16),
            pltpu.VMEM((2, group_rows, padded), BF16),
            pltpu.VMEM((2, group_rows, model_width), BF16),
            pltpu.SemaphoreType.DMA((1,)),
            pltpu.SemaphoreType.DMA((1,)),
            pltpu.SemaphoreType.DMA((1,)),
            pltpu.SemaphoreType.DMA((2, 4, 2)),
            pltpu.SemaphoreType.DMA((1,)),
            pltpu.SemaphoreType.DMA((3,)),
            pltpu.SemaphoreType.DMA((2, 3)),
        ]
        + line_sems(tokens)
        + line_sems(tokens)
        + gather_sems(3),
        compiler_params=pltpu.CompilerParams(
            collective_id=collective, has_side_effects=True, vmem_limit_bytes=61 << 20
        ),
        cost_estimate=pl.CostEstimate(
            flops=tokens * model_width * hidden_width * 12,
            bytes_accessed=360_000_000,
            transcendentals=tokens * hidden_width,
        ),
        name="middle",
    )(mix, cotangent, inputs, gain, gate_w, up_w, down_w)


def output_kernel(
    mesh_axes,
    head_count,
    key_scale,
    part,
    residual,
    gated_ref,
    mix_grad_ref,
    out_full,
    lead_ref,
    starts_ref,
    run_ref,
    carry_ref,
    decay_ref,
    link_ref,
    open_ref,
    count_ref,
    keep_ref,
    flags_ref,
    gain_ref,
    normed_hbm,
    pre_hbm,
    full_hbm,
    mixed_hbm,
    out_ref,
    gain_grad,
    floor_grad,
    total_ref,
    mixer_grads_hbm,
    arrived,
    back,
    back_arrived,
    left,
    right,
    full,
    mixer_stage,
    piece_rows_scr,
    pre,
    grad_mixed,
    back_scr,
    message,
    received,
    grad_scr,
    lifted_scr,
    lowered_scr,
    moved_scr,
    value_scr,
    load_sem,
    piece_sem,
    full_sem,
    pre_sem,
    stage_sem,
    grad_send,
    grad_recv,
    *sems,
):
    tokens, model_width = left.shape
    width = gated_ref.shape[1]
    lanes = width // head_count
    state_rows = head_count * lanes
    tiles, blocks = model_width // TILE, tokens // BLOCK
    piece_rows = 2 * BLOCK
    context, context_size = lax.axis_index("context"), lax.axis_size("context")

    left_load = pltpu.make_async_copy(normed_hbm, left, load_sem.at[0])
    left_load.start()

    def piece_loads(index):
        rows = pl.ds(pl.multiple_of(index * piece_rows, piece_rows), piece_rows)
        slot = lax.rem(index, 2)
        return (
            pltpu.make_async_copy(
                pre_hbm.at[rows, pl.ds(3 * width, width)],
                piece_rows_scr.at[slot, 0],
                piece_sem.at[slot, 0],
            ),
            pltpu.make_async_copy(
                mixed_hbm.at[rows], piece_rows_scr.at[slot, 1], piece_sem.at[slot, 1]
            ),
        )

    for load in piece_loads(0):
        load.start()
    gain_grad[...] = jnp.zeros_like(gain_grad)
    floor_grad[...] = jnp.zeros_like(floor_grad)
    back_scr[...] = jnp.zeros_like(back_scr)

    def turn(total, rows, own):
        out_ref[rows] = (residual[own] + total).astype(BF16)

    def earlier(shift):
        places = {axis: lax.axis_index(axis) for axis in mesh_axes}
        places["context"] = lax.rem(context + context_size - shift, context_size)
        return tuple(places[axis] for axis in mesh_axes)

    def keep_total(total, rows, own):
        total_ref[own] = total

    line = Line(mesh_axes, part, arrived, out_ref, sems[:4], turn)
    back_line = Line(mesh_axes, back, back_arrived, None, sems[4:], keep_total, backs=False)
    barrier = pltpu.get_barrier_semaphore()
    expected = line.greet(barrier)
    for shift in range(1, context_size):
        pl.semaphore_signal(barrier, inc=1, device_id=earlier(shift), device_id_type=MESH_ID)
    pl.semaphore_wait(barrier, expected + context_size - 1)

    def tile_columns(tile):
        return pl.ds(pl.multiple_of(tile * TILE, TILE), TILE)

    def stage_copy(tile):
        rows = tile_columns(tile)
        return pltpu.make_async_copy(mixer_stage, mixer_grads_hbm.at[rows], stage_sem.at[0])

    def gate_piece(index):
        rows = pl.ds(pl.multiple_of(index * piece_rows, piece_rows), piece_rows)
        slot = lax.rem(index, 2)

        @pl.when(index + 1 < tokens // piece_rows)
        def _():
            for load in piece_loads(index + 1):
                load.start()

        for load in piece_loads(index):
            load.wait()
        grads = mm_nn(mix_grad_ref[rows], out_full[...])
        gain = gain_ref[...]
        total = jnp.zeros_like(gain)
        for head in range(head_count):
            part_of = slice(head * lanes, (head + 1) * lanes)
            gate, mixed = piece_rows_scr[slot, 0, :, part_of], piece_rows_scr[slot, 1, :, part_of]
            grad = grads[:, part_of]
            inverse = inverse_rms(mixed)
            unit = mixed * inverse
            sigma = jax.nn.sigmoid(gate)
            scaled = grad * unit
            total = total + jnp.sum(scaled * (gate * sigma), axis=0, keepdims=True)
            grad_gate = scaled * gain * sigma * (1.0 + gate * (1.0 - sigma))
            first = 3 * width + head * lanes
            right[rows, first : first + lanes] = grad_gate.astype(BF16)
            lifted = grad * gain * (gate * sigma)
            mean = jnp.mean(lifted * unit, axis=-1, keepdims=True)
            grad_in = inverse * (lifted - unit * mean) * (key_scale * keep_ref[rows])
            grad_in = grad_in.astype(BF16)
            grad_mixed[rows, part_of] = grad_in
            back_scr[head] += mm_tn(grad_in, lead_ref[rows, part_of])
        gain_grad[...] += total

    def state_copy(shift):
        return pltpu.make_async_remote_copy(
            message,
            received.at[shift - 1],
            grad_send.at[shift - 1],
            grad_recv.at[shift - 1],
            device_id=earlier(shift),
            device_id_type=MESH_ID,
        )

    def block_of(index):
        return blocks - 1 - index

    def pre_load(index):
        rows = pl.ds(pl.multiple_of(block_of(index) * BLOCK, BLOCK), BLOCK)
        slot = lax.rem(index, 2)
        return pltpu.make_async_copy(
            pre_hbm.at[rows, pl.ds(0, 3 * width)], pre.at[slot], pre_sem.at[slot]
        )

    def send_back():
        for head in range(head_count):
            rows = slice(head * lanes, (head + 1) * lanes)
            message[rows] = back_scr[head] * link_ref[0:1]
            message[state_rows + head : state_rows + head + 1] = decay_ref[head] * link_ref[0:1]
        for shift in range(1, context_size):

            @pl.when(context >= shift)
            def _(shift=shift):
                state_copy(shift).start()

        pre_load(0).start()

    def take_back():
        grad_scr[...] = jnp.zeros_like(grad_scr)
        for shift in range(1, context_size):

            @pl.when(context + shift < context_size)
            def _(shift=shift):
                state_copy(shift).wait_recv()
                for head in range(head_count):
                    value = received[shift - 1, head * lanes : (head + 1) * lanes]
                    for near in range(shift - 1):
                        value = value * received[near, state_rows + head : state_rows + head + 1]
                    grad_scr[head] += value

        for shift in range(1, context_size):

            @pl.when(context >= shift)
            def _(shift=shift):
                state_copy(shift).wait_send()

    def mixer_block(index):
        block = block_of(index)
        slot = lax.rem(index, 2)
        block_rows = pl.ds(pl.multiple_of(block * BLOCK, BLOCK), BLOCK)

        @pl.when(index + 1 < blocks)
        def _():
            pre_load(index + 1).start()

        pre_load(index).wait()
        counts, keep, flags = count_ref[block_rows], keep_ref[block_rows], flags_ref[block]
        row_ids, col_ids, linked, fresh, tail, closing = block_masks(counts, flags)
        tri = (row_ids >= col_ids).astype(BF16)
        tri_back = (row_ids <= col_ids).astype(BF16)
        query_pre = pre[slot, :, :width]
        values = pre[slot, :, 2 * width : 3 * width].astype(BF16)
        opened = open_ref[...]
        closed = jax.nn.sigmoid(-pre[slot, :, width : 2 * width])
        keys = opened * closed
        cum = split_sum(tri, jnp.log1p(-keys))
        ending = cum[BLOCK - 1 : BLOCK, :]
        rise, fall = jnp.exp(cum), jnp.exp(-cum) * keep
        shift = jnp.exp(ending - cum) * (keep * tail)
        sigma_query = jax.nn.sigmoid(query_pre)
        lifted = (query_pre * sigma_query * rise).astype(BF16)
        lowered = (keys * fall).astype(BF16)
        moved = (keys * shift).astype(BF16)
        fresh_lifted = (lifted.astype(F32) * fresh).astype(BF16)
        end_decay = jnp.exp(ending) * closing
        lead_in = jnp.exp(run_ref[block]) * (flags[1:2, 0:1] == 0).astype(F32)
        for head in range(head_count):
            part_of = slice(head * lanes, (head + 1) * lanes)
            grad_out, value = grad_mixed[block_rows, part_of], values[:, part_of]
            lift, lower, move = lifted[:, part_of], lowered[:, part_of], moved[:, part_of]
            scores = jnp.where(linked, mm_nt(lift, lower), 0.0).astype(BF16)
            pulls = jnp.where(linked, mm_nt(grad_out, value), 0.0).astype(BF16)
            state = starts_ref[block, head] + lead_in[:, part_of] * carry_ref[head]
            grad_state = grad_scr[head]
            grad_low = grad_state.astype(BF16)
            lifted_scr[:, part_of] = mm_nn(pulls, lower) + fresh * mm_nn(
                grad_out, state.astype(BF16)
            )
            lowered_scr[:, part_of] = mm_tn(pulls, lift)
            grad_moved = mm_nn(value, grad_low)
            moved_scr[:, part_of] = grad_moved
            first = 2 * width + head * lanes
            right[block_rows, first : first + lanes] = (
                mm_tn(scores, grad_out) + mm_nt(move, grad_low)
            ).astype(BF16)
            value_scr[:, part_of] = jnp.sum(
                grad_moved * move.astype(F32), axis=0, keepdims=True
            ) + end_decay[:, part_of] * jnp.sum(state * grad_state, axis=0, keepdims=True)
            grad_scr[head] = grad_state * end_decay[:, part_of] + mm_tn(
                grad_out, fresh_lifted[:, part_of]
            )
        grad_lifted, grad_lowered, grad_moved = lifted_scr[...], lowered_scr[...], moved_scr[...]
        grad_cum = (
            grad_lifted * lifted.astype(F32)
            - grad_lowered * lowered.astype(F32)
            - grad_moved * moved.astype(F32)
        )
        grad_decay = split_sum(tri_back, grad_cum) + value_scr[...]
        key_total = grad_lowered * fall + grad_moved * shift - grad_decay / (1.0 - keys)
        floor_grad[...] -= jnp.sum(key_total * closed, axis=0, keepdims=True)
        right[block_rows, :width] = (
            grad_lifted * rise * sigma_query * (1.0 + query_pre * (1.0 - sigma_query))
        ).astype(BF16)
        right[block_rows, width : 2 * width] = (
            -key_total * opened * closed * (1.0 - closed)
        ).astype(BF16)

    def full_load(tile):
        slot = lax.rem(tile, 2)
        return pltpu.make_async_copy(
            full_hbm.at[tile_columns(tile)], full.at[slot], full_sem.at[slot]
        )

    def back_tile(tile):
        @pl.when(tile + 1 < tiles)
        def _():
            full_load(tile + 1).start()

        full_load(tile).wait()
        product = mm_nt(right[...], full[lax.rem(tile, 2)])
        back[:, tile_columns(tile)] = product.astype(BF16)

    def mixer_tile(tile):
        @pl.when(tile > 0)
        def _():
            stage_copy(tile - 1).wait()

        columns = tile_columns(tile)
        rows = left[:, columns]
        for first in range(0, 4 * width, 1024):
            some = slice(first, min(first + 1024, 4 * width))
            mixer_stage[:, some] = mm_tn(rows, right[:, some]).astype(BF16)
        product = mm_tn(mix_grad_ref[:, columns], gated_ref[...])
        mixer_stage[:, 4 * width :] = product.astype(BF16)
        stage_copy(tile).start()

    send_time = tokens // piece_rows
    block_time = send_time + 2
    back_time = block_time + blocks
    tile_time = back_time + tiles
    end_time = tile_time + tiles

    def piece(time):
        @pl.when(time < send_time)
        def _():
            gate_piece(time)

        @pl.when(time == send_time)
        def _():
            send_back()

        @pl.when(time == block_time)
        def _():
            take_back()

        @pl.when(jnp.logical_and(time >= block_time, time < back_time))
        def _():
            mixer_block(time - block_time)

        @pl.when(time == back_time - 1)
        def _():
            full_load(0).start()

        @pl.when(jnp.logical_and(time >= back_time, time < tile_time))
        def _():
            back_tile(time - back_time)

        @pl.when(time == tile_time)
        def _():
            left_load.wait()

        @pl.when(jnp.logical_and(time >= tile_time, time < end_time))
        def _():
            mixer_tile(time - tile_time)

    begin = -(-tile_time // 2)
    steps = max(line.steps, begin + back_line.steps, -(-end_time // 2))

    def body(time, _):
        @pl.when(time < line.steps)
        def _():
            line.step(time)

        @pl.when(time >= begin)
        def _():
            back_line.step(time - begin)

        def pieces(offset, _):
            piece(2 * time + offset)
            return 0

        lax.fori_loop(0, 2, pieces, 0)
        return 0

    lax.fori_loop(0, steps, body, 0)
    stage_copy(tiles - 1).wait()
    line.finish()
    back_line.finish()


def output_line(mesh_axes, collective, in_vmem, in_hbm, head_count):
    part, _, gated = in_vmem[:3]
    tokens, model_width = part.shape
    width = gated.shape[1]
    lanes = width // head_count
    context_size = lax.axis_size("context")
    messages = head_count * lanes + -(-head_count // 8) * 8
    whole = pl.BlockSpec(memory_space=pltpu.VMEM)
    remote = pl.BlockSpec(memory_space=pl.ANY)
    return pl.pallas_call(
        partial(output_kernel, mesh_axes, head_count, lanes ** (-0.5)),
        in_specs=[whole] * len(in_vmem) + [remote] * len(in_hbm),
        out_specs=[whole] * 4 + [remote],
        out_shape=[
            jax.ShapeDtypeStruct((tokens, model_width), BF16),
            jax.ShapeDtypeStruct((1, lanes), F32),
            jax.ShapeDtypeStruct((1, width), F32),
            jax.ShapeDtypeStruct((tokens // 2, model_width), F32),
            jax.ShapeDtypeStruct((model_width, 5 * width), BF16),
        ],
        scratch_shapes=[
            pltpu.VMEM((tokens, model_width), BF16),
            pltpu.VMEM((tokens, model_width), BF16),
            pltpu.VMEM((tokens, model_width), BF16),
            pltpu.VMEM((tokens, model_width), BF16),
            pltpu.VMEM((tokens, 4 * width), BF16),
            pltpu.VMEM((2, TILE, 4 * width), BF16),
            pltpu.VMEM((TILE, 5 * width), BF16),
            pltpu.VMEM((2, 2, 2 * BLOCK, width), F32),
            pltpu.VMEM((2, BLOCK, 3 * width), F32),
            pltpu.VMEM((tokens, width), BF16),
            pltpu.VMEM((head_count, lanes, lanes), F32),
            pltpu.VMEM((messages, lanes), F32),
            pltpu.VMEM((context_size - 1, messages, lanes), F32),
            pltpu.VMEM((head_count, lanes, lanes), F32),
            pltpu.VMEM((BLOCK, width), F32),
            pltpu.VMEM((BLOCK, width), F32),
            pltpu.VMEM((BLOCK, width), F32),
            pltpu.VMEM((1, width), F32),
            pltpu.SemaphoreType.DMA((1,)),
            pltpu.SemaphoreType.DMA((2, 2)),
            pltpu.SemaphoreType.DMA((2,)),
            pltpu.SemaphoreType.DMA((2,)),
            pltpu.SemaphoreType.DMA((1,)),
            pltpu.SemaphoreType.DMA((context_size - 1,)),
            pltpu.SemaphoreType.DMA((context_size - 1,)),
        ]
        + line_sems(tokens)
        + line_sems(tokens, 2),
        compiler_params=pltpu.CompilerParams(
            collective_id=collective, has_side_effects=True, vmem_limit_bytes=61 << 20
        ),
        cost_estimate=pl.CostEstimate(
            flops=tokens * model_width * width * 24,
            bytes_accessed=360_000_000,
            transcendentals=tokens * width * 12,
        ),
        name="output_line",
    )(*in_vmem, *in_hbm)


def input_kernel(
    mesh_axes,
    total_ref,
    hidden_ref,
    residual_grad,
    gain_ref,
    grads_hbm,
    out_ref,
    gain_grad,
    share_query,
    share_forget,
    share_input,
    share_gate,
    share_out,
    own,
    other,
    remote,
    load_sem,
    pair_send,
    pair_recv,
    chip_send,
    chip_recv,
    *sems,
):
    plane = Plane(mesh_axes)
    chips = plane.chips
    block = own.shape[1]
    gain_grad[...] = jnp.zeros_like(gain_grad)

    def turn(total, rows, own_rows):
        total = total_ref[own_rows]
        values = hidden_ref[rows].astype(F32)
        inverse = inverse_rms(values)
        unit = values * inverse
        gain_grad[...] += jnp.sum(total * unit, axis=0, keepdims=True)
        lifted = total * gain_ref[...]
        mean = jnp.mean(lifted * unit, axis=-1, keepdims=True)
        grad = residual_grad[own_rows] + inverse * (lifted - unit * mean)
        out_ref[rows] = grad.astype(BF16)

    line = Line(mesh_axes, None, None, out_ref, sems, turn, sums=False)
    barrier = pltpu.get_barrier_semaphore()
    expected = line.greet(barrier) + plane.greet(barrier)
    pl.semaphore_wait(barrier, expected)

    def rows_of(slot, core):
        return pl.ds(pl.multiple_of((2 * plane.ahead(slot) + core) * block, block), block)

    def load(slot):
        return pltpu.make_async_copy(
            grads_hbm.at[rows_of(slot, plane.core)], own.at[slot], load_sem.at[slot]
        )

    def pair_copy(slot):
        return pltpu.make_async_remote_copy(
            grads_hbm.at[rows_of(slot, 1 - plane.core)],
            other.at[slot],
            pair_send.at[slot],
            pair_recv.at[slot],
            device_id=plane.device(plane.chip, 1 - plane.core),
            device_id_type=MESH_ID,
        )

    def chip_copy(slot):
        return pltpu.make_async_remote_copy(
            own.at[slot],
            remote.at[slot - 1],
            chip_send.at[slot - 1],
            chip_recv.at[slot - 1],
            device_id=plane.device(plane.ahead(slot), plane.core),
            device_id_type=MESH_ID,
        )

    def start(index, _):
        slot = lax.rem(index + 1, chips)
        pair_copy(slot).start()
        load(slot).start()
        return 0

    lax.fori_loop(0, chips, start, 0)
    strip = 32

    def combine(time):
        slot = lax.rem(jnp.clip(time, 0, chips - 1) + 1, chips)

        @pl.when(time < chips)
        def _():
            load(slot).wait()
            pair_copy(slot).wait_recv()

            def add(index, _):
                rows = pl.ds(pl.multiple_of(index * strip, strip), strip)
                total = own[slot, rows].astype(F32) + other[slot, rows].astype(F32)
                own[slot, rows] = total.astype(BF16)
                return 0

            lax.fori_loop(0, block // strip, add, 0)

        @pl.when(time < chips - 1)
        def _():
            chip_copy(slot).start()

    line.run(0, line.steps, combine)

    def arrive(index, _):
        chip_copy(index).wait_recv()
        return 0

    lax.fori_loop(1, chips, arrive, 0)

    def total(index, _):
        rows = pl.ds(pl.multiple_of(index * strip, strip), strip)

        for which, share in enumerate(
            (share_query, share_forget, share_input, share_gate, share_out)
        ):
            columns = pl.ds(which * share.shape[1], share.shape[1])

            def add(slot, value, columns=columns):
                return value + remote[slot, rows, columns].astype(F32)

            share[rows] = lax.fori_loop(0, chips - 1, add, own[0, rows, columns].astype(F32))
        return 0

    lax.fori_loop(0, block // strip, total, 0)

    def sent(index, _):
        pair_copy(index).wait_send()
        return 0

    lax.fori_loop(0, chips, sent, 0)

    def chip_sent(index, _):
        chip_copy(index).wait_send()
        return 0

    lax.fori_loop(1, chips, chip_sent, 0)
    line.finish()


def input_line(mesh_axes, collective, total, hidden, residual_grad, gain, grads):
    tokens, model_width = hidden.shape
    all_width = grads.shape[1]
    chips = lax.axis_size("shard") * lax.axis_size("context") // 2
    block = model_width // (2 * chips)
    whole = pl.BlockSpec(memory_space=pltpu.VMEM)
    return pl.pallas_call(
        partial(input_kernel, mesh_axes),
        in_specs=[whole] * 4 + [pl.BlockSpec(memory_space=pl.ANY)],
        out_specs=[whole] * 7,
        out_shape=[
            jax.ShapeDtypeStruct((tokens, model_width), BF16),
            jax.ShapeDtypeStruct((1, model_width), F32),
        ]
        + [jax.ShapeDtypeStruct((block, all_width // 5), F32)] * 5,
        scratch_shapes=[
            pltpu.VMEM((chips, block, all_width), BF16),
            pltpu.VMEM((chips, block, all_width), BF16),
            pltpu.VMEM((chips - 1, block, all_width), BF16),
            pltpu.SemaphoreType.DMA((chips,)),
            pltpu.SemaphoreType.DMA((chips,)),
            pltpu.SemaphoreType.DMA((chips,)),
            pltpu.SemaphoreType.DMA((chips - 1,)),
            pltpu.SemaphoreType.DMA((chips - 1,)),
        ]
        + line_sems(tokens, 2),
        compiler_params=pltpu.CompilerParams(
            collective_id=collective, has_side_effects=True, vmem_limit_bytes=58 << 20
        ),
        cost_estimate=pl.CostEstimate(
            flops=tokens * model_width * 8, bytes_accessed=360_000_000, transcendentals=0
        ),
        name="input_line",
    )(total, hidden, residual_grad, gain, grads)


def forward_kernel(
    mesh_axes,
    head_count,
    key_scale,
    hidden_ref,
    gain_ref,
    query_hbm,
    forget_hbm,
    input_hbm,
    gate_hbm,
    out_shard_ref,
    down_shard_ref,
    floor_ref,
    segments_ref,
    head_gain_ref,
    normed_hbm,
    pre_hbm,
    full_hbm,
    out_full_hbm,
    mixed_hbm,
    lead_hbm,
    start_hbm,
    gated_hbm,
    mix_hbm,
    down_turned,
    open_ref,
    count_ref,
    keep_ref,
    flags_ref,
    run_ref,
    carry_ref,
    decay_ref,
    link_ref,
    normed,
    pre,
    mine,
    out_turned,
    full,
    out_full,
    mixed,
    lead,
    starts,
    gated,
    mix,
    state_scr,
    run_scr,
    message,
    received,
    mine_sem,
    full_sem,
    save_sem,
    pre_sem,
    mix_sem,
    state_send,
    state_recv,
    *sems,
):
    plane = Plane(mesh_axes)
    chips = plane.chips
    tokens, model_width = hidden_ref.shape
    block, width = query_hbm.shape
    lanes = width // head_count
    state_rows = head_count * lanes
    context, context_size = lax.axis_index("context"), lax.axis_size("context")

    mine_loads = [
        pltpu.make_async_copy(
            ref, mine.at[:, pl.ds(which * width, width)], mine_sem.at[which]
        )
        for which, ref in enumerate((query_hbm, forget_hbm, input_hbm, gate_hbm))
    ]
    for load in mine_loads:
        load.start()
    gather = Gather(plane, (mine,), (full,), sems[:5])
    out_gather = Gather(plane, (out_turned,), (out_full,), sems[5:])

    def later(shift):
        places = {axis: lax.axis_index(axis) for axis in mesh_axes}
        places["context"] = lax.rem(context + shift, context_size)
        return tuple(places[axis] for axis in mesh_axes)

    out_turned[...] = out_shard_ref[...].T
    barrier = pltpu.get_barrier_semaphore()
    expected = gather.greet(barrier)
    for shift in range(1, context_size):
        pl.semaphore_signal(barrier, inc=1, device_id=later(shift), device_id_type=MESH_ID)
    pl.semaphore_wait(barrier, expected + context_size - 1)
    for load in mine_loads:
        load.wait()
    gather.start()
    out_gather.start()
    down_turned[...] = down_shard_ref[...].T
    for head in range(head_count):
        open_ref[:, head * lanes : (head + 1) * lanes] = 1.0 - floor_ref[head : head + 1]

    segments = segments_ref[...]
    blocks = segments.shape[0]
    block_ids = lax.broadcasted_iota(jnp.int32, segments.shape, 0)
    slot_ids = lax.broadcasted_iota(jnp.int32, segments.shape, 1)
    before = pltpu.roll(segments, 1, 1)
    wrapped = pltpu.roll(before, 1, 0)
    before = jnp.where(slot_ids == 0, wrapped, before)
    first_slot = jnp.logical_and(slot_ids == 0, block_ids == 0)
    begins = jnp.where(jnp.logical_or(first_slot, segments == before), 0.0, 1.0)
    wide_rows = lax.broadcasted_iota(jnp.int32, (BLOCK, BLOCK), 0)
    wide_columns = lax.broadcasted_iota(jnp.int32, (BLOCK, BLOCK), 1)
    within = mm_nn(begins.astype(BF16), (wide_rows <= wide_columns).astype(BF16))
    count_rows = []
    running = jnp.zeros((1, 1), F32)
    flags_ref[...] = jnp.zeros_like(flags_ref)
    for index in range(blocks):
        row = within[index : index + 1] + running
        flags_ref[index, 0:1] = row
        flags_ref[index, 1:2] = jnp.broadcast_to(running, (1, BLOCK))
        running = row[:, BLOCK - 1 : BLOCK]
        flags_ref[index, 2:3] = jnp.broadcast_to(running, (1, BLOCK))
        count_rows.append(row)
    turned_counts = jnp.concatenate(count_rows, axis=0).T
    turned_keep = (segments > 0).astype(F32).T
    for index in range(blocks):
        rows = slice(index * BLOCK, (index + 1) * BLOCK)
        count_ref[rows] = turned_counts[:, index : index + 1]
        keep_ref[rows] = turned_keep[:, index : index + 1]
    first_id = jnp.broadcast_to(segments[0:1, 0:1], (1, lanes))
    last_id = jnp.broadcast_to(segments[blocks - 1 : blocks, BLOCK - 1 : BLOCK], (1, lanes))

    def norm(index, _):
        rows = pl.ds(pl.multiple_of(index * 128, 128), 128)
        values = hidden_ref[rows].astype(F32)
        normed[rows] = (values * inverse_rms(values) * gain_ref[...]).astype(BF16)
        return 0

    lax.fori_loop(0, tokens // 128, norm, 0)

    saves = [
        pltpu.make_async_copy(source, target, save_sem.at[which])
        for which, (source, target) in enumerate(
            (
                (normed, normed_hbm),
                (out_full, out_full_hbm),
                (mixed, mixed_hbm),
                (lead, lead_hbm),
                (starts, start_hbm),
                (gated, gated_hbm),
            )
        )
    ]
    saves[0].start()
    row_tile, column_tile = 256, 512

    def pre_save(index):
        rows = pl.ds(pl.multiple_of(index * row_tile, row_tile), row_tile)
        return pltpu.make_async_copy(pre.at[rows], pre_hbm.at[rows], pre_sem.at[index])

    def depth_of(distance):
        first = 2 * gather.partner(distance) * block
        return pl.ds(pl.multiple_of(first, 2 * block), 2 * block)

    def product(distance):
        depth = depth_of(distance)

        def row_body(index, _):
            rows = pl.ds(pl.multiple_of(index * row_tile, row_tile), row_tile)
            left = normed[rows, depth]

            def column_body(column, _):
                columns = pl.ds(pl.multiple_of(column * column_tile, column_tile), column_tile)
                value = mm_nn(left, full[depth, columns])
                if distance > 0:
                    value = value + pre[rows, columns]
                pre[rows, columns] = value
                return 0

            lax.fori_loop(0, full.shape[1] // column_tile, column_body, 0)
            if distance == chips - 1:
                pre_save(index).start()
            return 0

        lax.fori_loop(0, tokens // row_tile, row_body, 0)

    def full_save(distance):
        depth = depth_of(distance)
        return pltpu.make_async_copy(full.at[depth], full_hbm.at[depth], full_sem.at[distance])

    def use(distance):
        gather.arrive_from(distance)
        full_save(distance).start()
        product(distance)

    use(0)
    gather.stage(0)
    gather.stage(1)
    if gather.relayed:
        use(1)
        use(2)
    gather.stage(2)
    if gather.relayed:
        use(3)
    else:
        for distance in range(1, chips):
            use(distance)
    out_gather.stage(0)
    out_gather.stage(1)

    state_scr[...] = jnp.zeros_like(state_scr)
    run_scr[...] = jnp.zeros_like(run_scr)

    def recur(step, _):
        rows = pl.ds(pl.multiple_of(step * BLOCK, BLOCK), BLOCK)
        counts, keep = count_ref[rows], keep_ref[rows]
        row_ids, col_ids, linked, fresh, tail, closing = block_masks(counts, flags_ref[step])
        tri = (row_ids >= col_ids).astype(BF16)
        query_pre = pre[rows, :width]
        values = pre[rows, 2 * width : 3 * width].astype(BF16)
        keys = open_ref[...] * jax.nn.sigmoid(-pre[rows, width : 2 * width])
        cum = split_sum(tri, jnp.log1p(-keys))
        ending = cum[BLOCK - 1 : BLOCK, :]
        lifted = query_pre * jax.nn.sigmoid(query_pre) * jnp.exp(cum)
        lowered = (keys * jnp.exp(-cum) * keep).astype(BF16)
        moved = (keys * jnp.exp(ending - cum) * (keep * tail)).astype(BF16)
        run = run_scr[...]
        lead[rows] = (lifted * jnp.exp(run) * (counts == 0).astype(F32)).astype(BF16)
        run_ref[step] = run
        run_scr[...] = run + ending
        fresh_lifted = (lifted * fresh).astype(BF16)
        lifted = lifted.astype(BF16)
        end_decay = jnp.exp(ending) * closing
        for head in range(head_count):
            part = slice(head * lanes, (head + 1) * lanes)
            state = state_scr[head]
            starts[step, head] = state
            scores = jnp.where(linked, mm_nt(lifted[:, part], lowered[:, part]), 0.0)
            results = mm_nn(scores.astype(BF16), values[:, part])
            results = results + mm_nt(fresh_lifted[:, part], state.astype(BF16))
            mixed[rows, part] = results * (key_scale * keep)
            state_scr[head] = state * end_decay[:, part] + mm_tn(values[:, part], moved[:, part])
        return 0

    lax.fori_loop(0, tokens // BLOCK, recur, 0)
    saves[3].start()
    saves[4].start()

    last_count = flags_ref[tokens // BLOCK - 1][2:3, 0:1]
    for head in range(head_count):
        part = slice(head * lanes, (head + 1) * lanes)
        message[head * lanes : (head + 1) * lanes] = state_scr[head]
        decay = jnp.exp(run_scr[:, part]) * (last_count == 0).astype(F32)
        decay_ref[head] = decay
        message[state_rows + 8 + head : state_rows + 9 + head] = decay
    message[state_rows : state_rows + 1] = first_id
    message[state_rows + 1 : state_rows + 2] = last_id

    def state_copy(shift):
        return pltpu.make_async_remote_copy(
            message,
            received.at[shift - 1],
            state_send.at[shift - 1],
            state_recv.at[shift - 1],
            device_id=later(shift),
            device_id_type=MESH_ID,
        )

    for shift in range(1, context_size):

        @pl.when(context + shift < context_size)
        def _(shift=shift):
            state_copy(shift).start()

    out_gather.stage(2)
    carry_ref[...] = jnp.zeros_like(carry_ref)
    link_ref[...] = jnp.zeros_like(link_ref)
    for shift in range(1, context_size):

        @pl.when(context >= shift)
        def _(shift=shift):
            state_copy(shift).wait_recv()
            linked = jnp.ones((1, lanes), F32)
            follower = first_id
            factors = [jnp.ones((1, lanes), F32)] * head_count
            for near in range(shift):
                got = received.at[near]
                linked = (got[state_rows + 1 : state_rows + 2] == follower).astype(F32)
                follower = got[state_rows : state_rows + 1]
                factors = [factor * linked for factor in factors]
                if near < shift - 1:
                    factors = [
                        factor * got[state_rows + 8 + head : state_rows + 9 + head]
                        for head, factor in enumerate(factors)
                    ]
            if shift == 1:
                link_ref[0:1] = linked
            for head in range(head_count):
                rows = slice(head * lanes, (head + 1) * lanes)
                carry_ref[head] += factors[head] * received[shift - 1, rows]

    for shift in range(1, context_size):

        @pl.when(context + shift < context_size)
        def _(shift=shift):
            state_copy(shift).wait_send()

    for distance in range(chips):
        out_gather.arrive_from(distance)
    saves[1].start()

    def mix_save(index):
        rows = pl.ds(pl.multiple_of(index * row_tile, row_tile), row_tile)
        return pltpu.make_async_copy(mix.at[rows], mix_hbm.at[rows], mix_sem.at[index])

    def project(index, _):
        rows = pl.ds(pl.multiple_of(index * row_tile, row_tile), row_tile)
        for head in range(head_count):
            part = slice(head * lanes, (head + 1) * lanes)
            carried = mm_nt(lead[rows, part], carry_ref[head].astype(BF16))
            value = mixed[rows, part] + carried * (key_scale * keep_ref[rows])
            mixed[rows, part] = value
            gate = pre[rows, 3 * width + head * lanes : 3 * width + (head + 1) * lanes]
            unit = value * inverse_rms(value)
            gated[rows, part] = (
                unit * head_gain_ref[...] * (gate * jax.nn.sigmoid(gate))
            ).astype(BF16)
        left = gated[rows]

        def column_body(column, _):
            columns = pl.ds(pl.multiple_of(column * column_tile, column_tile), column_tile)
            mix[rows, columns] = mm_nt(left, out_full[columns, :]).astype(BF16)
            return 0

        lax.fori_loop(0, model_width // column_tile, column_body, 0)
        mix_save(index).start()
        return 0

    lax.fori_loop(0, tokens // row_tile, project, 0)
    saves[2].start()
    saves[5].start()
    gather.finish()
    out_gather.finish()
    for distance in range(chips):
        full_save(distance).wait()
    for save in saves:
        save.wait()
    for index in range(tokens // row_tile):
        pre_save(index).wait()
        mix_save(index).wait()


def forward(
    mesh_axes, collective, hidden, gain, shards, out_shard, down_shard, floor, segments, head_gain
):
    tokens, model_width = hidden.shape
    block, width = shards[0].shape
    lanes = head_gain.shape[1]
    head_count = width // lanes
    all_width = width * len(shards)
    blocks = tokens // BLOCK
    context_size = lax.axis_size("context")
    chips = lax.axis_size("shard") * context_size // 2
    messages = head_count * lanes + 8 + -(-head_count // 8) * 8
    whole = pl.BlockSpec(memory_space=pltpu.VMEM)
    remote = pl.BlockSpec(memory_space=pl.ANY)
    stored = [
        ((tokens, model_width), BF16),
        ((tokens, all_width), F32),
        ((model_width, all_width), BF16),
        ((model_width, width), BF16),
        ((tokens, width), F32),
        ((tokens, width), BF16),
        ((blocks, head_count, lanes, lanes), F32),
        ((tokens, width), BF16),
        ((tokens, model_width), BF16),
    ]
    kept = [
        (down_shard.shape[::-1], BF16),
        ((1, width), F32),
        ((tokens, 1), F32),
        ((tokens, 1), F32),
        ((blocks, 8, BLOCK), F32),
        ((blocks, 1, width), F32),
        ((head_count, lanes, lanes), F32),
        ((head_count, 1, lanes), F32),
        ((8, lanes), F32),
    ]
    return pl.pallas_call(
        partial(forward_kernel, mesh_axes, head_count, lanes ** (-0.5)),
        in_specs=[whole] * 2 + [remote] * 4 + [whole] * 5,
        out_specs=[remote] * len(stored) + [whole] * len(kept),
        out_shape=[jax.ShapeDtypeStruct(shape, kind) for shape, kind in stored + kept],
        scratch_shapes=[
            pltpu.VMEM((tokens, model_width), BF16),
            pltpu.VMEM((tokens, all_width), F32),
            pltpu.VMEM((block, all_width), BF16),
            pltpu.VMEM((block, width), BF16),
            pltpu.VMEM((model_width, all_width), BF16),
            pltpu.VMEM((model_width, width), BF16),
            pltpu.VMEM((tokens, width), F32),
            pltpu.VMEM((tokens, width), BF16),
            pltpu.VMEM((blocks, head_count, lanes, lanes), F32),
            pltpu.VMEM((tokens, width), BF16),
            pltpu.VMEM((tokens, model_width), BF16),
            pltpu.VMEM((head_count, lanes, lanes), F32),
            pltpu.VMEM((1, width), F32),
            pltpu.VMEM((messages, lanes), F32),
            pltpu.VMEM((context_size - 1, messages, lanes), F32),
            pltpu.SemaphoreType.DMA((4,)),
            pltpu.SemaphoreType.DMA((chips,)),
            pltpu.SemaphoreType.DMA((6,)),
            pltpu.SemaphoreType.DMA((tokens // 256,)),
            pltpu.SemaphoreType.DMA((tokens // 256,)),
            pltpu.SemaphoreType.DMA((context_size - 1,)),
            pltpu.SemaphoreType.DMA((context_size - 1,)),
        ]
        + gather_sems(1)
        + gather_sems(1),
        compiler_params=pltpu.CompilerParams(
            collective_id=collective, has_side_effects=True, vmem_limit_bytes=56 << 20
        ),
        cost_estimate=pl.CostEstimate(
            flops=2 * tokens * model_width * all_width,
            bytes_accessed=200_000_000,
            transcendentals=tokens * width * 9,
        ),
        name="forward",
    )(hidden, gain, *shards, out_shard, down_shard, floor, segments, head_gain)


def small_sum_kernel(
    mesh_axes, value, local_ref, total_ref, near, far, near_send, near_recv, far_send, far_recv
):
    shard_size, context_size = lax.axis_size("shard"), lax.axis_size("context")
    line_size = lax.axis_size("tensor")
    group = shard_size * context_size
    place = lax.axis_index("shard") * context_size + lax.axis_index("context")
    line_place = lax.axis_index("tensor")

    def device(position, line_position):
        places = {
            "shard": position // context_size,
            "context": lax.rem(position, context_size),
            "tensor": line_position,
        }
        return tuple(places[axis] for axis in mesh_axes)

    def near_target(step):
        return device(lax.rem(place + step, group), line_place)

    def far_target(step):
        return device(place, lax.rem(line_place + step, line_size))

    def near_copy(step):
        return pltpu.make_async_remote_copy(
            value,
            near.at[step - 1],
            near_send.at[step - 1],
            near_recv.at[step - 1],
            device_id=near_target(step),
            device_id_type=MESH_ID,
        )

    def far_copy(step):
        return pltpu.make_async_remote_copy(
            local_ref,
            far.at[step - 1],
            far_send.at[step - 1],
            far_recv.at[step - 1],
            device_id=far_target(step),
            device_id_type=MESH_ID,
        )

    barrier = pltpu.get_barrier_semaphore()
    for step in range(1, group):
        pl.semaphore_signal(barrier, inc=1, device_id=near_target(step), device_id_type=MESH_ID)
    for step in range(1, line_size):
        pl.semaphore_signal(barrier, inc=1, device_id=far_target(step), device_id_type=MESH_ID)
    pl.semaphore_wait(barrier, group + line_size - 2)
    for step in range(1, group):
        near_copy(step).start()
    total = value[...]
    for step in range(1, group):
        near_copy(step).wait_recv()
        total = total + near[step - 1]
    local_ref[...] = total
    for step in range(1, line_size):
        far_copy(step).start()
    for step in range(1, line_size):
        far_copy(step).wait_recv()
        total = total + far[step - 1]
    total_ref[...] = total
    for step in range(1, group):
        near_copy(step).wait_send()
    for step in range(1, line_size):
        far_copy(step).wait_send()


def small_sum(mesh_axes, collective, values):
    flat = jnp.concatenate([value.reshape(-1) for value in values])
    lanes = -(-flat.shape[0] // 1024) * 128
    flat = jnp.pad(flat, (0, 8 * lanes - flat.shape[0])).reshape(8, lanes)
    group = lax.axis_size("shard") * lax.axis_size("context")
    line_size = lax.axis_size("tensor")
    whole = pl.BlockSpec(memory_space=pltpu.VMEM)
    local, total = pl.pallas_call(
        partial(small_sum_kernel, mesh_axes),
        in_specs=[whole],
        out_specs=[whole] * 2,
        out_shape=[jax.ShapeDtypeStruct((8, lanes), F32)] * 2,
        scratch_shapes=[
            pltpu.VMEM((group - 1, 8, lanes), F32),
            pltpu.VMEM((line_size - 1, 8, lanes), F32),
            pltpu.SemaphoreType.DMA((group - 1,)),
            pltpu.SemaphoreType.DMA((group - 1,)),
            pltpu.SemaphoreType.DMA((line_size - 1,)),
            pltpu.SemaphoreType.DMA((line_size - 1,)),
        ],
        compiler_params=pltpu.CompilerParams(collective_id=collective, has_side_effects=True),
        cost_estimate=pl.CostEstimate(
            flops=8 * lanes * group, bytes_accessed=20_000_000, transcendentals=0
        ),
        name="small_sum",
    )(flat)
    return local.reshape(-1), total.reshape(-1)


def local(
    mesh_axes,
    hidden,
    segment_ids,
    norm1_gain,
    w_query,
    w_forget,
    w_input,
    w_gate_out,
    forget_floor,
    head_gain,
    w_out,
    norm2_gain,
    w_ffn_gate,
    w_ffn_up,
    w_ffn_down,
    out_grad,
):
    sequences, span_len, model_width = hidden.shape
    tokens = sequences * span_len
    head_count, key_dim = forget_floor.shape
    width = head_count * key_dim
    key_scale = key_dim ** (-0.5)
    both = ("shard", "context")
    gain_one, gain_two = norm1_gain.reshape(1, -1), norm2_gain.reshape(1, -1)
    hidden_rows = hidden.reshape(tokens, model_width)
    gain_row = head_gain.reshape(1, -1)
    segments = segment_ids.reshape(tokens // BLOCK, BLOCK).astype(F32)
    (
        normed_one,
        pre,
        mixer_full,
        out_full,
        mixed,
        lead,
        starts,
        gated_low,
        mix_part,
        down_turned,
        open_part,
        counts,
        keep,
        flags,
        runs,
        carry,
        decay,
        link,
    ) = forward(
        mesh_axes,
        4,
        hidden_rows,
        gain_one,
        (w_query, w_forget, w_input, w_gate_out),
        w_out,
        w_ffn_down,
        forget_floor,
        segments,
        gain_row,
    )
    grad_rows = out_grad.reshape(tokens, model_width)
    (
        _,
        grad_mix_low,
        grad_norm_two,
        residual,
        _,
        _,
        _,
        feed_part,
        grad_residual,
        grads_ffn,
    ) = middle(
        mesh_axes,
        2,
        mix_part,
        grad_rows,
        hidden_rows,
        gain_two,
        w_ffn_gate,
        w_ffn_up,
        down_turned,
    )
    (
        output_rows,
        grad_head_part,
        grad_floor_part,
        back_one,
        grads_mixer,
    ) = output_line(
        mesh_axes,
        1,
        (
            feed_part,
            residual,
            gated_low,
            grad_mix_low,
            out_full,
            lead,
            starts,
            runs,
            carry,
            decay,
            link,
            open_part,
            counts,
            keep,
            flags,
            gain_row,
        ),
        (normed_one, pre, mixer_full, mixed),
        head_count,
    )
    share_ffn = lax.psum_scatter(grads_ffn, both, scatter_dimension=0, tiled=True)
    hidden_width = w_ffn_gate.shape[1]

    def ffn_share(which):
        return share_ffn[:, which * hidden_width : (which + 1) * hidden_width].astype(F32)

    input_rows, grad_norm_one, *mixer_shares, share_out = input_line(
        mesh_axes, 3, back_one, hidden_rows, grad_residual, gain_one, grads_mixer
    )
    near, total = small_sum(
        mesh_axes, 5, (grad_norm_one, grad_norm_two, grad_head_part, grad_floor_part)
    )
    shares = lax.axis_size("shard") * lax.axis_size("context")
    position = lax.axis_index("shard") * lax.axis_size("context") + lax.axis_index("context")

    def own_slice(values, first, length):
        values = values[first : first + length].reshape(shares, length // shares)
        return lax.dynamic_index_in_dim(values, position, 0, False)

    floor_total = near[2 * model_width + key_dim : 2 * model_width + key_dim + width]
    floor_total = floor_total.reshape(head_count, shares, key_dim // shares)

    return (
        output_rows.reshape(hidden.shape),
        input_rows.reshape(hidden.shape),
        own_slice(total, 0, model_width),
        *mixer_shares,
        lax.dynamic_index_in_dim(floor_total, position, 1, False),
        own_slice(total, 2 * model_width, key_dim),
        share_out.T,
        own_slice(total, model_width, model_width),
        ffn_share(0),
        ffn_share(1),
        ffn_share(2).T,
    )


def solution(mesh):
    in_specs = (
        P("shard", "context", None),
        P("shard", "context"),
        P(),
        P(("shard", "context"), "tensor"),
        P(("shard", "context"), "tensor"),
        P(("shard", "context"), "tensor"),
        P(("shard", "context"), "tensor"),
        P("tensor", None),
        P(),
        P("tensor", ("shard", "context")),
        P(),
        P(("shard", "context"), "tensor"),
        P(("shard", "context"), "tensor"),
        P("tensor", ("shard", "context")),
        P("shard", "context", None),
    )
    out_specs = (
        P("shard", "context", None),
        P("shard", "context", None),
        P(("shard", "context")),
        P(("shard", "context"), "tensor"),
        P(("shard", "context"), "tensor"),
        P(("shard", "context"), "tensor"),
        P(("shard", "context"), "tensor"),
        P("tensor", ("shard", "context")),
        P(("shard", "context")),
        P("tensor", ("shard", "context")),
        P(("shard", "context")),
        P(("shard", "context"), "tensor"),
        P(("shard", "context"), "tensor"),
        P("tensor", ("shard", "context")),
    )
    return jax.shard_map(
        partial(local, mesh.axis_names), mesh=mesh, in_specs=in_specs, out_specs=out_specs, check_vma=False)
```

```python
from functools import partial

import jax
import jax.numpy as jnp
from jax import lax
from jax.experimental import pallas as pl
from jax.experimental.pallas import tpu as pltpu
from jax.sharding import PartitionSpec as P

EPSILON = 1e-05


BLOCK = 128
F32 = jnp.float32
BF16 = jnp.bfloat16


def mm(a, b, dims):
    return lax.dot_general(a, b, (dims, ((), ())), preferred_element_type=F32)


def mm_nn(a, b):
    return mm(a, b, ((1,), (0,)))


def mm_nt(a, b):
    return mm(a, b, ((1,), (1,)))


def mm_tn(a, b):
    return mm(a, b, ((0,), (0,)))


def split_sum(tri, values):
    high = values.astype(BF16)
    low = (values - high.astype(F32)).astype(BF16)
    return mm_nn(tri, high) + mm_nn(tri, low)


def block_masks(counts, flags_row):
    rows = counts.shape[0]
    row_ids = lax.broadcasted_iota(jnp.int32, (rows, rows), 0)
    col_ids = lax.broadcasted_iota(jnp.int32, (rows, rows), 1)
    linked = jnp.logical_and(counts == flags_row[0:1], row_ids >= col_ids)
    fresh = (counts == flags_row[1:2, 0:1]).astype(F32)
    tail = (counts == flags_row[2:3, 0:1]).astype(F32)
    closing = (flags_row[1:2, 0:1] == flags_row[2:3, 0:1]).astype(F32)
    return row_ids, col_ids, linked, fresh, tail, closing


CHUNK = 32
QUIET, MANY = 6, 2
LAG = 2
MESH_ID = pl.DeviceIdType.MESH


class Line:
    def __init__(self, mesh_axes, part, arrived, out, sems, transform, sums=True, backs=True):
        self.mesh_axes = mesh_axes
        self.sums, self.backs = sums, backs
        self.part, self.arrived, self.out = part, arrived, out
        if sums:
            self.sum_send, self.sum_recv = sems[:2]
        if backs:
            self.back_send, self.back_recv = sems[-2:]
        self.transform = transform
        self.half = (part if sums else out).shape[0] // 2
        self.chunks = self.half // CHUNK
        self.size = lax.axis_size("tensor")
        self.place = lax.axis_index("tensor")
        self.lines = ((self.size - 1 - self.place, -1), (self.place, 1))
        self.offset = LAG * (self.size - 1) if sums else 0
        self.steps = self.chunks + self.offset + (LAG * (self.size - 1) if backs else 0)

    def device(self, position):
        return tuple(
            jnp.clip(position, 0, self.size - 1) if axis == "tensor" else lax.axis_index(axis)
            for axis in self.mesh_axes
        )

    def greet(self, barrier):
        for step in (-1, 1):
            inside = jnp.logical_and(self.place + step >= 0, self.place + step < self.size)

            @pl.when(inside)
            def _(step=step):
                pl.semaphore_signal(
                    barrier, inc=1, device_id=self.device(self.place + step), device_id_type=MESH_ID
                )

        at_end = jnp.logical_or(self.place == 0, self.place == self.size - 1)
        return jnp.where(at_end, 1, 2)

    def rows_of(self, side, index):
        return pl.ds(pl.multiple_of(side * self.half + index * CHUNK, CHUNK), CHUNK)

    def sum_copy(self, side, index, source):
        rows = self.rows_of(side, index)
        return pltpu.make_async_remote_copy(
            source.at[rows],
            self.arrived.at[rows],
            self.sum_send.at[side, index],
            self.sum_recv.at[side, index],
            device_id=self.device(self.place + self.lines[side][1]),
            device_id_type=MESH_ID,
        )

    def back_copy(self, side, index):
        rows = self.rows_of(side, index)
        return pltpu.make_async_remote_copy(
            self.out.at[rows],
            self.out.at[rows],
            self.back_send.at[side, index],
            self.back_recv.at[side, index],
            device_id=self.device(self.place - self.lines[side][1]),
            device_id_type=MESH_ID,
        )

    def step(self, time):
        for side in (0, 1):
            hops = self.lines[side][0]
            at_source, at_owner = hops == 0, hops == self.size - 1
            if self.sums:
                self.sum_step(time, side, hops, at_source, at_owner)
            if self.backs:
                self.back_step(time, side, hops, at_owner)

    def sum_step(self, time, side, hops, at_source, at_owner):
        index = time - LAG * hops
        valid = jnp.logical_and(index >= 0, index < self.chunks)
        index = jnp.clip(index, 0, self.chunks - 1)
        rows = self.rows_of(side, index)

        @pl.when(jnp.logical_and(valid, at_source))
        def _():
            self.sum_copy(side, index, self.part).start()

        @pl.when(jnp.logical_and(valid, jnp.logical_not(at_source)))
        def _():
            self.sum_copy(side, index, self.arrived).wait_recv()

        between = jnp.logical_and(jnp.logical_not(at_source), jnp.logical_not(at_owner))

        @pl.when(jnp.logical_and(valid, between))
        def _():
            total = self.part[rows].astype(F32) + self.arrived[rows].astype(F32)
            self.arrived[rows] = total.astype(BF16)
            self.sum_copy(side, index, self.arrived).start()

        @pl.when(jnp.logical_and(valid, at_owner))
        def _():
            total = self.part[rows].astype(F32) + self.arrived[rows].astype(F32)
            self.turn(total, side, index)

    def turn(self, total, side, index):
        own = pl.ds(pl.multiple_of(index * CHUNK, CHUNK), CHUNK)
        self.transform(total, self.rows_of(side, index), own)
        if self.backs:
            self.back_copy(side, index).start()

    def back_step(self, time, side, hops, at_owner):
        if not self.sums:

            @pl.when(jnp.logical_and(at_owner, time < self.chunks))
            def _():
                self.turn(None, side, jnp.clip(time, 0, self.chunks - 1))

        away = self.size - 1 - hops
        index = time - self.offset - LAG * away
        valid = jnp.logical_and(jnp.logical_and(index >= 0, index < self.chunks), away > 0)
        index = jnp.clip(index, 0, self.chunks - 1)

        @pl.when(valid)
        def _():
            self.back_copy(side, index).wait_recv()

        @pl.when(jnp.logical_and(valid, away < self.size - 1))
        def _():
            self.back_copy(side, index).start()

    def run(self, first, last, beside=None):
        def body(time, _):
            self.step(time)
            if beside is not None:
                beside(time)
            return 0

        lax.fori_loop(first, last, body, 0)

    def source_sent(self, first, last):
        def body(index, _):
            for side in (0, 1):

                @pl.when(self.lines[side][0] == 0)
                def _(side=side):
                    self.sum_copy(side, index, self.part).wait_send()

            return 0

        lax.fori_loop(first, last, body, 0)

    def finish(self, source_waits=True):
        def body(index, _):
            for side in (0, 1):
                hops = self.lines[side][0]
                passed = hops < self.size - 1
                if not source_waits:
                    passed = jnp.logical_and(passed, hops > 0)

                if self.sums:

                    @pl.when(passed)
                    def _(side=side):
                        self.sum_copy(side, index, self.arrived).wait_send()

                if self.backs:

                    @pl.when(hops > 0)
                    def _(side=side):
                        self.back_copy(side, index).wait_send()

            return 0

        lax.fori_loop(0, self.chunks, body, 0)


def line_sems(tokens, count=4):
    return [pltpu.SemaphoreType.DMA((2, tokens // 2 // CHUNK))] * count


def inverse_rms(values):
    return lax.rsqrt(jnp.mean(values * values, axis=-1, keepdims=True) + EPSILON)


class Plane:
    def __init__(self, mesh_axes):
        self.mesh_axes = mesh_axes
        self.context = lax.axis_size("context")
        self.per_row = self.context // 2
        self.chips = lax.axis_size("shard") * self.per_row
        context_place = lax.axis_index("context")
        self.core = lax.rem(context_place, 2)
        self.chip = lax.axis_index("shard") * self.per_row + context_place // 2

    def device(self, chip, core):
        places = {
            "shard": chip // self.per_row,
            "context": 2 * lax.rem(chip, self.per_row) + core,
            "tensor": lax.axis_index("tensor"),
        }
        return tuple(places[axis] for axis in self.mesh_axes)

    def ahead(self, distance):
        return lax.rem(self.chip + distance, self.chips)

    def greet(self, barrier):
        targets = [self.device(self.chip, 1 - self.core)]
        targets += [self.device(self.ahead(step), self.core) for step in range(1, self.chips)]
        for target in targets:
            pl.semaphore_signal(barrier, inc=1, device_id=target, device_id_type=MESH_ID)
        return len(targets)


class Gather:
    def __init__(self, plane, sources, targets, sems):
        self.plane, self.sources, self.targets = plane, sources, targets
        self.load_sem, self.send_sem, self.recv_sem, self.pair_send, self.pair_recv = sems
        self.block = sources[0].shape[0]
        self.part = self.block // 2
        self.relayed = plane.chips == 4
        self.arrays = range(len(sources))

    def partner(self, distance):
        return jnp.bitwise_xor(self.plane.chip, distance)

    def greet(self, barrier):
        plane = self.plane
        targets = [plane.device(plane.chip, 1 - plane.core)]
        targets += [
            plane.device(self.partner(step), plane.core)
            for step in range(1, 3 if self.relayed else plane.chips)
        ]
        for target in targets:
            pl.semaphore_signal(barrier, inc=1, device_id=target, device_id_type=MESH_ID)
        return len(targets)

    def place(self, array, chip, core, half):
        first = (2 * chip + core) * self.block + half * self.part
        rows = pl.ds(pl.multiple_of(first, self.part), self.part)
        return self.targets[array].at[rows, pl.ds(0, self.sources[array].shape[1])]

    def mine(self, array, half):
        return self.sources[array].at[pl.ds(half * self.part, self.part)]

    def loads(self):
        plane = self.plane
        return [
            pltpu.make_async_copy(
                self.mine(array, half),
                self.place(array, plane.chip, plane.core, half),
                self.load_sem.at[array, half],
            )
            for array in self.arrays
            for half in range(2)
        ]

    def send(self, distance, half):
        plane = self.plane
        copies = []
        for array in self.arrays:
            chip, target = plane.chip, self.partner(distance)
            source = self.mine(array, half)
            if self.relayed and distance == 3:
                chip = self.partner(2 if half == 0 else 1)
                target = self.partner(1 if half == 0 else 2)
                source = self.place(array, chip, plane.core, half)
            copies.append(
                pltpu.make_async_remote_copy(
                    source,
                    self.place(array, chip, plane.core, half),
                    self.send_sem.at[array, distance - 1, half],
                    self.recv_sem.at[array, distance - 1, half],
                    device_id=plane.device(target, plane.core),
                    device_id_type=MESH_ID,
                )
            )
        return copies

    def forward(self, distance, half):
        plane = self.plane
        copies = []
        for array in self.arrays:
            place = self.place(array, self.partner(distance), plane.core, half)
            copies.append(
                pltpu.make_async_remote_copy(
                    self.mine(array, half) if distance == 0 else place,
                    place,
                    self.pair_send.at[array, distance, half],
                    self.pair_recv.at[array, distance, half],
                    device_id=plane.device(plane.chip, 1 - plane.core),
                    device_id_type=MESH_ID,
                )
            )
        return copies

    def start(self):
        if self.relayed:
            order = ((1, 1), (2, 0), (1, 0), (2, 1))
        else:
            order = [(step, half) for step in range(1, self.plane.chips) for half in range(2)]
        for distance, half in order:
            for copy in self.send(distance, half):
                copy.start()
        for copy in self.loads():
            copy.start()
        for half in range(2):
            for copy in self.forward(0, half):
                copy.start()

    def take(self, distance, half, relay):
        for copy in self.send(distance, half):
            copy.wait_recv()
        if relay:
            for copy in self.send(3, half):
                copy.start()
        for copy in self.forward(distance, half):
            copy.start()

    def stage(self, number):
        if self.relayed:
            if number == 0:
                self.take(1, 1, True)
                self.take(2, 0, True)
            elif number == 1:
                self.take(1, 0, False)
                self.take(2, 1, False)
            else:
                self.take(3, 0, False)
                self.take(3, 1, False)
        elif number == 2:
            for distance in range(1, self.plane.chips):
                for half in range(2):
                    self.take(distance, half, False)

    def arrive_from(self, distance):
        if distance == 0:
            for copy in self.loads():
                copy.wait()
        for half in range(2):
            for copy in self.forward(distance, half):
                copy.wait_recv()

    def arrive(self):
        for distance in range(self.plane.chips):
            self.arrive_from(distance)

    def finish(self):
        for distance in range(self.plane.chips):
            for half in range(2):
                for copy in self.forward(distance, half):
                    copy.wait_send()
                if distance > 0:
                    for copy in self.send(distance, half):
                        copy.wait_send()


def gather_sems(arrays):
    chips = lax.axis_size("shard") * lax.axis_size("context") // 2
    return [
        pltpu.SemaphoreType.DMA((arrays, 2)),
        pltpu.SemaphoreType.DMA((arrays, chips - 1, 2)),
        pltpu.SemaphoreType.DMA((arrays, chips - 1, 2)),
        pltpu.SemaphoreType.DMA((arrays, chips, 2)),
        pltpu.SemaphoreType.DMA((arrays, chips, 2)),
    ]


GROUP = 128
TILE = 256
WIDE = 512


def middle_kernel(
    mesh_axes,
    mix_hbm,
    cotangent_hbm,
    input_hbm,
    gain_ref,
    gate_hbm,
    up_hbm,
    down_hbm,
    out_ref,
    gain_grad,
    residual_hbm,
    hidden_hbm,
    grad_gate_hbm,
    grad_up_hbm,
    feed_hbm,
    grad_hbm,
    grads_hbm,
    normed_ref,
    cotangent_ref,
    gate_w,
    up_w,
    down_w,
    part,
    mix_arrived,
    arrived,
    inputs,
    residual,
    stage_hidden,
    stage_gate,
    stage_up,
    stage_feed,
    part_sem,
    input_sem,
    save_sem,
    stage_sem,
    grad_sem,
    back_sem,
    tile_sem,
    *sems,
):
    tokens, model_width = normed_ref.shape
    half = tokens // 2
    hidden_width = gate_hbm.shape[1]
    padded = gate_w.shape[1]
    groups = half // GROUP
    place, line_size = lax.axis_index("tensor"), lax.axis_size("tensor")
    own_half = pl.ds(pl.multiple_of(jnp.where(place == 0, 0, half), half), half)
    part_load = pltpu.make_async_copy(mix_hbm, part, part_sem.at[0])
    part_load.start()
    input_load = pltpu.make_async_copy(input_hbm.at[own_half], inputs, input_sem.at[0])
    input_load.start()
    cotangent_load = pltpu.make_async_copy(cotangent_hbm, cotangent_ref, input_sem.at[1])
    cotangent_load.start()
    if padded > hidden_width:
        spare = slice(hidden_width, padded)
        gate_w[:, spare] = jnp.zeros((model_width, padded - hidden_width), BF16)
        up_w[:, spare] = jnp.zeros((model_width, padded - hidden_width), BF16)
        down_w[:, spare] = jnp.zeros((model_width, padded - hidden_width), BF16)
    gain_grad[...] = jnp.zeros_like(gain_grad)

    def mix_turn(total, rows, own):
        values = inputs[own].astype(F32) + total
        residual[own] = values
        normed_ref[rows] = (values * inverse_rms(values) * gain_ref[...]).astype(BF16)

    def turn(total, rows, own):
        values = residual[own]
        inverse = inverse_rms(values)
        unit = values * inverse
        gain_grad[...] += jnp.sum(total * unit, axis=0, keepdims=True)
        lifted = total * gain_ref[...]
        mean = jnp.mean(lifted * unit, axis=-1, keepdims=True)
        grad = cotangent_ref[rows].astype(F32) + inverse * (lifted - unit * mean)
        residual[own] = grad
        out_ref[rows] = grad.astype(BF16)

    mix_line = Line(mesh_axes, part, mix_arrived, normed_ref, sems[:4], mix_turn)
    line = Line(mesh_axes, part, arrived, out_ref, sems[4:8], turn)
    gather = Gather(
        Plane(mesh_axes), (gate_hbm, up_hbm, down_hbm), (gate_w, up_w, down_w), sems[8:]
    )
    barrier = pltpu.get_barrier_semaphore()
    expected = mix_line.greet(barrier) + gather.greet(barrier)
    pl.semaphore_wait(barrier, expected)
    gather.start()
    part_load.wait()
    input_load.wait()
    pace = GROUP // CHUNK
    begin = pace + 2 * LAG * (line_size - 1) + 4
    mix_line.run(0, begin - 10)
    gather.stage(0)
    mix_line.run(begin - 10, begin - 4)
    gather.stage(1)
    mix_line.run(begin - 4, begin)
    gather.stage(2)
    gather.arrive()
    cotangent_load.wait()

    def both(ref, group):
        first = pl.ds(pl.multiple_of(group * GROUP, GROUP), GROUP)
        second = pl.ds(pl.multiple_of(half + group * GROUP, GROUP), GROUP)
        return first, second

    def stage_copies(group):
        slot = lax.rem(group, 2)
        copies = []
        for side, rows in enumerate(both(None, group)):
            from_rows = pl.ds(side * GROUP, GROUP)
            columns = pl.ds(0, hidden_width)
            for which, (stage, target) in enumerate(
                (
                    (stage_hidden, hidden_hbm),
                    (stage_gate, grad_gate_hbm),
                    (stage_up, grad_up_hbm),
                )
            ):
                copies.append(
                    pltpu.make_async_copy(
                        stage.at[slot, from_rows, columns],
                        target.at[rows],
                        stage_sem.at[slot, which, side],
                    )
                )
            copies.append(
                pltpu.make_async_copy(
                    stage_feed.at[slot, from_rows], feed_hbm.at[rows], stage_sem.at[slot, 3, side]
                )
            )
        return copies

    def hidden_tile(group, tile):
        first, second = both(normed_ref, group)
        slot = lax.rem(group, 2)
        columns = pl.ds(pl.multiple_of(tile * WIDE, WIDE), WIDE)
        rows = jnp.concatenate([normed_ref[first], normed_ref[second]], axis=0)
        gate = mm_nn(rows, gate_w[:, columns])
        up = mm_nn(rows, up_w[:, columns])
        grads = jnp.concatenate([cotangent_ref[first], cotangent_ref[second]], axis=0)
        grad = mm_nn(grads, down_w[:, columns])
        sigma = jax.nn.sigmoid(gate)
        active = gate * sigma
        stage_hidden[slot, :, columns] = (active * up).astype(BF16)
        stage_gate[slot, :, columns] = (grad * up * sigma * (1.0 + gate * (1.0 - sigma))).astype(
            BF16
        )
        stage_up[slot, :, columns] = (grad * active).astype(BF16)

    def model_tile(group, tile):
        first, second = both(part, group)
        slot = lax.rem(group, 2)
        columns = pl.ds(pl.multiple_of(tile * WIDE, WIDE), WIDE)
        back = mm_nt(stage_gate[slot], gate_w[columns, :])
        back = (back + mm_nt(stage_up[slot], up_w[columns, :])).astype(BF16)
        part[first, columns] = back[:GROUP]
        part[second, columns] = back[GROUP:]
        stage_feed[slot, :, columns] = mm_nt(stage_hidden[slot], down_w[columns, :]).astype(BF16)

    hidden_tiles, model_tiles = padded // WIDE, model_width // WIDE
    ticks = hidden_tiles + model_tiles
    piece = -(-ticks // pace)
    save = pltpu.make_async_copy(residual, residual_hbm, save_sem.at[0])

    def group_body(group, _):
        mix_line.source_sent(group * pace, (group + 1) * pace)

        @pl.when(group == 1)
        def _():
            save.start()

        @pl.when(group == 2)
        def _():
            save.wait()

        @pl.when(group >= 2)
        def _():
            for copy in stage_copies(group - 2):
                copy.wait()

        def piece_body(index, _):
            def tick_body(offset, _):
                tick = index * piece + offset

                @pl.when(tick < hidden_tiles)
                def _():
                    hidden_tile(group, tick)

                @pl.when(jnp.logical_and(tick >= hidden_tiles, tick < ticks))
                def _():
                    model_tile(group, tick - hidden_tiles)

                return 0

            lax.fori_loop(0, piece, tick_body, 0)

            mix_time = begin + group * pace + index

            @pl.when(mix_time < mix_line.steps)
            def _():
                mix_line.step(mix_time)

            @pl.when(group >= 1)
            def _():
                line.step((group - 1) * pace + index)

            return 0

        lax.fori_loop(0, pace, piece_body, 0)
        for copy in stage_copies(group):
            copy.start()
        return 0

    lax.fori_loop(0, groups, group_body, 0)
    for group in range(max(groups - 2, 0), groups):
        for copy in stage_copies(group):
            copy.wait()
    gather.finish()

    token_rows, hidden_columns = pl.ds(0, tokens), pl.ds(0, hidden_width)
    returned = [
        pltpu.make_async_copy(
            source, target.at[token_rows, hidden_columns], back_sem.at[which]
        )
        for which, (source, target) in enumerate(
            ((grad_gate_hbm, gate_w), (grad_up_hbm, up_w), (hidden_hbm, down_w))
        )
    ]
    for copy in returned:
        copy.start()
    tiles = model_width // TILE
    first_time = (groups - 1) * pace + 1
    stages = (stage_gate, stage_up, stage_hidden)

    def tile_copies(tile):
        rows = pl.ds(pl.multiple_of(tile * TILE, TILE), TILE)
        slot = lax.rem(tile, 2)
        return [
            pltpu.make_async_copy(
                stage.at[slot, pl.ds(0, TILE), hidden_columns],
                grads_hbm.at[rows, pl.ds(which * hidden_width, hidden_width)],
                tile_sem.at[slot, which],
            )
            for which, stage in enumerate(stages)
        ]

    def weight_tile(time):
        tile = time - first_time

        @pl.when(tile == 0)
        def _():
            for copy in returned:
                copy.wait()

        @pl.when(jnp.logical_and(tile >= 2, tile < tiles))
        def _():
            for copy in tile_copies(tile - 2):
                copy.wait()

        @pl.when(jnp.logical_and(tile >= 0, tile < tiles))
        def _():
            slot = lax.rem(tile, 2)
            columns = pl.ds(pl.multiple_of(tile * TILE, TILE), TILE)
            rows = normed_ref[:, columns]
            for source, right, stage in (
                (rows, gate_w, stage_gate),
                (rows, up_w, stage_up),
                (cotangent_ref[:, columns], down_w, stage_hidden),
            ):
                product = mm_tn(source, right[:tokens, :hidden_width])
                stage[slot, :TILE, :hidden_width] = product.astype(BF16)
            for copy in tile_copies(tile):
                copy.start()

    line.run((groups - 1) * pace, line.steps, weight_tile)
    grad_save = pltpu.make_async_copy(residual, grad_hbm, grad_sem.at[0])
    grad_save.start()
    for tile in range(max(tiles - 2, 0), tiles):
        for copy in tile_copies(tile):
            copy.wait()
    mix_line.finish(source_waits=False)
    line.finish()
    grad_save.wait()


def middle(mesh_axes, collective, mix, cotangent, inputs, gain, gate_w, up_w, down_w):
    tokens, model_width = mix.shape
    hidden_width = gate_w.shape[1]
    padded = -(-hidden_width // WIDE) * WIDE
    whole = pl.BlockSpec(memory_space=pltpu.VMEM)
    remote = pl.BlockSpec(memory_space=pl.ANY)
    group_rows = 2 * GROUP
    return pl.pallas_call(
        partial(middle_kernel, mesh_axes),
        in_specs=[remote, remote, remote, whole, remote, remote, remote],
        out_specs=[whole, whole] + [remote] * 7,
        out_shape=[
            jax.ShapeDtypeStruct((tokens, model_width), BF16),
            jax.ShapeDtypeStruct((1, model_width), F32),
            jax.ShapeDtypeStruct((tokens // 2, model_width), F32),
            jax.ShapeDtypeStruct((tokens, hidden_width), BF16),
            jax.ShapeDtypeStruct((tokens, hidden_width), BF16),
            jax.ShapeDtypeStruct((tokens, hidden_width), BF16),
            jax.ShapeDtypeStruct((tokens, model_width), BF16),
            jax.ShapeDtypeStruct((tokens // 2, model_width), F32),
            jax.ShapeDtypeStruct((model_width, 3 * hidden_width), BF16),
        ],
        scratch_shapes=[
            pltpu.VMEM((tokens, model_width), BF16),
            pltpu.VMEM((tokens, model_width), BF16),
            pltpu.VMEM((model_width, padded), BF16),
            pltpu.VMEM((model_width, padded), BF16),
            pltpu.VMEM((model_width, padded), BF16),
            pltpu.VMEM((tokens, model_width), BF16),
            pltpu.VMEM((tokens, model_width), BF16),
            pltpu.VMEM((tokens, model_width), BF16),
            pltpu.VMEM((tokens // 2, model_width), BF16),
            pltpu.VMEM((tokens // 2, model_width), F32),
            pltpu.VMEM((2, group_rows, padded), BF16),
            pltpu.VMEM((2, group_rows, padded), BF16),
            pltpu.VMEM((2, group_rows, padded), BF16),
            pltpu.VMEM((2, group_rows, model_width), BF16),
            pltpu.SemaphoreType.DMA((1,)),
            pltpu.SemaphoreType.DMA((2,)),
            pltpu.SemaphoreType.DMA((1,)),
            pltpu.SemaphoreType.DMA((2, 4, 2)),
            pltpu.SemaphoreType.DMA((1,)),
            pltpu.SemaphoreType.DMA((3,)),
            pltpu.SemaphoreType.DMA((2, 3)),
        ]
        + line_sems(tokens)
        + line_sems(tokens)
        + gather_sems(3),
        compiler_params=pltpu.CompilerParams(
            collective_id=collective, has_side_effects=True, vmem_limit_bytes=61 << 20
        ),
        cost_estimate=pl.CostEstimate(
            flops=tokens * model_width * hidden_width * 12,
            bytes_accessed=360_000_000,
            transcendentals=tokens * hidden_width,
        ),
        name="middle",
    )(mix, cotangent, inputs, gain, gate_w, up_w, down_w)


def output_kernel(
    mesh_axes,
    head_count,
    key_scale,
    run_ref,
    carry_ref,
    decay_ref,
    link_ref,
    open_ref,
    count_ref,
    keep_ref,
    flags_ref,
    gain_ref,
    part_hbm,
    residual_hbm,
    gated_hbm,
    mix_grad_hbm,
    out_full_hbm,
    lead_hbm,
    starts_hbm,
    normed_hbm,
    pre_hbm,
    full_hbm,
    mixed_hbm,
    out_ref,
    gain_grad,
    floor_grad,
    total_ref,
    mixer_grads_hbm,
    part,
    residual,
    gated_ref,
    mix_grad_ref,
    out_full,
    lead_ref,
    starts_ref,
    arrived,
    back,
    back_arrived,
    left,
    right,
    full,
    mixer_stage,
    piece_rows_scr,
    pre,
    grad_mixed,
    back_scr,
    message,
    received,
    grad_scr,
    lifted_scr,
    lowered_scr,
    moved_scr,
    value_scr,
    load_sem,
    piece_sem,
    full_sem,
    pre_sem,
    stage_sem,
    grad_send,
    grad_recv,
    *sems,
):
    tokens, model_width = left.shape
    width = gated_hbm.shape[1]
    lanes = width // head_count
    state_rows = head_count * lanes
    tiles, blocks = model_width // TILE, tokens // BLOCK
    piece_rows = 2 * BLOCK
    context, context_size = lax.axis_index("context"), lax.axis_size("context")

    loads = [
        pltpu.make_async_copy(source, target, load_sem.at[which])
        for which, (source, target) in enumerate(
            (
                (part_hbm, part),
                (out_full_hbm, out_full),
                (mix_grad_hbm, mix_grad_ref),
                (lead_hbm, lead_ref),
                (residual_hbm, residual),
                (starts_hbm, starts_ref),
                (gated_hbm, gated_ref),
                (normed_hbm, left),
            )
        )
    ]
    part_load, *gate_loads = loads[:5]
    starts_load, *tile_loads = loads[5:]
    for load in loads:
        load.start()

    def piece_loads(index):
        rows = pl.ds(pl.multiple_of(index * piece_rows, piece_rows), piece_rows)
        slot = lax.rem(index, 2)
        return (
            pltpu.make_async_copy(
                pre_hbm.at[rows, pl.ds(3 * width, width)],
                piece_rows_scr.at[slot, 0],
                piece_sem.at[slot, 0],
            ),
            pltpu.make_async_copy(
                mixed_hbm.at[rows], piece_rows_scr.at[slot, 1], piece_sem.at[slot, 1]
            ),
        )

    for load in piece_loads(0):
        load.start()
    gain_grad[...] = jnp.zeros_like(gain_grad)
    floor_grad[...] = jnp.zeros_like(floor_grad)
    back_scr[...] = jnp.zeros_like(back_scr)

    def turn(total, rows, own):
        out_ref[rows] = (residual[own] + total).astype(BF16)

    def earlier(shift):
        places = {axis: lax.axis_index(axis) for axis in mesh_axes}
        places["context"] = lax.rem(context + context_size - shift, context_size)
        return tuple(places[axis] for axis in mesh_axes)

    def keep_total(total, rows, own):
        total_ref[own] = total

    line = Line(mesh_axes, part, arrived, out_ref, sems[:4], turn)
    back_line = Line(mesh_axes, back, back_arrived, None, sems[4:], keep_total, backs=False)
    barrier = pltpu.get_barrier_semaphore()
    expected = line.greet(barrier)
    for shift in range(1, context_size):
        pl.semaphore_signal(barrier, inc=1, device_id=earlier(shift), device_id_type=MESH_ID)
    pl.semaphore_wait(barrier, expected + context_size - 1)

    def tile_columns(tile):
        return pl.ds(pl.multiple_of(tile * TILE, TILE), TILE)

    def stage_copy(tile):
        rows = tile_columns(tile)
        return pltpu.make_async_copy(mixer_stage, mixer_grads_hbm.at[rows], stage_sem.at[0])

    def gate_piece(index):
        rows = pl.ds(pl.multiple_of(index * piece_rows, piece_rows), piece_rows)
        slot = lax.rem(index, 2)

        @pl.when(index + 1 < tokens // piece_rows)
        def _():
            for load in piece_loads(index + 1):
                load.start()

        for load in piece_loads(index):
            load.wait()
        grads = mm_nn(mix_grad_ref[rows], out_full[...])
        gain = gain_ref[...]
        total = jnp.zeros_like(gain)
        for head in range(head_count):
            part_of = slice(head * lanes, (head + 1) * lanes)
            gate, mixed = piece_rows_scr[slot, 0, :, part_of], piece_rows_scr[slot, 1, :, part_of]
            grad = grads[:, part_of]
            inverse = inverse_rms(mixed)
            unit = mixed * inverse
            sigma = jax.nn.sigmoid(gate)
            scaled = grad * unit
            total = total + jnp.sum(scaled * (gate * sigma), axis=0, keepdims=True)
            grad_gate = scaled * gain * sigma * (1.0 + gate * (1.0 - sigma))
            first = 3 * width + head * lanes
            right[rows, first : first + lanes] = grad_gate.astype(BF16)
            lifted = grad * gain * (gate * sigma)
            mean = jnp.mean(lifted * unit, axis=-1, keepdims=True)
            grad_in = inverse * (lifted - unit * mean) * (key_scale * keep_ref[rows])
            grad_in = grad_in.astype(BF16)
            grad_mixed[rows, part_of] = grad_in
            back_scr[head] += mm_tn(grad_in, lead_ref[rows, part_of])
        gain_grad[...] += total

    def state_copy(shift):
        return pltpu.make_async_remote_copy(
            message,
            received.at[shift - 1],
            grad_send.at[shift - 1],
            grad_recv.at[shift - 1],
            device_id=earlier(shift),
            device_id_type=MESH_ID,
        )

    def block_of(index):
        return blocks - 1 - index

    def pre_load(index):
        rows = pl.ds(pl.multiple_of(block_of(index) * BLOCK, BLOCK), BLOCK)
        slot = lax.rem(index, 2)
        return pltpu.make_async_copy(
            pre_hbm.at[rows, pl.ds(0, 3 * width)], pre.at[slot], pre_sem.at[slot]
        )

    def send_back():
        for head in range(head_count):
            rows = slice(head * lanes, (head + 1) * lanes)
            message[rows] = back_scr[head] * link_ref[0:1]
            message[state_rows + head : state_rows + head + 1] = decay_ref[head] * link_ref[0:1]
        for shift in range(1, context_size):

            @pl.when(context >= shift)
            def _(shift=shift):
                state_copy(shift).start()

        pre_load(0).start()

    def take_back():
        grad_scr[...] = jnp.zeros_like(grad_scr)
        for shift in range(1, context_size):

            @pl.when(context + shift < context_size)
            def _(shift=shift):
                state_copy(shift).wait_recv()
                for head in range(head_count):
                    value = received[shift - 1, head * lanes : (head + 1) * lanes]
                    for near in range(shift - 1):
                        value = value * received[near, state_rows + head : state_rows + head + 1]
                    grad_scr[head] += value

        for shift in range(1, context_size):

            @pl.when(context >= shift)
            def _(shift=shift):
                state_copy(shift).wait_send()

    def mixer_block(index):
        block = block_of(index)
        slot = lax.rem(index, 2)
        block_rows = pl.ds(pl.multiple_of(block * BLOCK, BLOCK), BLOCK)

        @pl.when(index + 1 < blocks)
        def _():
            pre_load(index + 1).start()

        pre_load(index).wait()
        counts, keep, flags = count_ref[block_rows], keep_ref[block_rows], flags_ref[block]
        row_ids, col_ids, linked, fresh, tail, closing = block_masks(counts, flags)
        tri = (row_ids >= col_ids).astype(BF16)
        tri_back = (row_ids <= col_ids).astype(BF16)
        query_pre = pre[slot, :, :width]
        values = pre[slot, :, 2 * width : 3 * width].astype(BF16)
        opened = open_ref[...]
        closed = jax.nn.sigmoid(-pre[slot, :, width : 2 * width])
        keys = opened * closed
        cum = split_sum(tri, jnp.log1p(-keys))
        ending = cum[BLOCK - 1 : BLOCK, :]
        rise, fall = jnp.exp(cum), jnp.exp(-cum) * keep
        shift = jnp.exp(ending - cum) * (keep * tail)
        sigma_query = jax.nn.sigmoid(query_pre)
        lifted = (query_pre * sigma_query * rise).astype(BF16)
        lowered = (keys * fall).astype(BF16)
        moved = (keys * shift).astype(BF16)
        fresh_lifted = (lifted.astype(F32) * fresh).astype(BF16)
        end_decay = jnp.exp(ending) * closing
        lead_in = jnp.exp(run_ref[block]) * (flags[1:2, 0:1] == 0).astype(F32)
        for head in range(head_count):
            part_of = slice(head * lanes, (head + 1) * lanes)
            grad_out, value = grad_mixed[block_rows, part_of], values[:, part_of]
            lift, lower, move = lifted[:, part_of], lowered[:, part_of], moved[:, part_of]
            scores = jnp.where(linked, mm_nt(lift, lower), 0.0).astype(BF16)
            pulls = jnp.where(linked, mm_nt(grad_out, value), 0.0).astype(BF16)
            state = starts_ref[block, head] + lead_in[:, part_of] * carry_ref[head]
            grad_state = grad_scr[head]
            grad_low = grad_state.astype(BF16)
            lifted_scr[:, part_of] = mm_nn(pulls, lower) + fresh * mm_nn(
                grad_out, state.astype(BF16)
            )
            lowered_scr[:, part_of] = mm_tn(pulls, lift)
            grad_moved = mm_nn(value, grad_low)
            moved_scr[:, part_of] = grad_moved
            first = 2 * width + head * lanes
            right[block_rows, first : first + lanes] = (
                mm_tn(scores, grad_out) + mm_nt(move, grad_low)
            ).astype(BF16)
            value_scr[:, part_of] = jnp.sum(
                grad_moved * move.astype(F32), axis=0, keepdims=True
            ) + end_decay[:, part_of] * jnp.sum(state * grad_state, axis=0, keepdims=True)
            grad_scr[head] = grad_state * end_decay[:, part_of] + mm_tn(
                grad_out, fresh_lifted[:, part_of]
            )
        grad_lifted, grad_lowered, grad_moved = lifted_scr[...], lowered_scr[...], moved_scr[...]
        grad_cum = (
            grad_lifted * lifted.astype(F32)
            - grad_lowered * lowered.astype(F32)
            - grad_moved * moved.astype(F32)
        )
        grad_decay = split_sum(tri_back, grad_cum) + value_scr[...]
        key_total = grad_lowered * fall + grad_moved * shift - grad_decay / (1.0 - keys)
        floor_grad[...] -= jnp.sum(key_total * closed, axis=0, keepdims=True)
        right[block_rows, :width] = (
            grad_lifted * rise * sigma_query * (1.0 + query_pre * (1.0 - sigma_query))
        ).astype(BF16)
        right[block_rows, width : 2 * width] = (
            -key_total * opened * closed * (1.0 - closed)
        ).astype(BF16)

    def full_load(tile):
        slot = lax.rem(tile, 2)
        return pltpu.make_async_copy(
            full_hbm.at[tile_columns(tile)], full.at[slot], full_sem.at[slot]
        )

    def back_tile(tile):
        @pl.when(tile + 1 < tiles)
        def _():
            full_load(tile + 1).start()

        full_load(tile).wait()
        product = mm_nt(right[...], full[lax.rem(tile, 2)])
        back[:, tile_columns(tile)] = product.astype(BF16)

    def mixer_tile(tile):
        @pl.when(tile > 0)
        def _():
            stage_copy(tile - 1).wait()

        columns = tile_columns(tile)
        rows = left[:, columns]
        for first in range(0, 4 * width, 1024):
            some = slice(first, min(first + 1024, 4 * width))
            mixer_stage[:, some] = mm_tn(rows, right[:, some]).astype(BF16)
        product = mm_tn(mix_grad_ref[:, columns], gated_ref[...])
        mixer_stage[:, 4 * width :] = product.astype(BF16)
        stage_copy(tile).start()

    send_time = tokens // piece_rows
    block_time = send_time + 2
    back_time = block_time + blocks
    tile_time = back_time + tiles
    end_time = tile_time + tiles

    def piece(time):
        @pl.when(time == 0)
        def _():
            for load in gate_loads:
                load.wait()

        @pl.when(time < send_time)
        def _():
            gate_piece(time)

        @pl.when(time == send_time)
        def _():
            send_back()

        @pl.when(time == block_time)
        def _():
            starts_load.wait()
            take_back()

        @pl.when(jnp.logical_and(time >= block_time, time < back_time))
        def _():
            mixer_block(time - block_time)

        @pl.when(time == back_time - 1)
        def _():
            full_load(0).start()

        @pl.when(jnp.logical_and(time >= back_time, time < tile_time))
        def _():
            back_tile(time - back_time)

        @pl.when(time == tile_time)
        def _():
            for load in tile_loads:
                load.wait()

        @pl.when(jnp.logical_and(time >= tile_time, time < end_time))
        def _():
            mixer_tile(time - tile_time)

    slow = QUIET
    part_load.wait()
    begin = slow + -(-(tile_time - slow) // MANY)
    steps = max(line.steps, begin + back_line.steps, slow + -(-(end_time - slow) // MANY))

    def body(time, _):
        @pl.when(time < line.steps)
        def _():
            line.step(time)

        @pl.when(time >= begin)
        def _():
            back_line.step(time - begin)

        def pieces(index, _):
            piece(index)
            return 0

        first = jnp.where(time < slow, time, slow + MANY * (time - slow))
        lax.fori_loop(first, first + jnp.where(time < slow, 1, MANY), pieces, 0)
        return 0

    lax.fori_loop(0, steps, body, 0)
    stage_copy(tiles - 1).wait()
    line.finish()
    back_line.finish()


def output_line(mesh_axes, collective, in_vmem, in_hbm, head_count):
    part, residual, gated, mix_grad, out_full, lead, starts = in_hbm[:7]
    tokens, model_width = part.shape
    width = gated.shape[1]
    lanes = width // head_count
    context_size = lax.axis_size("context")
    messages = head_count * lanes + -(-head_count // 8) * 8
    whole = pl.BlockSpec(memory_space=pltpu.VMEM)
    remote = pl.BlockSpec(memory_space=pl.ANY)
    return pl.pallas_call(
        partial(output_kernel, mesh_axes, head_count, lanes ** (-0.5)),
        in_specs=[whole] * len(in_vmem) + [remote] * len(in_hbm),
        out_specs=[whole] * 4 + [remote],
        out_shape=[
            jax.ShapeDtypeStruct((tokens, model_width), BF16),
            jax.ShapeDtypeStruct((1, lanes), F32),
            jax.ShapeDtypeStruct((1, width), F32),
            jax.ShapeDtypeStruct((tokens // 2, model_width), F32),
            jax.ShapeDtypeStruct((model_width, 5 * width), BF16),
        ],
        scratch_shapes=[
            pltpu.VMEM(array.shape, array.dtype)
            for array in (part, residual, gated, mix_grad, out_full, lead, starts)
        ]
        + [
            pltpu.VMEM((tokens, model_width), BF16),
            pltpu.VMEM((tokens, model_width), BF16),
            pltpu.VMEM((tokens, model_width), BF16),
            pltpu.VMEM((tokens, model_width), BF16),
            pltpu.VMEM((tokens, 4 * width), BF16),
            pltpu.VMEM((2, TILE, 4 * width), BF16),
            pltpu.VMEM((TILE, 5 * width), BF16),
            pltpu.VMEM((2, 2, 2 * BLOCK, width), F32),
            pltpu.VMEM((2, BLOCK, 3 * width), F32),
            pltpu.VMEM((tokens, width), BF16),
            pltpu.VMEM((head_count, lanes, lanes), F32),
            pltpu.VMEM((messages, lanes), F32),
            pltpu.VMEM((context_size - 1, messages, lanes), F32),
            pltpu.VMEM((head_count, lanes, lanes), F32),
            pltpu.VMEM((BLOCK, width), F32),
            pltpu.VMEM((BLOCK, width), F32),
            pltpu.VMEM((BLOCK, width), F32),
            pltpu.VMEM((1, width), F32),
            pltpu.SemaphoreType.DMA((8,)),
            pltpu.SemaphoreType.DMA((2, 2)),
            pltpu.SemaphoreType.DMA((2,)),
            pltpu.SemaphoreType.DMA((2,)),
            pltpu.SemaphoreType.DMA((1,)),
            pltpu.SemaphoreType.DMA((context_size - 1,)),
            pltpu.SemaphoreType.DMA((context_size - 1,)),
        ]
        + line_sems(tokens)
        + line_sems(tokens, 2),
        compiler_params=pltpu.CompilerParams(
            collective_id=collective, has_side_effects=True, vmem_limit_bytes=61 << 20
        ),
        cost_estimate=pl.CostEstimate(
            flops=tokens * model_width * width * 24,
            bytes_accessed=360_000_000,
            transcendentals=tokens * width * 12,
        ),
        name="output_line",
    )(*in_vmem, *in_hbm)


def input_kernel(
    mesh_axes,
    gain_ref,
    total_hbm,
    hidden_hbm,
    residual_hbm,
    grads_hbm,
    out_ref,
    gain_grad,
    share_query,
    share_forget,
    share_input,
    share_gate,
    share_out,
    total_ref,
    hidden_ref,
    residual_grad,
    own,
    other,
    remote,
    quarter_sem,
    load_sem,
    pair_send,
    pair_recv,
    chip_send,
    chip_recv,
    *sems,
):
    plane = Plane(mesh_axes)
    chips = plane.chips
    block = own.shape[1]
    gain_grad[...] = jnp.zeros_like(gain_grad)
    half, line_size = total_ref.shape[0], lax.axis_size("tensor")
    place = lax.axis_index("tensor")
    at_end = jnp.logical_or(place == 0, place == line_size - 1)
    first_row = jnp.where(place == 0, 0, half)
    quarters = 4
    length = half // quarters

    def quarter_loads(index):
        rows = pl.ds(pl.multiple_of(index * length, length), length)
        inputs = pl.ds(pl.multiple_of(first_row + index * length, length), length)
        return [
            pltpu.make_async_copy(source, target.at[rows], quarter_sem.at[which, index])
            for which, (source, target) in enumerate(
                (
                    (total_hbm.at[rows], total_ref),
                    (hidden_hbm.at[inputs], hidden_ref),
                    (residual_hbm.at[rows], residual_grad),
                )
            )
        ]

    @pl.when(at_end)
    def _():
        for index in range(quarters):
            for load in quarter_loads(index):
                load.start()

    def turn(total, rows, own_rows):
        total = total_ref[own_rows]
        values = hidden_ref[own_rows].astype(F32)
        inverse = inverse_rms(values)
        unit = values * inverse
        gain_grad[...] += jnp.sum(total * unit, axis=0, keepdims=True)
        lifted = total * gain_ref[...]
        mean = jnp.mean(lifted * unit, axis=-1, keepdims=True)
        grad = residual_grad[own_rows] + inverse * (lifted - unit * mean)
        out_ref[rows] = grad.astype(BF16)

    line = Line(mesh_axes, None, None, out_ref, sems, turn, sums=False)
    barrier = pltpu.get_barrier_semaphore()
    expected = line.greet(barrier) + plane.greet(barrier)
    pl.semaphore_wait(barrier, expected)

    def rows_of(slot, core):
        return pl.ds(pl.multiple_of((2 * plane.ahead(slot) + core) * block, block), block)

    def load(slot):
        return pltpu.make_async_copy(
            grads_hbm.at[rows_of(slot, plane.core)], own.at[slot], load_sem.at[slot]
        )

    def pair_copy(slot):
        return pltpu.make_async_remote_copy(
            grads_hbm.at[rows_of(slot, 1 - plane.core)],
            other.at[slot],
            pair_send.at[slot],
            pair_recv.at[slot],
            device_id=plane.device(plane.chip, 1 - plane.core),
            device_id_type=MESH_ID,
        )

    def chip_copy(slot):
        return pltpu.make_async_remote_copy(
            own.at[slot],
            remote.at[slot - 1],
            chip_send.at[slot - 1],
            chip_recv.at[slot - 1],
            device_id=plane.device(plane.ahead(slot), plane.core),
            device_id_type=MESH_ID,
        )

    def start(index, _):
        slot = lax.rem(index + 1, chips)
        pair_copy(slot).start()
        load(slot).start()
        return 0

    lax.fori_loop(0, chips, start, 0)
    strip = 32

    def combine(time):
        slot = lax.rem(jnp.clip(time, 0, chips - 1) + 1, chips)

        @pl.when(time < chips)
        def _():
            load(slot).wait()
            pair_copy(slot).wait_recv()

            def add(index, _):
                rows = pl.ds(pl.multiple_of(index * strip, strip), strip)
                total = own[slot, rows].astype(F32) + other[slot, rows].astype(F32)
                own[slot, rows] = total.astype(BF16)
                return 0

            lax.fori_loop(0, block // strip, add, 0)

        @pl.when(time < chips - 1)
        def _():
            chip_copy(slot).start()

    def step(time, _):
        index = time * CHUNK // length
        fresh = jnp.logical_and(lax.rem(time * CHUNK, length) == 0, index < quarters)

        @pl.when(jnp.logical_and(at_end, fresh))
        def _():
            for load in quarter_loads(index):
                load.wait()

        line.step(time)
        combine(time)
        return 0

    lax.fori_loop(0, line.steps, step, 0)

    def arrive(index, _):
        chip_copy(index).wait_recv()
        return 0

    lax.fori_loop(1, chips, arrive, 0)

    def total(index, _):
        rows = pl.ds(pl.multiple_of(index * strip, strip), strip)

        for which, share in enumerate(
            (share_query, share_forget, share_input, share_gate, share_out)
        ):
            columns = pl.ds(which * share.shape[1], share.shape[1])

            def add(slot, value, columns=columns):
                return value + remote[slot, rows, columns].astype(F32)

            share[rows] = lax.fori_loop(0, chips - 1, add, own[0, rows, columns].astype(F32))
        return 0

    lax.fori_loop(0, block // strip, total, 0)

    def sent(index, _):
        pair_copy(index).wait_send()
        return 0

    lax.fori_loop(0, chips, sent, 0)

    def chip_sent(index, _):
        chip_copy(index).wait_send()
        return 0

    lax.fori_loop(1, chips, chip_sent, 0)
    line.finish()


def input_line(mesh_axes, collective, total, hidden, residual_grad, gain, grads):
    tokens, model_width = hidden.shape
    all_width = grads.shape[1]
    chips = lax.axis_size("shard") * lax.axis_size("context") // 2
    block = model_width // (2 * chips)
    whole = pl.BlockSpec(memory_space=pltpu.VMEM)
    return pl.pallas_call(
        partial(input_kernel, mesh_axes),
        in_specs=[whole] + [pl.BlockSpec(memory_space=pl.ANY)] * 4,
        out_specs=[whole] * 7,
        out_shape=[
            jax.ShapeDtypeStruct((tokens, model_width), BF16),
            jax.ShapeDtypeStruct((1, model_width), F32),
        ]
        + [jax.ShapeDtypeStruct((block, all_width // 5), F32)] * 5,
        scratch_shapes=[
            pltpu.VMEM((tokens // 2, model_width), F32),
            pltpu.VMEM((tokens // 2, model_width), BF16),
            pltpu.VMEM((tokens // 2, model_width), F32),
            pltpu.VMEM((chips, block, all_width), BF16),
            pltpu.VMEM((chips, block, all_width), BF16),
            pltpu.VMEM((chips - 1, block, all_width), BF16),
            pltpu.SemaphoreType.DMA((3, 4)),
            pltpu.SemaphoreType.DMA((chips,)),
            pltpu.SemaphoreType.DMA((chips,)),
            pltpu.SemaphoreType.DMA((chips,)),
            pltpu.SemaphoreType.DMA((chips - 1,)),
            pltpu.SemaphoreType.DMA((chips - 1,)),
        ]
        + line_sems(tokens, 2),
        compiler_params=pltpu.CompilerParams(
            collective_id=collective, has_side_effects=True, vmem_limit_bytes=58 << 20
        ),
        cost_estimate=pl.CostEstimate(
            flops=tokens * model_width * 8, bytes_accessed=360_000_000, transcendentals=0
        ),
        name="input_line",
    )(gain, total, hidden, residual_grad, grads)


def forward_kernel(
    mesh_axes,
    head_count,
    key_scale,
    hidden_ref,
    gain_ref,
    query_hbm,
    forget_hbm,
    input_hbm,
    gate_hbm,
    out_shard_ref,
    down_shard_ref,
    floor_ref,
    segments_ref,
    head_gain_ref,
    normed_hbm,
    pre_hbm,
    full_hbm,
    out_full_hbm,
    mixed_hbm,
    lead_hbm,
    start_hbm,
    gated_hbm,
    mix_hbm,
    down_turned,
    open_ref,
    count_ref,
    keep_ref,
    flags_ref,
    run_ref,
    carry_ref,
    decay_ref,
    link_ref,
    normed,
    pre,
    mine,
    out_turned,
    full,
    out_full,
    mixed,
    lead,
    starts,
    gated,
    mix,
    state_scr,
    run_scr,
    message,
    received,
    mine_sem,
    full_sem,
    save_sem,
    pre_sem,
    mix_sem,
    state_send,
    state_recv,
    *sems,
):
    plane = Plane(mesh_axes)
    chips = plane.chips
    tokens, model_width = hidden_ref.shape
    block, width = query_hbm.shape
    lanes = width // head_count
    state_rows = head_count * lanes
    context, context_size = lax.axis_index("context"), lax.axis_size("context")

    mine_loads = [
        pltpu.make_async_copy(
            ref, mine.at[:, pl.ds(which * width, width)], mine_sem.at[which]
        )
        for which, ref in enumerate((query_hbm, forget_hbm, input_hbm, gate_hbm))
    ]
    for load in mine_loads:
        load.start()
    gather = Gather(plane, (mine,), (full,), sems[:5])
    out_gather = Gather(plane, (out_turned,), (out_full,), sems[5:])

    def later(shift):
        places = {axis: lax.axis_index(axis) for axis in mesh_axes}
        places["context"] = lax.rem(context + shift, context_size)
        return tuple(places[axis] for axis in mesh_axes)

    out_turned[...] = out_shard_ref[...].T
    barrier = pltpu.get_barrier_semaphore()
    expected = gather.greet(barrier)
    for shift in range(1, context_size):
        pl.semaphore_signal(barrier, inc=1, device_id=later(shift), device_id_type=MESH_ID)
    pl.semaphore_wait(barrier, expected + context_size - 1)
    for load in mine_loads:
        load.wait()
    gather.start()
    out_gather.start()
    down_turned[...] = down_shard_ref[...].T
    for head in range(head_count):
        open_ref[:, head * lanes : (head + 1) * lanes] = 1.0 - floor_ref[head : head + 1]

    segments = segments_ref[...]
    blocks = segments.shape[0]
    block_ids = lax.broadcasted_iota(jnp.int32, segments.shape, 0)
    slot_ids = lax.broadcasted_iota(jnp.int32, segments.shape, 1)
    before = pltpu.roll(segments, 1, 1)
    wrapped = pltpu.roll(before, 1, 0)
    before = jnp.where(slot_ids == 0, wrapped, before)
    first_slot = jnp.logical_and(slot_ids == 0, block_ids == 0)
    begins = jnp.where(jnp.logical_or(first_slot, segments == before), 0.0, 1.0)
    wide_rows = lax.broadcasted_iota(jnp.int32, (BLOCK, BLOCK), 0)
    wide_columns = lax.broadcasted_iota(jnp.int32, (BLOCK, BLOCK), 1)
    within = mm_nn(begins.astype(BF16), (wide_rows <= wide_columns).astype(BF16))
    count_rows = []
    running = jnp.zeros((1, 1), F32)
    flags_ref[...] = jnp.zeros_like(flags_ref)
    for index in range(blocks):
        row = within[index : index + 1] + running
        flags_ref[index, 0:1] = row
        flags_ref[index, 1:2] = jnp.broadcast_to(running, (1, BLOCK))
        running = row[:, BLOCK - 1 : BLOCK]
        flags_ref[index, 2:3] = jnp.broadcast_to(running, (1, BLOCK))
        count_rows.append(row)
    turned_counts = jnp.concatenate(count_rows, axis=0).T
    turned_keep = (segments > 0).astype(F32).T
    for index in range(blocks):
        rows = slice(index * BLOCK, (index + 1) * BLOCK)
        count_ref[rows] = turned_counts[:, index : index + 1]
        keep_ref[rows] = turned_keep[:, index : index + 1]
    first_id = jnp.broadcast_to(segments[0:1, 0:1], (1, lanes))
    last_id = jnp.broadcast_to(segments[blocks - 1 : blocks, BLOCK - 1 : BLOCK], (1, lanes))

    def norm(index, _):
        rows = pl.ds(pl.multiple_of(index * 128, 128), 128)
        values = hidden_ref[rows].astype(F32)
        normed[rows] = (values * inverse_rms(values) * gain_ref[...]).astype(BF16)
        return 0

    lax.fori_loop(0, tokens // 128, norm, 0)

    saves = [
        pltpu.make_async_copy(source, target, save_sem.at[which])
        for which, (source, target) in enumerate(
            (
                (normed, normed_hbm),
                (out_full, out_full_hbm),
                (mixed, mixed_hbm),
                (lead, lead_hbm),
                (starts, start_hbm),
                (gated, gated_hbm),
            )
        )
    ]
    saves[0].start()
    row_tile, column_tile = 256, 512

    def pre_save(index):
        rows = pl.ds(pl.multiple_of(index * row_tile, row_tile), row_tile)
        return pltpu.make_async_copy(pre.at[rows], pre_hbm.at[rows], pre_sem.at[index])

    def depth_of(distance):
        first = 2 * gather.partner(distance) * block
        return pl.ds(pl.multiple_of(first, 2 * block), 2 * block)

    def product(distance):
        depth = depth_of(distance)

        def row_body(index, _):
            rows = pl.ds(pl.multiple_of(index * row_tile, row_tile), row_tile)
            left = normed[rows, depth]

            def column_body(column, _):
                columns = pl.ds(pl.multiple_of(column * column_tile, column_tile), column_tile)
                value = mm_nn(left, full[depth, columns])
                if distance > 0:
                    value = value + pre[rows, columns]
                pre[rows, columns] = value
                return 0

            lax.fori_loop(0, full.shape[1] // column_tile, column_body, 0)
            if distance == chips - 1:
                pre_save(index).start()
            return 0

        lax.fori_loop(0, tokens // row_tile, row_body, 0)

    def full_save(distance):
        depth = depth_of(distance)
        return pltpu.make_async_copy(full.at[depth], full_hbm.at[depth], full_sem.at[distance])

    def use(distance):
        gather.arrive_from(distance)
        full_save(distance).start()
        product(distance)

    use(0)
    gather.stage(0)
    gather.stage(1)
    if gather.relayed:
        use(1)
        use(2)
    gather.stage(2)
    if gather.relayed:
        use(3)
    else:
        for distance in range(1, chips):
            use(distance)
    out_gather.stage(0)
    out_gather.stage(1)

    state_scr[...] = jnp.zeros_like(state_scr)
    run_scr[...] = jnp.zeros_like(run_scr)

    def recur(step, _):
        rows = pl.ds(pl.multiple_of(step * BLOCK, BLOCK), BLOCK)
        counts, keep = count_ref[rows], keep_ref[rows]
        row_ids, col_ids, linked, fresh, tail, closing = block_masks(counts, flags_ref[step])
        tri = (row_ids >= col_ids).astype(BF16)
        query_pre = pre[rows, :width]
        values = pre[rows, 2 * width : 3 * width].astype(BF16)
        keys = open_ref[...] * jax.nn.sigmoid(-pre[rows, width : 2 * width])
        cum = split_sum(tri, jnp.log1p(-keys))
        ending = cum[BLOCK - 1 : BLOCK, :]
        lifted = query_pre * jax.nn.sigmoid(query_pre) * jnp.exp(cum)
        lowered = (keys * jnp.exp(-cum) * keep).astype(BF16)
        moved = (keys * jnp.exp(ending - cum) * (keep * tail)).astype(BF16)
        run = run_scr[...]
        lead[rows] = (lifted * jnp.exp(run) * (counts == 0).astype(F32)).astype(BF16)
        run_ref[step] = run
        run_scr[...] = run + ending
        fresh_lifted = (lifted * fresh).astype(BF16)
        lifted = lifted.astype(BF16)
        end_decay = jnp.exp(ending) * closing
        for head in range(head_count):
            part = slice(head * lanes, (head + 1) * lanes)
            state = state_scr[head]
            starts[step, head] = state
            scores = jnp.where(linked, mm_nt(lifted[:, part], lowered[:, part]), 0.0)
            results = mm_nn(scores.astype(BF16), values[:, part])
            results = results + mm_nt(fresh_lifted[:, part], state.astype(BF16))
            mixed[rows, part] = results * (key_scale * keep)
            state_scr[head] = state * end_decay[:, part] + mm_tn(values[:, part], moved[:, part])
        return 0

    lax.fori_loop(0, tokens // BLOCK, recur, 0)
    saves[3].start()
    saves[4].start()

    last_count = flags_ref[tokens // BLOCK - 1][2:3, 0:1]
    for head in range(head_count):
        part = slice(head * lanes, (head + 1) * lanes)
        message[head * lanes : (head + 1) * lanes] = state_scr[head]
        decay = jnp.exp(run_scr[:, part]) * (last_count == 0).astype(F32)
        decay_ref[head] = decay
        message[state_rows + 8 + head : state_rows + 9 + head] = decay
    message[state_rows : state_rows + 1] = first_id
    message[state_rows + 1 : state_rows + 2] = last_id

    def state_copy(shift):
        return pltpu.make_async_remote_copy(
            message,
            received.at[shift - 1],
            state_send.at[shift - 1],
            state_recv.at[shift - 1],
            device_id=later(shift),
            device_id_type=MESH_ID,
        )

    for shift in range(1, context_size):

        @pl.when(context + shift < context_size)
        def _(shift=shift):
            state_copy(shift).start()

    out_gather.stage(2)
    carry_ref[...] = jnp.zeros_like(carry_ref)
    link_ref[...] = jnp.zeros_like(link_ref)
    for shift in range(1, context_size):

        @pl.when(context >= shift)
        def _(shift=shift):
            state_copy(shift).wait_recv()
            linked = jnp.ones((1, lanes), F32)
            follower = first_id
            factors = [jnp.ones((1, lanes), F32)] * head_count
            for near in range(shift):
                got = received.at[near]
                linked = (got[state_rows + 1 : state_rows + 2] == follower).astype(F32)
                follower = got[state_rows : state_rows + 1]
                factors = [factor * linked for factor in factors]
                if near < shift - 1:
                    factors = [
                        factor * got[state_rows + 8 + head : state_rows + 9 + head]
                        for head, factor in enumerate(factors)
                    ]
            if shift == 1:
                link_ref[0:1] = linked
            for head in range(head_count):
                rows = slice(head * lanes, (head + 1) * lanes)
                carry_ref[head] += factors[head] * received[shift - 1, rows]

    for shift in range(1, context_size):

        @pl.when(context + shift < context_size)
        def _(shift=shift):
            state_copy(shift).wait_send()

    for distance in range(chips):
        out_gather.arrive_from(distance)
    saves[1].start()

    def mix_save(index):
        rows = pl.ds(pl.multiple_of(index * row_tile, row_tile), row_tile)
        return pltpu.make_async_copy(mix.at[rows], mix_hbm.at[rows], mix_sem.at[index])

    def project(index, _):
        rows = pl.ds(pl.multiple_of(index * row_tile, row_tile), row_tile)
        for head in range(head_count):
            part = slice(head * lanes, (head + 1) * lanes)
            carried = mm_nt(lead[rows, part], carry_ref[head].astype(BF16))
            value = mixed[rows, part] + carried * (key_scale * keep_ref[rows])
            mixed[rows, part] = value
            gate = pre[rows, 3 * width + head * lanes : 3 * width + (head + 1) * lanes]
            unit = value * inverse_rms(value)
            gated[rows, part] = (
                unit * head_gain_ref[...] * (gate * jax.nn.sigmoid(gate))
            ).astype(BF16)
        left = gated[rows]

        def column_body(column, _):
            columns = pl.ds(pl.multiple_of(column * column_tile, column_tile), column_tile)
            mix[rows, columns] = mm_nt(left, out_full[columns, :]).astype(BF16)
            return 0

        lax.fori_loop(0, model_width // column_tile, column_body, 0)
        mix_save(index).start()
        return 0

    lax.fori_loop(0, tokens // row_tile, project, 0)
    saves[2].start()
    saves[5].start()
    gather.finish()
    out_gather.finish()
    for distance in range(chips):
        full_save(distance).wait()
    for save in saves:
        save.wait()
    for index in range(tokens // row_tile):
        pre_save(index).wait()
        mix_save(index).wait()


def forward(
    mesh_axes, collective, hidden, gain, shards, out_shard, down_shard, floor, segments, head_gain
):
    tokens, model_width = hidden.shape
    block, width = shards[0].shape
    lanes = head_gain.shape[1]
    head_count = width // lanes
    all_width = width * len(shards)
    blocks = tokens // BLOCK
    context_size = lax.axis_size("context")
    chips = lax.axis_size("shard") * context_size // 2
    messages = head_count * lanes + 8 + -(-head_count // 8) * 8
    whole = pl.BlockSpec(memory_space=pltpu.VMEM)
    remote = pl.BlockSpec(memory_space=pl.ANY)
    stored = [
        ((tokens, model_width), BF16),
        ((tokens, all_width), F32),
        ((model_width, all_width), BF16),
        ((model_width, width), BF16),
        ((tokens, width), F32),
        ((tokens, width), BF16),
        ((blocks, head_count, lanes, lanes), F32),
        ((tokens, width), BF16),
        ((tokens, model_width), BF16),
    ]
    kept = [
        (down_shard.shape[::-1], BF16),
        ((1, width), F32),
        ((tokens, 1), F32),
        ((tokens, 1), F32),
        ((blocks, 8, BLOCK), F32),
        ((blocks, 1, width), F32),
        ((head_count, lanes, lanes), F32),
        ((head_count, 1, lanes), F32),
        ((8, lanes), F32),
    ]
    return pl.pallas_call(
        partial(forward_kernel, mesh_axes, head_count, lanes ** (-0.5)),
        in_specs=[whole] * 2 + [remote] * 4 + [whole] * 5,
        out_specs=[remote] * len(stored) + [whole] * len(kept),
        out_shape=[jax.ShapeDtypeStruct(shape, kind) for shape, kind in stored + kept],
        scratch_shapes=[
            pltpu.VMEM((tokens, model_width), BF16),
            pltpu.VMEM((tokens, all_width), F32),
            pltpu.VMEM((block, all_width), BF16),
            pltpu.VMEM((block, width), BF16),
            pltpu.VMEM((model_width, all_width), BF16),
            pltpu.VMEM((model_width, width), BF16),
            pltpu.VMEM((tokens, width), F32),
            pltpu.VMEM((tokens, width), BF16),
            pltpu.VMEM((blocks, head_count, lanes, lanes), F32),
            pltpu.VMEM((tokens, width), BF16),
            pltpu.VMEM((tokens, model_width), BF16),
            pltpu.VMEM((head_count, lanes, lanes), F32),
            pltpu.VMEM((1, width), F32),
            pltpu.VMEM((messages, lanes), F32),
            pltpu.VMEM((context_size - 1, messages, lanes), F32),
            pltpu.SemaphoreType.DMA((4,)),
            pltpu.SemaphoreType.DMA((chips,)),
            pltpu.SemaphoreType.DMA((6,)),
            pltpu.SemaphoreType.DMA((tokens // 256,)),
            pltpu.SemaphoreType.DMA((tokens // 256,)),
            pltpu.SemaphoreType.DMA((context_size - 1,)),
            pltpu.SemaphoreType.DMA((context_size - 1,)),
        ]
        + gather_sems(1)
        + gather_sems(1),
        compiler_params=pltpu.CompilerParams(
            collective_id=collective, has_side_effects=True, vmem_limit_bytes=56 << 20
        ),
        cost_estimate=pl.CostEstimate(
            flops=2 * tokens * model_width * all_width,
            bytes_accessed=200_000_000,
            transcendentals=tokens * width * 9,
        ),
        name="forward",
    )(hidden, gain, *shards, out_shard, down_shard, floor, segments, head_gain)


def small_sum_kernel(
    mesh_axes, value, local_ref, total_ref, near, far, near_send, near_recv, far_send, far_recv
):
    shard_size, context_size = lax.axis_size("shard"), lax.axis_size("context")
    line_size = lax.axis_size("tensor")
    group = shard_size * context_size
    place = lax.axis_index("shard") * context_size + lax.axis_index("context")
    line_place = lax.axis_index("tensor")

    def device(position, line_position):
        places = {
            "shard": position // context_size,
            "context": lax.rem(position, context_size),
            "tensor": line_position,
        }
        return tuple(places[axis] for axis in mesh_axes)

    def near_target(step):
        return device(lax.rem(place + step, group), line_place)

    def far_target(step):
        return device(place, lax.rem(line_place + step, line_size))

    def near_copy(step):
        return pltpu.make_async_remote_copy(
            value,
            near.at[step - 1],
            near_send.at[step - 1],
            near_recv.at[step - 1],
            device_id=near_target(step),
            device_id_type=MESH_ID,
        )

    def far_copy(step):
        return pltpu.make_async_remote_copy(
            local_ref,
            far.at[step - 1],
            far_send.at[step - 1],
            far_recv.at[step - 1],
            device_id=far_target(step),
            device_id_type=MESH_ID,
        )

    barrier = pltpu.get_barrier_semaphore()
    for step in range(1, group):
        pl.semaphore_signal(barrier, inc=1, device_id=near_target(step), device_id_type=MESH_ID)
    for step in range(1, line_size):
        pl.semaphore_signal(barrier, inc=1, device_id=far_target(step), device_id_type=MESH_ID)
    pl.semaphore_wait(barrier, group + line_size - 2)
    for step in range(1, group):
        near_copy(step).start()
    total = value[...]
    for step in range(1, group):
        near_copy(step).wait_recv()
        total = total + near[step - 1]
    local_ref[...] = total
    for step in range(1, line_size):
        far_copy(step).start()
    for step in range(1, line_size):
        far_copy(step).wait_recv()
        total = total + far[step - 1]
    total_ref[...] = total
    for step in range(1, group):
        near_copy(step).wait_send()
    for step in range(1, line_size):
        far_copy(step).wait_send()


def small_sum(mesh_axes, collective, values):
    flat = jnp.concatenate([value.reshape(-1) for value in values])
    lanes = -(-flat.shape[0] // 1024) * 128
    flat = jnp.pad(flat, (0, 8 * lanes - flat.shape[0])).reshape(8, lanes)
    group = lax.axis_size("shard") * lax.axis_size("context")
    line_size = lax.axis_size("tensor")
    whole = pl.BlockSpec(memory_space=pltpu.VMEM)
    local, total = pl.pallas_call(
        partial(small_sum_kernel, mesh_axes),
        in_specs=[whole],
        out_specs=[whole] * 2,
        out_shape=[jax.ShapeDtypeStruct((8, lanes), F32)] * 2,
        scratch_shapes=[
            pltpu.VMEM((group - 1, 8, lanes), F32),
            pltpu.VMEM((line_size - 1, 8, lanes), F32),
            pltpu.SemaphoreType.DMA((group - 1,)),
            pltpu.SemaphoreType.DMA((group - 1,)),
            pltpu.SemaphoreType.DMA((line_size - 1,)),
            pltpu.SemaphoreType.DMA((line_size - 1,)),
        ],
        compiler_params=pltpu.CompilerParams(collective_id=collective, has_side_effects=True),
        cost_estimate=pl.CostEstimate(
            flops=8 * lanes * group, bytes_accessed=20_000_000, transcendentals=0
        ),
        name="small_sum",
    )(flat)
    return local.reshape(-1), total.reshape(-1)


def local(
    mesh_axes,
    hidden,
    segment_ids,
    norm1_gain,
    w_query,
    w_forget,
    w_input,
    w_gate_out,
    forget_floor,
    head_gain,
    w_out,
    norm2_gain,
    w_ffn_gate,
    w_ffn_up,
    w_ffn_down,
    out_grad,
):
    sequences, span_len, model_width = hidden.shape
    tokens = sequences * span_len
    head_count, key_dim = forget_floor.shape
    width = head_count * key_dim
    key_scale = key_dim ** (-0.5)
    both = ("shard", "context")
    gain_one, gain_two = norm1_gain.reshape(1, -1), norm2_gain.reshape(1, -1)
    hidden_rows = hidden.reshape(tokens, model_width)
    gain_row = head_gain.reshape(1, -1)
    segments = segment_ids.reshape(tokens // BLOCK, BLOCK).astype(F32)
    (
        normed_one,
        pre,
        mixer_full,
        out_full,
        mixed,
        lead,
        starts,
        gated_low,
        mix_part,
        down_turned,
        open_part,
        counts,
        keep,
        flags,
        runs,
        carry,
        decay,
        link,
    ) = forward(
        mesh_axes,
        4,
        hidden_rows,
        gain_one,
        (w_query, w_forget, w_input, w_gate_out),
        w_out,
        w_ffn_down,
        forget_floor,
        segments,
        gain_row,
    )
    grad_rows = out_grad.reshape(tokens, model_width)
    (
        grad_mix_low,
        grad_norm_two,
        residual,
        _,
        _,
        _,
        feed_part,
        grad_residual,
        grads_ffn,
    ) = middle(
        mesh_axes,
        2,
        mix_part,
        grad_rows,
        hidden_rows,
        gain_two,
        w_ffn_gate,
        w_ffn_up,
        down_turned,
    )
    (
        output_rows,
        grad_head_part,
        grad_floor_part,
        back_one,
        grads_mixer,
    ) = output_line(
        mesh_axes,
        1,
        (
            runs,
            carry,
            decay,
            link,
            open_part,
            counts,
            keep,
            flags,
            gain_row,
        ),
        (
            feed_part,
            residual,
            gated_low,
            grad_mix_low,
            out_full,
            lead,
            starts,
            normed_one,
            pre,
            mixer_full,
            mixed,
        ),
        head_count,
    )
    share_ffn = lax.psum_scatter(grads_ffn, both, scatter_dimension=0, tiled=True)
    hidden_width = w_ffn_gate.shape[1]

    def ffn_share(which):
        return share_ffn[:, which * hidden_width : (which + 1) * hidden_width].astype(F32)

    input_rows, grad_norm_one, *mixer_shares, share_out = input_line(
        mesh_axes, 3, back_one, hidden_rows, grad_residual, gain_one, grads_mixer
    )
    near, total = small_sum(
        mesh_axes, 5, (grad_norm_one, grad_norm_two, grad_head_part, grad_floor_part)
    )
    shares = lax.axis_size("shard") * lax.axis_size("context")
    position = lax.axis_index("shard") * lax.axis_size("context") + lax.axis_index("context")

    def own_slice(values, first, length):
        values = values[first : first + length].reshape(shares, length // shares)
        return lax.dynamic_index_in_dim(values, position, 0, False)

    floor_total = near[2 * model_width + key_dim : 2 * model_width + key_dim + width]
    floor_total = floor_total.reshape(head_count, shares, key_dim // shares)

    return (
        output_rows.reshape(hidden.shape),
        input_rows.reshape(hidden.shape),
        own_slice(total, 0, model_width),
        *mixer_shares,
        lax.dynamic_index_in_dim(floor_total, position, 1, False),
        own_slice(total, 2 * model_width, key_dim),
        share_out.T,
        own_slice(total, model_width, model_width),
        ffn_share(0),
        ffn_share(1),
        ffn_share(2).T,
    )


def solution(mesh):
    in_specs = (
        P("shard", "context", None),
        P("shard", "context"),
        P(),
        P(("shard", "context"), "tensor"),
        P(("shard", "context"), "tensor"),
        P(("shard", "context"), "tensor"),
        P(("shard", "context"), "tensor"),
        P("tensor", None),
        P(),
        P("tensor", ("shard", "context")),
        P(),
        P(("shard", "context"), "tensor"),
        P(("shard", "context"), "tensor"),
        P("tensor", ("shard", "context")),
        P("shard", "context", None),
    )
    out_specs = (
        P("shard", "context", None),
        P("shard", "context", None),
        P(("shard", "context")),
        P(("shard", "context"), "tensor"),
        P(("shard", "context"), "tensor"),
        P(("shard", "context"), "tensor"),
        P(("shard", "context"), "tensor"),
        P("tensor", ("shard", "context")),
        P(("shard", "context")),
        P("tensor", ("shard", "context")),
        P(("shard", "context")),
        P(("shard", "context"), "tensor"),
        P(("shard", "context"), "tensor"),
        P("tensor", ("shard", "context")),
    )
    return jax.shard_map(
        partial(local, mesh.axis_names), mesh=mesh, in_specs=in_specs, out_specs=out_specs, check_vma=False)
```

```python
from functools import partial

import jax
import jax.numpy as jnp
from jax import lax
from jax.experimental import pallas as pl
from jax.experimental.pallas import tpu as pltpu
from jax.sharding import PartitionSpec as P

EPSILON = 1e-05


BLOCK = 128
F32 = jnp.float32
BF16 = jnp.bfloat16


def mm(a, b, dims):
    return lax.dot_general(a, b, (dims, ((), ())), preferred_element_type=F32)


def mm_nn(a, b):
    return mm(a, b, ((1,), (0,)))


def mm_nt(a, b):
    return mm(a, b, ((1,), (1,)))


def mm_tn(a, b):
    return mm(a, b, ((0,), (0,)))


def split_sum(tri, values):
    high = values.astype(BF16)
    low = (values - high.astype(F32)).astype(BF16)
    return mm_nn(tri, high) + mm_nn(tri, low)


def block_masks(counts, flags_row):
    rows = counts.shape[0]
    row_ids = lax.broadcasted_iota(jnp.int32, (rows, rows), 0)
    col_ids = lax.broadcasted_iota(jnp.int32, (rows, rows), 1)
    linked = jnp.logical_and(counts == flags_row[0:1], row_ids >= col_ids)
    fresh = (counts == flags_row[1:2, 0:1]).astype(F32)
    tail = (counts == flags_row[2:3, 0:1]).astype(F32)
    closing = (flags_row[1:2, 0:1] == flags_row[2:3, 0:1]).astype(F32)
    return row_ids, col_ids, linked, fresh, tail, closing


CHUNK = 32
QUIET, MANY = 6, 2
LAG = 2
MESH_ID = pl.DeviceIdType.MESH


class Line:
    def __init__(self, mesh_axes, part, arrived, out, sems, transform, sums=True, backs=True):
        self.mesh_axes = mesh_axes
        self.sums, self.backs = sums, backs
        self.part, self.arrived, self.out = part, arrived, out
        if sums:
            self.sum_send, self.sum_recv = sems[:2]
        if backs:
            self.back_send, self.back_recv = sems[-2:]
        self.transform = transform
        self.half = (part if sums else out).shape[0] // 2
        self.chunks = self.half // CHUNK
        self.size = lax.axis_size("tensor")
        self.place = lax.axis_index("tensor")
        self.lines = ((self.size - 1 - self.place, -1), (self.place, 1))
        self.offset = LAG * (self.size - 1) if sums else 0
        self.steps = self.chunks + self.offset + (LAG * (self.size - 1) if backs else 0)

    def device(self, position):
        return tuple(
            jnp.clip(position, 0, self.size - 1) if axis == "tensor" else lax.axis_index(axis)
            for axis in self.mesh_axes
        )

    def greet(self, barrier):
        for step in (-1, 1):
            inside = jnp.logical_and(self.place + step >= 0, self.place + step < self.size)

            @pl.when(inside)
            def _(step=step):
                pl.semaphore_signal(
                    barrier, inc=1, device_id=self.device(self.place + step), device_id_type=MESH_ID
                )

        at_end = jnp.logical_or(self.place == 0, self.place == self.size - 1)
        return jnp.where(at_end, 1, 2)

    def rows_of(self, side, index):
        return pl.ds(pl.multiple_of(side * self.half + index * CHUNK, CHUNK), CHUNK)

    def sum_copy(self, side, index, source):
        rows = self.rows_of(side, index)
        return pltpu.make_async_remote_copy(
            source.at[rows],
            self.arrived.at[rows],
            self.sum_send.at[side, index],
            self.sum_recv.at[side, index],
            device_id=self.device(self.place + self.lines[side][1]),
            device_id_type=MESH_ID,
        )

    def back_copy(self, side, index):
        rows = self.rows_of(side, index)
        return pltpu.make_async_remote_copy(
            self.out.at[rows],
            self.out.at[rows],
            self.back_send.at[side, index],
            self.back_recv.at[side, index],
            device_id=self.device(self.place - self.lines[side][1]),
            device_id_type=MESH_ID,
        )

    def step(self, time):
        for side in (0, 1):
            hops = self.lines[side][0]
            at_source, at_owner = hops == 0, hops == self.size - 1
            if self.sums:
                self.sum_step(time, side, hops, at_source, at_owner)
            if self.backs:
                self.back_step(time, side, hops, at_owner)

    def sum_step(self, time, side, hops, at_source, at_owner):
        index = time - LAG * hops
        valid = jnp.logical_and(index >= 0, index < self.chunks)
        index = jnp.clip(index, 0, self.chunks - 1)
        rows = self.rows_of(side, index)

        @pl.when(jnp.logical_and(valid, at_source))
        def _():
            self.sum_copy(side, index, self.part).start()

        @pl.when(jnp.logical_and(valid, jnp.logical_not(at_source)))
        def _():
            self.sum_copy(side, index, self.arrived).wait_recv()

        between = jnp.logical_and(jnp.logical_not(at_source), jnp.logical_not(at_owner))

        @pl.when(jnp.logical_and(valid, between))
        def _():
            total = self.part[rows].astype(F32) + self.arrived[rows].astype(F32)
            self.arrived[rows] = total.astype(BF16)
            self.sum_copy(side, index, self.arrived).start()

        @pl.when(jnp.logical_and(valid, at_owner))
        def _():
            total = self.part[rows].astype(F32) + self.arrived[rows].astype(F32)
            self.turn(total, side, index)

    def turn(self, total, side, index):
        own = pl.ds(pl.multiple_of(index * CHUNK, CHUNK), CHUNK)
        self.transform(total, self.rows_of(side, index), own)
        if self.backs:
            self.back_copy(side, index).start()

    def back_step(self, time, side, hops, at_owner):
        if not self.sums:

            @pl.when(jnp.logical_and(at_owner, time < self.chunks))
            def _():
                self.turn(None, side, jnp.clip(time, 0, self.chunks - 1))

        away = self.size - 1 - hops
        index = time - self.offset - LAG * away
        valid = jnp.logical_and(jnp.logical_and(index >= 0, index < self.chunks), away > 0)
        index = jnp.clip(index, 0, self.chunks - 1)

        @pl.when(valid)
        def _():
            self.back_copy(side, index).wait_recv()

        @pl.when(jnp.logical_and(valid, away < self.size - 1))
        def _():
            self.back_copy(side, index).start()

    def run(self, first, last, beside=None):
        def body(time, _):
            self.step(time)
            if beside is not None:
                beside(time)
            return 0

        lax.fori_loop(first, last, body, 0)

    def source_sent(self, first, last):
        def body(index, _):
            for side in (0, 1):

                @pl.when(self.lines[side][0] == 0)
                def _(side=side):
                    self.sum_copy(side, index, self.part).wait_send()

            return 0

        lax.fori_loop(first, last, body, 0)

    def finish(self, source_waits=True):
        def body(index, _):
            for side in (0, 1):
                hops = self.lines[side][0]
                passed = hops < self.size - 1
                if not source_waits:
                    passed = jnp.logical_and(passed, hops > 0)

                if self.sums:

                    @pl.when(passed)
                    def _(side=side):
                        self.sum_copy(side, index, self.arrived).wait_send()

                if self.backs:

                    @pl.when(hops > 0)
                    def _(side=side):
                        self.back_copy(side, index).wait_send()

            return 0

        lax.fori_loop(0, self.chunks, body, 0)


def line_sems(tokens, count=4):
    return [pltpu.SemaphoreType.DMA((2, tokens // 2 // CHUNK))] * count


def inverse_rms(values):
    return lax.rsqrt(jnp.mean(values * values, axis=-1, keepdims=True) + EPSILON)


class Plane:
    def __init__(self, mesh_axes):
        self.mesh_axes = mesh_axes
        self.context = lax.axis_size("context")
        self.per_row = self.context // 2
        self.chips = lax.axis_size("shard") * self.per_row
        context_place = lax.axis_index("context")
        self.core = lax.rem(context_place, 2)
        self.chip = lax.axis_index("shard") * self.per_row + context_place // 2

    def device(self, chip, core):
        places = {
            "shard": chip // self.per_row,
            "context": 2 * lax.rem(chip, self.per_row) + core,
            "tensor": lax.axis_index("tensor"),
        }
        return tuple(places[axis] for axis in self.mesh_axes)

    def ahead(self, distance):
        return lax.rem(self.chip + distance, self.chips)

    def greet(self, barrier):
        targets = [self.device(self.chip, 1 - self.core)]
        targets += [self.device(self.ahead(step), self.core) for step in range(1, self.chips)]
        for target in targets:
            pl.semaphore_signal(barrier, inc=1, device_id=target, device_id_type=MESH_ID)
        return len(targets)


class Gather:
    def __init__(self, plane, sources, targets, sems):
        self.plane, self.sources, self.targets = plane, sources, targets
        self.load_sem, self.send_sem, self.recv_sem, self.pair_send, self.pair_recv = sems
        self.block = sources[0].shape[0]
        self.part = self.block // 2
        self.relayed = plane.chips == 4
        self.arrays = range(len(sources))

    def partner(self, distance):
        return jnp.bitwise_xor(self.plane.chip, distance)

    def greet(self, barrier):
        plane = self.plane
        targets = [plane.device(plane.chip, 1 - plane.core)]
        targets += [
            plane.device(self.partner(step), plane.core)
            for step in range(1, 3 if self.relayed else plane.chips)
        ]
        for target in targets:
            pl.semaphore_signal(barrier, inc=1, device_id=target, device_id_type=MESH_ID)
        return len(targets)

    def place(self, array, chip, core, half):
        first = (2 * chip + core) * self.block + half * self.part
        rows = pl.ds(pl.multiple_of(first, self.part), self.part)
        return self.targets[array].at[rows, pl.ds(0, self.sources[array].shape[1])]

    def mine(self, array, half):
        return self.sources[array].at[pl.ds(half * self.part, self.part)]

    def loads(self):
        plane = self.plane
        return [
            pltpu.make_async_copy(
                self.mine(array, half),
                self.place(array, plane.chip, plane.core, half),
                self.load_sem.at[array, half],
            )
            for array in self.arrays
            for half in range(2)
        ]

    def send(self, distance, half):
        plane = self.plane
        copies = []
        for array in self.arrays:
            chip, target = plane.chip, self.partner(distance)
            source = self.mine(array, half)
            if self.relayed and distance == 3:
                chip = self.partner(2 if half == 0 else 1)
                target = self.partner(1 if half == 0 else 2)
                source = self.place(array, chip, plane.core, half)
            copies.append(
                pltpu.make_async_remote_copy(
                    source,
                    self.place(array, chip, plane.core, half),
                    self.send_sem.at[array, distance - 1, half],
                    self.recv_sem.at[array, distance - 1, half],
                    device_id=plane.device(target, plane.core),
                    device_id_type=MESH_ID,
                )
            )
        return copies

    def forward(self, distance, half):
        plane = self.plane
        copies = []
        for array in self.arrays:
            place = self.place(array, self.partner(distance), plane.core, half)
            copies.append(
                pltpu.make_async_remote_copy(
                    self.mine(array, half) if distance == 0 else place,
                    place,
                    self.pair_send.at[array, distance, half],
                    self.pair_recv.at[array, distance, half],
                    device_id=plane.device(plane.chip, 1 - plane.core),
                    device_id_type=MESH_ID,
                )
            )
        return copies

    def start(self):
        if self.relayed:
            order = ((1, 1), (2, 0), (1, 0), (2, 1))
        else:
            order = [(step, half) for step in range(1, self.plane.chips) for half in range(2)]
        for distance, half in order:
            for copy in self.send(distance, half):
                copy.start()
        for copy in self.loads():
            copy.start()
        for half in range(2):
            for copy in self.forward(0, half):
                copy.start()

    def take(self, distance, half, relay):
        for copy in self.send(distance, half):
            copy.wait_recv()
        if relay:
            for copy in self.send(3, half):
                copy.start()
        for copy in self.forward(distance, half):
            copy.start()

    def stage(self, number):
        if self.relayed:
            if number == 0:
                self.take(1, 1, True)
                self.take(2, 0, True)
            elif number == 1:
                self.take(1, 0, False)
                self.take(2, 1, False)
            else:
                self.take(3, 0, False)
                self.take(3, 1, False)
        elif number == 2:
            for distance in range(1, self.plane.chips):
                for half in range(2):
                    self.take(distance, half, False)

    def arrive_from(self, distance):
        if distance == 0:
            for copy in self.loads():
                copy.wait()
        for half in range(2):
            for copy in self.forward(distance, half):
                copy.wait_recv()

    def arrive(self):
        for distance in range(self.plane.chips):
            self.arrive_from(distance)

    def finish(self):
        for distance in range(self.plane.chips):
            for half in range(2):
                for copy in self.forward(distance, half):
                    copy.wait_send()
                if distance > 0:
                    for copy in self.send(distance, half):
                        copy.wait_send()


def gather_sems(arrays):
    chips = lax.axis_size("shard") * lax.axis_size("context") // 2
    return [
        pltpu.SemaphoreType.DMA((arrays, 2)),
        pltpu.SemaphoreType.DMA((arrays, chips - 1, 2)),
        pltpu.SemaphoreType.DMA((arrays, chips - 1, 2)),
        pltpu.SemaphoreType.DMA((arrays, chips, 2)),
        pltpu.SemaphoreType.DMA((arrays, chips, 2)),
    ]


GROUP = 128
TILE = 256
WIDE = 512


def middle_kernel(
    mesh_axes,
    mix_hbm,
    cotangent_hbm,
    input_hbm,
    gain_ref,
    gate_hbm,
    up_hbm,
    down_hbm,
    out_ref,
    gain_grad,
    residual_hbm,
    hidden_hbm,
    grad_gate_hbm,
    grad_up_hbm,
    feed_hbm,
    grad_hbm,
    grads_hbm,
    normed_ref,
    cotangent_ref,
    gate_w,
    up_w,
    down_w,
    part,
    mix_arrived,
    arrived,
    inputs,
    residual,
    stage_hidden,
    stage_gate,
    stage_up,
    stage_feed,
    part_sem,
    input_sem,
    save_sem,
    stage_sem,
    grad_sem,
    back_sem,
    tile_sem,
    *sems,
):
    tokens, model_width = normed_ref.shape
    half = tokens // 2
    hidden_width = gate_hbm.shape[1]
    padded = gate_w.shape[1]
    groups = half // GROUP
    place, line_size = lax.axis_index("tensor"), lax.axis_size("tensor")
    own_half = pl.ds(pl.multiple_of(jnp.where(place == 0, 0, half), half), half)
    part_load = pltpu.make_async_copy(mix_hbm, part, part_sem.at[0])
    part_load.start()
    input_load = pltpu.make_async_copy(input_hbm.at[own_half], inputs, input_sem.at[0])
    input_load.start()
    cotangent_load = pltpu.make_async_copy(cotangent_hbm, cotangent_ref, input_sem.at[1])
    cotangent_load.start()
    if padded > hidden_width:
        spare = slice(hidden_width, padded)
        gate_w[:, spare] = jnp.zeros((model_width, padded - hidden_width), BF16)
        up_w[:, spare] = jnp.zeros((model_width, padded - hidden_width), BF16)
        down_w[:, spare] = jnp.zeros((model_width, padded - hidden_width), BF16)
    gain_grad[...] = jnp.zeros_like(gain_grad)

    def mix_turn(total, rows, own):
        values = inputs[own].astype(F32) + total
        residual[own] = values
        normed_ref[rows] = (values * inverse_rms(values) * gain_ref[...]).astype(BF16)

    def turn(total, rows, own):
        values = residual[own]
        inverse = inverse_rms(values)
        unit = values * inverse
        gain_grad[...] += jnp.sum(total * unit, axis=0, keepdims=True)
        lifted = total * gain_ref[...]
        mean = jnp.mean(lifted * unit, axis=-1, keepdims=True)
        grad = cotangent_ref[rows].astype(F32) + inverse * (lifted - unit * mean)
        residual[own] = grad
        out_ref[rows] = grad.astype(BF16)

    mix_line = Line(mesh_axes, part, mix_arrived, normed_ref, sems[:4], mix_turn)
    line = Line(mesh_axes, part, arrived, out_ref, sems[4:8], turn)
    gather = Gather(
        Plane(mesh_axes), (gate_hbm, up_hbm, down_hbm), (gate_w, up_w, down_w), sems[8:]
    )
    barrier = pltpu.get_barrier_semaphore()
    expected = mix_line.greet(barrier) + gather.greet(barrier)
    pl.semaphore_wait(barrier, expected)
    gather.start()
    part_load.wait()
    input_load.wait()
    pace = GROUP // CHUNK
    begin = pace + 2 * LAG * (line_size - 1) + 2
    mix_line.run(0, begin - 10)
    gather.stage(0)
    mix_line.run(begin - 10, begin - 4)
    gather.stage(1)
    mix_line.run(begin - 4, begin)
    gather.stage(2)
    gather.arrive()
    cotangent_load.wait()

    def both(ref, group):
        first = pl.ds(pl.multiple_of(group * GROUP, GROUP), GROUP)
        second = pl.ds(pl.multiple_of(half + group * GROUP, GROUP), GROUP)
        return first, second

    def stage_copies(group):
        slot = lax.rem(group, 2)
        copies = []
        for side, rows in enumerate(both(None, group)):
            from_rows = pl.ds(side * GROUP, GROUP)
            columns = pl.ds(0, hidden_width)
            for which, (stage, target) in enumerate(
                (
                    (stage_hidden, hidden_hbm),
                    (stage_gate, grad_gate_hbm),
                    (stage_up, grad_up_hbm),
                )
            ):
                copies.append(
                    pltpu.make_async_copy(
                        stage.at[slot, from_rows, columns],
                        target.at[rows],
                        stage_sem.at[slot, which, side],
                    )
                )
            copies.append(
                pltpu.make_async_copy(
                    stage_feed.at[slot, from_rows], feed_hbm.at[rows], stage_sem.at[slot, 3, side]
                )
            )
        return copies

    def hidden_tile(group, tile):
        first, second = both(normed_ref, group)
        slot = lax.rem(group, 2)
        columns = pl.ds(pl.multiple_of(tile * WIDE, WIDE), WIDE)
        rows = jnp.concatenate([normed_ref[first], normed_ref[second]], axis=0)
        gate = mm_nn(rows, gate_w[:, columns])
        up = mm_nn(rows, up_w[:, columns])
        grads = jnp.concatenate([cotangent_ref[first], cotangent_ref[second]], axis=0)
        grad = mm_nn(grads, down_w[:, columns])
        sigma = jax.nn.sigmoid(gate)
        active = gate * sigma
        stage_hidden[slot, :, columns] = (active * up).astype(BF16)
        stage_gate[slot, :, columns] = (grad * up * sigma * (1.0 + gate * (1.0 - sigma))).astype(
            BF16
        )
        stage_up[slot, :, columns] = (grad * active).astype(BF16)

    def model_tile(group, tile):
        first, second = both(part, group)
        slot = lax.rem(group, 2)
        columns = pl.ds(pl.multiple_of(tile * WIDE, WIDE), WIDE)
        back = mm_nt(stage_gate[slot], gate_w[columns, :])
        back = (back + mm_nt(stage_up[slot], up_w[columns, :])).astype(BF16)
        part[first, columns] = back[:GROUP]
        part[second, columns] = back[GROUP:]
        stage_feed[slot, :, columns] = mm_nt(stage_hidden[slot], down_w[columns, :]).astype(BF16)

    hidden_tiles, model_tiles = padded // WIDE, model_width // WIDE
    ticks = hidden_tiles + model_tiles
    piece = -(-ticks // pace)
    save = pltpu.make_async_copy(residual, residual_hbm, save_sem.at[0])

    def group_body(group, _):
        mix_line.source_sent(group * pace, (group + 1) * pace)

        @pl.when(group == 1)
        def _():
            save.start()

        @pl.when(group == 2)
        def _():
            save.wait()

        @pl.when(group >= 2)
        def _():
            for copy in stage_copies(group - 2):
                copy.wait()

        def piece_body(index, _):
            def tick_body(offset, _):
                tick = index * piece + offset

                @pl.when(tick < hidden_tiles)
                def _():
                    hidden_tile(group, tick)

                @pl.when(jnp.logical_and(tick >= hidden_tiles, tick < ticks))
                def _():
                    model_tile(group, tick - hidden_tiles)

                return 0

            lax.fori_loop(0, piece, tick_body, 0)

            mix_time = begin + group * pace + index

            @pl.when(mix_time < mix_line.steps)
            def _():
                mix_line.step(mix_time)

            @pl.when(group >= 1)
            def _():
                line.step((group - 1) * pace + index)

            return 0

        lax.fori_loop(0, pace, piece_body, 0)
        for copy in stage_copies(group):
            copy.start()
        return 0

    lax.fori_loop(0, groups, group_body, 0)
    for group in range(max(groups - 2, 0), groups):
        for copy in stage_copies(group):
            copy.wait()
    gather.finish()

    token_rows, hidden_columns = pl.ds(0, tokens), pl.ds(0, hidden_width)
    returned = [
        pltpu.make_async_copy(
            source, target.at[token_rows, hidden_columns], back_sem.at[which]
        )
        for which, (source, target) in enumerate(
            ((grad_gate_hbm, gate_w), (grad_up_hbm, up_w), (hidden_hbm, down_w))
        )
    ]
    for copy in returned:
        copy.start()
    tiles = model_width // TILE
    first_time = (groups - 1) * pace + 1
    stages = (stage_gate, stage_up, stage_hidden)

    def tile_copies(tile):
        rows = pl.ds(pl.multiple_of(tile * TILE, TILE), TILE)
        slot = lax.rem(tile, 2)
        return [
            pltpu.make_async_copy(
                stage.at[slot, pl.ds(0, TILE), hidden_columns],
                grads_hbm.at[rows, pl.ds(which * hidden_width, hidden_width)],
                tile_sem.at[slot, which],
            )
            for which, stage in enumerate(stages)
        ]

    def weight_tile(time):
        tile = time - first_time

        @pl.when(tile == 0)
        def _():
            for copy in returned:
                copy.wait()

        @pl.when(jnp.logical_and(tile >= 2, tile < tiles))
        def _():
            for copy in tile_copies(tile - 2):
                copy.wait()

        @pl.when(jnp.logical_and(tile >= 0, tile < tiles))
        def _():
            slot = lax.rem(tile, 2)
            columns = pl.ds(pl.multiple_of(tile * TILE, TILE), TILE)
            rows = normed_ref[:, columns]
            for source, right, stage in (
                (rows, gate_w, stage_gate),
                (rows, up_w, stage_up),
                (cotangent_ref[:, columns], down_w, stage_hidden),
            ):
                product = mm_tn(source, right[:tokens, :hidden_width])
                stage[slot, :TILE, :hidden_width] = product.astype(BF16)
            for copy in tile_copies(tile):
                copy.start()

    line.run((groups - 1) * pace, line.steps, weight_tile)
    grad_save = pltpu.make_async_copy(residual, grad_hbm, grad_sem.at[0])
    grad_save.start()
    for tile in range(max(tiles - 2, 0), tiles):
        for copy in tile_copies(tile):
            copy.wait()
    mix_line.finish(source_waits=False)
    line.finish()
    grad_save.wait()


def middle(mesh_axes, collective, mix, cotangent, inputs, gain, gate_w, up_w, down_w):
    tokens, model_width = mix.shape
    hidden_width = gate_w.shape[1]
    padded = -(-hidden_width // WIDE) * WIDE
    whole = pl.BlockSpec(memory_space=pltpu.VMEM)
    remote = pl.BlockSpec(memory_space=pl.ANY)
    group_rows = 2 * GROUP
    return pl.pallas_call(
        partial(middle_kernel, mesh_axes),
        in_specs=[remote, remote, remote, whole, remote, remote, remote],
        out_specs=[whole, whole] + [remote] * 7,
        out_shape=[
            jax.ShapeDtypeStruct((tokens, model_width), BF16),
            jax.ShapeDtypeStruct((1, model_width), F32),
            jax.ShapeDtypeStruct((tokens // 2, model_width), F32),
            jax.ShapeDtypeStruct((tokens, hidden_width), BF16),
            jax.ShapeDtypeStruct((tokens, hidden_width), BF16),
            jax.ShapeDtypeStruct((tokens, hidden_width), BF16),
            jax.ShapeDtypeStruct((tokens, model_width), BF16),
            jax.ShapeDtypeStruct((tokens // 2, model_width), F32),
            jax.ShapeDtypeStruct((model_width, 3 * hidden_width), BF16),
        ],
        scratch_shapes=[
            pltpu.VMEM((tokens, model_width), BF16),
            pltpu.VMEM((tokens, model_width), BF16),
            pltpu.VMEM((model_width, padded), BF16),
            pltpu.VMEM((model_width, padded), BF16),
            pltpu.VMEM((model_width, padded), BF16),
            pltpu.VMEM((tokens, model_width), BF16),
            pltpu.VMEM((tokens, model_width), BF16),
            pltpu.VMEM((tokens, model_width), BF16),
            pltpu.VMEM((tokens // 2, model_width), BF16),
            pltpu.VMEM((tokens // 2, model_width), F32),
            pltpu.VMEM((2, group_rows, padded), BF16),
            pltpu.VMEM((2, group_rows, padded), BF16),
            pltpu.VMEM((2, group_rows, padded), BF16),
            pltpu.VMEM((2, group_rows, model_width), BF16),
            pltpu.SemaphoreType.DMA((1,)),
            pltpu.SemaphoreType.DMA((2,)),
            pltpu.SemaphoreType.DMA((1,)),
            pltpu.SemaphoreType.DMA((2, 4, 2)),
            pltpu.SemaphoreType.DMA((1,)),
            pltpu.SemaphoreType.DMA((3,)),
            pltpu.SemaphoreType.DMA((2, 3)),
        ]
        + line_sems(tokens)
        + line_sems(tokens)
        + gather_sems(3),
        compiler_params=pltpu.CompilerParams(
            collective_id=collective, has_side_effects=True, vmem_limit_bytes=61 << 20
        ),
        cost_estimate=pl.CostEstimate(
            flops=tokens * model_width * hidden_width * 12,
            bytes_accessed=360_000_000,
            transcendentals=tokens * hidden_width,
        ),
        name="middle",
    )(mix, cotangent, inputs, gain, gate_w, up_w, down_w)


def output_kernel(
    mesh_axes,
    head_count,
    key_scale,
    run_ref,
    carry_ref,
    decay_ref,
    link_ref,
    open_ref,
    count_ref,
    keep_ref,
    flags_ref,
    gain_ref,
    part_hbm,
    residual_hbm,
    gated_hbm,
    mix_grad_hbm,
    out_full_hbm,
    lead_hbm,
    starts_hbm,
    normed_hbm,
    pre_hbm,
    full_hbm,
    mixed_hbm,
    out_ref,
    gain_grad,
    floor_grad,
    total_ref,
    mixer_grads_hbm,
    part,
    residual,
    gated_ref,
    mix_grad_ref,
    out_full,
    lead_ref,
    starts_ref,
    arrived,
    back,
    back_arrived,
    left,
    right,
    full,
    mixer_stage,
    piece_rows_scr,
    pre,
    grad_mixed,
    back_scr,
    message,
    received,
    grad_scr,
    lifted_scr,
    lowered_scr,
    moved_scr,
    value_scr,
    load_sem,
    piece_sem,
    full_sem,
    pre_sem,
    stage_sem,
    grad_send,
    grad_recv,
    *sems,
):
    tokens, model_width = left.shape
    width = gated_hbm.shape[1]
    lanes = width // head_count
    state_rows = head_count * lanes
    tiles, blocks = model_width // TILE, tokens // BLOCK
    piece_rows = 2 * BLOCK
    context, context_size = lax.axis_index("context"), lax.axis_size("context")

    loads = [
        pltpu.make_async_copy(source, target, load_sem.at[which])
        for which, (source, target) in enumerate(
            (
                (part_hbm, part),
                (out_full_hbm, out_full),
                (mix_grad_hbm, mix_grad_ref),
                (lead_hbm, lead_ref),
                (residual_hbm, residual),
                (starts_hbm, starts_ref),
                (gated_hbm, gated_ref),
                (normed_hbm, left),
            )
        )
    ]
    part_load, *gate_loads = loads[:5]
    starts_load, *tile_loads = loads[5:]
    for load in loads:
        load.start()

    def piece_loads(index):
        rows = pl.ds(pl.multiple_of(index * piece_rows, piece_rows), piece_rows)
        slot = lax.rem(index, 2)
        return (
            pltpu.make_async_copy(
                pre_hbm.at[rows, pl.ds(3 * width, width)],
                piece_rows_scr.at[slot, 0],
                piece_sem.at[slot, 0],
            ),
            pltpu.make_async_copy(
                mixed_hbm.at[rows], piece_rows_scr.at[slot, 1], piece_sem.at[slot, 1]
            ),
        )

    for load in piece_loads(0):
        load.start()
    gain_grad[...] = jnp.zeros_like(gain_grad)
    floor_grad[...] = jnp.zeros_like(floor_grad)
    back_scr[...] = jnp.zeros_like(back_scr)

    def turn(total, rows, own):
        out_ref[rows] = (residual[own] + total).astype(BF16)

    def earlier(shift):
        places = {axis: lax.axis_index(axis) for axis in mesh_axes}
        places["context"] = lax.rem(context + context_size - shift, context_size)
        return tuple(places[axis] for axis in mesh_axes)

    def keep_total(total, rows, own):
        total_ref[own] = total

    line = Line(mesh_axes, part, arrived, out_ref, sems[:4], turn)
    back_line = Line(mesh_axes, back, back_arrived, None, sems[4:], keep_total, backs=False)
    barrier = pltpu.get_barrier_semaphore()
    expected = line.greet(barrier)
    for shift in range(1, context_size):
        pl.semaphore_signal(barrier, inc=1, device_id=earlier(shift), device_id_type=MESH_ID)
    pl.semaphore_wait(barrier, expected + context_size - 1)

    def tile_columns(tile):
        return pl.ds(pl.multiple_of(tile * TILE, TILE), TILE)

    def stage_copy(tile):
        rows = tile_columns(tile)
        return pltpu.make_async_copy(mixer_stage, mixer_grads_hbm.at[rows], stage_sem.at[0])

    def gate_piece(index):
        rows = pl.ds(pl.multiple_of(index * piece_rows, piece_rows), piece_rows)
        slot = lax.rem(index, 2)

        @pl.when(index + 1 < tokens // piece_rows)
        def _():
            for load in piece_loads(index + 1):
                load.start()

        for load in piece_loads(index):
            load.wait()
        grads = mm_nn(mix_grad_ref[rows], out_full[...])
        gain = gain_ref[...]
        total = jnp.zeros_like(gain)
        for head in range(head_count):
            part_of = slice(head * lanes, (head + 1) * lanes)
            gate, mixed = piece_rows_scr[slot, 0, :, part_of], piece_rows_scr[slot, 1, :, part_of]
            grad = grads[:, part_of]
            inverse = inverse_rms(mixed)
            unit = mixed * inverse
            sigma = jax.nn.sigmoid(gate)
            scaled = grad * unit
            total = total + jnp.sum(scaled * (gate * sigma), axis=0, keepdims=True)
            grad_gate = scaled * gain * sigma * (1.0 + gate * (1.0 - sigma))
            first = 3 * width + head * lanes
            right[rows, first : first + lanes] = grad_gate.astype(BF16)
            lifted = grad * gain * (gate * sigma)
            mean = jnp.mean(lifted * unit, axis=-1, keepdims=True)
            grad_in = inverse * (lifted - unit * mean) * (key_scale * keep_ref[rows])
            grad_in = grad_in.astype(BF16)
            grad_mixed[rows, part_of] = grad_in
            back_scr[head] += mm_tn(grad_in, lead_ref[rows, part_of])
        gain_grad[...] += total

    def state_copy(shift):
        return pltpu.make_async_remote_copy(
            message,
            received.at[shift - 1],
            grad_send.at[shift - 1],
            grad_recv.at[shift - 1],
            device_id=earlier(shift),
            device_id_type=MESH_ID,
        )

    def block_of(index):
        return blocks - 1 - index

    def pre_load(index):
        rows = pl.ds(pl.multiple_of(block_of(index) * BLOCK, BLOCK), BLOCK)
        slot = lax.rem(index, 2)
        return pltpu.make_async_copy(
            pre_hbm.at[rows, pl.ds(0, 3 * width)], pre.at[slot], pre_sem.at[slot]
        )

    def send_back():
        for head in range(head_count):
            rows = slice(head * lanes, (head + 1) * lanes)
            message[rows] = back_scr[head] * link_ref[0:1]
            message[state_rows + head : state_rows + head + 1] = decay_ref[head] * link_ref[0:1]
        for shift in range(1, context_size):

            @pl.when(context >= shift)
            def _(shift=shift):
                state_copy(shift).start()

        pre_load(0).start()

    def take_back():
        grad_scr[...] = jnp.zeros_like(grad_scr)
        for shift in range(1, context_size):

            @pl.when(context + shift < context_size)
            def _(shift=shift):
                state_copy(shift).wait_recv()
                for head in range(head_count):
                    value = received[shift - 1, head * lanes : (head + 1) * lanes]
                    for near in range(shift - 1):
                        value = value * received[near, state_rows + head : state_rows + head + 1]
                    grad_scr[head] += value

        for shift in range(1, context_size):

            @pl.when(context >= shift)
            def _(shift=shift):
                state_copy(shift).wait_send()

    def mixer_block(index):
        block = block_of(index)
        slot = lax.rem(index, 2)
        block_rows = pl.ds(pl.multiple_of(block * BLOCK, BLOCK), BLOCK)

        @pl.when(index + 1 < blocks)
        def _():
            pre_load(index + 1).start()

        pre_load(index).wait()
        counts, keep, flags = count_ref[block_rows], keep_ref[block_rows], flags_ref[block]
        row_ids, col_ids, linked, fresh, tail, closing = block_masks(counts, flags)
        tri = (row_ids >= col_ids).astype(BF16)
        tri_back = (row_ids <= col_ids).astype(BF16)
        query_pre = pre[slot, :, :width]
        values = pre[slot, :, 2 * width : 3 * width].astype(BF16)
        opened = open_ref[...]
        closed = jax.nn.sigmoid(-pre[slot, :, width : 2 * width])
        keys = opened * closed
        cum = split_sum(tri, jnp.log1p(-keys))
        ending = cum[BLOCK - 1 : BLOCK, :]
        rise, fall = jnp.exp(cum), jnp.exp(-cum) * keep
        shift = jnp.exp(ending - cum) * (keep * tail)
        sigma_query = jax.nn.sigmoid(query_pre)
        lifted = (query_pre * sigma_query * rise).astype(BF16)
        lowered = (keys * fall).astype(BF16)
        moved = (keys * shift).astype(BF16)
        fresh_lifted = (lifted.astype(F32) * fresh).astype(BF16)
        end_decay = jnp.exp(ending) * closing
        lead_in = jnp.exp(run_ref[block]) * (flags[1:2, 0:1] == 0).astype(F32)
        for head in range(head_count):
            part_of = slice(head * lanes, (head + 1) * lanes)
            grad_out, value = grad_mixed[block_rows, part_of], values[:, part_of]
            lift, lower, move = lifted[:, part_of], lowered[:, part_of], moved[:, part_of]
            scores = jnp.where(linked, mm_nt(lift, lower), 0.0).astype(BF16)
            pulls = jnp.where(linked, mm_nt(grad_out, value), 0.0).astype(BF16)
            state = starts_ref[block, head] + lead_in[:, part_of] * carry_ref[head]
            grad_state = grad_scr[head]
            grad_low = grad_state.astype(BF16)
            lifted_scr[:, part_of] = mm_nn(pulls, lower) + fresh * mm_nn(
                grad_out, state.astype(BF16)
            )
            lowered_scr[:, part_of] = mm_tn(pulls, lift)
            grad_moved = mm_nn(value, grad_low)
            moved_scr[:, part_of] = grad_moved
            first = 2 * width + head * lanes
            right[block_rows, first : first + lanes] = (
                mm_tn(scores, grad_out) + mm_nt(move, grad_low)
            ).astype(BF16)
            value_scr[:, part_of] = jnp.sum(
                grad_moved * move.astype(F32), axis=0, keepdims=True
            ) + end_decay[:, part_of] * jnp.sum(state * grad_state, axis=0, keepdims=True)
            grad_scr[head] = grad_state * end_decay[:, part_of] + mm_tn(
                grad_out, fresh_lifted[:, part_of]
            )
        grad_lifted, grad_lowered, grad_moved = lifted_scr[...], lowered_scr[...], moved_scr[...]
        grad_cum = (
            grad_lifted * lifted.astype(F32)
            - grad_lowered * lowered.astype(F32)
            - grad_moved * moved.astype(F32)
        )
        grad_decay = split_sum(tri_back, grad_cum) + value_scr[...]
        key_total = grad_lowered * fall + grad_moved * shift - grad_decay / (1.0 - keys)
        floor_grad[...] -= jnp.sum(key_total * closed, axis=0, keepdims=True)
        right[block_rows, :width] = (
            grad_lifted * rise * sigma_query * (1.0 + query_pre * (1.0 - sigma_query))
        ).astype(BF16)
        right[block_rows, width : 2 * width] = (
            -key_total * opened * closed * (1.0 - closed)
        ).astype(BF16)

    def full_load(tile):
        slot = lax.rem(tile, 2)
        return pltpu.make_async_copy(
            full_hbm.at[tile_columns(tile)], full.at[slot], full_sem.at[slot]
        )

    def back_tile(tile):
        @pl.when(tile + 1 < tiles)
        def _():
            full_load(tile + 1).start()

        full_load(tile).wait()
        product = mm_nt(right[...], full[lax.rem(tile, 2)])
        back[:, tile_columns(tile)] = product.astype(BF16)

    def mixer_tile(tile):
        @pl.when(tile > 0)
        def _():
            stage_copy(tile - 1).wait()

        columns = tile_columns(tile)
        rows = left[:, columns]
        for first in range(0, 4 * width, 1024):
            some = slice(first, min(first + 1024, 4 * width))
            mixer_stage[:, some] = mm_tn(rows, right[:, some]).astype(BF16)
        product = mm_tn(mix_grad_ref[:, columns], gated_ref[...])
        mixer_stage[:, 4 * width :] = product.astype(BF16)
        stage_copy(tile).start()

    send_time = tokens // piece_rows
    block_time = send_time + 2
    back_time = block_time + blocks
    tile_time = back_time + tiles
    end_time = tile_time + tiles

    def piece(time):
        @pl.when(time == 0)
        def _():
            for load in gate_loads:
                load.wait()

        @pl.when(time < send_time)
        def _():
            gate_piece(time)

        @pl.when(time == send_time)
        def _():
            send_back()

        @pl.when(time == block_time)
        def _():
            starts_load.wait()
            take_back()

        @pl.when(jnp.logical_and(time >= block_time, time < back_time))
        def _():
            mixer_block(time - block_time)

        @pl.when(time == back_time - 1)
        def _():
            full_load(0).start()

        @pl.when(jnp.logical_and(time >= back_time, time < tile_time))
        def _():
            back_tile(time - back_time)

        @pl.when(time == tile_time)
        def _():
            for load in tile_loads:
                load.wait()

        @pl.when(jnp.logical_and(time >= tile_time, time < end_time))
        def _():
            mixer_tile(time - tile_time)

    slow = QUIET
    part_load.wait()
    begin = slow + -(-(tile_time - slow) // MANY)
    steps = max(line.steps, begin + back_line.steps, slow + -(-(end_time - slow) // MANY))

    def body(time, _):
        @pl.when(time < line.steps)
        def _():
            line.step(time)

        @pl.when(time >= begin)
        def _():
            back_line.step(time - begin)

        def pieces(index, _):
            piece(index)
            return 0

        first = jnp.where(time < slow, time, slow + MANY * (time - slow))
        lax.fori_loop(first, first + jnp.where(time < slow, 1, MANY), pieces, 0)
        return 0

    lax.fori_loop(0, steps, body, 0)
    stage_copy(tiles - 1).wait()
    line.finish()
    back_line.finish()


def output_line(mesh_axes, collective, in_vmem, in_hbm, head_count):
    part, residual, gated, mix_grad, out_full, lead, starts = in_hbm[:7]
    tokens, model_width = part.shape
    width = gated.shape[1]
    lanes = width // head_count
    context_size = lax.axis_size("context")
    messages = head_count * lanes + -(-head_count // 8) * 8
    whole = pl.BlockSpec(memory_space=pltpu.VMEM)
    remote = pl.BlockSpec(memory_space=pl.ANY)
    return pl.pallas_call(
        partial(output_kernel, mesh_axes, head_count, lanes ** (-0.5)),
        in_specs=[whole] * len(in_vmem) + [remote] * len(in_hbm),
        out_specs=[whole] * 4 + [remote],
        out_shape=[
            jax.ShapeDtypeStruct((tokens, model_width), BF16),
            jax.ShapeDtypeStruct((1, lanes), F32),
            jax.ShapeDtypeStruct((1, width), F32),
            jax.ShapeDtypeStruct((tokens // 2, model_width), F32),
            jax.ShapeDtypeStruct((model_width, 5 * width), BF16),
        ],
        scratch_shapes=[
            pltpu.VMEM(array.shape, array.dtype)
            for array in (part, residual, gated, mix_grad, out_full, lead, starts)
        ]
        + [
            pltpu.VMEM((tokens, model_width), BF16),
            pltpu.VMEM((tokens, model_width), BF16),
            pltpu.VMEM((tokens, model_width), BF16),
            pltpu.VMEM((tokens, model_width), BF16),
            pltpu.VMEM((tokens, 4 * width), BF16),
            pltpu.VMEM((2, TILE, 4 * width), BF16),
            pltpu.VMEM((TILE, 5 * width), BF16),
            pltpu.VMEM((2, 2, 2 * BLOCK, width), F32),
            pltpu.VMEM((2, BLOCK, 3 * width), F32),
            pltpu.VMEM((tokens, width), BF16),
            pltpu.VMEM((head_count, lanes, lanes), F32),
            pltpu.VMEM((messages, lanes), F32),
            pltpu.VMEM((context_size - 1, messages, lanes), F32),
            pltpu.VMEM((head_count, lanes, lanes), F32),
            pltpu.VMEM((BLOCK, width), F32),
            pltpu.VMEM((BLOCK, width), F32),
            pltpu.VMEM((BLOCK, width), F32),
            pltpu.VMEM((1, width), F32),
            pltpu.SemaphoreType.DMA((8,)),
            pltpu.SemaphoreType.DMA((2, 2)),
            pltpu.SemaphoreType.DMA((2,)),
            pltpu.SemaphoreType.DMA((2,)),
            pltpu.SemaphoreType.DMA((1,)),
            pltpu.SemaphoreType.DMA((context_size - 1,)),
            pltpu.SemaphoreType.DMA((context_size - 1,)),
        ]
        + line_sems(tokens)
        + line_sems(tokens, 2),
        compiler_params=pltpu.CompilerParams(
            collective_id=collective, has_side_effects=True, vmem_limit_bytes=61 << 20
        ),
        cost_estimate=pl.CostEstimate(
            flops=tokens * model_width * width * 24,
            bytes_accessed=360_000_000,
            transcendentals=tokens * width * 12,
        ),
        name="output_line",
    )(*in_vmem, *in_hbm)


class SmallSum:
    def __init__(self, mesh_axes, value, local, total, near, far, sems):
        self.mesh_axes = mesh_axes
        self.value, self.local, self.total, self.near, self.far = value, local, total, near, far
        self.near_send, self.near_recv, self.far_send, self.far_recv = sems
        self.context_size = lax.axis_size("context")
        self.group = lax.axis_size("shard") * self.context_size
        self.line_size = lax.axis_size("tensor")
        self.place = lax.axis_index("shard") * self.context_size + lax.axis_index("context")
        self.line_place = lax.axis_index("tensor")

    def device(self, position, line_position):
        places = {
            "shard": position // self.context_size,
            "context": lax.rem(position, self.context_size),
            "tensor": line_position,
        }
        return tuple(places[axis] for axis in self.mesh_axes)

    def near_target(self, step):
        return self.device(lax.rem(self.place + step, self.group), self.line_place)

    def far_target(self, step):
        return self.device(self.place, lax.rem(self.line_place + step, self.line_size))

    def near_copy(self, step):
        return pltpu.make_async_remote_copy(
            self.value,
            self.near.at[step - 1],
            self.near_send.at[step - 1],
            self.near_recv.at[step - 1],
            device_id=self.near_target(step),
            device_id_type=MESH_ID,
        )

    def far_copy(self, step):
        return pltpu.make_async_remote_copy(
            self.local,
            self.far.at[step - 1],
            self.far_send.at[step - 1],
            self.far_recv.at[step - 1],
            device_id=self.far_target(step),
            device_id_type=MESH_ID,
        )

    def greet(self, barrier):
        targets = [self.near_target(step) for step in range(1, self.group)]
        targets += [self.far_target(step) for step in range(1, self.line_size)]
        for target in targets:
            pl.semaphore_signal(barrier, inc=1, device_id=target, device_id_type=MESH_ID)
        return len(targets)

    def start(self):
        for step in range(1, self.group):
            self.near_copy(step).start()

    def pass_on(self):
        total = self.value[...]
        for step in range(1, self.group):
            self.near_copy(step).wait_recv()
            total = total + self.near[step - 1]
        self.local[...] = total
        for step in range(1, self.line_size):
            self.far_copy(step).start()

    def finish(self):
        total = self.local[...]
        for step in range(1, self.line_size):
            self.far_copy(step).wait_recv()
            total = total + self.far[step - 1]
        self.total[...] = total
        for step in range(1, self.group):
            self.near_copy(step).wait_send()
        for step in range(1, self.line_size):
            self.far_copy(step).wait_send()


def input_kernel(
    mesh_axes,
    gain_ref,
    norm_two_ref,
    head_ref,
    floor_ref,
    total_hbm,
    hidden_hbm,
    residual_hbm,
    grads_hbm,
    out_ref,
    small_local,
    small_total,
    share_query,
    share_forget,
    share_input,
    share_gate,
    share_out,
    total_ref,
    hidden_ref,
    residual_grad,
    own,
    other,
    remote,
    gain_grad,
    small,
    small_near,
    small_far,
    quarter_sem,
    load_sem,
    pair_send,
    pair_recv,
    chip_send,
    chip_recv,
    *sems,
):
    plane = Plane(mesh_axes)
    chips = plane.chips
    block = own.shape[1]
    gain_grad[...] = jnp.zeros_like(gain_grad)
    half, line_size = total_ref.shape[0], lax.axis_size("tensor")
    place = lax.axis_index("tensor")
    at_end = jnp.logical_or(place == 0, place == line_size - 1)
    first_row = jnp.where(place == 0, 0, half)
    quarters = 4
    length = half // quarters

    def quarter_loads(index):
        rows = pl.ds(pl.multiple_of(index * length, length), length)
        inputs = pl.ds(pl.multiple_of(first_row + index * length, length), length)
        return [
            pltpu.make_async_copy(source, target.at[rows], quarter_sem.at[which, index])
            for which, (source, target) in enumerate(
                (
                    (total_hbm.at[rows], total_ref),
                    (hidden_hbm.at[inputs], hidden_ref),
                    (residual_hbm.at[rows], residual_grad),
                )
            )
        ]

    @pl.when(at_end)
    def _():
        for index in range(quarters):
            for load in quarter_loads(index):
                load.start()

    def turn(total, rows, own_rows):
        total = total_ref[own_rows]
        values = hidden_ref[own_rows].astype(F32)
        inverse = inverse_rms(values)
        unit = values * inverse
        gain_grad[...] += jnp.sum(total * unit, axis=0, keepdims=True)
        lifted = total * gain_ref[...]
        mean = jnp.mean(lifted * unit, axis=-1, keepdims=True)
        grad = residual_grad[own_rows] + inverse * (lifted - unit * mean)
        out_ref[rows] = grad.astype(BF16)

    line = Line(mesh_axes, None, None, out_ref, sems[:2], turn, sums=False)
    small_sum = SmallSum(
        mesh_axes, small, small_local, small_total, small_near, small_far, sems[2:]
    )
    barrier = pltpu.get_barrier_semaphore()
    expected = line.greet(barrier) + plane.greet(barrier) + small_sum.greet(barrier)
    pl.semaphore_wait(barrier, expected)

    def rows_of(slot, core):
        return pl.ds(pl.multiple_of((2 * plane.ahead(slot) + core) * block, block), block)

    def load(slot):
        return pltpu.make_async_copy(
            grads_hbm.at[rows_of(slot, plane.core)], own.at[slot], load_sem.at[slot]
        )

    def pair_copy(slot):
        return pltpu.make_async_remote_copy(
            grads_hbm.at[rows_of(slot, 1 - plane.core)],
            other.at[slot],
            pair_send.at[slot],
            pair_recv.at[slot],
            device_id=plane.device(plane.chip, 1 - plane.core),
            device_id_type=MESH_ID,
        )

    def chip_copy(slot):
        return pltpu.make_async_remote_copy(
            own.at[slot],
            remote.at[slot - 1],
            chip_send.at[slot - 1],
            chip_recv.at[slot - 1],
            device_id=plane.device(plane.ahead(slot), plane.core),
            device_id_type=MESH_ID,
        )

    def start(index, _):
        slot = lax.rem(index + 1, chips)
        pair_copy(slot).start()
        load(slot).start()
        return 0

    lax.fori_loop(0, chips, start, 0)
    strip = 32

    def combine(time):
        slot = lax.rem(jnp.clip(time, 0, chips - 1) + 1, chips)

        @pl.when(time < chips)
        def _():
            load(slot).wait()
            pair_copy(slot).wait_recv()

            def add(index, _):
                rows = pl.ds(pl.multiple_of(index * strip, strip), strip)
                total = own[slot, rows].astype(F32) + other[slot, rows].astype(F32)
                own[slot, rows] = total.astype(BF16)
                return 0

            lax.fori_loop(0, block // strip, add, 0)

        @pl.when(time < chips - 1)
        def _():
            chip_copy(slot).start()

    def step(time, _):
        index = time * CHUNK // length
        fresh = jnp.logical_and(lax.rem(time * CHUNK, length) == 0, index < quarters)

        @pl.when(jnp.logical_and(at_end, fresh))
        def _():
            for load in quarter_loads(index):
                load.wait()

        line.step(time)
        combine(time)
        return 0

    lax.fori_loop(0, line.steps, step, 0)
    small[...] = jnp.zeros_like(small)
    row = 0
    for ref in (gain_grad, norm_two_ref, head_ref, floor_ref):
        for first in range(0, ref.shape[1], 128):
            small[row : row + 1] = ref[:, first : first + 128]
            row += 1
    small_sum.start()

    def arrive(index, _):
        chip_copy(index).wait_recv()
        return 0

    lax.fori_loop(1, chips, arrive, 0)

    def total(index, _):
        rows = pl.ds(pl.multiple_of(index * strip, strip), strip)

        for which, share in enumerate(
            (share_query, share_forget, share_input, share_gate, share_out)
        ):
            columns = pl.ds(which * share.shape[1], share.shape[1])

            def add(slot, value, columns=columns):
                return value + remote[slot, rows, columns].astype(F32)

            share[rows] = lax.fori_loop(0, chips - 1, add, own[0, rows, columns].astype(F32))
        return 0

    small_sum.pass_on()
    lax.fori_loop(0, block // strip, total, 0)
    small_sum.finish()

    def sent(index, _):
        pair_copy(index).wait_send()
        return 0

    lax.fori_loop(0, chips, sent, 0)

    def chip_sent(index, _):
        chip_copy(index).wait_send()
        return 0

    lax.fori_loop(1, chips, chip_sent, 0)
    line.finish()


def input_line(mesh_axes, collective, total, hidden, residual_grad, gain, grads, small):
    tokens, model_width = hidden.shape
    all_width = grads.shape[1]
    chips = lax.axis_size("shard") * lax.axis_size("context") // 2
    block = model_width // (2 * chips)
    values = model_width + sum(value.shape[1] for value in small)
    small_shape = (-(-values // 1024) * 8, 128)
    group, line_size = 2 * chips, lax.axis_size("tensor")
    whole = pl.BlockSpec(memory_space=pltpu.VMEM)
    return pl.pallas_call(
        partial(input_kernel, mesh_axes),
        in_specs=[whole] * 4 + [pl.BlockSpec(memory_space=pl.ANY)] * 4,
        out_specs=[whole] * 8,
        out_shape=[
            jax.ShapeDtypeStruct((tokens, model_width), BF16),
            jax.ShapeDtypeStruct(small_shape, F32),
            jax.ShapeDtypeStruct(small_shape, F32),
        ]
        + [jax.ShapeDtypeStruct((block, all_width // 5), F32)] * 5,
        scratch_shapes=[
            pltpu.VMEM((tokens // 2, model_width), F32),
            pltpu.VMEM((tokens // 2, model_width), BF16),
            pltpu.VMEM((tokens // 2, model_width), F32),
            pltpu.VMEM((chips, block, all_width), BF16),
            pltpu.VMEM((chips, block, all_width), BF16),
            pltpu.VMEM((chips - 1, block, all_width), BF16),
            pltpu.VMEM((1, model_width), F32),
            pltpu.VMEM(small_shape, F32),
            pltpu.VMEM((group - 1, *small_shape), F32),
            pltpu.VMEM((line_size - 1, *small_shape), F32),
            pltpu.SemaphoreType.DMA((3, 4)),
            pltpu.SemaphoreType.DMA((chips,)),
            pltpu.SemaphoreType.DMA((chips,)),
            pltpu.SemaphoreType.DMA((chips,)),
            pltpu.SemaphoreType.DMA((chips - 1,)),
            pltpu.SemaphoreType.DMA((chips - 1,)),
        ]
        + line_sems(tokens, 2)
        + [
            pltpu.SemaphoreType.DMA((group - 1,)),
            pltpu.SemaphoreType.DMA((group - 1,)),
            pltpu.SemaphoreType.DMA((line_size - 1,)),
            pltpu.SemaphoreType.DMA((line_size - 1,)),
        ],
        compiler_params=pltpu.CompilerParams(
            collective_id=collective, has_side_effects=True, vmem_limit_bytes=58 << 20
        ),
        cost_estimate=pl.CostEstimate(
            flops=tokens * model_width * 8, bytes_accessed=360_000_000, transcendentals=0
        ),
        name="input_line",
    )(gain, *small, total, hidden, residual_grad, grads)


def forward_kernel(
    mesh_axes,
    head_count,
    key_scale,
    hidden_ref,
    gain_ref,
    query_hbm,
    forget_hbm,
    input_hbm,
    gate_hbm,
    out_shard_ref,
    down_shard_ref,
    floor_ref,
    segments_ref,
    head_gain_ref,
    normed_hbm,
    pre_hbm,
    full_hbm,
    out_full_hbm,
    mixed_hbm,
    lead_hbm,
    start_hbm,
    gated_hbm,
    mix_hbm,
    down_turned,
    open_ref,
    count_ref,
    keep_ref,
    flags_ref,
    run_ref,
    carry_ref,
    decay_ref,
    link_ref,
    normed,
    pre,
    mine,
    out_turned,
    full,
    out_full,
    mixed,
    lead,
    starts,
    gated,
    mix,
    state_scr,
    run_scr,
    message,
    received,
    mine_sem,
    full_sem,
    save_sem,
    pre_sem,
    mix_sem,
    state_send,
    state_recv,
    *sems,
):
    plane = Plane(mesh_axes)
    chips = plane.chips
    tokens, model_width = hidden_ref.shape
    block, width = query_hbm.shape
    lanes = width // head_count
    state_rows = head_count * lanes
    context, context_size = lax.axis_index("context"), lax.axis_size("context")

    mine_loads = [
        pltpu.make_async_copy(
            ref, mine.at[:, pl.ds(which * width, width)], mine_sem.at[which]
        )
        for which, ref in enumerate((query_hbm, forget_hbm, input_hbm, gate_hbm))
    ]
    for load in mine_loads:
        load.start()
    gather = Gather(plane, (mine,), (full,), sems[:5])
    out_gather = Gather(plane, (out_turned,), (out_full,), sems[5:])

    def later(shift):
        places = {axis: lax.axis_index(axis) for axis in mesh_axes}
        places["context"] = lax.rem(context + shift, context_size)
        return tuple(places[axis] for axis in mesh_axes)

    out_turned[...] = out_shard_ref[...].T
    barrier = pltpu.get_barrier_semaphore()
    expected = gather.greet(barrier)
    for shift in range(1, context_size):
        pl.semaphore_signal(barrier, inc=1, device_id=later(shift), device_id_type=MESH_ID)
    pl.semaphore_wait(barrier, expected + context_size - 1)
    for load in mine_loads:
        load.wait()
    gather.start()
    out_gather.start()
    down_turned[...] = down_shard_ref[...].T
    for head in range(head_count):
        open_ref[:, head * lanes : (head + 1) * lanes] = 1.0 - floor_ref[head : head + 1]

    segments = segments_ref[...]
    blocks = segments.shape[0]
    block_ids = lax.broadcasted_iota(jnp.int32, segments.shape, 0)
    slot_ids = lax.broadcasted_iota(jnp.int32, segments.shape, 1)
    before = pltpu.roll(segments, 1, 1)
    wrapped = pltpu.roll(before, 1, 0)
    before = jnp.where(slot_ids == 0, wrapped, before)
    first_slot = jnp.logical_and(slot_ids == 0, block_ids == 0)
    begins = jnp.where(jnp.logical_or(first_slot, segments == before), 0.0, 1.0)
    wide_rows = lax.broadcasted_iota(jnp.int32, (BLOCK, BLOCK), 0)
    wide_columns = lax.broadcasted_iota(jnp.int32, (BLOCK, BLOCK), 1)
    within = mm_nn(begins.astype(BF16), (wide_rows <= wide_columns).astype(BF16))
    count_rows = []
    running = jnp.zeros((1, 1), F32)
    flags_ref[...] = jnp.zeros_like(flags_ref)
    for index in range(blocks):
        row = within[index : index + 1] + running
        flags_ref[index, 0:1] = row
        flags_ref[index, 1:2] = jnp.broadcast_to(running, (1, BLOCK))
        running = row[:, BLOCK - 1 : BLOCK]
        flags_ref[index, 2:3] = jnp.broadcast_to(running, (1, BLOCK))
        count_rows.append(row)
    turned_counts = jnp.concatenate(count_rows, axis=0).T
    turned_keep = (segments > 0).astype(F32).T
    for index in range(blocks):
        rows = slice(index * BLOCK, (index + 1) * BLOCK)
        count_ref[rows] = turned_counts[:, index : index + 1]
        keep_ref[rows] = turned_keep[:, index : index + 1]
    first_id = jnp.broadcast_to(segments[0:1, 0:1], (1, lanes))
    last_id = jnp.broadcast_to(segments[blocks - 1 : blocks, BLOCK - 1 : BLOCK], (1, lanes))

    def norm(index, _):
        rows = pl.ds(pl.multiple_of(index * 128, 128), 128)
        values = hidden_ref[rows].astype(F32)
        normed[rows] = (values * inverse_rms(values) * gain_ref[...]).astype(BF16)
        return 0

    lax.fori_loop(0, tokens // 128, norm, 0)

    saves = [
        pltpu.make_async_copy(source, target, save_sem.at[which])
        for which, (source, target) in enumerate(
            (
                (normed, normed_hbm),
                (out_full, out_full_hbm),
                (mixed, mixed_hbm),
                (lead, lead_hbm),
                (starts, start_hbm),
                (gated, gated_hbm),
            )
        )
    ]
    saves[0].start()
    row_tile, column_tile = 256, 512

    def pre_save(index):
        rows = pl.ds(pl.multiple_of(index * row_tile, row_tile), row_tile)
        return pltpu.make_async_copy(pre.at[rows], pre_hbm.at[rows], pre_sem.at[index])

    def depth_of(distance):
        first = 2 * gather.partner(distance) * block
        return pl.ds(pl.multiple_of(first, 2 * block), 2 * block)

    def product(distance):
        depth = depth_of(distance)

        def row_body(index, _):
            rows = pl.ds(pl.multiple_of(index * row_tile, row_tile), row_tile)
            left = normed[rows, depth]

            def column_body(column, _):
                columns = pl.ds(pl.multiple_of(column * column_tile, column_tile), column_tile)
                value = mm_nn(left, full[depth, columns])
                if distance > 0:
                    value = value + pre[rows, columns]
                pre[rows, columns] = value
                return 0

            lax.fori_loop(0, full.shape[1] // column_tile, column_body, 0)
            if distance == chips - 1:
                pre_save(index).start()
            return 0

        lax.fori_loop(0, tokens // row_tile, row_body, 0)

    def full_save(distance):
        depth = depth_of(distance)
        return pltpu.make_async_copy(full.at[depth], full_hbm.at[depth], full_sem.at[distance])

    def use(distance):
        gather.arrive_from(distance)
        full_save(distance).start()
        product(distance)

    use(0)
    gather.stage(0)
    gather.stage(1)
    if gather.relayed:
        use(1)
        use(2)
    gather.stage(2)
    if gather.relayed:
        use(3)
    else:
        for distance in range(1, chips):
            use(distance)
    out_gather.stage(0)
    out_gather.stage(1)

    state_scr[...] = jnp.zeros_like(state_scr)
    run_scr[...] = jnp.zeros_like(run_scr)

    def recur(step, _):
        rows = pl.ds(pl.multiple_of(step * BLOCK, BLOCK), BLOCK)
        counts, keep = count_ref[rows], keep_ref[rows]
        row_ids, col_ids, linked, fresh, tail, closing = block_masks(counts, flags_ref[step])
        tri = (row_ids >= col_ids).astype(BF16)
        query_pre = pre[rows, :width]
        values = pre[rows, 2 * width : 3 * width].astype(BF16)
        keys = open_ref[...] * jax.nn.sigmoid(-pre[rows, width : 2 * width])
        cum = split_sum(tri, jnp.log1p(-keys))
        ending = cum[BLOCK - 1 : BLOCK, :]
        lifted = query_pre * jax.nn.sigmoid(query_pre) * jnp.exp(cum)
        lowered = (keys * jnp.exp(-cum) * keep).astype(BF16)
        moved = (keys * jnp.exp(ending - cum) * (keep * tail)).astype(BF16)
        run = run_scr[...]
        lead[rows] = (lifted * jnp.exp(run) * (counts == 0).astype(F32)).astype(BF16)
        run_ref[step] = run
        run_scr[...] = run + ending
        fresh_lifted = (lifted * fresh).astype(BF16)
        lifted = lifted.astype(BF16)
        end_decay = jnp.exp(ending) * closing
        for head in range(head_count):
            part = slice(head * lanes, (head + 1) * lanes)
            state = state_scr[head]
            starts[step, head] = state
            scores = jnp.where(linked, mm_nt(lifted[:, part], lowered[:, part]), 0.0)
            results = mm_nn(scores.astype(BF16), values[:, part])
            results = results + mm_nt(fresh_lifted[:, part], state.astype(BF16))
            mixed[rows, part] = results * (key_scale * keep)
            state_scr[head] = state * end_decay[:, part] + mm_tn(values[:, part], moved[:, part])
        return 0

    lax.fori_loop(0, tokens // BLOCK, recur, 0)
    saves[3].start()
    saves[4].start()

    last_count = flags_ref[tokens // BLOCK - 1][2:3, 0:1]
    for head in range(head_count):
        part = slice(head * lanes, (head + 1) * lanes)
        message[head * lanes : (head + 1) * lanes] = state_scr[head]
        decay = jnp.exp(run_scr[:, part]) * (last_count == 0).astype(F32)
        decay_ref[head] = decay
        message[state_rows + 8 + head : state_rows + 9 + head] = decay
    message[state_rows : state_rows + 1] = first_id
    message[state_rows + 1 : state_rows + 2] = last_id

    def state_copy(shift):
        return pltpu.make_async_remote_copy(
            message,
            received.at[shift - 1],
            state_send.at[shift - 1],
            state_recv.at[shift - 1],
            device_id=later(shift),
            device_id_type=MESH_ID,
        )

    for shift in range(1, context_size):

        @pl.when(context + shift < context_size)
        def _(shift=shift):
            state_copy(shift).start()

    out_gather.stage(2)
    carry_ref[...] = jnp.zeros_like(carry_ref)
    link_ref[...] = jnp.zeros_like(link_ref)
    for shift in range(1, context_size):

        @pl.when(context >= shift)
        def _(shift=shift):
            state_copy(shift).wait_recv()
            linked = jnp.ones((1, lanes), F32)
            follower = first_id
            factors = [jnp.ones((1, lanes), F32)] * head_count
            for near in range(shift):
                got = received.at[near]
                linked = (got[state_rows + 1 : state_rows + 2] == follower).astype(F32)
                follower = got[state_rows : state_rows + 1]
                factors = [factor * linked for factor in factors]
                if near < shift - 1:
                    factors = [
                        factor * got[state_rows + 8 + head : state_rows + 9 + head]
                        for head, factor in enumerate(factors)
                    ]
            if shift == 1:
                link_ref[0:1] = linked
            for head in range(head_count):
                rows = slice(head * lanes, (head + 1) * lanes)
                carry_ref[head] += factors[head] * received[shift - 1, rows]

    for shift in range(1, context_size):

        @pl.when(context + shift < context_size)
        def _(shift=shift):
            state_copy(shift).wait_send()

    for distance in range(chips):
        out_gather.arrive_from(distance)
    saves[1].start()

    def mix_save(index):
        rows = pl.ds(pl.multiple_of(index * row_tile, row_tile), row_tile)
        return pltpu.make_async_copy(mix.at[rows], mix_hbm.at[rows], mix_sem.at[index])

    def project(index, _):
        rows = pl.ds(pl.multiple_of(index * row_tile, row_tile), row_tile)
        for head in range(head_count):
            part = slice(head * lanes, (head + 1) * lanes)
            carried = mm_nt(lead[rows, part], carry_ref[head].astype(BF16))
            value = mixed[rows, part] + carried * (key_scale * keep_ref[rows])
            mixed[rows, part] = value
            gate = pre[rows, 3 * width + head * lanes : 3 * width + (head + 1) * lanes]
            unit = value * inverse_rms(value)
            gated[rows, part] = (
                unit * head_gain_ref[...] * (gate * jax.nn.sigmoid(gate))
            ).astype(BF16)
        left = gated[rows]

        def column_body(column, _):
            columns = pl.ds(pl.multiple_of(column * column_tile, column_tile), column_tile)
            mix[rows, columns] = mm_nt(left, out_full[columns, :]).astype(BF16)
            return 0

        lax.fori_loop(0, model_width // column_tile, column_body, 0)
        mix_save(index).start()
        return 0

    lax.fori_loop(0, tokens // row_tile, project, 0)
    saves[2].start()
    saves[5].start()
    gather.finish()
    out_gather.finish()
    for distance in range(chips):
        full_save(distance).wait()
    for save in saves:
        save.wait()
    for index in range(tokens // row_tile):
        pre_save(index).wait()
        mix_save(index).wait()


def forward(
    mesh_axes, collective, hidden, gain, shards, out_shard, down_shard, floor, segments, head_gain
):
    tokens, model_width = hidden.shape
    block, width = shards[0].shape
    lanes = head_gain.shape[1]
    head_count = width // lanes
    all_width = width * len(shards)
    blocks = tokens // BLOCK
    context_size = lax.axis_size("context")
    chips = lax.axis_size("shard") * context_size // 2
    messages = head_count * lanes + 8 + -(-head_count // 8) * 8
    whole = pl.BlockSpec(memory_space=pltpu.VMEM)
    remote = pl.BlockSpec(memory_space=pl.ANY)
    stored = [
        ((tokens, model_width), BF16),
        ((tokens, all_width), F32),
        ((model_width, all_width), BF16),
        ((model_width, width), BF16),
        ((tokens, width), F32),
        ((tokens, width), BF16),
        ((blocks, head_count, lanes, lanes), F32),
        ((tokens, width), BF16),
        ((tokens, model_width), BF16),
    ]
    kept = [
        (down_shard.shape[::-1], BF16),
        ((1, width), F32),
        ((tokens, 1), F32),
        ((tokens, 1), F32),
        ((blocks, 8, BLOCK), F32),
        ((blocks, 1, width), F32),
        ((head_count, lanes, lanes), F32),
        ((head_count, 1, lanes), F32),
        ((8, lanes), F32),
    ]
    return pl.pallas_call(
        partial(forward_kernel, mesh_axes, head_count, lanes ** (-0.5)),
        in_specs=[whole] * 2 + [remote] * 4 + [whole] * 5,
        out_specs=[remote] * len(stored) + [whole] * len(kept),
        out_shape=[jax.ShapeDtypeStruct(shape, kind) for shape, kind in stored + kept],
        scratch_shapes=[
            pltpu.VMEM((tokens, model_width), BF16),
            pltpu.VMEM((tokens, all_width), F32),
            pltpu.VMEM((block, all_width), BF16),
            pltpu.VMEM((block, width), BF16),
            pltpu.VMEM((model_width, all_width), BF16),
            pltpu.VMEM((model_width, width), BF16),
            pltpu.VMEM((tokens, width), F32),
            pltpu.VMEM((tokens, width), BF16),
            pltpu.VMEM((blocks, head_count, lanes, lanes), F32),
            pltpu.VMEM((tokens, width), BF16),
            pltpu.VMEM((tokens, model_width), BF16),
            pltpu.VMEM((head_count, lanes, lanes), F32),
            pltpu.VMEM((1, width), F32),
            pltpu.VMEM((messages, lanes), F32),
            pltpu.VMEM((context_size - 1, messages, lanes), F32),
            pltpu.SemaphoreType.DMA((4,)),
            pltpu.SemaphoreType.DMA((chips,)),
            pltpu.SemaphoreType.DMA((6,)),
            pltpu.SemaphoreType.DMA((tokens // 256,)),
            pltpu.SemaphoreType.DMA((tokens // 256,)),
            pltpu.SemaphoreType.DMA((context_size - 1,)),
            pltpu.SemaphoreType.DMA((context_size - 1,)),
        ]
        + gather_sems(1)
        + gather_sems(1),
        compiler_params=pltpu.CompilerParams(
            collective_id=collective, has_side_effects=True, vmem_limit_bytes=56 << 20
        ),
        cost_estimate=pl.CostEstimate(
            flops=2 * tokens * model_width * all_width,
            bytes_accessed=200_000_000,
            transcendentals=tokens * width * 9,
        ),
        name="forward",
    )(hidden, gain, *shards, out_shard, down_shard, floor, segments, head_gain)


def local(
    mesh_axes,
    hidden,
    segment_ids,
    norm1_gain,
    w_query,
    w_forget,
    w_input,
    w_gate_out,
    forget_floor,
    head_gain,
    w_out,
    norm2_gain,
    w_ffn_gate,
    w_ffn_up,
    w_ffn_down,
    out_grad,
):
    sequences, span_len, model_width = hidden.shape
    tokens = sequences * span_len
    head_count, key_dim = forget_floor.shape
    width = head_count * key_dim
    key_scale = key_dim ** (-0.5)
    both = ("shard", "context")
    gain_one, gain_two = norm1_gain.reshape(1, -1), norm2_gain.reshape(1, -1)
    hidden_rows = hidden.reshape(tokens, model_width)
    gain_row = head_gain.reshape(1, -1)
    segments = segment_ids.reshape(tokens // BLOCK, BLOCK).astype(F32)
    (
        normed_one,
        pre,
        mixer_full,
        out_full,
        mixed,
        lead,
        starts,
        gated_low,
        mix_part,
        down_turned,
        open_part,
        counts,
        keep,
        flags,
        runs,
        carry,
        decay,
        link,
    ) = forward(
        mesh_axes,
        4,
        hidden_rows,
        gain_one,
        (w_query, w_forget, w_input, w_gate_out),
        w_out,
        w_ffn_down,
        forget_floor,
        segments,
        gain_row,
    )
    grad_rows = out_grad.reshape(tokens, model_width)
    (
        grad_mix_low,
        grad_norm_two,
        residual,
        _,
        _,
        _,
        feed_part,
        grad_residual,
        grads_ffn,
    ) = middle(
        mesh_axes,
        2,
        mix_part,
        grad_rows,
        hidden_rows,
        gain_two,
        w_ffn_gate,
        w_ffn_up,
        down_turned,
    )
    (
        output_rows,
        grad_head_part,
        grad_floor_part,
        back_one,
        grads_mixer,
    ) = output_line(
        mesh_axes,
        1,
        (
            runs,
            carry,
            decay,
            link,
            open_part,
            counts,
            keep,
            flags,
            gain_row,
        ),
        (
            feed_part,
            residual,
            gated_low,
            grad_mix_low,
            out_full,
            lead,
            starts,
            normed_one,
            pre,
            mixer_full,
            mixed,
        ),
        head_count,
    )
    share_ffn = lax.psum_scatter(grads_ffn, both, scatter_dimension=0, tiled=True)
    hidden_width = w_ffn_gate.shape[1]

    def ffn_share(which):
        return share_ffn[:, which * hidden_width : (which + 1) * hidden_width].astype(F32)

    input_rows, near, total, *mixer_shares, share_out = input_line(
        mesh_axes,
        3,
        back_one,
        hidden_rows,
        grad_residual,
        gain_one,
        grads_mixer,
        (grad_norm_two, grad_head_part, grad_floor_part),
    )
    near, total = near.reshape(-1), total.reshape(-1)
    shares = lax.axis_size("shard") * lax.axis_size("context")
    position = lax.axis_index("shard") * lax.axis_size("context") + lax.axis_index("context")

    def own_slice(first, length):
        length = length // shares
        return lax.dynamic_slice_in_dim(total, first + position * length, length, 0)

    first = 2 * model_width + key_dim
    floor_total = near[first : first + width].reshape(head_count, key_dim)
    floor_part = key_dim // shares

    return (
        output_rows.reshape(hidden.shape),
        input_rows.reshape(hidden.shape),
        own_slice(0, model_width),
        *mixer_shares,
        lax.dynamic_slice_in_dim(floor_total, position * floor_part, floor_part, 1),
        own_slice(2 * model_width, key_dim),
        share_out.T,
        own_slice(model_width, model_width),
        ffn_share(0),
        ffn_share(1),
        ffn_share(2).T,
    )


def solution(mesh):
    in_specs = (
        P("shard", "context", None),
        P("shard", "context"),
        P(),
        P(("shard", "context"), "tensor"),
        P(("shard", "context"), "tensor"),
        P(("shard", "context"), "tensor"),
        P(("shard", "context"), "tensor"),
        P("tensor", None),
        P(),
        P("tensor", ("shard", "context")),
        P(),
        P(("shard", "context"), "tensor"),
        P(("shard", "context"), "tensor"),
        P("tensor", ("shard", "context")),
        P("shard", "context", None),
    )
    out_specs = (
        P("shard", "context", None),
        P("shard", "context", None),
        P(("shard", "context")),
        P(("shard", "context"), "tensor"),
        P(("shard", "context"), "tensor"),
        P(("shard", "context"), "tensor"),
        P(("shard", "context"), "tensor"),
        P("tensor", ("shard", "context")),
        P(("shard", "context")),
        P("tensor", ("shard", "context")),
        P(("shard", "context")),
        P(("shard", "context"), "tensor"),
        P(("shard", "context"), "tensor"),
        P("tensor", ("shard", "context")),
    )
    return jax.shard_map(
        partial(local, mesh.axis_names), mesh=mesh, in_specs=in_specs, out_specs=out_specs, check_vma=False)
```

```python
from functools import partial

import jax
import jax.numpy as jnp
from jax import lax
from jax.experimental import pallas as pl
from jax.experimental.pallas import tpu as pltpu
from jax.sharding import PartitionSpec as P

EPSILON = 1e-05


BLOCK = 128
F32 = jnp.float32
BF16 = jnp.bfloat16


def mm(a, b, dims):
    return lax.dot_general(a, b, (dims, ((), ())), preferred_element_type=F32)


def mm_nn(a, b):
    return mm(a, b, ((1,), (0,)))


def mm_nt(a, b):
    return mm(a, b, ((1,), (1,)))


def mm_tn(a, b):
    return mm(a, b, ((0,), (0,)))


def split_sum(tri, values):
    high = values.astype(BF16)
    low = (values - high.astype(F32)).astype(BF16)
    return mm_nn(tri, high) + mm_nn(tri, low)


def block_masks(counts, flags_row):
    rows = counts.shape[0]
    row_ids = lax.broadcasted_iota(jnp.int32, (rows, rows), 0)
    col_ids = lax.broadcasted_iota(jnp.int32, (rows, rows), 1)
    linked = jnp.logical_and(counts == flags_row[0:1], row_ids >= col_ids)
    fresh = (counts == flags_row[1:2, 0:1]).astype(F32)
    tail = (counts == flags_row[2:3, 0:1]).astype(F32)
    closing = (flags_row[1:2, 0:1] == flags_row[2:3, 0:1]).astype(F32)
    return row_ids, col_ids, linked, fresh, tail, closing


CHUNK = 32
QUIET, MANY = 6, 2
LAG = 2
MESH_ID = pl.DeviceIdType.MESH


class Line:
    def __init__(self, mesh_axes, part, arrived, out, sems, transform, sums=True, backs=True):
        self.mesh_axes = mesh_axes
        self.sums, self.backs = sums, backs
        self.part, self.arrived, self.out = part, arrived, out
        if sums:
            self.sum_send, self.sum_recv = sems[:2]
        if backs:
            self.back_send, self.back_recv = sems[-2:]
        self.transform = transform
        self.half = (part if sums else out).shape[0] // 2
        self.chunks = self.half // CHUNK
        self.size = lax.axis_size("tensor")
        self.place = lax.axis_index("tensor")
        self.lines = ((self.size - 1 - self.place, -1), (self.place, 1))
        self.offset = LAG * (self.size - 1) if sums else 0
        self.steps = self.chunks + self.offset + (LAG * (self.size - 1) if backs else 0)

    def device(self, position):
        return tuple(
            jnp.clip(position, 0, self.size - 1) if axis == "tensor" else lax.axis_index(axis)
            for axis in self.mesh_axes
        )

    def greet(self, barrier):
        for step in (-1, 1):
            inside = jnp.logical_and(self.place + step >= 0, self.place + step < self.size)

            @pl.when(inside)
            def _(step=step):
                pl.semaphore_signal(
                    barrier, inc=1, device_id=self.device(self.place + step), device_id_type=MESH_ID
                )

        at_end = jnp.logical_or(self.place == 0, self.place == self.size - 1)
        return jnp.where(at_end, 1, 2)

    def rows_of(self, side, index):
        return pl.ds(pl.multiple_of(side * self.half + index * CHUNK, CHUNK), CHUNK)

    def sum_copy(self, side, index, source):
        rows = self.rows_of(side, index)
        return pltpu.make_async_remote_copy(
            source.at[rows],
            self.arrived.at[rows],
            self.sum_send.at[side, index],
            self.sum_recv.at[side, index],
            device_id=self.device(self.place + self.lines[side][1]),
            device_id_type=MESH_ID,
        )

    def back_copy(self, side, index):
        rows = self.rows_of(side, index)
        return pltpu.make_async_remote_copy(
            self.out.at[rows],
            self.out.at[rows],
            self.back_send.at[side, index],
            self.back_recv.at[side, index],
            device_id=self.device(self.place - self.lines[side][1]),
            device_id_type=MESH_ID,
        )

    def step(self, time):
        for side in (0, 1):
            hops = self.lines[side][0]
            at_source, at_owner = hops == 0, hops == self.size - 1
            if self.sums:
                self.sum_step(time, side, hops, at_source, at_owner)
            if self.backs:
                self.back_step(time, side, hops, at_owner)

    def sum_step(self, time, side, hops, at_source, at_owner):
        index = time - LAG * hops
        valid = jnp.logical_and(index >= 0, index < self.chunks)
        index = jnp.clip(index, 0, self.chunks - 1)
        rows = self.rows_of(side, index)

        @pl.when(jnp.logical_and(valid, at_source))
        def _():
            self.sum_copy(side, index, self.part).start()

        @pl.when(jnp.logical_and(valid, jnp.logical_not(at_source)))
        def _():
            self.sum_copy(side, index, self.arrived).wait_recv()

        between = jnp.logical_and(jnp.logical_not(at_source), jnp.logical_not(at_owner))

        @pl.when(jnp.logical_and(valid, between))
        def _():
            total = self.part[rows].astype(F32) + self.arrived[rows].astype(F32)
            self.arrived[rows] = total.astype(BF16)
            self.sum_copy(side, index, self.arrived).start()

        @pl.when(jnp.logical_and(valid, at_owner))
        def _():
            total = self.part[rows].astype(F32) + self.arrived[rows].astype(F32)
            self.turn(total, side, index)

    def turn(self, total, side, index):
        own = pl.ds(pl.multiple_of(index * CHUNK, CHUNK), CHUNK)
        self.transform(total, self.rows_of(side, index), own)
        if self.backs:
            self.back_copy(side, index).start()

    def back_step(self, time, side, hops, at_owner):
        if not self.sums:

            @pl.when(jnp.logical_and(at_owner, time < self.chunks))
            def _():
                self.turn(None, side, jnp.clip(time, 0, self.chunks - 1))

        away = self.size - 1 - hops
        index = time - self.offset - LAG * away
        valid = jnp.logical_and(jnp.logical_and(index >= 0, index < self.chunks), away > 0)
        index = jnp.clip(index, 0, self.chunks - 1)

        @pl.when(valid)
        def _():
            self.back_copy(side, index).wait_recv()

        @pl.when(jnp.logical_and(valid, away < self.size - 1))
        def _():
            self.back_copy(side, index).start()

    def run(self, first, last, beside=None):
        def body(time, _):
            self.step(time)
            if beside is not None:
                beside(time)
            return 0

        lax.fori_loop(first, last, body, 0)

    def source_sent(self, first, last):
        def body(index, _):
            for side in (0, 1):

                @pl.when(self.lines[side][0] == 0)
                def _(side=side):
                    self.sum_copy(side, index, self.part).wait_send()

            return 0

        lax.fori_loop(first, last, body, 0)

    def finish(self, source_waits=True):
        def body(index, _):
            for side in (0, 1):
                hops = self.lines[side][0]
                passed = hops < self.size - 1
                if not source_waits:
                    passed = jnp.logical_and(passed, hops > 0)

                if self.sums:

                    @pl.when(passed)
                    def _(side=side):
                        self.sum_copy(side, index, self.arrived).wait_send()

                if self.backs:

                    @pl.when(hops > 0)
                    def _(side=side):
                        self.back_copy(side, index).wait_send()

            return 0

        lax.fori_loop(0, self.chunks, body, 0)


def line_sems(tokens, count=4):
    return [pltpu.SemaphoreType.DMA((2, tokens // 2 // CHUNK))] * count


def inverse_rms(values):
    return lax.rsqrt(jnp.mean(values * values, axis=-1, keepdims=True) + EPSILON)


class Plane:
    def __init__(self, mesh_axes):
        self.mesh_axes = mesh_axes
        self.context = lax.axis_size("context")
        self.per_row = self.context // 2
        self.chips = lax.axis_size("shard") * self.per_row
        context_place = lax.axis_index("context")
        self.core = lax.rem(context_place, 2)
        self.chip = lax.axis_index("shard") * self.per_row + context_place // 2

    def device(self, chip, core):
        places = {
            "shard": chip // self.per_row,
            "context": 2 * lax.rem(chip, self.per_row) + core,
            "tensor": lax.axis_index("tensor"),
        }
        return tuple(places[axis] for axis in self.mesh_axes)

    def ahead(self, distance):
        return lax.rem(self.chip + distance, self.chips)

    def greet(self, barrier):
        targets = [self.device(self.chip, 1 - self.core)]
        targets += [self.device(self.ahead(step), self.core) for step in range(1, self.chips)]
        for target in targets:
            pl.semaphore_signal(barrier, inc=1, device_id=target, device_id_type=MESH_ID)
        return len(targets)


class Gather:
    def __init__(self, plane, sources, targets, sems):
        self.plane, self.sources, self.targets = plane, sources, targets
        self.load_sem, self.send_sem, self.recv_sem, self.pair_send, self.pair_recv = sems
        self.block = sources[0].shape[0]
        self.part = self.block // 2
        self.relayed = plane.chips == 4
        self.arrays = range(len(sources))

    def partner(self, distance):
        return jnp.bitwise_xor(self.plane.chip, distance)

    def greet(self, barrier):
        plane = self.plane
        targets = [plane.device(plane.chip, 1 - plane.core)]
        targets += [
            plane.device(self.partner(step), plane.core)
            for step in range(1, 3 if self.relayed else plane.chips)
        ]
        for target in targets:
            pl.semaphore_signal(barrier, inc=1, device_id=target, device_id_type=MESH_ID)
        return len(targets)

    def place(self, array, chip, core, half):
        first = (2 * chip + core) * self.block + half * self.part
        rows = pl.ds(pl.multiple_of(first, self.part), self.part)
        return self.targets[array].at[rows, pl.ds(0, self.sources[array].shape[1])]

    def mine(self, array, half):
        return self.sources[array].at[pl.ds(half * self.part, self.part)]

    def loads(self):
        plane = self.plane
        return [
            pltpu.make_async_copy(
                self.mine(array, half),
                self.place(array, plane.chip, plane.core, half),
                self.load_sem.at[array, half],
            )
            for array in self.arrays
            for half in range(2)
        ]

    def send(self, distance, half):
        plane = self.plane
        copies = []
        for array in self.arrays:
            chip, target = plane.chip, self.partner(distance)
            source = self.mine(array, half)
            if self.relayed and distance == 3:
                chip = self.partner(2 if half == 0 else 1)
                target = self.partner(1 if half == 0 else 2)
                source = self.place(array, chip, plane.core, half)
            copies.append(
                pltpu.make_async_remote_copy(
                    source,
                    self.place(array, chip, plane.core, half),
                    self.send_sem.at[array, distance - 1, half],
                    self.recv_sem.at[array, distance - 1, half],
                    device_id=plane.device(target, plane.core),
                    device_id_type=MESH_ID,
                )
            )
        return copies

    def forward(self, distance, half):
        plane = self.plane
        copies = []
        for array in self.arrays:
            place = self.place(array, self.partner(distance), plane.core, half)
            copies.append(
                pltpu.make_async_remote_copy(
                    self.mine(array, half) if distance == 0 else place,
                    place,
                    self.pair_send.at[array, distance, half],
                    self.pair_recv.at[array, distance, half],
                    device_id=plane.device(plane.chip, 1 - plane.core),
                    device_id_type=MESH_ID,
                )
            )
        return copies

    def start(self):
        if self.relayed:
            order = ((1, 1), (2, 0), (1, 0), (2, 1))
        else:
            order = [(step, half) for step in range(1, self.plane.chips) for half in range(2)]
        for distance, half in order:
            for copy in self.send(distance, half):
                copy.start()
        for copy in self.loads():
            copy.start()
        for half in range(2):
            for copy in self.forward(0, half):
                copy.start()

    def take(self, distance, half, relay):
        for copy in self.send(distance, half):
            copy.wait_recv()
        if relay:
            for copy in self.send(3, half):
                copy.start()
        for copy in self.forward(distance, half):
            copy.start()

    def stage(self, number):
        if self.relayed:
            if number == 0:
                self.take(1, 1, True)
                self.take(2, 0, True)
            elif number == 1:
                self.take(1, 0, False)
                self.take(2, 1, False)
            else:
                self.take(3, 0, False)
                self.take(3, 1, False)
        elif number == 2:
            for distance in range(1, self.plane.chips):
                for half in range(2):
                    self.take(distance, half, False)

    def arrive_from(self, distance):
        if distance == 0:
            for copy in self.loads():
                copy.wait()
        for half in range(2):
            for copy in self.forward(distance, half):
                copy.wait_recv()

    def arrive(self):
        for distance in range(self.plane.chips):
            self.arrive_from(distance)

    def finish(self):
        for distance in range(self.plane.chips):
            for half in range(2):
                for copy in self.forward(distance, half):
                    copy.wait_send()
                if distance > 0:
                    for copy in self.send(distance, half):
                        copy.wait_send()


def gather_sems(arrays):
    chips = lax.axis_size("shard") * lax.axis_size("context") // 2
    return [
        pltpu.SemaphoreType.DMA((arrays, 2)),
        pltpu.SemaphoreType.DMA((arrays, chips - 1, 2)),
        pltpu.SemaphoreType.DMA((arrays, chips - 1, 2)),
        pltpu.SemaphoreType.DMA((arrays, chips, 2)),
        pltpu.SemaphoreType.DMA((arrays, chips, 2)),
    ]


GROUP = 128
TILE = 256
WIDE = 512


def middle_kernel(
    mesh_axes,
    mix_hbm,
    cotangent_hbm,
    input_hbm,
    gain_ref,
    gate_hbm,
    up_hbm,
    down_hbm,
    out_ref,
    gain_grad,
    residual_hbm,
    hidden_hbm,
    grad_gate_hbm,
    grad_up_hbm,
    feed_hbm,
    grad_hbm,
    grads_hbm,
    normed_ref,
    cotangent_ref,
    gate_w,
    up_w,
    down_w,
    part,
    mix_arrived,
    arrived,
    inputs,
    residual,
    stage_hidden,
    stage_gate,
    stage_up,
    stage_feed,
    part_sem,
    input_sem,
    save_sem,
    stage_sem,
    grad_sem,
    back_sem,
    tile_sem,
    *sems,
):
    tokens, model_width = normed_ref.shape
    half = tokens // 2
    hidden_width = gate_hbm.shape[1]
    padded = gate_w.shape[1]
    groups = half // GROUP
    place, line_size = lax.axis_index("tensor"), lax.axis_size("tensor")
    own_half = pl.ds(pl.multiple_of(jnp.where(place == 0, 0, half), half), half)
    part_load = pltpu.make_async_copy(mix_hbm, part, part_sem.at[0])
    part_load.start()
    input_load = pltpu.make_async_copy(input_hbm.at[own_half], inputs, input_sem.at[0])
    input_load.start()
    cotangent_load = pltpu.make_async_copy(cotangent_hbm, cotangent_ref, input_sem.at[1])
    cotangent_load.start()
    if padded > hidden_width:
        spare = slice(hidden_width, padded)
        gate_w[:, spare] = jnp.zeros((model_width, padded - hidden_width), BF16)
        up_w[:, spare] = jnp.zeros((model_width, padded - hidden_width), BF16)
        down_w[:, spare] = jnp.zeros((model_width, padded - hidden_width), BF16)
    gain_grad[...] = jnp.zeros_like(gain_grad)

    def mix_turn(total, rows, own):
        values = inputs[own].astype(F32) + total
        residual[own] = values
        normed_ref[rows] = (values * inverse_rms(values) * gain_ref[...]).astype(BF16)

    def turn(total, rows, own):
        values = residual[own]
        inverse = inverse_rms(values)
        unit = values * inverse
        gain_grad[...] += jnp.sum(total * unit, axis=0, keepdims=True)
        lifted = total * gain_ref[...]
        mean = jnp.mean(lifted * unit, axis=-1, keepdims=True)
        grad = cotangent_ref[rows].astype(F32) + inverse * (lifted - unit * mean)
        residual[own] = grad
        out_ref[rows] = grad.astype(BF16)

    mix_line = Line(mesh_axes, part, mix_arrived, normed_ref, sems[:4], mix_turn)
    line = Line(mesh_axes, part, arrived, out_ref, sems[4:8], turn)
    gather = Gather(
        Plane(mesh_axes), (gate_hbm, up_hbm, down_hbm), (gate_w, up_w, down_w), sems[8:]
    )
    barrier = pltpu.get_barrier_semaphore()
    expected = mix_line.greet(barrier) + gather.greet(barrier)
    pl.semaphore_wait(barrier, expected)
    gather.start()
    part_load.wait()
    input_load.wait()
    pace = GROUP // CHUNK
    begin = pace + 2 * LAG * (line_size - 1) + 2
    mix_line.run(0, begin - 10)
    gather.stage(0)
    mix_line.run(begin - 10, begin - 4)
    gather.stage(1)
    mix_line.run(begin - 4, begin)
    gather.stage(2)
    gather.arrive()
    cotangent_load.wait()

    def both(ref, group):
        first = pl.ds(pl.multiple_of(group * GROUP, GROUP), GROUP)
        second = pl.ds(pl.multiple_of(half + group * GROUP, GROUP), GROUP)
        return first, second

    def stage_copies(group):
        slot = lax.rem(group, 2)
        copies = []
        for side, rows in enumerate(both(None, group)):
            from_rows = pl.ds(side * GROUP, GROUP)
            columns = pl.ds(0, hidden_width)
            for which, (stage, target) in enumerate(
                (
                    (stage_hidden, hidden_hbm),
                    (stage_gate, grad_gate_hbm),
                    (stage_up, grad_up_hbm),
                )
            ):
                copies.append(
                    pltpu.make_async_copy(
                        stage.at[slot, from_rows, columns],
                        target.at[rows],
                        stage_sem.at[slot, which, side],
                    )
                )
            copies.append(
                pltpu.make_async_copy(
                    stage_feed.at[slot, from_rows], feed_hbm.at[rows], stage_sem.at[slot, 3, side]
                )
            )
        return copies

    def hidden_tile(group, tile):
        first, second = both(normed_ref, group)
        slot = lax.rem(group, 2)
        columns = pl.ds(pl.multiple_of(tile * WIDE, WIDE), WIDE)
        rows = jnp.concatenate([normed_ref[first], normed_ref[second]], axis=0)
        gate = mm_nn(rows, gate_w[:, columns])
        up = mm_nn(rows, up_w[:, columns])
        grads = jnp.concatenate([cotangent_ref[first], cotangent_ref[second]], axis=0)
        grad = mm_nn(grads, down_w[:, columns])
        sigma = jax.nn.sigmoid(gate)
        active = gate * sigma
        stage_hidden[slot, :, columns] = (active * up).astype(BF16)
        stage_gate[slot, :, columns] = (grad * up * sigma * (1.0 + gate * (1.0 - sigma))).astype(
            BF16
        )
        stage_up[slot, :, columns] = (grad * active).astype(BF16)

    def model_tile(group, tile):
        first, second = both(part, group)
        slot = lax.rem(group, 2)
        columns = pl.ds(pl.multiple_of(tile * WIDE, WIDE), WIDE)
        back = mm_nt(stage_gate[slot], gate_w[columns, :])
        back = (back + mm_nt(stage_up[slot], up_w[columns, :])).astype(BF16)
        part[first, columns] = back[:GROUP]
        part[second, columns] = back[GROUP:]
        stage_feed[slot, :, columns] = mm_nt(stage_hidden[slot], down_w[columns, :]).astype(BF16)

    hidden_tiles, model_tiles = padded // WIDE, model_width // WIDE
    ticks = hidden_tiles + model_tiles
    piece = -(-ticks // pace)
    save = pltpu.make_async_copy(residual, residual_hbm, save_sem.at[0])

    def group_body(group, _):
        mix_line.source_sent(group * pace, (group + 1) * pace)

        @pl.when(group == 1)
        def _():
            save.start()

        @pl.when(group == 2)
        def _():
            save.wait()

        @pl.when(group >= 2)
        def _():
            for copy in stage_copies(group - 2):
                copy.wait()

        def piece_body(index, _):
            def tick_body(offset, _):
                tick = index * piece + offset

                @pl.when(tick < hidden_tiles)
                def _():
                    hidden_tile(group, tick)

                @pl.when(jnp.logical_and(tick >= hidden_tiles, tick < ticks))
                def _():
                    model_tile(group, tick - hidden_tiles)

                return 0

            lax.fori_loop(0, piece, tick_body, 0)

            mix_time = begin + group * pace + index

            @pl.when(mix_time < mix_line.steps)
            def _():
                mix_line.step(mix_time)

            @pl.when(group >= 1)
            def _():
                line.step((group - 1) * pace + index)

            return 0

        lax.fori_loop(0, pace, piece_body, 0)
        for copy in stage_copies(group):
            copy.start()
        return 0

    lax.fori_loop(0, groups, group_body, 0)
    for group in range(max(groups - 2, 0), groups):
        for copy in stage_copies(group):
            copy.wait()
    gather.finish()

    token_rows, hidden_columns = pl.ds(0, tokens), pl.ds(0, hidden_width)
    returned = [
        pltpu.make_async_copy(
            source, target.at[token_rows, hidden_columns], back_sem.at[which]
        )
        for which, (source, target) in enumerate(
            ((grad_gate_hbm, gate_w), (grad_up_hbm, up_w), (hidden_hbm, down_w))
        )
    ]
    for copy in returned:
        copy.start()
    tiles = model_width // TILE
    first_time = (groups - 1) * pace + 1
    stages = (stage_gate, stage_up, stage_hidden)

    def tile_copies(tile):
        rows = pl.ds(pl.multiple_of(tile * TILE, TILE), TILE)
        slot = lax.rem(tile, 2)
        return [
            pltpu.make_async_copy(
                stage.at[slot, pl.ds(0, TILE), hidden_columns],
                grads_hbm.at[rows, pl.ds(which * hidden_width, hidden_width)],
                tile_sem.at[slot, which],
            )
            for which, stage in enumerate(stages)
        ]

    def weight_tile(time):
        tile = time - first_time

        @pl.when(tile == 0)
        def _():
            for copy in returned:
                copy.wait()

        @pl.when(jnp.logical_and(tile >= 2, tile < tiles))
        def _():
            for copy in tile_copies(tile - 2):
                copy.wait()

        @pl.when(jnp.logical_and(tile >= 0, tile < tiles))
        def _():
            slot = lax.rem(tile, 2)
            columns = pl.ds(pl.multiple_of(tile * TILE, TILE), TILE)
            rows = normed_ref[:, columns]
            for source, right, stage in (
                (rows, gate_w, stage_gate),
                (rows, up_w, stage_up),
                (cotangent_ref[:, columns], down_w, stage_hidden),
            ):
                product = mm_tn(source, right[:tokens, :hidden_width])
                stage[slot, :TILE, :hidden_width] = product.astype(BF16)
            for copy in tile_copies(tile):
                copy.start()

    line.run((groups - 1) * pace, line.steps, weight_tile)
    grad_save = pltpu.make_async_copy(residual, grad_hbm, grad_sem.at[0])
    grad_save.start()
    for tile in range(max(tiles - 2, 0), tiles):
        for copy in tile_copies(tile):
            copy.wait()
    mix_line.finish(source_waits=False)
    line.finish()
    grad_save.wait()


def middle(mesh_axes, collective, mix, cotangent, inputs, gain, gate_w, up_w, down_w):
    tokens, model_width = mix.shape
    hidden_width = gate_w.shape[1]
    padded = -(-hidden_width // WIDE) * WIDE
    whole = pl.BlockSpec(memory_space=pltpu.VMEM)
    remote = pl.BlockSpec(memory_space=pl.ANY)
    group_rows = 2 * GROUP
    return pl.pallas_call(
        partial(middle_kernel, mesh_axes),
        in_specs=[remote, remote, remote, whole, remote, remote, remote],
        out_specs=[whole, whole] + [remote] * 7,
        out_shape=[
            jax.ShapeDtypeStruct((tokens, model_width), BF16),
            jax.ShapeDtypeStruct((1, model_width), F32),
            jax.ShapeDtypeStruct((tokens // 2, model_width), F32),
            jax.ShapeDtypeStruct((tokens, hidden_width), BF16),
            jax.ShapeDtypeStruct((tokens, hidden_width), BF16),
            jax.ShapeDtypeStruct((tokens, hidden_width), BF16),
            jax.ShapeDtypeStruct((tokens, model_width), BF16),
            jax.ShapeDtypeStruct((tokens // 2, model_width), F32),
            jax.ShapeDtypeStruct((model_width, 3 * hidden_width), BF16),
        ],
        scratch_shapes=[
            pltpu.VMEM((tokens, model_width), BF16),
            pltpu.VMEM((tokens, model_width), BF16),
            pltpu.VMEM((model_width, padded), BF16),
            pltpu.VMEM((model_width, padded), BF16),
            pltpu.VMEM((model_width, padded), BF16),
            pltpu.VMEM((tokens, model_width), BF16),
            pltpu.VMEM((tokens, model_width), BF16),
            pltpu.VMEM((tokens, model_width), BF16),
            pltpu.VMEM((tokens // 2, model_width), BF16),
            pltpu.VMEM((tokens // 2, model_width), F32),
            pltpu.VMEM((2, group_rows, padded), BF16),
            pltpu.VMEM((2, group_rows, padded), BF16),
            pltpu.VMEM((2, group_rows, padded), BF16),
            pltpu.VMEM((2, group_rows, model_width), BF16),
            pltpu.SemaphoreType.DMA((1,)),
            pltpu.SemaphoreType.DMA((2,)),
            pltpu.SemaphoreType.DMA((1,)),
            pltpu.SemaphoreType.DMA((2, 4, 2)),
            pltpu.SemaphoreType.DMA((1,)),
            pltpu.SemaphoreType.DMA((3,)),
            pltpu.SemaphoreType.DMA((2, 3)),
        ]
        + line_sems(tokens)
        + line_sems(tokens)
        + gather_sems(3),
        compiler_params=pltpu.CompilerParams(
            collective_id=collective, has_side_effects=True, vmem_limit_bytes=61 << 20
        ),
        cost_estimate=pl.CostEstimate(
            flops=tokens * model_width * hidden_width * 12,
            bytes_accessed=360_000_000,
            transcendentals=tokens * hidden_width,
        ),
        name="middle",
    )(mix, cotangent, inputs, gain, gate_w, up_w, down_w)


def output_kernel(
    mesh_axes,
    head_count,
    key_scale,
    run_ref,
    carry_ref,
    decay_ref,
    link_ref,
    open_ref,
    count_ref,
    keep_ref,
    flags_ref,
    gain_ref,
    part_hbm,
    residual_hbm,
    gated_hbm,
    mix_grad_hbm,
    out_full_hbm,
    lead_hbm,
    starts_hbm,
    normed_hbm,
    pre_hbm,
    full_hbm,
    mixed_hbm,
    out_ref,
    gain_grad,
    floor_grad,
    total_ref,
    mixer_grads_hbm,
    part,
    residual,
    gated_ref,
    mix_grad_ref,
    out_full,
    lead_ref,
    starts_ref,
    arrived,
    back,
    back_arrived,
    left,
    right,
    full,
    mixer_stage,
    piece_rows_scr,
    pre,
    grad_mixed,
    back_scr,
    message,
    received,
    grad_scr,
    lifted_scr,
    lowered_scr,
    moved_scr,
    value_scr,
    load_sem,
    piece_sem,
    full_sem,
    pre_sem,
    stage_sem,
    grad_send,
    grad_recv,
    *sems,
):
    tokens, model_width = left.shape
    width = gated_hbm.shape[1]
    lanes = width // head_count
    state_rows = head_count * lanes
    tiles, blocks = model_width // TILE, tokens // BLOCK
    piece_rows = 2 * BLOCK
    context, context_size = lax.axis_index("context"), lax.axis_size("context")

    loads = [
        pltpu.make_async_copy(source, target, load_sem.at[which])
        for which, (source, target) in enumerate(
            (
                (part_hbm, part),
                (out_full_hbm, out_full),
                (mix_grad_hbm, mix_grad_ref),
                (lead_hbm, lead_ref),
                (residual_hbm, residual),
                (starts_hbm, starts_ref),
                (gated_hbm, gated_ref),
                (normed_hbm, left),
            )
        )
    ]
    part_load, *gate_loads = loads[:5]
    starts_load, *tile_loads = loads[5:]
    for load in loads:
        load.start()

    def piece_loads(index):
        rows = pl.ds(pl.multiple_of(index * piece_rows, piece_rows), piece_rows)
        slot = lax.rem(index, 2)
        return (
            pltpu.make_async_copy(
                pre_hbm.at[rows, pl.ds(3 * width, width)],
                piece_rows_scr.at[slot, 0],
                piece_sem.at[slot, 0],
            ),
            pltpu.make_async_copy(
                mixed_hbm.at[rows], piece_rows_scr.at[slot, 1], piece_sem.at[slot, 1]
            ),
        )

    for load in piece_loads(0):
        load.start()
    gain_grad[...] = jnp.zeros_like(gain_grad)
    floor_grad[...] = jnp.zeros_like(floor_grad)
    back_scr[...] = jnp.zeros_like(back_scr)

    def turn(total, rows, own):
        out_ref[rows] = (residual[own] + total).astype(BF16)

    def earlier(shift):
        places = {axis: lax.axis_index(axis) for axis in mesh_axes}
        places["context"] = lax.rem(context + context_size - shift, context_size)
        return tuple(places[axis] for axis in mesh_axes)

    def keep_total(total, rows, own):
        total_ref[own] = total

    line = Line(mesh_axes, part, arrived, out_ref, sems[:4], turn)
    back_line = Line(mesh_axes, back, back_arrived, None, sems[4:], keep_total, backs=False)
    barrier = pltpu.get_barrier_semaphore()
    expected = line.greet(barrier)
    for shift in range(1, context_size):
        pl.semaphore_signal(barrier, inc=1, device_id=earlier(shift), device_id_type=MESH_ID)
    pl.semaphore_wait(barrier, expected + context_size - 1)

    def tile_columns(tile):
        return pl.ds(pl.multiple_of(tile * TILE, TILE), TILE)

    def stage_copy(tile):
        rows = tile_columns(tile)
        return pltpu.make_async_copy(mixer_stage, mixer_grads_hbm.at[rows], stage_sem.at[0])

    def gate_piece(index):
        rows = pl.ds(pl.multiple_of(index * piece_rows, piece_rows), piece_rows)
        slot = lax.rem(index, 2)

        @pl.when(index + 1 < tokens // piece_rows)
        def _():
            for load in piece_loads(index + 1):
                load.start()

        for load in piece_loads(index):
            load.wait()
        grads = mm_nn(mix_grad_ref[rows], out_full[...])
        gain = gain_ref[...]
        total = jnp.zeros_like(gain)
        for head in range(head_count):
            part_of = slice(head * lanes, (head + 1) * lanes)
            gate, mixed = piece_rows_scr[slot, 0, :, part_of], piece_rows_scr[slot, 1, :, part_of]
            grad = grads[:, part_of]
            inverse = inverse_rms(mixed)
            unit = mixed * inverse
            sigma = jax.nn.sigmoid(gate)
            scaled = grad * unit
            total = total + jnp.sum(scaled * (gate * sigma), axis=0, keepdims=True)
            grad_gate = scaled * gain * sigma * (1.0 + gate * (1.0 - sigma))
            first = 3 * width + head * lanes
            right[rows, first : first + lanes] = grad_gate.astype(BF16)
            lifted = grad * gain * (gate * sigma)
            mean = jnp.mean(lifted * unit, axis=-1, keepdims=True)
            grad_in = inverse * (lifted - unit * mean) * (key_scale * keep_ref[rows])
            grad_in = grad_in.astype(BF16)
            grad_mixed[rows, part_of] = grad_in
            back_scr[head] += mm_tn(grad_in, lead_ref[rows, part_of])
        gain_grad[...] += total

    def state_copy(shift):
        return pltpu.make_async_remote_copy(
            message,
            received.at[shift - 1],
            grad_send.at[shift - 1],
            grad_recv.at[shift - 1],
            device_id=earlier(shift),
            device_id_type=MESH_ID,
        )

    def block_of(index):
        return blocks - 1 - index

    def pre_load(index):
        rows = pl.ds(pl.multiple_of(block_of(index) * BLOCK, BLOCK), BLOCK)
        slot = lax.rem(index, 2)
        return pltpu.make_async_copy(
            pre_hbm.at[rows, pl.ds(0, 3 * width)], pre.at[slot], pre_sem.at[slot]
        )

    def send_back():
        for head in range(head_count):
            rows = slice(head * lanes, (head + 1) * lanes)
            message[rows] = back_scr[head] * link_ref[0:1]
            message[state_rows + head : state_rows + head + 1] = decay_ref[head] * link_ref[0:1]
        for shift in range(1, context_size):

            @pl.when(context >= shift)
            def _(shift=shift):
                state_copy(shift).start()

        pre_load(0).start()

    def take_back():
        grad_scr[...] = jnp.zeros_like(grad_scr)
        for shift in range(1, context_size):

            @pl.when(context + shift < context_size)
            def _(shift=shift):
                state_copy(shift).wait_recv()
                for head in range(head_count):
                    value = received[shift - 1, head * lanes : (head + 1) * lanes]
                    for near in range(shift - 1):
                        value = value * received[near, state_rows + head : state_rows + head + 1]
                    grad_scr[head] += value

        for shift in range(1, context_size):

            @pl.when(context >= shift)
            def _(shift=shift):
                state_copy(shift).wait_send()

    def mixer_block(index):
        block = block_of(index)
        slot = lax.rem(index, 2)
        block_rows = pl.ds(pl.multiple_of(block * BLOCK, BLOCK), BLOCK)

        @pl.when(index + 1 < blocks)
        def _():
            pre_load(index + 1).start()

        pre_load(index).wait()
        counts, keep, flags = count_ref[block_rows], keep_ref[block_rows], flags_ref[block]
        row_ids, col_ids, linked, fresh, tail, closing = block_masks(counts, flags)
        tri = (row_ids >= col_ids).astype(BF16)
        tri_back = (row_ids <= col_ids).astype(BF16)
        query_pre = pre[slot, :, :width]
        values = pre[slot, :, 2 * width : 3 * width].astype(BF16)
        opened = open_ref[...]
        closed = jax.nn.sigmoid(-pre[slot, :, width : 2 * width])
        keys = opened * closed
        cum = split_sum(tri, jnp.log1p(-keys))
        ending = cum[BLOCK - 1 : BLOCK, :]
        rise, fall = jnp.exp(cum), jnp.exp(-cum) * keep
        shift = jnp.exp(ending - cum) * (keep * tail)
        sigma_query = jax.nn.sigmoid(query_pre)
        lifted = (query_pre * sigma_query * rise).astype(BF16)
        lowered = (keys * fall).astype(BF16)
        moved = (keys * shift).astype(BF16)
        fresh_lifted = (lifted.astype(F32) * fresh).astype(BF16)
        end_decay = jnp.exp(ending) * closing
        lead_in = jnp.exp(run_ref[block]) * (flags[1:2, 0:1] == 0).astype(F32)
        for head in range(head_count):
            part_of = slice(head * lanes, (head + 1) * lanes)
            grad_out, value = grad_mixed[block_rows, part_of], values[:, part_of]
            lift, lower, move = lifted[:, part_of], lowered[:, part_of], moved[:, part_of]
            scores = jnp.where(linked, mm_nt(lift, lower), 0.0).astype(BF16)
            pulls = jnp.where(linked, mm_nt(grad_out, value), 0.0).astype(BF16)
            state = starts_ref[block, head] + lead_in[:, part_of] * carry_ref[head]
            grad_state = grad_scr[head]
            grad_low = grad_state.astype(BF16)
            lifted_scr[:, part_of] = mm_nn(pulls, lower) + fresh * mm_nn(
                grad_out, state.astype(BF16)
            )
            lowered_scr[:, part_of] = mm_tn(pulls, lift)
            grad_moved = mm_nn(value, grad_low)
            moved_scr[:, part_of] = grad_moved
            first = 2 * width + head * lanes
            right[block_rows, first : first + lanes] = (
                mm_tn(scores, grad_out) + mm_nt(move, grad_low)
            ).astype(BF16)
            value_scr[:, part_of] = jnp.sum(
                grad_moved * move.astype(F32), axis=0, keepdims=True
            ) + end_decay[:, part_of] * jnp.sum(state * grad_state, axis=0, keepdims=True)
            grad_scr[head] = grad_state * end_decay[:, part_of] + mm_tn(
                grad_out, fresh_lifted[:, part_of]
            )
        grad_lifted, grad_lowered, grad_moved = lifted_scr[...], lowered_scr[...], moved_scr[...]
        grad_cum = (
            grad_lifted * lifted.astype(F32)
            - grad_lowered * lowered.astype(F32)
            - grad_moved * moved.astype(F32)
        )
        grad_decay = split_sum(tri_back, grad_cum) + value_scr[...]
        key_total = grad_lowered * fall + grad_moved * shift - grad_decay / (1.0 - keys)
        floor_grad[...] -= jnp.sum(key_total * closed, axis=0, keepdims=True)
        right[block_rows, :width] = (
            grad_lifted * rise * sigma_query * (1.0 + query_pre * (1.0 - sigma_query))
        ).astype(BF16)
        right[block_rows, width : 2 * width] = (
            -key_total * opened * closed * (1.0 - closed)
        ).astype(BF16)

    def full_load(tile):
        slot = lax.rem(tile, 2)
        return pltpu.make_async_copy(
            full_hbm.at[tile_columns(tile)], full.at[slot], full_sem.at[slot]
        )

    def back_tile(tile):
        @pl.when(tile + 1 < tiles)
        def _():
            full_load(tile + 1).start()

        full_load(tile).wait()
        product = mm_nt(right[...], full[lax.rem(tile, 2)])
        back[:, tile_columns(tile)] = product.astype(BF16)

    def mixer_tile(tile):
        @pl.when(tile > 0)
        def _():
            stage_copy(tile - 1).wait()

        columns = tile_columns(tile)
        rows = left[:, columns]
        for first in range(0, 4 * width, 1024):
            some = slice(first, min(first + 1024, 4 * width))
            mixer_stage[:, some] = mm_tn(rows, right[:, some]).astype(BF16)
        product = mm_tn(mix_grad_ref[:, columns], gated_ref[...])
        mixer_stage[:, 4 * width :] = product.astype(BF16)
        stage_copy(tile).start()

    send_time = tokens // piece_rows
    block_time = send_time + 2
    back_time = block_time + blocks
    tile_time = back_time + tiles
    end_time = tile_time + tiles

    def piece(time):
        @pl.when(time == 0)
        def _():
            for load in gate_loads:
                load.wait()

        @pl.when(time < send_time)
        def _():
            gate_piece(time)

        @pl.when(time == send_time)
        def _():
            send_back()

        @pl.when(time == block_time)
        def _():
            starts_load.wait()
            take_back()

        @pl.when(jnp.logical_and(time >= block_time, time < back_time))
        def _():
            mixer_block(time - block_time)

        @pl.when(time == back_time - 1)
        def _():
            full_load(0).start()

        @pl.when(jnp.logical_and(time >= back_time, time < tile_time))
        def _():
            back_tile(time - back_time)

        @pl.when(time == tile_time)
        def _():
            for load in tile_loads:
                load.wait()

        @pl.when(jnp.logical_and(time >= tile_time, time < end_time))
        def _():
            mixer_tile(time - tile_time)

    slow = QUIET
    part_load.wait()
    begin = slow + -(-(tile_time - slow) // MANY)
    steps = max(line.steps, begin + back_line.steps, slow + -(-(end_time - slow) // MANY))

    def body(time, _):
        @pl.when(time < line.steps)
        def _():
            line.step(time)

        @pl.when(time >= begin)
        def _():
            back_line.step(time - begin)

        def pieces(index, _):
            piece(index)
            return 0

        first = jnp.where(time < slow, time, slow + MANY * (time - slow))
        lax.fori_loop(first, first + jnp.where(time < slow, 1, MANY), pieces, 0)
        return 0

    lax.fori_loop(0, steps, body, 0)
    stage_copy(tiles - 1).wait()
    line.finish()
    back_line.finish()


def output_line(mesh_axes, collective, in_vmem, in_hbm, head_count):
    part, residual, gated, mix_grad, out_full, lead, starts = in_hbm[:7]
    tokens, model_width = part.shape
    width = gated.shape[1]
    lanes = width // head_count
    context_size = lax.axis_size("context")
    messages = head_count * lanes + -(-head_count // 8) * 8
    whole = pl.BlockSpec(memory_space=pltpu.VMEM)
    remote = pl.BlockSpec(memory_space=pl.ANY)
    return pl.pallas_call(
        partial(output_kernel, mesh_axes, head_count, lanes ** (-0.5)),
        in_specs=[whole] * len(in_vmem) + [remote] * len(in_hbm),
        out_specs=[whole] * 4 + [remote],
        out_shape=[
            jax.ShapeDtypeStruct((tokens, model_width), BF16),
            jax.ShapeDtypeStruct((1, lanes), F32),
            jax.ShapeDtypeStruct((1, width), F32),
            jax.ShapeDtypeStruct((tokens // 2, model_width), F32),
            jax.ShapeDtypeStruct((model_width, 5 * width), BF16),
        ],
        scratch_shapes=[
            pltpu.VMEM(array.shape, array.dtype)
            for array in (part, residual, gated, mix_grad, out_full, lead, starts)
        ]
        + [
            pltpu.VMEM((tokens, model_width), BF16),
            pltpu.VMEM((tokens, model_width), BF16),
            pltpu.VMEM((tokens, model_width), BF16),
            pltpu.VMEM((tokens, model_width), BF16),
            pltpu.VMEM((tokens, 4 * width), BF16),
            pltpu.VMEM((2, TILE, 4 * width), BF16),
            pltpu.VMEM((TILE, 5 * width), BF16),
            pltpu.VMEM((2, 2, 2 * BLOCK, width), F32),
            pltpu.VMEM((2, BLOCK, 3 * width), F32),
            pltpu.VMEM((tokens, width), BF16),
            pltpu.VMEM((head_count, lanes, lanes), F32),
            pltpu.VMEM((messages, lanes), F32),
            pltpu.VMEM((context_size - 1, messages, lanes), F32),
            pltpu.VMEM((head_count, lanes, lanes), F32),
            pltpu.VMEM((BLOCK, width), F32),
            pltpu.VMEM((BLOCK, width), F32),
            pltpu.VMEM((BLOCK, width), F32),
            pltpu.VMEM((1, width), F32),
            pltpu.SemaphoreType.DMA((8,)),
            pltpu.SemaphoreType.DMA((2, 2)),
            pltpu.SemaphoreType.DMA((2,)),
            pltpu.SemaphoreType.DMA((2,)),
            pltpu.SemaphoreType.DMA((1,)),
            pltpu.SemaphoreType.DMA((context_size - 1,)),
            pltpu.SemaphoreType.DMA((context_size - 1,)),
        ]
        + line_sems(tokens)
        + line_sems(tokens, 2),
        compiler_params=pltpu.CompilerParams(
            collective_id=collective, has_side_effects=True, vmem_limit_bytes=61 << 20
        ),
        cost_estimate=pl.CostEstimate(
            flops=tokens * model_width * width * 24,
            bytes_accessed=360_000_000,
            transcendentals=tokens * width * 12,
        ),
        name="output_line",
    )(*in_vmem, *in_hbm)


class SmallSum:
    def __init__(self, mesh_axes, value, local, total, near, far, sems):
        self.mesh_axes = mesh_axes
        self.value, self.local, self.total, self.near, self.far = value, local, total, near, far
        self.near_send, self.near_recv, self.far_send, self.far_recv = sems
        self.context_size = lax.axis_size("context")
        self.group = lax.axis_size("shard") * self.context_size
        self.line_size = lax.axis_size("tensor")
        self.place = lax.axis_index("shard") * self.context_size + lax.axis_index("context")
        self.line_place = lax.axis_index("tensor")

    def device(self, position, line_position):
        places = {
            "shard": position // self.context_size,
            "context": lax.rem(position, self.context_size),
            "tensor": line_position,
        }
        return tuple(places[axis] for axis in self.mesh_axes)

    def near_target(self, step):
        return self.device(lax.rem(self.place + step, self.group), self.line_place)

    def far_target(self, step):
        return self.device(self.place, lax.rem(self.line_place + step, self.line_size))

    def near_copy(self, step):
        return pltpu.make_async_remote_copy(
            self.value,
            self.near.at[step - 1],
            self.near_send.at[step - 1],
            self.near_recv.at[step - 1],
            device_id=self.near_target(step),
            device_id_type=MESH_ID,
        )

    def far_copy(self, step):
        return pltpu.make_async_remote_copy(
            self.local,
            self.far.at[step - 1],
            self.far_send.at[step - 1],
            self.far_recv.at[step - 1],
            device_id=self.far_target(step),
            device_id_type=MESH_ID,
        )

    def greet(self, barrier):
        targets = [self.near_target(step) for step in range(1, self.group)]
        targets += [self.far_target(step) for step in range(1, self.line_size)]
        for target in targets:
            pl.semaphore_signal(barrier, inc=1, device_id=target, device_id_type=MESH_ID)
        return len(targets)

    def start(self):
        for step in range(1, self.group):
            self.near_copy(step).start()

    def pass_on(self):
        total = self.value[...]
        for step in range(1, self.group):
            self.near_copy(step).wait_recv()
            total = total + self.near[step - 1]
        self.local[...] = total
        for step in range(1, self.line_size):
            self.far_copy(step).start()

    def finish(self):
        total = self.local[...]
        for step in range(1, self.line_size):
            self.far_copy(step).wait_recv()
            total = total + self.far[step - 1]
        self.total[...] = total
        for step in range(1, self.group):
            self.near_copy(step).wait_send()
        for step in range(1, self.line_size):
            self.far_copy(step).wait_send()


def input_kernel(
    mesh_axes,
    gain_ref,
    norm_two_ref,
    head_ref,
    floor_ref,
    total_hbm,
    hidden_hbm,
    residual_hbm,
    grads_hbm,
    out_ref,
    small_local,
    small_total,
    share_query,
    share_forget,
    share_input,
    share_gate,
    share_out,
    total_ref,
    hidden_ref,
    residual_grad,
    own,
    other,
    remote,
    gain_grad,
    small,
    small_near,
    small_far,
    quarter_sem,
    load_sem,
    pair_send,
    pair_recv,
    chip_send,
    chip_recv,
    *sems,
):
    plane = Plane(mesh_axes)
    chips = plane.chips
    block = own.shape[1]
    gain_grad[...] = jnp.zeros_like(gain_grad)
    half, line_size = total_ref.shape[0], lax.axis_size("tensor")
    place = lax.axis_index("tensor")
    at_end = jnp.logical_or(place == 0, place == line_size - 1)
    first_row = jnp.where(place == 0, 0, half)
    quarters = 4
    length = half // quarters

    def quarter_loads(index):
        rows = pl.ds(pl.multiple_of(index * length, length), length)
        inputs = pl.ds(pl.multiple_of(first_row + index * length, length), length)
        return [
            pltpu.make_async_copy(source, target.at[rows], quarter_sem.at[which, index])
            for which, (source, target) in enumerate(
                (
                    (total_hbm.at[rows], total_ref),
                    (hidden_hbm.at[inputs], hidden_ref),
                    (residual_hbm.at[rows], residual_grad),
                )
            )
        ]

    @pl.when(at_end)
    def _():
        for index in range(quarters):
            for load in quarter_loads(index):
                load.start()

    def turn(total, rows, own_rows):
        total = total_ref[own_rows]
        values = hidden_ref[own_rows].astype(F32)
        inverse = inverse_rms(values)
        unit = values * inverse
        gain_grad[...] += jnp.sum(total * unit, axis=0, keepdims=True)
        lifted = total * gain_ref[...]
        mean = jnp.mean(lifted * unit, axis=-1, keepdims=True)
        grad = residual_grad[own_rows] + inverse * (lifted - unit * mean)
        out_ref[rows] = grad.astype(BF16)

    line = Line(mesh_axes, None, None, out_ref, sems[:2], turn, sums=False)
    small_sum = SmallSum(
        mesh_axes, small, small_local, small_total, small_near, small_far, sems[2:]
    )
    barrier = pltpu.get_barrier_semaphore()
    expected = line.greet(barrier) + plane.greet(barrier) + small_sum.greet(barrier)
    pl.semaphore_wait(barrier, expected)

    def rows_of(slot, core):
        return pl.ds(pl.multiple_of((2 * plane.ahead(slot) + core) * block, block), block)

    def load(slot):
        return pltpu.make_async_copy(
            grads_hbm.at[rows_of(slot, plane.core)], own.at[slot], load_sem.at[slot]
        )

    def pair_copy(slot):
        return pltpu.make_async_remote_copy(
            grads_hbm.at[rows_of(slot, 1 - plane.core)],
            other.at[slot],
            pair_send.at[slot],
            pair_recv.at[slot],
            device_id=plane.device(plane.chip, 1 - plane.core),
            device_id_type=MESH_ID,
        )

    def chip_copy(slot):
        return pltpu.make_async_remote_copy(
            own.at[slot],
            remote.at[slot - 1],
            chip_send.at[slot - 1],
            chip_recv.at[slot - 1],
            device_id=plane.device(plane.ahead(slot), plane.core),
            device_id_type=MESH_ID,
        )

    def start(index, _):
        slot = lax.rem(index + 1, chips)
        pair_copy(slot).start()
        load(slot).start()
        return 0

    lax.fori_loop(0, chips, start, 0)
    strip = 32

    def combine(time):
        slot = lax.rem(jnp.clip(time, 0, chips - 1) + 1, chips)

        @pl.when(time < chips)
        def _():
            load(slot).wait()
            pair_copy(slot).wait_recv()

            def add(index, _):
                rows = pl.ds(pl.multiple_of(index * strip, strip), strip)
                total = own[slot, rows].astype(F32) + other[slot, rows].astype(F32)
                own[slot, rows] = total.astype(BF16)
                return 0

            lax.fori_loop(0, block // strip, add, 0)

        @pl.when(time < chips - 1)
        def _():
            chip_copy(slot).start()

    def step(time, _):
        index = time * CHUNK // length
        fresh = jnp.logical_and(lax.rem(time * CHUNK, length) == 0, index < quarters)

        @pl.when(jnp.logical_and(at_end, fresh))
        def _():
            for load in quarter_loads(index):
                load.wait()

        line.step(time)
        combine(time)
        return 0

    lax.fori_loop(0, line.steps, step, 0)
    small[...] = jnp.zeros_like(small)
    row = 0
    for ref in (gain_grad, norm_two_ref, head_ref, floor_ref):
        for first in range(0, ref.shape[1], 128):
            small[row : row + 1] = ref[:, first : first + 128]
            row += 1
    small_sum.start()

    def arrive(index, _):
        chip_copy(index).wait_recv()
        return 0

    lax.fori_loop(1, chips, arrive, 0)

    def total(index, _):
        rows = pl.ds(pl.multiple_of(index * strip, strip), strip)

        for which, share in enumerate(
            (share_query, share_forget, share_input, share_gate, share_out)
        ):
            columns = pl.ds(which * share.shape[1], share.shape[1])

            def add(slot, value, columns=columns):
                return value + remote[slot, rows, columns].astype(F32)

            share[rows] = lax.fori_loop(0, chips - 1, add, own[0, rows, columns].astype(F32))
        return 0

    small_sum.pass_on()
    lax.fori_loop(0, block // strip, total, 0)
    small_sum.finish()

    def sent(index, _):
        pair_copy(index).wait_send()
        return 0

    lax.fori_loop(0, chips, sent, 0)

    def chip_sent(index, _):
        chip_copy(index).wait_send()
        return 0

    lax.fori_loop(1, chips, chip_sent, 0)
    line.finish()


def input_line(mesh_axes, collective, total, hidden, residual_grad, gain, grads, small):
    tokens, model_width = hidden.shape
    all_width = grads.shape[1]
    chips = lax.axis_size("shard") * lax.axis_size("context") // 2
    block = model_width // (2 * chips)
    values = model_width + sum(value.shape[1] for value in small)
    small_shape = (-(-values // 1024) * 8, 128)
    group, line_size = 2 * chips, lax.axis_size("tensor")
    whole = pl.BlockSpec(memory_space=pltpu.VMEM)
    return pl.pallas_call(
        partial(input_kernel, mesh_axes),
        in_specs=[whole] * 4 + [pl.BlockSpec(memory_space=pl.ANY)] * 4,
        out_specs=[whole] * 8,
        out_shape=[
            jax.ShapeDtypeStruct((tokens, model_width), BF16),
            jax.ShapeDtypeStruct(small_shape, F32),
            jax.ShapeDtypeStruct(small_shape, F32),
        ]
        + [jax.ShapeDtypeStruct((block, all_width // 5), F32)] * 5,
        scratch_shapes=[
            pltpu.VMEM((tokens // 2, model_width), F32),
            pltpu.VMEM((tokens // 2, model_width), BF16),
            pltpu.VMEM((tokens // 2, model_width), F32),
            pltpu.VMEM((chips, block, all_width), BF16),
            pltpu.VMEM((chips, block, all_width), BF16),
            pltpu.VMEM((chips - 1, block, all_width), BF16),
            pltpu.VMEM((1, model_width), F32),
            pltpu.VMEM(small_shape, F32),
            pltpu.VMEM((group - 1, *small_shape), F32),
            pltpu.VMEM((line_size - 1, *small_shape), F32),
            pltpu.SemaphoreType.DMA((3, 4)),
            pltpu.SemaphoreType.DMA((chips,)),
            pltpu.SemaphoreType.DMA((chips,)),
            pltpu.SemaphoreType.DMA((chips,)),
            pltpu.SemaphoreType.DMA((chips - 1,)),
            pltpu.SemaphoreType.DMA((chips - 1,)),
        ]
        + line_sems(tokens, 2)
        + [
            pltpu.SemaphoreType.DMA((group - 1,)),
            pltpu.SemaphoreType.DMA((group - 1,)),
            pltpu.SemaphoreType.DMA((line_size - 1,)),
            pltpu.SemaphoreType.DMA((line_size - 1,)),
        ],
        compiler_params=pltpu.CompilerParams(
            collective_id=collective, has_side_effects=True, vmem_limit_bytes=58 << 20
        ),
        cost_estimate=pl.CostEstimate(
            flops=tokens * model_width * 8, bytes_accessed=360_000_000, transcendentals=0
        ),
        name="input_line",
    )(gain, *small, total, hidden, residual_grad, grads)


def forward_kernel(
    mesh_axes,
    head_count,
    key_scale,
    hidden_ref,
    gain_ref,
    query_hbm,
    forget_hbm,
    input_hbm,
    gate_hbm,
    out_shard_ref,
    down_shard_ref,
    floor_ref,
    segments_ref,
    head_gain_ref,
    normed_hbm,
    pre_hbm,
    full_hbm,
    out_full_hbm,
    mixed_hbm,
    lead_hbm,
    start_hbm,
    gated_hbm,
    mix_hbm,
    down_turned,
    open_ref,
    count_ref,
    keep_ref,
    flags_ref,
    run_ref,
    carry_ref,
    decay_ref,
    link_ref,
    normed,
    pre,
    mine,
    out_turned,
    full,
    out_full,
    mixed,
    lead,
    starts,
    gated,
    mix,
    state_scr,
    run_scr,
    message,
    received,
    mine_sem,
    full_sem,
    save_sem,
    pre_sem,
    mix_sem,
    state_send,
    state_recv,
    *sems,
):
    plane = Plane(mesh_axes)
    chips = plane.chips
    tokens, model_width = hidden_ref.shape
    block, width = query_hbm.shape
    lanes = width // head_count
    state_rows = head_count * lanes
    context, context_size = lax.axis_index("context"), lax.axis_size("context")

    mine_loads = [
        pltpu.make_async_copy(
            ref, mine.at[:, pl.ds(which * width, width)], mine_sem.at[which]
        )
        for which, ref in enumerate((query_hbm, forget_hbm, input_hbm, gate_hbm))
    ]
    for load in mine_loads:
        load.start()
    gather = Gather(plane, (mine,), (full,), sems[:5])
    out_gather = Gather(plane, (out_turned,), (out_full,), sems[5:])

    def later(shift):
        places = {axis: lax.axis_index(axis) for axis in mesh_axes}
        places["context"] = lax.rem(context + shift, context_size)
        return tuple(places[axis] for axis in mesh_axes)

    out_turned[...] = out_shard_ref[...].T
    barrier = pltpu.get_barrier_semaphore()
    expected = gather.greet(barrier)
    for shift in range(1, context_size):
        pl.semaphore_signal(barrier, inc=1, device_id=later(shift), device_id_type=MESH_ID)
    pl.semaphore_wait(barrier, expected + context_size - 1)
    for load in mine_loads:
        load.wait()
    gather.start()
    out_gather.start()
    down_turned[...] = down_shard_ref[...].T
    for head in range(head_count):
        open_ref[:, head * lanes : (head + 1) * lanes] = 1.0 - floor_ref[head : head + 1]

    segments = segments_ref[...]
    blocks = segments.shape[0]
    block_ids = lax.broadcasted_iota(jnp.int32, segments.shape, 0)
    slot_ids = lax.broadcasted_iota(jnp.int32, segments.shape, 1)
    before = pltpu.roll(segments, 1, 1)
    wrapped = pltpu.roll(before, 1, 0)
    before = jnp.where(slot_ids == 0, wrapped, before)
    first_slot = jnp.logical_and(slot_ids == 0, block_ids == 0)
    begins = jnp.where(jnp.logical_or(first_slot, segments == before), 0.0, 1.0)
    wide_rows = lax.broadcasted_iota(jnp.int32, (BLOCK, BLOCK), 0)
    wide_columns = lax.broadcasted_iota(jnp.int32, (BLOCK, BLOCK), 1)
    within = mm_nn(begins.astype(BF16), (wide_rows <= wide_columns).astype(BF16))
    count_rows = []
    running = jnp.zeros((1, 1), F32)
    flags_ref[...] = jnp.zeros_like(flags_ref)
    for index in range(blocks):
        row = within[index : index + 1] + running
        flags_ref[index, 0:1] = row
        flags_ref[index, 1:2] = jnp.broadcast_to(running, (1, BLOCK))
        running = row[:, BLOCK - 1 : BLOCK]
        flags_ref[index, 2:3] = jnp.broadcast_to(running, (1, BLOCK))
        count_rows.append(row)
    turned_counts = jnp.concatenate(count_rows, axis=0).T
    turned_keep = (segments > 0).astype(F32).T
    for index in range(blocks):
        rows = slice(index * BLOCK, (index + 1) * BLOCK)
        count_ref[rows] = turned_counts[:, index : index + 1]
        keep_ref[rows] = turned_keep[:, index : index + 1]
    first_id = jnp.broadcast_to(segments[0:1, 0:1], (1, lanes))
    last_id = jnp.broadcast_to(segments[blocks - 1 : blocks, BLOCK - 1 : BLOCK], (1, lanes))

    def norm(index, _):
        rows = pl.ds(pl.multiple_of(index * 128, 128), 128)
        values = hidden_ref[rows].astype(F32)
        normed[rows] = (values * inverse_rms(values) * gain_ref[...]).astype(BF16)
        return 0

    lax.fori_loop(0, tokens // 128, norm, 0)

    saves = [
        pltpu.make_async_copy(source, target, save_sem.at[which])
        for which, (source, target) in enumerate(
            (
                (normed, normed_hbm),
                (out_full, out_full_hbm),
                (mixed, mixed_hbm),
                (lead, lead_hbm),
                (starts, start_hbm),
                (gated, gated_hbm),
            )
        )
    ]
    saves[0].start()
    row_tile, column_tile = 256, 512

    def pre_save(index):
        rows = pl.ds(pl.multiple_of(index * row_tile, row_tile), row_tile)
        return pltpu.make_async_copy(pre.at[rows], pre_hbm.at[rows], pre_sem.at[index])

    def depth_of(distance):
        first = 2 * gather.partner(distance) * block
        return pl.ds(pl.multiple_of(first, 2 * block), 2 * block)

    def product(distance):
        depth = depth_of(distance)

        def row_body(index, _):
            rows = pl.ds(pl.multiple_of(index * row_tile, row_tile), row_tile)
            left = normed[rows, depth]

            def column_body(column, _):
                columns = pl.ds(pl.multiple_of(column * column_tile, column_tile), column_tile)
                value = mm_nn(left, full[depth, columns])
                if distance > 0:
                    value = value + pre[rows, columns]
                pre[rows, columns] = value
                return 0

            lax.fori_loop(0, full.shape[1] // column_tile, column_body, 0)
            if distance == chips - 1:
                pre_save(index).start()
            return 0

        lax.fori_loop(0, tokens // row_tile, row_body, 0)

    def full_save(distance):
        depth = depth_of(distance)
        return pltpu.make_async_copy(full.at[depth], full_hbm.at[depth], full_sem.at[distance])

    def use(distance):
        gather.arrive_from(distance)
        full_save(distance).start()
        product(distance)

    use(0)
    gather.stage(0)
    gather.stage(1)
    if gather.relayed:
        use(1)
        use(2)
    gather.stage(2)
    if gather.relayed:
        use(3)
    else:
        for distance in range(1, chips):
            use(distance)
    out_gather.stage(0)
    out_gather.stage(1)

    state_scr[...] = jnp.zeros_like(state_scr)
    run_scr[...] = jnp.zeros_like(run_scr)

    def recur(step, _):
        rows = pl.ds(pl.multiple_of(step * BLOCK, BLOCK), BLOCK)
        counts, keep = count_ref[rows], keep_ref[rows]
        row_ids, col_ids, linked, fresh, tail, closing = block_masks(counts, flags_ref[step])
        tri = (row_ids >= col_ids).astype(BF16)
        query_pre = pre[rows, :width]
        values = pre[rows, 2 * width : 3 * width].astype(BF16)
        keys = open_ref[...] * jax.nn.sigmoid(-pre[rows, width : 2 * width])
        cum = split_sum(tri, jnp.log1p(-keys))
        ending = cum[BLOCK - 1 : BLOCK, :]
        lifted = query_pre * jax.nn.sigmoid(query_pre) * jnp.exp(cum)
        lowered = (keys * jnp.exp(-cum) * keep).astype(BF16)
        moved = (keys * jnp.exp(ending - cum) * (keep * tail)).astype(BF16)
        run = run_scr[...]
        lead[rows] = (lifted * jnp.exp(run) * (counts == 0).astype(F32)).astype(BF16)
        run_ref[step] = run
        run_scr[...] = run + ending
        fresh_lifted = (lifted * fresh).astype(BF16)
        lifted = lifted.astype(BF16)
        end_decay = jnp.exp(ending) * closing
        for head in range(head_count):
            part = slice(head * lanes, (head + 1) * lanes)
            state = state_scr[head]
            starts[step, head] = state
            scores = jnp.where(linked, mm_nt(lifted[:, part], lowered[:, part]), 0.0)
            results = mm_nn(scores.astype(BF16), values[:, part])
            results = results + mm_nt(fresh_lifted[:, part], state.astype(BF16))
            mixed[rows, part] = results * (key_scale * keep)
            state_scr[head] = state * end_decay[:, part] + mm_tn(values[:, part], moved[:, part])
        return 0

    lax.fori_loop(0, tokens // BLOCK, recur, 0)
    saves[3].start()
    saves[4].start()

    last_count = flags_ref[tokens // BLOCK - 1][2:3, 0:1]
    for head in range(head_count):
        part = slice(head * lanes, (head + 1) * lanes)
        message[head * lanes : (head + 1) * lanes] = state_scr[head]
        decay = jnp.exp(run_scr[:, part]) * (last_count == 0).astype(F32)
        decay_ref[head] = decay
        message[state_rows + 8 + head : state_rows + 9 + head] = decay
    message[state_rows : state_rows + 1] = first_id
    message[state_rows + 1 : state_rows + 2] = last_id

    def state_copy(shift):
        return pltpu.make_async_remote_copy(
            message,
            received.at[shift - 1],
            state_send.at[shift - 1],
            state_recv.at[shift - 1],
            device_id=later(shift),
            device_id_type=MESH_ID,
        )

    for shift in range(1, context_size):

        @pl.when(context + shift < context_size)
        def _(shift=shift):
            state_copy(shift).start()

    out_gather.stage(2)
    carry_ref[...] = jnp.zeros_like(carry_ref)
    link_ref[...] = jnp.zeros_like(link_ref)
    for shift in range(1, context_size):

        @pl.when(context >= shift)
        def _(shift=shift):
            state_copy(shift).wait_recv()
            linked = jnp.ones((1, lanes), F32)
            follower = first_id
            factors = [jnp.ones((1, lanes), F32)] * head_count
            for near in range(shift):
                got = received.at[near]
                linked = (got[state_rows + 1 : state_rows + 2] == follower).astype(F32)
                follower = got[state_rows : state_rows + 1]
                factors = [factor * linked for factor in factors]
                if near < shift - 1:
                    factors = [
                        factor * got[state_rows + 8 + head : state_rows + 9 + head]
                        for head, factor in enumerate(factors)
                    ]
            if shift == 1:
                link_ref[0:1] = linked
            for head in range(head_count):
                rows = slice(head * lanes, (head + 1) * lanes)
                carry_ref[head] += factors[head] * received[shift - 1, rows]

    for shift in range(1, context_size):

        @pl.when(context + shift < context_size)
        def _(shift=shift):
            state_copy(shift).wait_send()

    for distance in range(chips):
        out_gather.arrive_from(distance)
    saves[1].start()

    def mix_save(index):
        rows = pl.ds(pl.multiple_of(index * row_tile, row_tile), row_tile)
        return pltpu.make_async_copy(mix.at[rows], mix_hbm.at[rows], mix_sem.at[index])

    def project(index, _):
        rows = pl.ds(pl.multiple_of(index * row_tile, row_tile), row_tile)
        for head in range(head_count):
            part = slice(head * lanes, (head + 1) * lanes)
            carried = mm_nt(lead[rows, part], carry_ref[head].astype(BF16))
            value = mixed[rows, part] + carried * (key_scale * keep_ref[rows])
            mixed[rows, part] = value
            gate = pre[rows, 3 * width + head * lanes : 3 * width + (head + 1) * lanes]
            unit = value * inverse_rms(value)
            gated[rows, part] = (
                unit * head_gain_ref[...] * (gate * jax.nn.sigmoid(gate))
            ).astype(BF16)
        left = gated[rows]

        def column_body(column, _):
            columns = pl.ds(pl.multiple_of(column * column_tile, column_tile), column_tile)
            mix[rows, columns] = mm_nt(left, out_full[columns, :]).astype(BF16)
            return 0

        lax.fori_loop(0, model_width // column_tile, column_body, 0)
        mix_save(index).start()
        return 0

    lax.fori_loop(0, tokens // row_tile, project, 0)
    saves[2].start()
    saves[5].start()
    gather.finish()
    out_gather.finish()
    for distance in range(chips):
        full_save(distance).wait()
    for save in saves:
        save.wait()
    for index in range(tokens // row_tile):
        pre_save(index).wait()
        mix_save(index).wait()


def forward(
    mesh_axes, collective, hidden, gain, shards, out_shard, down_shard, floor, segments, head_gain
):
    tokens, model_width = hidden.shape
    block, width = shards[0].shape
    lanes = head_gain.shape[1]
    head_count = width // lanes
    all_width = width * len(shards)
    blocks = tokens // BLOCK
    context_size = lax.axis_size("context")
    chips = lax.axis_size("shard") * context_size // 2
    messages = head_count * lanes + 8 + -(-head_count // 8) * 8
    whole = pl.BlockSpec(memory_space=pltpu.VMEM)
    remote = pl.BlockSpec(memory_space=pl.ANY)
    stored = [
        ((tokens, model_width), BF16),
        ((tokens, all_width), F32),
        ((model_width, all_width), BF16),
        ((model_width, width), BF16),
        ((tokens, width), F32),
        ((tokens, width), BF16),
        ((blocks, head_count, lanes, lanes), F32),
        ((tokens, width), BF16),
        ((tokens, model_width), BF16),
    ]
    kept = [
        (down_shard.shape[::-1], BF16),
        ((1, width), F32),
        ((tokens, 1), F32),
        ((tokens, 1), F32),
        ((blocks, 8, BLOCK), F32),
        ((blocks, 1, width), F32),
        ((head_count, lanes, lanes), F32),
        ((head_count, 1, lanes), F32),
        ((8, lanes), F32),
    ]
    return pl.pallas_call(
        partial(forward_kernel, mesh_axes, head_count, lanes ** (-0.5)),
        in_specs=[whole] * 2 + [remote] * 4 + [whole] * 5,
        out_specs=[remote] * len(stored) + [whole] * len(kept),
        out_shape=[jax.ShapeDtypeStruct(shape, kind) for shape, kind in stored + kept],
        scratch_shapes=[
            pltpu.VMEM((tokens, model_width), BF16),
            pltpu.VMEM((tokens, all_width), F32),
            pltpu.VMEM((block, all_width), BF16),
            pltpu.VMEM((block, width), BF16),
            pltpu.VMEM((model_width, all_width), BF16),
            pltpu.VMEM((model_width, width), BF16),
            pltpu.VMEM((tokens, width), F32),
            pltpu.VMEM((tokens, width), BF16),
            pltpu.VMEM((blocks, head_count, lanes, lanes), F32),
            pltpu.VMEM((tokens, width), BF16),
            pltpu.VMEM((tokens, model_width), BF16),
            pltpu.VMEM((head_count, lanes, lanes), F32),
            pltpu.VMEM((1, width), F32),
            pltpu.VMEM((messages, lanes), F32),
            pltpu.VMEM((context_size - 1, messages, lanes), F32),
            pltpu.SemaphoreType.DMA((4,)),
            pltpu.SemaphoreType.DMA((chips,)),
            pltpu.SemaphoreType.DMA((6,)),
            pltpu.SemaphoreType.DMA((tokens // 256,)),
            pltpu.SemaphoreType.DMA((tokens // 256,)),
            pltpu.SemaphoreType.DMA((context_size - 1,)),
            pltpu.SemaphoreType.DMA((context_size - 1,)),
        ]
        + gather_sems(1)
        + gather_sems(1),
        compiler_params=pltpu.CompilerParams(
            collective_id=collective, has_side_effects=True, vmem_limit_bytes=56 << 20
        ),
        cost_estimate=pl.CostEstimate(
            flops=2 * tokens * model_width * all_width,
            bytes_accessed=200_000_000,
            transcendentals=tokens * width * 9,
        ),
        name="forward",
    )(hidden, gain, *shards, out_shard, down_shard, floor, segments, head_gain)


def closing_kernel(
    count,
    ffn_ref,
    out_share_ref,
    *refs,
):
    moved_in, refs = refs[:count], refs[count:]
    gate_ref, up_ref, down_ref, out_ref = refs[:4]
    moved_out, sem = refs[4 : 4 + count], refs[4 + count]
    pieces = 4
    copies = []
    for which, (source, target) in enumerate(zip(moved_in, moved_out)):
        length = source.shape[0] // pieces
        for index in range(pieces):
            rows = pl.ds(index * length, length)
            copies.append(
                pltpu.make_async_copy(source.at[rows], target.at[rows], sem.at[which, index])
            )
    for copy in copies:
        copy.start()
    hidden_width = gate_ref.shape[1]
    gate_ref[...] = ffn_ref[:, :hidden_width].astype(F32)
    up_ref[...] = ffn_ref[:, hidden_width : 2 * hidden_width].astype(F32)
    for first in range(0, hidden_width, 128):
        columns = slice(2 * hidden_width + first, 2 * hidden_width + first + 128)
        down_ref[first : first + 128] = ffn_ref[:, columns].astype(F32).T
    for first in range(0, out_share_ref.shape[1], 128):
        out_ref[first : first + 128] = out_share_ref[:, first : first + 128].T
    for copy in copies:
        copy.wait()


def closing(share_ffn, share_out, moved):
    block, all_width = share_ffn.shape
    hidden_width = all_width // 3
    whole = pl.BlockSpec(memory_space=pltpu.VMEM)
    remote = pl.BlockSpec(memory_space=pl.ANY)
    return pl.pallas_call(
        partial(closing_kernel, len(moved)),
        in_specs=[whole] * 2 + [remote] * len(moved),
        out_specs=[whole] * 4 + [remote] * len(moved),
        out_shape=[
            jax.ShapeDtypeStruct((block, hidden_width), F32),
            jax.ShapeDtypeStruct((block, hidden_width), F32),
            jax.ShapeDtypeStruct((hidden_width, block), F32),
            jax.ShapeDtypeStruct(share_out.shape[::-1], F32),
        ]
        + [jax.ShapeDtypeStruct(value.shape, value.dtype) for value in moved],
        scratch_shapes=[pltpu.SemaphoreType.DMA((len(moved), 4))],
        compiler_params=pltpu.CompilerParams(vmem_limit_bytes=40 << 20),
        cost_estimate=pl.CostEstimate(flops=0, bytes_accessed=30_000_000, transcendentals=0),
        name="closing",
    )(share_ffn, share_out, *moved)


def local(
    mesh_axes,
    hidden,
    segment_ids,
    norm1_gain,
    w_query,
    w_forget,
    w_input,
    w_gate_out,
    forget_floor,
    head_gain,
    w_out,
    norm2_gain,
    w_ffn_gate,
    w_ffn_up,
    w_ffn_down,
    out_grad,
):
    sequences, span_len, model_width = hidden.shape
    tokens = sequences * span_len
    head_count, key_dim = forget_floor.shape
    width = head_count * key_dim
    key_scale = key_dim ** (-0.5)
    both = ("shard", "context")
    gain_one, gain_two = norm1_gain.reshape(1, -1), norm2_gain.reshape(1, -1)
    hidden_rows = hidden.reshape(tokens, model_width)
    gain_row = head_gain.reshape(1, -1)
    segments = segment_ids.reshape(tokens // BLOCK, BLOCK).astype(F32)
    (
        normed_one,
        pre,
        mixer_full,
        out_full,
        mixed,
        lead,
        starts,
        gated_low,
        mix_part,
        down_turned,
        open_part,
        counts,
        keep,
        flags,
        runs,
        carry,
        decay,
        link,
    ) = forward(
        mesh_axes,
        4,
        hidden_rows,
        gain_one,
        (w_query, w_forget, w_input, w_gate_out),
        w_out,
        w_ffn_down,
        forget_floor,
        segments,
        gain_row,
    )
    grad_rows = out_grad.reshape(tokens, model_width)
    (
        grad_mix_low,
        grad_norm_two,
        residual,
        _,
        _,
        _,
        feed_part,
        grad_residual,
        grads_ffn,
    ) = middle(
        mesh_axes,
        2,
        mix_part,
        grad_rows,
        hidden_rows,
        gain_two,
        w_ffn_gate,
        w_ffn_up,
        down_turned,
    )
    (
        output_rows,
        grad_head_part,
        grad_floor_part,
        back_one,
        grads_mixer,
    ) = output_line(
        mesh_axes,
        1,
        (
            runs,
            carry,
            decay,
            link,
            open_part,
            counts,
            keep,
            flags,
            gain_row,
        ),
        (
            feed_part,
            residual,
            gated_low,
            grad_mix_low,
            out_full,
            lead,
            starts,
            normed_one,
            pre,
            mixer_full,
            mixed,
        ),
        head_count,
    )
    share_ffn = lax.psum_scatter(grads_ffn, both, scatter_dimension=0, tiled=True)
    input_rows, near, total, *mixer_shares, share_out = input_line(
        mesh_axes,
        3,
        back_one,
        hidden_rows,
        grad_residual,
        gain_one,
        grads_mixer,
        (grad_norm_two, grad_head_part, grad_floor_part),
    )
    near, total = near.reshape(-1), total.reshape(-1)
    shares = lax.axis_size("shard") * lax.axis_size("context")
    position = lax.axis_index("shard") * lax.axis_size("context") + lax.axis_index("context")

    def own_slice(first, length):
        length = length // shares
        return lax.dynamic_slice_in_dim(total, first + position * length, length, 0)

    first = 2 * model_width + key_dim
    floor_total = near[first : first + width].reshape(head_count, key_dim)
    floor_part = key_dim // shares

    share_gate, share_up, share_down, share_out, output_rows, input_rows, *mixer_shares = closing(
        share_ffn, share_out, (output_rows, input_rows, *mixer_shares)
    )
    return (
        output_rows.reshape(hidden.shape),
        input_rows.reshape(hidden.shape),
        own_slice(0, model_width),
        *mixer_shares,
        lax.dynamic_slice_in_dim(floor_total, position * floor_part, floor_part, 1),
        own_slice(2 * model_width, key_dim),
        share_out,
        own_slice(model_width, model_width),
        share_gate,
        share_up,
        share_down,
    )


def solution(mesh):
    in_specs = (
        P("shard", "context", None),
        P("shard", "context"),
        P(),
        P(("shard", "context"), "tensor"),
        P(("shard", "context"), "tensor"),
        P(("shard", "context"), "tensor"),
        P(("shard", "context"), "tensor"),
        P("tensor", None),
        P(),
        P("tensor", ("shard", "context")),
        P(),
        P(("shard", "context"), "tensor"),
        P(("shard", "context"), "tensor"),
        P("tensor", ("shard", "context")),
        P("shard", "context", None),
    )
    out_specs = (
        P("shard", "context", None),
        P("shard", "context", None),
        P(("shard", "context")),
        P(("shard", "context"), "tensor"),
        P(("shard", "context"), "tensor"),
        P(("shard", "context"), "tensor"),
        P(("shard", "context"), "tensor"),
        P("tensor", ("shard", "context")),
        P(("shard", "context")),
        P("tensor", ("shard", "context")),
        P(("shard", "context")),
        P(("shard", "context"), "tensor"),
        P(("shard", "context"), "tensor"),
        P("tensor", ("shard", "context")),
    )
    return jax.shard_map(
        partial(local, mesh.axis_names), mesh=mesh, in_specs=in_specs, out_specs=out_specs, check_vma=False)
```

```python
from functools import partial

import jax
import jax.numpy as jnp
from jax import lax
from jax.experimental import pallas as pl
from jax.experimental.pallas import tpu as pltpu
from jax.sharding import PartitionSpec as P

EPSILON = 1e-05


BLOCK = 128
F32 = jnp.float32
BF16 = jnp.bfloat16


def mm(a, b, dims):
    return lax.dot_general(a, b, (dims, ((), ())), preferred_element_type=F32)


def mm_nn(a, b):
    return mm(a, b, ((1,), (0,)))


def mm_nt(a, b):
    return mm(a, b, ((1,), (1,)))


def mm_tn(a, b):
    return mm(a, b, ((0,), (0,)))


def split_sum(tri, values):
    high = values.astype(BF16)
    low = (values - high.astype(F32)).astype(BF16)
    return mm_nn(tri, high) + mm_nn(tri, low)


def block_masks(counts, flags_row):
    rows = counts.shape[0]
    row_ids = lax.broadcasted_iota(jnp.int32, (rows, rows), 0)
    col_ids = lax.broadcasted_iota(jnp.int32, (rows, rows), 1)
    linked = jnp.logical_and(counts == flags_row[0:1], row_ids >= col_ids)
    fresh = (counts == flags_row[1:2, 0:1]).astype(F32)
    tail = (counts == flags_row[2:3, 0:1]).astype(F32)
    closing = (flags_row[1:2, 0:1] == flags_row[2:3, 0:1]).astype(F32)
    return row_ids, col_ids, linked, fresh, tail, closing


CHUNK = 32
QUIET, MANY = 6, 2
LAG = 2
MESH_ID = pl.DeviceIdType.MESH


class Line:
    def __init__(self, mesh_axes, part, arrived, out, sems, transform, sums=True, backs=True):
        self.mesh_axes = mesh_axes
        self.sums, self.backs = sums, backs
        self.part, self.arrived, self.out = part, arrived, out
        if sums:
            self.sum_send, self.sum_recv = sems[:2]
        if backs:
            self.back_send, self.back_recv = sems[-2:]
        self.transform = transform
        self.half = (part if sums else out).shape[0] // 2
        self.chunks = self.half // CHUNK
        self.size = lax.axis_size("tensor")
        self.place = lax.axis_index("tensor")
        self.lines = ((self.size - 1 - self.place, -1), (self.place, 1))
        self.offset = LAG * (self.size - 1) if sums else 0
        self.steps = self.chunks + self.offset + (LAG * (self.size - 1) if backs else 0)

    def device(self, position):
        return tuple(
            jnp.clip(position, 0, self.size - 1) if axis == "tensor" else lax.axis_index(axis)
            for axis in self.mesh_axes
        )

    def greet(self, barrier):
        for step in (-1, 1):
            inside = jnp.logical_and(self.place + step >= 0, self.place + step < self.size)

            @pl.when(inside)
            def _(step=step):
                pl.semaphore_signal(
                    barrier, inc=1, device_id=self.device(self.place + step), device_id_type=MESH_ID
                )

        at_end = jnp.logical_or(self.place == 0, self.place == self.size - 1)
        return jnp.where(at_end, 1, 2)

    def rows_of(self, side, index):
        return pl.ds(pl.multiple_of(side * self.half + index * CHUNK, CHUNK), CHUNK)

    def sum_copy(self, side, index, source):
        rows = self.rows_of(side, index)
        return pltpu.make_async_remote_copy(
            source.at[rows],
            self.arrived.at[rows],
            self.sum_send.at[side, index],
            self.sum_recv.at[side, index],
            device_id=self.device(self.place + self.lines[side][1]),
            device_id_type=MESH_ID,
        )

    def back_copy(self, side, index):
        rows = self.rows_of(side, index)
        return pltpu.make_async_remote_copy(
            self.out.at[rows],
            self.out.at[rows],
            self.back_send.at[side, index],
            self.back_recv.at[side, index],
            device_id=self.device(self.place - self.lines[side][1]),
            device_id_type=MESH_ID,
        )

    def step(self, time):
        for side in (0, 1):
            hops = self.lines[side][0]
            at_source, at_owner = hops == 0, hops == self.size - 1
            if self.sums:
                self.sum_step(time, side, hops, at_source, at_owner)
            if self.backs:
                self.back_step(time, side, hops, at_owner)

    def sum_step(self, time, side, hops, at_source, at_owner):
        index = time - LAG * hops
        valid = jnp.logical_and(index >= 0, index < self.chunks)
        index = jnp.clip(index, 0, self.chunks - 1)
        rows = self.rows_of(side, index)

        @pl.when(jnp.logical_and(valid, at_source))
        def _():
            self.sum_copy(side, index, self.part).start()

        @pl.when(jnp.logical_and(valid, jnp.logical_not(at_source)))
        def _():
            self.sum_copy(side, index, self.arrived).wait_recv()

        between = jnp.logical_and(jnp.logical_not(at_source), jnp.logical_not(at_owner))

        @pl.when(jnp.logical_and(valid, between))
        def _():
            total = self.part[rows].astype(F32) + self.arrived[rows].astype(F32)
            self.arrived[rows] = total.astype(BF16)
            self.sum_copy(side, index, self.arrived).start()

        @pl.when(jnp.logical_and(valid, at_owner))
        def _():
            total = self.part[rows].astype(F32) + self.arrived[rows].astype(F32)
            self.turn(total, side, index)

    def turn(self, total, side, index):
        own = pl.ds(pl.multiple_of(index * CHUNK, CHUNK), CHUNK)
        self.transform(total, self.rows_of(side, index), own)
        if self.backs:
            self.back_copy(side, index).start()

    def back_step(self, time, side, hops, at_owner):
        if not self.sums:

            @pl.when(jnp.logical_and(at_owner, time < self.chunks))
            def _():
                self.turn(None, side, jnp.clip(time, 0, self.chunks - 1))

        away = self.size - 1 - hops
        index = time - self.offset - LAG * away
        valid = jnp.logical_and(jnp.logical_and(index >= 0, index < self.chunks), away > 0)
        index = jnp.clip(index, 0, self.chunks - 1)

        @pl.when(valid)
        def _():
            self.back_copy(side, index).wait_recv()

        @pl.when(jnp.logical_and(valid, away < self.size - 1))
        def _():
            self.back_copy(side, index).start()

    def run(self, first, last, beside=None):
        def body(time, _):
            self.step(time)
            if beside is not None:
                beside(time)
            return 0

        lax.fori_loop(first, last, body, 0)

    def source_sent(self, first, last):
        def body(index, _):
            for side in (0, 1):

                @pl.when(self.lines[side][0] == 0)
                def _(side=side):
                    self.sum_copy(side, index, self.part).wait_send()

            return 0

        lax.fori_loop(first, last, body, 0)

    def finish(self, source_waits=True):
        def body(index, _):
            for side in (0, 1):
                hops = self.lines[side][0]
                passed = hops < self.size - 1
                if not source_waits:
                    passed = jnp.logical_and(passed, hops > 0)

                if self.sums:

                    @pl.when(passed)
                    def _(side=side):
                        self.sum_copy(side, index, self.arrived).wait_send()

                if self.backs:

                    @pl.when(hops > 0)
                    def _(side=side):
                        self.back_copy(side, index).wait_send()

            return 0

        lax.fori_loop(0, self.chunks, body, 0)


def line_sems(tokens, count=4):
    return [pltpu.SemaphoreType.DMA((2, tokens // 2 // CHUNK))] * count


def inverse_rms(values):
    return lax.rsqrt(jnp.mean(values * values, axis=-1, keepdims=True) + EPSILON)


class Plane:
    def __init__(self, mesh_axes):
        self.mesh_axes = mesh_axes
        self.context = lax.axis_size("context")
        self.per_row = self.context // 2
        self.chips = lax.axis_size("shard") * self.per_row
        context_place = lax.axis_index("context")
        self.core = lax.rem(context_place, 2)
        self.chip = lax.axis_index("shard") * self.per_row + context_place // 2

    def device(self, chip, core):
        places = {
            "shard": chip // self.per_row,
            "context": 2 * lax.rem(chip, self.per_row) + core,
            "tensor": lax.axis_index("tensor"),
        }
        return tuple(places[axis] for axis in self.mesh_axes)

    def ahead(self, distance):
        return lax.rem(self.chip + distance, self.chips)

    def greet(self, barrier):
        targets = [self.device(self.chip, 1 - self.core)]
        targets += [self.device(self.ahead(step), self.core) for step in range(1, self.chips)]
        for target in targets:
            pl.semaphore_signal(barrier, inc=1, device_id=target, device_id_type=MESH_ID)
        return len(targets)


class Gather:
    def __init__(self, plane, sources, targets, sems):
        self.plane, self.sources, self.targets = plane, sources, targets
        self.load_sem, self.send_sem, self.recv_sem, self.pair_send, self.pair_recv = sems
        self.block = sources[0].shape[0]
        self.part = self.block // 2
        self.relayed = plane.chips == 4
        self.arrays = range(len(sources))

    def partner(self, distance):
        return jnp.bitwise_xor(self.plane.chip, distance)

    def greet(self, barrier):
        plane = self.plane
        targets = [plane.device(plane.chip, 1 - plane.core)]
        targets += [
            plane.device(self.partner(step), plane.core)
            for step in range(1, 3 if self.relayed else plane.chips)
        ]
        for target in targets:
            pl.semaphore_signal(barrier, inc=1, device_id=target, device_id_type=MESH_ID)
        return len(targets)

    def place(self, array, chip, core, half):
        first = (2 * chip + core) * self.block + half * self.part
        rows = pl.ds(pl.multiple_of(first, self.part), self.part)
        return self.targets[array].at[rows, pl.ds(0, self.sources[array].shape[1])]

    def mine(self, array, half):
        return self.sources[array].at[pl.ds(half * self.part, self.part)]

    def loads(self):
        plane = self.plane
        return [
            pltpu.make_async_copy(
                self.mine(array, half),
                self.place(array, plane.chip, plane.core, half),
                self.load_sem.at[array, half],
            )
            for array in self.arrays
            for half in range(2)
        ]

    def send(self, distance, half):
        plane = self.plane
        copies = []
        for array in self.arrays:
            chip, target = plane.chip, self.partner(distance)
            source = self.mine(array, half)
            if self.relayed and distance == 3:
                chip = self.partner(2 if half == 0 else 1)
                target = self.partner(1 if half == 0 else 2)
                source = self.place(array, chip, plane.core, half)
            copies.append(
                pltpu.make_async_remote_copy(
                    source,
                    self.place(array, chip, plane.core, half),
                    self.send_sem.at[array, distance - 1, half],
                    self.recv_sem.at[array, distance - 1, half],
                    device_id=plane.device(target, plane.core),
                    device_id_type=MESH_ID,
                )
            )
        return copies

    def forward(self, distance, half):
        plane = self.plane
        copies = []
        for array in self.arrays:
            place = self.place(array, self.partner(distance), plane.core, half)
            copies.append(
                pltpu.make_async_remote_copy(
                    self.mine(array, half) if distance == 0 else place,
                    place,
                    self.pair_send.at[array, distance, half],
                    self.pair_recv.at[array, distance, half],
                    device_id=plane.device(plane.chip, 1 - plane.core),
                    device_id_type=MESH_ID,
                )
            )
        return copies

    def start(self):
        if self.relayed:
            order = ((1, 1), (2, 0), (1, 0), (2, 1))
        else:
            order = [(step, half) for step in range(1, self.plane.chips) for half in range(2)]
        for distance, half in order:
            for copy in self.send(distance, half):
                copy.start()
        for copy in self.loads():
            copy.start()
        for half in range(2):
            for copy in self.forward(0, half):
                copy.start()

    def take(self, distance, half, relay):
        for copy in self.send(distance, half):
            copy.wait_recv()
        if relay:
            for copy in self.send(3, half):
                copy.start()
        for copy in self.forward(distance, half):
            copy.start()

    def stage(self, number):
        if self.relayed:
            if number == 0:
                self.take(1, 1, True)
                self.take(2, 0, True)
            elif number == 1:
                self.take(1, 0, False)
                self.take(2, 1, False)
            else:
                self.take(3, 0, False)
                self.take(3, 1, False)
        elif number == 2:
            for distance in range(1, self.plane.chips):
                for half in range(2):
                    self.take(distance, half, False)

    def arrive_from(self, distance):
        if distance == 0:
            for copy in self.loads():
                copy.wait()
        for half in range(2):
            for copy in self.forward(distance, half):
                copy.wait_recv()

    def arrive(self):
        for distance in range(self.plane.chips):
            self.arrive_from(distance)

    def finish(self):
        for distance in range(self.plane.chips):
            for half in range(2):
                for copy in self.forward(distance, half):
                    copy.wait_send()
                if distance > 0:
                    for copy in self.send(distance, half):
                        copy.wait_send()


def gather_sems(arrays):
    chips = lax.axis_size("shard") * lax.axis_size("context") // 2
    return [
        pltpu.SemaphoreType.DMA((arrays, 2)),
        pltpu.SemaphoreType.DMA((arrays, chips - 1, 2)),
        pltpu.SemaphoreType.DMA((arrays, chips - 1, 2)),
        pltpu.SemaphoreType.DMA((arrays, chips, 2)),
        pltpu.SemaphoreType.DMA((arrays, chips, 2)),
    ]


GROUP = 128
TILE = 256
WIDE = 512


def middle_kernel(
    mesh_axes,
    mix_hbm,
    cotangent_hbm,
    input_hbm,
    gain_ref,
    gate_hbm,
    up_hbm,
    down_hbm,
    out_ref,
    gain_grad,
    residual_hbm,
    hidden_hbm,
    grad_gate_hbm,
    grad_up_hbm,
    feed_hbm,
    grad_hbm,
    grads_hbm,
    normed_ref,
    cotangent_ref,
    gate_w,
    up_w,
    down_w,
    part,
    mix_arrived,
    arrived,
    inputs,
    residual,
    stage_hidden,
    stage_gate,
    stage_up,
    stage_feed,
    part_sem,
    input_sem,
    save_sem,
    stage_sem,
    grad_sem,
    back_sem,
    tile_sem,
    *sems,
):
    tokens, model_width = normed_ref.shape
    half = tokens // 2
    hidden_width = gate_hbm.shape[1]
    padded = gate_w.shape[1]
    groups = half // GROUP
    place, line_size = lax.axis_index("tensor"), lax.axis_size("tensor")
    own_half = pl.ds(pl.multiple_of(jnp.where(place == 0, 0, half), half), half)
    part_load = pltpu.make_async_copy(mix_hbm, part, part_sem.at[0])
    part_load.start()
    input_load = pltpu.make_async_copy(input_hbm.at[own_half], inputs, input_sem.at[0])
    input_load.start()
    cotangent_load = pltpu.make_async_copy(cotangent_hbm, cotangent_ref, input_sem.at[1])
    cotangent_load.start()
    if padded > hidden_width:
        spare = slice(hidden_width, padded)
        gate_w[:, spare] = jnp.zeros((model_width, padded - hidden_width), BF16)
        up_w[:, spare] = jnp.zeros((model_width, padded - hidden_width), BF16)
        down_w[:, spare] = jnp.zeros((model_width, padded - hidden_width), BF16)
    gain_grad[...] = jnp.zeros_like(gain_grad)

    def mix_turn(total, rows, own):
        values = inputs[own].astype(F32) + total
        residual[own] = values
        normed_ref[rows] = (values * inverse_rms(values) * gain_ref[...]).astype(BF16)

    def turn(total, rows, own):
        values = residual[own]
        inverse = inverse_rms(values)
        unit = values * inverse
        gain_grad[...] += jnp.sum(total * unit, axis=0, keepdims=True)
        lifted = total * gain_ref[...]
        mean = jnp.mean(lifted * unit, axis=-1, keepdims=True)
        grad = cotangent_ref[rows].astype(F32) + inverse * (lifted - unit * mean)
        residual[own] = grad
        out_ref[rows] = grad.astype(BF16)

    mix_line = Line(mesh_axes, part, mix_arrived, normed_ref, sems[:4], mix_turn)
    line = Line(mesh_axes, part, arrived, out_ref, sems[4:8], turn)
    gather = Gather(
        Plane(mesh_axes), (gate_hbm, up_hbm, down_hbm), (gate_w, up_w, down_w), sems[8:]
    )
    barrier = pltpu.get_barrier_semaphore()
    expected = mix_line.greet(barrier) + gather.greet(barrier)
    pl.semaphore_wait(barrier, expected)
    gather.start()
    part_load.wait()
    input_load.wait()
    pace = GROUP // CHUNK
    begin = pace + 2 * LAG * (line_size - 1) + 2
    mix_line.run(0, begin - 10)
    gather.stage(0)
    mix_line.run(begin - 10, begin - 4)
    gather.stage(1)
    mix_line.run(begin - 4, begin)
    gather.stage(2)
    gather.arrive()
    cotangent_load.wait()

    def both(ref, group):
        first = pl.ds(pl.multiple_of(group * GROUP, GROUP), GROUP)
        second = pl.ds(pl.multiple_of(half + group * GROUP, GROUP), GROUP)
        return first, second

    def stage_copies(group):
        slot = lax.rem(group, 2)
        copies = []
        for side, rows in enumerate(both(None, group)):
            from_rows = pl.ds(side * GROUP, GROUP)
            columns = pl.ds(0, hidden_width)
            for which, (stage, target) in enumerate(
                (
                    (stage_hidden, hidden_hbm),
                    (stage_gate, grad_gate_hbm),
                    (stage_up, grad_up_hbm),
                )
            ):
                copies.append(
                    pltpu.make_async_copy(
                        stage.at[slot, from_rows, columns],
                        target.at[rows],
                        stage_sem.at[slot, which, side],
                    )
                )
            copies.append(
                pltpu.make_async_copy(
                    stage_feed.at[slot, from_rows], feed_hbm.at[rows], stage_sem.at[slot, 3, side]
                )
            )
        return copies

    def hidden_tile(group, tile):
        first, second = both(normed_ref, group)
        slot = lax.rem(group, 2)
        columns = pl.ds(pl.multiple_of(tile * WIDE, WIDE), WIDE)
        rows = jnp.concatenate([normed_ref[first], normed_ref[second]], axis=0)
        gate = mm_nn(rows, gate_w[:, columns])
        up = mm_nn(rows, up_w[:, columns])
        grads = jnp.concatenate([cotangent_ref[first], cotangent_ref[second]], axis=0)
        grad = mm_nn(grads, down_w[:, columns])
        sigma = jax.nn.sigmoid(gate)
        active = gate * sigma
        stage_hidden[slot, :, columns] = (active * up).astype(BF16)
        stage_gate[slot, :, columns] = (grad * up * sigma * (1.0 + gate * (1.0 - sigma))).astype(
            BF16
        )
        stage_up[slot, :, columns] = (grad * active).astype(BF16)

    def model_tile(group, tile):
        first, second = both(part, group)
        slot = lax.rem(group, 2)
        columns = pl.ds(pl.multiple_of(tile * WIDE, WIDE), WIDE)
        back = mm_nt(stage_gate[slot], gate_w[columns, :])
        back = (back + mm_nt(stage_up[slot], up_w[columns, :])).astype(BF16)
        part[first, columns] = back[:GROUP]
        part[second, columns] = back[GROUP:]
        stage_feed[slot, :, columns] = mm_nt(stage_hidden[slot], down_w[columns, :]).astype(BF16)

    hidden_tiles, model_tiles = padded // WIDE, model_width // WIDE
    ticks = hidden_tiles + model_tiles
    piece = -(-ticks // pace)
    save = pltpu.make_async_copy(residual, residual_hbm, save_sem.at[0])

    def group_body(group, _):
        mix_line.source_sent(group * pace, (group + 1) * pace)

        @pl.when(group == 1)
        def _():
            save.start()

        @pl.when(group == 2)
        def _():
            save.wait()

        @pl.when(group >= 2)
        def _():
            for copy in stage_copies(group - 2):
                copy.wait()

        def piece_body(index, _):
            def tick_body(offset, _):
                tick = index * piece + offset

                @pl.when(tick < hidden_tiles)
                def _():
                    hidden_tile(group, tick)

                @pl.when(jnp.logical_and(tick >= hidden_tiles, tick < ticks))
                def _():
                    model_tile(group, tick - hidden_tiles)

                return 0

            lax.fori_loop(0, piece, tick_body, 0)

            mix_time = begin + group * pace + index

            @pl.when(mix_time < mix_line.steps)
            def _():
                mix_line.step(mix_time)

            @pl.when(group >= 1)
            def _():
                line.step((group - 1) * pace + index)

            return 0

        lax.fori_loop(0, pace, piece_body, 0)
        for copy in stage_copies(group):
            copy.start()
        return 0

    lax.fori_loop(0, groups, group_body, 0)
    for group in range(max(groups - 2, 0), groups):
        for copy in stage_copies(group):
            copy.wait()
    gather.finish()

    token_rows, hidden_columns = pl.ds(0, tokens), pl.ds(0, hidden_width)
    returned = [
        pltpu.make_async_copy(
            source, target.at[token_rows, hidden_columns], back_sem.at[which]
        )
        for which, (source, target) in enumerate(
            ((grad_gate_hbm, gate_w), (grad_up_hbm, up_w), (hidden_hbm, down_w))
        )
    ]
    for copy in returned:
        copy.start()
    tiles = model_width // TILE
    first_time = (groups - 1) * pace + 1
    stages = (stage_gate, stage_up, stage_hidden)

    def tile_copies(tile):
        rows = pl.ds(pl.multiple_of(tile * TILE, TILE), TILE)
        slot = lax.rem(tile, 2)
        return [
            pltpu.make_async_copy(
                stage.at[slot, pl.ds(0, TILE), hidden_columns],
                grads_hbm.at[rows, pl.ds(which * hidden_width, hidden_width)],
                tile_sem.at[slot, which],
            )
            for which, stage in enumerate(stages)
        ]

    def weight_tile(time):
        tile = time - first_time

        @pl.when(tile == 0)
        def _():
            for copy in returned:
                copy.wait()

        @pl.when(jnp.logical_and(tile >= 2, tile < tiles))
        def _():
            for copy in tile_copies(tile - 2):
                copy.wait()

        @pl.when(jnp.logical_and(tile >= 0, tile < tiles))
        def _():
            slot = lax.rem(tile, 2)
            columns = pl.ds(pl.multiple_of(tile * TILE, TILE), TILE)
            rows = normed_ref[:, columns]
            for source, right, stage in (
                (rows, gate_w, stage_gate),
                (rows, up_w, stage_up),
                (cotangent_ref[:, columns], down_w, stage_hidden),
            ):
                product = mm_tn(source, right[:tokens, :hidden_width])
                stage[slot, :TILE, :hidden_width] = product.astype(BF16)
            for copy in tile_copies(tile):
                copy.start()

    line.run((groups - 1) * pace, line.steps, weight_tile)
    grad_save = pltpu.make_async_copy(residual, grad_hbm, grad_sem.at[0])
    grad_save.start()
    for tile in range(max(tiles - 2, 0), tiles):
        for copy in tile_copies(tile):
            copy.wait()
    mix_line.finish(source_waits=False)
    line.finish()
    grad_save.wait()


def middle(mesh_axes, collective, mix, cotangent, inputs, gain, gate_w, up_w, down_w):
    tokens, model_width = mix.shape
    hidden_width = gate_w.shape[1]
    padded = -(-hidden_width // WIDE) * WIDE
    whole = pl.BlockSpec(memory_space=pltpu.VMEM)
    remote = pl.BlockSpec(memory_space=pl.ANY)
    group_rows = 2 * GROUP
    return pl.pallas_call(
        partial(middle_kernel, mesh_axes),
        in_specs=[remote, remote, remote, whole, remote, remote, remote],
        out_specs=[whole, whole] + [remote] * 7,
        out_shape=[
            jax.ShapeDtypeStruct((tokens, model_width), BF16),
            jax.ShapeDtypeStruct((1, model_width), F32),
            jax.ShapeDtypeStruct((tokens // 2, model_width), F32),
            jax.ShapeDtypeStruct((tokens, hidden_width), BF16),
            jax.ShapeDtypeStruct((tokens, hidden_width), BF16),
            jax.ShapeDtypeStruct((tokens, hidden_width), BF16),
            jax.ShapeDtypeStruct((tokens, model_width), BF16),
            jax.ShapeDtypeStruct((tokens // 2, model_width), F32),
            jax.ShapeDtypeStruct((model_width, 3 * hidden_width), BF16),
        ],
        scratch_shapes=[
            pltpu.VMEM((tokens, model_width), BF16),
            pltpu.VMEM((tokens, model_width), BF16),
            pltpu.VMEM((model_width, padded), BF16),
            pltpu.VMEM((model_width, padded), BF16),
            pltpu.VMEM((model_width, padded), BF16),
            pltpu.VMEM((tokens, model_width), BF16),
            pltpu.VMEM((tokens, model_width), BF16),
            pltpu.VMEM((tokens, model_width), BF16),
            pltpu.VMEM((tokens // 2, model_width), BF16),
            pltpu.VMEM((tokens // 2, model_width), F32),
            pltpu.VMEM((2, group_rows, padded), BF16),
            pltpu.VMEM((2, group_rows, padded), BF16),
            pltpu.VMEM((2, group_rows, padded), BF16),
            pltpu.VMEM((2, group_rows, model_width), BF16),
            pltpu.SemaphoreType.DMA((1,)),
            pltpu.SemaphoreType.DMA((2,)),
            pltpu.SemaphoreType.DMA((1,)),
            pltpu.SemaphoreType.DMA((2, 4, 2)),
            pltpu.SemaphoreType.DMA((1,)),
            pltpu.SemaphoreType.DMA((3,)),
            pltpu.SemaphoreType.DMA((2, 3)),
        ]
        + line_sems(tokens)
        + line_sems(tokens)
        + gather_sems(3),
        compiler_params=pltpu.CompilerParams(
            collective_id=collective, has_side_effects=True, vmem_limit_bytes=61 << 20
        ),
        cost_estimate=pl.CostEstimate(
            flops=tokens * model_width * hidden_width * 12,
            bytes_accessed=360_000_000,
            transcendentals=tokens * hidden_width,
        ),
        name="middle",
    )(mix, cotangent, inputs, gain, gate_w, up_w, down_w)


def output_kernel(
    mesh_axes,
    head_count,
    key_scale,
    run_ref,
    carry_ref,
    decay_ref,
    link_ref,
    open_ref,
    count_ref,
    keep_ref,
    flags_ref,
    gain_ref,
    part_hbm,
    residual_hbm,
    gated_hbm,
    mix_grad_hbm,
    out_full_hbm,
    lead_hbm,
    starts_hbm,
    normed_hbm,
    pre_hbm,
    full_hbm,
    mixed_hbm,
    out_ref,
    gain_grad,
    floor_grad,
    total_ref,
    mixer_grads_hbm,
    part,
    residual,
    gated_ref,
    mix_grad_ref,
    out_full,
    lead_ref,
    starts_ref,
    arrived,
    back,
    back_arrived,
    left,
    right,
    full,
    mixer_stage,
    piece_rows_scr,
    pre,
    grad_mixed,
    back_scr,
    message,
    received,
    grad_scr,
    lifted_scr,
    lowered_scr,
    moved_scr,
    value_scr,
    load_sem,
    piece_sem,
    full_sem,
    pre_sem,
    stage_sem,
    grad_send,
    grad_recv,
    *sems,
):
    tokens, model_width = left.shape
    width = gated_hbm.shape[1]
    lanes = width // head_count
    state_rows = head_count * lanes
    tiles, blocks = model_width // TILE, tokens // BLOCK
    piece_rows = 2 * BLOCK
    context, context_size = lax.axis_index("context"), lax.axis_size("context")

    loads = [
        pltpu.make_async_copy(source, target, load_sem.at[which])
        for which, (source, target) in enumerate(
            (
                (part_hbm, part),
                (out_full_hbm, out_full),
                (mix_grad_hbm, mix_grad_ref),
                (lead_hbm, lead_ref),
                (residual_hbm, residual),
                (starts_hbm, starts_ref),
                (gated_hbm, gated_ref),
                (normed_hbm, left),
            )
        )
    ]
    part_load, *gate_loads = loads[:5]
    starts_load, *tile_loads = loads[5:]
    for load in loads:
        load.start()

    def piece_loads(index):
        rows = pl.ds(pl.multiple_of(index * piece_rows, piece_rows), piece_rows)
        slot = lax.rem(index, 2)
        return (
            pltpu.make_async_copy(
                pre_hbm.at[rows, pl.ds(3 * width, width)],
                piece_rows_scr.at[slot, 0],
                piece_sem.at[slot, 0],
            ),
            pltpu.make_async_copy(
                mixed_hbm.at[rows], piece_rows_scr.at[slot, 1], piece_sem.at[slot, 1]
            ),
        )

    for load in piece_loads(0):
        load.start()
    gain_grad[...] = jnp.zeros_like(gain_grad)
    floor_grad[...] = jnp.zeros_like(floor_grad)
    back_scr[...] = jnp.zeros_like(back_scr)

    def turn(total, rows, own):
        out_ref[rows] = (residual[own] + total).astype(BF16)

    def earlier(shift):
        places = {axis: lax.axis_index(axis) for axis in mesh_axes}
        places["context"] = lax.rem(context + context_size - shift, context_size)
        return tuple(places[axis] for axis in mesh_axes)

    def keep_total(total, rows, own):
        total_ref[own] = total

    line = Line(mesh_axes, part, arrived, out_ref, sems[:4], turn)
    back_line = Line(mesh_axes, back, back_arrived, None, sems[4:], keep_total, backs=False)
    barrier = pltpu.get_barrier_semaphore()
    expected = line.greet(barrier)
    for shift in range(1, context_size):
        pl.semaphore_signal(barrier, inc=1, device_id=earlier(shift), device_id_type=MESH_ID)
    pl.semaphore_wait(barrier, expected + context_size - 1)

    def tile_columns(tile):
        return pl.ds(pl.multiple_of(tile * TILE, TILE), TILE)

    def stage_copy(tile):
        rows = tile_columns(tile)
        return pltpu.make_async_copy(mixer_stage, mixer_grads_hbm.at[rows], stage_sem.at[0])

    def gate_piece(index):
        rows = pl.ds(pl.multiple_of(index * piece_rows, piece_rows), piece_rows)
        slot = lax.rem(index, 2)

        @pl.when(index + 1 < tokens // piece_rows)
        def _():
            for load in piece_loads(index + 1):
                load.start()

        for load in piece_loads(index):
            load.wait()
        grads = mm_nn(mix_grad_ref[rows], out_full[...])
        gain = gain_ref[...]
        total = jnp.zeros_like(gain)
        for head in range(head_count):
            part_of = slice(head * lanes, (head + 1) * lanes)
            gate, mixed = piece_rows_scr[slot, 0, :, part_of], piece_rows_scr[slot, 1, :, part_of]
            grad = grads[:, part_of]
            inverse = inverse_rms(mixed)
            unit = mixed * inverse
            sigma = jax.nn.sigmoid(gate)
            scaled = grad * unit
            total = total + jnp.sum(scaled * (gate * sigma), axis=0, keepdims=True)
            grad_gate = scaled * gain * sigma * (1.0 + gate * (1.0 - sigma))
            first = 3 * width + head * lanes
            right[rows, first : first + lanes] = grad_gate.astype(BF16)
            lifted = grad * gain * (gate * sigma)
            mean = jnp.mean(lifted * unit, axis=-1, keepdims=True)
            grad_in = inverse * (lifted - unit * mean) * (key_scale * keep_ref[rows])
            grad_in = grad_in.astype(BF16)
            grad_mixed[rows, part_of] = grad_in
            back_scr[head] += mm_tn(grad_in, lead_ref[rows, part_of])
        gain_grad[...] += total

    def state_copy(shift):
        return pltpu.make_async_remote_copy(
            message,
            received.at[shift - 1],
            grad_send.at[shift - 1],
            grad_recv.at[shift - 1],
            device_id=earlier(shift),
            device_id_type=MESH_ID,
        )

    def block_of(index):
        return blocks - 1 - index

    def pre_load(index):
        rows = pl.ds(pl.multiple_of(block_of(index) * BLOCK, BLOCK), BLOCK)
        slot = lax.rem(index, 2)
        return pltpu.make_async_copy(
            pre_hbm.at[rows, pl.ds(0, 3 * width)], pre.at[slot], pre_sem.at[slot]
        )

    def send_back():
        for head in range(head_count):
            rows = slice(head * lanes, (head + 1) * lanes)
            message[rows] = back_scr[head] * link_ref[0:1]
            message[state_rows + head : state_rows + head + 1] = decay_ref[head] * link_ref[0:1]
        for shift in range(1, context_size):

            @pl.when(context >= shift)
            def _(shift=shift):
                state_copy(shift).start()

        pre_load(0).start()

    def take_back():
        grad_scr[...] = jnp.zeros_like(grad_scr)
        for shift in range(1, context_size):

            @pl.when(context + shift < context_size)
            def _(shift=shift):
                state_copy(shift).wait_recv()
                for head in range(head_count):
                    value = received[shift - 1, head * lanes : (head + 1) * lanes]
                    for near in range(shift - 1):
                        value = value * received[near, state_rows + head : state_rows + head + 1]
                    grad_scr[head] += value

        for shift in range(1, context_size):

            @pl.when(context >= shift)
            def _(shift=shift):
                state_copy(shift).wait_send()

    def mixer_block(index):
        block = block_of(index)
        slot = lax.rem(index, 2)
        block_rows = pl.ds(pl.multiple_of(block * BLOCK, BLOCK), BLOCK)

        @pl.when(index + 1 < blocks)
        def _():
            pre_load(index + 1).start()

        pre_load(index).wait()
        counts, keep, flags = count_ref[block_rows], keep_ref[block_rows], flags_ref[block]
        row_ids, col_ids, linked, fresh, tail, closing = block_masks(counts, flags)
        tri = (row_ids >= col_ids).astype(BF16)
        tri_back = (row_ids <= col_ids).astype(BF16)
        query_pre = pre[slot, :, :width]
        values = pre[slot, :, 2 * width : 3 * width].astype(BF16)
        opened = open_ref[...]
        closed = jax.nn.sigmoid(-pre[slot, :, width : 2 * width])
        keys = opened * closed
        cum = split_sum(tri, jnp.log1p(-keys))
        ending = cum[BLOCK - 1 : BLOCK, :]
        rise, fall = jnp.exp(cum), jnp.exp(-cum) * keep
        shift = jnp.exp(ending - cum) * (keep * tail)
        sigma_query = jax.nn.sigmoid(query_pre)
        lifted = (query_pre * sigma_query * rise).astype(BF16)
        lowered = (keys * fall).astype(BF16)
        moved = (keys * shift).astype(BF16)
        fresh_lifted = (lifted.astype(F32) * fresh).astype(BF16)
        end_decay = jnp.exp(ending) * closing
        lead_in = jnp.exp(run_ref[block]) * (flags[1:2, 0:1] == 0).astype(F32)
        for head in range(head_count):
            part_of = slice(head * lanes, (head + 1) * lanes)
            grad_out, value = grad_mixed[block_rows, part_of], values[:, part_of]
            lift, lower, move = lifted[:, part_of], lowered[:, part_of], moved[:, part_of]
            scores = jnp.where(linked, mm_nt(lift, lower), 0.0).astype(BF16)
            pulls = jnp.where(linked, mm_nt(grad_out, value), 0.0).astype(BF16)
            state = starts_ref[block, head] + lead_in[:, part_of] * carry_ref[head]
            grad_state = grad_scr[head]
            grad_low = grad_state.astype(BF16)
            lifted_scr[:, part_of] = mm_nn(pulls, lower) + fresh * mm_nn(
                grad_out, state.astype(BF16)
            )
            lowered_scr[:, part_of] = mm_tn(pulls, lift)
            grad_moved = mm_nn(value, grad_low)
            moved_scr[:, part_of] = grad_moved
            first = 2 * width + head * lanes
            right[block_rows, first : first + lanes] = (
                mm_tn(scores, grad_out) + mm_nt(move, grad_low)
            ).astype(BF16)
            value_scr[:, part_of] = jnp.sum(
                grad_moved * move.astype(F32), axis=0, keepdims=True
            ) + end_decay[:, part_of] * jnp.sum(state * grad_state, axis=0, keepdims=True)
            grad_scr[head] = grad_state * end_decay[:, part_of] + mm_tn(
                grad_out, fresh_lifted[:, part_of]
            )
        grad_lifted, grad_lowered, grad_moved = lifted_scr[...], lowered_scr[...], moved_scr[...]
        grad_cum = (
            grad_lifted * lifted.astype(F32)
            - grad_lowered * lowered.astype(F32)
            - grad_moved * moved.astype(F32)
        )
        grad_decay = split_sum(tri_back, grad_cum) + value_scr[...]
        key_total = grad_lowered * fall + grad_moved * shift - grad_decay / (1.0 - keys)
        floor_grad[...] -= jnp.sum(key_total * closed, axis=0, keepdims=True)
        right[block_rows, :width] = (
            grad_lifted * rise * sigma_query * (1.0 + query_pre * (1.0 - sigma_query))
        ).astype(BF16)
        right[block_rows, width : 2 * width] = (
            -key_total * opened * closed * (1.0 - closed)
        ).astype(BF16)

    def full_load(tile):
        slot = lax.rem(tile, 2)
        return pltpu.make_async_copy(
            full_hbm.at[tile_columns(tile)], full.at[slot], full_sem.at[slot]
        )

    def back_tile(tile):
        @pl.when(tile + 1 < tiles)
        def _():
            full_load(tile + 1).start()

        full_load(tile).wait()
        product = mm_nt(right[...], full[lax.rem(tile, 2)])
        back[:, tile_columns(tile)] = product.astype(BF16)

    def mixer_tile(tile):
        @pl.when(tile > 0)
        def _():
            stage_copy(tile - 1).wait()

        columns = tile_columns(tile)
        rows = left[:, columns]
        for first in range(0, 4 * width, 1024):
            some = slice(first, min(first + 1024, 4 * width))
            mixer_stage[:, some] = mm_tn(rows, right[:, some]).astype(BF16)
        product = mm_tn(mix_grad_ref[:, columns], gated_ref[...])
        mixer_stage[:, 4 * width :] = product.astype(BF16)
        stage_copy(tile).start()

    send_time = tokens // piece_rows
    block_time = send_time + 2
    back_time = block_time + blocks
    tile_time = back_time + tiles
    end_time = tile_time + tiles

    def piece(time):
        @pl.when(time == 0)
        def _():
            for load in gate_loads:
                load.wait()

        @pl.when(time < send_time)
        def _():
            gate_piece(time)

        @pl.when(time == send_time)
        def _():
            send_back()

        @pl.when(time == block_time)
        def _():
            starts_load.wait()
            take_back()

        @pl.when(jnp.logical_and(time >= block_time, time < back_time))
        def _():
            mixer_block(time - block_time)

        @pl.when(time == back_time - 1)
        def _():
            full_load(0).start()

        @pl.when(jnp.logical_and(time >= back_time, time < tile_time))
        def _():
            back_tile(time - back_time)

        @pl.when(time == tile_time)
        def _():
            for load in tile_loads:
                load.wait()

        @pl.when(jnp.logical_and(time >= tile_time, time < end_time))
        def _():
            mixer_tile(time - tile_time)

    slow = QUIET
    part_load.wait()
    begin = slow + -(-(tile_time - slow) // MANY)
    steps = max(line.steps, begin + back_line.steps, slow + -(-(end_time - slow) // MANY))

    def body(time, _):
        @pl.when(time < line.steps)
        def _():
            line.step(time)

        @pl.when(time >= begin)
        def _():
            back_line.step(time - begin)

        def pieces(index, _):
            piece(index)
            return 0

        first = jnp.where(time < slow, time, slow + MANY * (time - slow))
        lax.fori_loop(first, first + jnp.where(time < slow, 1, MANY), pieces, 0)
        return 0

    lax.fori_loop(0, steps, body, 0)
    stage_copy(tiles - 1).wait()
    line.finish()
    back_line.finish()


def output_line(mesh_axes, collective, in_vmem, in_hbm, head_count):
    part, residual, gated, mix_grad, out_full, lead, starts = in_hbm[:7]
    tokens, model_width = part.shape
    width = gated.shape[1]
    lanes = width // head_count
    context_size = lax.axis_size("context")
    messages = head_count * lanes + -(-head_count // 8) * 8
    whole = pl.BlockSpec(memory_space=pltpu.VMEM)
    remote = pl.BlockSpec(memory_space=pl.ANY)
    return pl.pallas_call(
        partial(output_kernel, mesh_axes, head_count, lanes ** (-0.5)),
        in_specs=[whole] * len(in_vmem) + [remote] * len(in_hbm),
        out_specs=[whole] * 4 + [remote],
        out_shape=[
            jax.ShapeDtypeStruct((tokens, model_width), BF16),
            jax.ShapeDtypeStruct((1, lanes), F32),
            jax.ShapeDtypeStruct((1, width), F32),
            jax.ShapeDtypeStruct((tokens // 2, model_width), F32),
            jax.ShapeDtypeStruct((model_width, 5 * width), BF16),
        ],
        scratch_shapes=[
            pltpu.VMEM(array.shape, array.dtype)
            for array in (part, residual, gated, mix_grad, out_full, lead, starts)
        ]
        + [
            pltpu.VMEM((tokens, model_width), BF16),
            pltpu.VMEM((tokens, model_width), BF16),
            pltpu.VMEM((tokens, model_width), BF16),
            pltpu.VMEM((tokens, model_width), BF16),
            pltpu.VMEM((tokens, 4 * width), BF16),
            pltpu.VMEM((2, TILE, 4 * width), BF16),
            pltpu.VMEM((TILE, 5 * width), BF16),
            pltpu.VMEM((2, 2, 2 * BLOCK, width), F32),
            pltpu.VMEM((2, BLOCK, 3 * width), F32),
            pltpu.VMEM((tokens, width), BF16),
            pltpu.VMEM((head_count, lanes, lanes), F32),
            pltpu.VMEM((messages, lanes), F32),
            pltpu.VMEM((context_size - 1, messages, lanes), F32),
            pltpu.VMEM((head_count, lanes, lanes), F32),
            pltpu.VMEM((BLOCK, width), F32),
            pltpu.VMEM((BLOCK, width), F32),
            pltpu.VMEM((BLOCK, width), F32),
            pltpu.VMEM((1, width), F32),
            pltpu.SemaphoreType.DMA((8,)),
            pltpu.SemaphoreType.DMA((2, 2)),
            pltpu.SemaphoreType.DMA((2,)),
            pltpu.SemaphoreType.DMA((2,)),
            pltpu.SemaphoreType.DMA((1,)),
            pltpu.SemaphoreType.DMA((context_size - 1,)),
            pltpu.SemaphoreType.DMA((context_size - 1,)),
        ]
        + line_sems(tokens)
        + line_sems(tokens, 2),
        compiler_params=pltpu.CompilerParams(
            collective_id=collective, has_side_effects=True, vmem_limit_bytes=61 << 20
        ),
        cost_estimate=pl.CostEstimate(
            flops=tokens * model_width * width * 24,
            bytes_accessed=360_000_000,
            transcendentals=tokens * width * 12,
        ),
        name="output_line",
    )(*in_vmem, *in_hbm)


class SmallSum:
    def __init__(self, mesh_axes, value, local, total, near, far, sems):
        self.mesh_axes = mesh_axes
        self.value, self.local, self.total, self.near, self.far = value, local, total, near, far
        self.near_send, self.near_recv, self.far_send, self.far_recv = sems
        self.context_size = lax.axis_size("context")
        self.group = lax.axis_size("shard") * self.context_size
        self.line_size = lax.axis_size("tensor")
        self.place = lax.axis_index("shard") * self.context_size + lax.axis_index("context")
        self.line_place = lax.axis_index("tensor")

    def device(self, position, line_position):
        places = {
            "shard": position // self.context_size,
            "context": lax.rem(position, self.context_size),
            "tensor": line_position,
        }
        return tuple(places[axis] for axis in self.mesh_axes)

    def near_target(self, step):
        return self.device(lax.rem(self.place + step, self.group), self.line_place)

    def far_target(self, step):
        return self.device(self.place, lax.rem(self.line_place + step, self.line_size))

    def near_copy(self, step):
        return pltpu.make_async_remote_copy(
            self.value,
            self.near.at[step - 1],
            self.near_send.at[step - 1],
            self.near_recv.at[step - 1],
            device_id=self.near_target(step),
            device_id_type=MESH_ID,
        )

    def far_copy(self, step):
        return pltpu.make_async_remote_copy(
            self.local,
            self.far.at[step - 1],
            self.far_send.at[step - 1],
            self.far_recv.at[step - 1],
            device_id=self.far_target(step),
            device_id_type=MESH_ID,
        )

    def greet(self, barrier):
        targets = [self.near_target(step) for step in range(1, self.group)]
        targets += [self.far_target(step) for step in range(1, self.line_size)]
        for target in targets:
            pl.semaphore_signal(barrier, inc=1, device_id=target, device_id_type=MESH_ID)
        return len(targets)

    def start(self):
        for step in range(1, self.group):
            self.near_copy(step).start()

    def pass_on(self):
        total = self.value[...]
        for step in range(1, self.group):
            self.near_copy(step).wait_recv()
            total = total + self.near[step - 1]
        self.local[...] = total
        for step in range(1, self.line_size):
            self.far_copy(step).start()

    def finish(self):
        total = self.local[...]
        for step in range(1, self.line_size):
            self.far_copy(step).wait_recv()
            total = total + self.far[step - 1]
        self.total[...] = total
        for step in range(1, self.group):
            self.near_copy(step).wait_send()
        for step in range(1, self.line_size):
            self.far_copy(step).wait_send()


def input_kernel(
    mesh_axes,
    gain_ref,
    norm_two_ref,
    head_ref,
    floor_ref,
    total_hbm,
    hidden_hbm,
    residual_hbm,
    grads_hbm,
    out_ref,
    small_local,
    small_total,
    share_query,
    share_forget,
    share_input,
    share_gate,
    share_out,
    total_ref,
    hidden_ref,
    residual_grad,
    own,
    other,
    remote,
    gain_grad,
    small,
    small_near,
    small_far,
    quarter_sem,
    load_sem,
    pair_send,
    pair_recv,
    chip_send,
    chip_recv,
    *sems,
):
    plane = Plane(mesh_axes)
    chips = plane.chips
    block = own.shape[1]
    gain_grad[...] = jnp.zeros_like(gain_grad)
    half, line_size = total_ref.shape[0], lax.axis_size("tensor")
    place = lax.axis_index("tensor")
    at_end = jnp.logical_or(place == 0, place == line_size - 1)
    first_row = jnp.where(place == 0, 0, half)
    quarters = 4
    length = half // quarters

    def quarter_loads(index):
        rows = pl.ds(pl.multiple_of(index * length, length), length)
        inputs = pl.ds(pl.multiple_of(first_row + index * length, length), length)
        return [
            pltpu.make_async_copy(source, target.at[rows], quarter_sem.at[which, index])
            for which, (source, target) in enumerate(
                (
                    (total_hbm.at[rows], total_ref),
                    (hidden_hbm.at[inputs], hidden_ref),
                    (residual_hbm.at[rows], residual_grad),
                )
            )
        ]

    @pl.when(at_end)
    def _():
        for index in range(quarters):
            for load in quarter_loads(index):
                load.start()

    def turn(total, rows, own_rows):
        total = total_ref[own_rows]
        values = hidden_ref[own_rows].astype(F32)
        inverse = inverse_rms(values)
        unit = values * inverse
        gain_grad[...] += jnp.sum(total * unit, axis=0, keepdims=True)
        lifted = total * gain_ref[...]
        mean = jnp.mean(lifted * unit, axis=-1, keepdims=True)
        grad = residual_grad[own_rows] + inverse * (lifted - unit * mean)
        out_ref[rows] = grad.astype(BF16)

    line = Line(mesh_axes, None, None, out_ref, sems[:2], turn, sums=False)
    small_sum = SmallSum(
        mesh_axes, small, small_local, small_total, small_near, small_far, sems[2:]
    )
    barrier = pltpu.get_barrier_semaphore()
    expected = line.greet(barrier) + plane.greet(barrier) + small_sum.greet(barrier)
    pl.semaphore_wait(barrier, expected)

    def rows_of(slot, core):
        return pl.ds(pl.multiple_of((2 * plane.ahead(slot) + core) * block, block), block)

    def load(slot):
        return pltpu.make_async_copy(
            grads_hbm.at[rows_of(slot, plane.core)], own.at[slot], load_sem.at[slot]
        )

    def pair_copy(slot):
        return pltpu.make_async_remote_copy(
            grads_hbm.at[rows_of(slot, 1 - plane.core)],
            other.at[slot],
            pair_send.at[slot],
            pair_recv.at[slot],
            device_id=plane.device(plane.chip, 1 - plane.core),
            device_id_type=MESH_ID,
        )

    def chip_copy(slot):
        return pltpu.make_async_remote_copy(
            own.at[slot],
            remote.at[slot - 1],
            chip_send.at[slot - 1],
            chip_recv.at[slot - 1],
            device_id=plane.device(plane.ahead(slot), plane.core),
            device_id_type=MESH_ID,
        )

    def start(index, _):
        slot = lax.rem(index + 1, chips)
        pair_copy(slot).start()
        load(slot).start()
        return 0

    lax.fori_loop(0, chips, start, 0)
    strip = 32

    def combine(time):
        slot = lax.rem(jnp.clip(time, 0, chips - 1) + 1, chips)

        @pl.when(time < chips)
        def _():
            load(slot).wait()
            pair_copy(slot).wait_recv()

            def add(index, _):
                rows = pl.ds(pl.multiple_of(index * strip, strip), strip)
                total = own[slot, rows].astype(F32) + other[slot, rows].astype(F32)
                own[slot, rows] = total.astype(BF16)
                return 0

            lax.fori_loop(0, block // strip, add, 0)

        @pl.when(time < chips - 1)
        def _():
            chip_copy(slot).start()

    def step(time, _):
        index = time * CHUNK // length
        fresh = jnp.logical_and(lax.rem(time * CHUNK, length) == 0, index < quarters)

        @pl.when(jnp.logical_and(at_end, fresh))
        def _():
            for load in quarter_loads(index):
                load.wait()

        line.step(time)
        combine(time)
        return 0

    lax.fori_loop(0, line.steps, step, 0)
    small[...] = jnp.zeros_like(small)
    row = 0
    for ref in (gain_grad, norm_two_ref, head_ref, floor_ref):
        for first in range(0, ref.shape[1], 128):
            small[row : row + 1] = ref[:, first : first + 128]
            row += 1
    small_sum.start()

    def arrive(index, _):
        chip_copy(index).wait_recv()
        return 0

    lax.fori_loop(1, chips, arrive, 0)

    def total(index, _):
        rows = pl.ds(pl.multiple_of(index * strip, strip), strip)

        for which, share in enumerate(
            (share_query, share_forget, share_input, share_gate, share_out)
        ):
            columns = pl.ds(which * share.shape[1], share.shape[1])

            def add(slot, value, columns=columns):
                return value + remote[slot, rows, columns].astype(F32)

            share[rows] = lax.fori_loop(0, chips - 1, add, own[0, rows, columns].astype(F32))
        return 0

    small_sum.pass_on()
    lax.fori_loop(0, block // strip, total, 0)
    small_sum.finish()

    def sent(index, _):
        pair_copy(index).wait_send()
        return 0

    lax.fori_loop(0, chips, sent, 0)

    def chip_sent(index, _):
        chip_copy(index).wait_send()
        return 0

    lax.fori_loop(1, chips, chip_sent, 0)
    line.finish()


def input_line(mesh_axes, collective, total, hidden, residual_grad, gain, grads, small):
    tokens, model_width = hidden.shape
    all_width = grads.shape[1]
    chips = lax.axis_size("shard") * lax.axis_size("context") // 2
    block = model_width // (2 * chips)
    values = model_width + sum(value.shape[1] for value in small)
    small_shape = (-(-values // 1024) * 8, 128)
    group, line_size = 2 * chips, lax.axis_size("tensor")
    whole = pl.BlockSpec(memory_space=pltpu.VMEM)
    return pl.pallas_call(
        partial(input_kernel, mesh_axes),
        in_specs=[whole] * 4 + [pl.BlockSpec(memory_space=pl.ANY)] * 4,
        out_specs=[whole] * 8,
        out_shape=[
            jax.ShapeDtypeStruct((tokens, model_width), BF16),
            jax.ShapeDtypeStruct(small_shape, F32),
            jax.ShapeDtypeStruct(small_shape, F32),
        ]
        + [jax.ShapeDtypeStruct((block, all_width // 5), F32)] * 5,
        scratch_shapes=[
            pltpu.VMEM((tokens // 2, model_width), F32),
            pltpu.VMEM((tokens // 2, model_width), BF16),
            pltpu.VMEM((tokens // 2, model_width), F32),
            pltpu.VMEM((chips, block, all_width), BF16),
            pltpu.VMEM((chips, block, all_width), BF16),
            pltpu.VMEM((chips - 1, block, all_width), BF16),
            pltpu.VMEM((1, model_width), F32),
            pltpu.VMEM(small_shape, F32),
            pltpu.VMEM((group - 1, *small_shape), F32),
            pltpu.VMEM((line_size - 1, *small_shape), F32),
            pltpu.SemaphoreType.DMA((3, 4)),
            pltpu.SemaphoreType.DMA((chips,)),
            pltpu.SemaphoreType.DMA((chips,)),
            pltpu.SemaphoreType.DMA((chips,)),
            pltpu.SemaphoreType.DMA((chips - 1,)),
            pltpu.SemaphoreType.DMA((chips - 1,)),
        ]
        + line_sems(tokens, 2)
        + [
            pltpu.SemaphoreType.DMA((group - 1,)),
            pltpu.SemaphoreType.DMA((group - 1,)),
            pltpu.SemaphoreType.DMA((line_size - 1,)),
            pltpu.SemaphoreType.DMA((line_size - 1,)),
        ],
        compiler_params=pltpu.CompilerParams(
            collective_id=collective, has_side_effects=True, vmem_limit_bytes=58 << 20
        ),
        cost_estimate=pl.CostEstimate(
            flops=tokens * model_width * 8, bytes_accessed=360_000_000, transcendentals=0
        ),
        name="input_line",
    )(gain, *small, total, hidden, residual_grad, grads)


def forward_kernel(
    mesh_axes,
    head_count,
    key_scale,
    hidden_ref,
    gain_ref,
    query_hbm,
    forget_hbm,
    input_hbm,
    gate_hbm,
    out_shard_ref,
    down_shard_ref,
    floor_ref,
    segments_ref,
    head_gain_ref,
    normed_hbm,
    pre_hbm,
    full_hbm,
    out_full_hbm,
    mixed_hbm,
    lead_hbm,
    start_hbm,
    gated_hbm,
    mix_hbm,
    down_turned,
    open_ref,
    count_ref,
    keep_ref,
    flags_ref,
    run_ref,
    carry_ref,
    decay_ref,
    link_ref,
    normed,
    pre,
    mine,
    out_turned,
    full,
    out_full,
    mixed,
    lead,
    starts,
    gated,
    mix,
    state_scr,
    run_scr,
    message,
    received,
    mine_sem,
    full_sem,
    save_sem,
    pre_sem,
    mix_sem,
    state_send,
    state_recv,
    *sems,
):
    plane = Plane(mesh_axes)
    chips = plane.chips
    tokens, model_width = hidden_ref.shape
    block, width = query_hbm.shape
    lanes = width // head_count
    state_rows = head_count * lanes
    context, context_size = lax.axis_index("context"), lax.axis_size("context")

    mine_loads = [
        pltpu.make_async_copy(
            ref, mine.at[:, pl.ds(which * width, width)], mine_sem.at[which]
        )
        for which, ref in enumerate((query_hbm, forget_hbm, input_hbm, gate_hbm))
    ]
    for load in mine_loads:
        load.start()
    gather = Gather(plane, (mine,), (full,), sems[:5])
    out_gather = Gather(plane, (out_turned,), (out_full,), sems[5:])

    def later(shift):
        places = {axis: lax.axis_index(axis) for axis in mesh_axes}
        places["context"] = lax.rem(context + shift, context_size)
        return tuple(places[axis] for axis in mesh_axes)

    out_turned[...] = out_shard_ref[...].T
    barrier = pltpu.get_barrier_semaphore()
    expected = gather.greet(barrier)
    for shift in range(1, context_size):
        pl.semaphore_signal(barrier, inc=1, device_id=later(shift), device_id_type=MESH_ID)
    pl.semaphore_wait(barrier, expected + context_size - 1)
    for load in mine_loads:
        load.wait()
    gather.start()
    out_gather.start()
    down_turned[...] = down_shard_ref[...].T
    for head in range(head_count):
        open_ref[:, head * lanes : (head + 1) * lanes] = 1.0 - floor_ref[head : head + 1]

    segments = segments_ref[...]
    blocks = segments.shape[0]
    block_ids = lax.broadcasted_iota(jnp.int32, segments.shape, 0)
    slot_ids = lax.broadcasted_iota(jnp.int32, segments.shape, 1)
    before = pltpu.roll(segments, 1, 1)
    wrapped = pltpu.roll(before, 1, 0)
    before = jnp.where(slot_ids == 0, wrapped, before)
    first_slot = jnp.logical_and(slot_ids == 0, block_ids == 0)
    begins = jnp.where(jnp.logical_or(first_slot, segments == before), 0.0, 1.0)
    wide_rows = lax.broadcasted_iota(jnp.int32, (BLOCK, BLOCK), 0)
    wide_columns = lax.broadcasted_iota(jnp.int32, (BLOCK, BLOCK), 1)
    within = mm_nn(begins.astype(BF16), (wide_rows <= wide_columns).astype(BF16))
    count_rows = []
    running = jnp.zeros((1, 1), F32)
    flags_ref[...] = jnp.zeros_like(flags_ref)
    for index in range(blocks):
        row = within[index : index + 1] + running
        flags_ref[index, 0:1] = row
        flags_ref[index, 1:2] = jnp.broadcast_to(running, (1, BLOCK))
        running = row[:, BLOCK - 1 : BLOCK]
        flags_ref[index, 2:3] = jnp.broadcast_to(running, (1, BLOCK))
        count_rows.append(row)
    turned_counts = jnp.concatenate(count_rows, axis=0).T
    turned_keep = (segments > 0).astype(F32).T
    for index in range(blocks):
        rows = slice(index * BLOCK, (index + 1) * BLOCK)
        count_ref[rows] = turned_counts[:, index : index + 1]
        keep_ref[rows] = turned_keep[:, index : index + 1]
    first_id = jnp.broadcast_to(segments[0:1, 0:1], (1, lanes))
    last_id = jnp.broadcast_to(segments[blocks - 1 : blocks, BLOCK - 1 : BLOCK], (1, lanes))

    def norm(index, _):
        rows = pl.ds(pl.multiple_of(index * 128, 128), 128)
        values = hidden_ref[rows].astype(F32)
        normed[rows] = (values * inverse_rms(values) * gain_ref[...]).astype(BF16)
        return 0

    lax.fori_loop(0, tokens // 128, norm, 0)

    saves = [
        pltpu.make_async_copy(source, target, save_sem.at[which])
        for which, (source, target) in enumerate(
            (
                (normed, normed_hbm),
                (out_full, out_full_hbm),
                (mixed, mixed_hbm),
                (lead, lead_hbm),
                (starts, start_hbm),
                (gated, gated_hbm),
            )
        )
    ]
    saves[0].start()
    row_tile, column_tile = 256, 512

    def pre_save(index):
        rows = pl.ds(pl.multiple_of(index * row_tile, row_tile), row_tile)
        return pltpu.make_async_copy(pre.at[rows], pre_hbm.at[rows], pre_sem.at[index])

    def depth_of(distance):
        first = 2 * gather.partner(distance) * block
        return pl.ds(pl.multiple_of(first, 2 * block), 2 * block)

    def product(distance):
        depth = depth_of(distance)

        def row_body(index, _):
            rows = pl.ds(pl.multiple_of(index * row_tile, row_tile), row_tile)
            left = normed[rows, depth]

            def column_body(column, _):
                columns = pl.ds(pl.multiple_of(column * column_tile, column_tile), column_tile)
                value = mm_nn(left, full[depth, columns])
                if distance > 0:
                    value = value + pre[rows, columns]
                pre[rows, columns] = value
                return 0

            lax.fori_loop(0, full.shape[1] // column_tile, column_body, 0)
            if distance == chips - 1:
                pre_save(index).start()
            return 0

        lax.fori_loop(0, tokens // row_tile, row_body, 0)

    def full_save(distance):
        depth = depth_of(distance)
        return pltpu.make_async_copy(full.at[depth], full_hbm.at[depth], full_sem.at[distance])

    def use(distance):
        gather.arrive_from(distance)
        full_save(distance).start()
        product(distance)

    use(0)
    gather.stage(0)
    gather.stage(1)
    if gather.relayed:
        use(1)
        use(2)
    gather.stage(2)
    if gather.relayed:
        use(3)
    else:
        for distance in range(1, chips):
            use(distance)
    out_gather.stage(0)
    out_gather.stage(1)

    state_scr[...] = jnp.zeros_like(state_scr)
    run_scr[...] = jnp.zeros_like(run_scr)

    def recur(step, _):
        rows = pl.ds(pl.multiple_of(step * BLOCK, BLOCK), BLOCK)
        counts, keep = count_ref[rows], keep_ref[rows]
        row_ids, col_ids, linked, fresh, tail, closing = block_masks(counts, flags_ref[step])
        tri = (row_ids >= col_ids).astype(BF16)
        query_pre = pre[rows, :width]
        values = pre[rows, 2 * width : 3 * width].astype(BF16)
        keys = open_ref[...] * jax.nn.sigmoid(-pre[rows, width : 2 * width])
        cum = split_sum(tri, jnp.log1p(-keys))
        ending = cum[BLOCK - 1 : BLOCK, :]
        lifted = query_pre * jax.nn.sigmoid(query_pre) * jnp.exp(cum)
        lowered = (keys * jnp.exp(-cum) * keep).astype(BF16)
        moved = (keys * jnp.exp(ending - cum) * (keep * tail)).astype(BF16)
        run = run_scr[...]
        lead[rows] = (lifted * jnp.exp(run) * (counts == 0).astype(F32)).astype(BF16)
        run_ref[step] = run
        run_scr[...] = run + ending
        fresh_lifted = (lifted * fresh).astype(BF16)
        lifted = lifted.astype(BF16)
        end_decay = jnp.exp(ending) * closing
        for head in range(head_count):
            part = slice(head * lanes, (head + 1) * lanes)
            state = state_scr[head]
            starts[step, head] = state
            scores = jnp.where(linked, mm_nt(lifted[:, part], lowered[:, part]), 0.0)
            results = mm_nn(scores.astype(BF16), values[:, part])
            results = results + mm_nt(fresh_lifted[:, part], state.astype(BF16))
            mixed[rows, part] = results * (key_scale * keep)
            state_scr[head] = state * end_decay[:, part] + mm_tn(values[:, part], moved[:, part])
        return 0

    lax.fori_loop(0, tokens // BLOCK, recur, 0)
    saves[3].start()
    saves[4].start()

    last_count = flags_ref[tokens // BLOCK - 1][2:3, 0:1]
    for head in range(head_count):
        part = slice(head * lanes, (head + 1) * lanes)
        message[head * lanes : (head + 1) * lanes] = state_scr[head]
        decay = jnp.exp(run_scr[:, part]) * (last_count == 0).astype(F32)
        decay_ref[head] = decay
        message[state_rows + 8 + head : state_rows + 9 + head] = decay
    message[state_rows : state_rows + 1] = first_id
    message[state_rows + 1 : state_rows + 2] = last_id

    def state_copy(shift):
        return pltpu.make_async_remote_copy(
            message,
            received.at[shift - 1],
            state_send.at[shift - 1],
            state_recv.at[shift - 1],
            device_id=later(shift),
            device_id_type=MESH_ID,
        )

    for shift in range(1, context_size):

        @pl.when(context + shift < context_size)
        def _(shift=shift):
            state_copy(shift).start()

    out_gather.stage(2)
    carry_ref[...] = jnp.zeros_like(carry_ref)
    link_ref[...] = jnp.zeros_like(link_ref)
    for shift in range(1, context_size):

        @pl.when(context >= shift)
        def _(shift=shift):
            state_copy(shift).wait_recv()
            linked = jnp.ones((1, lanes), F32)
            follower = first_id
            factors = [jnp.ones((1, lanes), F32)] * head_count
            for near in range(shift):
                got = received.at[near]
                linked = (got[state_rows + 1 : state_rows + 2] == follower).astype(F32)
                follower = got[state_rows : state_rows + 1]
                factors = [factor * linked for factor in factors]
                if near < shift - 1:
                    factors = [
                        factor * got[state_rows + 8 + head : state_rows + 9 + head]
                        for head, factor in enumerate(factors)
                    ]
            if shift == 1:
                link_ref[0:1] = linked
            for head in range(head_count):
                rows = slice(head * lanes, (head + 1) * lanes)
                carry_ref[head] += factors[head] * received[shift - 1, rows]

    for shift in range(1, context_size):

        @pl.when(context + shift < context_size)
        def _(shift=shift):
            state_copy(shift).wait_send()

    for distance in range(chips):
        out_gather.arrive_from(distance)
    saves[1].start()

    def mix_save(index):
        rows = pl.ds(pl.multiple_of(index * row_tile, row_tile), row_tile)
        return pltpu.make_async_copy(mix.at[rows], mix_hbm.at[rows], mix_sem.at[index])

    def project(index, _):
        rows = pl.ds(pl.multiple_of(index * row_tile, row_tile), row_tile)
        for head in range(head_count):
            part = slice(head * lanes, (head + 1) * lanes)
            carried = mm_nt(lead[rows, part], carry_ref[head].astype(BF16))
            value = mixed[rows, part] + carried * (key_scale * keep_ref[rows])
            mixed[rows, part] = value
            gate = pre[rows, 3 * width + head * lanes : 3 * width + (head + 1) * lanes]
            unit = value * inverse_rms(value)
            gated[rows, part] = (
                unit * head_gain_ref[...] * (gate * jax.nn.sigmoid(gate))
            ).astype(BF16)
        left = gated[rows]

        def column_body(column, _):
            columns = pl.ds(pl.multiple_of(column * column_tile, column_tile), column_tile)
            mix[rows, columns] = mm_nt(left, out_full[columns, :]).astype(BF16)
            return 0

        lax.fori_loop(0, model_width // column_tile, column_body, 0)
        mix_save(index).start()
        return 0

    lax.fori_loop(0, tokens // row_tile, project, 0)
    saves[2].start()
    saves[5].start()
    gather.finish()
    out_gather.finish()
    for distance in range(chips):
        full_save(distance).wait()
    for save in saves:
        save.wait()
    for index in range(tokens // row_tile):
        pre_save(index).wait()
        mix_save(index).wait()


def forward(
    mesh_axes, collective, hidden, gain, shards, out_shard, down_shard, floor, segments, head_gain
):
    tokens, model_width = hidden.shape
    block, width = shards[0].shape
    lanes = head_gain.shape[1]
    head_count = width // lanes
    all_width = width * len(shards)
    blocks = tokens // BLOCK
    context_size = lax.axis_size("context")
    chips = lax.axis_size("shard") * context_size // 2
    messages = head_count * lanes + 8 + -(-head_count // 8) * 8
    whole = pl.BlockSpec(memory_space=pltpu.VMEM)
    remote = pl.BlockSpec(memory_space=pl.ANY)
    stored = [
        ((tokens, model_width), BF16),
        ((tokens, all_width), F32),
        ((model_width, all_width), BF16),
        ((model_width, width), BF16),
        ((tokens, width), F32),
        ((tokens, width), BF16),
        ((blocks, head_count, lanes, lanes), F32),
        ((tokens, width), BF16),
        ((tokens, model_width), BF16),
    ]
    kept = [
        (down_shard.shape[::-1], BF16),
        ((1, width), F32),
        ((tokens, 1), F32),
        ((tokens, 1), F32),
        ((blocks, 8, BLOCK), F32),
        ((blocks, 1, width), F32),
        ((head_count, lanes, lanes), F32),
        ((head_count, 1, lanes), F32),
        ((8, lanes), F32),
    ]
    return pl.pallas_call(
        partial(forward_kernel, mesh_axes, head_count, lanes ** (-0.5)),
        in_specs=[whole] * 2 + [remote] * 4 + [whole] * 5,
        out_specs=[remote] * len(stored) + [whole] * len(kept),
        out_shape=[jax.ShapeDtypeStruct(shape, kind) for shape, kind in stored + kept],
        scratch_shapes=[
            pltpu.VMEM((tokens, model_width), BF16),
            pltpu.VMEM((tokens, all_width), F32),
            pltpu.VMEM((block, all_width), BF16),
            pltpu.VMEM((block, width), BF16),
            pltpu.VMEM((model_width, all_width), BF16),
            pltpu.VMEM((model_width, width), BF16),
            pltpu.VMEM((tokens, width), F32),
            pltpu.VMEM((tokens, width), BF16),
            pltpu.VMEM((blocks, head_count, lanes, lanes), F32),
            pltpu.VMEM((tokens, width), BF16),
            pltpu.VMEM((tokens, model_width), BF16),
            pltpu.VMEM((head_count, lanes, lanes), F32),
            pltpu.VMEM((1, width), F32),
            pltpu.VMEM((messages, lanes), F32),
            pltpu.VMEM((context_size - 1, messages, lanes), F32),
            pltpu.SemaphoreType.DMA((4,)),
            pltpu.SemaphoreType.DMA((chips,)),
            pltpu.SemaphoreType.DMA((6,)),
            pltpu.SemaphoreType.DMA((tokens // 256,)),
            pltpu.SemaphoreType.DMA((tokens // 256,)),
            pltpu.SemaphoreType.DMA((context_size - 1,)),
            pltpu.SemaphoreType.DMA((context_size - 1,)),
        ]
        + gather_sems(1)
        + gather_sems(1),
        compiler_params=pltpu.CompilerParams(
            collective_id=collective, has_side_effects=True, vmem_limit_bytes=56 << 20
        ),
        cost_estimate=pl.CostEstimate(
            flops=2 * tokens * model_width * all_width,
            bytes_accessed=200_000_000,
            transcendentals=tokens * width * 9,
        ),
        name="forward",
    )(hidden, gain, *shards, out_shard, down_shard, floor, segments, head_gain)


def closing_kernel(
    count,
    ffn_ref,
    out_share_ref,
    *refs,
):
    moved_in, refs = refs[:count], refs[count:]
    gate_ref, up_ref, down_ref, out_ref = refs[:4]
    moved_out, sem = refs[4 : 4 + count], refs[4 + count]
    pieces = 4
    copies = []
    for which, (source, target) in enumerate(zip(moved_in, moved_out)):
        length = source.shape[0] // pieces
        for index in range(pieces):
            rows = pl.ds(index * length, length)
            copies.append(
                pltpu.make_async_copy(source.at[rows], target.at[rows], sem.at[which, index])
            )
    for copy in copies:
        copy.start()
    hidden_width = gate_ref.shape[1]
    gate_ref[...] = ffn_ref[:, :hidden_width].astype(F32)
    up_ref[...] = ffn_ref[:, hidden_width : 2 * hidden_width].astype(F32)
    for first in range(0, hidden_width, 128):
        columns = slice(2 * hidden_width + first, 2 * hidden_width + first + 128)
        down_ref[first : first + 128] = ffn_ref[:, columns].astype(F32).T
    for first in range(0, out_share_ref.shape[1], 128):
        out_ref[first : first + 128] = out_share_ref[:, first : first + 128].T
    for copy in copies:
        copy.wait()


def closing(share_ffn, share_out, moved):
    block, all_width = share_ffn.shape
    hidden_width = all_width // 3
    whole = pl.BlockSpec(memory_space=pltpu.VMEM)
    remote = pl.BlockSpec(memory_space=pl.ANY)
    return pl.pallas_call(
        partial(closing_kernel, len(moved)),
        in_specs=[whole] * 2 + [remote] * len(moved),
        out_specs=[whole] * 4 + [remote] * len(moved),
        out_shape=[
            jax.ShapeDtypeStruct((block, hidden_width), F32),
            jax.ShapeDtypeStruct((block, hidden_width), F32),
            jax.ShapeDtypeStruct((hidden_width, block), F32),
            jax.ShapeDtypeStruct(share_out.shape[::-1], F32),
        ]
        + [jax.ShapeDtypeStruct(value.shape, value.dtype) for value in moved],
        scratch_shapes=[pltpu.SemaphoreType.DMA((len(moved), 4))],
        compiler_params=pltpu.CompilerParams(vmem_limit_bytes=61 << 20),
        cost_estimate=pl.CostEstimate(flops=0, bytes_accessed=30_000_000, transcendentals=0),
        name="closing",
    )(share_ffn, share_out, *moved)


def local(
    mesh_axes,
    hidden,
    segment_ids,
    norm1_gain,
    w_query,
    w_forget,
    w_input,
    w_gate_out,
    forget_floor,
    head_gain,
    w_out,
    norm2_gain,
    w_ffn_gate,
    w_ffn_up,
    w_ffn_down,
    out_grad,
):
    sequences, span_len, model_width = hidden.shape
    tokens = sequences * span_len
    head_count, key_dim = forget_floor.shape
    width = head_count * key_dim
    key_scale = key_dim ** (-0.5)
    both = ("shard", "context")
    gain_one, gain_two = norm1_gain.reshape(1, -1), norm2_gain.reshape(1, -1)
    hidden_rows = hidden.reshape(tokens, model_width)
    gain_row = head_gain.reshape(1, -1)
    segments = segment_ids.reshape(tokens // BLOCK, BLOCK).astype(F32)
    (
        normed_one,
        pre,
        mixer_full,
        out_full,
        mixed,
        lead,
        starts,
        gated_low,
        mix_part,
        down_turned,
        open_part,
        counts,
        keep,
        flags,
        runs,
        carry,
        decay,
        link,
    ) = forward(
        mesh_axes,
        4,
        hidden_rows,
        gain_one,
        (w_query, w_forget, w_input, w_gate_out),
        w_out,
        w_ffn_down,
        forget_floor,
        segments,
        gain_row,
    )
    grad_rows = out_grad.reshape(tokens, model_width)
    (
        grad_mix_low,
        grad_norm_two,
        residual,
        _,
        _,
        _,
        feed_part,
        grad_residual,
        grads_ffn,
    ) = middle(
        mesh_axes,
        2,
        mix_part,
        grad_rows,
        hidden_rows,
        gain_two,
        w_ffn_gate,
        w_ffn_up,
        down_turned,
    )
    (
        output_rows,
        grad_head_part,
        grad_floor_part,
        back_one,
        grads_mixer,
    ) = output_line(
        mesh_axes,
        1,
        (
            runs,
            carry,
            decay,
            link,
            open_part,
            counts,
            keep,
            flags,
            gain_row,
        ),
        (
            feed_part,
            residual,
            gated_low,
            grad_mix_low,
            out_full,
            lead,
            starts,
            normed_one,
            pre,
            mixer_full,
            mixed,
        ),
        head_count,
    )
    share_ffn = lax.psum_scatter(grads_ffn, both, scatter_dimension=0, tiled=True)
    input_rows, near, total, *mixer_shares, share_out = input_line(
        mesh_axes,
        3,
        back_one,
        hidden_rows,
        grad_residual,
        gain_one,
        grads_mixer,
        (grad_norm_two, grad_head_part, grad_floor_part),
    )
    near, total = near.reshape(-1), total.reshape(-1)
    shares = lax.axis_size("shard") * lax.axis_size("context")
    position = lax.axis_index("shard") * lax.axis_size("context") + lax.axis_index("context")

    def own_slice(first, length):
        length = length // shares
        return lax.dynamic_slice_in_dim(total, first + position * length, length, 0)

    first = 2 * model_width + key_dim
    floor_total = near[first : first + width].reshape(head_count, key_dim)
    floor_part = key_dim // shares

    share_gate, share_up, share_down, share_out, output_rows, input_rows, *mixer_shares = closing(
        share_ffn, share_out, (output_rows, input_rows, *mixer_shares)
    )
    return (
        output_rows.reshape(hidden.shape),
        input_rows.reshape(hidden.shape),
        own_slice(0, model_width),
        *mixer_shares,
        lax.dynamic_slice_in_dim(floor_total, position * floor_part, floor_part, 1),
        own_slice(2 * model_width, key_dim),
        share_out,
        own_slice(model_width, model_width),
        share_gate,
        share_up,
        share_down,
    )


def solution(mesh):
    in_specs = (
        P("shard", "context", None),
        P("shard", "context"),
        P(),
        P(("shard", "context"), "tensor"),
        P(("shard", "context"), "tensor"),
        P(("shard", "context"), "tensor"),
        P(("shard", "context"), "tensor"),
        P("tensor", None),
        P(),
        P("tensor", ("shard", "context")),
        P(),
        P(("shard", "context"), "tensor"),
        P(("shard", "context"), "tensor"),
        P("tensor", ("shard", "context")),
        P("shard", "context", None),
    )
    out_specs = (
        P("shard", "context", None),
        P("shard", "context", None),
        P(("shard", "context")),
        P(("shard", "context"), "tensor"),
        P(("shard", "context"), "tensor"),
        P(("shard", "context"), "tensor"),
        P(("shard", "context"), "tensor"),
        P("tensor", ("shard", "context")),
        P(("shard", "context")),
        P("tensor", ("shard", "context")),
        P(("shard", "context")),
        P(("shard", "context"), "tensor"),
        P(("shard", "context"), "tensor"),
        P("tensor", ("shard", "context")),
    )
    return jax.shard_map(
        partial(local, mesh.axis_names), mesh=mesh, in_specs=in_specs, out_specs=out_specs, check_vma=False)
```

```python
from functools import partial

import jax
import jax.numpy as jnp
from jax import lax
from jax.experimental import pallas as pl
from jax.experimental.pallas import tpu as pltpu
from jax.sharding import PartitionSpec as P

EPSILON = 1e-05


BLOCK = 128
F32 = jnp.float32
BF16 = jnp.bfloat16


def mm(a, b, dims):
    return lax.dot_general(a, b, (dims, ((), ())), preferred_element_type=F32)


def mm_nn(a, b):
    return mm(a, b, ((1,), (0,)))


def mm_nt(a, b):
    return mm(a, b, ((1,), (1,)))


def mm_tn(a, b):
    return mm(a, b, ((0,), (0,)))


def split_sum(tri, values):
    high = values.astype(BF16)
    low = (values - high.astype(F32)).astype(BF16)
    return mm_nn(tri, high) + mm_nn(tri, low)


def block_masks(counts, flags_row):
    rows = counts.shape[0]
    row_ids = lax.broadcasted_iota(jnp.int32, (rows, rows), 0)
    col_ids = lax.broadcasted_iota(jnp.int32, (rows, rows), 1)
    linked = jnp.logical_and(counts == flags_row[0:1], row_ids >= col_ids)
    fresh = (counts == flags_row[1:2, 0:1]).astype(F32)
    tail = (counts == flags_row[2:3, 0:1]).astype(F32)
    closing = (flags_row[1:2, 0:1] == flags_row[2:3, 0:1]).astype(F32)
    return row_ids, col_ids, linked, fresh, tail, closing


CHUNK = 32
QUIET, MANY = 6, 2
LAG = 2
MESH_ID = pl.DeviceIdType.MESH


class Line:
    def __init__(self, mesh_axes, part, arrived, out, sems, transform, sums=True, backs=True):
        self.mesh_axes = mesh_axes
        self.sums, self.backs = sums, backs
        self.part, self.arrived, self.out = part, arrived, out
        if sums:
            self.sum_send, self.sum_recv = sems[:2]
        if backs:
            self.back_send, self.back_recv = sems[-2:]
        self.transform = transform
        self.half = (part if sums else out).shape[0] // 2
        self.chunks = self.half // CHUNK
        self.size = lax.axis_size("tensor")
        self.place = lax.axis_index("tensor")
        self.lines = ((self.size - 1 - self.place, -1), (self.place, 1))
        self.offset = LAG * (self.size - 1) if sums else 0
        self.steps = self.chunks + self.offset + (LAG * (self.size - 1) if backs else 0)

    def device(self, position):
        return tuple(
            jnp.clip(position, 0, self.size - 1) if axis == "tensor" else lax.axis_index(axis)
            for axis in self.mesh_axes
        )

    def greet(self, barrier):
        for step in (-1, 1):
            inside = jnp.logical_and(self.place + step >= 0, self.place + step < self.size)

            @pl.when(inside)
            def _(step=step):
                pl.semaphore_signal(
                    barrier, inc=1, device_id=self.device(self.place + step), device_id_type=MESH_ID
                )

        at_end = jnp.logical_or(self.place == 0, self.place == self.size - 1)
        return jnp.where(at_end, 1, 2)

    def rows_of(self, side, index):
        return pl.ds(pl.multiple_of(side * self.half + index * CHUNK, CHUNK), CHUNK)

    def sum_copy(self, side, index, source):
        rows = self.rows_of(side, index)
        return pltpu.make_async_remote_copy(
            source.at[rows],
            self.arrived.at[rows],
            self.sum_send.at[side, index],
            self.sum_recv.at[side, index],
            device_id=self.device(self.place + self.lines[side][1]),
            device_id_type=MESH_ID,
        )

    def back_copy(self, side, index):
        rows = self.rows_of(side, index)
        return pltpu.make_async_remote_copy(
            self.out.at[rows],
            self.out.at[rows],
            self.back_send.at[side, index],
            self.back_recv.at[side, index],
            device_id=self.device(self.place - self.lines[side][1]),
            device_id_type=MESH_ID,
        )

    def step(self, time):
        for side in (0, 1):
            hops = self.lines[side][0]
            at_source, at_owner = hops == 0, hops == self.size - 1
            if self.sums:
                self.sum_step(time, side, hops, at_source, at_owner)
            if self.backs:
                self.back_step(time, side, hops, at_owner)

    def sum_step(self, time, side, hops, at_source, at_owner):
        index = time - LAG * hops
        valid = jnp.logical_and(index >= 0, index < self.chunks)
        index = jnp.clip(index, 0, self.chunks - 1)
        rows = self.rows_of(side, index)

        @pl.when(jnp.logical_and(valid, at_source))
        def _():
            self.sum_copy(side, index, self.part).start()

        @pl.when(jnp.logical_and(valid, jnp.logical_not(at_source)))
        def _():
            self.sum_copy(side, index, self.arrived).wait_recv()

        between = jnp.logical_and(jnp.logical_not(at_source), jnp.logical_not(at_owner))

        @pl.when(jnp.logical_and(valid, between))
        def _():
            total = self.part[rows].astype(F32) + self.arrived[rows].astype(F32)
            self.arrived[rows] = total.astype(BF16)
            self.sum_copy(side, index, self.arrived).start()

        @pl.when(jnp.logical_and(valid, at_owner))
        def _():
            total = self.part[rows].astype(F32) + self.arrived[rows].astype(F32)
            self.turn(total, side, index)

    def turn(self, total, side, index):
        own = pl.ds(pl.multiple_of(index * CHUNK, CHUNK), CHUNK)
        self.transform(total, self.rows_of(side, index), own)
        if self.backs:
            self.back_copy(side, index).start()

    def back_step(self, time, side, hops, at_owner):
        if not self.sums:

            @pl.when(jnp.logical_and(at_owner, time < self.chunks))
            def _():
                self.turn(None, side, jnp.clip(time, 0, self.chunks - 1))

        away = self.size - 1 - hops
        index = time - self.offset - LAG * away
        valid = jnp.logical_and(jnp.logical_and(index >= 0, index < self.chunks), away > 0)
        index = jnp.clip(index, 0, self.chunks - 1)

        @pl.when(valid)
        def _():
            self.back_copy(side, index).wait_recv()

        @pl.when(jnp.logical_and(valid, away < self.size - 1))
        def _():
            self.back_copy(side, index).start()

    def run(self, first, last, beside=None):
        def body(time, _):
            self.step(time)
            if beside is not None:
                beside(time)
            return 0

        lax.fori_loop(first, last, body, 0)

    def source_sent(self, first, last):
        def body(index, _):
            for side in (0, 1):

                @pl.when(self.lines[side][0] == 0)
                def _(side=side):
                    self.sum_copy(side, index, self.part).wait_send()

            return 0

        lax.fori_loop(first, last, body, 0)

    def finish(self, source_waits=True):
        def body(index, _):
            for side in (0, 1):
                hops = self.lines[side][0]
                passed = hops < self.size - 1
                if not source_waits:
                    passed = jnp.logical_and(passed, hops > 0)

                if self.sums:

                    @pl.when(passed)
                    def _(side=side):
                        self.sum_copy(side, index, self.arrived).wait_send()

                if self.backs:

                    @pl.when(hops > 0)
                    def _(side=side):
                        self.back_copy(side, index).wait_send()

            return 0

        lax.fori_loop(0, self.chunks, body, 0)


def line_sems(tokens, count=4):
    return [pltpu.SemaphoreType.DMA((2, tokens // 2 // CHUNK))] * count


def inverse_rms(values):
    return lax.rsqrt(jnp.mean(values * values, axis=-1, keepdims=True) + EPSILON)


class Plane:
    def __init__(self, mesh_axes):
        self.mesh_axes = mesh_axes
        self.context = lax.axis_size("context")
        self.per_row = self.context // 2
        self.chips = lax.axis_size("shard") * self.per_row
        context_place = lax.axis_index("context")
        self.core = lax.rem(context_place, 2)
        self.chip = lax.axis_index("shard") * self.per_row + context_place // 2

    def device(self, chip, core):
        places = {
            "shard": chip // self.per_row,
            "context": 2 * lax.rem(chip, self.per_row) + core,
            "tensor": lax.axis_index("tensor"),
        }
        return tuple(places[axis] for axis in self.mesh_axes)

    def ahead(self, distance):
        return lax.rem(self.chip + distance, self.chips)

    def greet(self, barrier):
        targets = [self.device(self.chip, 1 - self.core)]
        targets += [self.device(self.ahead(step), self.core) for step in range(1, self.chips)]
        for target in targets:
            pl.semaphore_signal(barrier, inc=1, device_id=target, device_id_type=MESH_ID)
        return len(targets)


class Gather:
    def __init__(self, plane, sources, targets, sems):
        self.plane, self.sources, self.targets = plane, sources, targets
        self.load_sem, self.send_sem, self.recv_sem, self.pair_send, self.pair_recv = sems
        self.block = sources[0].shape[0]
        self.part = self.block // 2
        self.relayed = plane.chips == 4
        self.arrays = range(len(sources))

    def partner(self, distance):
        return jnp.bitwise_xor(self.plane.chip, distance)

    def greet(self, barrier):
        plane = self.plane
        targets = [plane.device(plane.chip, 1 - plane.core)]
        targets += [
            plane.device(self.partner(step), plane.core)
            for step in range(1, 3 if self.relayed else plane.chips)
        ]
        for target in targets:
            pl.semaphore_signal(barrier, inc=1, device_id=target, device_id_type=MESH_ID)
        return len(targets)

    def place(self, array, chip, core, half):
        first = (2 * chip + core) * self.block + half * self.part
        rows = pl.ds(pl.multiple_of(first, self.part), self.part)
        return self.targets[array].at[rows, pl.ds(0, self.sources[array].shape[1])]

    def mine(self, array, half):
        return self.sources[array].at[pl.ds(half * self.part, self.part)]

    def loads(self):
        plane = self.plane
        return [
            pltpu.make_async_copy(
                self.mine(array, half),
                self.place(array, plane.chip, plane.core, half),
                self.load_sem.at[array, half],
            )
            for array in self.arrays
            for half in range(2)
        ]

    def send(self, distance, half):
        plane = self.plane
        copies = []
        for array in self.arrays:
            chip, target = plane.chip, self.partner(distance)
            source = self.mine(array, half)
            if self.relayed and distance == 3:
                chip = self.partner(2 if half == 0 else 1)
                target = self.partner(1 if half == 0 else 2)
                source = self.place(array, chip, plane.core, half)
            copies.append(
                pltpu.make_async_remote_copy(
                    source,
                    self.place(array, chip, plane.core, half),
                    self.send_sem.at[array, distance - 1, half],
                    self.recv_sem.at[array, distance - 1, half],
                    device_id=plane.device(target, plane.core),
                    device_id_type=MESH_ID,
                )
            )
        return copies

    def forward(self, distance, half):
        plane = self.plane
        copies = []
        for array in self.arrays:
            place = self.place(array, self.partner(distance), plane.core, half)
            copies.append(
                pltpu.make_async_remote_copy(
                    self.mine(array, half) if distance == 0 else place,
                    place,
                    self.pair_send.at[array, distance, half],
                    self.pair_recv.at[array, distance, half],
                    device_id=plane.device(plane.chip, 1 - plane.core),
                    device_id_type=MESH_ID,
                )
            )
        return copies

    def start(self):
        if self.relayed:
            order = ((1, 1), (2, 0), (1, 0), (2, 1))
        else:
            order = [(step, half) for step in range(1, self.plane.chips) for half in range(2)]
        for distance, half in order:
            for copy in self.send(distance, half):
                copy.start()
        for copy in self.loads():
            copy.start()
        for half in range(2):
            for copy in self.forward(0, half):
                copy.start()

    def take(self, distance, half, relay):
        for copy in self.send(distance, half):
            copy.wait_recv()
        if relay:
            for copy in self.send(3, half):
                copy.start()
        for copy in self.forward(distance, half):
            copy.start()

    def stage(self, number):
        if self.relayed:
            if number == 0:
                self.take(1, 1, True)
                self.take(2, 0, True)
            elif number == 1:
                self.take(1, 0, False)
                self.take(2, 1, False)
            else:
                self.take(3, 0, False)
                self.take(3, 1, False)
        elif number == 2:
            for distance in range(1, self.plane.chips):
                for half in range(2):
                    self.take(distance, half, False)

    def arrive_from(self, distance):
        if distance == 0:
            for copy in self.loads():
                copy.wait()
        for half in range(2):
            for copy in self.forward(distance, half):
                copy.wait_recv()

    def arrive(self):
        for distance in range(self.plane.chips):
            self.arrive_from(distance)

    def finish(self):
        for distance in range(self.plane.chips):
            for half in range(2):
                for copy in self.forward(distance, half):
                    copy.wait_send()
                if distance > 0:
                    for copy in self.send(distance, half):
                        copy.wait_send()


def gather_sems(arrays):
    chips = lax.axis_size("shard") * lax.axis_size("context") // 2
    return [
        pltpu.SemaphoreType.DMA((arrays, 2)),
        pltpu.SemaphoreType.DMA((arrays, chips - 1, 2)),
        pltpu.SemaphoreType.DMA((arrays, chips - 1, 2)),
        pltpu.SemaphoreType.DMA((arrays, chips, 2)),
        pltpu.SemaphoreType.DMA((arrays, chips, 2)),
    ]


GROUP = 128
TILE = 256
WIDE = 512


def middle_kernel(
    mesh_axes,
    mix_hbm,
    cotangent_hbm,
    input_hbm,
    gain_ref,
    gate_hbm,
    up_hbm,
    down_hbm,
    out_ref,
    gain_grad,
    residual_hbm,
    hidden_hbm,
    grad_gate_hbm,
    grad_up_hbm,
    feed_hbm,
    grad_hbm,
    grads_hbm,
    normed_ref,
    cotangent_ref,
    gate_w,
    up_w,
    down_w,
    part,
    mix_arrived,
    arrived,
    inputs,
    residual,
    stage_hidden,
    stage_gate,
    stage_up,
    stage_feed,
    part_sem,
    input_sem,
    save_sem,
    stage_sem,
    grad_sem,
    back_sem,
    tile_sem,
    *sems,
):
    tokens, model_width = normed_ref.shape
    half = tokens // 2
    hidden_width = gate_hbm.shape[1]
    padded = gate_w.shape[1]
    groups = half // GROUP
    place, line_size = lax.axis_index("tensor"), lax.axis_size("tensor")
    own_half = pl.ds(pl.multiple_of(jnp.where(place == 0, 0, half), half), half)
    part_load = pltpu.make_async_copy(mix_hbm, part, part_sem.at[0])
    part_load.start()
    input_load = pltpu.make_async_copy(input_hbm.at[own_half], inputs, input_sem.at[0])
    input_load.start()
    cotangent_load = pltpu.make_async_copy(cotangent_hbm, cotangent_ref, input_sem.at[1])
    cotangent_load.start()
    if padded > hidden_width:
        spare = slice(hidden_width, padded)
        gate_w[:, spare] = jnp.zeros((model_width, padded - hidden_width), BF16)
        up_w[:, spare] = jnp.zeros((model_width, padded - hidden_width), BF16)
        down_w[:, spare] = jnp.zeros((model_width, padded - hidden_width), BF16)
    gain_grad[...] = jnp.zeros_like(gain_grad)

    def mix_turn(total, rows, own):
        values = inputs[own].astype(F32) + total
        residual[own] = values
        normed_ref[rows] = (values * inverse_rms(values) * gain_ref[...]).astype(BF16)

    def turn(total, rows, own):
        values = residual[own]
        inverse = inverse_rms(values)
        unit = values * inverse
        gain_grad[...] += jnp.sum(total * unit, axis=0, keepdims=True)
        lifted = total * gain_ref[...]
        mean = jnp.mean(lifted * unit, axis=-1, keepdims=True)
        grad = cotangent_ref[rows].astype(F32) + inverse * (lifted - unit * mean)
        residual[own] = grad
        out_ref[rows] = grad.astype(BF16)

    mix_line = Line(mesh_axes, part, mix_arrived, normed_ref, sems[:4], mix_turn)
    line = Line(mesh_axes, part, arrived, out_ref, sems[4:8], turn)
    gather = Gather(
        Plane(mesh_axes), (gate_hbm, up_hbm, down_hbm), (gate_w, up_w, down_w), sems[8:]
    )
    barrier = pltpu.get_barrier_semaphore()
    expected = mix_line.greet(barrier) + gather.greet(barrier)
    pl.semaphore_wait(barrier, expected)
    gather.start()
    part_load.wait()
    input_load.wait()
    pace = GROUP // CHUNK
    begin = pace + 2 * LAG * (line_size - 1) + 2
    mix_line.run(0, begin - 10)
    gather.stage(0)
    mix_line.run(begin - 10, begin - 4)
    gather.stage(1)
    mix_line.run(begin - 4, begin)
    gather.stage(2)
    gather.arrive()
    cotangent_load.wait()

    def both(ref, group):
        first = pl.ds(pl.multiple_of(group * GROUP, GROUP), GROUP)
        second = pl.ds(pl.multiple_of(half + group * GROUP, GROUP), GROUP)
        return first, second

    def stage_copies(group):
        slot = lax.rem(group, 2)
        copies = []
        for side, rows in enumerate(both(None, group)):
            from_rows = pl.ds(side * GROUP, GROUP)
            columns = pl.ds(0, hidden_width)
            for which, (stage, target) in enumerate(
                (
                    (stage_hidden, hidden_hbm),
                    (stage_gate, grad_gate_hbm),
                    (stage_up, grad_up_hbm),
                )
            ):
                copies.append(
                    pltpu.make_async_copy(
                        stage.at[slot, from_rows, columns],
                        target.at[rows],
                        stage_sem.at[slot, which, side],
                    )
                )
            copies.append(
                pltpu.make_async_copy(
                    stage_feed.at[slot, from_rows], feed_hbm.at[rows], stage_sem.at[slot, 3, side]
                )
            )
        return copies

    def hidden_tile(group, tile):
        first, second = both(normed_ref, group)
        slot = lax.rem(group, 2)
        columns = pl.ds(pl.multiple_of(tile * WIDE, WIDE), WIDE)
        rows = jnp.concatenate([normed_ref[first], normed_ref[second]], axis=0)
        gate = mm_nn(rows, gate_w[:, columns])
        up = mm_nn(rows, up_w[:, columns])
        grads = jnp.concatenate([cotangent_ref[first], cotangent_ref[second]], axis=0)
        grad = mm_nn(grads, down_w[:, columns])
        sigma = jax.nn.sigmoid(gate)
        active = gate * sigma
        stage_hidden[slot, :, columns] = (active * up).astype(BF16)
        stage_gate[slot, :, columns] = (grad * up * sigma * (1.0 + gate * (1.0 - sigma))).astype(
            BF16
        )
        stage_up[slot, :, columns] = (grad * active).astype(BF16)

    def model_tile(group, tile):
        first, second = both(part, group)
        slot = lax.rem(group, 2)
        columns = pl.ds(pl.multiple_of(tile * WIDE, WIDE), WIDE)
        back = mm_nt(stage_gate[slot], gate_w[columns, :])
        back = (back + mm_nt(stage_up[slot], up_w[columns, :])).astype(BF16)
        part[first, columns] = back[:GROUP]
        part[second, columns] = back[GROUP:]
        stage_feed[slot, :, columns] = mm_nt(stage_hidden[slot], down_w[columns, :]).astype(BF16)

    hidden_tiles, model_tiles = padded // WIDE, model_width // WIDE
    ticks = hidden_tiles + model_tiles
    piece = -(-ticks // pace)
    save = pltpu.make_async_copy(residual, residual_hbm, save_sem.at[0])

    def group_body(group, _):
        mix_line.source_sent(group * pace, (group + 1) * pace)

        @pl.when(group == 1)
        def _():
            save.start()

        @pl.when(group == 2)
        def _():
            save.wait()

        @pl.when(group >= 2)
        def _():
            for copy in stage_copies(group - 2):
                copy.wait()

        def piece_body(index, _):
            def tick_body(offset, _):
                tick = index * piece + offset

                @pl.when(tick < hidden_tiles)
                def _():
                    hidden_tile(group, tick)

                @pl.when(jnp.logical_and(tick >= hidden_tiles, tick < ticks))
                def _():
                    model_tile(group, tick - hidden_tiles)

                return 0

            lax.fori_loop(0, piece, tick_body, 0)

            mix_time = begin + group * pace + index

            @pl.when(mix_time < mix_line.steps)
            def _():
                mix_line.step(mix_time)

            @pl.when(group >= 1)
            def _():
                line.step((group - 1) * pace + index)

            return 0

        lax.fori_loop(0, pace, piece_body, 0)
        for copy in stage_copies(group):
            copy.start()
        return 0

    lax.fori_loop(0, groups, group_body, 0)
    for group in range(max(groups - 2, 0), groups):
        for copy in stage_copies(group):
            copy.wait()
    gather.finish()

    token_rows, hidden_columns = pl.ds(0, tokens), pl.ds(0, hidden_width)
    returned = [
        pltpu.make_async_copy(
            source, target.at[token_rows, hidden_columns], back_sem.at[which]
        )
        for which, (source, target) in enumerate(
            ((grad_gate_hbm, gate_w), (grad_up_hbm, up_w), (hidden_hbm, down_w))
        )
    ]
    for copy in returned:
        copy.start()
    tiles = model_width // TILE
    first_time = (groups - 1) * pace + 1
    stages = (stage_gate, stage_up, stage_hidden)

    def tile_copies(tile):
        rows = pl.ds(pl.multiple_of(tile * TILE, TILE), TILE)
        slot = lax.rem(tile, 2)
        return [
            pltpu.make_async_copy(
                stage.at[slot, pl.ds(0, TILE), hidden_columns],
                grads_hbm.at[rows, pl.ds(which * hidden_width, hidden_width)],
                tile_sem.at[slot, which],
            )
            for which, stage in enumerate(stages)
        ]

    def weight_tile(time):
        tile = time - first_time

        @pl.when(tile == 0)
        def _():
            for copy in returned:
                copy.wait()

        @pl.when(jnp.logical_and(tile >= 2, tile < tiles))
        def _():
            for copy in tile_copies(tile - 2):
                copy.wait()

        @pl.when(jnp.logical_and(tile >= 0, tile < tiles))
        def _():
            slot = lax.rem(tile, 2)
            columns = pl.ds(pl.multiple_of(tile * TILE, TILE), TILE)
            rows = normed_ref[:, columns]
            for source, right, stage in (
                (rows, gate_w, stage_gate),
                (rows, up_w, stage_up),
                (cotangent_ref[:, columns], down_w, stage_hidden),
            ):
                product = mm_tn(source, right[:tokens, :hidden_width])
                stage[slot, :TILE, :hidden_width] = product.astype(BF16)
            for copy in tile_copies(tile):
                copy.start()

    line.run((groups - 1) * pace, line.steps, weight_tile)
    grad_save = pltpu.make_async_copy(residual, grad_hbm, grad_sem.at[0])
    grad_save.start()
    for tile in range(max(tiles - 2, 0), tiles):
        for copy in tile_copies(tile):
            copy.wait()
    mix_line.finish(source_waits=False)
    line.finish()
    grad_save.wait()


def middle(mesh_axes, collective, mix, cotangent, inputs, gain, gate_w, up_w, down_w):
    tokens, model_width = mix.shape
    hidden_width = gate_w.shape[1]
    padded = -(-hidden_width // WIDE) * WIDE
    whole = pl.BlockSpec(memory_space=pltpu.VMEM)
    remote = pl.BlockSpec(memory_space=pl.ANY)
    group_rows = 2 * GROUP
    return pl.pallas_call(
        partial(middle_kernel, mesh_axes),
        in_specs=[remote, remote, remote, whole, remote, remote, remote],
        out_specs=[whole, whole] + [remote] * 7,
        out_shape=[
            jax.ShapeDtypeStruct((tokens, model_width), BF16),
            jax.ShapeDtypeStruct((1, model_width), F32),
            jax.ShapeDtypeStruct((tokens // 2, model_width), F32),
            jax.ShapeDtypeStruct((tokens, hidden_width), BF16),
            jax.ShapeDtypeStruct((tokens, hidden_width), BF16),
            jax.ShapeDtypeStruct((tokens, hidden_width), BF16),
            jax.ShapeDtypeStruct((tokens, model_width), BF16),
            jax.ShapeDtypeStruct((tokens // 2, model_width), F32),
            jax.ShapeDtypeStruct((model_width, 3 * hidden_width), BF16),
        ],
        scratch_shapes=[
            pltpu.VMEM((tokens, model_width), BF16),
            pltpu.VMEM((tokens, model_width), BF16),
            pltpu.VMEM((model_width, padded), BF16),
            pltpu.VMEM((model_width, padded), BF16),
            pltpu.VMEM((model_width, padded), BF16),
            pltpu.VMEM((tokens, model_width), BF16),
            pltpu.VMEM((tokens, model_width), BF16),
            pltpu.VMEM((tokens, model_width), BF16),
            pltpu.VMEM((tokens // 2, model_width), BF16),
            pltpu.VMEM((tokens // 2, model_width), F32),
            pltpu.VMEM((2, group_rows, padded), BF16),
            pltpu.VMEM((2, group_rows, padded), BF16),
            pltpu.VMEM((2, group_rows, padded), BF16),
            pltpu.VMEM((2, group_rows, model_width), BF16),
            pltpu.SemaphoreType.DMA((1,)),
            pltpu.SemaphoreType.DMA((2,)),
            pltpu.SemaphoreType.DMA((1,)),
            pltpu.SemaphoreType.DMA((2, 4, 2)),
            pltpu.SemaphoreType.DMA((1,)),
            pltpu.SemaphoreType.DMA((3,)),
            pltpu.SemaphoreType.DMA((2, 3)),
        ]
        + line_sems(tokens)
        + line_sems(tokens)
        + gather_sems(3),
        compiler_params=pltpu.CompilerParams(
            collective_id=collective, has_side_effects=True, vmem_limit_bytes=61 << 20
        ),
        cost_estimate=pl.CostEstimate(
            flops=tokens * model_width * hidden_width * 12,
            bytes_accessed=360_000_000,
            transcendentals=tokens * hidden_width,
        ),
        name="middle",
    )(mix, cotangent, inputs, gain, gate_w, up_w, down_w)


def output_kernel(
    mesh_axes,
    head_count,
    key_scale,
    run_ref,
    carry_ref,
    decay_ref,
    link_ref,
    open_ref,
    count_ref,
    keep_ref,
    flags_ref,
    gain_ref,
    part_hbm,
    residual_hbm,
    gated_hbm,
    mix_grad_hbm,
    out_full_hbm,
    lead_hbm,
    starts_hbm,
    normed_hbm,
    pre_hbm,
    full_hbm,
    mixed_hbm,
    out_ref,
    gain_grad,
    floor_grad,
    total_ref,
    mixer_grads_hbm,
    part,
    residual,
    gated_ref,
    mix_grad_ref,
    out_full,
    lead_ref,
    starts_ref,
    arrived,
    back,
    back_arrived,
    left,
    right,
    full,
    mixer_stage,
    piece_rows_scr,
    pre,
    grad_mixed,
    back_scr,
    message,
    received,
    grad_scr,
    lifted_scr,
    lowered_scr,
    moved_scr,
    value_scr,
    load_sem,
    piece_sem,
    full_sem,
    pre_sem,
    stage_sem,
    grad_send,
    grad_recv,
    *sems,
):
    tokens, model_width = left.shape
    width = gated_hbm.shape[1]
    lanes = width // head_count
    state_rows = head_count * lanes
    tiles, blocks = model_width // TILE, tokens // BLOCK
    piece_rows = 2 * BLOCK
    context, context_size = lax.axis_index("context"), lax.axis_size("context")

    loads = [
        pltpu.make_async_copy(source, target, load_sem.at[which])
        for which, (source, target) in enumerate(
            (
                (part_hbm, part),
                (out_full_hbm, out_full),
                (mix_grad_hbm, mix_grad_ref),
                (lead_hbm, lead_ref),
                (residual_hbm, residual),
                (starts_hbm, starts_ref),
                (gated_hbm, gated_ref),
                (normed_hbm, left),
            )
        )
    ]
    part_load, *gate_loads = loads[:5]
    starts_load, *tile_loads = loads[5:]
    for load in loads:
        load.start()

    def piece_loads(index):
        rows = pl.ds(pl.multiple_of(index * piece_rows, piece_rows), piece_rows)
        slot = lax.rem(index, 2)
        return (
            pltpu.make_async_copy(
                pre_hbm.at[rows, pl.ds(3 * width, width)],
                piece_rows_scr.at[slot, 0],
                piece_sem.at[slot, 0],
            ),
            pltpu.make_async_copy(
                mixed_hbm.at[rows], piece_rows_scr.at[slot, 1], piece_sem.at[slot, 1]
            ),
        )

    for load in piece_loads(0):
        load.start()
    gain_grad[...] = jnp.zeros_like(gain_grad)
    floor_grad[...] = jnp.zeros_like(floor_grad)
    back_scr[...] = jnp.zeros_like(back_scr)

    def turn(total, rows, own):
        out_ref[rows] = (residual[own] + total).astype(BF16)

    def earlier(shift):
        places = {axis: lax.axis_index(axis) for axis in mesh_axes}
        places["context"] = lax.rem(context + context_size - shift, context_size)
        return tuple(places[axis] for axis in mesh_axes)

    def keep_total(total, rows, own):
        total_ref[own] = total

    line = Line(mesh_axes, part, arrived, out_ref, sems[:4], turn)
    back_line = Line(mesh_axes, back, back_arrived, None, sems[4:], keep_total, backs=False)
    barrier = pltpu.get_barrier_semaphore()
    expected = line.greet(barrier)
    for shift in range(1, context_size):
        pl.semaphore_signal(barrier, inc=1, device_id=earlier(shift), device_id_type=MESH_ID)
    pl.semaphore_wait(barrier, expected + context_size - 1)

    def tile_columns(tile):
        return pl.ds(pl.multiple_of(tile * TILE, TILE), TILE)

    def stage_copy(tile):
        rows = tile_columns(tile)
        return pltpu.make_async_copy(mixer_stage, mixer_grads_hbm.at[rows], stage_sem.at[0])

    def gate_piece(index):
        rows = pl.ds(pl.multiple_of(index * piece_rows, piece_rows), piece_rows)
        slot = lax.rem(index, 2)

        @pl.when(index + 1 < tokens // piece_rows)
        def _():
            for load in piece_loads(index + 1):
                load.start()

        for load in piece_loads(index):
            load.wait()
        grads = mm_nn(mix_grad_ref[rows], out_full[...])
        gain = gain_ref[...]
        total = jnp.zeros_like(gain)
        for head in range(head_count):
            part_of = slice(head * lanes, (head + 1) * lanes)
            gate, mixed = piece_rows_scr[slot, 0, :, part_of], piece_rows_scr[slot, 1, :, part_of]
            grad = grads[:, part_of]
            inverse = inverse_rms(mixed)
            unit = mixed * inverse
            sigma = jax.nn.sigmoid(gate)
            scaled = grad * unit
            total = total + jnp.sum(scaled * (gate * sigma), axis=0, keepdims=True)
            grad_gate = scaled * gain * sigma * (1.0 + gate * (1.0 - sigma))
            first = 3 * width + head * lanes
            right[rows, first : first + lanes] = grad_gate.astype(BF16)
            lifted = grad * gain * (gate * sigma)
            mean = jnp.mean(lifted * unit, axis=-1, keepdims=True)
            grad_in = inverse * (lifted - unit * mean) * (key_scale * keep_ref[rows])
            grad_in = grad_in.astype(BF16)
            grad_mixed[rows, part_of] = grad_in
            back_scr[head] += mm_tn(grad_in, lead_ref[rows, part_of])
        gain_grad[...] += total

    def state_copy(shift):
        return pltpu.make_async_remote_copy(
            message,
            received.at[shift - 1],
            grad_send.at[shift - 1],
            grad_recv.at[shift - 1],
            device_id=earlier(shift),
            device_id_type=MESH_ID,
        )

    def block_of(index):
        return blocks - 1 - index

    def pre_load(index):
        rows = pl.ds(pl.multiple_of(block_of(index) * BLOCK, BLOCK), BLOCK)
        slot = lax.rem(index, 2)
        return pltpu.make_async_copy(
            pre_hbm.at[rows, pl.ds(0, 3 * width)], pre.at[slot], pre_sem.at[slot]
        )

    def send_back():
        for head in range(head_count):
            rows = slice(head * lanes, (head + 1) * lanes)
            message[rows] = back_scr[head] * link_ref[0:1]
            message[state_rows + head : state_rows + head + 1] = decay_ref[head] * link_ref[0:1]
        for shift in range(1, context_size):

            @pl.when(context >= shift)
            def _(shift=shift):
                state_copy(shift).start()

        pre_load(0).start()

    def take_back():
        grad_scr[...] = jnp.zeros_like(grad_scr)
        for shift in range(1, context_size):

            @pl.when(context + shift < context_size)
            def _(shift=shift):
                state_copy(shift).wait_recv()
                for head in range(head_count):
                    value = received[shift - 1, head * lanes : (head + 1) * lanes]
                    for near in range(shift - 1):
                        value = value * received[near, state_rows + head : state_rows + head + 1]
                    grad_scr[head] += value

        for shift in range(1, context_size):

            @pl.when(context >= shift)
            def _(shift=shift):
                state_copy(shift).wait_send()

    def mixer_block(index):
        block = block_of(index)
        slot = lax.rem(index, 2)
        block_rows = pl.ds(pl.multiple_of(block * BLOCK, BLOCK), BLOCK)

        @pl.when(index + 1 < blocks)
        def _():
            pre_load(index + 1).start()

        pre_load(index).wait()
        counts, keep, flags = count_ref[block_rows], keep_ref[block_rows], flags_ref[block]
        row_ids, col_ids, linked, fresh, tail, closing = block_masks(counts, flags)
        tri = (row_ids >= col_ids).astype(BF16)
        tri_back = (row_ids <= col_ids).astype(BF16)
        query_pre = pre[slot, :, :width]
        values = pre[slot, :, 2 * width : 3 * width].astype(BF16)
        opened = open_ref[...]
        closed = jax.nn.sigmoid(-pre[slot, :, width : 2 * width])
        keys = opened * closed
        cum = split_sum(tri, jnp.log1p(-keys))
        ending = cum[BLOCK - 1 : BLOCK, :]
        rise, fall = jnp.exp(cum), jnp.exp(-cum) * keep
        shift = jnp.exp(ending - cum) * (keep * tail)
        sigma_query = jax.nn.sigmoid(query_pre)
        lifted = (query_pre * sigma_query * rise).astype(BF16)
        lowered = (keys * fall).astype(BF16)
        moved = (keys * shift).astype(BF16)
        fresh_lifted = (lifted.astype(F32) * fresh).astype(BF16)
        end_decay = jnp.exp(ending) * closing
        lead_in = jnp.exp(run_ref[block]) * (flags[1:2, 0:1] == 0).astype(F32)
        for head in range(head_count):
            part_of = slice(head * lanes, (head + 1) * lanes)
            grad_out, value = grad_mixed[block_rows, part_of], values[:, part_of]
            lift, lower, move = lifted[:, part_of], lowered[:, part_of], moved[:, part_of]
            scores = jnp.where(linked, mm_nt(lift, lower), 0.0).astype(BF16)
            pulls = jnp.where(linked, mm_nt(grad_out, value), 0.0).astype(BF16)
            state = starts_ref[block, head] + lead_in[:, part_of] * carry_ref[head]
            grad_state = grad_scr[head]
            grad_low = grad_state.astype(BF16)
            lifted_scr[:, part_of] = mm_nn(pulls, lower) + fresh * mm_nn(
                grad_out, state.astype(BF16)
            )
            lowered_scr[:, part_of] = mm_tn(pulls, lift)
            grad_moved = mm_nn(value, grad_low)
            moved_scr[:, part_of] = grad_moved
            first = 2 * width + head * lanes
            right[block_rows, first : first + lanes] = (
                mm_tn(scores, grad_out) + mm_nt(move, grad_low)
            ).astype(BF16)
            value_scr[:, part_of] = jnp.sum(
                grad_moved * move.astype(F32), axis=0, keepdims=True
            ) + end_decay[:, part_of] * jnp.sum(state * grad_state, axis=0, keepdims=True)
            grad_scr[head] = grad_state * end_decay[:, part_of] + mm_tn(
                grad_out, fresh_lifted[:, part_of]
            )
        grad_lifted, grad_lowered, grad_moved = lifted_scr[...], lowered_scr[...], moved_scr[...]
        grad_cum = (
            grad_lifted * lifted.astype(F32)
            - grad_lowered * lowered.astype(F32)
            - grad_moved * moved.astype(F32)
        )
        grad_decay = split_sum(tri_back, grad_cum) + value_scr[...]
        key_total = grad_lowered * fall + grad_moved * shift - grad_decay / (1.0 - keys)
        floor_grad[...] -= jnp.sum(key_total * closed, axis=0, keepdims=True)
        right[block_rows, :width] = (
            grad_lifted * rise * sigma_query * (1.0 + query_pre * (1.0 - sigma_query))
        ).astype(BF16)
        right[block_rows, width : 2 * width] = (
            -key_total * opened * closed * (1.0 - closed)
        ).astype(BF16)

    def full_load(tile):
        slot = lax.rem(tile, 2)
        return pltpu.make_async_copy(
            full_hbm.at[tile_columns(tile)], full.at[slot], full_sem.at[slot]
        )

    def back_tile(tile):
        @pl.when(tile + 1 < tiles)
        def _():
            full_load(tile + 1).start()

        full_load(tile).wait()
        product = mm_nt(right[...], full[lax.rem(tile, 2)])
        back[:, tile_columns(tile)] = product.astype(BF16)

    def mixer_tile(tile):
        @pl.when(tile > 0)
        def _():
            stage_copy(tile - 1).wait()

        columns = tile_columns(tile)
        rows = left[:, columns]
        for first in range(0, 4 * width, 1024):
            some = slice(first, min(first + 1024, 4 * width))
            mixer_stage[:, some] = mm_tn(rows, right[:, some]).astype(BF16)
        product = mm_tn(mix_grad_ref[:, columns], gated_ref[...])
        mixer_stage[:, 4 * width :] = product.astype(BF16)
        stage_copy(tile).start()

    send_time = tokens // piece_rows
    block_time = send_time + 2
    back_time = block_time + blocks
    tile_time = back_time + tiles
    end_time = tile_time + tiles

    def piece(time):
        @pl.when(time == 0)
        def _():
            for load in gate_loads:
                load.wait()

        @pl.when(time < send_time)
        def _():
            gate_piece(time)

        @pl.when(time == send_time)
        def _():
            send_back()

        @pl.when(time == block_time)
        def _():
            starts_load.wait()
            take_back()

        @pl.when(jnp.logical_and(time >= block_time, time < back_time))
        def _():
            mixer_block(time - block_time)

        @pl.when(time == back_time - 1)
        def _():
            full_load(0).start()

        @pl.when(jnp.logical_and(time >= back_time, time < tile_time))
        def _():
            back_tile(time - back_time)

        @pl.when(time == tile_time)
        def _():
            for load in tile_loads:
                load.wait()

        @pl.when(jnp.logical_and(time >= tile_time, time < end_time))
        def _():
            mixer_tile(time - tile_time)

    slow = QUIET
    part_load.wait()
    begin = slow + -(-(tile_time - slow) // MANY)
    steps = max(line.steps, begin + back_line.steps, slow + -(-(end_time - slow) // MANY))

    def body(time, _):
        @pl.when(time < line.steps)
        def _():
            line.step(time)

        @pl.when(time >= begin)
        def _():
            back_line.step(time - begin)

        def pieces(index, _):
            piece(index)
            return 0

        first = jnp.where(time < slow, time, slow + MANY * (time - slow))
        lax.fori_loop(first, first + jnp.where(time < slow, 1, MANY), pieces, 0)
        return 0

    lax.fori_loop(0, steps, body, 0)
    stage_copy(tiles - 1).wait()
    line.finish()
    back_line.finish()


def output_line(mesh_axes, collective, in_vmem, in_hbm, head_count):
    part, residual, gated, mix_grad, out_full, lead, starts = in_hbm[:7]
    tokens, model_width = part.shape
    width = gated.shape[1]
    lanes = width // head_count
    context_size = lax.axis_size("context")
    messages = head_count * lanes + -(-head_count // 8) * 8
    whole = pl.BlockSpec(memory_space=pltpu.VMEM)
    remote = pl.BlockSpec(memory_space=pl.ANY)
    return pl.pallas_call(
        partial(output_kernel, mesh_axes, head_count, lanes ** (-0.5)),
        in_specs=[whole] * len(in_vmem) + [remote] * len(in_hbm),
        out_specs=[whole] * 4 + [remote],
        out_shape=[
            jax.ShapeDtypeStruct((tokens, model_width), BF16),
            jax.ShapeDtypeStruct((1, lanes), F32),
            jax.ShapeDtypeStruct((1, width), F32),
            jax.ShapeDtypeStruct((tokens // 2, model_width), F32),
            jax.ShapeDtypeStruct((model_width, 5 * width), BF16),
        ],
        scratch_shapes=[
            pltpu.VMEM(array.shape, array.dtype)
            for array in (part, residual, gated, mix_grad, out_full, lead, starts)
        ]
        + [
            pltpu.VMEM((tokens, model_width), BF16),
            pltpu.VMEM((tokens, model_width), BF16),
            pltpu.VMEM((tokens, model_width), BF16),
            pltpu.VMEM((tokens, model_width), BF16),
            pltpu.VMEM((tokens, 4 * width), BF16),
            pltpu.VMEM((2, TILE, 4 * width), BF16),
            pltpu.VMEM((TILE, 5 * width), BF16),
            pltpu.VMEM((2, 2, 2 * BLOCK, width), F32),
            pltpu.VMEM((2, BLOCK, 3 * width), F32),
            pltpu.VMEM((tokens, width), BF16),
            pltpu.VMEM((head_count, lanes, lanes), F32),
            pltpu.VMEM((messages, lanes), F32),
            pltpu.VMEM((context_size - 1, messages, lanes), F32),
            pltpu.VMEM((head_count, lanes, lanes), F32),
            pltpu.VMEM((BLOCK, width), F32),
            pltpu.VMEM((BLOCK, width), F32),
            pltpu.VMEM((BLOCK, width), F32),
            pltpu.VMEM((1, width), F32),
            pltpu.SemaphoreType.DMA((8,)),
            pltpu.SemaphoreType.DMA((2, 2)),
            pltpu.SemaphoreType.DMA((2,)),
            pltpu.SemaphoreType.DMA((2,)),
            pltpu.SemaphoreType.DMA((1,)),
            pltpu.SemaphoreType.DMA((context_size - 1,)),
            pltpu.SemaphoreType.DMA((context_size - 1,)),
        ]
        + line_sems(tokens)
        + line_sems(tokens, 2),
        compiler_params=pltpu.CompilerParams(
            collective_id=collective, has_side_effects=True, vmem_limit_bytes=61 << 20
        ),
        cost_estimate=pl.CostEstimate(
            flops=tokens * model_width * width * 24,
            bytes_accessed=360_000_000,
            transcendentals=tokens * width * 12,
        ),
        name="output_line",
    )(*in_vmem, *in_hbm)


class SmallSum:
    def __init__(self, mesh_axes, value, local, total, near, far, sems):
        self.mesh_axes = mesh_axes
        self.value, self.local, self.total, self.near, self.far = value, local, total, near, far
        self.near_send, self.near_recv, self.far_send, self.far_recv = sems
        self.context_size = lax.axis_size("context")
        self.group = lax.axis_size("shard") * self.context_size
        self.line_size = lax.axis_size("tensor")
        self.place = lax.axis_index("shard") * self.context_size + lax.axis_index("context")
        self.line_place = lax.axis_index("tensor")

    def device(self, position, line_position):
        places = {
            "shard": position // self.context_size,
            "context": lax.rem(position, self.context_size),
            "tensor": line_position,
        }
        return tuple(places[axis] for axis in self.mesh_axes)

    def near_target(self, step):
        return self.device(lax.rem(self.place + step, self.group), self.line_place)

    def far_target(self, step):
        return self.device(self.place, lax.rem(self.line_place + step, self.line_size))

    def near_copy(self, step):
        return pltpu.make_async_remote_copy(
            self.value,
            self.near.at[step - 1],
            self.near_send.at[step - 1],
            self.near_recv.at[step - 1],
            device_id=self.near_target(step),
            device_id_type=MESH_ID,
        )

    def far_copy(self, step):
        return pltpu.make_async_remote_copy(
            self.local,
            self.far.at[step - 1],
            self.far_send.at[step - 1],
            self.far_recv.at[step - 1],
            device_id=self.far_target(step),
            device_id_type=MESH_ID,
        )

    def greet(self, barrier):
        targets = [self.near_target(step) for step in range(1, self.group)]
        targets += [self.far_target(step) for step in range(1, self.line_size)]
        for target in targets:
            pl.semaphore_signal(barrier, inc=1, device_id=target, device_id_type=MESH_ID)
        return len(targets)

    def start(self):
        for step in range(1, self.group):
            self.near_copy(step).start()

    def pass_on(self):
        total = self.value[...]
        for step in range(1, self.group):
            self.near_copy(step).wait_recv()
            total = total + self.near[step - 1]
        self.local[...] = total
        for step in range(1, self.line_size):
            self.far_copy(step).start()

    def finish(self):
        total = self.local[...]
        for step in range(1, self.line_size):
            self.far_copy(step).wait_recv()
            total = total + self.far[step - 1]
        self.total[...] = total
        for step in range(1, self.group):
            self.near_copy(step).wait_send()
        for step in range(1, self.line_size):
            self.far_copy(step).wait_send()


def input_kernel(
    mesh_axes,
    gain_ref,
    norm_two_ref,
    head_ref,
    floor_ref,
    total_hbm,
    hidden_hbm,
    residual_hbm,
    grads_hbm,
    out_ref,
    small_local,
    small_total,
    share_query,
    share_forget,
    share_input,
    share_gate,
    share_out,
    total_ref,
    hidden_ref,
    residual_grad,
    own,
    other,
    remote,
    gain_grad,
    small,
    small_near,
    small_far,
    quarter_sem,
    load_sem,
    pair_send,
    pair_recv,
    chip_send,
    chip_recv,
    *sems,
):
    plane = Plane(mesh_axes)
    chips = plane.chips
    block = own.shape[1]
    gain_grad[...] = jnp.zeros_like(gain_grad)
    half, line_size = total_ref.shape[0], lax.axis_size("tensor")
    place = lax.axis_index("tensor")
    at_end = jnp.logical_or(place == 0, place == line_size - 1)
    first_row = jnp.where(place == 0, 0, half)
    quarters = 4
    length = half // quarters

    def quarter_loads(index):
        rows = pl.ds(pl.multiple_of(index * length, length), length)
        inputs = pl.ds(pl.multiple_of(first_row + index * length, length), length)
        return [
            pltpu.make_async_copy(source, target.at[rows], quarter_sem.at[which, index])
            for which, (source, target) in enumerate(
                (
                    (total_hbm.at[rows], total_ref),
                    (hidden_hbm.at[inputs], hidden_ref),
                    (residual_hbm.at[rows], residual_grad),
                )
            )
        ]

    @pl.when(at_end)
    def _():
        for index in range(quarters):
            for load in quarter_loads(index):
                load.start()

    def turn(total, rows, own_rows):
        total = total_ref[own_rows]
        values = hidden_ref[own_rows].astype(F32)
        inverse = inverse_rms(values)
        unit = values * inverse
        gain_grad[...] += jnp.sum(total * unit, axis=0, keepdims=True)
        lifted = total * gain_ref[...]
        mean = jnp.mean(lifted * unit, axis=-1, keepdims=True)
        grad = residual_grad[own_rows] + inverse * (lifted - unit * mean)
        out_ref[rows] = grad.astype(BF16)

    line = Line(mesh_axes, None, None, out_ref, sems[:2], turn, sums=False)
    small_sum = SmallSum(
        mesh_axes, small, small_local, small_total, small_near, small_far, sems[2:]
    )
    barrier = pltpu.get_barrier_semaphore()
    expected = line.greet(barrier) + plane.greet(barrier) + small_sum.greet(barrier)
    pl.semaphore_wait(barrier, expected)

    def rows_of(slot, core):
        return pl.ds(pl.multiple_of((2 * plane.ahead(slot) + core) * block, block), block)

    def load(slot):
        return pltpu.make_async_copy(
            grads_hbm.at[rows_of(slot, plane.core)], own.at[slot], load_sem.at[slot]
        )

    def pair_copy(slot):
        return pltpu.make_async_remote_copy(
            grads_hbm.at[rows_of(slot, 1 - plane.core)],
            other.at[slot],
            pair_send.at[slot],
            pair_recv.at[slot],
            device_id=plane.device(plane.chip, 1 - plane.core),
            device_id_type=MESH_ID,
        )

    def chip_copy(slot):
        return pltpu.make_async_remote_copy(
            own.at[slot],
            remote.at[slot - 1],
            chip_send.at[slot - 1],
            chip_recv.at[slot - 1],
            device_id=plane.device(plane.ahead(slot), plane.core),
            device_id_type=MESH_ID,
        )

    def start(index, _):
        slot = lax.rem(index + 1, chips)
        pair_copy(slot).start()
        load(slot).start()
        return 0

    lax.fori_loop(0, chips, start, 0)
    strip = 32

    def combine(time):
        slot = lax.rem(jnp.clip(time, 0, chips - 1) + 1, chips)

        @pl.when(time < chips)
        def _():
            load(slot).wait()
            pair_copy(slot).wait_recv()

            def add(index, _):
                rows = pl.ds(pl.multiple_of(index * strip, strip), strip)
                total = own[slot, rows].astype(F32) + other[slot, rows].astype(F32)
                own[slot, rows] = total.astype(BF16)
                return 0

            lax.fori_loop(0, block // strip, add, 0)

        @pl.when(time < chips - 1)
        def _():
            chip_copy(slot).start()

    def step(time, _):
        index = time * CHUNK // length
        fresh = jnp.logical_and(lax.rem(time * CHUNK, length) == 0, index < quarters)

        @pl.when(jnp.logical_and(at_end, fresh))
        def _():
            for load in quarter_loads(index):
                load.wait()

        line.step(time)
        combine(time)
        return 0

    lax.fori_loop(0, line.steps, step, 0)
    small[...] = jnp.zeros_like(small)
    row = 0
    for ref in (gain_grad, norm_two_ref, head_ref, floor_ref):
        for first in range(0, ref.shape[1], 128):
            small[row : row + 1] = ref[:, first : first + 128]
            row += 1
    small_sum.start()

    def arrive(index, _):
        chip_copy(index).wait_recv()
        return 0

    lax.fori_loop(1, chips, arrive, 0)

    def total(index, _):
        rows = pl.ds(pl.multiple_of(index * strip, strip), strip)

        for which, share in enumerate(
            (share_query, share_forget, share_input, share_gate, share_out)
        ):
            columns = pl.ds(which * share.shape[1], share.shape[1])

            def add(slot, value, columns=columns):
                return value + remote[slot, rows, columns].astype(F32)

            share[rows] = lax.fori_loop(0, chips - 1, add, own[0, rows, columns].astype(F32))
        return 0

    small_sum.pass_on()
    lax.fori_loop(0, block // strip, total, 0)
    small_sum.finish()

    def sent(index, _):
        pair_copy(index).wait_send()
        return 0

    lax.fori_loop(0, chips, sent, 0)

    def chip_sent(index, _):
        chip_copy(index).wait_send()
        return 0

    lax.fori_loop(1, chips, chip_sent, 0)
    line.finish()


def input_line(mesh_axes, collective, total, hidden, residual_grad, gain, grads, small):
    tokens, model_width = hidden.shape
    all_width = grads.shape[1]
    chips = lax.axis_size("shard") * lax.axis_size("context") // 2
    block = model_width // (2 * chips)
    values = model_width + sum(value.shape[1] for value in small)
    small_shape = (-(-values // 1024) * 8, 128)
    group, line_size = 2 * chips, lax.axis_size("tensor")
    whole = pl.BlockSpec(memory_space=pltpu.VMEM)
    return pl.pallas_call(
        partial(input_kernel, mesh_axes),
        in_specs=[whole] * 4 + [pl.BlockSpec(memory_space=pl.ANY)] * 4,
        out_specs=[whole] * 8,
        out_shape=[
            jax.ShapeDtypeStruct((tokens, model_width), BF16),
            jax.ShapeDtypeStruct(small_shape, F32),
            jax.ShapeDtypeStruct(small_shape, F32),
        ]
        + [jax.ShapeDtypeStruct((block, all_width // 5), F32)] * 5,
        scratch_shapes=[
            pltpu.VMEM((tokens // 2, model_width), F32),
            pltpu.VMEM((tokens // 2, model_width), BF16),
            pltpu.VMEM((tokens // 2, model_width), F32),
            pltpu.VMEM((chips, block, all_width), BF16),
            pltpu.VMEM((chips, block, all_width), BF16),
            pltpu.VMEM((chips - 1, block, all_width), BF16),
            pltpu.VMEM((1, model_width), F32),
            pltpu.VMEM(small_shape, F32),
            pltpu.VMEM((group - 1, *small_shape), F32),
            pltpu.VMEM((line_size - 1, *small_shape), F32),
            pltpu.SemaphoreType.DMA((3, 4)),
            pltpu.SemaphoreType.DMA((chips,)),
            pltpu.SemaphoreType.DMA((chips,)),
            pltpu.SemaphoreType.DMA((chips,)),
            pltpu.SemaphoreType.DMA((chips - 1,)),
            pltpu.SemaphoreType.DMA((chips - 1,)),
        ]
        + line_sems(tokens, 2)
        + [
            pltpu.SemaphoreType.DMA((group - 1,)),
            pltpu.SemaphoreType.DMA((group - 1,)),
            pltpu.SemaphoreType.DMA((line_size - 1,)),
            pltpu.SemaphoreType.DMA((line_size - 1,)),
        ],
        compiler_params=pltpu.CompilerParams(
            collective_id=collective, has_side_effects=True, vmem_limit_bytes=58 << 20
        ),
        cost_estimate=pl.CostEstimate(
            flops=tokens * model_width * 8, bytes_accessed=360_000_000, transcendentals=0
        ),
        name="input_line",
    )(gain, *small, total, hidden, residual_grad, grads)


def forward_kernel(
    mesh_axes,
    head_count,
    key_scale,
    hidden_ref,
    gain_ref,
    query_hbm,
    forget_hbm,
    input_hbm,
    gate_hbm,
    out_shard_ref,
    down_shard_ref,
    floor_ref,
    segments_ref,
    head_gain_ref,
    normed_hbm,
    pre_hbm,
    full_hbm,
    out_full_hbm,
    mixed_hbm,
    lead_hbm,
    start_hbm,
    gated_hbm,
    mix_hbm,
    down_turned,
    open_ref,
    count_ref,
    keep_ref,
    flags_ref,
    run_ref,
    carry_ref,
    decay_ref,
    link_ref,
    normed,
    pre,
    mine,
    out_turned,
    full,
    out_full,
    mixed,
    lead,
    starts,
    gated,
    mix,
    state_scr,
    run_scr,
    message,
    received,
    mine_sem,
    full_sem,
    save_sem,
    pre_sem,
    mix_sem,
    state_send,
    state_recv,
    *sems,
):
    plane = Plane(mesh_axes)
    chips = plane.chips
    tokens, model_width = hidden_ref.shape
    block, width = query_hbm.shape
    lanes = width // head_count
    state_rows = head_count * lanes
    context, context_size = lax.axis_index("context"), lax.axis_size("context")

    mine_loads = [
        pltpu.make_async_copy(
            ref, mine.at[:, pl.ds(which * width, width)], mine_sem.at[which]
        )
        for which, ref in enumerate((query_hbm, forget_hbm, input_hbm, gate_hbm))
    ]
    for load in mine_loads:
        load.start()
    gather = Gather(plane, (mine,), (full,), sems[:5])
    out_gather = Gather(plane, (out_turned,), (out_full,), sems[5:])

    def later(shift):
        places = {axis: lax.axis_index(axis) for axis in mesh_axes}
        places["context"] = lax.rem(context + shift, context_size)
        return tuple(places[axis] for axis in mesh_axes)

    out_turned[...] = out_shard_ref[...].T
    barrier = pltpu.get_barrier_semaphore()
    expected = gather.greet(barrier)
    for shift in range(1, context_size):
        pl.semaphore_signal(barrier, inc=1, device_id=later(shift), device_id_type=MESH_ID)
    pl.semaphore_wait(barrier, expected + context_size - 1)
    for load in mine_loads:
        load.wait()
    gather.start()
    out_gather.start()
    down_turned[...] = down_shard_ref[...].T
    for head in range(head_count):
        open_ref[:, head * lanes : (head + 1) * lanes] = 1.0 - floor_ref[head : head + 1]

    segments = segments_ref[...]
    blocks = segments.shape[0]
    block_ids = lax.broadcasted_iota(jnp.int32, segments.shape, 0)
    slot_ids = lax.broadcasted_iota(jnp.int32, segments.shape, 1)
    before = pltpu.roll(segments, 1, 1)
    wrapped = pltpu.roll(before, 1, 0)
    before = jnp.where(slot_ids == 0, wrapped, before)
    first_slot = jnp.logical_and(slot_ids == 0, block_ids == 0)
    begins = jnp.where(jnp.logical_or(first_slot, segments == before), 0.0, 1.0)
    wide_rows = lax.broadcasted_iota(jnp.int32, (BLOCK, BLOCK), 0)
    wide_columns = lax.broadcasted_iota(jnp.int32, (BLOCK, BLOCK), 1)
    within = mm_nn(begins.astype(BF16), (wide_rows <= wide_columns).astype(BF16))
    count_rows = []
    running = jnp.zeros((1, 1), F32)
    flags_ref[...] = jnp.zeros_like(flags_ref)
    for index in range(blocks):
        row = within[index : index + 1] + running
        flags_ref[index, 0:1] = row
        flags_ref[index, 1:2] = jnp.broadcast_to(running, (1, BLOCK))
        running = row[:, BLOCK - 1 : BLOCK]
        flags_ref[index, 2:3] = jnp.broadcast_to(running, (1, BLOCK))
        count_rows.append(row)
    turned_counts = jnp.concatenate(count_rows, axis=0).T
    turned_keep = (segments > 0).astype(F32).T
    for index in range(blocks):
        rows = slice(index * BLOCK, (index + 1) * BLOCK)
        count_ref[rows] = turned_counts[:, index : index + 1]
        keep_ref[rows] = turned_keep[:, index : index + 1]
    first_id = jnp.broadcast_to(segments[0:1, 0:1], (1, lanes))
    last_id = jnp.broadcast_to(segments[blocks - 1 : blocks, BLOCK - 1 : BLOCK], (1, lanes))

    def norm(index, _):
        rows = pl.ds(pl.multiple_of(index * 128, 128), 128)
        values = hidden_ref[rows].astype(F32)
        normed[rows] = (values * inverse_rms(values) * gain_ref[...]).astype(BF16)
        return 0

    lax.fori_loop(0, tokens // 128, norm, 0)

    saves = [
        pltpu.make_async_copy(source, target, save_sem.at[which])
        for which, (source, target) in enumerate(
            (
                (normed, normed_hbm),
                (out_full, out_full_hbm),
                (mixed, mixed_hbm),
                (lead, lead_hbm),
                (starts, start_hbm),
                (gated, gated_hbm),
            )
        )
    ]
    saves[0].start()
    row_tile, column_tile = 256, 512

    def pre_save(index):
        rows = pl.ds(pl.multiple_of(index * row_tile, row_tile), row_tile)
        return pltpu.make_async_copy(pre.at[rows], pre_hbm.at[rows], pre_sem.at[index])

    def depth_of(distance):
        first = 2 * gather.partner(distance) * block
        return pl.ds(pl.multiple_of(first, 2 * block), 2 * block)

    def product(distance):
        depth = depth_of(distance)

        def row_body(index, _):
            rows = pl.ds(pl.multiple_of(index * row_tile, row_tile), row_tile)
            left = normed[rows, depth]

            def column_body(column, _):
                columns = pl.ds(pl.multiple_of(column * column_tile, column_tile), column_tile)
                value = mm_nn(left, full[depth, columns])
                if distance > 0:
                    value = value + pre[rows, columns]
                pre[rows, columns] = value
                return 0

            lax.fori_loop(0, full.shape[1] // column_tile, column_body, 0)
            if distance == chips - 1:
                pre_save(index).start()
            return 0

        lax.fori_loop(0, tokens // row_tile, row_body, 0)

    def full_save(distance):
        depth = depth_of(distance)
        return pltpu.make_async_copy(full.at[depth], full_hbm.at[depth], full_sem.at[distance])

    def use(distance):
        gather.arrive_from(distance)
        full_save(distance).start()
        product(distance)

    use(0)
    gather.stage(0)
    gather.stage(1)
    if gather.relayed:
        use(1)
        use(2)
    gather.stage(2)
    if gather.relayed:
        use(3)
    else:
        for distance in range(1, chips):
            use(distance)
    out_gather.stage(0)
    out_gather.stage(1)

    state_scr[...] = jnp.zeros_like(state_scr)
    run_scr[...] = jnp.zeros_like(run_scr)

    def recur(step, _):
        rows = pl.ds(pl.multiple_of(step * BLOCK, BLOCK), BLOCK)
        counts, keep = count_ref[rows], keep_ref[rows]
        row_ids, col_ids, linked, fresh, tail, closing = block_masks(counts, flags_ref[step])
        tri = (row_ids >= col_ids).astype(BF16)
        query_pre = pre[rows, :width]
        values = pre[rows, 2 * width : 3 * width].astype(BF16)
        keys = open_ref[...] * jax.nn.sigmoid(-pre[rows, width : 2 * width])
        cum = split_sum(tri, jnp.log1p(-keys))
        ending = cum[BLOCK - 1 : BLOCK, :]
        lifted = query_pre * jax.nn.sigmoid(query_pre) * jnp.exp(cum)
        lowered = (keys * jnp.exp(-cum) * keep).astype(BF16)
        moved = (keys * jnp.exp(ending - cum) * (keep * tail)).astype(BF16)
        run = run_scr[...]
        lead[rows] = (lifted * jnp.exp(run) * (counts == 0).astype(F32)).astype(BF16)
        run_ref[step] = run
        run_scr[...] = run + ending
        fresh_lifted = (lifted * fresh).astype(BF16)
        lifted = lifted.astype(BF16)
        end_decay = jnp.exp(ending) * closing
        for head in range(head_count):
            part = slice(head * lanes, (head + 1) * lanes)
            state = state_scr[head]
            starts[step, head] = state
            scores = jnp.where(linked, mm_nt(lifted[:, part], lowered[:, part]), 0.0)
            results = mm_nn(scores.astype(BF16), values[:, part])
            results = results + mm_nt(fresh_lifted[:, part], state.astype(BF16))
            mixed[rows, part] = results * (key_scale * keep)
            state_scr[head] = state * end_decay[:, part] + mm_tn(values[:, part], moved[:, part])
        return 0

    lax.fori_loop(0, tokens // BLOCK, recur, 0)
    saves[3].start()
    saves[4].start()

    last_count = flags_ref[tokens // BLOCK - 1][2:3, 0:1]
    for head in range(head_count):
        part = slice(head * lanes, (head + 1) * lanes)
        message[head * lanes : (head + 1) * lanes] = state_scr[head]
        decay = jnp.exp(run_scr[:, part]) * (last_count == 0).astype(F32)
        decay_ref[head] = decay
        message[state_rows + 8 + head : state_rows + 9 + head] = decay
    message[state_rows : state_rows + 1] = first_id
    message[state_rows + 1 : state_rows + 2] = last_id

    def state_copy(shift):
        return pltpu.make_async_remote_copy(
            message,
            received.at[shift - 1],
            state_send.at[shift - 1],
            state_recv.at[shift - 1],
            device_id=later(shift),
            device_id_type=MESH_ID,
        )

    for shift in range(1, context_size):

        @pl.when(context + shift < context_size)
        def _(shift=shift):
            state_copy(shift).start()

    out_gather.stage(2)
    carry_ref[...] = jnp.zeros_like(carry_ref)
    link_ref[...] = jnp.zeros_like(link_ref)
    for shift in range(1, context_size):

        @pl.when(context >= shift)
        def _(shift=shift):
            state_copy(shift).wait_recv()
            linked = jnp.ones((1, lanes), F32)
            follower = first_id
            factors = [jnp.ones((1, lanes), F32)] * head_count
            for near in range(shift):
                got = received.at[near]
                linked = (got[state_rows + 1 : state_rows + 2] == follower).astype(F32)
                follower = got[state_rows : state_rows + 1]
                factors = [factor * linked for factor in factors]
                if near < shift - 1:
                    factors = [
                        factor * got[state_rows + 8 + head : state_rows + 9 + head]
                        for head, factor in enumerate(factors)
                    ]
            if shift == 1:
                link_ref[0:1] = linked
            for head in range(head_count):
                rows = slice(head * lanes, (head + 1) * lanes)
                carry_ref[head] += factors[head] * received[shift - 1, rows]

    for shift in range(1, context_size):

        @pl.when(context + shift < context_size)
        def _(shift=shift):
            state_copy(shift).wait_send()

    for distance in range(chips):
        out_gather.arrive_from(distance)
    saves[1].start()

    def mix_save(index):
        rows = pl.ds(pl.multiple_of(index * row_tile, row_tile), row_tile)
        return pltpu.make_async_copy(mix.at[rows], mix_hbm.at[rows], mix_sem.at[index])

    def project(index, _):
        rows = pl.ds(pl.multiple_of(index * row_tile, row_tile), row_tile)
        for head in range(head_count):
            part = slice(head * lanes, (head + 1) * lanes)
            carried = mm_nt(lead[rows, part], carry_ref[head].astype(BF16))
            value = mixed[rows, part] + carried * (key_scale * keep_ref[rows])
            mixed[rows, part] = value
            gate = pre[rows, 3 * width + head * lanes : 3 * width + (head + 1) * lanes]
            unit = value * inverse_rms(value)
            gated[rows, part] = (
                unit * head_gain_ref[...] * (gate * jax.nn.sigmoid(gate))
            ).astype(BF16)
        left = gated[rows]

        def column_body(column, _):
            columns = pl.ds(pl.multiple_of(column * column_tile, column_tile), column_tile)
            mix[rows, columns] = mm_nt(left, out_full[columns, :]).astype(BF16)
            return 0

        lax.fori_loop(0, model_width // column_tile, column_body, 0)
        mix_save(index).start()
        return 0

    lax.fori_loop(0, tokens // row_tile, project, 0)
    saves[2].start()
    saves[5].start()
    gather.finish()
    out_gather.finish()
    for distance in range(chips):
        full_save(distance).wait()
    for save in saves:
        save.wait()
    for index in range(tokens // row_tile):
        pre_save(index).wait()
        mix_save(index).wait()


def forward(
    mesh_axes, collective, hidden, gain, shards, out_shard, down_shard, floor, segments, head_gain
):
    tokens, model_width = hidden.shape
    block, width = shards[0].shape
    lanes = head_gain.shape[1]
    head_count = width // lanes
    all_width = width * len(shards)
    blocks = tokens // BLOCK
    context_size = lax.axis_size("context")
    chips = lax.axis_size("shard") * context_size // 2
    messages = head_count * lanes + 8 + -(-head_count // 8) * 8
    whole = pl.BlockSpec(memory_space=pltpu.VMEM)
    remote = pl.BlockSpec(memory_space=pl.ANY)
    stored = [
        ((tokens, model_width), BF16),
        ((tokens, all_width), F32),
        ((model_width, all_width), BF16),
        ((model_width, width), BF16),
        ((tokens, width), F32),
        ((tokens, width), BF16),
        ((blocks, head_count, lanes, lanes), F32),
        ((tokens, width), BF16),
        ((tokens, model_width), BF16),
    ]
    kept = [
        (down_shard.shape[::-1], BF16),
        ((1, width), F32),
        ((tokens, 1), F32),
        ((tokens, 1), F32),
        ((blocks, 8, BLOCK), F32),
        ((blocks, 1, width), F32),
        ((head_count, lanes, lanes), F32),
        ((head_count, 1, lanes), F32),
        ((8, lanes), F32),
    ]
    return pl.pallas_call(
        partial(forward_kernel, mesh_axes, head_count, lanes ** (-0.5)),
        in_specs=[whole] * 2 + [remote] * 4 + [whole] * 5,
        out_specs=[remote] * len(stored) + [whole] * len(kept),
        out_shape=[jax.ShapeDtypeStruct(shape, kind) for shape, kind in stored + kept],
        scratch_shapes=[
            pltpu.VMEM((tokens, model_width), BF16),
            pltpu.VMEM((tokens, all_width), F32),
            pltpu.VMEM((block, all_width), BF16),
            pltpu.VMEM((block, width), BF16),
            pltpu.VMEM((model_width, all_width), BF16),
            pltpu.VMEM((model_width, width), BF16),
            pltpu.VMEM((tokens, width), F32),
            pltpu.VMEM((tokens, width), BF16),
            pltpu.VMEM((blocks, head_count, lanes, lanes), F32),
            pltpu.VMEM((tokens, width), BF16),
            pltpu.VMEM((tokens, model_width), BF16),
            pltpu.VMEM((head_count, lanes, lanes), F32),
            pltpu.VMEM((1, width), F32),
            pltpu.VMEM((messages, lanes), F32),
            pltpu.VMEM((context_size - 1, messages, lanes), F32),
            pltpu.SemaphoreType.DMA((4,)),
            pltpu.SemaphoreType.DMA((chips,)),
            pltpu.SemaphoreType.DMA((6,)),
            pltpu.SemaphoreType.DMA((tokens // 256,)),
            pltpu.SemaphoreType.DMA((tokens // 256,)),
            pltpu.SemaphoreType.DMA((context_size - 1,)),
            pltpu.SemaphoreType.DMA((context_size - 1,)),
        ]
        + gather_sems(1)
        + gather_sems(1),
        compiler_params=pltpu.CompilerParams(
            collective_id=collective, has_side_effects=True, vmem_limit_bytes=56 << 20
        ),
        cost_estimate=pl.CostEstimate(
            flops=2 * tokens * model_width * all_width,
            bytes_accessed=200_000_000,
            transcendentals=tokens * width * 9,
        ),
        name="forward",
    )(hidden, gain, *shards, out_shard, down_shard, floor, segments, head_gain)


def closing_kernel(
    count,
    ffn_ref,
    out_share_ref,
    *refs,
):
    moved_in, refs = refs[:count], refs[count:]
    gate_ref, up_ref, down_ref, out_ref = refs[:4]
    moved_out, held = refs[4 : 4 + count], refs[4 + count : 4 + 2 * count]
    load_sem, store_sem = refs[4 + 2 * count :]
    pieces = 4
    loads, stores = [], []
    for which, (source, middle_ref, target) in enumerate(zip(moved_in, held, moved_out)):
        length = source.shape[0] // pieces
        for index in range(pieces):
            rows = pl.ds(index * length, length)
            inside = middle_ref.at[rows]
            loads.append(
                pltpu.make_async_copy(source.at[rows], inside, load_sem.at[which, index])
            )
            stores.append(
                pltpu.make_async_copy(inside, target.at[rows], store_sem.at[which, index])
            )
    for load in loads:
        load.start()
    hidden_width = gate_ref.shape[1]
    for load, store in zip(loads, stores):
        load.wait()
        store.start()
    gate_ref[...] = ffn_ref[:, :hidden_width].astype(F32)
    up_ref[...] = ffn_ref[:, hidden_width : 2 * hidden_width].astype(F32)
    for first in range(0, hidden_width, 128):
        columns = slice(2 * hidden_width + first, 2 * hidden_width + first + 128)
        down_ref[first : first + 128] = ffn_ref[:, columns].astype(F32).T
    for first in range(0, out_share_ref.shape[1], 128):
        out_ref[first : first + 128] = out_share_ref[:, first : first + 128].T
    for store in stores:
        store.wait()


def closing(share_ffn, share_out, moved):
    block, all_width = share_ffn.shape
    hidden_width = all_width // 3
    whole = pl.BlockSpec(memory_space=pltpu.VMEM)
    remote = pl.BlockSpec(memory_space=pl.ANY)
    return pl.pallas_call(
        partial(closing_kernel, len(moved)),
        in_specs=[whole] * 2 + [remote] * len(moved),
        out_specs=[whole] * 4 + [remote] * len(moved),
        out_shape=[
            jax.ShapeDtypeStruct((block, hidden_width), F32),
            jax.ShapeDtypeStruct((block, hidden_width), F32),
            jax.ShapeDtypeStruct((hidden_width, block), F32),
            jax.ShapeDtypeStruct(share_out.shape[::-1], F32),
        ]
        + [jax.ShapeDtypeStruct(value.shape, value.dtype) for value in moved],
        scratch_shapes=[pltpu.VMEM(value.shape, value.dtype) for value in moved]
        + [pltpu.SemaphoreType.DMA((len(moved), 4))] * 2,
        compiler_params=pltpu.CompilerParams(vmem_limit_bytes=61 << 20),
        cost_estimate=pl.CostEstimate(flops=0, bytes_accessed=30_000_000, transcendentals=0),
        name="closing",
    )(share_ffn, share_out, *moved)


def local(
    mesh_axes,
    hidden,
    segment_ids,
    norm1_gain,
    w_query,
    w_forget,
    w_input,
    w_gate_out,
    forget_floor,
    head_gain,
    w_out,
    norm2_gain,
    w_ffn_gate,
    w_ffn_up,
    w_ffn_down,
    out_grad,
):
    sequences, span_len, model_width = hidden.shape
    tokens = sequences * span_len
    head_count, key_dim = forget_floor.shape
    width = head_count * key_dim
    key_scale = key_dim ** (-0.5)
    both = ("shard", "context")
    gain_one, gain_two = norm1_gain.reshape(1, -1), norm2_gain.reshape(1, -1)
    hidden_rows = hidden.reshape(tokens, model_width)
    gain_row = head_gain.reshape(1, -1)
    segments = segment_ids.reshape(tokens // BLOCK, BLOCK).astype(F32)
    (
        normed_one,
        pre,
        mixer_full,
        out_full,
        mixed,
        lead,
        starts,
        gated_low,
        mix_part,
        down_turned,
        open_part,
        counts,
        keep,
        flags,
        runs,
        carry,
        decay,
        link,
    ) = forward(
        mesh_axes,
        4,
        hidden_rows,
        gain_one,
        (w_query, w_forget, w_input, w_gate_out),
        w_out,
        w_ffn_down,
        forget_floor,
        segments,
        gain_row,
    )
    grad_rows = out_grad.reshape(tokens, model_width)
    (
        grad_mix_low,
        grad_norm_two,
        residual,
        _,
        _,
        _,
        feed_part,
        grad_residual,
        grads_ffn,
    ) = middle(
        mesh_axes,
        2,
        mix_part,
        grad_rows,
        hidden_rows,
        gain_two,
        w_ffn_gate,
        w_ffn_up,
        down_turned,
    )
    (
        output_rows,
        grad_head_part,
        grad_floor_part,
        back_one,
        grads_mixer,
    ) = output_line(
        mesh_axes,
        1,
        (
            runs,
            carry,
            decay,
            link,
            open_part,
            counts,
            keep,
            flags,
            gain_row,
        ),
        (
            feed_part,
            residual,
            gated_low,
            grad_mix_low,
            out_full,
            lead,
            starts,
            normed_one,
            pre,
            mixer_full,
            mixed,
        ),
        head_count,
    )
    share_ffn = lax.psum_scatter(grads_ffn, both, scatter_dimension=0, tiled=True)
    input_rows, near, total, *mixer_shares, share_out = input_line(
        mesh_axes,
        3,
        back_one,
        hidden_rows,
        grad_residual,
        gain_one,
        grads_mixer,
        (grad_norm_two, grad_head_part, grad_floor_part),
    )
    near, total = near.reshape(-1), total.reshape(-1)
    shares = lax.axis_size("shard") * lax.axis_size("context")
    position = lax.axis_index("shard") * lax.axis_size("context") + lax.axis_index("context")

    def own_slice(first, length):
        length = length // shares
        return lax.dynamic_slice_in_dim(total, first + position * length, length, 0)

    first = 2 * model_width + key_dim
    floor_total = near[first : first + width].reshape(head_count, key_dim)
    floor_part = key_dim // shares

    share_gate, share_up, share_down, share_out, output_rows, input_rows, *mixer_shares = closing(
        share_ffn, share_out, (output_rows, input_rows, *mixer_shares)
    )
    return (
        output_rows.reshape(hidden.shape),
        input_rows.reshape(hidden.shape),
        own_slice(0, model_width),
        *mixer_shares,
        lax.dynamic_slice_in_dim(floor_total, position * floor_part, floor_part, 1),
        own_slice(2 * model_width, key_dim),
        share_out,
        own_slice(model_width, model_width),
        share_gate,
        share_up,
        share_down,
    )


def solution(mesh):
    in_specs = (
        P("shard", "context", None),
        P("shard", "context"),
        P(),
        P(("shard", "context"), "tensor"),
        P(("shard", "context"), "tensor"),
        P(("shard", "context"), "tensor"),
        P(("shard", "context"), "tensor"),
        P("tensor", None),
        P(),
        P("tensor", ("shard", "context")),
        P(),
        P(("shard", "context"), "tensor"),
        P(("shard", "context"), "tensor"),
        P("tensor", ("shard", "context")),
        P("shard", "context", None),
    )
    out_specs = (
        P("shard", "context", None),
        P("shard", "context", None),
        P(("shard", "context")),
        P(("shard", "context"), "tensor"),
        P(("shard", "context"), "tensor"),
        P(("shard", "context"), "tensor"),
        P(("shard", "context"), "tensor"),
        P("tensor", ("shard", "context")),
        P(("shard", "context")),
        P("tensor", ("shard", "context")),
        P(("shard", "context")),
        P(("shard", "context"), "tensor"),
        P(("shard", "context"), "tensor"),
        P("tensor", ("shard", "context")),
    )
    return jax.shard_map(
        partial(local, mesh.axis_names), mesh=mesh, in_specs=in_specs, out_specs=out_specs, check_vma=False)
```
